32 devices in a mesh: dp: 4 (over y, x), mp: 8 (over z, core).
Axes of the slice: x: 2, y: 2, z: 4, core: 2. Of those that a mesh axis runs over, the one named last changes fastest.
Arguments:
- fields: float32 [4, 2048, 192], P('dp', 'mp'), may hold values from -6 to 6
- targets: float32 [4, 2, 2048, 192], P('dp', None, 'mp'), may hold values from -6 to 6
- land_mask: int32 [4, 2048, 4], P('dp', 'mp'), may hold values 0 or 1
- lead_index: int32 [4, 2], P('dp'), may hold values from 0 to 6
- var_ids: int32 [48], replicated, may hold values from 0 to 47, each once
- tables: float32 [440, 1024], replicated, may hold values from -4 to 4
- norm_gains: float32 [6, 1024], replicated, may hold values from -0.5 to 1.4, as said below
- tables_first: float32 [440, 1024], replicated, may hold values from -9.536743e-06 to 9.536743e-06
- tables_second: float32 [440, 1024], replicated, may hold values from 9.586172e-14 to 1.5337875e-12
- gains_first: float32 [6, 1024], replicated, may hold values from -3.8146973e-05 to 3.8146973e-05
- gains_second: float32 [6, 1024], replicated, may hold values from 1.5337875e-12 to 2.45406e-11
- w_qkv: float32 [1024, 3072], P(None, 'mp'), may hold values from -0.1875 to 0.1875
- qkv_first: float32 [1024, 3072], P('dp', 'mp'), may hold values from -9.536743e-06 to 9.536743e-06
- qkv_second: float32 [1024, 3072], P('dp', 'mp'), may hold values from 9.586172e-14 to 1.5337875e-12
- w_out: float32 [1024, 1024], P('mp'), may hold values from -0.5 to 0.5
- out_first: float32 [1024, 1024], P('mp', 'dp'), may hold values from -9.536743e-06 to 9.536743e-06
- out_second: float32 [1024, 1024], P('mp', 'dp'), may hold values from 9.586172e-14 to 1.5337875e-12
- w_up: float32 [1024, 4096], P(None, 'mp'), may hold values from -0.1875 to 0.1875
- up_first: float32 [1024, 4096], P('dp', 'mp'), may hold values from -9.536743e-06 to 9.536743e-06
- up_second: float32 [1024, 4096], P('dp', 'mp'), may hold values from 9.586172e-14 to 1.5337875e-12
- w_down: float32 [4096, 1024], P('mp'), may hold values from -0.09375 to 0.09375
- down_first: float32 [4096, 1024], P('mp', 'dp'), may hold values from -9.536743e-06 to 9.536743e-06
- down_second: float32 [4096, 1024], P('mp', 'dp'), may hold values from 9.586172e-14 to 1.5337875e-12
- qkv_average: float32 [1024, 3072], P('dp', 'mp'), may hold values from -0.1875 to 0.1875
Outputs:
- loss: float32 [], replicated
- grad_norm: float32 [], replicated
- tables_new: float32 [440, 1024], replicated
- tables_first_new: float32 [440, 1024], replicated
- tables_second_new: float32 [440, 1024], replicated
- gains_new: float32 [6, 1024], replicated
- gains_first_new: float32 [6, 1024], replicated
- gains_second_new: float32 [6, 1024], replicated
- qkv_new: float32 [1024, 3072], P('dp', 'mp')
- qkv_first_new: float32 [1024, 3072], P('dp', 'mp')
- qkv_second_new: float32 [1024, 3072], P('dp', 'mp')
- out_new: float32 [1024, 1024], P('mp', 'dp')
- out_first_new: float32 [1024, 1024], P('mp', 'dp')
- out_second_new: float32 [1024, 1024], P('mp', 'dp')
- up_new: float32 [1024, 4096], P('dp', 'mp')
- up_first_new: float32 [1024, 4096], P('dp', 'mp')
- up_second_new: float32 [1024, 4096], P('dp', 'mp')
- down_new: float32 [4096, 1024], P('mp', 'dp')
- down_first_new: float32 [4096, 1024], P('mp', 'dp')
- down_second_new: float32 [4096, 1024], P('mp', 'dp')
- qkv_average_new: float32 [1024, 3072], P('dp', 'mp')
The draws below stay inside these ranges and needn't reach their ends.
Inputs may be any that keep to these rules, and one draw needn't show every extreme that they name: `var_ids`: each value once. `norm_gains`: even rows gains, odd rows biases.
All inputs are finite; a program needn't handle non-finite values. No bound on the sum of `land_mask` on one device may be relied on, other than what follows from the above.
Results may differ from the reference program's by a relative error of at most 0.0054.
The reference program's roundings to bfloat16 on the way count: a program that leaves them out, or rounds other values in their place, can miss the bound.
Values may be sent and summed in bfloat16 or wider, within the bound.
A program may use at most 256 MiB of HBM per device.

```python
import math
import jax
import jax.numpy as jnp
from jax import lax

D = 1024
HEADS = 16
HEAD_DIM = 64
FF = 4096
V = 48
PATCH_ROWS = 32
PATCH_COLS = 64
LEADS = 7
QBLOCK = 512
PATCHES = 2048
SAMPLES = 4


def draw_tables(key, part):
    count_rows = 9 * V + LEADS + 1
    row_index = jnp.arange(count_rows)
    row_scale = jnp.where(row_index < 5 * V + LEADS, 0.5, jnp.where(row_index == 5 * V + LEADS, 1.5, D ** (-0.5)))
    drawn = jnp.clip(jax.random.normal(key, (count_rows, D), jnp.float32), -2.6, 2.6)
    return drawn * row_scale[:, None].astype(jnp.float32)


def draw_norm_gains(key, part):
    drawn = jnp.clip(jax.random.normal(key, (6, D), jnp.float32), -2.4, 2.4)
    is_gain = (jnp.arange(6) % 2 == 0)[:, None]
    return jnp.where(is_gain, 1.0 + 0.15 * drawn, 0.2 * drawn).astype(jnp.float32)


def set_ends(entries, rng, least, top_value):
    shape = entries.shape
    place = [jax.random.randint(jax.random.fold_in(rng, axis), (), 0, shape[axis]) for axis in range(len(shape))]
    entries = entries.at[tuple(place)].set(least)
    longest = shape.index(max(shape))
    place[longest] = (place[longest] + 1) % shape[longest]
    return entries.at[tuple(place)].set(top_value)


def level_of(stream_key, extent, shards, least, high):
    level = 1.0
    for position, shards_of in shards:
        heights = jax.random.uniform(jax.random.fold_in(jax.random.fold_in(stream_key, 6), position), (shards_of,), jnp.float32, least / len(shards), high / len(shards))
        level = level * jnp.repeat(jnp.exp(heights), extent[position] // shards_of).reshape((-1,) + (1,) * (len(extent) - 1 - position))
    return level


def scatter_about(key, extent, scale, most, shards=(), kind=jnp.bfloat16):
    array = jax.random.normal(key, extent, jnp.float32) * scale
    if len(shards) > 0:
        array = level_of(key, extent, shards, -0.22, 0.18) * array
    return jnp.clip(array, min=-most, max=most).astype(kind)


def setup_inputs(seed: int = 0) -> dict:
    splits = jax.random.split(jax.random.key(seed), 25)
    fields = scatter_about(splits[0], (SAMPLES, PATCHES, 4 * V), 1.0, 6.0, ((0, 4), (1, 8)), jnp.float32)
    targets = scatter_about(splits[1], (SAMPLES, 2, PATCHES, 4 * V), 1.0, 6.0, ((0, 4), (2, 8)), jnp.float32)
    land_mask = set_ends((jax.random.randint(splits[2], (SAMPLES, PATCHES, 4), 0, 10) < 3).astype(jnp.int32), jax.random.fold_in(splits[2], 1), 0, 1)
    lead_index = set_ends(jax.random.randint(splits[3], (SAMPLES, 2), 0, LEADS), jax.random.fold_in(splits[3], 1), 0, LEADS - 1).astype(jnp.int32)
    var_ids = jax.random.permutation(splits[4], V).astype(jnp.int32)
    tables = draw_tables(jax.random.fold_in(splits[24], 71), 0)
    norm_gains = draw_norm_gains(jax.random.fold_in(splits[24], 71), 0)
    tables_first = scatter_about(splits[7], (9 * V + LEADS + 1, D), (0.0056 * (4 * D * D + 2 * D * FF + (9 * V + LEADS + 7) * D) ** -0.5), 9.5367431640625e-06, (), jnp.float32)
    tables_second = jnp.clip(jnp.exp(jax.random.uniform(splits[8], (9 * V + LEADS + 1, D), jnp.float32, math.log(9.586172052553424e-14), math.log(1.5337875284085478e-12))), 9.586172052553424e-14, 1.5337875284085478e-12)
    gains_first = scatter_about(splits[9], (6, D), (0.022 * (4 * D * D + 2 * D * FF + (9 * V + LEADS + 7) * D) ** -0.5), 3.814697265625e-05, (), jnp.float32)
    gains_second = jnp.clip(jnp.exp(jax.random.uniform(splits[10], (6, D), jnp.float32, math.log(1.5337875284085478e-12), math.log(2.4540600454536765e-11))), 1.5337875284085478e-12, 2.4540600454536765e-11)
    w_qkv = scatter_about(splits[11], (D, 3 * D), D ** -0.5, 0.1875, ((1, 8),), jnp.float32)
    qkv_first = scatter_about(splits[12], (D, 3 * D), (0.0056 * (4 * D * D + 2 * D * FF + (9 * V + LEADS + 7) * D) ** -0.5), 9.5367431640625e-06, ((0, 4), (1, 8)), jnp.float32)
    qkv_second = jnp.clip(jnp.exp(math.log(1.5337875284085478e-12) - 2.7725887 * jax.random.uniform(splits[13], (D, 3 * D), jnp.float32) ** level_of(splits[13], (D, 3 * D), ((0, 4), (1, 8)), -0.2, 0.2)), 9.586172052553424e-14, 1.5337875284085478e-12)
    w_out = scatter_about(splits[14], (D, D), (D // 8) ** -0.5, 0.5, ((0, 8),), jnp.float32)
    out_first = scatter_about(splits[15], (D, D), (0.0056 * (4 * D * D + 2 * D * FF + (9 * V + LEADS + 7) * D) ** -0.5), 9.5367431640625e-06, ((0, 8), (1, 4)), jnp.float32)
    out_second = jnp.clip(jnp.exp(math.log(1.5337875284085478e-12) - 2.7725887 * jax.random.uniform(splits[16], (D, D), jnp.float32) ** level_of(splits[16], (D, D), ((0, 8), (1, 4)), -0.2, 0.2)), 9.586172052553424e-14, 1.5337875284085478e-12)
    w_up = scatter_about(splits[17], (D, FF), D ** -0.5, 0.1875, ((1, 8),), jnp.float32)
    up_first = scatter_about(splits[18], (D, FF), (0.0056 * (4 * D * D + 2 * D * FF + (9 * V + LEADS + 7) * D) ** -0.5), 9.5367431640625e-06, ((0, 4), (1, 8)), jnp.float32)
    up_second = jnp.clip(jnp.exp(math.log(1.5337875284085478e-12) - 2.7725887 * jax.random.uniform(splits[19], (D, FF), jnp.float32) ** level_of(splits[19], (D, FF), ((0, 4), (1, 8)), -0.2, 0.2)), 9.586172052553424e-14, 1.5337875284085478e-12)
    w_down = scatter_about(splits[20], (FF, D), FF ** -0.5, 0.09375, ((0, 8),), jnp.float32)
    down_first = scatter_about(splits[21], (FF, D), (0.0056 * (4 * D * D + 2 * D * FF + (9 * V + LEADS + 7) * D) ** -0.5), 9.5367431640625e-06, ((0, 8), (1, 4)), jnp.float32)
    down_second = jnp.clip(jnp.exp(math.log(1.5337875284085478e-12) - 2.7725887 * jax.random.uniform(splits[22], (FF, D), jnp.float32) ** level_of(splits[22], (FF, D), ((0, 8), (1, 4)), -0.2, 0.2)), 9.586172052553424e-14, 1.5337875284085478e-12)
    qkv_average = scatter_about(splits[23], (D, 3 * D), D ** -0.5, 0.1875, ((0, 4), (1, 8)), jnp.float32)
    return dict(fields=fields, targets=targets, land_mask=land_mask, lead_index=lead_index, var_ids=var_ids, tables=tables, norm_gains=norm_gains, tables_first=tables_first, tables_second=tables_second, gains_first=gains_first, gains_second=gains_second, w_qkv=w_qkv, qkv_first=qkv_first, qkv_second=qkv_second, w_out=w_out, out_first=out_first, out_second=out_second, w_up=w_up, up_first=up_first, up_second=up_second, w_down=w_down, down_first=down_first, down_second=down_second, qkv_average=qkv_average)


@jax.custom_vjp
def low(v):
    return lax.optimization_barrier(v.astype(jnp.bfloat16)).astype(jnp.float32)

@jax.custom_vjp
def low_back(v):
    return v

def low_keep(v):
    return (low(v), None)

def low_pass(kept, grad):
    return (grad,)

def back_keep(v):
    return (v, None)

def back_low(kept, grad):
    return (low(grad),)
low.defvjp(low_keep, low_pass)
low_back.defvjp(back_keep, back_low)
highest = lax.Precision.HIGHEST
eps_norm = 1e-05
clip_norm = 0.05
beta_first = 0.9
beta_second = 0.999
adam_eps = 1e-08
decay_rate = 0.1
lr_matrix = 0.04
lr_table = 0.1
lr_gain = 0.3
average_keep = 0.9
first_fix = 1.0 - 0.9 ** 10
second_fix = 1.0 - 0.999 ** 10

def layer_norm(values, gain, bias):
    center = values - lax.optimization_barrier(jnp.mean(values, axis=-1, keepdims=True))
    spread = lax.optimization_barrier(jnp.mean(center * center, axis=-1, keepdims=True))
    return center * lax.rsqrt(spread + eps_norm) * gain + bias

def lat_weights(pixel_rows):
    row_index = jnp.arange(pixel_rows, dtype=jnp.float32)
    cosine = jnp.cos(((row_index + 0.5) / pixel_rows - 0.5) * math.pi)
    return cosine / jnp.mean(cosine)

def embed_tokens(cells, tables, var_hot, lead_hot):
    count_rows = cells.shape[0]
    patch_tab = tables[:4 * V].reshape(V, 4, HEADS, HEAD_DIM)
    var_tab = jnp.dot(var_hot, tables[4 * V:5 * V], precision=highest).reshape(V, HEADS, HEAD_DIM)
    lead_vec = jnp.dot(lead_hot, tables[5 * V:5 * V + LEADS], precision=highest)
    query = tables[5 * V + LEADS].reshape(HEADS, HEAD_DIM)
    keyed = jnp.einsum('vphc,hc->vph', patch_tab, query, precision=highest)
    biased = jnp.einsum('vhc,hc->vh', var_tab, query, precision=highest)
    pixels = cells.reshape(count_rows, V, 4)
    scores = (jnp.einsum('tvp,vph->tvh', pixels, keyed, precision=highest) + biased) * HEAD_DIM ** (-0.5)
    shares = jax.nn.softmax(scores, axis=1)
    mixed = (shares[:, :, None, :] * pixels[:, :, :, None]).reshape(count_rows, 4 * V, HEADS)
    merged = jnp.einsum('tkh,khc->thc', mixed, patch_tab.reshape(4 * V, HEADS, HEAD_DIM), precision=highest)
    merged = merged + jnp.einsum('tvh,vhc->thc', shares, var_tab, precision=highest)
    return merged.reshape(count_rows, D) + lead_vec

def predict(last_rows, gain, bias, tables):
    normed = layer_norm(last_rows, gain, bias)
    return lax.dot_general(normed, tables[5 * V + LEADS + 1:], (((1,), (1,)), ((), ())), precision=highest)

def attend_ref(queries, keys, values):
    blocks = queries.reshape(PATCHES // QBLOCK, QBLOCK, HEADS, HEAD_DIM)

    def one_block(block):
        scores = low_back(jnp.einsum('qhc,khc->hqk', block, keys, precision=highest)) * HEAD_DIM ** (-0.5)
        probs = low(jax.nn.softmax(scores, axis=-1))
        return jnp.einsum('hqk,khc->qhc', probs, values, precision=highest)
    return lax.map(jax.checkpoint(one_block), blocks).reshape(PATCHES, D)

def layer_ref(x_first, norm_gains, w_qkv, w_out, w_up, w_down):
    rows_one = low(layer_norm(x_first, norm_gains[0], norm_gains[1]))
    packed = low_back(low(jnp.dot(rows_one, low(w_qkv), precision=highest))).reshape(PATCHES, HEADS, 3, HEAD_DIM)
    attended = low_back(low(attend_ref(packed[:, :, 0], packed[:, :, 1], packed[:, :, 2])))
    x_mid = x_first + low_back(jnp.dot(attended, low(w_out), precision=highest))
    rows_two = low(layer_norm(x_mid, norm_gains[2], norm_gains[3]))
    hidden = low_back(jnp.dot(rows_two, low(w_up), precision=highest))
    active = low(jax.nn.gelu(hidden, approximate=False))
    return x_mid + low_back(jnp.dot(active, low(w_down), precision=highest))

def sample_loss(params, inputs, answers, weighted, leads, var_hot):
    tables, norm_gains, w_qkv, w_out, w_up, w_down = params
    cells = inputs
    total = jnp.float32(0.0)
    for rollout in range(2):
        lead_hot = (jnp.arange(LEADS, dtype=jnp.int32) == leads[rollout]).astype(jnp.float32)
        start_rows = embed_tokens(cells, tables, var_hot, lead_hot)
        last_rows = layer_ref(start_rows, norm_gains, w_qkv, w_out, w_up, w_down)
        guess = predict(last_rows, norm_gains[4], norm_gains[5], tables)
        miss = guess - answers[rollout]
        total = total + jnp.sum(weighted * miss * miss)
        cells = guess
    return total

def adam_step(master, grad, first, second, rate):
    first_new = beta_first * first + (1.0 - beta_first) * grad
    second_new = beta_second * second + (1.0 - beta_second) * grad * grad
    update = first_new / first_fix / (jnp.sqrt(second_new / second_fix) + adam_eps)
    return (master - rate * (update + decay_rate * master), first_new, second_new)

def reference(fields, targets, land_mask, lead_index, var_ids, tables, norm_gains, tables_first, tables_second, gains_first, gains_second, w_qkv, qkv_first, qkv_second, w_out, out_first, out_second, w_up, up_first, up_second, w_down, down_first, down_second, qkv_average):
    ocean = 1.0 - land_mask.astype(jnp.float32)
    denom = 2.0 * V * jnp.maximum(jnp.sum(ocean), 1.0)
    var_hot = (var_ids[:, None] == jnp.arange(V, dtype=jnp.int32)[None, :]).astype(jnp.float32)
    lat_rows = lat_weights(2 * PATCH_ROWS).reshape(PATCH_ROWS, 2)
    lat_pixels = jnp.broadcast_to(jnp.repeat(lat_rows, PATCH_COLS, axis=0)[:, :, None], (PATCHES, 2, 2)).reshape(PATCHES, 4)
    weighted = jnp.tile(ocean * lat_pixels[None], (1, 1, V))
    params = (tables, norm_gains, w_qkv, w_out, w_up, w_down)

    def total_loss(params):

        def add_sample(total, item):
            inputs, answers, weight_rows, leads = item
            return (total + jax.checkpoint(sample_loss)(params, inputs, answers, weight_rows, leads, var_hot), None)
        total, _ = lax.scan(add_sample, jnp.float32(0.0), (fields, targets, weighted, lead_index))
        return total / denom
    loss, pull = jax.vjp(total_loss, params)
    grads = pull(jnp.ones_like(loss))[0]
    grad_norm = jnp.sqrt(sum((jnp.sum(grad * grad) for grad in grads)))
    factor = jnp.minimum(1.0, clip_norm / (grad_norm + 1e-06))
    tab = adam_step(tables, factor * grads[0], tables_first, tables_second, lr_table)
    gai = adam_step(norm_gains, factor * grads[1], gains_first, gains_second, lr_gain)
    qkv = adam_step(w_qkv, factor * grads[2], qkv_first, qkv_second, lr_matrix)
    outp = adam_step(w_out, factor * grads[3], out_first, out_second, lr_matrix)
    upp = adam_step(w_up, factor * grads[4], up_first, up_second, lr_matrix)
    down = adam_step(w_down, factor * grads[5], down_first, down_second, lr_matrix)
    average = average_keep * qkv_average + (1.0 - average_keep) * qkv[0]
    return (loss, grad_norm, tab[0], tab[1], tab[2], gai[0], gai[1], gai[2], qkv[0], qkv[1], qkv[2], outp[0], outp[1], outp[2], upp[0], upp[1], upp[2], down[0], down[1], down[2], average)
```

```python
from functools import partial
import math

import jax
import jax.numpy as jnp
from jax import lax
from jax.experimental import pallas as pl
from jax.experimental.pallas import tpu as pltpu
from jax.sharding import PartitionSpec as P

D = 1024
HEADS = 16
HEAD_DIM = 64
V = 48
PATCH_ROWS = 32
PATCH_COLS = 64
LEADS = 7


highest = lax.Precision.HIGHEST
eps_norm = 1e-05
clip_norm = 0.05
beta_first = 0.9
beta_second = 0.999
adam_eps = 1e-08
decay_rate = 0.1
lr_matrix = 0.04
lr_table = 0.1
lr_gain = 0.3
average_keep = 0.9
first_fix = 1.0 - 0.9**10
second_fix = 1.0 - 0.999**10


def layer_norm(values, gain, bias):
    center = values - jnp.mean(values, axis=-1, keepdims=True)
    spread = jnp.mean(center * center, axis=-1, keepdims=True)
    return center * lax.rsqrt(spread + eps_norm) * gain + bias


def lat_weights(pixel_rows):
    row_index = jnp.arange(pixel_rows, dtype=jnp.float32)
    cosine = jnp.cos(((row_index + 0.5) / pixel_rows - 0.5) * math.pi)
    return cosine / jnp.mean(cosine)


def embed_tokens(cells, tables, var_hot, lead_hot):
    count_rows = cells.shape[0]
    patch_tab = tables[: 4 * V].reshape(V, 4, HEADS, HEAD_DIM)
    var_tab = jnp.dot(var_hot, tables[4 * V : 5 * V], precision=highest).reshape(V, HEADS, HEAD_DIM)
    lead_vec = jnp.dot(lead_hot, tables[5 * V : 5 * V + LEADS], precision=highest)
    query = tables[5 * V + LEADS].reshape(HEADS, HEAD_DIM)
    keyed = jnp.einsum("vphc,hc->vph", patch_tab, query, precision=highest)
    biased = jnp.einsum("vhc,hc->vh", var_tab, query, precision=highest)
    pixels = cells.reshape(count_rows, V, 4)
    scores = (jnp.einsum("tvp,vph->tvh", pixels, keyed, precision=highest) + biased) * HEAD_DIM ** (
        -0.5
    )
    shares = jax.nn.softmax(scores, axis=1)
    mixed = (shares[:, :, None, :] * pixels[:, :, :, None]).reshape(count_rows, 4 * V, HEADS)
    merged = jnp.einsum(
        "tkh,khc->thc", mixed, patch_tab.reshape(4 * V, HEADS, HEAD_DIM), precision=highest
    )
    merged = merged + jnp.einsum("tvh,vhc->thc", shares, var_tab, precision=highest)
    return merged.reshape(count_rows, D) + lead_vec


bf16 = jnp.bfloat16
f32 = jnp.float32
MESH = pl.DeviceIdType.MESH
NT = (((1,), (1,)), ((), ()))
TN = (((0,), (0,)), ((), ()))
VMEM = pl.BlockSpec(memory_space=pltpu.VMEM)
BIG = 56 * 2**20


def is_crossed(sizes):
    return sizes["dp"] == 4 and sizes["mp"] == 8


def mesh_place():
    dp = lax.axis_index("dp")
    mp = lax.axis_index("mp")
    return dp, mp // 2, lax.rem(mp, 2)


def device_of(dp, level, core):
    return {"dp": dp, "mp": level * 2 + core}


def cross_pairs():
    groups = lax.axis_size("dp")
    pairs = []
    for dp in range(groups):
        for level in range(groups):
            for core in range(2):
                source = (dp * groups + level) * 2 + core
                target = (level * groups + dp) * 2 + core
                pairs.append((source, target))
    return pairs


def cross(crossed, value):
    if not crossed:
        return value
    return lax.ppermute(value, ("dp", "mp"), cross_pairs())


def gather_kernel(x_ref, o_ref, send_sem, recv_sem):
    rows = x_ref.shape[0]
    half = rows // 2
    dp, level, core = mesh_place()
    side = dp + 1 - 2 * lax.rem(dp, 2)
    down = lax.rem(dp + 2, 4)
    far = 3 - dp
    to_side = device_of(side, level, core)
    to_down = device_of(down, level, core)
    to_core = device_of(dp, level, 1 - core)

    def rows_of(owner, who, first, size):
        return pl.ds(pl.multiple_of((owner * 2 + who) * rows + first, half), size)

    barrier = pltpu.get_barrier_semaphore()
    for target in (to_side, to_down, to_core):
        pl.semaphore_signal(barrier, inc=1, device_id=target, device_id_type=MESH)
    pl.semaphore_wait(barrier, 3)

    def send(slot, source, where, target):
        copy = pltpu.make_async_remote_copy(
            src_ref=source,
            dst_ref=o_ref.at[where],
            send_sem=send_sem.at[slot],
            recv_sem=recv_sem.at[slot],
            device_id=target,
            device_id_type=MESH,
        )
        copy.start()
        return copy

    first = x_ref.at[pl.ds(0, half)]
    second = x_ref.at[pl.ds(half, half)]
    side_a = send(0, first, rows_of(dp, core, 0, half), to_side)
    down_b = send(1, second, rows_of(dp, core, half, half), to_down)
    side_b = send(2, second, rows_of(dp, core, half, half), to_side)
    down_a = send(3, first, rows_of(dp, core, 0, half), to_down)
    near = send(4, x_ref, rows_of(dp, core, 0, rows), to_core)
    o_ref[rows_of(dp, core, 0, rows)] = x_ref[...]
    side_a.wait_recv()
    place = rows_of(side, core, 0, half)
    far_a = send(5, o_ref.at[place], place, to_down)
    down_b.wait_recv()
    place = rows_of(down, core, half, half)
    far_b = send(6, o_ref.at[place], place, to_side)
    side_b.wait_recv()
    place = rows_of(side, core, 0, rows)
    near_side = send(7, o_ref.at[place], place, to_core)
    down_a.wait_recv()
    place = rows_of(down, core, 0, rows)
    near_down = send(8, o_ref.at[place], place, to_core)
    far_a.wait_recv()
    far_b.wait_recv()
    place = rows_of(far, core, 0, rows)
    near_far = send(9, o_ref.at[place], place, to_core)
    for copy in (near, near_side, near_down, near_far):
        copy.wait_recv()
    for copy in (side_a, down_b, side_b, down_a, near, far_a, far_b, near_side, near_down, near_far):
        copy.wait_send()


def spread_rows(crossed, normed):
    if not crossed:
        return lax.all_gather(normed, "mp", axis=0, tiled=True)
    rows, width = normed.shape
    return pl.pallas_call(
        gather_kernel,
        out_shape=jax.ShapeDtypeStruct((8 * rows, width), normed.dtype),
        in_specs=[VMEM],
        out_specs=VMEM,
        scratch_shapes=[pltpu.SemaphoreType.DMA((10,)), pltpu.SemaphoreType.DMA((10,))],
        compiler_params=pltpu.CompilerParams(
            collective_id=1, has_side_effects=True, vmem_limit_bytes=BIG
        ),
        name="gather_rows",
    )(normed)


def exchange_kernel(to_columns, rows, width, x_ref, o_ref, send_sem, recv_sem):
    dp, level, core = mesh_place()
    me = dp * 2 + core
    barrier = pltpu.get_barrier_semaphore()
    others = []
    for step in (7, 6, 5, 4, 3, 2, 1):
        part = lax.rem(me + step, 8)
        others.append((step, part, device_of(part // 2, level, lax.rem(part, 2))))
    for step, part, target in others:
        pl.semaphore_signal(barrier, inc=1, device_id=target, device_id_type=MESH)
    pl.semaphore_wait(barrier, 7)

    def row_block(ref, part):
        return ref.at[pl.ds(pl.multiple_of(part * rows, rows), rows), :]

    def column_block(ref, part):
        return ref.at[:, pl.ds(pl.multiple_of(part * width, width), width)]

    source_block, target_block = (
        (row_block, column_block) if to_columns else (column_block, row_block)
    )
    copies = []
    for step, part, target in others:
        copy = pltpu.make_async_remote_copy(
            src_ref=source_block(x_ref, part),
            dst_ref=target_block(o_ref, me),
            send_sem=send_sem.at[step],
            recv_sem=recv_sem.at[step],
            device_id=target,
            device_id_type=MESH,
        )
        copy.start()
        copies.append(copy)
    target_block(o_ref, me)[...] = source_block(x_ref, me)[...]
    for copy in copies:
        copy.wait()


def exchange(crossed, value, to_columns, number):
    parts = lax.axis_size("mp")
    if to_columns:
        rows, width = value.shape[0] // parts, value.shape[1]
        shape = (rows, width * parts)
    else:
        rows, width = value.shape[0], value.shape[1] // parts
        shape = (rows * parts, width)
    if not crossed:
        split, joined = (0, 1) if to_columns else (1, 0)
        return lax.all_to_all(value, "mp", split_axis=split, concat_axis=joined, tiled=True)
    return pl.pallas_call(
        partial(exchange_kernel, to_columns, rows, width),
        out_shape=jax.ShapeDtypeStruct(shape, value.dtype),
        in_specs=[VMEM],
        out_specs=VMEM,
        scratch_shapes=[pltpu.SemaphoreType.DMA((8,)), pltpu.SemaphoreType.DMA((8,))],
        compiler_params=pltpu.CompilerParams(
            collective_id=number, has_side_effects=True, vmem_limit_bytes=BIG
        ),
        name="exchange_parts",
    )(value)


def pick_head(value, head, heads):
    if heads == 1:
        return value
    lane = lax.broadcasted_iota(jnp.int32, value.shape, 1) // HEAD_DIM
    return jnp.where(lane == head, value, jnp.zeros_like(value))


def attend_kernel(heads, q_ref, k_ref, v_ref, o_ref, full_ref, lse_ref, vt_ref):
    @pl.when(pl.program_id(0) == 0)
    def _():
        vt_ref[...] = v_ref[...].T

    queries = q_ref[...] * bf16(HEAD_DIM**-0.5)
    keys = k_ref[...]
    outs = []
    for head in range(heads):
        scores = lax.dot_general(
            keys, pick_head(queries, head, heads), NT, preferred_element_type=f32
        )
        largest = jnp.max(scores, axis=0, keepdims=True)
        raised = jnp.exp(scores - largest)
        total = jnp.sum(raised, axis=0, keepdims=True)
        probs = (raised * (1.0 / total)).astype(bf16)
        values = vt_ref[head * HEAD_DIM : (head + 1) * HEAD_DIM, :]
        outs.append(jnp.dot(values, probs, preferred_element_type=f32))
        lse_ref[head : head + 1, :] = largest + jnp.log(total)
    flipped = outs[0] if heads == 1 else jnp.concatenate(outs, axis=0)
    full = flipped.T
    full_ref[...] = full
    o_ref[...] = full.astype(bf16)


def attend(packed):
    total, width = packed.shape[0], packed.shape[1] // 3
    heads = width // HEAD_DIM
    block = min(512, total)
    row_block = pl.BlockSpec((block, width), lambda i: (i, 0))
    return pl.pallas_call(
        partial(attend_kernel, heads),
        grid=(total // block,),
        out_shape=(
            jax.ShapeDtypeStruct((total, width), bf16),
            jax.ShapeDtypeStruct((total, width), f32),
            jax.ShapeDtypeStruct((heads, total), f32),
        ),
        in_specs=[
            row_block,
            pl.BlockSpec((total, width), lambda i: (0, 0)),
            pl.BlockSpec((total, width), lambda i: (0, 0)),
        ],
        out_specs=[row_block, row_block, pl.BlockSpec((heads, block), lambda i: (0, i))],
        scratch_shapes=[pltpu.VMEM((width, total), bf16)],
        compiler_params=pltpu.CompilerParams(vmem_limit_bytes=BIG),
        cost_estimate=pl.CostEstimate(
            flops=16 * total * total * width,
            bytes_accessed=10 * total * width,
            transcendentals=heads * total * total,
        ),
        name="attend",
    )(packed[:, :width], packed[:, width : 2 * width], packed[:, 2 * width :])


def attend_back_kernel(
    heads, q_ref, do_ref, full_ref, lse_ref, k_ref, v_ref, dq_ref, dk_ref, dv_ref, kt_ref, dk_sum, dv_sum
):
    step = pl.program_id(0)
    total = k_ref.shape[0]
    chunk = min(1024, total)

    @pl.when(step == 0)
    def _():
        kt_ref[...] = k_ref[...].T
        dk_sum[...] = jnp.zeros_like(dk_sum)
        dv_sum[...] = jnp.zeros_like(dv_sum)

    scale = HEAD_DIM**-0.5
    queries = q_ref[...]
    grads = do_ref[...]
    products = (grads.astype(f32) * full_ref[...]).T
    query_heads = [pick_head(queries, head, heads) for head in range(heads)]
    grad_heads = [pick_head(grads, head, heads) for head in range(heads)]
    inner = [
        jnp.sum(products[head * HEAD_DIM : (head + 1) * HEAD_DIM], axis=0, keepdims=True) * scale
        for head in range(heads)
    ]
    query_grads = [None] * heads
    for start in range(0, total, chunk):
        rows = slice(start, start + chunk)
        keys = k_ref[rows, :]
        values = v_ref[rows, :]
        value_part = None
        key_part = None
        for head in range(heads):
            scores = lax.dot_general(
                keys, query_heads[head] * bf16(scale), NT, preferred_element_type=f32
            )
            probs = jnp.exp(scores - lse_ref[head : head + 1, :])
            prob_grad = lax.dot_general(
                values, grad_heads[head] * bf16(scale), NT, preferred_element_type=f32
            )
            score_grad = (probs * (prob_grad - inner[head])).astype(bf16)
            one = jnp.dot(probs.astype(bf16), grad_heads[head], preferred_element_type=f32)
            two = jnp.dot(score_grad, query_heads[head], preferred_element_type=f32)
            value_part = one if value_part is None else value_part + one
            key_part = two if key_part is None else key_part + two
            three = jnp.dot(
                kt_ref[head * HEAD_DIM : (head + 1) * HEAD_DIM, rows],
                score_grad,
                preferred_element_type=f32,
            )
            query_grads[head] = three if query_grads[head] is None else query_grads[head] + three
        dv_sum[rows, :] += value_part
        dk_sum[rows, :] += key_part
    flipped = query_grads[0] if heads == 1 else jnp.concatenate(query_grads, axis=0)
    dq_ref[...] = flipped.T.astype(bf16)

    @pl.when(step == pl.num_programs(0) - 1)
    def _():
        dk_ref[...] = dk_sum[...].astype(bf16)
        dv_ref[...] = dv_sum[...].astype(bf16)


def attend_back(grad_out, packed, full, logsum):
    total, width = grad_out.shape
    heads = width // HEAD_DIM
    block = min(256, total)
    row_block = pl.BlockSpec((block, width), lambda i: (i, 0))
    whole = pl.BlockSpec((total, width), lambda i: (0, 0))
    query_grad, key_grad, value_grad = pl.pallas_call(
        partial(attend_back_kernel, heads),
        grid=(total // block,),
        out_shape=(jax.ShapeDtypeStruct((total, width), bf16),) * 3,
        in_specs=[
            row_block,
            row_block,
            row_block,
            pl.BlockSpec((heads, block), lambda i: (0, i)),
            whole,
            whole,
        ],
        out_specs=[row_block, whole, whole],
        scratch_shapes=[
            pltpu.VMEM((width, total), bf16),
            pltpu.VMEM((total, width), f32),
            pltpu.VMEM((total, width), f32),
        ],
        compiler_params=pltpu.CompilerParams(vmem_limit_bytes=BIG),
        cost_estimate=pl.CostEstimate(
            flops=40 * total * total * width,
            bytes_accessed=16 * total * width,
            transcendentals=heads * total * total,
        ),
        name="attend_back",
    )(
        packed[:, :width],
        grad_out,
        full,
        logsum,
        packed[:, width : 2 * width],
        packed[:, 2 * width :],
    )
    return jnp.concatenate((query_grad, key_grad, value_grad), axis=1)


def normed_parts(values):
    center = values - jnp.mean(values, axis=-1, keepdims=True)
    spread = jnp.mean(center * center, axis=-1, keepdims=True)
    inverse = lax.rsqrt(spread + eps_norm)
    return center * inverse, inverse


def norm_grad(unit, inverse, gain, grad):
    scaled = grad * gain
    middle = jnp.mean(scaled, axis=-1, keepdims=True)
    along = jnp.mean(scaled * unit, axis=-1, keepdims=True)
    gain_grad = jnp.sum(grad * unit, axis=0, keepdims=True)
    bias_grad = jnp.sum(grad, axis=0, keepdims=True)
    return inverse * (scaled - middle - unit * along), gain_grad, bias_grad


def gauss_share(values):
    return 0.5 * (1.0 + lax.erf(values * (0.5**0.5)))


def branch_kernel(
    o_ref, x0_ref, gains_ref, out_ref, up_ref, down_ref, head_ref,
    x1_ref, h2_ref, g_ref, act_ref, x2_ref, pred_ref,
):
    step = pl.program_id(0)

    @pl.when(step == 0)
    def _():
        x1_ref[...] = x0_ref[...] + jnp.dot(
            o_ref[...], out_ref[...], preferred_element_type=f32
        )
        unit, _ = normed_parts(x1_ref[...])
        h2_ref[...] = (unit * gains_ref[2:3, :] + gains_ref[3:4, :]).astype(bf16)
        x2_ref[...] = x1_ref[...]

    hidden = jnp.dot(h2_ref[...], up_ref[0], preferred_element_type=f32)
    g_ref[...] = hidden
    active = (hidden * gauss_share(hidden)).astype(bf16)
    act_ref[...] = active
    x2_ref[...] += jnp.dot(active, down_ref[...], preferred_element_type=f32)

    @pl.when(step == pl.num_programs(0) - 1)
    def _():
        unit, _ = normed_parts(x2_ref[...])
        last = unit * gains_ref[4:5, :] + gains_ref[5:6, :]
        pred_ref[...] = lax.dot_general(
            last, head_ref[...], NT, precision=highest, preferred_element_type=f32
        )


def weight_specs(w_out, w_up, w_down):
    _, width, units = w_up.shape
    return (
        pl.BlockSpec(w_out.shape, lambda i: (0, 0)),
        pl.BlockSpec((1, width, units), lambda i: (i, 0, 0)),
        pl.BlockSpec((units, width), lambda i: (i, 0)),
    )


def branch_forward(attended, x_first, norm_gains, gathered, head):
    w_out, w_up, w_down, _ = gathered
    rows, width = x_first.shape
    parts, units = w_up.shape[0], w_up.shape[2]
    fixed = lambda shape: pl.BlockSpec(shape, lambda i: (0, 0))
    by_units = pl.BlockSpec((rows, units), lambda i: (0, i))
    columns = head.shape[0]
    flops = 2 * rows * (width * width + 2 * width * parts * units + 6 * width * columns)
    return pl.pallas_call(
        branch_kernel,
        grid=(parts,),
        out_shape=(
            jax.ShapeDtypeStruct((rows, width), f32),
            jax.ShapeDtypeStruct((rows, width), bf16),
            jax.ShapeDtypeStruct((rows, parts * units), f32),
            jax.ShapeDtypeStruct((rows, parts * units), bf16),
            jax.ShapeDtypeStruct((rows, width), f32),
            jax.ShapeDtypeStruct((rows, columns), f32),
        ),
        in_specs=[
            fixed((rows, width)),
            fixed((rows, width)),
            fixed(norm_gains.shape),
            *weight_specs(w_out, w_up, w_down),
            fixed(head.shape),
        ],
        out_specs=[
            fixed((rows, width)),
            fixed((rows, width)),
            by_units,
            by_units,
            fixed((rows, width)),
            fixed((rows, columns)),
        ],
        compiler_params=pltpu.CompilerParams(vmem_limit_bytes=BIG),
        cost_estimate=pl.CostEstimate(
            flops=flops,
            bytes_accessed=4 * width * parts * units + 6 * rows * parts * units,
            transcendentals=rows * parts * units,
        ),
        name="branch_forward",
    )(attended, x_first, norm_gains, w_out, w_up, w_down, head)


def branch_back_kernel(
    dpred_ref, x2_ref, x1_ref, gains_ref, g_ref, out_ref, up_ref, down_ref, head_ref,
    dx2_ref, dg_ref, dx1_ref, low_ref, do_ref, gain_ref, dhead_ref,
    wide_ref, sum_ref,
):
    step = pl.program_id(0)

    @pl.when(step == 0)
    def _():
        grad = dpred_ref[...]
        unit, inverse = normed_parts(x2_ref[...])
        gain = gains_ref[4:5, :]
        last = unit * gain + gains_ref[5:6, :]
        dhead_ref[...] = lax.dot_general(
            grad, last, TN, precision=highest, preferred_element_type=f32
        )
        row_grad = jnp.dot(grad, head_ref[...], precision=highest, preferred_element_type=f32)
        wide, gain_grad, bias_grad = norm_grad(unit, inverse, gain, row_grad)
        gain_ref[...] = jnp.zeros_like(gain_ref)
        gain_ref[4:5, :] = gain_grad
        gain_ref[5:6, :] = bias_grad
        wide_ref[...] = wide
        dx2_ref[...] = wide.astype(bf16)
        sum_ref[...] = jnp.zeros_like(sum_ref)

    active_grad = lax.dot_general(dx2_ref[...], down_ref[...], NT, preferred_element_type=f32)
    hidden = g_ref[...]
    slope = gauss_share(hidden) + hidden * (
        jnp.exp(-0.5 * hidden * hidden) * (2.0 * math.pi) ** -0.5
    )
    hidden_grad = (active_grad * slope).astype(bf16)
    dg_ref[...] = hidden_grad
    sum_ref[...] += lax.dot_general(hidden_grad, up_ref[0], NT, preferred_element_type=f32)

    @pl.when(step == pl.num_programs(0) - 1)
    def _():
        unit, inverse = normed_parts(x1_ref[...])
        middle, gain_grad, bias_grad = norm_grad(unit, inverse, gains_ref[2:3, :], sum_ref[...])
        gain_ref[2:3, :] = gain_grad
        gain_ref[3:4, :] = bias_grad
        middle = wide_ref[...] + middle
        dx1_ref[...] = middle
        low_ref[...] = middle.astype(bf16)
        total = lax.dot_general(low_ref[...], out_ref[...], NT, preferred_element_type=f32)
        do_ref[...] = total.astype(bf16)


def branch_backward(pred_grad, x_last, x_mid, norm_gains, hidden, gathered, head):
    w_out, w_up, w_down, _ = gathered
    rows, width = x_last.shape
    parts, units = w_up.shape[0], w_up.shape[2]
    fixed = lambda shape: pl.BlockSpec(shape, lambda i: (0, 0))
    by_units = pl.BlockSpec((rows, units), lambda i: (0, i))
    columns = head.shape[0]
    wide = (rows, width)
    flops = 2 * rows * (width * width + 2 * width * parts * units + 12 * width * columns)
    return pl.pallas_call(
        branch_back_kernel,
        grid=(parts,),
        out_shape=(
            jax.ShapeDtypeStruct(wide, bf16),
            jax.ShapeDtypeStruct((rows, parts * units), bf16),
            jax.ShapeDtypeStruct(wide, f32),
            jax.ShapeDtypeStruct(wide, bf16),
            jax.ShapeDtypeStruct(wide, bf16),
            jax.ShapeDtypeStruct((6, width), f32),
            jax.ShapeDtypeStruct((columns, width), f32),
        ),
        in_specs=[
            fixed((rows, columns)),
            fixed(wide),
            fixed(wide),
            fixed(norm_gains.shape),
            by_units,
            *weight_specs(w_out, w_up, w_down),
            fixed(head.shape),
        ],
        out_specs=[
            fixed(wide),
            by_units,
            fixed(wide),
            fixed(wide),
            fixed(wide),
            fixed((6, width)),
            fixed((columns, width)),
        ],
        scratch_shapes=[pltpu.VMEM(wide, f32), pltpu.VMEM(wide, f32)],
        compiler_params=pltpu.CompilerParams(vmem_limit_bytes=BIG),
        cost_estimate=pl.CostEstimate(
            flops=flops,
            bytes_accessed=4 * width * parts * units + 6 * rows * parts * units,
            transcendentals=2 * rows * parts * units,
        ),
        name="branch_backward",
    )(pred_grad, x_last, x_mid, norm_gains, hidden, w_out, w_up, w_down, head)


def wide_piece(piece):
    half = piece.shape[0] // 2
    return jnp.concatenate((piece[:half], piece[half:]), axis=1)


def tall_piece(piece):
    half = piece.shape[1] // 2
    return jnp.concatenate((piece[:, :half], piece[:, half:]), axis=0)


def both_steps(left_a, right_a, left_b, right_b):
    product = lax.dot_general(left_a[...], right_a[...], TN, preferred_element_type=f32)
    return product + lax.dot_general(left_b[...], right_b[...], TN, preferred_element_type=f32)


def down_pieces(refs):
    product = both_steps(*refs)
    share = product.shape[1] // 4
    return [wide_piece(product[:, i * share : (i + 1) * share]) for i in range(4)]


def up_out_pieces(refs):
    up = both_steps(*refs[:4])
    share = up.shape[0] // 4
    out = both_steps(*refs[4:])
    size = out.shape[1] // 4
    return [
        jnp.concatenate(
            (up[i * share : (i + 1) * share], wide_piece(out[:, i * size : (i + 1) * size])), axis=0
        )
        for i in range(4)
    ]


def outer_other_kernel(make, count, where_ref, *refs):
    o_ref = refs[count]
    for split, piece in enumerate(make(refs[:count])):
        o_ref[0, split] = piece.astype(bf16)


def outer_own_kernel(make, count, where_ref, *refs):
    other_ref, send_ref, keep_ref, held_ref = refs[count:]
    for split, piece in enumerate(make(refs[:count])):
        held_ref[split] = (piece + other_ref[0, split].astype(f32)).astype(bf16)
    x, y = where_ref[1], where_ref[2]
    early = pl.program_id(0) < 2
    for which in range(2):
        send_ref[0, which] = held_ref[jnp.where(early, which * 2 + 1 - x, (1 - y) * 2 + which)]
        keep_ref[0, which] = held_ref[jnp.where(early, which * 2 + x, y * 2 + which)]


def outer_half(operands, make, height, where, other):
    specs = []
    for value, blocked in operands:
        rows, size = value.shape
        if blocked:
            specs.append(pl.BlockSpec((rows, size // 8), lambda i, w: (0, i * 2 + w[0])))
        else:
            specs.append(pl.BlockSpec((rows, size), lambda i, w: (0, 0)))
    values = [value for value, _ in operands]
    count = len(values)
    whole = pl.BlockSpec((1, 4, height, 512), lambda i, w: (i, 0, 0, 0))
    half = pl.BlockSpec((1, 2, height, 512), lambda i, w: (i, 0, 0, 0))
    rows = values[0].shape[0]
    cost = pl.CostEstimate(
        flops=2 * 2 * rows * 16 * height * 512, bytes_accessed=3 * 16 * height * 512, transcendentals=0
    )
    params = pltpu.CompilerParams(vmem_limit_bytes=BIG)
    if other is None:
        return pl.pallas_call(
            partial(outer_other_kernel, make, count),
            out_shape=jax.ShapeDtypeStruct((4, 4, height, 512), bf16),
            grid_spec=pltpu.PrefetchScalarGridSpec(
                num_scalar_prefetch=1, grid=(4,), in_specs=specs, out_specs=whole
            ),
            compiler_params=params,
            cost_estimate=cost,
            name="outer_other",
        )(where, *values)
    return pl.pallas_call(
        partial(outer_own_kernel, make, count),
        out_shape=(jax.ShapeDtypeStruct((4, 2, height, 512), bf16),) * 2,
        grid_spec=pltpu.PrefetchScalarGridSpec(
            num_scalar_prefetch=1,
            grid=(4,),
            in_specs=specs + [whole],
            out_specs=[half, half],
            scratch_shapes=[pltpu.VMEM((4, height, 512), bf16)],
        ),
        compiler_params=params,
        cost_estimate=cost,
        name="outer_own",
    )(where, *values, other)


def device_pairs(move):
    pairs = []
    for dp in range(4):
        for level in range(4):
            for core in range(2):
                to_dp, to_level, to_core = move(dp, level, core)
                pairs.append(((dp * 4 + level) * 2 + core, (to_dp * 4 + to_level) * 2 + to_core))
    return pairs


def shift(value, move):
    return lax.ppermute(value, ("dp", "mp"), device_pairs(move))


def to_core(dp, level, core):
    return dp, level, 1 - core


def to_side(dp, level, core):
    return dp ^ 1, level, core


def to_down(dp, level, core):
    return dp ^ 2, level, core


def choose(value, index, axis=0):
    return lax.dynamic_index_in_dim(value, index, axis, keepdims=False)


def sum_levels(pieces, level):
    total = choose(pieces, level).astype(f32)
    for step in range(1, 4):
        piece = choose(pieces, lax.rem(level + step, 4)).astype(bf16)
        moved = shift(piece, lambda dp, z, core: (dp, (z + step) % 4, core))
        total = total + moved.astype(f32)
    return total


def tie(*values):
    return lax.optimization_barrier(values)


def first_sums(send, keep):
    first = keep[:2].astype(f32) + shift(send[:2], to_side).astype(f32)
    second = keep[2:].astype(f32) + shift(send[2:], to_down).astype(f32)
    return first.astype(bf16), second.astype(bf16)


def second_sums(first, second, x, y):
    first_moved = shift(choose(first, 1 - y, 1), to_down)
    second_moved = shift(choose(second, 1 - x, 1), to_side)
    first = choose(first, y, 1).astype(f32) + first_moved.astype(f32)
    second = choose(second, x, 1).astype(f32) + second_moved.astype(f32)
    return jnp.concatenate((first, second))


def outer_plain(lefts, rights, by_rows):
    dp, mp = lax.axis_size("dp"), lax.axis_size("mp")
    grads = sum(
        lax.dot_general(left, right, TN, preferred_element_type=f32)
        for left, right in zip(lefts, rights)
    ).astype(bf16)
    rows, width = grads.shape
    if by_rows:
        grads = grads.reshape(dp, rows // dp, mp, width // mp).transpose(0, 2, 1, 3)
    else:
        grads = grads.reshape(mp, rows // mp, dp, width // dp).transpose(2, 0, 1, 3)
    grads = grads.reshape((dp * mp,) + grads.shape[2:])
    return lax.psum_scatter(grads, ("dp", "mp"), scatter_dimension=0, tiled=False).astype(f32)


def exchange_sum_kernel(
    x_ref, t_ref, o_ref, s_ref, work_ref, pair_ref, quad_ref, eight_ref, deep_ref, tile_ref,
    send_sem, recv_sem,
):
    dp, level, core = mesh_place()
    x, y = lax.rem(dp, 2), dp // 2
    side = device_of(dp + 1 - 2 * x, level, core)
    down = device_of(lax.rem(dp + 2, 4), level, core)
    near = device_of(dp, level, 1 - core)
    deep = [device_of(dp, lax.rem(level + step, 4), core) for step in (1, 2, 3)]
    barrier = pltpu.get_barrier_semaphore()
    for target in (side, down, near, *deep):
        pl.semaphore_signal(barrier, inc=1, device_id=target, device_id_type=MESH)
    pl.semaphore_wait(barrier, 6)
    started = []

    def send(source, target_ref, target):
        slot = len(started)
        copy = pltpu.make_async_remote_copy(
            src_ref=source,
            dst_ref=target_ref,
            send_sem=send_sem.at[slot],
            recv_sem=recv_sem.at[slot],
            device_id=target,
            device_id_type=MESH,
        )
        copy.start()
        started.append(copy)
        return copy

    half = x_ref.shape[0] // 2
    quarter, eighth, part, unit = half // 2, half // 4, half // 8, half // 16

    def rows(start, size):
        return pl.ds(pl.multiple_of(start, unit), size)

    copy = send(x_ref.at[rows((1 - core) * half, half)], pair_ref, near)
    copy.wait_recv()
    work_ref[...] = x_ref[rows(core * half, half)] + pair_ref[...]
    one = send(work_ref.at[rows((1 - x) * eighth, eighth)], quad_ref.at[0], side)
    two = send(work_ref.at[rows(quarter + (1 - y) * eighth, eighth)], quad_ref.at[1], down)
    base_a = x * eighth
    base_b = quarter + y * eighth
    wide_a, wide_b = core * half + base_a, core * half + base_b
    one.wait_recv()
    work_ref[rows(base_a, eighth)] += quad_ref[0]
    one = send(work_ref.at[rows(base_a + (1 - y) * part, part)], eight_ref.at[0], down)
    two.wait_recv()
    work_ref[rows(base_b, eighth)] += quad_ref[1]
    two = send(work_ref.at[rows(base_b + (1 - x) * part, part)], eight_ref.at[1], side)
    base_a = base_a + y * part
    base_b = base_b + x * part
    one.wait_recv()
    work_ref[rows(base_a, part)] += eight_ref[0]
    two.wait_recv()
    work_ref[rows(base_b, part)] += eight_ref[1]

    def level_start(which):
        late = which // 2
        return (1 - late) * base_a + late * base_b + lax.rem(which, 2) * unit

    copies = []
    for step in (1, 2, 3):
        source = work_ref.at[rows(level_start(lax.rem(level + step, 4)), unit)]
        copies.append(send(source, deep_ref.at[step - 1], deep[step - 1]))
    for copy in copies:
        copy.wait_recv()
    total = work_ref[rows(level_start(level), unit)] + deep_ref[0] + deep_ref[1] + deep_ref[2]
    mine = rows(core * half + level_start(level), unit)
    base_a = core * half + base_a
    base_b = core * half + base_b
    o_ref[mine] = total
    row = lax.broadcasted_iota(jnp.int32, t_ref.shape, 0)
    tile_ref[0] = t_ref[...] + jnp.where(row == 0, jnp.sum(total * total), 0.0)
    copies = []
    for step in (1, 2, 3):
        copies.append(send(o_ref.at[mine], o_ref.at[mine], deep[step - 1]))
        copies.append(send(tile_ref.at[0], tile_ref.at[step], deep[step - 1]))
    for copy in copies:
        copy.wait_recv()
    one = send(o_ref.at[rows(base_a, part)], o_ref.at[rows(base_a, part)], down)
    two = send(o_ref.at[rows(base_b, part)], o_ref.at[rows(base_b, part)], side)
    tile_ref[4] = tile_ref[0] + tile_ref[1] + tile_ref[2] + tile_ref[3]
    three = send(tile_ref.at[4], tile_ref.at[5], side)
    one.wait_recv()
    one = send(o_ref.at[rows(wide_a, eighth)], o_ref.at[rows(wide_a, eighth)], side)
    two.wait_recv()
    two = send(o_ref.at[rows(wide_b, eighth)], o_ref.at[rows(wide_b, eighth)], down)
    three.wait_recv()
    tile_ref[6] = tile_ref[4] + tile_ref[5]
    three = send(tile_ref.at[6], tile_ref.at[7], down)
    one.wait_recv()
    two.wait_recv()
    one = send(o_ref.at[rows(core * half, half)], o_ref.at[rows(core * half, half)], near)
    three.wait_recv()
    tile_ref[8] = tile_ref[6] + tile_ref[7]
    three = send(tile_ref.at[8], tile_ref.at[9], near)
    one.wait_recv()
    three.wait_recv()
    s_ref[...] = tile_ref[8] + tile_ref[9]
    for copy in started:
        copy.wait_send()


def exchange_sum(value, tile):
    rows, width = value.shape
    return pl.pallas_call(
        exchange_sum_kernel,
        out_shape=(jax.ShapeDtypeStruct(value.shape, f32), jax.ShapeDtypeStruct(tile.shape, f32)),
        in_specs=[VMEM, VMEM],
        out_specs=[VMEM, VMEM],
        scratch_shapes=[
            pltpu.VMEM((rows // 2, width), f32),
            pltpu.VMEM((rows // 2, width), f32),
            pltpu.VMEM((2, rows // 8, width), f32),
            pltpu.VMEM((2, rows // 16, width), f32),
            pltpu.VMEM((3, rows // 32, width), f32),
            pltpu.VMEM((10,) + tile.shape, f32),
            pltpu.SemaphoreType.DMA((24,)),
            pltpu.SemaphoreType.DMA((24,)),
        ],
        compiler_params=pltpu.CompilerParams(
            collective_id=5, has_side_effects=True, vmem_limit_bytes=BIG
        ),
        name="exchange_sum",
    )(value, tile)


def tile_sum_kernel(t_ref, s_ref, tile_ref, send_sem, recv_sem):
    dp, level, core = mesh_place()
    x = lax.rem(dp, 2)
    side = device_of(dp + 1 - 2 * x, level, core)
    down = device_of(lax.rem(dp + 2, 4), level, core)
    near = device_of(dp, level, 1 - core)
    deep = [device_of(dp, lax.rem(level + step, 4), core) for step in (1, 2, 3)]
    barrier = pltpu.get_barrier_semaphore()
    for target in (side, down, near, *deep):
        pl.semaphore_signal(barrier, inc=1, device_id=target, device_id_type=MESH)
    pl.semaphore_wait(barrier, 6)

    def send(slot, source, target_ref, target):
        copy = pltpu.make_async_remote_copy(
            src_ref=source,
            dst_ref=target_ref,
            send_sem=send_sem.at[slot],
            recv_sem=recv_sem.at[slot],
            device_id=target,
            device_id_type=MESH,
        )
        copy.start()
        return copy

    copies = [send(step, t_ref, tile_ref.at[step], deep[step]) for step in range(3)]
    for copy in copies:
        copy.wait()
    tile_ref[3] = t_ref[...] + tile_ref[0] + tile_ref[1] + tile_ref[2]
    send(3, tile_ref.at[3], tile_ref.at[4], side).wait()
    tile_ref[5] = tile_ref[3] + tile_ref[4]
    send(4, tile_ref.at[5], tile_ref.at[6], down).wait()
    tile_ref[7] = tile_ref[5] + tile_ref[6]
    send(5, tile_ref.at[7], tile_ref.at[8], near).wait()
    s_ref[...] = tile_ref[7] + tile_ref[8]


def sum_everywhere(crossed, value):
    if not crossed:
        return lax.psum(value, ("dp", "mp"))
    tile = jnp.broadcast_to(value, (8, 128))
    total = pl.pallas_call(
        tile_sum_kernel,
        out_shape=jax.ShapeDtypeStruct(tile.shape, f32),
        in_specs=[VMEM],
        out_specs=VMEM,
        scratch_shapes=[
            pltpu.VMEM((9,) + tile.shape, f32),
            pltpu.SemaphoreType.DMA((6,)),
            pltpu.SemaphoreType.DMA((6,)),
        ],
        compiler_params=pltpu.CompilerParams(collective_id=6, has_side_effects=True),
        name="tile_sum",
    )(tile)
    return total[0, 0]


def entry_back_kernel(grad_ref, qkv_ref, x0_ref, mid_ref, gains_ref, o_ref, gain_ref, sum_ref):
    sum_ref[...] = jnp.dot(grad_ref[...], qkv_ref[...], preferred_element_type=f32)
    unit, inverse = normed_parts(x0_ref[...])
    part, gain_grad, bias_grad = norm_grad(unit, inverse, gains_ref[0:1, :], sum_ref[...])
    o_ref[...] = mid_ref[...] + part
    gain_ref[0:1, :] = gain_grad
    gain_ref[1:2, :] = bias_grad


def entry_backward(token_grad, qkv_t, x_first, mid_grad, norm_gains):
    rows, width = x_first.shape
    return pl.pallas_call(
        entry_back_kernel,
        out_shape=(jax.ShapeDtypeStruct((rows, width), f32), jax.ShapeDtypeStruct((2, width), f32)),
        scratch_shapes=[pltpu.VMEM((rows, width), f32)],
        compiler_params=pltpu.CompilerParams(vmem_limit_bytes=BIG),
        name="entry_backward",
    )(token_grad, qkv_t, x_first, mid_grad, norm_gains)


def adam_step(master, grad, first, second, rate):
    first_new = beta_first * first + (1.0 - beta_first) * grad
    second_new = beta_second * second + (1.0 - beta_second) * grad * grad
    update = first_new / first_fix / (jnp.sqrt(second_new / second_fix) + adam_eps)
    return (master - rate * (update + decay_rate * master), first_new, second_new)


def by_kind(shard):
    rows = shard.shape[0]
    return shard.reshape(rows, -1, 3, HEAD_DIM).transpose(0, 2, 1, 3).reshape(rows, -1)


def by_head(shard):
    rows = shard.shape[0]
    return shard.reshape(rows, 3, -1, HEAD_DIM).transpose(0, 2, 1, 3).reshape(rows, -1)


def gather_weights_kernel(count, *refs):
    shards, outs = refs[:count], refs[count : 2 * count]
    send_sem, recv_sem, own_sem = refs[2 * count :]
    dp, level, core = mesh_place()
    x = lax.rem(dp, 2)
    columns = {"here": dp, "side": dp + 1 - 2 * x, "down": lax.rem(dp + 2, 4), "far": 3 - dp}
    side = device_of(columns["side"], level, core)
    down = device_of(columns["down"], level, core)
    near = device_of(dp, level, 1 - core)
    deep = [device_of(dp, lax.rem(level + step, 4), core) for step in (1, 2, 3)]
    barrier = pltpu.get_barrier_semaphore()
    for target in (side, down, near, *deep):
        pl.semaphore_signal(barrier, inc=1, device_id=target, device_id_type=MESH)
    pl.semaphore_wait(barrier, 6)
    started = []

    def send(source, target_ref, target):
        slot = len(started)
        copy = pltpu.make_async_remote_copy(
            src_ref=source,
            dst_ref=target_ref,
            send_sem=send_sem.at[slot],
            recv_sem=recv_sem.at[slot],
            device_id=target,
            device_id_type=MESH,
        )
        copy.start()
        started.append(copy)
        return copy

    def place(out, source, column, half=None):
        rows = out.shape[1] // 4
        start, size = columns[column] * rows, rows
        if half is not None:
            start, size = start + half * (rows // 2), rows // 2
        return out.at[source * 2 + core, pl.ds(pl.multiple_of(start, rows // 2), size), :]

    def pass_on(out, source, column, target, half=None):
        where = place(out, source, column, half)
        return send(where, where, target)

    chunks = []
    for index in range(count):
        rows = outs[index].shape[1] // 4
        own = shards[index].at[pl.ds(pl.multiple_of(dp * rows, rows), rows), :]
        for step in (1, 2, 3):
            copy = send(own, place(outs[index], level, "here"), deep[step - 1])
            chunks.append((outs[index], lax.rem(level + 4 - step, 4), copy))
    ends = []
    locals_ = []
    for index in range(count):
        ends.append(send(shards[index], outs[index].at[level * 2 + core], near))
        copy = pltpu.make_async_copy(
            shards[index], outs[index].at[level * 2 + core], own_sem.at[index]
        )
        copy.start()
        locals_.append(copy)
    plane, hops = {}, {}
    total = len(chunks)
    for step in range(total + 2):
        if step < total:
            out, source, copy = chunks[step]
            copy.wait_recv()
            plane[step] = (
                pass_on(out, source, "here", side),
                pass_on(out, source, "here", down),
            )
            ends.append(pass_on(out, source, "here", near))
        if 0 <= step - 1 < total:
            out, source, _ = chunks[step - 1]
            from_side, from_down = plane[step - 1]
            from_side.wait_recv()
            one = pass_on(out, source, "side", down, 0)
            from_down.wait_recv()
            two = pass_on(out, source, "down", side, 1)
            hops[step - 1] = (one, two)
            ends.append(pass_on(out, source, "side", near))
            ends.append(pass_on(out, source, "down", near))
        if 0 <= step - 2 < total:
            out, source, _ = chunks[step - 2]
            for copy in hops[step - 2]:
                copy.wait_recv()
            ends.append(pass_on(out, source, "far", near))
    for copy in ends:
        copy.wait_recv()
    for copy in started:
        copy.wait_send()
    for copy in locals_:
        copy.wait()


def gather_weights(crossed, shards):
    if not crossed:
        dp, mp = lax.axis_size("dp"), lax.axis_size("mp")
        return [lax.all_gather(shard, "mp") for shard in shards]
    count = len(shards)
    copies = count * 3 * 9 + count
    anywhere = pl.BlockSpec(memory_space=pl.ANY)
    return pl.pallas_call(
        partial(gather_weights_kernel, count),
        out_shape=[jax.ShapeDtypeStruct((8,) + shard.shape, bf16) for shard in shards],
        in_specs=[anywhere] * count,
        out_specs=[anywhere] * count,
        scratch_shapes=[
            pltpu.SemaphoreType.DMA((copies,)),
            pltpu.SemaphoreType.DMA((copies,)),
            pltpu.SemaphoreType.DMA((count,)),
        ],
        compiler_params=pltpu.CompilerParams(
            collective_id=7, has_side_effects=True, vmem_limit_bytes=BIG
        ),
        name="gather_weights",
    )(*shards)


def own_qkv_share(crossed, grad):
    dp = lax.axis_size("dp")
    rows = grad.shape[0] // dp
    if not crossed:
        return lax.psum_scatter(grad, "dp", scatter_dimension=0, tiled=True)
    _, level, _ = mesh_place()
    return cross(crossed, sum_levels(grad.reshape((dp, rows) + grad.shape[1:]), level))


def shards(
    crossed,
    fields,
    targets,
    land_mask,
    lead_index,
    var_ids,
    tables,
    norm_gains,
    tables_first,
    tables_second,
    gains_first,
    gains_second,
    w_qkv,
    qkv_first,
    qkv_second,
    w_out,
    out_first,
    out_second,
    w_up,
    up_first,
    up_second,
    w_down,
    down_first,
    down_second,
    qkv_average,
):
    local_samples, shard_rows, _ = fields.shape
    dp_size, parts = lax.axis_size("dp"), lax.axis_size("mp")
    dp_index = lax.axis_index("dp")
    place, level, core = mesh_place()
    part = place * 2 + core if crossed else lax.axis_index("mp")
    share_rows = D // dp_size

    def own_share(full, dim):
        return lax.dynamic_slice_in_dim(full, dp_index * share_rows, share_rows, dim)

    masters = (own_share(w_qkv, 0), own_share(w_out, 1), own_share(w_up, 0), own_share(w_down, 1))
    inputs = cross(crossed, fields[0])
    leads = cross(crossed, lead_index[0])
    qkv_local = cross(crossed, by_kind(w_qkv.astype(bf16)))
    low = lambda master: master.astype(bf16)
    w_outs, w_ups, w_downs = gather_weights(crossed, (low(w_out), low(w_up), low(w_down)))
    qkv_rows = 3 * D // (parts * dp_size)
    qkv_piece = lax.dynamic_slice_in_dim(by_kind(low(w_qkv)).T, dp_index * qkv_rows, qkv_rows, 0)
    w_outs, qkv_piece = tie(w_outs, qkv_piece)
    qkv_t = lax.all_gather(qkv_piece, ("mp", "dp"), axis=0, tiled=True)
    gathered = (w_outs.reshape(D, D), w_ups, w_downs.reshape(-1, D), qkv_t)
    answers = cross(crossed, targets[0])
    ocean = 1.0 - cross(crossed, land_mask[0]).astype(f32)
    count = sum_everywhere(crossed, jnp.sum(ocean))
    denom = 2.0 * V * jnp.maximum(count, 1.0)
    var_hot = (var_ids[:, None] == jnp.arange(V, dtype=jnp.int32)[None, :]).astype(f32)
    first_row = part * shard_rows
    patch_row = (first_row + jnp.arange(shard_rows, dtype=jnp.int32)) // PATCH_COLS
    row_hot = (patch_row[:, None] == jnp.arange(PATCH_ROWS, dtype=jnp.int32)[None, :]).astype(f32)
    lat_rows = jnp.dot(
        row_hot, lat_weights(2 * PATCH_ROWS).reshape(PATCH_ROWS, 2), precision=highest
    )
    lat_pixels = jnp.broadcast_to(lat_rows[:, :, None], (shard_rows, 2, 2)).reshape(shard_rows, 4)
    weighted = jnp.tile(ocean * lat_pixels, (1, V))
    head = tables[5 * V + LEADS + 1 :]
    loss_part = f32(0.0)
    records = []
    for rollout in range(2):
        lead_hot = (jnp.arange(LEADS, dtype=jnp.int32) == leads[rollout]).astype(f32)
        x_first, embed_pull = jax.vjp(
            lambda cells, table: embed_tokens(cells, table, var_hot, lead_hot), inputs, tables
        )
        normed = layer_norm(x_first, norm_gains[0], norm_gains[1]).astype(bf16)
        rows_one = spread_rows(crossed, normed)
        packed = jnp.dot(rows_one, qkv_local, preferred_element_type=f32).astype(bf16)
        own_out, full, logsum = attend(packed)
        attended = exchange(crossed, own_out, True, 2)
        x_mid, rows_two, hidden, active, x_last, guess = branch_forward(
            attended, x_first, norm_gains, gathered, head
        )
        miss = guess - answers[rollout]
        loss_part = loss_part + jnp.sum(weighted * miss * miss)
        records.append(
            (embed_pull, x_first, rows_one, packed, full, logsum, attended, x_mid, rows_two,
             hidden, active, x_last, 2.0 * weighted * miss / denom)
        )
        inputs = guess
    carried = jnp.zeros_like(inputs)
    table_grad = jnp.zeros((5 * V + LEADS + 1, D), f32)
    head_total = jnp.zeros_like(head)
    gain_grad = jnp.zeros_like(norm_gains)
    qkv_grad = jnp.zeros((D, qkv_local.shape[1]), f32)
    kept = []

    def sources(index, other, blocked):
        listed = []
        for step in kept:
            listed += [(step[index], blocked), (step[other], not blocked)]
        return listed

    for rollout in (1, 0):
        (embed_pull, x_first, rows_one, packed, full, logsum, attended, x_mid, rows_two,
         hidden, active, x_last, loss_grad) = records[rollout]
        last_low, hidden_grad, mid_grad, mid_low, out_grad, gain_part, head_grad = branch_backward(
            loss_grad + carried, x_last, x_mid, norm_gains, hidden, gathered, head
        )
        kept.append((attended, rows_two, active, mid_low, hidden_grad, last_low))
        last_turn = crossed and rollout == 0
        if last_turn:
            listed = (
                (sources(2, 5, True), down_pieces, 256),
                (sources(1, 4, False) + sources(0, 3, True), up_out_pieces, 320),
            )
            x, y = lax.rem(place, 2), place // 2
            where = lambda which: jnp.stack((which, x, y)).astype(jnp.int32)
            others = [outer_half(*group, where(1 - core), None) for group in listed]
            out_grad, *others = tie(out_grad, *others)
            others = [shift(other, to_core) for other in others]
        own_grad = exchange(crossed, out_grad, False, 3)
        if last_turn:
            halves = []
            for group, other in zip(listed, others):
                halves += outer_half(*group, where(core), other)
            own_grad, *halves = tie(own_grad, *halves)
            sums = [first_sums(*halves[:2]), first_sums(*halves[2:])]
        packed_grad = attend_back(own_grad, packed, full, logsum)
        if last_turn:
            packed_grad, *sums[0] = tie(packed_grad, *sums[0])
            down_pieces_sum = second_sums(*sums[0], x, y)
        token_grad = exchange(crossed, packed_grad, True, 4)
        if last_turn:
            token_grad, *sums[1] = tie(token_grad, *sums[1])
            up_out_sum = second_sums(*sums[1], x, y)
        qkv_grad = qkv_grad + lax.dot_general(
            rows_one, packed_grad, TN, preferred_element_type=f32
        )
        row_grad, gain_one = entry_backward(token_grad, gathered[3], x_first, mid_grad, norm_gains)
        gain_part = gain_part + jnp.pad(gain_one, ((0, 4), (0, 0)))
        carried, embed_tables = embed_pull(row_grad)
        table_grad = table_grad + embed_tables[: 5 * V + LEADS + 1]
        head_total = head_total + head_grad
        gain_grad = gain_grad + gain_part

    def pair(index):
        return (kept[0][index], kept[1][index])

    if crossed:
        down_share = tall_piece(sum_levels(down_pieces_sum, level))
        up_out = sum_levels(up_out_sum, level)
        up_share = up_out[:256]
        out_share = tall_piece(up_out[256:])
    else:
        down_share = outer_plain(pair(2), pair(5), False)
        up_share = outer_plain(pair(1), pair(4), True)
        out_share = outer_plain(pair(0), pair(3), False)
    shares = (by_head(own_qkv_share(crossed, qkv_grad)), out_share, up_share, down_share)
    share_square = sum(jnp.sum(share * share) for share in shares)
    head_sum = lax.psum(jnp.concatenate((head_total, gain_grad[2:])), ("dp", "mp"))
    last_rows = jnp.concatenate((table_grad, gain_grad[:2]))
    if crossed:
        last_rows = jnp.pad(last_rows, ((0, -last_rows.shape[0] % 256), (0, 0)))
        row = jnp.arange(8, dtype=jnp.int32)[:, None]
        tile = jnp.where(row == 0, share_square, jnp.where(row == 1, loss_part, 0.0))
        last_sum, tile_sum = exchange_sum(last_rows, jnp.broadcast_to(tile, (8, 128)))
        square_sum, loss_sum = tile_sum[0, 0], tile_sum[1, 0]
    else:
        last_sum, loss_sum, square_sum = lax.psum(
            (last_rows, loss_part, share_square), ("dp", "mp")
        )
        square_sum = square_sum + jnp.sum(last_sum * last_sum)
    square_sum = square_sum + jnp.sum(head_sum * head_sum)
    embed_rows = 5 * V + LEADS + 1
    table_sum = jnp.concatenate((last_sum[:embed_rows], head_sum[: 4 * V]))
    gain_sum = jnp.concatenate((last_sum[embed_rows : embed_rows + 2], head_sum[4 * V :]))
    grad_norm = jnp.sqrt(square_sum)
    factor = jnp.minimum(1.0, clip_norm / (grad_norm + 1e-06))
    tab = adam_step(tables, factor * table_sum, tables_first, tables_second, lr_table)
    gai = adam_step(norm_gains, factor * gain_sum, gains_first, gains_second, lr_gain)
    qkv = adam_step(masters[0], factor * shares[0], qkv_first, qkv_second, lr_matrix)
    outp = adam_step(masters[1], factor * shares[1], out_first, out_second, lr_matrix)
    upp = adam_step(masters[2], factor * shares[2], up_first, up_second, lr_matrix)
    down = adam_step(masters[3], factor * shares[3], down_first, down_second, lr_matrix)
    average = average_keep * qkv_average + (1.0 - average_keep) * qkv[0]
    return (
        loss_sum / denom,
        grad_norm,
        tab[0],
        tab[1],
        tab[2],
        gai[0],
        gai[1],
        gai[2],
        qkv[0],
        qkv[1],
        qkv[2],
        outp[0],
        outp[1],
        outp[2],
        upp[0],
        upp[1],
        upp[2],
        down[0],
        down[1],
        down[2],
        average,
    )


def solution(mesh):
    return jax.shard_map(
        partial(shards, is_crossed(mesh.shape)),
        mesh=mesh,
        in_specs=(
            P("dp", "mp", None),
            P("dp", None, "mp", None),
            P("dp", "mp", None),
            P("dp", None),
            P(),
            P(),
            P(),
            P(),
            P(),
            P(),
            P(),
            P(None, "mp"),
            P("dp", "mp"),
            P("dp", "mp"),
            P("mp", None),
            P("mp", "dp"),
            P("mp", "dp"),
            P(None, "mp"),
            P("dp", "mp"),
            P("dp", "mp"),
            P("mp", None),
            P("mp", "dp"),
            P("mp", "dp"),
            P("dp", "mp"),
        ),
        out_specs=(
            P(),
            P(),
            P(),
            P(),
            P(),
            P(),
            P(),
            P(),
            P("dp", "mp"),
            P("dp", "mp"),
            P("dp", "mp"),
            P("mp", "dp"),
            P("mp", "dp"),
            P("mp", "dp"),
            P("dp", "mp"),
            P("dp", "mp"),
            P("dp", "mp"),
            P("mp", "dp"),
            P("mp", "dp"),
            P("mp", "dp"),
            P("dp", "mp"),
        ),
        check_vma=False,
    )
```

```python
from functools import partial
import math

import jax
import jax.numpy as jnp
from jax import lax
from jax.experimental import pallas as pl
from jax.experimental.pallas import tpu as pltpu
from jax.sharding import PartitionSpec as P

D = 1024
HEADS = 16
HEAD_DIM = 64
V = 48
PATCH_ROWS = 32
PATCH_COLS = 64
LEADS = 7


highest = lax.Precision.HIGHEST
eps_norm = 1e-05
clip_norm = 0.05
beta_first = 0.9
beta_second = 0.999
adam_eps = 1e-08
decay_rate = 0.1
lr_matrix = 0.04
lr_table = 0.1
lr_gain = 0.3
average_keep = 0.9
first_fix = 1.0 - 0.9**10
second_fix = 1.0 - 0.999**10


def layer_norm(values, gain, bias):
    center = values - jnp.mean(values, axis=-1, keepdims=True)
    spread = jnp.mean(center * center, axis=-1, keepdims=True)
    return center * lax.rsqrt(spread + eps_norm) * gain + bias


def lat_weights(pixel_rows):
    row_index = jnp.arange(pixel_rows, dtype=jnp.float32)
    cosine = jnp.cos(((row_index + 0.5) / pixel_rows - 0.5) * math.pi)
    return cosine / jnp.mean(cosine)


bf16 = jnp.bfloat16
f32 = jnp.float32
MESH = pl.DeviceIdType.MESH
NT = (((1,), (1,)), ((), ()))
TN = (((0,), (0,)), ((), ()))
VMEM = pl.BlockSpec(memory_space=pltpu.VMEM)
BIG = 56 * 2**20


def is_crossed(sizes):
    return sizes["dp"] == 4 and sizes["mp"] == 8


def mesh_place():
    dp = lax.axis_index("dp")
    mp = lax.axis_index("mp")
    return dp, mp // 2, lax.rem(mp, 2)


def device_of(dp, level, core):
    return {"dp": dp, "mp": level * 2 + core}


def cross_pairs():
    groups = lax.axis_size("dp")
    pairs = []
    for dp in range(groups):
        for level in range(groups):
            for core in range(2):
                source = (dp * groups + level) * 2 + core
                target = (level * groups + dp) * 2 + core
                pairs.append((source, target))
    return pairs


def cross(crossed, value):
    if not crossed:
        return value
    return lax.ppermute(value, ("dp", "mp"), cross_pairs())


def gather_kernel(x_ref, o_ref, send_sem, recv_sem):
    rows = x_ref.shape[0]
    half = rows // 2
    dp, level, core = mesh_place()
    side = dp + 1 - 2 * lax.rem(dp, 2)
    down = lax.rem(dp + 2, 4)
    far = 3 - dp
    to_side = device_of(side, level, core)
    to_down = device_of(down, level, core)
    to_core = device_of(dp, level, 1 - core)

    def rows_of(owner, who, first, size):
        return pl.ds(pl.multiple_of((owner * 2 + who) * rows + first, half), size)

    barrier = pltpu.get_barrier_semaphore()
    for target in (to_side, to_down, to_core):
        pl.semaphore_signal(barrier, inc=1, device_id=target, device_id_type=MESH)
    pl.semaphore_wait(barrier, 3)

    def send(slot, source, where, target):
        copy = pltpu.make_async_remote_copy(
            src_ref=source,
            dst_ref=o_ref.at[where],
            send_sem=send_sem.at[slot],
            recv_sem=recv_sem.at[slot],
            device_id=target,
            device_id_type=MESH,
        )
        copy.start()
        return copy

    first = x_ref.at[pl.ds(0, half)]
    second = x_ref.at[pl.ds(half, half)]
    side_a = send(0, first, rows_of(dp, core, 0, half), to_side)
    down_b = send(1, second, rows_of(dp, core, half, half), to_down)
    side_b = send(2, second, rows_of(dp, core, half, half), to_side)
    down_a = send(3, first, rows_of(dp, core, 0, half), to_down)
    near = send(4, x_ref, rows_of(dp, core, 0, rows), to_core)
    o_ref[rows_of(dp, core, 0, rows)] = x_ref[...]
    side_a.wait_recv()
    place = rows_of(side, core, 0, half)
    far_a = send(5, o_ref.at[place], place, to_down)
    down_b.wait_recv()
    place = rows_of(down, core, half, half)
    far_b = send(6, o_ref.at[place], place, to_side)
    side_b.wait_recv()
    place = rows_of(side, core, 0, rows)
    near_side = send(7, o_ref.at[place], place, to_core)
    down_a.wait_recv()
    place = rows_of(down, core, 0, rows)
    near_down = send(8, o_ref.at[place], place, to_core)
    far_a.wait_recv()
    far_b.wait_recv()
    place = rows_of(far, core, 0, rows)
    near_far = send(9, o_ref.at[place], place, to_core)
    for copy in (near, near_side, near_down, near_far):
        copy.wait_recv()
    for copy in (side_a, down_b, side_b, down_a, near, far_a, far_b, near_side, near_down, near_far):
        copy.wait_send()


def spread_rows(crossed, normed):
    if not crossed:
        return lax.all_gather(normed, "mp", axis=0, tiled=True)
    rows, width = normed.shape
    return pl.pallas_call(
        gather_kernel,
        out_shape=jax.ShapeDtypeStruct((8 * rows, width), normed.dtype),
        in_specs=[VMEM],
        out_specs=VMEM,
        scratch_shapes=[pltpu.SemaphoreType.DMA((10,)), pltpu.SemaphoreType.DMA((10,))],
        compiler_params=pltpu.CompilerParams(
            collective_id=1, has_side_effects=True, vmem_limit_bytes=BIG
        ),
        name="gather_rows",
    )(normed)


def exchange_kernel(to_columns, rows, width, x_ref, o_ref, send_sem, recv_sem):
    dp, level, core = mesh_place()
    me = dp * 2 + core
    barrier = pltpu.get_barrier_semaphore()
    others = []
    for step in (7, 6, 5, 4, 3, 2, 1):
        part = lax.rem(me + step, 8)
        others.append((step, part, device_of(part // 2, level, lax.rem(part, 2))))
    for step, part, target in others:
        pl.semaphore_signal(barrier, inc=1, device_id=target, device_id_type=MESH)
    pl.semaphore_wait(barrier, 7)

    def row_block(ref, part):
        return ref.at[pl.ds(pl.multiple_of(part * rows, rows), rows), :]

    def column_block(ref, part):
        return ref.at[:, pl.ds(pl.multiple_of(part * width, width), width)]

    source_block, target_block = (
        (row_block, column_block) if to_columns else (column_block, row_block)
    )
    copies = []
    for step, part, target in others:
        copy = pltpu.make_async_remote_copy(
            src_ref=source_block(x_ref, part),
            dst_ref=target_block(o_ref, me),
            send_sem=send_sem.at[step],
            recv_sem=recv_sem.at[step],
            device_id=target,
            device_id_type=MESH,
        )
        copy.start()
        copies.append(copy)
    target_block(o_ref, me)[...] = source_block(x_ref, me)[...]
    for copy in copies:
        copy.wait()


def exchange(crossed, value, to_columns, number):
    parts = lax.axis_size("mp")
    if to_columns:
        rows, width = value.shape[0] // parts, value.shape[1]
        shape = (rows, width * parts)
    else:
        rows, width = value.shape[0], value.shape[1] // parts
        shape = (rows * parts, width)
    if not crossed:
        split, joined = (0, 1) if to_columns else (1, 0)
        return lax.all_to_all(value, "mp", split_axis=split, concat_axis=joined, tiled=True)
    return pl.pallas_call(
        partial(exchange_kernel, to_columns, rows, width),
        out_shape=jax.ShapeDtypeStruct(shape, value.dtype),
        in_specs=[VMEM],
        out_specs=VMEM,
        scratch_shapes=[pltpu.SemaphoreType.DMA((8,)), pltpu.SemaphoreType.DMA((8,))],
        compiler_params=pltpu.CompilerParams(
            collective_id=number, has_side_effects=True, vmem_limit_bytes=BIG
        ),
        name="exchange_parts",
    )(value)


def pick_head(value, head, heads):
    if heads == 1:
        return value
    lane = lax.broadcasted_iota(jnp.int32, value.shape, 1) // HEAD_DIM
    return jnp.where(lane == head, value, jnp.zeros_like(value))


def attend_kernel(heads, q_ref, k_ref, v_ref, o_ref, full_ref, lse_ref, vt_ref):
    @pl.when(pl.program_id(0) == 0)
    def _():
        vt_ref[...] = v_ref[...].T

    queries = q_ref[...] * bf16(HEAD_DIM**-0.5)
    keys = k_ref[...]
    outs = []
    for head in range(heads):
        scores = lax.dot_general(
            keys, pick_head(queries, head, heads), NT, preferred_element_type=f32
        )
        largest = jnp.max(scores, axis=0, keepdims=True)
        raised = jnp.exp(scores - largest)
        total = jnp.sum(raised, axis=0, keepdims=True)
        probs = (raised * (1.0 / total)).astype(bf16)
        values = vt_ref[head * HEAD_DIM : (head + 1) * HEAD_DIM, :]
        outs.append(jnp.dot(values, probs, preferred_element_type=f32))
        lse_ref[head : head + 1, :] = largest + jnp.log(total)
    flipped = outs[0] if heads == 1 else jnp.concatenate(outs, axis=0)
    full = flipped.T
    full_ref[...] = full
    o_ref[...] = full.astype(bf16)


def attend(packed):
    total, width = packed.shape[0], packed.shape[1] // 3
    heads = width // HEAD_DIM
    block = min(512, total)
    row_block = pl.BlockSpec((block, width), lambda i: (i, 0))
    return pl.pallas_call(
        partial(attend_kernel, heads),
        grid=(total // block,),
        out_shape=(
            jax.ShapeDtypeStruct((total, width), bf16),
            jax.ShapeDtypeStruct((total, width), f32),
            jax.ShapeDtypeStruct((heads, total), f32),
        ),
        in_specs=[
            row_block,
            pl.BlockSpec((total, width), lambda i: (0, 0)),
            pl.BlockSpec((total, width), lambda i: (0, 0)),
        ],
        out_specs=[row_block, row_block, pl.BlockSpec((heads, block), lambda i: (0, i))],
        scratch_shapes=[pltpu.VMEM((width, total), bf16)],
        compiler_params=pltpu.CompilerParams(vmem_limit_bytes=BIG),
        cost_estimate=pl.CostEstimate(
            flops=16 * total * total * width,
            bytes_accessed=10 * total * width,
            transcendentals=heads * total * total,
        ),
        name="attend",
    )(packed[:, :width], packed[:, width : 2 * width], packed[:, 2 * width :])


def attend_back_kernel(
    heads, q_ref, do_ref, full_ref, lse_ref, k_ref, v_ref, dq_ref, dk_ref, dv_ref, kt_ref, dk_sum, dv_sum
):
    step = pl.program_id(0)
    total = k_ref.shape[0]
    chunk = min(1024, total)

    @pl.when(step == 0)
    def _():
        kt_ref[...] = k_ref[...].T
        dk_sum[...] = jnp.zeros_like(dk_sum)
        dv_sum[...] = jnp.zeros_like(dv_sum)

    scale = HEAD_DIM**-0.5
    queries = q_ref[...]
    grads = do_ref[...]
    products = (grads.astype(f32) * full_ref[...]).T
    query_heads = [pick_head(queries, head, heads) for head in range(heads)]
    grad_heads = [pick_head(grads, head, heads) for head in range(heads)]
    inner = [
        jnp.sum(products[head * HEAD_DIM : (head + 1) * HEAD_DIM], axis=0, keepdims=True) * scale
        for head in range(heads)
    ]
    query_grads = [None] * heads
    for start in range(0, total, chunk):
        rows = slice(start, start + chunk)
        keys = k_ref[rows, :]
        values = v_ref[rows, :]
        value_part = None
        key_part = None
        for head in range(heads):
            scores = lax.dot_general(
                keys, query_heads[head] * bf16(scale), NT, preferred_element_type=f32
            )
            probs = jnp.exp(scores - lse_ref[head : head + 1, :])
            prob_grad = lax.dot_general(
                values, grad_heads[head] * bf16(scale), NT, preferred_element_type=f32
            )
            score_grad = (probs * (prob_grad - inner[head])).astype(bf16)
            one = jnp.dot(probs.astype(bf16), grad_heads[head], preferred_element_type=f32)
            two = jnp.dot(score_grad, query_heads[head], preferred_element_type=f32)
            value_part = one if value_part is None else value_part + one
            key_part = two if key_part is None else key_part + two
            three = jnp.dot(
                kt_ref[head * HEAD_DIM : (head + 1) * HEAD_DIM, rows],
                score_grad,
                preferred_element_type=f32,
            )
            query_grads[head] = three if query_grads[head] is None else query_grads[head] + three
        dv_sum[rows, :] += value_part
        dk_sum[rows, :] += key_part
    flipped = query_grads[0] if heads == 1 else jnp.concatenate(query_grads, axis=0)
    dq_ref[...] = flipped.T.astype(bf16)

    @pl.when(step == pl.num_programs(0) - 1)
    def _():
        dk_ref[...] = dk_sum[...].astype(bf16)
        dv_ref[...] = dv_sum[...].astype(bf16)


def attend_back(grad_out, packed, full, logsum):
    total, width = grad_out.shape
    heads = width // HEAD_DIM
    block = min(256, total)
    row_block = pl.BlockSpec((block, width), lambda i: (i, 0))
    whole = pl.BlockSpec((total, width), lambda i: (0, 0))
    query_grad, key_grad, value_grad = pl.pallas_call(
        partial(attend_back_kernel, heads),
        grid=(total // block,),
        out_shape=(jax.ShapeDtypeStruct((total, width), bf16),) * 3,
        in_specs=[
            row_block,
            row_block,
            row_block,
            pl.BlockSpec((heads, block), lambda i: (0, i)),
            whole,
            whole,
        ],
        out_specs=[row_block, whole, whole],
        scratch_shapes=[
            pltpu.VMEM((width, total), bf16),
            pltpu.VMEM((total, width), f32),
            pltpu.VMEM((total, width), f32),
        ],
        compiler_params=pltpu.CompilerParams(vmem_limit_bytes=BIG),
        cost_estimate=pl.CostEstimate(
            flops=40 * total * total * width,
            bytes_accessed=16 * total * width,
            transcendentals=heads * total * total,
        ),
        name="attend_back",
    )(
        packed[:, :width],
        grad_out,
        full,
        logsum,
        packed[:, width : 2 * width],
        packed[:, 2 * width :],
    )
    return jnp.concatenate((query_grad, key_grad, value_grad), axis=1)


def normed_parts(values):
    center = values - jnp.mean(values, axis=-1, keepdims=True)
    spread = jnp.mean(center * center, axis=-1, keepdims=True)
    inverse = lax.rsqrt(spread + eps_norm)
    return center * inverse, inverse


def norm_grad(unit, inverse, gain, grad):
    scaled = grad * gain
    middle = jnp.mean(scaled, axis=-1, keepdims=True)
    along = jnp.mean(scaled * unit, axis=-1, keepdims=True)
    gain_grad = jnp.sum(grad * unit, axis=0, keepdims=True)
    bias_grad = jnp.sum(grad, axis=0, keepdims=True)
    return inverse * (scaled - middle - unit * along), gain_grad, bias_grad


def gauss_share(values):
    return 0.5 * (1.0 + lax.erf(values * (0.5**0.5)))


def branch_kernel(
    o_ref, x0_ref, gains_ref, out_ref, up_ref, down_ref, head_ref,
    x1_ref, h2_ref, g_ref, act_ref, x2_ref, pred_ref,
):
    step = pl.program_id(0)

    @pl.when(step == 0)
    def _():
        x1_ref[...] = x0_ref[...] + jnp.dot(
            o_ref[...], out_ref[...], preferred_element_type=f32
        )
        unit, _ = normed_parts(x1_ref[...])
        h2_ref[...] = (unit * gains_ref[2:3, :] + gains_ref[3:4, :]).astype(bf16)
        x2_ref[...] = x1_ref[...]

    hidden = jnp.dot(h2_ref[...], up_ref[0], preferred_element_type=f32)
    g_ref[...] = hidden
    active = (hidden * gauss_share(hidden)).astype(bf16)
    act_ref[...] = active
    x2_ref[...] += jnp.dot(active, down_ref[...], preferred_element_type=f32)

    @pl.when(step == pl.num_programs(0) - 1)
    def _():
        unit, _ = normed_parts(x2_ref[...])
        last = unit * gains_ref[4:5, :] + gains_ref[5:6, :]
        pred_ref[...] = lax.dot_general(
            last, head_ref[...], NT, precision=highest, preferred_element_type=f32
        )


def weight_specs(w_out, w_up, w_down):
    _, width, units = w_up.shape
    return (
        pl.BlockSpec(w_out.shape, lambda i: (0, 0)),
        pl.BlockSpec((1, width, units), lambda i: (i, 0, 0)),
        pl.BlockSpec((units, width), lambda i: (i, 0)),
    )


def branch_forward(attended, x_first, norm_gains, gathered, head):
    w_out, w_up, w_down, _ = gathered
    rows, width = x_first.shape
    parts, units = w_up.shape[0], w_up.shape[2]
    fixed = lambda shape: pl.BlockSpec(shape, lambda i: (0, 0))
    by_units = pl.BlockSpec((rows, units), lambda i: (0, i))
    columns = head.shape[0]
    flops = 2 * rows * (width * width + 2 * width * parts * units + 6 * width * columns)
    return pl.pallas_call(
        branch_kernel,
        grid=(parts,),
        out_shape=(
            jax.ShapeDtypeStruct((rows, width), f32),
            jax.ShapeDtypeStruct((rows, width), bf16),
            jax.ShapeDtypeStruct((rows, parts * units), f32),
            jax.ShapeDtypeStruct((rows, parts * units), bf16),
            jax.ShapeDtypeStruct((rows, width), f32),
            jax.ShapeDtypeStruct((rows, columns), f32),
        ),
        in_specs=[
            fixed((rows, width)),
            fixed((rows, width)),
            fixed(norm_gains.shape),
            *weight_specs(w_out, w_up, w_down),
            fixed(head.shape),
        ],
        out_specs=[
            fixed((rows, width)),
            fixed((rows, width)),
            by_units,
            by_units,
            fixed((rows, width)),
            fixed((rows, columns)),
        ],
        compiler_params=pltpu.CompilerParams(vmem_limit_bytes=BIG),
        cost_estimate=pl.CostEstimate(
            flops=flops,
            bytes_accessed=4 * width * parts * units + 6 * rows * parts * units,
            transcendentals=rows * parts * units,
        ),
        name="branch_forward",
    )(attended, x_first, norm_gains, w_out, w_up, w_down, head)


def branch_back_kernel(
    dpred_ref, x2_ref, x1_ref, gains_ref, g_ref, out_ref, up_ref, down_ref, head_ref,
    dx2_ref, dg_ref, dx1_ref, low_ref, do_ref, gain_ref, dhead_ref,
    wide_ref, sum_ref,
):
    step = pl.program_id(0)

    @pl.when(step == 0)
    def _():
        grad = dpred_ref[...]
        unit, inverse = normed_parts(x2_ref[...])
        gain = gains_ref[4:5, :]
        last = unit * gain + gains_ref[5:6, :]
        dhead_ref[...] = lax.dot_general(
            grad, last, TN, precision=highest, preferred_element_type=f32
        )
        row_grad = jnp.dot(grad, head_ref[...], precision=highest, preferred_element_type=f32)
        wide, gain_grad, bias_grad = norm_grad(unit, inverse, gain, row_grad)
        gain_ref[...] = jnp.zeros_like(gain_ref)
        gain_ref[4:5, :] = gain_grad
        gain_ref[5:6, :] = bias_grad
        wide_ref[...] = wide
        dx2_ref[...] = wide.astype(bf16)
        sum_ref[...] = jnp.zeros_like(sum_ref)

    active_grad = lax.dot_general(dx2_ref[...], down_ref[...], NT, preferred_element_type=f32)
    hidden = g_ref[...]
    slope = gauss_share(hidden) + hidden * (
        jnp.exp(-0.5 * hidden * hidden) * (2.0 * math.pi) ** -0.5
    )
    hidden_grad = (active_grad * slope).astype(bf16)
    dg_ref[...] = hidden_grad
    sum_ref[...] += lax.dot_general(hidden_grad, up_ref[0], NT, preferred_element_type=f32)

    @pl.when(step == pl.num_programs(0) - 1)
    def _():
        unit, inverse = normed_parts(x1_ref[...])
        middle, gain_grad, bias_grad = norm_grad(unit, inverse, gains_ref[2:3, :], sum_ref[...])
        gain_ref[2:3, :] = gain_grad
        gain_ref[3:4, :] = bias_grad
        middle = wide_ref[...] + middle
        dx1_ref[...] = middle
        low_ref[...] = middle.astype(bf16)
        total = lax.dot_general(low_ref[...], out_ref[...], NT, preferred_element_type=f32)
        do_ref[...] = total.astype(bf16)


def branch_backward(pred_grad, x_last, x_mid, norm_gains, hidden, gathered, head):
    w_out, w_up, w_down, _ = gathered
    rows, width = x_last.shape
    parts, units = w_up.shape[0], w_up.shape[2]
    fixed = lambda shape: pl.BlockSpec(shape, lambda i: (0, 0))
    by_units = pl.BlockSpec((rows, units), lambda i: (0, i))
    columns = head.shape[0]
    wide = (rows, width)
    flops = 2 * rows * (width * width + 2 * width * parts * units + 12 * width * columns)
    return pl.pallas_call(
        branch_back_kernel,
        grid=(parts,),
        out_shape=(
            jax.ShapeDtypeStruct(wide, bf16),
            jax.ShapeDtypeStruct((rows, parts * units), bf16),
            jax.ShapeDtypeStruct(wide, f32),
            jax.ShapeDtypeStruct(wide, bf16),
            jax.ShapeDtypeStruct(wide, bf16),
            jax.ShapeDtypeStruct((6, width), f32),
            jax.ShapeDtypeStruct((columns, width), f32),
        ),
        in_specs=[
            fixed((rows, columns)),
            fixed(wide),
            fixed(wide),
            fixed(norm_gains.shape),
            by_units,
            *weight_specs(w_out, w_up, w_down),
            fixed(head.shape),
        ],
        out_specs=[
            fixed(wide),
            by_units,
            fixed(wide),
            fixed(wide),
            fixed(wide),
            fixed((6, width)),
            fixed((columns, width)),
        ],
        scratch_shapes=[pltpu.VMEM(wide, f32), pltpu.VMEM(wide, f32)],
        compiler_params=pltpu.CompilerParams(vmem_limit_bytes=BIG),
        cost_estimate=pl.CostEstimate(
            flops=flops,
            bytes_accessed=4 * width * parts * units + 6 * rows * parts * units,
            transcendentals=2 * rows * parts * units,
        ),
        name="branch_backward",
    )(pred_grad, x_last, x_mid, norm_gains, hidden, w_out, w_up, w_down, head)


def wide_piece(piece):
    half = piece.shape[0] // 2
    return jnp.concatenate((piece[:half], piece[half:]), axis=1)


def tall_piece(piece):
    half = piece.shape[1] // 2
    return jnp.concatenate((piece[:, :half], piece[:, half:]), axis=0)


def both_steps(left_a, right_a, left_b, right_b):
    product = lax.dot_general(left_a[...], right_a[...], TN, preferred_element_type=f32)
    return product + lax.dot_general(left_b[...], right_b[...], TN, preferred_element_type=f32)


def down_pieces(refs):
    product = both_steps(*refs)
    share = product.shape[1] // 4
    return [wide_piece(product[:, i * share : (i + 1) * share]) for i in range(4)]


def up_out_pieces(refs):
    up = both_steps(*refs[:4])
    share = up.shape[0] // 4
    out = both_steps(*refs[4:])
    size = out.shape[1] // 4
    return [
        jnp.concatenate(
            (up[i * share : (i + 1) * share], wide_piece(out[:, i * size : (i + 1) * size])), axis=0
        )
        for i in range(4)
    ]


def outer_other_kernel(make, count, where_ref, *refs):
    o_ref = refs[count]
    for split, piece in enumerate(make(refs[:count])):
        o_ref[0, split] = piece.astype(bf16)


def outer_own_kernel(make, count, where_ref, *refs):
    other_ref, send_ref, keep_ref, held_ref = refs[count:]
    for split, piece in enumerate(make(refs[:count])):
        held_ref[split] = (piece + other_ref[0, split].astype(f32)).astype(bf16)
    x, y = where_ref[1], where_ref[2]
    early = pl.program_id(0) < 2
    for which in range(2):
        send_ref[0, which] = held_ref[jnp.where(early, which * 2 + 1 - x, (1 - y) * 2 + which)]
        keep_ref[0, which] = held_ref[jnp.where(early, which * 2 + x, y * 2 + which)]


def outer_half(operands, make, height, where, other):
    specs = []
    for value, blocked in operands:
        rows, size = value.shape
        if blocked:
            specs.append(pl.BlockSpec((rows, size // 8), lambda i, w: (0, i * 2 + w[0])))
        else:
            specs.append(pl.BlockSpec((rows, size), lambda i, w: (0, 0)))
    values = [value for value, _ in operands]
    count = len(values)
    whole = pl.BlockSpec((1, 4, height, 512), lambda i, w: (i, 0, 0, 0))
    half = pl.BlockSpec((1, 2, height, 512), lambda i, w: (i, 0, 0, 0))
    rows = values[0].shape[0]
    cost = pl.CostEstimate(
        flops=2 * 2 * rows * 16 * height * 512, bytes_accessed=3 * 16 * height * 512, transcendentals=0
    )
    params = pltpu.CompilerParams(vmem_limit_bytes=BIG)
    if other is None:
        return pl.pallas_call(
            partial(outer_other_kernel, make, count),
            out_shape=jax.ShapeDtypeStruct((4, 4, height, 512), bf16),
            grid_spec=pltpu.PrefetchScalarGridSpec(
                num_scalar_prefetch=1, grid=(4,), in_specs=specs, out_specs=whole
            ),
            compiler_params=params,
            cost_estimate=cost,
            name="outer_other",
        )(where, *values)
    return pl.pallas_call(
        partial(outer_own_kernel, make, count),
        out_shape=(jax.ShapeDtypeStruct((4, 2, height, 512), bf16),) * 2,
        grid_spec=pltpu.PrefetchScalarGridSpec(
            num_scalar_prefetch=1,
            grid=(4,),
            in_specs=specs + [whole],
            out_specs=[half, half],
            scratch_shapes=[pltpu.VMEM((4, height, 512), bf16)],
        ),
        compiler_params=params,
        cost_estimate=cost,
        name="outer_own",
    )(where, *values, other)


def device_pairs(move):
    pairs = []
    for dp in range(4):
        for level in range(4):
            for core in range(2):
                to_dp, to_level, to_core = move(dp, level, core)
                pairs.append(((dp * 4 + level) * 2 + core, (to_dp * 4 + to_level) * 2 + to_core))
    return pairs


def shift(value, move):
    return lax.ppermute(value, ("dp", "mp"), device_pairs(move))


def to_core(dp, level, core):
    return dp, level, 1 - core


def to_side(dp, level, core):
    return dp ^ 1, level, core


def to_down(dp, level, core):
    return dp ^ 2, level, core


def choose(value, index, axis=0):
    return lax.dynamic_index_in_dim(value, index, axis, keepdims=False)


def sum_levels(pieces, level):
    total = choose(pieces, level).astype(f32)
    for step in range(1, 4):
        piece = choose(pieces, lax.rem(level + step, 4)).astype(bf16)
        moved = shift(piece, lambda dp, z, core: (dp, (z + step) % 4, core))
        total = total + moved.astype(f32)
    return total


def tie(*values):
    return lax.optimization_barrier(values)


def first_sums(send, keep):
    first = keep[:2].astype(f32) + shift(send[:2], to_side).astype(f32)
    second = keep[2:].astype(f32) + shift(send[2:], to_down).astype(f32)
    return first.astype(bf16), second.astype(bf16)


def second_sums(first, second, x, y):
    first_moved = shift(choose(first, 1 - y, 1), to_down)
    second_moved = shift(choose(second, 1 - x, 1), to_side)
    first = choose(first, y, 1).astype(f32) + first_moved.astype(f32)
    second = choose(second, x, 1).astype(f32) + second_moved.astype(f32)
    return jnp.concatenate((first, second))


def outer_plain(lefts, rights, by_rows):
    dp, mp = lax.axis_size("dp"), lax.axis_size("mp")
    grads = sum(
        lax.dot_general(left, right, TN, preferred_element_type=f32)
        for left, right in zip(lefts, rights)
    ).astype(bf16)
    rows, width = grads.shape
    if by_rows:
        grads = grads.reshape(dp, rows // dp, mp, width // mp).transpose(0, 2, 1, 3)
    else:
        grads = grads.reshape(mp, rows // mp, dp, width // dp).transpose(2, 0, 1, 3)
    grads = grads.reshape((dp * mp,) + grads.shape[2:])
    return lax.psum_scatter(grads, ("dp", "mp"), scatter_dimension=0, tiled=False).astype(f32)


def exchange_sum_kernel(
    x_ref, t_ref, o_ref, s_ref, work_ref, pair_ref, quad_ref, eight_ref, deep_ref, tile_ref,
    send_sem, recv_sem,
):
    dp, level, core = mesh_place()
    x, y = lax.rem(dp, 2), dp // 2
    side = device_of(dp + 1 - 2 * x, level, core)
    down = device_of(lax.rem(dp + 2, 4), level, core)
    near = device_of(dp, level, 1 - core)
    deep = [device_of(dp, lax.rem(level + step, 4), core) for step in (1, 2, 3)]
    barrier = pltpu.get_barrier_semaphore()
    for target in (side, down, near, *deep):
        pl.semaphore_signal(barrier, inc=1, device_id=target, device_id_type=MESH)
    pl.semaphore_wait(barrier, 6)
    started = []

    def send(source, target_ref, target):
        slot = len(started)
        copy = pltpu.make_async_remote_copy(
            src_ref=source,
            dst_ref=target_ref,
            send_sem=send_sem.at[slot],
            recv_sem=recv_sem.at[slot],
            device_id=target,
            device_id_type=MESH,
        )
        copy.start()
        started.append(copy)
        return copy

    half = x_ref.shape[0] // 2
    quarter, eighth, part, unit = half // 2, half // 4, half // 8, half // 16

    def rows(start, size):
        return pl.ds(pl.multiple_of(start, unit), size)

    copy = send(x_ref.at[rows((1 - core) * half, half)], pair_ref, near)
    copy.wait_recv()
    work_ref[...] = x_ref[rows(core * half, half)] + pair_ref[...]
    one = send(work_ref.at[rows((1 - x) * eighth, eighth)], quad_ref.at[0], side)
    two = send(work_ref.at[rows(quarter + (1 - y) * eighth, eighth)], quad_ref.at[1], down)
    base_a = x * eighth
    base_b = quarter + y * eighth
    wide_a, wide_b = core * half + base_a, core * half + base_b
    one.wait_recv()
    work_ref[rows(base_a, eighth)] += quad_ref[0]
    one = send(work_ref.at[rows(base_a + (1 - y) * part, part)], eight_ref.at[0], down)
    two.wait_recv()
    work_ref[rows(base_b, eighth)] += quad_ref[1]
    two = send(work_ref.at[rows(base_b + (1 - x) * part, part)], eight_ref.at[1], side)
    base_a = base_a + y * part
    base_b = base_b + x * part
    one.wait_recv()
    work_ref[rows(base_a, part)] += eight_ref[0]
    two.wait_recv()
    work_ref[rows(base_b, part)] += eight_ref[1]

    def level_start(which):
        late = which // 2
        return (1 - late) * base_a + late * base_b + lax.rem(which, 2) * unit

    copies = []
    for step in (1, 2, 3):
        source = work_ref.at[rows(level_start(lax.rem(level + step, 4)), unit)]
        copies.append(send(source, deep_ref.at[step - 1], deep[step - 1]))
    for copy in copies:
        copy.wait_recv()
    total = work_ref[rows(level_start(level), unit)] + deep_ref[0] + deep_ref[1] + deep_ref[2]
    mine = rows(core * half + level_start(level), unit)
    base_a = core * half + base_a
    base_b = core * half + base_b
    o_ref[mine] = total
    row = lax.broadcasted_iota(jnp.int32, t_ref.shape, 0)
    tile_ref[0] = t_ref[...] + jnp.where(row == 0, jnp.sum(total * total), 0.0)
    copies = []
    for step in (1, 2, 3):
        copies.append(send(o_ref.at[mine], o_ref.at[mine], deep[step - 1]))
        copies.append(send(tile_ref.at[0], tile_ref.at[step], deep[step - 1]))
    for copy in copies:
        copy.wait_recv()
    one = send(o_ref.at[rows(base_a, part)], o_ref.at[rows(base_a, part)], down)
    two = send(o_ref.at[rows(base_b, part)], o_ref.at[rows(base_b, part)], side)
    tile_ref[4] = tile_ref[0] + tile_ref[1] + tile_ref[2] + tile_ref[3]
    three = send(tile_ref.at[4], tile_ref.at[5], side)
    one.wait_recv()
    one = send(o_ref.at[rows(wide_a, eighth)], o_ref.at[rows(wide_a, eighth)], side)
    two.wait_recv()
    two = send(o_ref.at[rows(wide_b, eighth)], o_ref.at[rows(wide_b, eighth)], down)
    three.wait_recv()
    tile_ref[6] = tile_ref[4] + tile_ref[5]
    three = send(tile_ref.at[6], tile_ref.at[7], down)
    one.wait_recv()
    two.wait_recv()
    one = send(o_ref.at[rows(core * half, half)], o_ref.at[rows(core * half, half)], near)
    three.wait_recv()
    tile_ref[8] = tile_ref[6] + tile_ref[7]
    three = send(tile_ref.at[8], tile_ref.at[9], near)
    one.wait_recv()
    three.wait_recv()
    s_ref[...] = tile_ref[8] + tile_ref[9]
    for copy in started:
        copy.wait_send()


def exchange_sum(value, tile):
    rows, width = value.shape
    return pl.pallas_call(
        exchange_sum_kernel,
        out_shape=(jax.ShapeDtypeStruct(value.shape, f32), jax.ShapeDtypeStruct(tile.shape, f32)),
        in_specs=[VMEM, VMEM],
        out_specs=[VMEM, VMEM],
        scratch_shapes=[
            pltpu.VMEM((rows // 2, width), f32),
            pltpu.VMEM((rows // 2, width), f32),
            pltpu.VMEM((2, rows // 8, width), f32),
            pltpu.VMEM((2, rows // 16, width), f32),
            pltpu.VMEM((3, rows // 32, width), f32),
            pltpu.VMEM((10,) + tile.shape, f32),
            pltpu.SemaphoreType.DMA((24,)),
            pltpu.SemaphoreType.DMA((24,)),
        ],
        compiler_params=pltpu.CompilerParams(
            collective_id=5, has_side_effects=True, vmem_limit_bytes=BIG
        ),
        name="exchange_sum",
    )(value, tile)


def tile_sum_kernel(t_ref, s_ref, tile_ref, send_sem, recv_sem):
    dp, level, core = mesh_place()
    x = lax.rem(dp, 2)
    side = device_of(dp + 1 - 2 * x, level, core)
    down = device_of(lax.rem(dp + 2, 4), level, core)
    near = device_of(dp, level, 1 - core)
    deep = [device_of(dp, lax.rem(level + step, 4), core) for step in (1, 2, 3)]
    barrier = pltpu.get_barrier_semaphore()
    for target in (side, down, near, *deep):
        pl.semaphore_signal(barrier, inc=1, device_id=target, device_id_type=MESH)
    pl.semaphore_wait(barrier, 6)

    def send(slot, source, target_ref, target):
        copy = pltpu.make_async_remote_copy(
            src_ref=source,
            dst_ref=target_ref,
            send_sem=send_sem.at[slot],
            recv_sem=recv_sem.at[slot],
            device_id=target,
            device_id_type=MESH,
        )
        copy.start()
        return copy

    copies = [send(step, t_ref, tile_ref.at[step], deep[step]) for step in range(3)]
    for copy in copies:
        copy.wait()
    tile_ref[3] = t_ref[...] + tile_ref[0] + tile_ref[1] + tile_ref[2]
    send(3, tile_ref.at[3], tile_ref.at[4], side).wait()
    tile_ref[5] = tile_ref[3] + tile_ref[4]
    send(4, tile_ref.at[5], tile_ref.at[6], down).wait()
    tile_ref[7] = tile_ref[5] + tile_ref[6]
    send(5, tile_ref.at[7], tile_ref.at[8], near).wait()
    s_ref[...] = tile_ref[7] + tile_ref[8]


def sum_everywhere(crossed, value):
    if not crossed:
        return lax.psum(value, ("dp", "mp"))
    tile = jnp.broadcast_to(value, (8, 128))
    total = pl.pallas_call(
        tile_sum_kernel,
        out_shape=jax.ShapeDtypeStruct(tile.shape, f32),
        in_specs=[VMEM],
        out_specs=VMEM,
        scratch_shapes=[
            pltpu.VMEM((9,) + tile.shape, f32),
            pltpu.SemaphoreType.DMA((6,)),
            pltpu.SemaphoreType.DMA((6,)),
        ],
        compiler_params=pltpu.CompilerParams(collective_id=6, has_side_effects=True),
        name="tile_sum",
    )(tile)
    return total[0, 0]


def split_low(values):
    high = values.astype(bf16)
    return high, (values - high.astype(f32)).astype(bf16)


def three_products(left, right, dims=(((1,), (0,)), ((), ()))):
    def product(one, two):
        return lax.dot_general(one, two, dims, preferred_element_type=f32)

    return product(left[0], right[0]) + (product(left[1], right[0]) + product(left[0], right[1]))


def exact_product(left, right, dims=(((1,), (0,)), ((), ()))):
    return lax.dot_general(left, right, dims, precision=highest, preferred_element_type=f32)


def head_marks(width):
    head = lax.broadcasted_iota(jnp.int32, (HEADS, width), 0)
    column = lax.broadcasted_iota(jnp.int32, (HEADS, width), 1)
    return jnp.where(column // HEAD_DIM == head, 1.0, 0.0).astype(f32)


def quarter_marks(padded):
    row = lax.broadcasted_iota(jnp.int32, (padded, V), 0)
    column = lax.broadcasted_iota(jnp.int32, (padded, V), 1)
    return jnp.where(row // 4 == column, 0.25, 0.0).astype(f32)


def tables_kernel(tables_ref, hot_ref, patch_ref, var_ref, keyed_ref, bias_ref):
    padded, width = patch_ref.shape
    query = tables_ref[5 * V + LEADS : 5 * V + LEADS + 1, :]
    patch_ref[...] = jnp.zeros_like(patch_ref)
    patch_ref[: 4 * V, :] = tables_ref[: 4 * V, :]
    chosen = exact_product(hot_ref[...], tables_ref[4 * V : 5 * V, :])
    var_ref[...] = exact_product(quarter_marks(padded), chosen)
    marks = head_marks(width)
    scale = HEAD_DIM**-0.5
    keyed_ref[...] = exact_product(marks, patch_ref[...] * query, NT) * scale
    bias = exact_product(marks, var_ref[...] * query, NT) * (4.0 * scale)
    column = lax.broadcasted_iota(jnp.int32, bias.shape, 1)
    bias_ref[...] = jnp.where(column < 4 * V, bias, -1e30)


def prepare_tables(tables, var_hot):
    padded = 256
    return pl.pallas_call(
        tables_kernel,
        out_shape=(
            jax.ShapeDtypeStruct((padded, D), f32),
            jax.ShapeDtypeStruct((padded, D), f32),
            jax.ShapeDtypeStruct((HEADS, padded), f32),
            jax.ShapeDtypeStruct((HEADS, padded), f32),
        ),
        compiler_params=pltpu.CompilerParams(vmem_limit_bytes=BIG),
        name="prepare_tables",
    )(tables, var_hot)


def four_sum(values):
    size = values.shape[1]
    lane = lax.broadcasted_iota(jnp.int32, values.shape, 1)
    values = values + jnp.where(
        lane % 2 == 0, pltpu.roll(values, size - 1, 1), pltpu.roll(values, 1, 1)
    )
    return values + jnp.where(
        lane % 4 < 2, pltpu.roll(values, size - 2, 1), pltpu.roll(values, 2, 1)
    )


def cell_shares(cells, keyed, bias):
    scores = four_sum(cells * keyed) + bias
    raised = jnp.exp(scores - jnp.max(scores, axis=1, keepdims=True))
    total = jnp.sum(raised, axis=1, keepdims=True) * 0.25
    return raised * (1.0 / total)


def embed_pair(pair, cells, keyed_ref, bias_ref, patch_ref, var_ref, x0_ref):
    patch = split_low(patch_ref[...])
    variable = split_low(var_ref[...])
    outs = []
    for which in range(2):
        row = pl.ds(pair * 2 + which, 1)
        shares = cell_shares(cells, keyed_ref[row, :], bias_ref[row, :])
        outs.append(
            three_products(split_low(shares * cells), patch)
            + three_products(split_low(shares), variable)
        )
    lane = lax.broadcasted_iota(jnp.int32, outs[0].shape, 1)
    columns = pl.ds(pl.multiple_of(pair * 2 * HEAD_DIM, 2 * HEAD_DIM), 2 * HEAD_DIM)
    x0_ref[:, columns] = jnp.where(lane < HEAD_DIM, outs[0], outs[1])


def embed_kernel(
    u_ref, keyed_ref, bias_ref, patch_ref, var_ref, lead_ref, gains_ref, x0_ref, h1_ref
):
    pair = pl.program_id(0)
    embed_pair(pair, u_ref[...], keyed_ref, bias_ref, patch_ref, var_ref, x0_ref)

    @pl.when(pair == pl.num_programs(0) - 1)
    def _():
        x0_ref[...] += lead_ref[...]
        unit, _ = normed_parts(x0_ref[...])
        h1_ref[...] = (unit * gains_ref[0:1, :] + gains_ref[1:2, :]).astype(bf16)


def embed_forward(cells, prepared, lead_row, norm_gains):
    patch, variable, keyed, bias = prepared
    rows, padded = cells.shape
    fixed = lambda shape: pl.BlockSpec(shape, lambda i: (0, 0))
    by_pair = pl.BlockSpec((padded, 2 * HEAD_DIM), lambda i: (0, i))
    return pl.pallas_call(
        embed_kernel,
        grid=(HEADS // 2,),
        out_shape=(
            jax.ShapeDtypeStruct((rows, D), f32),
            jax.ShapeDtypeStruct((rows, D), bf16),
        ),
        in_specs=[
            fixed((rows, padded)),
            fixed(keyed.shape),
            fixed(bias.shape),
            by_pair,
            by_pair,
            fixed((1, D)),
            fixed(norm_gains.shape),
        ],
        out_specs=[fixed((rows, D)), fixed((rows, D))],
        compiler_params=pltpu.CompilerParams(vmem_limit_bytes=BIG),
        cost_estimate=pl.CostEstimate(
            flops=24 * rows * padded * D, bytes_accessed=14 * rows * D, transcendentals=16 * rows * padded
        ),
        name="embed_forward",
    )(cells, keyed, bias, patch, variable, lead_row, norm_gains)


def entry_back_kernel(
    grad_ref, qkv_ref, x0_ref, mid_ref, gains_ref, u_ref, keyed_ref, bias_ref, patch_ref, var_ref,
    du_ref, gain_ref, lead_ref, dpatch_ref, dvar_ref, dkeyed_ref, dbias_ref,
    dx_ref, flip_ref,
):
    pair = pl.program_id(0)

    @pl.when(pair == 0)
    def _():
        row_grad = jnp.dot(grad_ref[...], qkv_ref[...], preferred_element_type=f32)
        unit, inverse = normed_parts(x0_ref[...])
        part, gain_grad, bias_grad = norm_grad(unit, inverse, gains_ref[0:1, :], row_grad)
        total = mid_ref[...] + part
        dx_ref[...] = total
        flip_ref[...] = total.T
        lead_ref[...] = jnp.sum(total, axis=0, keepdims=True)
        gain_ref[0:1, :] = gain_grad
        gain_ref[1:2, :] = bias_grad
        du_ref[...] = jnp.zeros_like(du_ref)

    cells = u_ref[...]
    size = 2 * HEAD_DIM
    columns = pl.ds(pl.multiple_of(pair * size, size), size)
    grads = dx_ref[:, columns]
    lane = lax.broadcasted_iota(jnp.int32, grads.shape, 1)
    patch = split_low(patch_ref[...])
    variable = split_low(var_ref[...])
    cells_grad = None
    for which in range(2):
        row = pl.ds(pair * 2 + which, 1)
        keyed = keyed_ref[row, :]
        shares = cell_shares(cells, keyed, bias_ref[row, :])
        one = split_low(jnp.where(lane // HEAD_DIM == which, grads, 0.0))
        mixed_grad = three_products(one, patch, NT)
        share_grad = mixed_grad * cells + three_products(one, variable, NT)
        weighted = shares * share_grad
        inner = jnp.sum(weighted, axis=1, keepdims=True)
        score_grad = four_sum(weighted) - shares * inner
        piece = mixed_grad * shares + score_grad * keyed
        cells_grad = piece if cells_grad is None else cells_grad + piece
        scale = HEAD_DIM**-0.5
        dkeyed_ref[row, :] = jnp.sum(score_grad * cells, axis=0, keepdims=True) * scale
        dbias_ref[row, :] = jnp.sum(score_grad, axis=0, keepdims=True) * scale
        rows = pl.ds(pl.multiple_of(pair * size + which * HEAD_DIM, HEAD_DIM), HEAD_DIM)
        flipped = split_low(flip_ref[rows, :])
        mine = slice(which * HEAD_DIM, (which + 1) * HEAD_DIM)
        dpatch_ref[mine, :] = three_products(flipped, split_low(shares * cells))
        dvar_ref[mine, :] = three_products(flipped, split_low(shares))
    du_ref[...] += cells_grad


def entry_backward(token_grad, qkv_t, x_first, mid_grad, norm_gains, cells, prepared):
    patch, variable, keyed, bias = prepared
    rows, width = x_first.shape
    padded = cells.shape[1]
    fixed = lambda shape: pl.BlockSpec(shape, lambda i: (0, 0))
    by_pair = pl.BlockSpec((padded, 2 * HEAD_DIM), lambda i: (0, i))
    flipped = pl.BlockSpec((2 * HEAD_DIM, padded), lambda i: (i, 0))
    return pl.pallas_call(
        entry_back_kernel,
        grid=(HEADS // 2,),
        out_shape=(
            jax.ShapeDtypeStruct((rows, padded), f32),
            jax.ShapeDtypeStruct((2, width), f32),
            jax.ShapeDtypeStruct((1, width), f32),
            jax.ShapeDtypeStruct((width, padded), f32),
            jax.ShapeDtypeStruct((width, padded), f32),
            jax.ShapeDtypeStruct(keyed.shape, f32),
            jax.ShapeDtypeStruct(bias.shape, f32),
        ),
        in_specs=[
            fixed(token_grad.shape),
            fixed(qkv_t.shape),
            fixed((rows, width)),
            fixed((rows, width)),
            fixed(norm_gains.shape),
            fixed(cells.shape),
            fixed(keyed.shape),
            fixed(bias.shape),
            by_pair,
            by_pair,
        ],
        out_specs=[
            fixed((rows, padded)),
            fixed((2, width)),
            fixed((1, width)),
            flipped,
            flipped,
            fixed(keyed.shape),
            fixed(bias.shape),
        ],
        scratch_shapes=[pltpu.VMEM((rows, width), f32), pltpu.VMEM((width, rows), f32)],
        compiler_params=pltpu.CompilerParams(vmem_limit_bytes=BIG),
        cost_estimate=pl.CostEstimate(
            flops=60 * rows * padded * D, bytes_accessed=40 * rows * D, transcendentals=16 * rows * padded
        ),
        name="entry_backward",
    )(token_grad, qkv_t, x_first, mid_grad, norm_gains, cells, keyed, bias, patch, variable)


def table_grads_kernel(
    pa_ref, pb_ref, va_ref, vb_ref, ka_ref, kb_ref, ba_ref, bb_ref,
    patch_ref, var_ref, query_ref, hot_ref, lead_hot_ref, lead_ref, gain_ref, head_ref, high_ref, o_ref,
):
    padded, width = patch_ref.shape
    marks = head_marks(width)
    query = query_ref[...]
    keyed_grad = exact_product(ka_ref[...] + kb_ref[...], marks, TN)
    bias_grad = exact_product(ba_ref[...] + bb_ref[...], marks, TN)
    o_ref[...] = jnp.zeros_like(o_ref)
    patch_grad = (pa_ref[...] + pb_ref[...]).T + keyed_grad * query
    o_ref[: 4 * V, :] = patch_grad[: 4 * V, :]
    var_grad = (va_ref[...] + vb_ref[...]).T + bias_grad * query
    var_rows = exact_product(quarter_marks(padded), var_grad, TN)
    o_ref[4 * V : 5 * V, :] = exact_product(hot_ref[...], var_rows, TN)
    lead_rows = exact_product(lead_hot_ref[...], lead_ref[...], TN)
    o_ref[5 * V : 5 * V + LEADS, :] = lead_rows[:LEADS, :]
    query_grad = jnp.sum(
        keyed_grad * patch_ref[...] + bias_grad * var_ref[...], axis=0, keepdims=True
    )
    o_ref[5 * V + LEADS : 5 * V + LEADS + 1, :] = query_grad
    o_ref[5 * V + LEADS + 1 : 5 * V + LEADS + 3, :] = gain_ref[...]
    o_ref[padded : padded + 4 * V, :] = head_ref[...]
    o_ref[padded + 4 * V : padded + 4 * V + 4, :] = high_ref[...]


def table_grads(first, second, prepared, query, var_hot, lead_hots, leads, gain_rows, head, high):
    patch, variable, _, _ = prepared
    operands = []
    for one, two in zip(first, second):
        operands += [one, two]
    return pl.pallas_call(
        table_grads_kernel,
        out_shape=jax.ShapeDtypeStruct((2 * patch.shape[0], D), f32),
        compiler_params=pltpu.CompilerParams(vmem_limit_bytes=BIG),
        name="table_grads",
    )(*operands, patch, variable, query, var_hot, lead_hots, leads, gain_rows, head, high)


def adam_step(master, grad, first, second, rate):
    first_new = beta_first * first + (1.0 - beta_first) * grad
    second_new = beta_second * second + (1.0 - beta_second) * grad * grad
    update = first_new / first_fix / (jnp.sqrt(second_new / second_fix) + adam_eps)
    return (master - rate * (update + decay_rate * master), first_new, second_new)


def by_kind(shard):
    rows = shard.shape[0]
    return shard.reshape(rows, -1, 3, HEAD_DIM).transpose(0, 2, 1, 3).reshape(rows, -1)


def by_head(shard):
    rows = shard.shape[0]
    return shard.reshape(rows, 3, -1, HEAD_DIM).transpose(0, 2, 1, 3).reshape(rows, -1)


def start_kernel(halves, *refs):
    count = len(halves)
    packed_ref, qkv_ref, targets_ref, keyed_ref, bias_ref, patch_ref, var_ref, lead_ref, gains_ref = refs[:9]
    shards = refs[9 : 9 + count]
    x0_ref, h1_ref, cells_ref, qkv_out, targets_out = refs[9 + count : 14 + count]
    outs = refs[14 + count : 14 + 2 * count]
    held_ref, send_sem, recv_sem, own_sem = refs[14 + 2 * count :]
    step = pl.program_id(0)
    dp, level, core = mesh_place()
    x = lax.rem(dp, 2)
    columns = {"here": dp, "side": dp + 1 - 2 * x, "down": lax.rem(dp + 2, 4), "far": 3 - dp}
    side = device_of(columns["side"], level, core)
    down = device_of(columns["down"], level, core)
    near = device_of(dp, level, 1 - core)
    across = device_of(level, dp, core)
    deep = [device_of(dp, lax.rem(level + move, 4), core) for move in (1, 2, 3)]
    slots = [0]

    def remote(source, target_ref, target):
        slot = slots[0]
        slots[0] += 1
        return pltpu.make_async_remote_copy(
            src_ref=source,
            dst_ref=target_ref,
            send_sem=send_sem.at[slot],
            recv_sem=recv_sem.at[slot],
            device_id=target,
            device_id_type=MESH,
        )

    def place(out, source, column, half, pieces):
        rows = out.shape[1] // 4
        size = rows // pieces
        start = pl.multiple_of(columns[column] * rows + half * size, size)
        return out.at[source * 2 + core, pl.ds(start, size), :]

    def pass_on(out, source, column, target, cut):
        where = place(out, source, column, *cut)
        return remote(where, where, target)

    moves = [(packed_ref, held_ref), (qkv_ref, qkv_out), (targets_ref, targets_out)]
    crossing = [remote(source, target_ref, across) for source, target_ref in moves]
    staying = [
        pltpu.make_async_copy(source, target_ref, own_sem.at[count + index])
        for index, (source, target_ref) in enumerate(moves)
    ]
    mine = [outs[index].at[level * 2 + core] for index in range(count)]
    given = [remote(shards[index], mine[index], near) for index in range(count)]
    kept = [
        pltpu.make_async_copy(shards[index], mine[index], own_sem.at[index]) for index in range(count)
    ]
    chunks = []
    for index in range(count):
        out, pieces = outs[index], halves[index]
        for half in range(pieces):
            full = out.shape[1] // 4
            size = full // pieces
            own = shards[index].at[pl.ds(pl.multiple_of(dp * full + half * size, size), size), :]
            cut = (half, pieces)
            for move in (1, 2, 3):
                source = lax.rem(level + 4 - move, 4)
                chunks.append(
                    {
                        "level": remote(own, place(out, level, "here", *cut), deep[move - 1]),
                        "side": pass_on(out, source, "here", side, cut),
                        "down": pass_on(out, source, "here", down, cut),
                        "hop_down": pass_on(out, source, "side", down, (2 * half, 2 * pieces)),
                        "hop_side": pass_on(out, source, "down", side, (2 * half + 1, 2 * pieces)),
                        "here_near": pass_on(out, source, "here", near, cut),
                        "side_near": pass_on(out, source, "side", near, cut),
                        "down_near": pass_on(out, source, "down", near, cut),
                        "far_near": pass_on(out, source, "far", near, cut),
                    }
                )
    total = len(chunks)
    groups = total // 3

    def start_group(number):
        for chunk in chunks[3 * number : 3 * number + 3]:
            chunk["level"].start()

    @pl.when(step == 0)
    def _():
        barrier = pltpu.get_barrier_semaphore()
        for target in (side, down, near, *deep):
            pl.semaphore_signal(barrier, inc=1, device_id=target, device_id_type=MESH)

        @pl.when(dp != level)
        def _():
            pl.semaphore_signal(barrier, inc=1, device_id=across, device_id_type=MESH)
            pl.semaphore_wait(barrier, 7)
            for copy in crossing[:2]:
                copy.start()

        @pl.when(dp == level)
        def _():
            pl.semaphore_wait(barrier, 6)
            for copy in staying:
                copy.start()

        start_group(0)
        start_group(1)
        for copy in (*given, *kept):
            copy.start()

    for number in range(total + 2):

        @pl.when(step == number)
        def _(number=number):
            if number < total:
                chunk = chunks[number]
                chunk["level"].wait_recv()
                chunk["side"].start()
                chunk["down"].start()
                chunk["here_near"].start()
                if number % 3 == 2 and number // 3 + 2 < groups:
                    start_group(number // 3 + 2)
            if 0 <= number - 1 < total:
                chunk = chunks[number - 1]
                chunk["side"].wait_recv()
                chunk["hop_down"].start()
                chunk["down"].wait_recv()
                chunk["hop_side"].start()
                chunk["side_near"].start()
                chunk["down_near"].start()
            if 0 <= number - 2 < total:
                chunk = chunks[number - 2]
                chunk["hop_down"].wait_recv()
                chunk["hop_side"].wait_recv()
                chunk["far_near"].start()

    @pl.when(step == 1)
    def _():
        @pl.when(dp != level)
        def _():
            crossing[2].start()
            crossing[0].wait_recv()

        @pl.when(dp == level)
        def _():
            staying[0].wait()

        cells_ref[...] = held_ref[...]

    @pl.when((step >= 1) & (step <= HEADS // 2))
    def _():
        embed_pair(step - 1, held_ref[...], keyed_ref, bias_ref, patch_ref, var_ref, x0_ref)

    @pl.when(step == HEADS // 2 + 1)
    def _():
        lead = held_ref[0:1, 4 * V + 4 : 4 * V + 5]
        row = lax.broadcasted_iota(jnp.int32, (1, 8), 1).astype(f32)
        lead_hot = jnp.where(row == lead, 1.0, 0.0).astype(f32)
        x0_ref[...] += exact_product(lead_hot, lead_ref[...])
        unit, _ = normed_parts(x0_ref[...])
        h1_ref[...] = (unit * gains_ref[0:1, :] + gains_ref[1:2, :]).astype(bf16)

    @pl.when(step == total + 1)
    def _():
        for copy in given:
            copy.wait()
        for copy in kept:
            copy.wait()
        for chunk in chunks:
            for name in ("here_near", "side_near", "down_near", "far_near"):
                chunk[name].wait_recv()
            for copy in chunk.values():
                copy.wait_send()

        @pl.when(dp != level)
        def _():
            crossing[1].wait_recv()
            crossing[2].wait_recv()
            for copy in crossing:
                copy.wait_send()

        @pl.when(dp == level)
        def _():
            for copy in staying[1:]:
                copy.wait()


def start_program(packed, qkv, targets, prepared, lead_table, norm_gains, shards, halves):
    patch, variable, keyed, bias = prepared
    count = len(shards)
    copies = sum(halves) * 27 + count + 3
    rows, padded = packed.shape
    anywhere = pl.BlockSpec(memory_space=pl.ANY)
    fixed = lambda shape: pl.BlockSpec(shape, lambda i: (0, 0))
    by_pair = pl.BlockSpec(
        (padded, 2 * HEAD_DIM), lambda i: (0, jnp.clip(i - 1, 0, HEADS // 2 - 1))
    )
    return pl.pallas_call(
        partial(start_kernel, halves),
        grid=(sum(halves) * 3 + 2,),
        out_shape=[
            jax.ShapeDtypeStruct((rows, D), f32),
            jax.ShapeDtypeStruct((rows, D), bf16),
            jax.ShapeDtypeStruct(packed.shape, f32),
            jax.ShapeDtypeStruct(qkv.shape, bf16),
            jax.ShapeDtypeStruct(targets.shape, f32),
        ]
        + [jax.ShapeDtypeStruct((8,) + shard.shape, bf16) for shard in shards],
        in_specs=[anywhere] * 3
        + [fixed(keyed.shape), fixed(bias.shape), by_pair, by_pair]
        + [fixed(lead_table.shape), fixed(norm_gains.shape)]
        + [anywhere] * count,
        out_specs=[fixed((rows, D)), fixed((rows, D)), fixed(packed.shape)]
        + [anywhere] * (count + 2),
        scratch_shapes=[
            pltpu.VMEM(packed.shape, f32),
            pltpu.SemaphoreType.DMA((copies,)),
            pltpu.SemaphoreType.DMA((copies,)),
            pltpu.SemaphoreType.DMA((count + 3,)),
        ],
        compiler_params=pltpu.CompilerParams(
            collective_id=7, has_side_effects=True, vmem_limit_bytes=BIG
        ),
        name="start_program",
    )(packed, qkv, targets, keyed, bias, patch, variable, lead_table, norm_gains, *shards)


def own_qkv_share(crossed, grad):
    dp = lax.axis_size("dp")
    rows = grad.shape[0] // dp
    if not crossed:
        return lax.psum_scatter(grad, "dp", scatter_dimension=0, tiled=True)
    _, level, _ = mesh_place()
    return cross(crossed, sum_levels(grad.reshape((dp, rows) + grad.shape[1:]), level))


def shards(
    crossed,
    fields,
    targets,
    land_mask,
    lead_index,
    var_ids,
    tables,
    norm_gains,
    tables_first,
    tables_second,
    gains_first,
    gains_second,
    w_qkv,
    qkv_first,
    qkv_second,
    w_out,
    out_first,
    out_second,
    w_up,
    up_first,
    up_second,
    w_down,
    down_first,
    down_second,
    qkv_average,
):
    local_samples, shard_rows, _ = fields.shape
    dp_size, parts = lax.axis_size("dp"), lax.axis_size("mp")
    dp_index = lax.axis_index("dp")
    place, level, core = mesh_place()
    part = place * 2 + core if crossed else lax.axis_index("mp")
    share_rows = D // dp_size

    def own_share(full, dim):
        return lax.dynamic_slice_in_dim(full, dp_index * share_rows, share_rows, dim)

    masters = (own_share(w_qkv, 0), own_share(w_out, 1), own_share(w_up, 0), own_share(w_down, 1))
    var_hot = (var_ids[:, None] == jnp.arange(V, dtype=jnp.int32)[None, :]).astype(f32)
    prepared = prepare_tables(tables, var_hot)
    low = lambda master: master.astype(bf16)
    qkv_low = by_kind(low(w_qkv))
    packed = jnp.concatenate(
        (
            fields[0],
            land_mask[0].astype(f32),
            jnp.broadcast_to(lead_index.astype(f32), (shard_rows, 2)),
            jnp.zeros((shard_rows, 64 - 6), f32),
        ),
        axis=1,
    )
    if crossed:
        x_first, normed, packed, qkv_local, answers, w_outs, w_ups, w_downs, qkv_t = start_program(
            packed, qkv_low, targets[0], prepared, tables[5 * V : 5 * V + 8], norm_gains,
            (low(w_out), low(w_up), low(w_down), qkv_low.T), (1, 2, 2, 1),
        )
    else:
        qkv_local, answers = qkv_low, targets[0]
        w_outs, w_ups, w_downs, qkv_t = [
            lax.all_gather(shard, "mp")
            for shard in (low(w_out), low(w_up), low(w_down), qkv_low.T)
        ]
    gathered = (w_outs.reshape(D, D), w_ups, w_downs.reshape(-1, D), qkv_t.reshape(3 * D, D))
    leads = packed[0, 4 * V + 4 : 4 * V + 6].astype(jnp.int32)
    ocean = 1.0 - packed[:, 4 * V : 4 * V + 4]
    count = sum_everywhere(crossed, jnp.sum(ocean))
    denom = 2.0 * V * jnp.maximum(count, 1.0)
    first_row = part * shard_rows
    patch_row = (first_row + jnp.arange(shard_rows, dtype=jnp.int32)) // PATCH_COLS
    row_hot = (patch_row[:, None] == jnp.arange(PATCH_ROWS, dtype=jnp.int32)[None, :]).astype(f32)
    lat_rows = jnp.dot(
        row_hot, lat_weights(2 * PATCH_ROWS).reshape(PATCH_ROWS, 2), precision=highest
    )
    lat_pixels = jnp.broadcast_to(lat_rows[:, :, None], (shard_rows, 2, 2)).reshape(shard_rows, 4)
    weighted = jnp.tile(ocean * lat_pixels, (1, V))
    head = tables[5 * V + LEADS + 1 :]
    loss_part = f32(0.0)
    records = []
    for rollout in range(2):
        cells = packed
        if rollout == 1:
            cells = jnp.pad(guess, ((0, 0), (0, 64)))
        if rollout == 1 or not crossed:
            lead_row = lax.dynamic_slice_in_dim(tables, 5 * V + leads[rollout], 1, 0)
            x_first, normed = embed_forward(cells, prepared, lead_row, norm_gains)
        rows_one = spread_rows(crossed, normed)
        packed = jnp.dot(rows_one, qkv_local, preferred_element_type=f32).astype(bf16)
        own_out, full, logsum = attend(packed)
        attended = exchange(crossed, own_out, True, 2)
        x_mid, rows_two, hidden, active, x_last, guess = branch_forward(
            attended, x_first, norm_gains, gathered, head
        )
        miss = guess - answers[rollout]
        loss_part = loss_part + jnp.sum(weighted * miss * miss)
        records.append(
            (cells, x_first, rows_one, packed, full, logsum, attended, x_mid, rows_two,
             hidden, active, x_last, 2.0 * weighted * miss / denom)
        )
    carried = jnp.zeros_like(guess)
    head_total = jnp.zeros_like(head)
    gain_high = jnp.zeros((4, D), f32)
    gain_low = jnp.zeros((2, D), f32)
    table_parts, lead_sums = [], []
    qkv_grad = jnp.zeros((D, qkv_local.shape[1]), f32)
    kept = []

    def sources(index, other, blocked):
        listed = []
        for step in kept:
            listed += [(step[index], blocked), (step[other], not blocked)]
        return listed

    for rollout in (1, 0):
        (cells, x_first, rows_one, packed, full, logsum, attended, x_mid, rows_two,
         hidden, active, x_last, loss_grad) = records[rollout]
        last_low, hidden_grad, mid_grad, mid_low, out_grad, gain_part, head_grad = branch_backward(
            loss_grad + carried, x_last, x_mid, norm_gains, hidden, gathered, head
        )
        head_total = head_total + head_grad
        gain_high = gain_high + gain_part[2:]
        kept.append((attended, rows_two, active, mid_low, hidden_grad, last_low))
        last_turn = crossed and rollout == 0
        if last_turn:
            listed = (
                (sources(2, 5, True), down_pieces, 256),
                (sources(1, 4, False) + sources(0, 3, True), up_out_pieces, 320),
            )
            x, y = lax.rem(place, 2), place // 2
            where = lambda which: jnp.stack((which, x, y)).astype(jnp.int32)
            others = [outer_half(*group, where(1 - core), None) for group in listed]
            out_grad, *others = tie(out_grad, *others)
            others = [shift(other, to_core) for other in others]
        own_grad = exchange(crossed, out_grad, False, 3)
        if last_turn:
            halves = []
            for group, other in zip(listed, others):
                halves += outer_half(*group, where(core), other)
            own_grad, *halves = tie(own_grad, *halves)
            sums = [first_sums(*halves[:2]), first_sums(*halves[2:])]
        packed_grad = attend_back(own_grad, packed, full, logsum)
        if last_turn:
            packed_grad, *sums[0] = tie(packed_grad, *sums[0])
            down_pieces_sum = second_sums(*sums[0], x, y)
        token_grad = exchange(crossed, packed_grad, True, 4)
        if last_turn:
            token_grad, *sums[1] = tie(token_grad, *sums[1])
            up_out_sum = second_sums(*sums[1], x, y)
        qkv_grad = qkv_grad + lax.dot_general(
            rows_one, packed_grad, TN, preferred_element_type=f32
        )
        cells_grad, gain_one, lead_sum, *table_part = entry_backward(
            token_grad, gathered[3], x_first, mid_grad, norm_gains, cells, prepared
        )
        carried = cells_grad[:, : 4 * V]
        gain_low = gain_low + gain_one
        table_parts.append(table_part)
        lead_sums.append(lead_sum)

    def pair(index):
        return (kept[0][index], kept[1][index])

    if crossed:
        down_share = tall_piece(sum_levels(down_pieces_sum, level))
        up_out = sum_levels(up_out_sum, level)
        up_share = up_out[:256]
        out_share = tall_piece(up_out[256:])
    else:
        down_share = outer_plain(pair(2), pair(5), False)
        up_share = outer_plain(pair(1), pair(4), True)
        out_share = outer_plain(pair(0), pair(3), False)
    shares = (by_head(own_qkv_share(crossed, qkv_grad)), out_share, up_share, down_share)
    share_square = sum(jnp.sum(share * share) for share in shares)
    lead_hots = (leads[:, None] == jnp.arange(8, dtype=jnp.int32)[None, :]).astype(f32)
    lead_hots = jnp.pad(lead_hots, ((0, 6), (0, 0)))
    lead_rows = jnp.pad(jnp.concatenate((lead_sums[1], lead_sums[0])), ((0, 6), (0, 0)))
    query = tables[5 * V + LEADS : 5 * V + LEADS + 1]
    last_rows = table_grads(
        *table_parts, prepared, query, var_hot, lead_hots, lead_rows, gain_low, head_total, gain_high
    )
    if crossed:
        row = jnp.arange(8, dtype=jnp.int32)[:, None]
        tile = jnp.where(row == 0, share_square, jnp.where(row == 1, loss_part, 0.0))
        last_sum, tile_sum = exchange_sum(last_rows, jnp.broadcast_to(tile, (8, 128)))
        square_sum, loss_sum = tile_sum[0, 0], tile_sum[1, 0]
    else:
        last_sum, loss_sum, square_sum = lax.psum(
            (last_rows, loss_part, share_square), ("dp", "mp")
        )
        square_sum = square_sum + jnp.sum(last_sum * last_sum)
    head_sum = last_sum[256:]
    embed_rows = 5 * V + LEADS + 1
    table_sum = jnp.concatenate((last_sum[:embed_rows], head_sum[: 4 * V]))
    gain_sum = jnp.concatenate((last_sum[embed_rows : embed_rows + 2], head_sum[4 * V : 4 * V + 4]))
    grad_norm = jnp.sqrt(square_sum)
    factor = jnp.minimum(1.0, clip_norm / (grad_norm + 1e-06))
    tab = adam_step(tables, factor * table_sum, tables_first, tables_second, lr_table)
    gai = adam_step(norm_gains, factor * gain_sum, gains_first, gains_second, lr_gain)
    qkv = adam_step(masters[0], factor * shares[0], qkv_first, qkv_second, lr_matrix)
    outp = adam_step(masters[1], factor * shares[1], out_first, out_second, lr_matrix)
    upp = adam_step(masters[2], factor * shares[2], up_first, up_second, lr_matrix)
    down = adam_step(masters[3], factor * shares[3], down_first, down_second, lr_matrix)
    average = average_keep * qkv_average + (1.0 - average_keep) * qkv[0]
    return (
        loss_sum / denom,
        grad_norm,
        tab[0],
        tab[1],
        tab[2],
        gai[0],
        gai[1],
        gai[2],
        qkv[0],
        qkv[1],
        qkv[2],
        outp[0],
        outp[1],
        outp[2],
        upp[0],
        upp[1],
        upp[2],
        down[0],
        down[1],
        down[2],
        average,
    )


def solution(mesh):
    return jax.shard_map(
        partial(shards, is_crossed(mesh.shape)),
        mesh=mesh,
        in_specs=(
            P("dp", "mp", None),
            P("dp", None, "mp", None),
            P("dp", "mp", None),
            P("dp", None),
            P(),
            P(),
            P(),
            P(),
            P(),
            P(),
            P(),
            P(None, "mp"),
            P("dp", "mp"),
            P("dp", "mp"),
            P("mp", None),
            P("mp", "dp"),
            P("mp", "dp"),
            P(None, "mp"),
            P("dp", "mp"),
            P("dp", "mp"),
            P("mp", None),
            P("mp", "dp"),
            P("mp", "dp"),
            P("dp", "mp"),
        ),
        out_specs=(
            P(),
            P(),
            P(),
            P(),
            P(),
            P(),
            P(),
            P(),
            P("dp", "mp"),
            P("dp", "mp"),
            P("dp", "mp"),
            P("mp", "dp"),
            P("mp", "dp"),
            P("mp", "dp"),
            P("dp", "mp"),
            P("dp", "mp"),
            P("dp", "mp"),
            P("mp", "dp"),
            P("mp", "dp"),
            P("mp", "dp"),
            P("dp", "mp"),
        ),
        check_vma=False,
    )
```

```python
from functools import partial
import math

import jax
import jax.numpy as jnp
from jax import lax
from jax.experimental import pallas as pl
from jax.experimental.pallas import tpu as pltpu
from jax.sharding import PartitionSpec as P

D = 1024
HEADS = 16
HEAD_DIM = 64
V = 48
PATCH_ROWS = 32
PATCH_COLS = 64
LEADS = 7


highest = lax.Precision.HIGHEST
eps_norm = 1e-05
clip_norm = 0.05
beta_first = 0.9
beta_second = 0.999
adam_eps = 1e-08
decay_rate = 0.1
lr_matrix = 0.04
lr_table = 0.1
lr_gain = 0.3
average_keep = 0.9
first_fix = 1.0 - 0.9**10
second_fix = 1.0 - 0.999**10


def layer_norm(values, gain, bias):
    center = values - jnp.mean(values, axis=-1, keepdims=True)
    spread = jnp.mean(center * center, axis=-1, keepdims=True)
    return center * lax.rsqrt(spread + eps_norm) * gain + bias


def lat_weights(pixel_rows):
    row_index = jnp.arange(pixel_rows, dtype=jnp.float32)
    cosine = jnp.cos(((row_index + 0.5) / pixel_rows - 0.5) * math.pi)
    return cosine / jnp.mean(cosine)


bf16 = jnp.bfloat16
f32 = jnp.float32
MESH = pl.DeviceIdType.MESH
NT = (((1,), (1,)), ((), ()))
TN = (((0,), (0,)), ((), ()))
VMEM = pl.BlockSpec(memory_space=pltpu.VMEM)
BIG = 56 * 2**20


def is_crossed(sizes):
    return sizes["dp"] == 4 and sizes["mp"] == 8


def mesh_place():
    dp = lax.axis_index("dp")
    mp = lax.axis_index("mp")
    return dp, mp // 2, lax.rem(mp, 2)


def device_of(dp, level, core):
    return {"dp": dp, "mp": level * 2 + core}


def cross_pairs():
    groups = lax.axis_size("dp")
    pairs = []
    for dp in range(groups):
        for level in range(groups):
            for core in range(2):
                source = (dp * groups + level) * 2 + core
                target = (level * groups + dp) * 2 + core
                pairs.append((source, target))
    return pairs


def cross(crossed, value):
    if not crossed:
        return value
    return lax.ppermute(value, ("dp", "mp"), cross_pairs())


def gather_kernel(x_ref, o_ref, send_sem, recv_sem):
    rows = x_ref.shape[0]
    half = rows // 2
    dp, level, core = mesh_place()
    side = dp + 1 - 2 * lax.rem(dp, 2)
    down = lax.rem(dp + 2, 4)
    far = 3 - dp
    to_side = device_of(side, level, core)
    to_down = device_of(down, level, core)
    to_core = device_of(dp, level, 1 - core)

    def rows_of(owner, who, first, size):
        return pl.ds(pl.multiple_of((owner * 2 + who) * rows + first, half), size)

    barrier = pltpu.get_barrier_semaphore()
    for target in (to_side, to_down, to_core):
        pl.semaphore_signal(barrier, inc=1, device_id=target, device_id_type=MESH)
    pl.semaphore_wait(barrier, 3)

    def send(slot, source, where, target):
        copy = pltpu.make_async_remote_copy(
            src_ref=source,
            dst_ref=o_ref.at[where],
            send_sem=send_sem.at[slot],
            recv_sem=recv_sem.at[slot],
            device_id=target,
            device_id_type=MESH,
        )
        copy.start()
        return copy

    first = x_ref.at[pl.ds(0, half)]
    second = x_ref.at[pl.ds(half, half)]
    side_a = send(0, first, rows_of(dp, core, 0, half), to_side)
    down_b = send(1, second, rows_of(dp, core, half, half), to_down)
    side_b = send(2, second, rows_of(dp, core, half, half), to_side)
    down_a = send(3, first, rows_of(dp, core, 0, half), to_down)
    near = send(4, x_ref, rows_of(dp, core, 0, rows), to_core)
    o_ref[rows_of(dp, core, 0, rows)] = x_ref[...]
    side_a.wait_recv()
    place = rows_of(side, core, 0, half)
    far_a = send(5, o_ref.at[place], place, to_down)
    down_b.wait_recv()
    place = rows_of(down, core, half, half)
    far_b = send(6, o_ref.at[place], place, to_side)
    side_b.wait_recv()
    place = rows_of(side, core, 0, rows)
    near_side = send(7, o_ref.at[place], place, to_core)
    down_a.wait_recv()
    place = rows_of(down, core, 0, rows)
    near_down = send(8, o_ref.at[place], place, to_core)
    far_a.wait_recv()
    far_b.wait_recv()
    place = rows_of(far, core, 0, rows)
    near_far = send(9, o_ref.at[place], place, to_core)
    for copy in (near, near_side, near_down, near_far):
        copy.wait_recv()
    for copy in (side_a, down_b, side_b, down_a, near, far_a, far_b, near_side, near_down, near_far):
        copy.wait_send()


def spread_rows(crossed, normed):
    if not crossed:
        return lax.all_gather(normed, "mp", axis=0, tiled=True)
    rows, width = normed.shape
    return pl.pallas_call(
        gather_kernel,
        out_shape=jax.ShapeDtypeStruct((8 * rows, width), normed.dtype),
        in_specs=[VMEM],
        out_specs=VMEM,
        scratch_shapes=[pltpu.SemaphoreType.DMA((10,)), pltpu.SemaphoreType.DMA((10,))],
        compiler_params=pltpu.CompilerParams(
            collective_id=1, has_side_effects=True, vmem_limit_bytes=BIG
        ),
        name="gather_rows",
    )(normed)


def exchange_kernel(to_columns, rows, width, x_ref, o_ref, send_sem, recv_sem):
    dp, level, core = mesh_place()
    me = dp * 2 + core
    barrier = pltpu.get_barrier_semaphore()
    others = []
    for step in (7, 6, 5, 4, 3, 2, 1):
        part = lax.rem(me + step, 8)
        others.append((step, part, device_of(part // 2, level, lax.rem(part, 2))))
    for step, part, target in others:
        pl.semaphore_signal(barrier, inc=1, device_id=target, device_id_type=MESH)
    pl.semaphore_wait(barrier, 7)

    def row_block(ref, part):
        return ref.at[pl.ds(pl.multiple_of(part * rows, rows), rows), :]

    def column_block(ref, part):
        return ref.at[:, pl.ds(pl.multiple_of(part * width, width), width)]

    source_block, target_block = (
        (row_block, column_block) if to_columns else (column_block, row_block)
    )
    copies = []
    for step, part, target in others:
        copy = pltpu.make_async_remote_copy(
            src_ref=source_block(x_ref, part),
            dst_ref=target_block(o_ref, me),
            send_sem=send_sem.at[step],
            recv_sem=recv_sem.at[step],
            device_id=target,
            device_id_type=MESH,
        )
        copy.start()
        copies.append(copy)
    target_block(o_ref, me)[...] = source_block(x_ref, me)[...]
    for copy in copies:
        copy.wait()


def exchange(crossed, value, to_columns, number):
    parts = lax.axis_size("mp")
    if to_columns:
        rows, width = value.shape[0] // parts, value.shape[1]
        shape = (rows, width * parts)
    else:
        rows, width = value.shape[0], value.shape[1] // parts
        shape = (rows * parts, width)
    if not crossed:
        split, joined = (0, 1) if to_columns else (1, 0)
        return lax.all_to_all(value, "mp", split_axis=split, concat_axis=joined, tiled=True)
    return pl.pallas_call(
        partial(exchange_kernel, to_columns, rows, width),
        out_shape=jax.ShapeDtypeStruct(shape, value.dtype),
        in_specs=[VMEM],
        out_specs=VMEM,
        scratch_shapes=[pltpu.SemaphoreType.DMA((8,)), pltpu.SemaphoreType.DMA((8,))],
        compiler_params=pltpu.CompilerParams(
            collective_id=number, has_side_effects=True, vmem_limit_bytes=BIG
        ),
        name="exchange_parts",
    )(value)


def pick_head(value, head, heads):
    if heads == 1:
        return value
    lane = lax.broadcasted_iota(jnp.int32, value.shape, 1) // HEAD_DIM
    return jnp.where(lane == head, value, jnp.zeros_like(value))


def attend_rows(heads, queries, k_ref, vt_ref):
    queries = queries * bf16(HEAD_DIM**-0.5)
    keys = k_ref[...]
    outs, sums = [], []
    for head in range(heads):
        scores = lax.dot_general(
            keys, pick_head(queries, head, heads), NT, preferred_element_type=f32
        )
        largest = jnp.max(scores, axis=0, keepdims=True)
        raised = jnp.exp(scores - largest)
        total = jnp.sum(raised, axis=0, keepdims=True)
        probs = (raised * (1.0 / total)).astype(bf16)
        values = vt_ref[head * HEAD_DIM : (head + 1) * HEAD_DIM, :]
        outs.append(jnp.dot(values, probs, preferred_element_type=f32))
        sums.append(largest + jnp.log(total))
    flipped = outs[0] if heads == 1 else jnp.concatenate(outs, axis=0)
    return flipped.T, sums


def attend_kernel(heads, q_ref, k_ref, v_ref, o_ref, full_ref, lse_ref, vt_ref):
    @pl.when(pl.program_id(0) == 0)
    def _():
        vt_ref[...] = v_ref[...].T

    full, sums = attend_rows(heads, q_ref[...], k_ref, vt_ref)
    for head in range(heads):
        lse_ref[head : head + 1, :] = sums[head]
    full_ref[...] = full
    o_ref[...] = full.astype(bf16)


def attend(packed):
    total, width = packed.shape[0], packed.shape[1] // 3
    heads = width // HEAD_DIM
    block = min(512, total)
    row_block = pl.BlockSpec((block, width), lambda i: (i, 0))
    return pl.pallas_call(
        partial(attend_kernel, heads),
        grid=(total // block,),
        out_shape=(
            jax.ShapeDtypeStruct((total, width), bf16),
            jax.ShapeDtypeStruct((total, width), f32),
            jax.ShapeDtypeStruct((heads, total), f32),
        ),
        in_specs=[
            row_block,
            pl.BlockSpec((total, width), lambda i: (0, 0)),
            pl.BlockSpec((total, width), lambda i: (0, 0)),
        ],
        out_specs=[row_block, row_block, pl.BlockSpec((heads, block), lambda i: (0, i))],
        scratch_shapes=[pltpu.VMEM((width, total), bf16)],
        compiler_params=pltpu.CompilerParams(vmem_limit_bytes=BIG),
        cost_estimate=pl.CostEstimate(
            flops=16 * total * total * width,
            bytes_accessed=10 * total * width,
            transcendentals=heads * total * total,
        ),
        name="attend",
    )(packed[:, :width], packed[:, width : 2 * width], packed[:, 2 * width :])


def attend_back_kernel(
    heads, q_ref, do_ref, full_ref, lse_ref, k_ref, v_ref, dq_ref, dk_ref, dv_ref, kt_ref, dk_sum, dv_sum
):
    step = pl.program_id(0)
    total = k_ref.shape[0]
    chunk = min(1024, total)

    @pl.when(step == 0)
    def _():
        kt_ref[...] = k_ref[...].T
        dk_sum[...] = jnp.zeros_like(dk_sum)
        dv_sum[...] = jnp.zeros_like(dv_sum)

    scale = HEAD_DIM**-0.5
    queries = q_ref[...]
    grads = do_ref[...]
    products = (grads.astype(f32) * full_ref[...]).T
    query_heads = [pick_head(queries, head, heads) for head in range(heads)]
    grad_heads = [pick_head(grads, head, heads) for head in range(heads)]
    inner = [
        jnp.sum(products[head * HEAD_DIM : (head + 1) * HEAD_DIM], axis=0, keepdims=True) * scale
        for head in range(heads)
    ]
    query_grads = [None] * heads
    for start in range(0, total, chunk):
        rows = slice(start, start + chunk)
        keys = k_ref[rows, :]
        values = v_ref[rows, :]
        value_part = None
        key_part = None
        for head in range(heads):
            scores = lax.dot_general(
                keys, query_heads[head] * bf16(scale), NT, preferred_element_type=f32
            )
            probs = jnp.exp(scores - lse_ref[head : head + 1, :])
            prob_grad = lax.dot_general(
                values, grad_heads[head] * bf16(scale), NT, preferred_element_type=f32
            )
            score_grad = (probs * (prob_grad - inner[head])).astype(bf16)
            one = jnp.dot(probs.astype(bf16), grad_heads[head], preferred_element_type=f32)
            two = jnp.dot(score_grad, query_heads[head], preferred_element_type=f32)
            value_part = one if value_part is None else value_part + one
            key_part = two if key_part is None else key_part + two
            three = jnp.dot(
                kt_ref[head * HEAD_DIM : (head + 1) * HEAD_DIM, rows],
                score_grad,
                preferred_element_type=f32,
            )
            query_grads[head] = three if query_grads[head] is None else query_grads[head] + three
        dv_sum[rows, :] += value_part
        dk_sum[rows, :] += key_part
    flipped = query_grads[0] if heads == 1 else jnp.concatenate(query_grads, axis=0)
    dq_ref[...] = flipped.T.astype(bf16)

    @pl.when(step == pl.num_programs(0) - 1)
    def _():
        dk_ref[...] = dk_sum[...].astype(bf16)
        dv_ref[...] = dv_sum[...].astype(bf16)


def attend_back(grad_out, packed, full, logsum):
    total, width = grad_out.shape
    heads = width // HEAD_DIM
    block = min(256, total)
    row_block = pl.BlockSpec((block, width), lambda i: (i, 0))
    whole = pl.BlockSpec((total, width), lambda i: (0, 0))
    query_grad, key_grad, value_grad = pl.pallas_call(
        partial(attend_back_kernel, heads),
        grid=(total // block,),
        out_shape=(jax.ShapeDtypeStruct((total, width), bf16),) * 3,
        in_specs=[
            row_block,
            row_block,
            row_block,
            pl.BlockSpec((heads, block), lambda i: (0, i)),
            whole,
            whole,
        ],
        out_specs=[row_block, whole, whole],
        scratch_shapes=[
            pltpu.VMEM((width, total), bf16),
            pltpu.VMEM((total, width), f32),
            pltpu.VMEM((total, width), f32),
        ],
        compiler_params=pltpu.CompilerParams(vmem_limit_bytes=BIG),
        cost_estimate=pl.CostEstimate(
            flops=40 * total * total * width,
            bytes_accessed=16 * total * width,
            transcendentals=heads * total * total,
        ),
        name="attend_back",
    )(
        packed[:, :width],
        grad_out,
        full,
        logsum,
        packed[:, width : 2 * width],
        packed[:, 2 * width :],
    )
    return jnp.concatenate((query_grad, key_grad, value_grad), axis=1)


def normed_parts(values):
    center = values - jnp.mean(values, axis=-1, keepdims=True)
    spread = jnp.mean(center * center, axis=-1, keepdims=True)
    inverse = lax.rsqrt(spread + eps_norm)
    return center * inverse, inverse


def norm_grad(unit, inverse, gain, grad):
    scaled = grad * gain
    middle = jnp.mean(scaled, axis=-1, keepdims=True)
    along = jnp.mean(scaled * unit, axis=-1, keepdims=True)
    gain_grad = jnp.sum(grad * unit, axis=0, keepdims=True)
    bias_grad = jnp.sum(grad, axis=0, keepdims=True)
    return inverse * (scaled - middle - unit * along), gain_grad, bias_grad


def gauss_share(values):
    return 0.5 * (1.0 + lax.erf(values * (0.5**0.5)))


def branch_kernel(
    o_ref, x0_ref, gains_ref, out_ref, up_ref, down_ref, head_ref,
    x1_ref, h2_ref, g_ref, act_ref, x2_ref, pred_ref,
):
    step = pl.program_id(0)

    @pl.when(step == 0)
    def _():
        x1_ref[...] = x0_ref[...] + jnp.dot(
            o_ref[...], out_ref[...], preferred_element_type=f32
        )
        unit, _ = normed_parts(x1_ref[...])
        h2_ref[...] = (unit * gains_ref[2:3, :] + gains_ref[3:4, :]).astype(bf16)
        x2_ref[...] = x1_ref[...]

    hidden = jnp.dot(h2_ref[...], up_ref[0], preferred_element_type=f32)
    g_ref[...] = hidden
    active = (hidden * gauss_share(hidden)).astype(bf16)
    act_ref[...] = active
    x2_ref[...] += jnp.dot(active, down_ref[...], preferred_element_type=f32)

    @pl.when(step == pl.num_programs(0) - 1)
    def _():
        unit, _ = normed_parts(x2_ref[...])
        last = unit * gains_ref[4:5, :] + gains_ref[5:6, :]
        pred_ref[...] = lax.dot_general(
            last, head_ref[...], NT, precision=highest, preferred_element_type=f32
        )


def weight_specs(w_out, w_up, w_down):
    _, width, units = w_up.shape
    return (
        pl.BlockSpec(w_out.shape, lambda i: (0, 0)),
        pl.BlockSpec((1, width, units), lambda i: (i, 0, 0)),
        pl.BlockSpec((units, width), lambda i: (i, 0)),
    )


def branch_forward(attended, x_first, norm_gains, gathered, head):
    w_out, w_up, w_down, _ = gathered
    rows, width = x_first.shape
    parts, units = w_up.shape[0], w_up.shape[2]
    fixed = lambda shape: pl.BlockSpec(shape, lambda i: (0, 0))
    by_units = pl.BlockSpec((rows, units), lambda i: (0, i))
    columns = head.shape[0]
    flops = 2 * rows * (width * width + 2 * width * parts * units + 6 * width * columns)
    return pl.pallas_call(
        branch_kernel,
        grid=(parts,),
        out_shape=(
            jax.ShapeDtypeStruct((rows, width), f32),
            jax.ShapeDtypeStruct((rows, width), bf16),
            jax.ShapeDtypeStruct((rows, parts * units), f32),
            jax.ShapeDtypeStruct((rows, parts * units), bf16),
            jax.ShapeDtypeStruct((rows, width), f32),
            jax.ShapeDtypeStruct((rows, columns), f32),
        ),
        in_specs=[
            fixed((rows, width)),
            fixed((rows, width)),
            fixed(norm_gains.shape),
            *weight_specs(w_out, w_up, w_down),
            fixed(head.shape),
        ],
        out_specs=[
            fixed((rows, width)),
            fixed((rows, width)),
            by_units,
            by_units,
            fixed((rows, width)),
            fixed((rows, columns)),
        ],
        compiler_params=pltpu.CompilerParams(vmem_limit_bytes=BIG),
        cost_estimate=pl.CostEstimate(
            flops=flops,
            bytes_accessed=4 * width * parts * units + 6 * rows * parts * units,
            transcendentals=rows * parts * units,
        ),
        name="branch_forward",
    )(attended, x_first, norm_gains, w_out, w_up, w_down, head)


def branch_back_kernel(
    dpred_ref, x2_ref, x1_ref, gains_ref, g_ref, out_ref, up_ref, down_ref, head_ref,
    dx2_ref, dg_ref, dx1_ref, low_ref, do_ref, gain_ref, dhead_ref,
    wide_ref, sum_ref,
):
    step = pl.program_id(0)

    @pl.when(step == 0)
    def _():
        grad = dpred_ref[...]
        unit, inverse = normed_parts(x2_ref[...])
        gain = gains_ref[4:5, :]
        last = unit * gain + gains_ref[5:6, :]
        dhead_ref[...] = lax.dot_general(
            grad, last, TN, precision=highest, preferred_element_type=f32
        )
        row_grad = jnp.dot(grad, head_ref[...], precision=highest, preferred_element_type=f32)
        wide, gain_grad, bias_grad = norm_grad(unit, inverse, gain, row_grad)
        gain_ref[...] = jnp.zeros_like(gain_ref)
        gain_ref[4:5, :] = gain_grad
        gain_ref[5:6, :] = bias_grad
        wide_ref[...] = wide
        dx2_ref[...] = wide.astype(bf16)
        sum_ref[...] = jnp.zeros_like(sum_ref)

    active_grad = lax.dot_general(dx2_ref[...], down_ref[...], NT, preferred_element_type=f32)
    hidden = g_ref[...]
    slope = gauss_share(hidden) + hidden * (
        jnp.exp(-0.5 * hidden * hidden) * (2.0 * math.pi) ** -0.5
    )
    hidden_grad = (active_grad * slope).astype(bf16)
    dg_ref[...] = hidden_grad
    sum_ref[...] += lax.dot_general(hidden_grad, up_ref[0], NT, preferred_element_type=f32)

    @pl.when(step == pl.num_programs(0) - 1)
    def _():
        unit, inverse = normed_parts(x1_ref[...])
        middle, gain_grad, bias_grad = norm_grad(unit, inverse, gains_ref[2:3, :], sum_ref[...])
        gain_ref[2:3, :] = gain_grad
        gain_ref[3:4, :] = bias_grad
        middle = wide_ref[...] + middle
        dx1_ref[...] = middle
        low_ref[...] = middle.astype(bf16)
        total = lax.dot_general(low_ref[...], out_ref[...], NT, preferred_element_type=f32)
        do_ref[...] = total.astype(bf16)


def branch_backward(pred_grad, x_last, x_mid, norm_gains, hidden, gathered, head):
    w_out, w_up, w_down, _ = gathered
    rows, width = x_last.shape
    parts, units = w_up.shape[0], w_up.shape[2]
    fixed = lambda shape: pl.BlockSpec(shape, lambda i: (0, 0))
    by_units = pl.BlockSpec((rows, units), lambda i: (0, i))
    columns = head.shape[0]
    wide = (rows, width)
    flops = 2 * rows * (width * width + 2 * width * parts * units + 12 * width * columns)
    return pl.pallas_call(
        branch_back_kernel,
        grid=(parts,),
        out_shape=(
            jax.ShapeDtypeStruct(wide, bf16),
            jax.ShapeDtypeStruct((rows, parts * units), bf16),
            jax.ShapeDtypeStruct(wide, f32),
            jax.ShapeDtypeStruct(wide, bf16),
            jax.ShapeDtypeStruct(wide, bf16),
            jax.ShapeDtypeStruct((6, width), f32),
            jax.ShapeDtypeStruct((columns, width), f32),
        ),
        in_specs=[
            fixed((rows, columns)),
            fixed(wide),
            fixed(wide),
            fixed(norm_gains.shape),
            by_units,
            *weight_specs(w_out, w_up, w_down),
            fixed(head.shape),
        ],
        out_specs=[
            fixed(wide),
            by_units,
            fixed(wide),
            fixed(wide),
            fixed(wide),
            fixed((6, width)),
            fixed((columns, width)),
        ],
        scratch_shapes=[pltpu.VMEM(wide, f32), pltpu.VMEM(wide, f32)],
        compiler_params=pltpu.CompilerParams(vmem_limit_bytes=BIG),
        cost_estimate=pl.CostEstimate(
            flops=flops,
            bytes_accessed=4 * width * parts * units + 6 * rows * parts * units,
            transcendentals=2 * rows * parts * units,
        ),
        name="branch_backward",
    )(pred_grad, x_last, x_mid, norm_gains, hidden, w_out, w_up, w_down, head)


def wide_piece(piece):
    half = piece.shape[0] // 2
    return jnp.concatenate((piece[:half], piece[half:]), axis=1)


def tall_piece(piece):
    half = piece.shape[1] // 2
    return jnp.concatenate((piece[:, :half], piece[:, half:]), axis=0)


def both_steps(left_a, right_a, left_b, right_b):
    product = lax.dot_general(left_a[...], right_a[...], TN, preferred_element_type=f32)
    return product + lax.dot_general(left_b[...], right_b[...], TN, preferred_element_type=f32)


def down_pieces(refs):
    product = both_steps(*refs)
    share = product.shape[1] // 4
    return [wide_piece(product[:, i * share : (i + 1) * share]) for i in range(4)]


def up_out_pieces(refs):
    up = both_steps(*refs[:4])
    share = up.shape[0] // 4
    out = both_steps(*refs[4:])
    size = out.shape[1] // 4
    return [
        jnp.concatenate(
            (up[i * share : (i + 1) * share], wide_piece(out[:, i * size : (i + 1) * size])), axis=0
        )
        for i in range(4)
    ]


def outer_other_kernel(make, count, where_ref, *refs):
    o_ref = refs[count]
    for split, piece in enumerate(make(refs[:count])):
        o_ref[0, split] = piece.astype(bf16)


def outer_own_kernel(make, count, where_ref, *refs):
    other_ref, send_ref, keep_ref, held_ref = refs[count:]
    for split, piece in enumerate(make(refs[:count])):
        held_ref[split] = (piece + other_ref[0, split].astype(f32)).astype(bf16)
    x, y = where_ref[1], where_ref[2]
    early = pl.program_id(0) < 2
    for which in range(2):
        send_ref[0, which] = held_ref[jnp.where(early, which * 2 + 1 - x, (1 - y) * 2 + which)]
        keep_ref[0, which] = held_ref[jnp.where(early, which * 2 + x, y * 2 + which)]


def outer_half(operands, make, height, where, other):
    specs = []
    for value, blocked in operands:
        rows, size = value.shape
        if blocked:
            specs.append(pl.BlockSpec((rows, size // 8), lambda i, w: (0, i * 2 + w[0])))
        else:
            specs.append(pl.BlockSpec((rows, size), lambda i, w: (0, 0)))
    values = [value for value, _ in operands]
    count = len(values)
    whole = pl.BlockSpec((1, 4, height, 512), lambda i, w: (i, 0, 0, 0))
    half = pl.BlockSpec((1, 2, height, 512), lambda i, w: (i, 0, 0, 0))
    rows = values[0].shape[0]
    cost = pl.CostEstimate(
        flops=2 * 2 * rows * 16 * height * 512, bytes_accessed=3 * 16 * height * 512, transcendentals=0
    )
    params = pltpu.CompilerParams(vmem_limit_bytes=BIG)
    if other is None:
        return pl.pallas_call(
            partial(outer_other_kernel, make, count),
            out_shape=jax.ShapeDtypeStruct((4, 4, height, 512), bf16),
            grid_spec=pltpu.PrefetchScalarGridSpec(
                num_scalar_prefetch=1, grid=(4,), in_specs=specs, out_specs=whole
            ),
            compiler_params=params,
            cost_estimate=cost,
            name="outer_other",
        )(where, *values)
    return pl.pallas_call(
        partial(outer_own_kernel, make, count),
        out_shape=(jax.ShapeDtypeStruct((4, 2, height, 512), bf16),) * 2,
        grid_spec=pltpu.PrefetchScalarGridSpec(
            num_scalar_prefetch=1,
            grid=(4,),
            in_specs=specs + [whole],
            out_specs=[half, half],
            scratch_shapes=[pltpu.VMEM((4, height, 512), bf16)],
        ),
        compiler_params=params,
        cost_estimate=cost,
        name="outer_own",
    )(where, *values, other)


def device_pairs(move):
    pairs = []
    for dp in range(4):
        for level in range(4):
            for core in range(2):
                to_dp, to_level, to_core = move(dp, level, core)
                pairs.append(((dp * 4 + level) * 2 + core, (to_dp * 4 + to_level) * 2 + to_core))
    return pairs


def shift(value, move):
    return lax.ppermute(value, ("dp", "mp"), device_pairs(move))


def to_core(dp, level, core):
    return dp, level, 1 - core


def to_side(dp, level, core):
    return dp ^ 1, level, core


def to_down(dp, level, core):
    return dp ^ 2, level, core


def choose(value, index, axis=0):
    return lax.dynamic_index_in_dim(value, index, axis, keepdims=False)


def sum_levels(pieces, level):
    total = choose(pieces, level).astype(f32)
    for step in range(1, 4):
        piece = choose(pieces, lax.rem(level + step, 4)).astype(bf16)
        moved = shift(piece, lambda dp, z, core: (dp, (z + step) % 4, core))
        total = total + moved.astype(f32)
    return total


def tie(*values):
    return lax.optimization_barrier(values)


def first_sums(send, keep):
    first = keep[:2].astype(f32) + shift(send[:2], to_side).astype(f32)
    second = keep[2:].astype(f32) + shift(send[2:], to_down).astype(f32)
    return first.astype(bf16), second.astype(bf16)


def second_sums(first, second, x, y):
    first_moved = shift(choose(first, 1 - y, 1), to_down)
    second_moved = shift(choose(second, 1 - x, 1), to_side)
    first = choose(first, y, 1).astype(f32) + first_moved.astype(f32)
    second = choose(second, x, 1).astype(f32) + second_moved.astype(f32)
    return jnp.concatenate((first, second))


def outer_plain(lefts, rights, by_rows):
    dp, mp = lax.axis_size("dp"), lax.axis_size("mp")
    grads = sum(
        lax.dot_general(left, right, TN, preferred_element_type=f32)
        for left, right in zip(lefts, rights)
    ).astype(bf16)
    rows, width = grads.shape
    if by_rows:
        grads = grads.reshape(dp, rows // dp, mp, width // mp).transpose(0, 2, 1, 3)
    else:
        grads = grads.reshape(mp, rows // mp, dp, width // dp).transpose(2, 0, 1, 3)
    grads = grads.reshape((dp * mp,) + grads.shape[2:])
    return lax.psum_scatter(grads, ("dp", "mp"), scatter_dimension=0, tiled=False).astype(f32)


def exchange_sum_kernel(
    x_ref, t_ref, o_ref, s_ref, work_ref, pair_ref, quad_ref, eight_ref, deep_ref, tile_ref,
    send_sem, recv_sem,
):
    dp, level, core = mesh_place()
    x, y = lax.rem(dp, 2), dp // 2
    side = device_of(dp + 1 - 2 * x, level, core)
    down = device_of(lax.rem(dp + 2, 4), level, core)
    near = device_of(dp, level, 1 - core)
    deep = [device_of(dp, lax.rem(level + step, 4), core) for step in (1, 2, 3)]
    barrier = pltpu.get_barrier_semaphore()
    for target in (side, down, near, *deep):
        pl.semaphore_signal(barrier, inc=1, device_id=target, device_id_type=MESH)
    pl.semaphore_wait(barrier, 6)
    started = []

    def send(source, target_ref, target):
        slot = len(started)
        copy = pltpu.make_async_remote_copy(
            src_ref=source,
            dst_ref=target_ref,
            send_sem=send_sem.at[slot],
            recv_sem=recv_sem.at[slot],
            device_id=target,
            device_id_type=MESH,
        )
        copy.start()
        started.append(copy)
        return copy

    half = x_ref.shape[0] // 2
    quarter, eighth, part, unit = half // 2, half // 4, half // 8, half // 16

    def rows(start, size):
        return pl.ds(pl.multiple_of(start, unit), size)

    copy = send(x_ref.at[rows((1 - core) * half, half)], pair_ref, near)
    copy.wait_recv()
    work_ref[...] = x_ref[rows(core * half, half)] + pair_ref[...]
    one = send(work_ref.at[rows((1 - x) * eighth, eighth)], quad_ref.at[0], side)
    two = send(work_ref.at[rows(quarter + (1 - y) * eighth, eighth)], quad_ref.at[1], down)
    base_a = x * eighth
    base_b = quarter + y * eighth
    wide_a, wide_b = core * half + base_a, core * half + base_b
    one.wait_recv()
    work_ref[rows(base_a, eighth)] += quad_ref[0]
    one = send(work_ref.at[rows(base_a + (1 - y) * part, part)], eight_ref.at[0], down)
    two.wait_recv()
    work_ref[rows(base_b, eighth)] += quad_ref[1]
    two = send(work_ref.at[rows(base_b + (1 - x) * part, part)], eight_ref.at[1], side)
    base_a = base_a + y * part
    base_b = base_b + x * part
    one.wait_recv()
    work_ref[rows(base_a, part)] += eight_ref[0]
    two.wait_recv()
    work_ref[rows(base_b, part)] += eight_ref[1]

    def level_start(which):
        late = which // 2
        return (1 - late) * base_a + late * base_b + lax.rem(which, 2) * unit

    copies = []
    for step in (1, 2, 3):
        source = work_ref.at[rows(level_start(lax.rem(level + step, 4)), unit)]
        copies.append(send(source, deep_ref.at[step - 1], deep[step - 1]))
    for copy in copies:
        copy.wait_recv()
    total = work_ref[rows(level_start(level), unit)] + deep_ref[0] + deep_ref[1] + deep_ref[2]
    mine = rows(core * half + level_start(level), unit)
    base_a = core * half + base_a
    base_b = core * half + base_b
    o_ref[mine] = total
    row = lax.broadcasted_iota(jnp.int32, t_ref.shape, 0)
    tile_ref[0] = t_ref[...] + jnp.where(row == 0, jnp.sum(total * total), 0.0)
    copies = []
    for step in (1, 2, 3):
        copies.append(send(o_ref.at[mine], o_ref.at[mine], deep[step - 1]))
        copies.append(send(tile_ref.at[0], tile_ref.at[step], deep[step - 1]))
    for copy in copies:
        copy.wait_recv()
    one = send(o_ref.at[rows(base_a, part)], o_ref.at[rows(base_a, part)], down)
    two = send(o_ref.at[rows(base_b, part)], o_ref.at[rows(base_b, part)], side)
    tile_ref[4] = tile_ref[0] + tile_ref[1] + tile_ref[2] + tile_ref[3]
    three = send(tile_ref.at[4], tile_ref.at[5], side)
    one.wait_recv()
    one = send(o_ref.at[rows(wide_a, eighth)], o_ref.at[rows(wide_a, eighth)], side)
    two.wait_recv()
    two = send(o_ref.at[rows(wide_b, eighth)], o_ref.at[rows(wide_b, eighth)], down)
    three.wait_recv()
    tile_ref[6] = tile_ref[4] + tile_ref[5]
    three = send(tile_ref.at[6], tile_ref.at[7], down)
    one.wait_recv()
    two.wait_recv()
    one = send(o_ref.at[rows(core * half, half)], o_ref.at[rows(core * half, half)], near)
    three.wait_recv()
    tile_ref[8] = tile_ref[6] + tile_ref[7]
    three = send(tile_ref.at[8], tile_ref.at[9], near)
    one.wait_recv()
    three.wait_recv()
    s_ref[...] = tile_ref[8] + tile_ref[9]
    for copy in started:
        copy.wait_send()


def exchange_sum(value, tile):
    rows, width = value.shape
    return pl.pallas_call(
        exchange_sum_kernel,
        out_shape=(jax.ShapeDtypeStruct(value.shape, f32), jax.ShapeDtypeStruct(tile.shape, f32)),
        in_specs=[VMEM, VMEM],
        out_specs=[VMEM, VMEM],
        scratch_shapes=[
            pltpu.VMEM((rows // 2, width), f32),
            pltpu.VMEM((rows // 2, width), f32),
            pltpu.VMEM((2, rows // 8, width), f32),
            pltpu.VMEM((2, rows // 16, width), f32),
            pltpu.VMEM((3, rows // 32, width), f32),
            pltpu.VMEM((10,) + tile.shape, f32),
            pltpu.SemaphoreType.DMA((24,)),
            pltpu.SemaphoreType.DMA((24,)),
        ],
        compiler_params=pltpu.CompilerParams(
            collective_id=5, has_side_effects=True, vmem_limit_bytes=BIG
        ),
        name="exchange_sum",
    )(value, tile)


def tile_sum_kernel(t_ref, s_ref, tile_ref, send_sem, recv_sem):
    dp, level, core = mesh_place()
    x = lax.rem(dp, 2)
    side = device_of(dp + 1 - 2 * x, level, core)
    down = device_of(lax.rem(dp + 2, 4), level, core)
    near = device_of(dp, level, 1 - core)
    deep = [device_of(dp, lax.rem(level + step, 4), core) for step in (1, 2, 3)]
    barrier = pltpu.get_barrier_semaphore()
    for target in (side, down, near, *deep):
        pl.semaphore_signal(barrier, inc=1, device_id=target, device_id_type=MESH)
    pl.semaphore_wait(barrier, 6)

    def send(slot, source, target_ref, target):
        copy = pltpu.make_async_remote_copy(
            src_ref=source,
            dst_ref=target_ref,
            send_sem=send_sem.at[slot],
            recv_sem=recv_sem.at[slot],
            device_id=target,
            device_id_type=MESH,
        )
        copy.start()
        return copy

    copies = [send(step, t_ref, tile_ref.at[step], deep[step]) for step in range(3)]
    for copy in copies:
        copy.wait()
    tile_ref[3] = t_ref[...] + tile_ref[0] + tile_ref[1] + tile_ref[2]
    send(3, tile_ref.at[3], tile_ref.at[4], side).wait()
    tile_ref[5] = tile_ref[3] + tile_ref[4]
    send(4, tile_ref.at[5], tile_ref.at[6], down).wait()
    tile_ref[7] = tile_ref[5] + tile_ref[6]
    send(5, tile_ref.at[7], tile_ref.at[8], near).wait()
    s_ref[...] = tile_ref[7] + tile_ref[8]


def sum_everywhere(crossed, value):
    if not crossed:
        return lax.psum(value, ("dp", "mp"))
    tile = jnp.broadcast_to(value, (8, 128))
    total = pl.pallas_call(
        tile_sum_kernel,
        out_shape=jax.ShapeDtypeStruct(tile.shape, f32),
        in_specs=[VMEM],
        out_specs=VMEM,
        scratch_shapes=[
            pltpu.VMEM((9,) + tile.shape, f32),
            pltpu.SemaphoreType.DMA((6,)),
            pltpu.SemaphoreType.DMA((6,)),
        ],
        compiler_params=pltpu.CompilerParams(collective_id=6, has_side_effects=True),
        name="tile_sum",
    )(tile)
    return total[0, 0]


def split_low(values):
    high = values.astype(bf16)
    return high, (values - high.astype(f32)).astype(bf16)


def three_products(left, right, dims=(((1,), (0,)), ((), ()))):
    def product(one, two):
        return lax.dot_general(one, two, dims, preferred_element_type=f32)

    return product(left[0], right[0]) + (product(left[1], right[0]) + product(left[0], right[1]))


def exact_product(left, right, dims=(((1,), (0,)), ((), ()))):
    return lax.dot_general(left, right, dims, precision=highest, preferred_element_type=f32)


def head_marks(width):
    head = lax.broadcasted_iota(jnp.int32, (HEADS, width), 0)
    column = lax.broadcasted_iota(jnp.int32, (HEADS, width), 1)
    return jnp.where(column // HEAD_DIM == head, 1.0, 0.0).astype(f32)


def quarter_marks(padded):
    row = lax.broadcasted_iota(jnp.int32, (padded, V), 0)
    column = lax.broadcasted_iota(jnp.int32, (padded, V), 1)
    return jnp.where(row // 4 == column, 0.25, 0.0).astype(f32)


def tables_kernel(tables_ref, hot_ref, patch_ref, var_ref, keyed_ref, bias_ref):
    padded, width = patch_ref.shape
    query = tables_ref[5 * V + LEADS : 5 * V + LEADS + 1, :]
    patch_ref[...] = jnp.zeros_like(patch_ref)
    patch_ref[: 4 * V, :] = tables_ref[: 4 * V, :]
    chosen = exact_product(hot_ref[...], tables_ref[4 * V : 5 * V, :])
    var_ref[...] = exact_product(quarter_marks(padded), chosen)
    marks = head_marks(width)
    scale = HEAD_DIM**-0.5
    keyed_ref[...] = exact_product(marks, patch_ref[...] * query, NT) * scale
    bias = exact_product(marks, var_ref[...] * query, NT) * (4.0 * scale)
    column = lax.broadcasted_iota(jnp.int32, bias.shape, 1)
    bias_ref[...] = jnp.where(column < 4 * V, bias, -1e30)


def prepare_tables(tables, var_hot):
    padded = 256
    return pl.pallas_call(
        tables_kernel,
        out_shape=(
            jax.ShapeDtypeStruct((padded, D), f32),
            jax.ShapeDtypeStruct((padded, D), f32),
            jax.ShapeDtypeStruct((HEADS, padded), f32),
            jax.ShapeDtypeStruct((HEADS, padded), f32),
        ),
        compiler_params=pltpu.CompilerParams(vmem_limit_bytes=BIG),
        name="prepare_tables",
    )(tables, var_hot)


def four_sum(values):
    size = values.shape[1]
    lane = lax.broadcasted_iota(jnp.int32, values.shape, 1)
    values = values + jnp.where(
        lane % 2 == 0, pltpu.roll(values, size - 1, 1), pltpu.roll(values, 1, 1)
    )
    return values + jnp.where(
        lane % 4 < 2, pltpu.roll(values, size - 2, 1), pltpu.roll(values, 2, 1)
    )


def cell_shares(cells, keyed, bias):
    scores = four_sum(cells * keyed) + bias
    raised = jnp.exp(scores - jnp.max(scores, axis=1, keepdims=True))
    total = jnp.sum(raised, axis=1, keepdims=True) * 0.25
    return raised * (1.0 / total)


def embed_pair(pair, cells, keyed_ref, bias_ref, patch_ref, var_ref, x0_ref):
    patch = split_low(patch_ref[...])
    variable = split_low(var_ref[...])
    outs = []
    for which in range(2):
        row = pl.ds(pair * 2 + which, 1)
        shares = cell_shares(cells, keyed_ref[row, :], bias_ref[row, :])
        outs.append(
            three_products(split_low(shares * cells), patch)
            + three_products(split_low(shares), variable)
        )
    lane = lax.broadcasted_iota(jnp.int32, outs[0].shape, 1)
    columns = pl.ds(pl.multiple_of(pair * 2 * HEAD_DIM, 2 * HEAD_DIM), 2 * HEAD_DIM)
    x0_ref[:, columns] = jnp.where(lane < HEAD_DIM, outs[0], outs[1])


def embed_kernel(
    u_ref, keyed_ref, bias_ref, patch_ref, var_ref, lead_ref, gains_ref, x0_ref, h1_ref
):
    pair = pl.program_id(0)
    embed_pair(pair, u_ref[...], keyed_ref, bias_ref, patch_ref, var_ref, x0_ref)

    @pl.when(pair == pl.num_programs(0) - 1)
    def _():
        x0_ref[...] += lead_ref[...]
        unit, _ = normed_parts(x0_ref[...])
        h1_ref[...] = (unit * gains_ref[0:1, :] + gains_ref[1:2, :]).astype(bf16)


def embed_forward(cells, prepared, lead_row, norm_gains):
    patch, variable, keyed, bias = prepared
    rows, padded = cells.shape
    fixed = lambda shape: pl.BlockSpec(shape, lambda i: (0, 0))
    by_pair = pl.BlockSpec((padded, 2 * HEAD_DIM), lambda i: (0, i))
    return pl.pallas_call(
        embed_kernel,
        grid=(HEADS // 2,),
        out_shape=(
            jax.ShapeDtypeStruct((rows, D), f32),
            jax.ShapeDtypeStruct((rows, D), bf16),
        ),
        in_specs=[
            fixed((rows, padded)),
            fixed(keyed.shape),
            fixed(bias.shape),
            by_pair,
            by_pair,
            fixed((1, D)),
            fixed(norm_gains.shape),
        ],
        out_specs=[fixed((rows, D)), fixed((rows, D))],
        compiler_params=pltpu.CompilerParams(vmem_limit_bytes=BIG),
        cost_estimate=pl.CostEstimate(
            flops=24 * rows * padded * D, bytes_accessed=14 * rows * D, transcendentals=16 * rows * padded
        ),
        name="embed_forward",
    )(cells, keyed, bias, patch, variable, lead_row, norm_gains)


def entry_back_kernel(
    grad_ref, qkv_ref, x0_ref, mid_ref, gains_ref, u_ref, keyed_ref, bias_ref, patch_ref, var_ref,
    du_ref, gain_ref, lead_ref, dpatch_ref, dvar_ref, dkeyed_ref, dbias_ref,
    dx_ref, flip_ref,
):
    pair = pl.program_id(0)

    @pl.when(pair == 0)
    def _():
        row_grad = jnp.dot(grad_ref[...], qkv_ref[...], preferred_element_type=f32)
        unit, inverse = normed_parts(x0_ref[...])
        part, gain_grad, bias_grad = norm_grad(unit, inverse, gains_ref[0:1, :], row_grad)
        total = mid_ref[...] + part
        dx_ref[...] = total
        flip_ref[...] = total.T
        lead_ref[...] = jnp.sum(total, axis=0, keepdims=True)
        gain_ref[0:1, :] = gain_grad
        gain_ref[1:2, :] = bias_grad
        du_ref[...] = jnp.zeros_like(du_ref)

    cells = u_ref[...]
    size = 2 * HEAD_DIM
    columns = pl.ds(pl.multiple_of(pair * size, size), size)
    grads = dx_ref[:, columns]
    lane = lax.broadcasted_iota(jnp.int32, grads.shape, 1)
    patch = split_low(patch_ref[...])
    variable = split_low(var_ref[...])
    cells_grad = None
    for which in range(2):
        row = pl.ds(pair * 2 + which, 1)
        keyed = keyed_ref[row, :]
        shares = cell_shares(cells, keyed, bias_ref[row, :])
        one = split_low(jnp.where(lane // HEAD_DIM == which, grads, 0.0))
        mixed_grad = three_products(one, patch, NT)
        share_grad = mixed_grad * cells + three_products(one, variable, NT)
        weighted = shares * share_grad
        inner = jnp.sum(weighted, axis=1, keepdims=True)
        score_grad = four_sum(weighted) - shares * inner
        piece = mixed_grad * shares + score_grad * keyed
        cells_grad = piece if cells_grad is None else cells_grad + piece
        scale = HEAD_DIM**-0.5
        dkeyed_ref[row, :] = jnp.sum(score_grad * cells, axis=0, keepdims=True) * scale
        dbias_ref[row, :] = jnp.sum(score_grad, axis=0, keepdims=True) * scale
        rows = pl.ds(pl.multiple_of(pair * size + which * HEAD_DIM, HEAD_DIM), HEAD_DIM)
        flipped = split_low(flip_ref[rows, :])
        mine = slice(which * HEAD_DIM, (which + 1) * HEAD_DIM)
        dpatch_ref[mine, :] = three_products(flipped, split_low(shares * cells))
        dvar_ref[mine, :] = three_products(flipped, split_low(shares))
    du_ref[...] += cells_grad


def entry_backward(token_grad, qkv_t, x_first, mid_grad, norm_gains, cells, prepared):
    patch, variable, keyed, bias = prepared
    rows, width = x_first.shape
    padded = cells.shape[1]
    fixed = lambda shape: pl.BlockSpec(shape, lambda i: (0, 0))
    by_pair = pl.BlockSpec((padded, 2 * HEAD_DIM), lambda i: (0, i))
    flipped = pl.BlockSpec((2 * HEAD_DIM, padded), lambda i: (i, 0))
    return pl.pallas_call(
        entry_back_kernel,
        grid=(HEADS // 2,),
        out_shape=(
            jax.ShapeDtypeStruct((rows, padded), f32),
            jax.ShapeDtypeStruct((2, width), f32),
            jax.ShapeDtypeStruct((1, width), f32),
            jax.ShapeDtypeStruct((width, padded), f32),
            jax.ShapeDtypeStruct((width, padded), f32),
            jax.ShapeDtypeStruct(keyed.shape, f32),
            jax.ShapeDtypeStruct(bias.shape, f32),
        ),
        in_specs=[
            fixed(token_grad.shape),
            fixed(qkv_t.shape),
            fixed((rows, width)),
            fixed((rows, width)),
            fixed(norm_gains.shape),
            fixed(cells.shape),
            fixed(keyed.shape),
            fixed(bias.shape),
            by_pair,
            by_pair,
        ],
        out_specs=[
            fixed((rows, padded)),
            fixed((2, width)),
            fixed((1, width)),
            flipped,
            flipped,
            fixed(keyed.shape),
            fixed(bias.shape),
        ],
        scratch_shapes=[pltpu.VMEM((rows, width), f32), pltpu.VMEM((width, rows), f32)],
        compiler_params=pltpu.CompilerParams(vmem_limit_bytes=BIG),
        cost_estimate=pl.CostEstimate(
            flops=60 * rows * padded * D, bytes_accessed=40 * rows * D, transcendentals=16 * rows * padded
        ),
        name="entry_backward",
    )(token_grad, qkv_t, x_first, mid_grad, norm_gains, cells, keyed, bias, patch, variable)


def table_grads_kernel(
    pa_ref, pb_ref, va_ref, vb_ref, ka_ref, kb_ref, ba_ref, bb_ref,
    patch_ref, var_ref, query_ref, hot_ref, lead_hot_ref, lead_ref, gain_ref, head_ref, high_ref, o_ref,
):
    padded, width = patch_ref.shape
    marks = head_marks(width)
    query = query_ref[...]
    keyed_grad = exact_product(ka_ref[...] + kb_ref[...], marks, TN)
    bias_grad = exact_product(ba_ref[...] + bb_ref[...], marks, TN)
    o_ref[...] = jnp.zeros_like(o_ref)
    patch_grad = (pa_ref[...] + pb_ref[...]).T + keyed_grad * query
    o_ref[: 4 * V, :] = patch_grad[: 4 * V, :]
    var_grad = (va_ref[...] + vb_ref[...]).T + bias_grad * query
    var_rows = exact_product(quarter_marks(padded), var_grad, TN)
    o_ref[4 * V : 5 * V, :] = exact_product(hot_ref[...], var_rows, TN)
    lead_rows = exact_product(lead_hot_ref[...], lead_ref[...], TN)
    o_ref[5 * V : 5 * V + LEADS, :] = lead_rows[:LEADS, :]
    query_grad = jnp.sum(
        keyed_grad * patch_ref[...] + bias_grad * var_ref[...], axis=0, keepdims=True
    )
    o_ref[5 * V + LEADS : 5 * V + LEADS + 1, :] = query_grad
    o_ref[5 * V + LEADS + 1 : 5 * V + LEADS + 3, :] = gain_ref[...]
    o_ref[padded : padded + 4 * V, :] = head_ref[...]
    o_ref[padded + 4 * V : padded + 4 * V + 4, :] = high_ref[...]


def table_grads(first, second, prepared, query, var_hot, lead_hots, leads, gain_rows, head, high):
    patch, variable, _, _ = prepared
    operands = []
    for one, two in zip(first, second):
        operands += [one, two]
    return pl.pallas_call(
        table_grads_kernel,
        out_shape=jax.ShapeDtypeStruct((2 * patch.shape[0], D), f32),
        compiler_params=pltpu.CompilerParams(vmem_limit_bytes=BIG),
        name="table_grads",
    )(*operands, patch, variable, query, var_hot, lead_hots, leads, gain_rows, head, high)


def adam_step(master, grad, first, second, rate):
    first_new = beta_first * first + (1.0 - beta_first) * grad
    second_new = beta_second * second + (1.0 - beta_second) * grad * grad
    update = first_new / first_fix / (jnp.sqrt(second_new / second_fix) + adam_eps)
    return (master - rate * (update + decay_rate * master), first_new, second_new)


def by_kind(shard):
    rows = shard.shape[0]
    return shard.reshape(rows, -1, 3, HEAD_DIM).transpose(0, 2, 1, 3).reshape(rows, -1)


def by_head(shard):
    rows = shard.shape[0]
    return shard.reshape(rows, 3, -1, HEAD_DIM).transpose(0, 2, 1, 3).reshape(rows, -1)


lag_one, lag_two, ahead = 2, 4, 3
embed_at, gather_at, project_at, attend_at = 3, 11, 14, 18


def start_kernel(halves, *refs):
    count = len(halves)
    packed_ref, keyed_ref, bias_ref, patch_ref, var_ref, lead_ref, gains_ref = refs[:7]
    shards = refs[7 : 7 + count]
    x0_ref, cells_ref, qkv_ref, o_ref, full_ref, lse_ref, rows_out = refs[7 + count : 14 + count]
    outs = refs[14 + count : 14 + 2 * count]
    (held_ref, h1_ref, rows_ref, weight_ref, vt_ref, send_sem, recv_sem,
     level_send, level_recv, own_sem) = refs[14 + 2 * count :]
    step = pl.program_id(0)
    dp, level, core = mesh_place()
    x = lax.rem(dp, 2)
    columns = {"here": dp, "side": dp + 1 - 2 * x, "down": lax.rem(dp + 2, 4), "far": 3 - dp}
    side = device_of(columns["side"], level, core)
    down = device_of(columns["down"], level, core)
    near = device_of(dp, level, 1 - core)
    across = device_of(level, dp, core)
    middle = lax.rem(level, 3) != 0
    late = level // 2
    sources = (level + 1 - 2 * lax.rem(level, 2), 2 - late, 3 * (1 - late))
    onward = (3 - level, lax.rem(3 * level + 1, 4), lax.rem(3 * level + 1, 4))
    slots = [0]

    def remote(source, target_ref, target):
        slot = slots[0]
        slots[0] += 1
        return pltpu.make_async_remote_copy(
            src_ref=source,
            dst_ref=target_ref,
            send_sem=send_sem.at[slot],
            recv_sem=recv_sem.at[slot],
            device_id=target,
            device_id_type=MESH,
        )

    def place(out, source, column, half, pieces):
        rows = out.shape[1] // 4
        size = rows // pieces
        start = pl.multiple_of(columns[column] * rows + half * size, size)
        return out.at[source * 2 + core, pl.ds(start, size), :]

    def pass_on(out, source, column, target, cut):
        where = place(out, source, column, *cut)
        return remote(where, where, target)

    crossing = remote(packed_ref, held_ref, across)
    staying = pltpu.make_async_copy(packed_ref, held_ref, own_sem.at[count])
    mine = [outs[index].at[level * 2 + core] for index in range(count)]
    given = [remote(shards[index], mine[index], near) for index in range(count)]
    kept = [
        pltpu.make_async_copy(shards[index], mine[index], own_sem.at[index]) for index in range(count)
    ]
    chunks, openings = [], []
    for index in range(count):
        out, pieces = outs[index], halves[index]
        for half in range(pieces):
            group = len(openings)
            full = out.shape[1] // 4
            size = full // pieces
            own = shards[index].at[pl.ds(pl.multiple_of(dp * full + half * size, size), size), :]
            cut = (half, pieces)

            def along(source_ref, source, target_level, slot):
                return pltpu.make_async_remote_copy(
                    src_ref=source_ref,
                    dst_ref=place(out, source, "here", *cut),
                    send_sem=level_send.at[group * 5 + slot],
                    recv_sem=level_recv.at[group * 4 + source],
                    device_id=device_of(dp, target_level, core),
                    device_id_type=MESH,
                )

            openings.append(
                (
                    along(own, level, lax.rem(level + 1, 4), 0),
                    along(own, level, lax.rem(level + 3, 4), 1),
                )
            )
            for turn in range(3):
                source = sources[turn]
                chunks.append(
                    {
                        "level": along(place(out, source, "here", *cut), source, onward[turn], 2 + turn),
                        "side": pass_on(out, source, "here", side, cut),
                        "down": pass_on(out, source, "here", down, cut),
                        "hop_down": pass_on(out, source, "side", down, (2 * half, 2 * pieces)),
                        "hop_side": pass_on(out, source, "down", side, (2 * half + 1, 2 * pieces)),
                        "here_near": pass_on(out, source, "here", near, cut),
                        "side_near": pass_on(out, source, "side", near, cut),
                        "down_near": pass_on(out, source, "down", near, cut),
                        "far_near": pass_on(out, source, "far", near, cut),
                    }
                )
    groups = len(openings)
    order = []
    for number in range(groups + 2):
        for turn in range(3):
            if 0 <= number - turn < groups:
                order.append((number - turn, turn))
    chunks = [chunks[3 * group + turn] for group, turn in order]
    total = len(chunks)

    def start_group(number):
        @pl.when(level < 3)
        def _():
            openings[number][0].start()

        @pl.when(level > 0)
        def _():
            openings[number][1].start()

    rows = h1_ref.shape[0]
    cut = rows // 2

    def rows_of(owner, who, first, size):
        return rows_ref.at[pl.ds(pl.multiple_of((owner * 2 + who) * rows + first, cut), size)]

    def relay(place_ref, target):
        return remote(place_ref, place_ref, target)

    first_half, second_half = h1_ref.at[pl.ds(0, cut)], h1_ref.at[pl.ds(cut, cut)]
    beside, below, far = columns["side"], columns["down"], columns["far"]
    side_a = remote(first_half, rows_of(dp, core, 0, cut), side)
    down_b = remote(second_half, rows_of(dp, core, cut, cut), down)
    side_b = remote(second_half, rows_of(dp, core, cut, cut), side)
    down_a = remote(first_half, rows_of(dp, core, 0, cut), down)
    near_own = remote(h1_ref, rows_of(dp, core, 0, rows), near)
    far_a = relay(rows_of(beside, core, 0, cut), down)
    far_b = relay(rows_of(below, core, cut, cut), side)
    near_side = relay(rows_of(beside, core, 0, rows), near)
    near_down = relay(rows_of(below, core, 0, rows), near)
    near_far = relay(rows_of(far, core, 0, rows), near)
    weight = pltpu.make_async_copy(outs[0].at[dp * 2 + core], weight_ref, own_sem.at[count + 1])
    save = pltpu.make_async_copy(rows_ref, rows_out, own_sem.at[count + 2])

    @pl.when(step == 0)
    def _():
        barrier = pltpu.get_barrier_semaphore()
        deep = [device_of(dp, lax.rem(level + move, 4), core) for move in (1, 2, 3)]
        for target in (side, down, near, *deep):
            pl.semaphore_signal(barrier, inc=1, device_id=target, device_id_type=MESH)

        @pl.when(dp != level)
        def _():
            pl.semaphore_signal(barrier, inc=1, device_id=across, device_id_type=MESH)
            pl.semaphore_wait(barrier, 7)
            crossing.start()

        @pl.when(dp == level)
        def _():
            pl.semaphore_wait(barrier, 6)
            staying.start()

        for number in range(ahead):
            start_group(number)
        for copy in (*given, *kept):
            copy.start()

    for number in range(total + lag_two):

        @pl.when(step == number)
        def _(number=number):
            if number < total:
                chunk = chunks[number]
                chunk["level"].wait_recv()

                @pl.when(middle)
                def _():
                    chunk["level"].start()

                chunk["side"].start()
                chunk["down"].start()
                chunk["here_near"].start()
                group, turn = order[number]
                if turn == 0 and group + ahead < groups:
                    start_group(group + ahead)
            if 0 <= number - lag_one < total:
                chunk = chunks[number - lag_one]
                chunk["side"].wait_recv()
                chunk["hop_down"].start()
                chunk["down"].wait_recv()
                chunk["hop_side"].start()
                chunk["side_near"].start()
                chunk["down_near"].start()
            if 0 <= number - lag_two < total:
                chunk = chunks[number - lag_two]
                chunk["hop_down"].wait_recv()
                chunk["hop_side"].wait_recv()
                chunk["far_near"].start()

    @pl.when(step == embed_at)
    def _():
        @pl.when(dp != level)
        def _():
            crossing.wait_recv()

        @pl.when(dp == level)
        def _():
            staying.wait()

        cells_ref[...] = held_ref[...]

    @pl.when((step >= embed_at) & (step < embed_at + HEADS // 2))
    def _():
        embed_pair(step - embed_at, held_ref[...], keyed_ref, bias_ref, patch_ref, var_ref, x0_ref)

    @pl.when(step == gather_at)
    def _():
        lead = held_ref[0:1, 4 * V + 4 : 4 * V + 5]
        row = lax.broadcasted_iota(jnp.int32, (1, 8), 1).astype(f32)
        lead_hot = jnp.where(row == lead, 1.0, 0.0).astype(f32)
        x0_ref[...] += exact_product(lead_hot, lead_ref[...])
        unit, _ = normed_parts(x0_ref[...])
        h1_ref[...] = (unit * gains_ref[0:1, :] + gains_ref[1:2, :]).astype(bf16)
        for copy in (side_a, down_b, side_b, down_a, near_own):
            copy.start()
        rows_of(dp, core, 0, rows)[...] = h1_ref[...]
        kept[0].wait()
        weight.start()

    @pl.when(step == gather_at + 1)
    def _():
        side_a.wait_recv()
        far_a.start()
        down_b.wait_recv()
        far_b.start()
        side_b.wait_recv()
        near_side.start()
        down_a.wait_recv()
        near_down.start()

    @pl.when(step == gather_at + 2)
    def _():
        far_a.wait_recv()
        far_b.wait_recv()
        near_far.start()
        for copy in (near_own, near_side, near_down):
            copy.wait_recv()

    block = rows_ref.shape[0] // 4

    @pl.when(step == project_at)
    def _():
        near_far.wait_recv()
        save.start()
        weight.wait()

    @pl.when((step >= project_at) & (step < project_at + 4))
    def _():
        where = pl.ds(pl.multiple_of((step - project_at) * block, block), block)
        qkv_ref[where, :] = lax.dot_general(
            rows_ref[where, :], weight_ref[...], NT, preferred_element_type=f32
        ).astype(bf16)

    width = o_ref.shape[1]
    heads = width // HEAD_DIM

    @pl.when(step == attend_at)
    def _():
        vt_ref[...] = qkv_ref[:, 2 * width :].T

    @pl.when((step >= attend_at) & (step < attend_at + 4))
    def _():
        where = pl.ds(pl.multiple_of((step - attend_at) * block, block), block)
        full, sums = attend_rows(
            heads, qkv_ref[where, :width], qkv_ref.at[:, width : 2 * width], vt_ref
        )
        for head in range(heads):
            lse_ref[head : head + 1, where] = sums[head]
        full_ref[where, :] = full
        o_ref[where, :] = full.astype(bf16)

    @pl.when(step == total + lag_two - 1)
    def _():
        for copy in given:
            copy.wait()
        for copy in kept[1:]:
            copy.wait()
        for number in range(groups):

            @pl.when(level < 3)
            def _(number=number):
                openings[number][0].wait_send()

            @pl.when(level > 0)
            def _(number=number):
                openings[number][1].wait_send()

        for chunk in chunks:
            for name in ("here_near", "side_near", "down_near", "far_near"):
                chunk[name].wait_recv()
            for name, copy in chunk.items():
                if name != "level":
                    copy.wait_send()

            @pl.when(middle)
            def _(chunk=chunk):
                chunk["level"].wait_send()

        for copy in (side_a, down_b, side_b, down_a, near_own, far_a, far_b, near_side, near_down, near_far):
            copy.wait_send()
        save.wait()

        @pl.when(dp != level)
        def _():
            crossing.wait_send()


def start_program(packed, prepared, lead_table, norm_gains, shards, halves):
    patch, variable, keyed, bias = prepared
    count = len(shards)
    groups = sum(halves)
    copies = groups * 24 + count + 11
    rows, padded = packed.shape
    total = 8 * rows
    width = shards[0].shape[0] // 3
    heads = width // HEAD_DIM
    anywhere = pl.BlockSpec(memory_space=pl.ANY)
    fixed = lambda shape: pl.BlockSpec(shape, lambda i: (0, 0))
    by_pair = pl.BlockSpec(
        (padded, 2 * HEAD_DIM), lambda i: (0, jnp.clip(i - embed_at, 0, HEADS // 2 - 1))
    )
    shapes = [
        ((rows, D), f32),
        (packed.shape, f32),
        ((total, 3 * width), bf16),
        ((total, width), bf16),
        ((total, width), f32),
        ((heads, total), f32),
    ]
    return pl.pallas_call(
        partial(start_kernel, halves),
        grid=(groups * 3 + lag_two,),
        out_shape=[jax.ShapeDtypeStruct(shape, kind) for shape, kind in shapes]
        + [jax.ShapeDtypeStruct((total, D), bf16)]
        + [jax.ShapeDtypeStruct((8,) + shard.shape, bf16) for shard in shards],
        in_specs=[anywhere]
        + [fixed(keyed.shape), fixed(bias.shape), by_pair, by_pair]
        + [fixed(lead_table.shape), fixed(norm_gains.shape)]
        + [fixed(shard.shape) for shard in shards],
        out_specs=[fixed(shape) for shape, _ in shapes] + [anywhere] * (count + 1),
        scratch_shapes=[
            pltpu.VMEM(packed.shape, f32),
            pltpu.VMEM((rows, D), bf16),
            pltpu.VMEM((total, D), bf16),
            pltpu.VMEM(shards[0].shape, bf16),
            pltpu.VMEM((width, total), bf16),
            pltpu.SemaphoreType.DMA((copies,)),
            pltpu.SemaphoreType.DMA((copies,)),
            pltpu.SemaphoreType.DMA((groups * 5,)),
            pltpu.SemaphoreType.DMA((groups * 4,)),
            pltpu.SemaphoreType.DMA((count + 3,)),
        ],
        compiler_params=pltpu.CompilerParams(
            collective_id=7, has_side_effects=True, vmem_limit_bytes=BIG
        ),
        name="start_program",
    )(packed, keyed, bias, patch, variable, lead_table, norm_gains, *shards)


def own_qkv_share(crossed, grad):
    dp = lax.axis_size("dp")
    rows = grad.shape[0] // dp
    if not crossed:
        return lax.psum_scatter(grad, "dp", scatter_dimension=0, tiled=True)
    _, level, _ = mesh_place()
    return cross(crossed, sum_levels(grad.reshape((dp, rows) + grad.shape[1:]), level))


def shards(
    crossed,
    fields,
    targets,
    land_mask,
    lead_index,
    var_ids,
    tables,
    norm_gains,
    tables_first,
    tables_second,
    gains_first,
    gains_second,
    w_qkv,
    qkv_first,
    qkv_second,
    w_out,
    out_first,
    out_second,
    w_up,
    up_first,
    up_second,
    w_down,
    down_first,
    down_second,
    qkv_average,
):
    local_samples, shard_rows, _ = fields.shape
    dp_size, parts = lax.axis_size("dp"), lax.axis_size("mp")
    dp_index = lax.axis_index("dp")
    place, level, core = mesh_place()
    part = place * 2 + core if crossed else lax.axis_index("mp")
    share_rows = D // dp_size

    def own_share(full, dim):
        return lax.dynamic_slice_in_dim(full, dp_index * share_rows, share_rows, dim)

    masters = (own_share(w_qkv, 0), own_share(w_out, 1), own_share(w_up, 0), own_share(w_down, 1))
    var_hot = (var_ids[:, None] == jnp.arange(V, dtype=jnp.int32)[None, :]).astype(f32)
    prepared = prepare_tables(tables, var_hot)
    low = lambda master: master.astype(bf16)
    qkv_low = by_kind(low(w_qkv))
    packed = jnp.concatenate(
        (
            fields[0],
            land_mask[0].astype(f32),
            jnp.broadcast_to(lead_index.astype(f32), (shard_rows, 2)),
            jnp.zeros((shard_rows, 64 - 6), f32),
        ),
        axis=1,
    )
    if crossed:
        (
            x_first, cells, packed, own_out, full, logsum, rows_one, qkv_t, w_outs, w_ups, w_downs
        ) = start_program(
            packed, prepared, tables[5 * V : 5 * V + 8], norm_gains,
            (qkv_low.T, low(w_out), low(w_up), low(w_down)), (1, 1, 2, 2),
        )
        later_targets, own_out = tie(targets[0], own_out)
        answers = cross(crossed, later_targets)
    else:
        cells = packed
        answers = targets[0]
        w_outs, w_ups, w_downs, qkv_t = [
            lax.all_gather(shard, "mp")
            for shard in (low(w_out), low(w_up), low(w_down), qkv_low.T)
        ]
    gathered = (w_outs.reshape(D, D), w_ups, w_downs.reshape(-1, D), qkv_t.reshape(3 * D, D))
    qkv_local = choose(qkv_t, part)
    leads = cells[0, 4 * V + 4 : 4 * V + 6].astype(jnp.int32)
    ocean = 1.0 - cells[:, 4 * V : 4 * V + 4]
    count = sum_everywhere(crossed, jnp.sum(ocean))
    denom = 2.0 * V * jnp.maximum(count, 1.0)
    first_row = part * shard_rows
    patch_row = (first_row + jnp.arange(shard_rows, dtype=jnp.int32)) // PATCH_COLS
    row_hot = (patch_row[:, None] == jnp.arange(PATCH_ROWS, dtype=jnp.int32)[None, :]).astype(f32)
    lat_rows = jnp.dot(
        row_hot, lat_weights(2 * PATCH_ROWS).reshape(PATCH_ROWS, 2), precision=highest
    )
    lat_pixels = jnp.broadcast_to(lat_rows[:, :, None], (shard_rows, 2, 2)).reshape(shard_rows, 4)
    weighted = jnp.tile(ocean * lat_pixels, (1, V))
    head = tables[5 * V + LEADS + 1 :]
    loss_part = f32(0.0)
    records = []
    for rollout in range(2):
        if rollout == 1:
            cells = jnp.pad(guess, ((0, 0), (0, 64)))
        if rollout == 1 or not crossed:
            lead_row = lax.dynamic_slice_in_dim(tables, 5 * V + leads[rollout], 1, 0)
            x_first, normed = embed_forward(cells, prepared, lead_row, norm_gains)
            rows_one = spread_rows(crossed, normed)
            packed = lax.dot_general(
                rows_one, qkv_local, NT, preferred_element_type=f32
            ).astype(bf16)
            own_out, full, logsum = attend(packed)
        attended = exchange(crossed, own_out, True, 2)
        x_mid, rows_two, hidden, active, x_last, guess = branch_forward(
            attended, x_first, norm_gains, gathered, head
        )
        miss = guess - answers[rollout]
        loss_part = loss_part + jnp.sum(weighted * miss * miss)
        records.append(
            (cells, x_first, rows_one, packed, full, logsum, attended, x_mid, rows_two,
             hidden, active, x_last, 2.0 * weighted * miss / denom)
        )
    carried = jnp.zeros_like(guess)
    head_total = jnp.zeros_like(head)
    gain_high = jnp.zeros((4, D), f32)
    gain_low = jnp.zeros((2, D), f32)
    table_parts, lead_sums = [], []
    qkv_grad = jnp.zeros((D, qkv_local.shape[0]), f32)
    kept = []

    def sources(index, other, blocked):
        listed = []
        for step in kept:
            listed += [(step[index], blocked), (step[other], not blocked)]
        return listed

    for rollout in (1, 0):
        (cells, x_first, rows_one, packed, full, logsum, attended, x_mid, rows_two,
         hidden, active, x_last, loss_grad) = records[rollout]
        last_low, hidden_grad, mid_grad, mid_low, out_grad, gain_part, head_grad = branch_backward(
            loss_grad + carried, x_last, x_mid, norm_gains, hidden, gathered, head
        )
        head_total = head_total + head_grad
        gain_high = gain_high + gain_part[2:]
        kept.append((attended, rows_two, active, mid_low, hidden_grad, last_low))
        last_turn = crossed and rollout == 0
        if last_turn:
            listed = (
                (sources(2, 5, True), down_pieces, 256),
                (sources(1, 4, False) + sources(0, 3, True), up_out_pieces, 320),
            )
            x, y = lax.rem(place, 2), place // 2
            where = lambda which: jnp.stack((which, x, y)).astype(jnp.int32)
            others = [outer_half(*group, where(1 - core), None) for group in listed]
            out_grad, *others = tie(out_grad, *others)
            others = [shift(other, to_core) for other in others]
        own_grad = exchange(crossed, out_grad, False, 3)
        if last_turn:
            halves = []
            for group, other in zip(listed, others):
                halves += outer_half(*group, where(core), other)
            own_grad, *halves = tie(own_grad, *halves)
            sums = [first_sums(*halves[:2]), first_sums(*halves[2:])]
        packed_grad = attend_back(own_grad, packed, full, logsum)
        if last_turn:
            packed_grad, *sums[0] = tie(packed_grad, *sums[0])
            down_pieces_sum = second_sums(*sums[0], x, y)
        token_grad = exchange(crossed, packed_grad, True, 4)
        if last_turn:
            token_grad, *sums[1] = tie(token_grad, *sums[1])
            up_out_sum = second_sums(*sums[1], x, y)
        qkv_grad = qkv_grad + lax.dot_general(
            rows_one, packed_grad, TN, preferred_element_type=f32
        )
        cells_grad, gain_one, lead_sum, *table_part = entry_backward(
            token_grad, gathered[3], x_first, mid_grad, norm_gains, cells, prepared
        )
        carried = cells_grad[:, : 4 * V]
        gain_low = gain_low + gain_one
        table_parts.append(table_part)
        lead_sums.append(lead_sum)

    def pair(index):
        return (kept[0][index], kept[1][index])

    if crossed:
        down_share = tall_piece(sum_levels(down_pieces_sum, level))
        up_out = sum_levels(up_out_sum, level)
        up_share = up_out[:256]
        out_share = tall_piece(up_out[256:])
    else:
        down_share = outer_plain(pair(2), pair(5), False)
        up_share = outer_plain(pair(1), pair(4), True)
        out_share = outer_plain(pair(0), pair(3), False)
    shares = (by_head(own_qkv_share(crossed, qkv_grad)), out_share, up_share, down_share)
    share_square = sum(jnp.sum(share * share) for share in shares)
    lead_hots = (leads[:, None] == jnp.arange(8, dtype=jnp.int32)[None, :]).astype(f32)
    lead_hots = jnp.pad(lead_hots, ((0, 6), (0, 0)))
    lead_rows = jnp.pad(jnp.concatenate((lead_sums[1], lead_sums[0])), ((0, 6), (0, 0)))
    query = tables[5 * V + LEADS : 5 * V + LEADS + 1]
    last_rows = table_grads(
        *table_parts, prepared, query, var_hot, lead_hots, lead_rows, gain_low, head_total, gain_high
    )
    if crossed:
        row = jnp.arange(8, dtype=jnp.int32)[:, None]
        tile = jnp.where(row == 0, share_square, jnp.where(row == 1, loss_part, 0.0))
        last_sum, tile_sum = exchange_sum(last_rows, jnp.broadcast_to(tile, (8, 128)))
        square_sum, loss_sum = tile_sum[0, 0], tile_sum[1, 0]
    else:
        last_sum, loss_sum, square_sum = lax.psum(
            (last_rows, loss_part, share_square), ("dp", "mp")
        )
        square_sum = square_sum + jnp.sum(last_sum * last_sum)
    head_sum = last_sum[256:]
    embed_rows = 5 * V + LEADS + 1
    table_sum = jnp.concatenate((last_sum[:embed_rows], head_sum[: 4 * V]))
    gain_sum = jnp.concatenate((last_sum[embed_rows : embed_rows + 2], head_sum[4 * V : 4 * V + 4]))
    grad_norm = jnp.sqrt(square_sum)
    factor = jnp.minimum(1.0, clip_norm / (grad_norm + 1e-06))
    tab = adam_step(tables, factor * table_sum, tables_first, tables_second, lr_table)
    gai = adam_step(norm_gains, factor * gain_sum, gains_first, gains_second, lr_gain)
    qkv = adam_step(masters[0], factor * shares[0], qkv_first, qkv_second, lr_matrix)
    outp = adam_step(masters[1], factor * shares[1], out_first, out_second, lr_matrix)
    upp = adam_step(masters[2], factor * shares[2], up_first, up_second, lr_matrix)
    down = adam_step(masters[3], factor * shares[3], down_first, down_second, lr_matrix)
    average = average_keep * qkv_average + (1.0 - average_keep) * qkv[0]
    return (
        loss_sum / denom,
        grad_norm,
        tab[0],
        tab[1],
        tab[2],
        gai[0],
        gai[1],
        gai[2],
        qkv[0],
        qkv[1],
        qkv[2],
        outp[0],
        outp[1],
        outp[2],
        upp[0],
        upp[1],
        upp[2],
        down[0],
        down[1],
        down[2],
        average,
    )


def solution(mesh):
    return jax.shard_map(
        partial(shards, is_crossed(mesh.shape)),
        mesh=mesh,
        in_specs=(
            P("dp", "mp", None),
            P("dp", None, "mp", None),
            P("dp", "mp", None),
            P("dp", None),
            P(),
            P(),
            P(),
            P(),
            P(),
            P(),
            P(),
            P(None, "mp"),
            P("dp", "mp"),
            P("dp", "mp"),
            P("mp", None),
            P("mp", "dp"),
            P("mp", "dp"),
            P(None, "mp"),
            P("dp", "mp"),
            P("dp", "mp"),
            P("mp", None),
            P("mp", "dp"),
            P("mp", "dp"),
            P("dp", "mp"),
        ),
        out_specs=(
            P(),
            P(),
            P(),
            P(),
            P(),
            P(),
            P(),
            P(),
            P("dp", "mp"),
            P("dp", "mp"),
            P("dp", "mp"),
            P("mp", "dp"),
            P("mp", "dp"),
            P("mp", "dp"),
            P("dp", "mp"),
            P("dp", "mp"),
            P("dp", "mp"),
            P("mp", "dp"),
            P("mp", "dp"),
            P("mp", "dp"),
            P("dp", "mp"),
        ),
        check_vma=False,
    )
```

```python
from functools import partial
import math

import jax
import jax.numpy as jnp
from jax import lax
from jax.experimental import pallas as pl
from jax.experimental.pallas import tpu as pltpu
from jax.sharding import PartitionSpec as P

D = 1024
HEADS = 16
HEAD_DIM = 64
V = 48
PATCH_ROWS = 32
PATCH_COLS = 64
LEADS = 7


highest = lax.Precision.HIGHEST
eps_norm = 1e-05
clip_norm = 0.05
beta_first = 0.9
beta_second = 0.999
adam_eps = 1e-08
decay_rate = 0.1
lr_matrix = 0.04
lr_table = 0.1
lr_gain = 0.3
average_keep = 0.9
first_fix = 1.0 - 0.9**10
second_fix = 1.0 - 0.999**10


def layer_norm(values, gain, bias):
    center = values - jnp.mean(values, axis=-1, keepdims=True)
    spread = jnp.mean(center * center, axis=-1, keepdims=True)
    return center * lax.rsqrt(spread + eps_norm) * gain + bias


def lat_weights(pixel_rows):
    row_index = jnp.arange(pixel_rows, dtype=jnp.float32)
    cosine = jnp.cos(((row_index + 0.5) / pixel_rows - 0.5) * math.pi)
    return cosine / jnp.mean(cosine)


bf16 = jnp.bfloat16
f32 = jnp.float32
MESH = pl.DeviceIdType.MESH
NT = (((1,), (1,)), ((), ()))
TN = (((0,), (0,)), ((), ()))
VMEM = pl.BlockSpec(memory_space=pltpu.VMEM)
BIG = 56 * 2**20


def is_crossed(sizes):
    return sizes["dp"] == 4 and sizes["mp"] == 8


def mesh_place():
    dp = lax.axis_index("dp")
    mp = lax.axis_index("mp")
    return dp, mp // 2, lax.rem(mp, 2)


def device_of(dp, level, core):
    return {"dp": dp, "mp": level * 2 + core}


def cross_pairs():
    groups = lax.axis_size("dp")
    pairs = []
    for dp in range(groups):
        for level in range(groups):
            for core in range(2):
                source = (dp * groups + level) * 2 + core
                target = (level * groups + dp) * 2 + core
                pairs.append((source, target))
    return pairs


def cross(crossed, value):
    if not crossed:
        return value
    return lax.ppermute(value, ("dp", "mp"), cross_pairs())


def gather_kernel(x_ref, o_ref, send_sem, recv_sem):
    rows = x_ref.shape[0]
    half = rows // 2
    dp, level, core = mesh_place()
    side = dp + 1 - 2 * lax.rem(dp, 2)
    down = lax.rem(dp + 2, 4)
    far = 3 - dp
    to_side = device_of(side, level, core)
    to_down = device_of(down, level, core)
    to_core = device_of(dp, level, 1 - core)

    def rows_of(owner, who, first, size):
        return pl.ds(pl.multiple_of((owner * 2 + who) * rows + first, half), size)

    barrier = pltpu.get_barrier_semaphore()
    for target in (to_side, to_down, to_core):
        pl.semaphore_signal(barrier, inc=1, device_id=target, device_id_type=MESH)
    pl.semaphore_wait(barrier, 3)

    def send(slot, source, where, target):
        copy = pltpu.make_async_remote_copy(
            src_ref=source,
            dst_ref=o_ref.at[where],
            send_sem=send_sem.at[slot],
            recv_sem=recv_sem.at[slot],
            device_id=target,
            device_id_type=MESH,
        )
        copy.start()
        return copy

    first = x_ref.at[pl.ds(0, half)]
    second = x_ref.at[pl.ds(half, half)]
    side_a = send(0, first, rows_of(dp, core, 0, half), to_side)
    down_b = send(1, second, rows_of(dp, core, half, half), to_down)
    side_b = send(2, second, rows_of(dp, core, half, half), to_side)
    down_a = send(3, first, rows_of(dp, core, 0, half), to_down)
    near = send(4, x_ref, rows_of(dp, core, 0, rows), to_core)
    o_ref[rows_of(dp, core, 0, rows)] = x_ref[...]
    side_a.wait_recv()
    place = rows_of(side, core, 0, half)
    far_a = send(5, o_ref.at[place], place, to_down)
    down_b.wait_recv()
    place = rows_of(down, core, half, half)
    far_b = send(6, o_ref.at[place], place, to_side)
    side_b.wait_recv()
    place = rows_of(side, core, 0, rows)
    near_side = send(7, o_ref.at[place], place, to_core)
    down_a.wait_recv()
    place = rows_of(down, core, 0, rows)
    near_down = send(8, o_ref.at[place], place, to_core)
    far_a.wait_recv()
    far_b.wait_recv()
    place = rows_of(far, core, 0, rows)
    near_far = send(9, o_ref.at[place], place, to_core)
    for copy in (near, near_side, near_down, near_far):
        copy.wait_recv()
    for copy in (side_a, down_b, side_b, down_a, near, far_a, far_b, near_side, near_down, near_far):
        copy.wait_send()


def spread_rows(crossed, normed):
    if not crossed:
        return lax.all_gather(normed, "mp", axis=0, tiled=True)
    rows, width = normed.shape
    return pl.pallas_call(
        gather_kernel,
        out_shape=jax.ShapeDtypeStruct((8 * rows, width), normed.dtype),
        in_specs=[VMEM],
        out_specs=VMEM,
        scratch_shapes=[pltpu.SemaphoreType.DMA((10,)), pltpu.SemaphoreType.DMA((10,))],
        compiler_params=pltpu.CompilerParams(
            collective_id=1, has_side_effects=True, vmem_limit_bytes=BIG
        ),
        name="gather_rows",
    )(normed)


def exchange_kernel(to_columns, rows, width, x_ref, o_ref, send_sem, recv_sem):
    dp, level, core = mesh_place()
    me = dp * 2 + core
    barrier = pltpu.get_barrier_semaphore()
    others = []
    for step in (7, 6, 5, 4, 3, 2, 1):
        part = lax.rem(me + step, 8)
        others.append((step, part, device_of(part // 2, level, lax.rem(part, 2))))
    for step, part, target in others:
        pl.semaphore_signal(barrier, inc=1, device_id=target, device_id_type=MESH)
    pl.semaphore_wait(barrier, 7)

    def row_block(ref, part):
        return ref.at[pl.ds(pl.multiple_of(part * rows, rows), rows), :]

    def column_block(ref, part):
        return ref.at[:, pl.ds(pl.multiple_of(part * width, width), width)]

    source_block, target_block = (
        (row_block, column_block) if to_columns else (column_block, row_block)
    )
    copies = []
    for step, part, target in others:
        copy = pltpu.make_async_remote_copy(
            src_ref=source_block(x_ref, part),
            dst_ref=target_block(o_ref, me),
            send_sem=send_sem.at[step],
            recv_sem=recv_sem.at[step],
            device_id=target,
            device_id_type=MESH,
        )
        copy.start()
        copies.append(copy)
    target_block(o_ref, me)[...] = source_block(x_ref, me)[...]
    for copy in copies:
        copy.wait()


def exchange(crossed, value, to_columns, number):
    parts = lax.axis_size("mp")
    if to_columns:
        rows, width = value.shape[0] // parts, value.shape[1]
        shape = (rows, width * parts)
    else:
        rows, width = value.shape[0], value.shape[1] // parts
        shape = (rows * parts, width)
    if not crossed:
        split, joined = (0, 1) if to_columns else (1, 0)
        return lax.all_to_all(value, "mp", split_axis=split, concat_axis=joined, tiled=True)
    return pl.pallas_call(
        partial(exchange_kernel, to_columns, rows, width),
        out_shape=jax.ShapeDtypeStruct(shape, value.dtype),
        in_specs=[VMEM],
        out_specs=VMEM,
        scratch_shapes=[pltpu.SemaphoreType.DMA((8,)), pltpu.SemaphoreType.DMA((8,))],
        compiler_params=pltpu.CompilerParams(
            collective_id=number, has_side_effects=True, vmem_limit_bytes=BIG
        ),
        name="exchange_parts",
    )(value)


def pick_head(value, head, heads):
    if heads == 1:
        return value
    lane = lax.broadcasted_iota(jnp.int32, value.shape, 1) // HEAD_DIM
    return jnp.where(lane == head, value, jnp.zeros_like(value))


def attend_rows(heads, queries, k_ref, vt_ref):
    queries = queries * bf16(HEAD_DIM**-0.5)
    keys = k_ref[...]
    outs, sums = [], []
    for head in range(heads):
        scores = lax.dot_general(
            keys, pick_head(queries, head, heads), NT, preferred_element_type=f32
        )
        largest = jnp.max(scores, axis=0, keepdims=True)
        raised = jnp.exp(scores - largest)
        total = jnp.sum(raised, axis=0, keepdims=True)
        probs = (raised * (1.0 / total)).astype(bf16)
        values = vt_ref[head * HEAD_DIM : (head + 1) * HEAD_DIM, :]
        outs.append(jnp.dot(values, probs, preferred_element_type=f32))
        sums.append(largest + jnp.log(total))
    flipped = outs[0] if heads == 1 else jnp.concatenate(outs, axis=0)
    return flipped.T, sums


def attend_kernel(heads, q_ref, k_ref, v_ref, o_ref, full_ref, lse_ref, vt_ref):
    @pl.when(pl.program_id(0) == 0)
    def _():
        vt_ref[...] = v_ref[...].T

    full, sums = attend_rows(heads, q_ref[...], k_ref, vt_ref)
    for head in range(heads):
        lse_ref[head : head + 1, :] = sums[head]
    full_ref[...] = full
    o_ref[...] = full.astype(bf16)


def attend(packed):
    total, width = packed.shape[0], packed.shape[1] // 3
    heads = width // HEAD_DIM
    block = min(512, total)
    row_block = pl.BlockSpec((block, width), lambda i: (i, 0))
    return pl.pallas_call(
        partial(attend_kernel, heads),
        grid=(total // block,),
        out_shape=(
            jax.ShapeDtypeStruct((total, width), bf16),
            jax.ShapeDtypeStruct((total, width), f32),
            jax.ShapeDtypeStruct((heads, total), f32),
        ),
        in_specs=[
            row_block,
            pl.BlockSpec((total, width), lambda i: (0, 0)),
            pl.BlockSpec((total, width), lambda i: (0, 0)),
        ],
        out_specs=[row_block, row_block, pl.BlockSpec((heads, block), lambda i: (0, i))],
        scratch_shapes=[pltpu.VMEM((width, total), bf16)],
        compiler_params=pltpu.CompilerParams(vmem_limit_bytes=BIG),
        cost_estimate=pl.CostEstimate(
            flops=16 * total * total * width,
            bytes_accessed=10 * total * width,
            transcendentals=heads * total * total,
        ),
        name="attend",
    )(packed[:, :width], packed[:, width : 2 * width], packed[:, 2 * width :])


def attend_back_kernel(
    heads, q_ref, do_ref, full_ref, lse_ref, k_ref, v_ref, dq_ref, dk_ref, dv_ref, kt_ref, dk_sum, dv_sum
):
    step = pl.program_id(0)
    total = k_ref.shape[0]
    chunk = min(1024, total)

    @pl.when(step == 0)
    def _():
        kt_ref[...] = k_ref[...].T
        dk_sum[...] = jnp.zeros_like(dk_sum)
        dv_sum[...] = jnp.zeros_like(dv_sum)

    scale = HEAD_DIM**-0.5
    queries = q_ref[...]
    grads = do_ref[...]
    products = (grads.astype(f32) * full_ref[...]).T
    query_heads = [pick_head(queries, head, heads) for head in range(heads)]
    grad_heads = [pick_head(grads, head, heads) for head in range(heads)]
    inner = [
        jnp.sum(products[head * HEAD_DIM : (head + 1) * HEAD_DIM], axis=0, keepdims=True) * scale
        for head in range(heads)
    ]
    query_grads = [None] * heads
    for start in range(0, total, chunk):
        rows = slice(start, start + chunk)
        keys = k_ref[rows, :]
        values = v_ref[rows, :]
        value_part = None
        key_part = None
        for head in range(heads):
            scores = lax.dot_general(
                keys, query_heads[head] * bf16(scale), NT, preferred_element_type=f32
            )
            probs = jnp.exp(scores - lse_ref[head : head + 1, :])
            prob_grad = lax.dot_general(
                values, grad_heads[head] * bf16(scale), NT, preferred_element_type=f32
            )
            score_grad = (probs * (prob_grad - inner[head])).astype(bf16)
            one = jnp.dot(probs.astype(bf16), grad_heads[head], preferred_element_type=f32)
            two = jnp.dot(score_grad, query_heads[head], preferred_element_type=f32)
            value_part = one if value_part is None else value_part + one
            key_part = two if key_part is None else key_part + two
            three = jnp.dot(
                kt_ref[head * HEAD_DIM : (head + 1) * HEAD_DIM, rows],
                score_grad,
                preferred_element_type=f32,
            )
            query_grads[head] = three if query_grads[head] is None else query_grads[head] + three
        dv_sum[rows, :] += value_part
        dk_sum[rows, :] += key_part
    flipped = query_grads[0] if heads == 1 else jnp.concatenate(query_grads, axis=0)
    dq_ref[...] = flipped.T.astype(bf16)

    @pl.when(step == pl.num_programs(0) - 1)
    def _():
        dk_ref[...] = dk_sum[...].astype(bf16)
        dv_ref[...] = dv_sum[...].astype(bf16)


def attend_back(grad_out, packed, full, logsum):
    total, width = grad_out.shape
    heads = width // HEAD_DIM
    block = min(256, total)
    row_block = pl.BlockSpec((block, width), lambda i: (i, 0))
    whole = pl.BlockSpec((total, width), lambda i: (0, 0))
    query_grad, key_grad, value_grad = pl.pallas_call(
        partial(attend_back_kernel, heads),
        grid=(total // block,),
        out_shape=(jax.ShapeDtypeStruct((total, width), bf16),) * 3,
        in_specs=[
            row_block,
            row_block,
            row_block,
            pl.BlockSpec((heads, block), lambda i: (0, i)),
            whole,
            whole,
        ],
        out_specs=[row_block, whole, whole],
        scratch_shapes=[
            pltpu.VMEM((width, total), bf16),
            pltpu.VMEM((total, width), f32),
            pltpu.VMEM((total, width), f32),
        ],
        compiler_params=pltpu.CompilerParams(vmem_limit_bytes=BIG),
        cost_estimate=pl.CostEstimate(
            flops=40 * total * total * width,
            bytes_accessed=16 * total * width,
            transcendentals=heads * total * total,
        ),
        name="attend_back",
    )(
        packed[:, :width],
        grad_out,
        full,
        logsum,
        packed[:, width : 2 * width],
        packed[:, 2 * width :],
    )
    return jnp.concatenate((query_grad, key_grad, value_grad), axis=1)


def normed_parts(values):
    center = values - jnp.mean(values, axis=-1, keepdims=True)
    spread = jnp.mean(center * center, axis=-1, keepdims=True)
    inverse = lax.rsqrt(spread + eps_norm)
    return center * inverse, inverse


def norm_grad(unit, inverse, gain, grad):
    scaled = grad * gain
    middle = jnp.mean(scaled, axis=-1, keepdims=True)
    along = jnp.mean(scaled * unit, axis=-1, keepdims=True)
    gain_grad = jnp.sum(grad * unit, axis=0, keepdims=True)
    bias_grad = jnp.sum(grad, axis=0, keepdims=True)
    return inverse * (scaled - middle - unit * along), gain_grad, bias_grad


def gauss_share(values):
    return 0.5 * (1.0 + lax.erf(values * (0.5**0.5)))


def branch_kernel(
    o_ref, x0_ref, gains_ref, out_ref, up_ref, down_ref, head_ref,
    x1_ref, h2_ref, g_ref, act_ref, x2_ref, pred_ref,
):
    step = pl.program_id(0)

    @pl.when(step == 0)
    def _():
        x1_ref[...] = x0_ref[...] + jnp.dot(
            o_ref[...], out_ref[...], preferred_element_type=f32
        )
        unit, _ = normed_parts(x1_ref[...])
        h2_ref[...] = (unit * gains_ref[2:3, :] + gains_ref[3:4, :]).astype(bf16)
        x2_ref[...] = x1_ref[...]

    hidden = jnp.dot(h2_ref[...], up_ref[0], preferred_element_type=f32)
    g_ref[...] = hidden
    active = (hidden * gauss_share(hidden)).astype(bf16)
    act_ref[...] = active
    x2_ref[...] += jnp.dot(active, down_ref[...], preferred_element_type=f32)

    @pl.when(step == pl.num_programs(0) - 1)
    def _():
        unit, _ = normed_parts(x2_ref[...])
        last = unit * gains_ref[4:5, :] + gains_ref[5:6, :]
        pred_ref[...] = lax.dot_general(
            last, head_ref[...], NT, precision=highest, preferred_element_type=f32
        )


def weight_specs(w_out, w_up, w_down):
    _, width, units = w_up.shape
    return (
        pl.BlockSpec(w_out.shape, lambda i: (0, 0)),
        pl.BlockSpec((1, width, units), lambda i: (i, 0, 0)),
        pl.BlockSpec((units, width), lambda i: (i, 0)),
    )


def branch_forward(attended, x_first, norm_gains, gathered, head):
    w_out, w_up, w_down, _ = gathered
    rows, width = x_first.shape
    parts, units = w_up.shape[0], w_up.shape[2]
    fixed = lambda shape: pl.BlockSpec(shape, lambda i: (0, 0))
    by_units = pl.BlockSpec((rows, units), lambda i: (0, i))
    columns = head.shape[0]
    flops = 2 * rows * (width * width + 2 * width * parts * units + 6 * width * columns)
    return pl.pallas_call(
        branch_kernel,
        grid=(parts,),
        out_shape=(
            jax.ShapeDtypeStruct((rows, width), f32),
            jax.ShapeDtypeStruct((rows, width), bf16),
            jax.ShapeDtypeStruct((rows, parts * units), f32),
            jax.ShapeDtypeStruct((rows, parts * units), bf16),
            jax.ShapeDtypeStruct((rows, width), f32),
            jax.ShapeDtypeStruct((rows, columns), f32),
        ),
        in_specs=[
            fixed((rows, width)),
            fixed((rows, width)),
            fixed(norm_gains.shape),
            *weight_specs(w_out, w_up, w_down),
            fixed(head.shape),
        ],
        out_specs=[
            fixed((rows, width)),
            fixed((rows, width)),
            by_units,
            by_units,
            fixed((rows, width)),
            fixed((rows, columns)),
        ],
        compiler_params=pltpu.CompilerParams(vmem_limit_bytes=BIG),
        cost_estimate=pl.CostEstimate(
            flops=flops,
            bytes_accessed=4 * width * parts * units + 6 * rows * parts * units,
            transcendentals=rows * parts * units,
        ),
        name="branch_forward",
    )(attended, x_first, norm_gains, w_out, w_up, w_down, head)


def branch_back_kernel(
    dpred_ref, x2_ref, x1_ref, gains_ref, g_ref, out_ref, up_ref, down_ref, head_ref,
    dx2_ref, dg_ref, dx1_ref, low_ref, do_ref, gain_ref, dhead_ref,
    wide_ref, sum_ref,
):
    step = pl.program_id(0)

    @pl.when(step == 0)
    def _():
        grad = dpred_ref[...]
        unit, inverse = normed_parts(x2_ref[...])
        gain = gains_ref[4:5, :]
        last = unit * gain + gains_ref[5:6, :]
        dhead_ref[...] = lax.dot_general(
            grad, last, TN, precision=highest, preferred_element_type=f32
        )
        row_grad = jnp.dot(grad, head_ref[...], precision=highest, preferred_element_type=f32)
        wide, gain_grad, bias_grad = norm_grad(unit, inverse, gain, row_grad)
        gain_ref[...] = jnp.zeros_like(gain_ref)
        gain_ref[4:5, :] = gain_grad
        gain_ref[5:6, :] = bias_grad
        wide_ref[...] = wide
        dx2_ref[...] = wide.astype(bf16)
        sum_ref[...] = jnp.zeros_like(sum_ref)

    active_grad = lax.dot_general(dx2_ref[...], down_ref[...], NT, preferred_element_type=f32)
    hidden = g_ref[...]
    slope = gauss_share(hidden) + hidden * (
        jnp.exp(-0.5 * hidden * hidden) * (2.0 * math.pi) ** -0.5
    )
    hidden_grad = (active_grad * slope).astype(bf16)
    dg_ref[...] = hidden_grad
    sum_ref[...] += lax.dot_general(hidden_grad, up_ref[0], NT, preferred_element_type=f32)

    @pl.when(step == pl.num_programs(0) - 1)
    def _():
        unit, inverse = normed_parts(x1_ref[...])
        middle, gain_grad, bias_grad = norm_grad(unit, inverse, gains_ref[2:3, :], sum_ref[...])
        gain_ref[2:3, :] = gain_grad
        gain_ref[3:4, :] = bias_grad
        middle = wide_ref[...] + middle
        dx1_ref[...] = middle
        low_ref[...] = middle.astype(bf16)
        total = lax.dot_general(low_ref[...], out_ref[...], NT, preferred_element_type=f32)
        do_ref[...] = total.astype(bf16)


def branch_backward(pred_grad, x_last, x_mid, norm_gains, hidden, gathered, head):
    w_out, w_up, w_down, _ = gathered
    rows, width = x_last.shape
    parts, units = w_up.shape[0], w_up.shape[2]
    fixed = lambda shape: pl.BlockSpec(shape, lambda i: (0, 0))
    by_units = pl.BlockSpec((rows, units), lambda i: (0, i))
    columns = head.shape[0]
    wide = (rows, width)
    flops = 2 * rows * (width * width + 2 * width * parts * units + 12 * width * columns)
    return pl.pallas_call(
        branch_back_kernel,
        grid=(parts,),
        out_shape=(
            jax.ShapeDtypeStruct(wide, bf16),
            jax.ShapeDtypeStruct((rows, parts * units), bf16),
            jax.ShapeDtypeStruct(wide, f32),
            jax.ShapeDtypeStruct(wide, bf16),
            jax.ShapeDtypeStruct(wide, bf16),
            jax.ShapeDtypeStruct((6, width), f32),
            jax.ShapeDtypeStruct((columns, width), f32),
        ),
        in_specs=[
            fixed((rows, columns)),
            fixed(wide),
            fixed(wide),
            fixed(norm_gains.shape),
            by_units,
            *weight_specs(w_out, w_up, w_down),
            fixed(head.shape),
        ],
        out_specs=[
            fixed(wide),
            by_units,
            fixed(wide),
            fixed(wide),
            fixed(wide),
            fixed((6, width)),
            fixed((columns, width)),
        ],
        scratch_shapes=[pltpu.VMEM(wide, f32), pltpu.VMEM(wide, f32)],
        compiler_params=pltpu.CompilerParams(vmem_limit_bytes=BIG),
        cost_estimate=pl.CostEstimate(
            flops=flops,
            bytes_accessed=4 * width * parts * units + 6 * rows * parts * units,
            transcendentals=2 * rows * parts * units,
        ),
        name="branch_backward",
    )(pred_grad, x_last, x_mid, norm_gains, hidden, w_out, w_up, w_down, head)


def wide_piece(piece):
    half = piece.shape[0] // 2
    return jnp.concatenate((piece[:half], piece[half:]), axis=1)


def tall_piece(piece):
    half = piece.shape[1] // 2
    return jnp.concatenate((piece[:, :half], piece[:, half:]), axis=0)


def both_steps(left_a, right_a, left_b, right_b):
    product = lax.dot_general(left_a[...], right_a[...], TN, preferred_element_type=f32)
    return product + lax.dot_general(left_b[...], right_b[...], TN, preferred_element_type=f32)


def down_pieces(refs):
    product = both_steps(*refs)
    share = product.shape[1] // 4
    return [wide_piece(product[:, i * share : (i + 1) * share]) for i in range(4)]


def up_out_pieces(refs):
    up = both_steps(*refs[:4])
    share = up.shape[0] // 4
    out = both_steps(*refs[4:])
    size = out.shape[1] // 4
    return [
        jnp.concatenate(
            (up[i * share : (i + 1) * share], wide_piece(out[:, i * size : (i + 1) * size])), axis=0
        )
        for i in range(4)
    ]


def outer_other_kernel(make, count, where_ref, *refs):
    o_ref = refs[count]
    for split, piece in enumerate(make(refs[:count])):
        o_ref[0, split] = piece.astype(bf16)


def outer_own_kernel(make, count, where_ref, *refs):
    other_ref, send_ref, keep_ref, held_ref = refs[count:]
    for split, piece in enumerate(make(refs[:count])):
        held_ref[split] = (piece + other_ref[0, split].astype(f32)).astype(bf16)
    x, y = where_ref[1], where_ref[2]
    early = pl.program_id(0) < 2
    for which in range(2):
        send_ref[0, which] = held_ref[jnp.where(early, which * 2 + 1 - x, (1 - y) * 2 + which)]
        keep_ref[0, which] = held_ref[jnp.where(early, which * 2 + x, y * 2 + which)]


def outer_half(operands, make, height, where, other):
    specs = []
    for value, blocked in operands:
        rows, size = value.shape
        if blocked:
            specs.append(pl.BlockSpec((rows, size // 8), lambda i, w: (0, i * 2 + w[0])))
        else:
            specs.append(pl.BlockSpec((rows, size), lambda i, w: (0, 0)))
    values = [value for value, _ in operands]
    count = len(values)
    whole = pl.BlockSpec((1, 4, height, 512), lambda i, w: (i, 0, 0, 0))
    half = pl.BlockSpec((1, 2, height, 512), lambda i, w: (i, 0, 0, 0))
    rows = values[0].shape[0]
    cost = pl.CostEstimate(
        flops=2 * 2 * rows * 16 * height * 512, bytes_accessed=3 * 16 * height * 512, transcendentals=0
    )
    params = pltpu.CompilerParams(vmem_limit_bytes=BIG)
    if other is None:
        return pl.pallas_call(
            partial(outer_other_kernel, make, count),
            out_shape=jax.ShapeDtypeStruct((4, 4, height, 512), bf16),
            grid_spec=pltpu.PrefetchScalarGridSpec(
                num_scalar_prefetch=1, grid=(4,), in_specs=specs, out_specs=whole
            ),
            compiler_params=params,
            cost_estimate=cost,
            name="outer_other",
        )(where, *values)
    return pl.pallas_call(
        partial(outer_own_kernel, make, count),
        out_shape=(jax.ShapeDtypeStruct((4, 2, height, 512), bf16),) * 2,
        grid_spec=pltpu.PrefetchScalarGridSpec(
            num_scalar_prefetch=1,
            grid=(4,),
            in_specs=specs + [whole],
            out_specs=[half, half],
            scratch_shapes=[pltpu.VMEM((4, height, 512), bf16)],
        ),
        compiler_params=params,
        cost_estimate=cost,
        name="outer_own",
    )(where, *values, other)


def device_pairs(move):
    pairs = []
    for dp in range(4):
        for level in range(4):
            for core in range(2):
                to_dp, to_level, to_core = move(dp, level, core)
                pairs.append(((dp * 4 + level) * 2 + core, (to_dp * 4 + to_level) * 2 + to_core))
    return pairs


def shift(value, move):
    return lax.ppermute(value, ("dp", "mp"), device_pairs(move))


def to_core(dp, level, core):
    return dp, level, 1 - core


def to_side(dp, level, core):
    return dp ^ 1, level, core


def to_down(dp, level, core):
    return dp ^ 2, level, core


def choose(value, index, axis=0):
    return lax.dynamic_index_in_dim(value, index, axis, keepdims=False)


def sum_levels(pieces, level):
    total = choose(pieces, level).astype(f32)
    for step in range(1, 4):
        piece = choose(pieces, lax.rem(level + step, 4)).astype(bf16)
        moved = shift(piece, lambda dp, z, core: (dp, (z + step) % 4, core))
        total = total + moved.astype(f32)
    return total


def tie(*values):
    return lax.optimization_barrier(values)


def first_sums(send, keep):
    first = keep[:2].astype(f32) + shift(send[:2], to_side).astype(f32)
    second = keep[2:].astype(f32) + shift(send[2:], to_down).astype(f32)
    return first.astype(bf16), second.astype(bf16)


def second_sums(first, second, x, y):
    first_moved = shift(choose(first, 1 - y, 1), to_down)
    second_moved = shift(choose(second, 1 - x, 1), to_side)
    first = choose(first, y, 1).astype(f32) + first_moved.astype(f32)
    second = choose(second, x, 1).astype(f32) + second_moved.astype(f32)
    return jnp.concatenate((first, second))


def outer_plain(lefts, rights, by_rows):
    dp, mp = lax.axis_size("dp"), lax.axis_size("mp")
    grads = sum(
        lax.dot_general(left, right, TN, preferred_element_type=f32)
        for left, right in zip(lefts, rights)
    ).astype(bf16)
    rows, width = grads.shape
    if by_rows:
        grads = grads.reshape(dp, rows // dp, mp, width // mp).transpose(0, 2, 1, 3)
    else:
        grads = grads.reshape(mp, rows // mp, dp, width // dp).transpose(2, 0, 1, 3)
    grads = grads.reshape((dp * mp,) + grads.shape[2:])
    return lax.psum_scatter(grads, ("dp", "mp"), scatter_dimension=0, tiled=False).astype(f32)


def exchange_sum_kernel(
    x_ref, loss_ref, qkv_ref, up_out_ref, down_ref, o_ref, s_ref, work_ref, pair_ref, quad_ref, eight_ref, deep_ref, tile_ref,
    send_sem, recv_sem,
):
    dp, level, core = mesh_place()
    x, y = lax.rem(dp, 2), dp // 2
    side = device_of(dp + 1 - 2 * x, level, core)
    down = device_of(lax.rem(dp + 2, 4), level, core)
    near = device_of(dp, level, 1 - core)
    deep = [device_of(dp, lax.rem(level + step, 4), core) for step in (1, 2, 3)]
    barrier = pltpu.get_barrier_semaphore()
    for target in (side, down, near, *deep):
        pl.semaphore_signal(barrier, inc=1, device_id=target, device_id_type=MESH)
    pl.semaphore_wait(barrier, 6)
    started = []

    def send(source, target_ref, target):
        slot = len(started)
        copy = pltpu.make_async_remote_copy(
            src_ref=source,
            dst_ref=target_ref,
            send_sem=send_sem.at[slot],
            recv_sem=recv_sem.at[slot],
            device_id=target,
            device_id_type=MESH,
        )
        copy.start()
        started.append(copy)
        return copy

    half = x_ref.shape[0] // 2
    quarter, eighth, part, unit = half // 2, half // 4, half // 8, half // 16

    def rows(start, size):
        return pl.ds(pl.multiple_of(start, unit), size)

    copy = send(x_ref.at[rows((1 - core) * half, half)], pair_ref, near)
    copy.wait_recv()
    work_ref[...] = x_ref[rows(core * half, half)] + pair_ref[...]
    one = send(work_ref.at[rows((1 - x) * eighth, eighth)], quad_ref.at[0], side)
    two = send(work_ref.at[rows(quarter + (1 - y) * eighth, eighth)], quad_ref.at[1], down)
    base_a = x * eighth
    base_b = quarter + y * eighth
    wide_a, wide_b = core * half + base_a, core * half + base_b
    one.wait_recv()
    work_ref[rows(base_a, eighth)] += quad_ref[0]
    one = send(work_ref.at[rows(base_a + (1 - y) * part, part)], eight_ref.at[0], down)
    two.wait_recv()
    work_ref[rows(base_b, eighth)] += quad_ref[1]
    two = send(work_ref.at[rows(base_b + (1 - x) * part, part)], eight_ref.at[1], side)
    base_a = base_a + y * part
    base_b = base_b + x * part
    one.wait_recv()
    work_ref[rows(base_a, part)] += eight_ref[0]
    two.wait_recv()
    work_ref[rows(base_b, part)] += eight_ref[1]

    def level_start(which):
        late = which // 2
        return (1 - late) * base_a + late * base_b + lax.rem(which, 2) * unit

    copies = []
    for step in (1, 2, 3):
        source = work_ref.at[rows(level_start(lax.rem(level + step, 4)), unit)]
        copies.append(send(source, deep_ref.at[step - 1], deep[step - 1]))
    for copy in copies:
        copy.wait_recv()
    total = work_ref[rows(level_start(level), unit)] + deep_ref[0] + deep_ref[1] + deep_ref[2]
    mine = rows(core * half + level_start(level), unit)
    base_a = core * half + base_a
    base_b = core * half + base_b
    o_ref[mine] = total
    row = lax.broadcasted_iota(jnp.int32, s_ref.shape, 0)
    squares = jnp.sum(total * total)
    for ref in (qkv_ref, up_out_ref, down_ref):
        squares += jnp.sum(ref[...] * ref[...])
    tile_ref[0] = jnp.where(row == 0, squares, jnp.where(row == 1, loss_ref[...], 0.0))
    copies = []
    for step in (1, 2, 3):
        copies.append(send(o_ref.at[mine], o_ref.at[mine], deep[step - 1]))
        copies.append(send(tile_ref.at[0], tile_ref.at[step], deep[step - 1]))
    for copy in copies:
        copy.wait_recv()
    one = send(o_ref.at[rows(base_a, part)], o_ref.at[rows(base_a, part)], down)
    two = send(o_ref.at[rows(base_b, part)], o_ref.at[rows(base_b, part)], side)
    tile_ref[4] = tile_ref[0] + tile_ref[1] + tile_ref[2] + tile_ref[3]
    three = send(tile_ref.at[4], tile_ref.at[5], side)
    one.wait_recv()
    one = send(o_ref.at[rows(wide_a, eighth)], o_ref.at[rows(wide_a, eighth)], side)
    two.wait_recv()
    two = send(o_ref.at[rows(wide_b, eighth)], o_ref.at[rows(wide_b, eighth)], down)
    three.wait_recv()
    tile_ref[6] = tile_ref[4] + tile_ref[5]
    three = send(tile_ref.at[6], tile_ref.at[7], down)
    one.wait_recv()
    two.wait_recv()
    one = send(o_ref.at[rows(core * half, half)], o_ref.at[rows(core * half, half)], near)
    three.wait_recv()
    tile_ref[8] = tile_ref[6] + tile_ref[7]
    three = send(tile_ref.at[8], tile_ref.at[9], near)
    one.wait_recv()
    three.wait_recv()
    s_ref[...] = tile_ref[8] + tile_ref[9]
    for copy in started:
        copy.wait_send()


def exchange_sum(value, loss, *shares):
    rows, width = value.shape
    tile = jax.ShapeDtypeStruct((8, 128), f32)
    return pl.pallas_call(
        exchange_sum_kernel,
        out_shape=(jax.ShapeDtypeStruct(value.shape, f32), tile),
        in_specs=[VMEM] * 5,
        out_specs=[VMEM, VMEM],
        scratch_shapes=[
            pltpu.VMEM((rows // 2, width), f32),
            pltpu.VMEM((rows // 2, width), f32),
            pltpu.VMEM((2, rows // 8, width), f32),
            pltpu.VMEM((2, rows // 16, width), f32),
            pltpu.VMEM((3, rows // 32, width), f32),
            pltpu.VMEM((10,) + tile.shape, f32),
            pltpu.SemaphoreType.DMA((24,)),
            pltpu.SemaphoreType.DMA((24,)),
        ],
        compiler_params=pltpu.CompilerParams(
            collective_id=5, has_side_effects=True, vmem_limit_bytes=BIG
        ),
        name="exchange_sum",
    )(value, loss.reshape(1, 1), *shares)


def split_low(values):
    high = values.astype(bf16)
    return high, (values - high.astype(f32)).astype(bf16)


def three_products(left, right, dims=(((1,), (0,)), ((), ()))):
    def product(one, two):
        return lax.dot_general(one, two, dims, preferred_element_type=f32)

    return product(left[0], right[0]) + (product(left[1], right[0]) + product(left[0], right[1]))


def exact_product(left, right, dims=(((1,), (0,)), ((), ()))):
    return lax.dot_general(left, right, dims, precision=highest, preferred_element_type=f32)


def head_marks(width):
    head = lax.broadcasted_iota(jnp.int32, (HEADS, width), 0)
    column = lax.broadcasted_iota(jnp.int32, (HEADS, width), 1)
    return jnp.where(column // HEAD_DIM == head, 1.0, 0.0).astype(f32)


def quarter_marks(padded):
    row = lax.broadcasted_iota(jnp.int32, (padded, V), 0)
    column = lax.broadcasted_iota(jnp.int32, (padded, V), 1)
    return jnp.where(row // 4 == column, 0.25, 0.0).astype(f32)


def tables_kernel(tables_ref, hot_ref, patch_ref, var_ref, keyed_ref, bias_ref):
    padded, width = patch_ref.shape
    query = tables_ref[5 * V + LEADS : 5 * V + LEADS + 1, :]
    patch_ref[...] = jnp.zeros_like(patch_ref)
    patch_ref[: 4 * V, :] = tables_ref[: 4 * V, :]
    chosen = exact_product(hot_ref[...], tables_ref[4 * V : 5 * V, :])
    var_ref[...] = exact_product(quarter_marks(padded), chosen)
    marks = head_marks(width)
    scale = HEAD_DIM**-0.5
    keyed_ref[...] = exact_product(marks, patch_ref[...] * query, NT) * scale
    bias = exact_product(marks, var_ref[...] * query, NT) * (4.0 * scale)
    column = lax.broadcasted_iota(jnp.int32, bias.shape, 1)
    bias_ref[...] = jnp.where(column < 4 * V, bias, -1e30)


def prepare_tables(tables, var_hot):
    padded = 256
    return pl.pallas_call(
        tables_kernel,
        out_shape=(
            jax.ShapeDtypeStruct((padded, D), f32),
            jax.ShapeDtypeStruct((padded, D), f32),
            jax.ShapeDtypeStruct((HEADS, padded), f32),
            jax.ShapeDtypeStruct((HEADS, padded), f32),
        ),
        compiler_params=pltpu.CompilerParams(vmem_limit_bytes=BIG),
        name="prepare_tables",
    )(tables, var_hot)


def four_sum(values):
    size = values.shape[1]
    lane = lax.broadcasted_iota(jnp.int32, values.shape, 1)
    values = values + jnp.where(
        lane % 2 == 0, pltpu.roll(values, size - 1, 1), pltpu.roll(values, 1, 1)
    )
    return values + jnp.where(
        lane % 4 < 2, pltpu.roll(values, size - 2, 1), pltpu.roll(values, 2, 1)
    )


def cell_shares(cells, keyed, bias):
    scores = four_sum(cells * keyed) + bias
    raised = jnp.exp(scores - jnp.max(scores, axis=1, keepdims=True))
    total = jnp.sum(raised, axis=1, keepdims=True) * 0.25
    return raised * (1.0 / total)


def embed_pair(pair, cells, keyed_ref, bias_ref, patch_ref, var_ref, x0_ref):
    patch = split_low(patch_ref[...])
    variable = split_low(var_ref[...])
    outs = []
    for which in range(2):
        row = pl.ds(pair * 2 + which, 1)
        shares = cell_shares(cells, keyed_ref[row, :], bias_ref[row, :])
        outs.append(
            three_products(split_low(shares * cells), patch)
            + three_products(split_low(shares), variable)
        )
    lane = lax.broadcasted_iota(jnp.int32, outs[0].shape, 1)
    columns = pl.ds(pl.multiple_of(pair * 2 * HEAD_DIM, 2 * HEAD_DIM), 2 * HEAD_DIM)
    x0_ref[:, columns] = jnp.where(lane < HEAD_DIM, outs[0], outs[1])


def embed_kernel(
    u_ref, keyed_ref, bias_ref, patch_ref, var_ref, lead_ref, gains_ref, x0_ref, h1_ref
):
    pair = pl.program_id(0)
    embed_pair(pair, u_ref[...], keyed_ref, bias_ref, patch_ref, var_ref, x0_ref)

    @pl.when(pair == pl.num_programs(0) - 1)
    def _():
        x0_ref[...] += lead_ref[...]
        unit, _ = normed_parts(x0_ref[...])
        h1_ref[...] = (unit * gains_ref[0:1, :] + gains_ref[1:2, :]).astype(bf16)


def embed_forward(cells, prepared, lead_row, norm_gains):
    patch, variable, keyed, bias = prepared
    rows, padded = cells.shape
    fixed = lambda shape: pl.BlockSpec(shape, lambda i: (0, 0))
    by_pair = pl.BlockSpec((padded, 2 * HEAD_DIM), lambda i: (0, i))
    return pl.pallas_call(
        embed_kernel,
        grid=(HEADS // 2,),
        out_shape=(
            jax.ShapeDtypeStruct((rows, D), f32),
            jax.ShapeDtypeStruct((rows, D), bf16),
        ),
        in_specs=[
            fixed((rows, padded)),
            fixed(keyed.shape),
            fixed(bias.shape),
            by_pair,
            by_pair,
            fixed((1, D)),
            fixed(norm_gains.shape),
        ],
        out_specs=[fixed((rows, D)), fixed((rows, D))],
        compiler_params=pltpu.CompilerParams(vmem_limit_bytes=BIG),
        cost_estimate=pl.CostEstimate(
            flops=24 * rows * padded * D, bytes_accessed=14 * rows * D, transcendentals=16 * rows * padded
        ),
        name="embed_forward",
    )(cells, keyed, bias, patch, variable, lead_row, norm_gains)


def entry_back_kernel(
    grad_ref, qkv_ref, x0_ref, mid_ref, gains_ref, u_ref, keyed_ref, bias_ref, patch_ref, var_ref,
    du_ref, gain_ref, lead_ref, dpatch_ref, dvar_ref, dkeyed_ref, dbias_ref,
    dx_ref, flip_ref,
):
    pair = pl.program_id(0)

    @pl.when(pair == 0)
    def _():
        row_grad = jnp.dot(grad_ref[...], qkv_ref[...], preferred_element_type=f32)
        unit, inverse = normed_parts(x0_ref[...])
        part, gain_grad, bias_grad = norm_grad(unit, inverse, gains_ref[0:1, :], row_grad)
        total = mid_ref[...] + part
        dx_ref[...] = total
        flip_ref[...] = total.T
        lead_ref[...] = jnp.sum(total, axis=0, keepdims=True)
        gain_ref[0:1, :] = gain_grad
        gain_ref[1:2, :] = bias_grad
        du_ref[...] = jnp.zeros_like(du_ref)

    cells = u_ref[...]
    size = 2 * HEAD_DIM
    columns = pl.ds(pl.multiple_of(pair * size, size), size)
    grads = dx_ref[:, columns]
    lane = lax.broadcasted_iota(jnp.int32, grads.shape, 1)
    patch = split_low(patch_ref[...])
    variable = split_low(var_ref[...])
    cells_grad = None
    for which in range(2):
        row = pl.ds(pair * 2 + which, 1)
        keyed = keyed_ref[row, :]
        shares = cell_shares(cells, keyed, bias_ref[row, :])
        one = split_low(jnp.where(lane // HEAD_DIM == which, grads, 0.0))
        mixed_grad = three_products(one, patch, NT)
        share_grad = mixed_grad * cells + three_products(one, variable, NT)
        weighted = shares * share_grad
        inner = jnp.sum(weighted, axis=1, keepdims=True)
        score_grad = four_sum(weighted) - shares * inner
        piece = mixed_grad * shares + score_grad * keyed
        cells_grad = piece if cells_grad is None else cells_grad + piece
        scale = HEAD_DIM**-0.5
        dkeyed_ref[row, :] = jnp.sum(score_grad * cells, axis=0, keepdims=True) * scale
        dbias_ref[row, :] = jnp.sum(score_grad, axis=0, keepdims=True) * scale
        rows = pl.ds(pl.multiple_of(pair * size + which * HEAD_DIM, HEAD_DIM), HEAD_DIM)
        flipped = split_low(flip_ref[rows, :])
        mine = slice(which * HEAD_DIM, (which + 1) * HEAD_DIM)
        dpatch_ref[mine, :] = three_products(flipped, split_low(shares * cells))
        dvar_ref[mine, :] = three_products(flipped, split_low(shares))
    du_ref[...] += cells_grad


def entry_backward(token_grad, qkv_t, x_first, mid_grad, norm_gains, cells, prepared):
    patch, variable, keyed, bias = prepared
    rows, width = x_first.shape
    padded = cells.shape[1]
    fixed = lambda shape: pl.BlockSpec(shape, lambda i: (0, 0))
    by_pair = pl.BlockSpec((padded, 2 * HEAD_DIM), lambda i: (0, i))
    flipped = pl.BlockSpec((2 * HEAD_DIM, padded), lambda i: (i, 0))
    return pl.pallas_call(
        entry_back_kernel,
        grid=(HEADS // 2,),
        out_shape=(
            jax.ShapeDtypeStruct((rows, padded), f32),
            jax.ShapeDtypeStruct((2, width), f32),
            jax.ShapeDtypeStruct((1, width), f32),
            jax.ShapeDtypeStruct((width, padded), f32),
            jax.ShapeDtypeStruct((width, padded), f32),
            jax.ShapeDtypeStruct(keyed.shape, f32),
            jax.ShapeDtypeStruct(bias.shape, f32),
        ),
        in_specs=[
            fixed(token_grad.shape),
            fixed(qkv_t.shape),
            fixed((rows, width)),
            fixed((rows, width)),
            fixed(norm_gains.shape),
            fixed(cells.shape),
            fixed(keyed.shape),
            fixed(bias.shape),
            by_pair,
            by_pair,
        ],
        out_specs=[
            fixed((rows, padded)),
            fixed((2, width)),
            fixed((1, width)),
            flipped,
            flipped,
            fixed(keyed.shape),
            fixed(bias.shape),
        ],
        scratch_shapes=[pltpu.VMEM((rows, width), f32), pltpu.VMEM((width, rows), f32)],
        compiler_params=pltpu.CompilerParams(vmem_limit_bytes=BIG),
        cost_estimate=pl.CostEstimate(
            flops=60 * rows * padded * D, bytes_accessed=40 * rows * D, transcendentals=16 * rows * padded
        ),
        name="entry_backward",
    )(token_grad, qkv_t, x_first, mid_grad, norm_gains, cells, keyed, bias, patch, variable)


def table_grads_kernel(
    pa_ref, pb_ref, va_ref, vb_ref, ka_ref, kb_ref, ba_ref, bb_ref,
    patch_ref, var_ref, query_ref, hot_ref, lead_hot_ref, lead_ref, gain_ref, head_ref, high_ref, o_ref,
):
    padded, width = patch_ref.shape
    marks = head_marks(width)
    query = query_ref[...]
    keyed_grad = exact_product(ka_ref[...] + kb_ref[...], marks, TN)
    bias_grad = exact_product(ba_ref[...] + bb_ref[...], marks, TN)
    o_ref[...] = jnp.zeros_like(o_ref)
    patch_grad = (pa_ref[...] + pb_ref[...]).T + keyed_grad * query
    o_ref[: 4 * V, :] = patch_grad[: 4 * V, :]
    var_grad = (va_ref[...] + vb_ref[...]).T + bias_grad * query
    var_rows = exact_product(quarter_marks(padded), var_grad, TN)
    o_ref[4 * V : 5 * V, :] = exact_product(hot_ref[...], var_rows, TN)
    lead_rows = exact_product(lead_hot_ref[...], lead_ref[...], TN)
    o_ref[5 * V : 5 * V + LEADS, :] = lead_rows[:LEADS, :]
    query_grad = jnp.sum(
        keyed_grad * patch_ref[...] + bias_grad * var_ref[...], axis=0, keepdims=True
    )
    o_ref[5 * V + LEADS : 5 * V + LEADS + 1, :] = query_grad
    o_ref[5 * V + LEADS + 1 : 5 * V + LEADS + 3, :] = gain_ref[...]
    o_ref[padded : padded + 4 * V, :] = head_ref[...]
    o_ref[padded + 4 * V : padded + 4 * V + 4, :] = high_ref[...]


def table_grads(first, second, prepared, query, var_hot, lead_hots, leads, gain_rows, head, high):
    patch, variable, _, _ = prepared
    operands = []
    for one, two in zip(first, second):
        operands += [one, two]
    return pl.pallas_call(
        table_grads_kernel,
        out_shape=jax.ShapeDtypeStruct((2 * patch.shape[0], D), f32),
        compiler_params=pltpu.CompilerParams(vmem_limit_bytes=BIG),
        name="table_grads",
    )(*operands, patch, variable, query, var_hot, lead_hots, leads, gain_rows, head, high)


def adam_step(master, grad, first, second, rate):
    first_new = beta_first * first + (1.0 - beta_first) * grad
    second_new = beta_second * second + (1.0 - beta_second) * grad * grad
    update = first_new / first_fix / (jnp.sqrt(second_new / second_fix) + adam_eps)
    return (master - rate * (update + decay_rate * master), first_new, second_new)


def update_kernel(packed, *refs):
    where_ref, sums_ref, tile_ref, count_ref = refs[:4]
    shares = list(refs[4 : 4 + (3 if packed else 4)])
    rest = refs[4 + len(shares) :]
    states, average_ref, outs = rest[:18], rest[18], rest[19:]
    norm = jnp.sqrt(tile_ref[0:1, 0:1])
    factor = jnp.minimum(1.0, clip_norm / (norm + 1e-06))
    outs[1][...] = norm
    outs[0][...] = tile_ref[1:2, 0:1] / (2.0 * V * jnp.maximum(count_ref[...], 1.0))
    embed_rows = 5 * V + LEADS + 1
    padded = 256

    def apply(index, grad, rate, rows=slice(None)):
        master, first, second = (ref[rows, :] for ref in states[3 * index : 3 * index + 3])
        new = adam_step(master, factor * grad, first, second, rate)
        for ref, value in zip(outs[2 + 3 * index : 5 + 3 * index], new):
            ref[rows, :] = value
        return new[0]

    apply(0, sums_ref[:embed_rows, :], lr_table, slice(0, embed_rows))
    apply(0, sums_ref[padded : padded + 4 * V, :], lr_table, slice(embed_rows, embed_rows + 4 * V))
    apply(1, sums_ref[embed_rows : embed_rows + 2, :], lr_gain, slice(0, 2))
    apply(1, sums_ref[padded + 4 * V : padded + 4 * V + 4, :], lr_gain, slice(2, 6))
    if packed:
        up_out = shares[1]
        grads = (
            shares[0][...], tall_piece(up_out[256:, :]), up_out[:256, :], tall_piece(shares[2][...])
        )
    else:
        grads = [share[...] for share in shares]
    qkv_new = apply(2, grads[0], lr_matrix)
    for index in range(1, 4):
        apply(2 + index, grads[index], lr_matrix)
    outs[20][...] = average_keep * average_ref[...] + (1.0 - average_keep) * qkv_new


def update_all(packed, where, sums, tile, count, shares, states, average):
    operands = [sums, tile, count.reshape(1, 1), *shares]
    fixed = lambda shape: pl.BlockSpec(shape, lambda i, w: (0, 0))
    in_specs = [fixed(value.shape) for value in operands]
    out_shapes = [(1, 1), (1, 1)]
    for master, first, second in states:
        if master.shape == first.shape:
            in_specs.append(fixed(master.shape))
        elif master.shape[0] == first.shape[0]:
            in_specs.append(pl.BlockSpec(first.shape, lambda i, w: (0, w[0])))
        else:
            in_specs.append(pl.BlockSpec(first.shape, lambda i, w: (w[0], 0)))
        in_specs += [fixed(first.shape)] * 2
        operands += [master, first, second]
        out_shapes += [first.shape] * 3
    operands.append(average)
    in_specs.append(fixed(average.shape))
    out_shapes.append(average.shape)
    return pl.pallas_call(
        partial(update_kernel, packed),
        grid_spec=pltpu.PrefetchScalarGridSpec(
            num_scalar_prefetch=1,
            grid=(1,),
            in_specs=in_specs,
            out_specs=[fixed(shape) for shape in out_shapes],
        ),
        out_shape=[jax.ShapeDtypeStruct(shape, f32) for shape in out_shapes],
        compiler_params=pltpu.CompilerParams(vmem_limit_bytes=60 * 2**20),
        name="update_all",
    )(where, *operands)


def by_kind(shard):
    rows = shard.shape[0]
    return shard.reshape(rows, -1, 3, HEAD_DIM).transpose(0, 2, 1, 3).reshape(rows, -1)


def by_head(shard):
    rows = shard.shape[0]
    return shard.reshape(rows, 3, -1, HEAD_DIM).transpose(0, 2, 1, 3).reshape(rows, -1)


lag_one, lag_two, ahead = 2, 4, 3
embed_at, gather_at, project_at, attend_at = 3, 11, 14, 18


def start_kernel(halves, *refs):
    count = len(halves)
    packed_ref, keyed_ref, bias_ref, patch_ref, var_ref, lead_ref, gains_ref = refs[:7]
    shards = refs[7 : 7 + count]
    x0_ref, cells_ref, qkv_ref, o_ref, full_ref, lse_ref, count_ref, rows_out = refs[7 + count : 15 + count]
    outs = refs[15 + count : 15 + 2 * count]
    (held_ref, h1_ref, rows_ref, weight_ref, vt_ref, tile_ref, send_sem, recv_sem,
     level_send, level_recv, own_sem) = refs[15 + 2 * count :]
    step = pl.program_id(0)
    dp, level, core = mesh_place()
    x = lax.rem(dp, 2)
    columns = {"here": dp, "side": dp + 1 - 2 * x, "down": lax.rem(dp + 2, 4), "far": 3 - dp}
    side = device_of(columns["side"], level, core)
    down = device_of(columns["down"], level, core)
    near = device_of(dp, level, 1 - core)
    across = device_of(level, dp, core)
    middle = lax.rem(level, 3) != 0
    late = level // 2
    sources = (level + 1 - 2 * lax.rem(level, 2), 2 - late, 3 * (1 - late))
    onward = (3 - level, lax.rem(3 * level + 1, 4), lax.rem(3 * level + 1, 4))
    slots = [0]

    def remote(source, target_ref, target):
        slot = slots[0]
        slots[0] += 1
        return pltpu.make_async_remote_copy(
            src_ref=source,
            dst_ref=target_ref,
            send_sem=send_sem.at[slot],
            recv_sem=recv_sem.at[slot],
            device_id=target,
            device_id_type=MESH,
        )

    def place(out, source, column, half, pieces):
        rows = out.shape[1] // 4
        size = rows // pieces
        start = pl.multiple_of(columns[column] * rows + half * size, size)
        return out.at[source * 2 + core, pl.ds(start, size), :]

    def pass_on(out, source, column, target, cut):
        where = place(out, source, column, *cut)
        return remote(where, where, target)

    crossing = remote(packed_ref, held_ref, across)
    staying = pltpu.make_async_copy(packed_ref, held_ref, own_sem.at[count])
    mine = [outs[index].at[level * 2 + core] for index in range(count)]
    given = [remote(shards[index], mine[index], near) for index in range(count)]
    kept = [
        pltpu.make_async_copy(shards[index], mine[index], own_sem.at[index]) for index in range(count)
    ]
    chunks, openings = [], []
    for index in range(count):
        out, pieces = outs[index], halves[index]
        for half in range(pieces):
            group = len(openings)
            full = out.shape[1] // 4
            size = full // pieces
            own = shards[index].at[pl.ds(pl.multiple_of(dp * full + half * size, size), size), :]
            cut = (half, pieces)

            def along(source_ref, source, target_level, slot):
                return pltpu.make_async_remote_copy(
                    src_ref=source_ref,
                    dst_ref=place(out, source, "here", *cut),
                    send_sem=level_send.at[group * 5 + slot],
                    recv_sem=level_recv.at[group * 4 + source],
                    device_id=device_of(dp, target_level, core),
                    device_id_type=MESH,
                )

            openings.append(
                (
                    along(own, level, lax.rem(level + 1, 4), 0),
                    along(own, level, lax.rem(level + 3, 4), 1),
                )
            )
            for turn in range(3):
                source = sources[turn]
                chunks.append(
                    {
                        "level": along(place(out, source, "here", *cut), source, onward[turn], 2 + turn),
                        "side": pass_on(out, source, "here", side, cut),
                        "down": pass_on(out, source, "here", down, cut),
                        "hop_down": pass_on(out, source, "side", down, (2 * half, 2 * pieces)),
                        "hop_side": pass_on(out, source, "down", side, (2 * half + 1, 2 * pieces)),
                        "here_near": pass_on(out, source, "here", near, cut),
                        "side_near": pass_on(out, source, "side", near, cut),
                        "down_near": pass_on(out, source, "down", near, cut),
                        "far_near": pass_on(out, source, "far", near, cut),
                    }
                )
    groups = len(openings)
    order = []
    for number in range(groups + 2):
        for turn in range(3):
            if 0 <= number - turn < groups:
                order.append((number - turn, turn))
    chunks = [chunks[3 * group + turn] for group, turn in order]
    total = len(chunks)

    def start_group(number):
        @pl.when(level < 3)
        def _():
            openings[number][0].start()

        @pl.when(level > 0)
        def _():
            openings[number][1].start()

    rows = h1_ref.shape[0]
    cut = rows // 2

    def rows_of(owner, who, first, size):
        return rows_ref.at[pl.ds(pl.multiple_of((owner * 2 + who) * rows + first, cut), size)]

    def relay(place_ref, target):
        return remote(place_ref, place_ref, target)

    first_half, second_half = h1_ref.at[pl.ds(0, cut)], h1_ref.at[pl.ds(cut, cut)]
    beside, below, far = columns["side"], columns["down"], columns["far"]
    side_a = remote(first_half, rows_of(dp, core, 0, cut), side)
    down_b = remote(second_half, rows_of(dp, core, cut, cut), down)
    side_b = remote(second_half, rows_of(dp, core, cut, cut), side)
    down_a = remote(first_half, rows_of(dp, core, 0, cut), down)
    near_own = remote(h1_ref, rows_of(dp, core, 0, rows), near)
    far_a = relay(rows_of(beside, core, 0, cut), down)
    far_b = relay(rows_of(below, core, cut, cut), side)
    near_side = relay(rows_of(beside, core, 0, rows), near)
    near_down = relay(rows_of(below, core, 0, rows), near)
    near_far = relay(rows_of(far, core, 0, rows), near)
    tiles = [
        remote(tile_ref.at[0], tile_ref.at[1], side),
        remote(tile_ref.at[2], tile_ref.at[3], down),
        remote(tile_ref.at[4], tile_ref.at[5], near),
    ]
    deep = [device_of(dp, lax.rem(level + move, 4), core) for move in (1, 2, 3)]
    level_tiles = [remote(tile_ref.at[6], tile_ref.at[7 + move], deep[move]) for move in range(3)]
    weight = pltpu.make_async_copy(outs[0].at[dp * 2 + core], weight_ref, own_sem.at[count + 1])
    save = pltpu.make_async_copy(rows_ref, rows_out, own_sem.at[count + 2])

    @pl.when(step == 0)
    def _():
        barrier = pltpu.get_barrier_semaphore()
        for target in (side, down, near, *deep):
            pl.semaphore_signal(barrier, inc=1, device_id=target, device_id_type=MESH)

        @pl.when(dp != level)
        def _():
            pl.semaphore_signal(barrier, inc=1, device_id=across, device_id_type=MESH)
            pl.semaphore_wait(barrier, 7)
            crossing.start()

        @pl.when(dp == level)
        def _():
            pl.semaphore_wait(barrier, 6)
            staying.start()

        for number in range(ahead):
            start_group(number)
        for copy in (*given, *kept):
            copy.start()

    for number in range(total + lag_two):

        @pl.when(step == number)
        def _(number=number):
            if number < total:
                chunk = chunks[number]
                chunk["level"].wait_recv()

                @pl.when(middle)
                def _():
                    chunk["level"].start()

                chunk["side"].start()
                chunk["down"].start()
                chunk["here_near"].start()
                group, turn = order[number]
                if turn == 0 and group + ahead < groups:
                    start_group(group + ahead)
            if 0 <= number - lag_one < total:
                chunk = chunks[number - lag_one]
                chunk["side"].wait_recv()
                chunk["hop_down"].start()
                chunk["down"].wait_recv()
                chunk["hop_side"].start()
                chunk["side_near"].start()
                chunk["down_near"].start()
            if 0 <= number - lag_two < total:
                chunk = chunks[number - lag_two]
                chunk["hop_down"].wait_recv()
                chunk["hop_side"].wait_recv()
                chunk["far_near"].start()

    @pl.when(step == embed_at)
    def _():
        @pl.when(dp != level)
        def _():
            crossing.wait_recv()

        @pl.when(dp == level)
        def _():
            staying.wait()

        cells_ref[...] = held_ref[...]
        lane = lax.broadcasted_iota(jnp.int32, held_ref.shape, 1)
        ocean = jnp.where((lane >= 4 * V) & (lane < 4 * V + 4), 1.0 - held_ref[...], 0.0)
        tile_ref[0] = jnp.broadcast_to(jnp.sum(ocean), tile_ref.shape[1:])
        tiles[0].start()

    for turn in range(3):

        @pl.when(step == embed_at + 2 + turn)
        def _(turn=turn):
            tiles[turn].wait_recv()
            tile_ref[2 * turn + 2] = tile_ref[2 * turn] + tile_ref[2 * turn + 1]
            for copy in (tiles[1:2], tiles[2:3], level_tiles)[turn]:
                copy.start()

    @pl.when(step == embed_at + 6)
    def _():
        for copy in level_tiles:
            copy.wait_recv()
        count_ref[...] = tile_ref[6] + tile_ref[7] + tile_ref[8] + tile_ref[9]

    @pl.when((step >= embed_at) & (step < embed_at + HEADS // 2))
    def _():
        embed_pair(step - embed_at, held_ref[...], keyed_ref, bias_ref, patch_ref, var_ref, x0_ref)

    @pl.when(step == gather_at)
    def _():
        lead = held_ref[0:1, 4 * V + 4 : 4 * V + 5]
        row = lax.broadcasted_iota(jnp.int32, (1, 8), 1).astype(f32)
        lead_hot = jnp.where(row == lead, 1.0, 0.0).astype(f32)
        x0_ref[...] += exact_product(lead_hot, lead_ref[...])
        unit, _ = normed_parts(x0_ref[...])
        h1_ref[...] = (unit * gains_ref[0:1, :] + gains_ref[1:2, :]).astype(bf16)
        for copy in (side_a, down_b, side_b, down_a, near_own):
            copy.start()
        rows_of(dp, core, 0, rows)[...] = h1_ref[...]
        kept[0].wait()
        weight.start()

    @pl.when(step == gather_at + 1)
    def _():
        side_a.wait_recv()
        far_a.start()
        down_b.wait_recv()
        far_b.start()
        side_b.wait_recv()
        near_side.start()
        down_a.wait_recv()
        near_down.start()

    @pl.when(step == gather_at + 2)
    def _():
        far_a.wait_recv()
        far_b.wait_recv()
        near_far.start()
        for copy in (near_own, near_side, near_down):
            copy.wait_recv()

    block = rows_ref.shape[0] // 4

    @pl.when(step == project_at)
    def _():
        near_far.wait_recv()
        save.start()
        weight.wait()

    @pl.when((step >= project_at) & (step < project_at + 4))
    def _():
        where = pl.ds(pl.multiple_of((step - project_at) * block, block), block)
        qkv_ref[where, :] = lax.dot_general(
            rows_ref[where, :], weight_ref[...], NT, preferred_element_type=f32
        ).astype(bf16)

    width = o_ref.shape[1]
    heads = width // HEAD_DIM

    @pl.when(step == attend_at)
    def _():
        vt_ref[...] = qkv_ref[:, 2 * width :].T

    @pl.when((step >= attend_at) & (step < attend_at + 4))
    def _():
        where = pl.ds(pl.multiple_of((step - attend_at) * block, block), block)
        full, sums = attend_rows(
            heads, qkv_ref[where, :width], qkv_ref.at[:, width : 2 * width], vt_ref
        )
        for head in range(heads):
            lse_ref[head : head + 1, where] = sums[head]
        full_ref[where, :] = full
        o_ref[where, :] = full.astype(bf16)

    @pl.when(step == total + lag_two - 1)
    def _():
        for copy in given:
            copy.wait()
        for copy in kept[1:]:
            copy.wait()
        for number in range(groups):

            @pl.when(level < 3)
            def _(number=number):
                openings[number][0].wait_send()

            @pl.when(level > 0)
            def _(number=number):
                openings[number][1].wait_send()

        for chunk in chunks:
            for name in ("here_near", "side_near", "down_near", "far_near"):
                chunk[name].wait_recv()
            for name, copy in chunk.items():
                if name != "level":
                    copy.wait_send()

            @pl.when(middle)
            def _(chunk=chunk):
                chunk["level"].wait_send()

        for copy in (side_a, down_b, side_b, down_a, near_own, far_a, far_b, near_side, near_down, near_far):
            copy.wait_send()
        for copy in (*tiles, *level_tiles):
            copy.wait_send()
        save.wait()

        @pl.when(dp != level)
        def _():
            crossing.wait_send()


def start_program(packed, prepared, lead_table, norm_gains, shards, halves):
    patch, variable, keyed, bias = prepared
    count = len(shards)
    groups = sum(halves)
    copies = groups * 24 + count + 17
    rows, padded = packed.shape
    total = 8 * rows
    width = shards[0].shape[0] // 3
    heads = width // HEAD_DIM
    anywhere = pl.BlockSpec(memory_space=pl.ANY)
    fixed = lambda shape: pl.BlockSpec(shape, lambda i: (0, 0))
    by_pair = pl.BlockSpec(
        (padded, 2 * HEAD_DIM), lambda i: (0, jnp.clip(i - embed_at, 0, HEADS // 2 - 1))
    )
    shapes = [
        ((rows, D), f32),
        (packed.shape, f32),
        ((total, 3 * width), bf16),
        ((total, width), bf16),
        ((total, width), f32),
        ((heads, total), f32),
        ((8, 128), f32),
    ]
    return pl.pallas_call(
        partial(start_kernel, halves),
        grid=(groups * 3 + lag_two,),
        out_shape=[jax.ShapeDtypeStruct(shape, kind) for shape, kind in shapes]
        + [jax.ShapeDtypeStruct((total, D), bf16)]
        + [jax.ShapeDtypeStruct((8,) + shard.shape, bf16) for shard in shards],
        in_specs=[anywhere]
        + [fixed(keyed.shape), fixed(bias.shape), by_pair, by_pair]
        + [fixed(lead_table.shape), fixed(norm_gains.shape)]
        + [fixed(shard.shape) for shard in shards],
        out_specs=[fixed(shape) for shape, _ in shapes] + [anywhere] * (count + 1),
        scratch_shapes=[
            pltpu.VMEM(packed.shape, f32),
            pltpu.VMEM((rows, D), bf16),
            pltpu.VMEM((total, D), bf16),
            pltpu.VMEM(shards[0].shape, bf16),
            pltpu.VMEM((width, total), bf16),
            pltpu.VMEM((10, 8, 128), f32),
            pltpu.SemaphoreType.DMA((copies,)),
            pltpu.SemaphoreType.DMA((copies,)),
            pltpu.SemaphoreType.DMA((groups * 5,)),
            pltpu.SemaphoreType.DMA((groups * 4,)),
            pltpu.SemaphoreType.DMA((count + 3,)),
        ],
        compiler_params=pltpu.CompilerParams(
            collective_id=7, has_side_effects=True, vmem_limit_bytes=BIG
        ),
        name="start_program",
    )(packed, keyed, bias, patch, variable, lead_table, norm_gains, *shards)


def own_qkv_share(crossed, grad):
    dp = lax.axis_size("dp")
    rows = grad.shape[0] // dp
    if not crossed:
        return lax.psum_scatter(grad, "dp", scatter_dimension=0, tiled=True)
    _, level, _ = mesh_place()
    return cross(crossed, sum_levels(grad.reshape((dp, rows) + grad.shape[1:]), level))


def shards(
    crossed,
    fields,
    targets,
    land_mask,
    lead_index,
    var_ids,
    tables,
    norm_gains,
    tables_first,
    tables_second,
    gains_first,
    gains_second,
    w_qkv,
    qkv_first,
    qkv_second,
    w_out,
    out_first,
    out_second,
    w_up,
    up_first,
    up_second,
    w_down,
    down_first,
    down_second,
    qkv_average,
):
    local_samples, shard_rows, _ = fields.shape
    dp_size, parts = lax.axis_size("dp"), lax.axis_size("mp")
    dp_index = lax.axis_index("dp")
    place, level, core = mesh_place()
    part = place * 2 + core if crossed else lax.axis_index("mp")
    share_rows = D // dp_size

    def own_share(full, dim):
        return lax.dynamic_slice_in_dim(full, dp_index * share_rows, share_rows, dim)

    var_hot = (var_ids[:, None] == jnp.arange(V, dtype=jnp.int32)[None, :]).astype(f32)
    prepared = prepare_tables(tables, var_hot)
    low = lambda master: master.astype(bf16)
    qkv_low = by_kind(low(w_qkv))
    packed = jnp.concatenate(
        (
            fields[0],
            land_mask[0].astype(f32),
            jnp.broadcast_to(lead_index.astype(f32), (shard_rows, 2)),
            jnp.zeros((shard_rows, 64 - 6), f32),
        ),
        axis=1,
    )
    if crossed:
        (
            x_first, cells, packed, own_out, full, logsum, count, rows_one,
            qkv_t, w_outs, w_ups, w_downs
        ) = start_program(
            packed, prepared, tables[5 * V : 5 * V + 8], norm_gains,
            (qkv_low.T, low(w_out), low(w_up), low(w_down)), (1, 1, 2, 2),
        )
        count = count[0, 0]
    else:
        cells = packed
        answers = targets[0]
        count = lax.psum(jnp.sum(1.0 - cells[:, 4 * V : 4 * V + 4]), ("dp", "mp"))
        w_outs, w_ups, w_downs, qkv_t = [
            lax.all_gather(shard, "mp")
            for shard in (low(w_out), low(w_up), low(w_down), qkv_low.T)
        ]
    gathered = (w_outs.reshape(D, D), w_ups, w_downs.reshape(-1, D), qkv_t.reshape(3 * D, D))
    qkv_local = choose(qkv_t, part)
    leads = cells[0, 4 * V + 4 : 4 * V + 6].astype(jnp.int32)
    ocean = 1.0 - cells[:, 4 * V : 4 * V + 4]
    denom = 2.0 * V * jnp.maximum(count, 1.0)
    first_row = part * shard_rows
    patch_row = (first_row + jnp.arange(shard_rows, dtype=jnp.int32)) // PATCH_COLS
    row_hot = (patch_row[:, None] == jnp.arange(PATCH_ROWS, dtype=jnp.int32)[None, :]).astype(f32)
    lat_rows = jnp.dot(
        row_hot, lat_weights(2 * PATCH_ROWS).reshape(PATCH_ROWS, 2), precision=highest
    )
    lat_pixels = jnp.broadcast_to(lat_rows[:, :, None], (shard_rows, 2, 2)).reshape(shard_rows, 4)
    weighted = jnp.tile(ocean * lat_pixels, (1, V))
    head = tables[5 * V + LEADS + 1 :]
    loss_part = f32(0.0)
    records = []
    for rollout in range(2):
        if rollout == 1:
            cells = jnp.pad(guess, ((0, 0), (0, 64)))
        if rollout == 1 or not crossed:
            lead_row = lax.dynamic_slice_in_dim(tables, 5 * V + leads[rollout], 1, 0)
            x_first, normed = embed_forward(cells, prepared, lead_row, norm_gains)
            rows_one = spread_rows(crossed, normed)
            packed = lax.dot_general(
                rows_one, qkv_local, NT, preferred_element_type=f32
            ).astype(bf16)
            own_out, full, logsum = attend(packed)
        attended = exchange(crossed, own_out, True, 2)
        if crossed and rollout == 0:
            later_targets, attended = tie(targets[0], attended)
            answers = cross(crossed, later_targets)
        x_mid, rows_two, hidden, active, x_last, guess = branch_forward(
            attended, x_first, norm_gains, gathered, head
        )
        miss = guess - answers[rollout]
        loss_part = loss_part + jnp.sum(weighted * miss * miss)
        records.append(
            (cells, x_first, rows_one, packed, full, logsum, attended, x_mid, rows_two,
             hidden, active, x_last, 2.0 * weighted * miss / denom)
        )
    carried = jnp.zeros_like(guess)
    head_total = jnp.zeros_like(head)
    gain_high = jnp.zeros((4, D), f32)
    gain_low = jnp.zeros((2, D), f32)
    table_parts, lead_sums = [], []
    qkv_grad = jnp.zeros((D, qkv_local.shape[0]), f32)
    kept = []

    def sources(index, other, blocked):
        listed = []
        for step in kept:
            listed += [(step[index], blocked), (step[other], not blocked)]
        return listed

    for rollout in (1, 0):
        (cells, x_first, rows_one, packed, full, logsum, attended, x_mid, rows_two,
         hidden, active, x_last, loss_grad) = records[rollout]
        last_low, hidden_grad, mid_grad, mid_low, out_grad, gain_part, head_grad = branch_backward(
            loss_grad + carried, x_last, x_mid, norm_gains, hidden, gathered, head
        )
        head_total = head_total + head_grad
        gain_high = gain_high + gain_part[2:]
        kept.append((attended, rows_two, active, mid_low, hidden_grad, last_low))
        last_turn = crossed and rollout == 0
        if last_turn:
            listed = (
                (sources(2, 5, True), down_pieces, 256),
                (sources(1, 4, False) + sources(0, 3, True), up_out_pieces, 320),
            )
            x, y = lax.rem(place, 2), place // 2
            where = lambda which: jnp.stack((which, x, y)).astype(jnp.int32)
            others = [outer_half(*group, where(1 - core), None) for group in listed]
            out_grad, *others = tie(out_grad, *others)
            others = [shift(other, to_core) for other in others]
        own_grad = exchange(crossed, out_grad, False, 3)
        if last_turn:
            halves = []
            for group, other in zip(listed, others):
                halves += outer_half(*group, where(core), other)
            own_grad, *halves = tie(own_grad, *halves)
            sums = [first_sums(*halves[:2]), first_sums(*halves[2:])]
        packed_grad = attend_back(own_grad, packed, full, logsum)
        if last_turn:
            packed_grad, *sums[0] = tie(packed_grad, *sums[0])
            down_pieces_sum = second_sums(*sums[0], x, y)
        token_grad = exchange(crossed, packed_grad, True, 4)
        if last_turn:
            token_grad, *sums[1] = tie(token_grad, *sums[1])
            up_out_sum = second_sums(*sums[1], x, y)
        qkv_grad = qkv_grad + lax.dot_general(
            rows_one, packed_grad, TN, preferred_element_type=f32
        )
        cells_grad, gain_one, lead_sum, *table_part = entry_backward(
            token_grad, gathered[3], x_first, mid_grad, norm_gains, cells, prepared
        )
        carried = cells_grad[:, : 4 * V]
        gain_low = gain_low + gain_one
        table_parts.append(table_part)
        lead_sums.append(lead_sum)

    def pair(index):
        return (kept[0][index], kept[1][index])

    lead_hots = (leads[:, None] == jnp.arange(8, dtype=jnp.int32)[None, :]).astype(f32)
    lead_hots = jnp.pad(lead_hots, ((0, 6), (0, 0)))
    lead_rows = jnp.pad(jnp.concatenate((lead_sums[1], lead_sums[0])), ((0, 6), (0, 0)))
    query = tables[5 * V + LEADS : 5 * V + LEADS + 1]
    last_rows = table_grads(
        *table_parts, prepared, query, var_hot, lead_hots, lead_rows, gain_low, head_total, gain_high
    )
    qkv_share = by_head(own_qkv_share(crossed, qkv_grad))
    where = dp_index.astype(jnp.int32).reshape(1)
    if crossed:
        shares = (qkv_share, sum_levels(up_out_sum, level), sum_levels(down_pieces_sum, level))
        last_sum, tile = exchange_sum(last_rows, loss_part, *shares)
        masters = (w_qkv, w_out, w_up, w_down)
    else:
        shares = (
            qkv_share,
            outer_plain(pair(0), pair(3), False),
            outer_plain(pair(1), pair(4), True),
            outer_plain(pair(2), pair(5), False),
        )
        squares = sum(jnp.sum(share * share) for share in shares)
        last_sum, loss_sum, squares = lax.psum((last_rows, loss_part, squares), ("dp", "mp"))
        squares = squares + jnp.sum(last_sum * last_sum)
        row = jnp.arange(8, dtype=jnp.int32)[:, None]
        tile = jnp.where(row == 0, squares, jnp.where(row == 1, loss_sum, 0.0))
        tile = jnp.broadcast_to(tile, (8, 128))
        masters = (own_share(w_qkv, 0), own_share(w_out, 1), own_share(w_up, 0), own_share(w_down, 1))
    states = (
        (tables, tables_first, tables_second),
        (norm_gains, gains_first, gains_second),
        (masters[0], qkv_first, qkv_second),
        (masters[1], out_first, out_second),
        (masters[2], up_first, up_second),
        (masters[3], down_first, down_second),
    )
    results = update_all(crossed, where, last_sum, tile, count, shares, states, qkv_average)
    return (results[0][0, 0], results[1][0, 0], *results[2:])


def solution(mesh):
    return jax.shard_map(
        partial(shards, is_crossed(mesh.shape)),
        mesh=mesh,
        in_specs=(
            P("dp", "mp", None),
            P("dp", None, "mp", None),
            P("dp", "mp", None),
            P("dp", None),
            P(),
            P(),
            P(),
            P(),
            P(),
            P(),
            P(),
            P(None, "mp"),
            P("dp", "mp"),
            P("dp", "mp"),
            P("mp", None),
            P("mp", "dp"),
            P("mp", "dp"),
            P(None, "mp"),
            P("dp", "mp"),
            P("dp", "mp"),
            P("mp", None),
            P("mp", "dp"),
            P("mp", "dp"),
            P("dp", "mp"),
        ),
        out_specs=(
            P(),
            P(),
            P(),
            P(),
            P(),
            P(),
            P(),
            P(),
            P("dp", "mp"),
            P("dp", "mp"),
            P("dp", "mp"),
            P("mp", "dp"),
            P("mp", "dp"),
            P("mp", "dp"),
            P("dp", "mp"),
            P("dp", "mp"),
            P("dp", "mp"),
            P("mp", "dp"),
            P("mp", "dp"),
            P("mp", "dp"),
            P("dp", "mp"),
        ),
        check_vma=False,
    )
```

```python
from functools import partial
import math

import jax
import jax.numpy as jnp
from jax import lax
from jax.experimental import pallas as pl
from jax.experimental.pallas import tpu as pltpu
from jax.sharding import PartitionSpec as P

D = 1024
HEADS = 16
HEAD_DIM = 64
V = 48
PATCH_ROWS = 32
PATCH_COLS = 64
LEADS = 7


highest = lax.Precision.HIGHEST
eps_norm = 1e-05
clip_norm = 0.05
beta_first = 0.9
beta_second = 0.999
adam_eps = 1e-08
decay_rate = 0.1
lr_matrix = 0.04
lr_table = 0.1
lr_gain = 0.3
average_keep = 0.9
first_fix = 1.0 - 0.9**10
second_fix = 1.0 - 0.999**10


def layer_norm(values, gain, bias):
    center = values - jnp.mean(values, axis=-1, keepdims=True)
    spread = jnp.mean(center * center, axis=-1, keepdims=True)
    return center * lax.rsqrt(spread + eps_norm) * gain + bias


def lat_weights(pixel_rows):
    row_index = jnp.arange(pixel_rows, dtype=jnp.float32)
    cosine = jnp.cos(((row_index + 0.5) / pixel_rows - 0.5) * math.pi)
    return cosine / jnp.mean(cosine)


bf16 = jnp.bfloat16
f32 = jnp.float32
MESH = pl.DeviceIdType.MESH
NT = (((1,), (1,)), ((), ()))
TN = (((0,), (0,)), ((), ()))
VMEM = pl.BlockSpec(memory_space=pltpu.VMEM)
BIG = 56 * 2**20


def is_crossed(sizes):
    return sizes["dp"] == 4 and sizes["mp"] == 8


def mesh_place():
    dp = lax.axis_index("dp")
    mp = lax.axis_index("mp")
    return dp, mp // 2, lax.rem(mp, 2)


def device_of(dp, level, core):
    return {"dp": dp, "mp": level * 2 + core}


def cross_pairs():
    groups = lax.axis_size("dp")
    pairs = []
    for dp in range(groups):
        for level in range(groups):
            for core in range(2):
                source = (dp * groups + level) * 2 + core
                target = (level * groups + dp) * 2 + core
                pairs.append((source, target))
    return pairs


def cross(crossed, value):
    if not crossed:
        return value
    return lax.ppermute(value, ("dp", "mp"), cross_pairs())


def gather_kernel(x_ref, o_ref, send_sem, recv_sem):
    rows = x_ref.shape[0]
    half = rows // 2
    dp, level, core = mesh_place()
    side = dp + 1 - 2 * lax.rem(dp, 2)
    down = lax.rem(dp + 2, 4)
    far = 3 - dp
    to_side = device_of(side, level, core)
    to_down = device_of(down, level, core)
    to_core = device_of(dp, level, 1 - core)

    def rows_of(owner, who, first, size):
        return pl.ds(pl.multiple_of((owner * 2 + who) * rows + first, half), size)

    barrier = pltpu.get_barrier_semaphore()
    for target in (to_side, to_down, to_core):
        pl.semaphore_signal(barrier, inc=1, device_id=target, device_id_type=MESH)
    pl.semaphore_wait(barrier, 3)

    def send(slot, source, where, target):
        copy = pltpu.make_async_remote_copy(
            src_ref=source,
            dst_ref=o_ref.at[where],
            send_sem=send_sem.at[slot],
            recv_sem=recv_sem.at[slot],
            device_id=target,
            device_id_type=MESH,
        )
        copy.start()
        return copy

    first = x_ref.at[pl.ds(0, half)]
    second = x_ref.at[pl.ds(half, half)]
    side_a = send(0, first, rows_of(dp, core, 0, half), to_side)
    down_b = send(1, second, rows_of(dp, core, half, half), to_down)
    side_b = send(2, second, rows_of(dp, core, half, half), to_side)
    down_a = send(3, first, rows_of(dp, core, 0, half), to_down)
    near = send(4, x_ref, rows_of(dp, core, 0, rows), to_core)
    o_ref[rows_of(dp, core, 0, rows)] = x_ref[...]
    side_a.wait_recv()
    place = rows_of(side, core, 0, half)
    far_a = send(5, o_ref.at[place], place, to_down)
    down_b.wait_recv()
    place = rows_of(down, core, half, half)
    far_b = send(6, o_ref.at[place], place, to_side)
    side_b.wait_recv()
    place = rows_of(side, core, 0, rows)
    near_side = send(7, o_ref.at[place], place, to_core)
    down_a.wait_recv()
    place = rows_of(down, core, 0, rows)
    near_down = send(8, o_ref.at[place], place, to_core)
    far_a.wait_recv()
    far_b.wait_recv()
    place = rows_of(far, core, 0, rows)
    near_far = send(9, o_ref.at[place], place, to_core)
    for copy in (near, near_side, near_down, near_far):
        copy.wait_recv()
    for copy in (side_a, down_b, side_b, down_a, near, far_a, far_b, near_side, near_down, near_far):
        copy.wait_send()


def spread_rows(crossed, normed):
    if not crossed:
        return lax.all_gather(normed, "mp", axis=0, tiled=True)
    rows, width = normed.shape
    return pl.pallas_call(
        gather_kernel,
        out_shape=jax.ShapeDtypeStruct((8 * rows, width), normed.dtype),
        in_specs=[VMEM],
        out_specs=VMEM,
        scratch_shapes=[pltpu.SemaphoreType.DMA((10,)), pltpu.SemaphoreType.DMA((10,))],
        compiler_params=pltpu.CompilerParams(
            collective_id=1, has_side_effects=True, vmem_limit_bytes=BIG
        ),
        name="gather_rows",
    )(normed)


def exchange_kernel(to_columns, rows, width, x_ref, o_ref, send_sem, recv_sem):
    dp, level, core = mesh_place()
    me = dp * 2 + core
    barrier = pltpu.get_barrier_semaphore()
    others = []
    for step in (7, 6, 5, 4, 3, 2, 1):
        part = lax.rem(me + step, 8)
        others.append((step, part, device_of(part // 2, level, lax.rem(part, 2))))
    for step, part, target in others:
        pl.semaphore_signal(barrier, inc=1, device_id=target, device_id_type=MESH)
    pl.semaphore_wait(barrier, 7)

    def row_block(ref, part):
        return ref.at[pl.ds(pl.multiple_of(part * rows, rows), rows), :]

    def column_block(ref, part):
        return ref.at[:, pl.ds(pl.multiple_of(part * width, width), width)]

    source_block, target_block = (
        (row_block, column_block) if to_columns else (column_block, row_block)
    )
    copies = []
    for step, part, target in others:
        copy = pltpu.make_async_remote_copy(
            src_ref=source_block(x_ref, part),
            dst_ref=target_block(o_ref, me),
            send_sem=send_sem.at[step],
            recv_sem=recv_sem.at[step],
            device_id=target,
            device_id_type=MESH,
        )
        copy.start()
        copies.append(copy)
    target_block(o_ref, me)[...] = source_block(x_ref, me)[...]
    for copy in copies:
        copy.wait()


def exchange(crossed, value, to_columns, number):
    parts = lax.axis_size("mp")
    if to_columns:
        rows, width = value.shape[0] // parts, value.shape[1]
        shape = (rows, width * parts)
    else:
        rows, width = value.shape[0], value.shape[1] // parts
        shape = (rows * parts, width)
    if not crossed:
        split, joined = (0, 1) if to_columns else (1, 0)
        return lax.all_to_all(value, "mp", split_axis=split, concat_axis=joined, tiled=True)
    return pl.pallas_call(
        partial(exchange_kernel, to_columns, rows, width),
        out_shape=jax.ShapeDtypeStruct(shape, value.dtype),
        in_specs=[VMEM],
        out_specs=VMEM,
        scratch_shapes=[pltpu.SemaphoreType.DMA((8,)), pltpu.SemaphoreType.DMA((8,))],
        compiler_params=pltpu.CompilerParams(
            collective_id=number, has_side_effects=True, vmem_limit_bytes=BIG
        ),
        name="exchange_parts",
    )(value)


def pick_head(value, head, heads):
    if heads == 1:
        return value
    lane = lax.broadcasted_iota(jnp.int32, value.shape, 1) // HEAD_DIM
    return jnp.where(lane == head, value, jnp.zeros_like(value))


def attend_rows(heads, queries, k_ref, vt_ref):
    queries = queries * bf16(HEAD_DIM**-0.5)
    keys = k_ref[...]
    outs, sums = [], []
    for head in range(heads):
        scores = lax.dot_general(
            keys, pick_head(queries, head, heads), NT, preferred_element_type=f32
        )
        largest = jnp.max(scores, axis=0, keepdims=True)
        raised = jnp.exp(scores - largest)
        total = jnp.sum(raised, axis=0, keepdims=True)
        probs = (raised * (1.0 / total)).astype(bf16)
        values = vt_ref[head * HEAD_DIM : (head + 1) * HEAD_DIM, :]
        outs.append(jnp.dot(values, probs, preferred_element_type=f32))
        sums.append(largest + jnp.log(total))
    flipped = outs[0] if heads == 1 else jnp.concatenate(outs, axis=0)
    return flipped.T, sums


def attend_kernel(heads, q_ref, k_ref, v_ref, o_ref, full_ref, lse_ref, vt_ref):
    @pl.when(pl.program_id(0) == 0)
    def _():
        vt_ref[...] = v_ref[...].T

    full, sums = attend_rows(heads, q_ref[...], k_ref, vt_ref)
    for head in range(heads):
        lse_ref[head : head + 1, :] = sums[head]
    full_ref[...] = full
    o_ref[...] = full.astype(bf16)


def attend(packed):
    total, width = packed.shape[0], packed.shape[1] // 3
    heads = width // HEAD_DIM
    block = min(512, total)
    row_block = pl.BlockSpec((block, width), lambda i: (i, 0))
    return pl.pallas_call(
        partial(attend_kernel, heads),
        grid=(total // block,),
        out_shape=(
            jax.ShapeDtypeStruct((total, width), bf16),
            jax.ShapeDtypeStruct((total, width), f32),
            jax.ShapeDtypeStruct((heads, total), f32),
        ),
        in_specs=[
            row_block,
            pl.BlockSpec((total, width), lambda i: (0, 0)),
            pl.BlockSpec((total, width), lambda i: (0, 0)),
        ],
        out_specs=[row_block, row_block, pl.BlockSpec((heads, block), lambda i: (0, i))],
        scratch_shapes=[pltpu.VMEM((width, total), bf16)],
        compiler_params=pltpu.CompilerParams(vmem_limit_bytes=BIG),
        cost_estimate=pl.CostEstimate(
            flops=16 * total * total * width,
            bytes_accessed=10 * total * width,
            transcendentals=heads * total * total,
        ),
        name="attend",
    )(packed[:, :width], packed[:, width : 2 * width], packed[:, 2 * width :])


def attend_back_rows(
    heads, chunk, queries, grads, full, sums, k_ref, v_ref, kt_ref, dk_sum, dv_sum
):
    total = k_ref.shape[0]
    scale = HEAD_DIM**-0.5
    products = (grads.astype(f32) * full).T
    query_heads = [pick_head(queries, head, heads) for head in range(heads)]
    grad_heads = [pick_head(grads, head, heads) for head in range(heads)]
    inner = [
        jnp.sum(products[head * HEAD_DIM : (head + 1) * HEAD_DIM], axis=0, keepdims=True) * scale
        for head in range(heads)
    ]
    query_grads = [None] * heads
    for start in range(0, total, chunk):
        rows = slice(start, start + chunk)
        keys = k_ref[rows, :]
        values = v_ref[rows, :]
        value_part = None
        key_part = None
        for head in range(heads):
            scores = lax.dot_general(
                keys, query_heads[head] * bf16(scale), NT, preferred_element_type=f32
            )
            probs = jnp.exp(scores - sums[head])
            prob_grad = lax.dot_general(
                values, grad_heads[head] * bf16(scale), NT, preferred_element_type=f32
            )
            score_grad = (probs * (prob_grad - inner[head])).astype(bf16)
            one = jnp.dot(probs.astype(bf16), grad_heads[head], preferred_element_type=f32)
            two = jnp.dot(score_grad, query_heads[head], preferred_element_type=f32)
            value_part = one if value_part is None else value_part + one
            key_part = two if key_part is None else key_part + two
            three = jnp.dot(
                kt_ref[head * HEAD_DIM : (head + 1) * HEAD_DIM, rows],
                score_grad,
                preferred_element_type=f32,
            )
            query_grads[head] = three if query_grads[head] is None else query_grads[head] + three
        dv_sum[rows, :] += value_part
        dk_sum[rows, :] += key_part
    flipped = query_grads[0] if heads == 1 else jnp.concatenate(query_grads, axis=0)
    return flipped.T.astype(bf16)


def attend_back_kernel(
    heads, q_ref, do_ref, full_ref, lse_ref, k_ref, v_ref, dq_ref, dk_ref, dv_ref, kt_ref, dk_sum, dv_sum
):
    step = pl.program_id(0)

    @pl.when(step == 0)
    def _():
        kt_ref[...] = k_ref[...].T
        dk_sum[...] = jnp.zeros_like(dk_sum)
        dv_sum[...] = jnp.zeros_like(dv_sum)

    sums = [lse_ref[head : head + 1, :] for head in range(heads)]
    dq_ref[...] = attend_back_rows(
        heads, min(1024, k_ref.shape[0]), q_ref[...], do_ref[...], full_ref[...], sums,
        k_ref, v_ref, kt_ref, dk_sum, dv_sum,
    )

    @pl.when(step == pl.num_programs(0) - 1)
    def _():
        dk_ref[...] = dk_sum[...].astype(bf16)
        dv_ref[...] = dv_sum[...].astype(bf16)


def attend_back(grad_out, packed, full, logsum):
    total, width = grad_out.shape
    heads = width // HEAD_DIM
    block = min(256, total)
    row_block = pl.BlockSpec((block, width), lambda i: (i, 0))
    whole = pl.BlockSpec((total, width), lambda i: (0, 0))
    query_grad, key_grad, value_grad = pl.pallas_call(
        partial(attend_back_kernel, heads),
        grid=(total // block,),
        out_shape=(jax.ShapeDtypeStruct((total, width), bf16),) * 3,
        in_specs=[
            row_block,
            row_block,
            row_block,
            pl.BlockSpec((heads, block), lambda i: (0, i)),
            whole,
            whole,
        ],
        out_specs=[row_block, whole, whole],
        scratch_shapes=[
            pltpu.VMEM((width, total), bf16),
            pltpu.VMEM((total, width), f32),
            pltpu.VMEM((total, width), f32),
        ],
        compiler_params=pltpu.CompilerParams(vmem_limit_bytes=BIG),
        cost_estimate=pl.CostEstimate(
            flops=40 * total * total * width,
            bytes_accessed=16 * total * width,
            transcendentals=heads * total * total,
        ),
        name="attend_back",
    )(
        packed[:, :width],
        grad_out,
        full,
        logsum,
        packed[:, width : 2 * width],
        packed[:, 2 * width :],
    )
    return jnp.concatenate((query_grad, key_grad, value_grad), axis=1)


def normed_parts(values):
    center = values - jnp.mean(values, axis=-1, keepdims=True)
    spread = jnp.mean(center * center, axis=-1, keepdims=True)
    inverse = lax.rsqrt(spread + eps_norm)
    return center * inverse, inverse


def norm_grad(unit, inverse, gain, grad):
    scaled = grad * gain
    middle = jnp.mean(scaled, axis=-1, keepdims=True)
    along = jnp.mean(scaled * unit, axis=-1, keepdims=True)
    gain_grad = jnp.sum(grad * unit, axis=0, keepdims=True)
    bias_grad = jnp.sum(grad, axis=0, keepdims=True)
    return inverse * (scaled - middle - unit * along), gain_grad, bias_grad


def gauss_share(values):
    return 0.5 * (1.0 + lax.erf(values * (0.5**0.5)))


def branch_kernel(
    o_ref, x0_ref, gains_ref, out_ref, up_ref, down_ref, head_ref,
    x1_ref, h2_ref, g_ref, act_ref, x2_ref, pred_ref,
):
    step = pl.program_id(0)

    @pl.when(step == 0)
    def _():
        x1_ref[...] = x0_ref[...] + jnp.dot(
            o_ref[...], out_ref[...], preferred_element_type=f32
        )
        unit, _ = normed_parts(x1_ref[...])
        h2_ref[...] = (unit * gains_ref[2:3, :] + gains_ref[3:4, :]).astype(bf16)
        x2_ref[...] = x1_ref[...]

    hidden = jnp.dot(h2_ref[...], up_ref[0], preferred_element_type=f32)
    g_ref[...] = hidden
    active = (hidden * gauss_share(hidden)).astype(bf16)
    act_ref[0, 0] = active
    x2_ref[...] += jnp.dot(active, down_ref[...], preferred_element_type=f32)

    @pl.when(step == pl.num_programs(0) - 1)
    def _():
        unit, _ = normed_parts(x2_ref[...])
        last = unit * gains_ref[4:5, :] + gains_ref[5:6, :]
        pred_ref[...] = lax.dot_general(
            last, head_ref[...], NT, precision=highest, preferred_element_type=f32
        )


def weight_specs(w_out, w_up, w_down):
    _, width, units = w_up.shape
    return (
        pl.BlockSpec(w_out.shape, lambda i: (0, 0)),
        pl.BlockSpec((1, width, units), lambda i: (i, 0, 0)),
        pl.BlockSpec((units, width), lambda i: (i, 0)),
    )


def branch_forward(attended, x_first, norm_gains, gathered, head):
    w_out, w_up, w_down, _ = gathered
    rows, width = x_first.shape
    parts, units = w_up.shape[0], w_up.shape[2]
    fixed = lambda shape: pl.BlockSpec(shape, lambda i: (0, 0))
    by_units = pl.BlockSpec((rows, units), lambda i: (0, i))
    by_core = pl.BlockSpec((1, 1, rows, units), lambda i: (i % 2, i // 2, 0, 0))
    columns = head.shape[0]
    flops = 2 * rows * (width * width + 2 * width * parts * units + 6 * width * columns)
    return pl.pallas_call(
        branch_kernel,
        grid=(parts,),
        out_shape=(
            jax.ShapeDtypeStruct((rows, width), f32),
            jax.ShapeDtypeStruct((rows, width), bf16),
            jax.ShapeDtypeStruct((rows, parts * units), f32),
            jax.ShapeDtypeStruct((2, parts // 2, rows, units), bf16),
            jax.ShapeDtypeStruct((rows, width), f32),
            jax.ShapeDtypeStruct((rows, columns), f32),
        ),
        in_specs=[
            fixed((rows, width)),
            fixed((rows, width)),
            fixed(norm_gains.shape),
            *weight_specs(w_out, w_up, w_down),
            fixed(head.shape),
        ],
        out_specs=[
            fixed((rows, width)),
            fixed((rows, width)),
            by_units,
            by_core,
            fixed((rows, width)),
            fixed((rows, columns)),
        ],
        compiler_params=pltpu.CompilerParams(vmem_limit_bytes=BIG),
        cost_estimate=pl.CostEstimate(
            flops=flops,
            bytes_accessed=4 * width * parts * units + 6 * rows * parts * units,
            transcendentals=rows * parts * units,
        ),
        name="branch_forward",
    )(attended, x_first, norm_gains, w_out, w_up, w_down, head)


def branch_back_kernel(
    dpred_ref, x2_ref, x1_ref, gains_ref, g_ref, out_ref, up_ref, down_ref, head_ref,
    dx2_ref, dg_ref, dx1_ref, low_ref, do_ref, gain_ref, dhead_ref,
    wide_ref, sum_ref,
):
    step = pl.program_id(0)

    @pl.when(step == 0)
    def _():
        grad = dpred_ref[...]
        unit, inverse = normed_parts(x2_ref[...])
        gain = gains_ref[4:5, :]
        last = unit * gain + gains_ref[5:6, :]
        dhead_ref[...] = lax.dot_general(
            grad, last, TN, precision=highest, preferred_element_type=f32
        )
        row_grad = jnp.dot(grad, head_ref[...], precision=highest, preferred_element_type=f32)
        wide, gain_grad, bias_grad = norm_grad(unit, inverse, gain, row_grad)
        gain_ref[...] = jnp.zeros_like(gain_ref)
        gain_ref[4:5, :] = gain_grad
        gain_ref[5:6, :] = bias_grad
        wide_ref[...] = wide
        dx2_ref[...] = wide.astype(bf16)
        sum_ref[...] = jnp.zeros_like(sum_ref)

    active_grad = lax.dot_general(dx2_ref[...], down_ref[...], NT, preferred_element_type=f32)
    hidden = g_ref[...]
    slope = gauss_share(hidden) + hidden * (
        jnp.exp(-0.5 * hidden * hidden) * (2.0 * math.pi) ** -0.5
    )
    hidden_grad = (active_grad * slope).astype(bf16)
    dg_ref[0, 0] = hidden_grad
    sum_ref[...] += lax.dot_general(hidden_grad, up_ref[0], NT, preferred_element_type=f32)

    @pl.when(step == pl.num_programs(0) - 1)
    def _():
        unit, inverse = normed_parts(x1_ref[...])
        middle, gain_grad, bias_grad = norm_grad(unit, inverse, gains_ref[2:3, :], sum_ref[...])
        gain_ref[2:3, :] = gain_grad
        gain_ref[3:4, :] = bias_grad
        middle = wide_ref[...] + middle
        dx1_ref[...] = middle
        low_ref[...] = middle.astype(bf16)
        total = lax.dot_general(low_ref[...], out_ref[...], NT, preferred_element_type=f32)
        do_ref[...] = total.astype(bf16)


def branch_backward(pred_grad, x_last, x_mid, norm_gains, hidden, gathered, head):
    w_out, w_up, w_down, _ = gathered
    rows, width = x_last.shape
    parts, units = w_up.shape[0], w_up.shape[2]
    fixed = lambda shape: pl.BlockSpec(shape, lambda i: (0, 0))
    by_units = pl.BlockSpec((rows, units), lambda i: (0, i))
    by_core = pl.BlockSpec((1, 1, rows, units), lambda i: (i % 2, i // 2, 0, 0))
    columns = head.shape[0]
    wide = (rows, width)
    flops = 2 * rows * (width * width + 2 * width * parts * units + 12 * width * columns)
    return pl.pallas_call(
        branch_back_kernel,
        grid=(parts,),
        out_shape=(
            jax.ShapeDtypeStruct(wide, bf16),
            jax.ShapeDtypeStruct((2, parts // 2, rows, units), bf16),
            jax.ShapeDtypeStruct(wide, f32),
            jax.ShapeDtypeStruct(wide, bf16),
            jax.ShapeDtypeStruct(wide, bf16),
            jax.ShapeDtypeStruct((6, width), f32),
            jax.ShapeDtypeStruct((columns, width), f32),
        ),
        in_specs=[
            fixed((rows, columns)),
            fixed(wide),
            fixed(wide),
            fixed(norm_gains.shape),
            by_units,
            *weight_specs(w_out, w_up, w_down),
            fixed(head.shape),
        ],
        out_specs=[
            fixed(wide),
            by_core,
            fixed(wide),
            fixed(wide),
            fixed(wide),
            fixed((6, width)),
            fixed((columns, width)),
        ],
        scratch_shapes=[pltpu.VMEM(wide, f32), pltpu.VMEM(wide, f32)],
        compiler_params=pltpu.CompilerParams(vmem_limit_bytes=BIG),
        cost_estimate=pl.CostEstimate(
            flops=flops,
            bytes_accessed=4 * width * parts * units + 6 * rows * parts * units,
            transcendentals=2 * rows * parts * units,
        ),
        name="branch_backward",
    )(pred_grad, x_last, x_mid, norm_gains, hidden, w_out, w_up, w_down, head)


def plane_parts(me):
    return [(move, lax.rem(me + move, 8)) for move in (7, 6, 5, 4, 3, 2, 1)]


def swap_kernel(*refs):
    value_ref, act_ref, dg_ref, o_ref, dx2_ref, h2_ref, dx1_ref = refs[:7]
    rows_ref, act_out, dg_out, o_out, dx2_out, h2_out, dx1_out = refs[7:14]
    send_sem, recv_sem, own_sem = refs[14:]
    dp, level, core = mesh_place()
    me = dp * 2 + core
    rows, width = value_ref.shape[0], value_ref.shape[1] // 8
    near = device_of(dp, level, 1 - core)
    barrier = pltpu.get_barrier_semaphore()
    others = [
        (part, device_of(part // 2, level, lax.rem(part, 2))) for _, part in plane_parts(me)
    ]
    for _, target in others:
        pl.semaphore_signal(barrier, inc=1, device_id=target, device_id_type=MESH)
    pl.semaphore_wait(barrier, 7)
    started = []

    def send(source, target_ref, target):
        slot = len(started)
        copy = pltpu.make_async_remote_copy(
            src_ref=source,
            dst_ref=target_ref,
            send_sem=send_sem.at[slot],
            recv_sem=recv_sem.at[slot],
            device_id=target,
            device_id_type=MESH,
        )
        copy.start()
        started.append(copy)

    def row_block(part):
        return rows_ref.at[pl.ds(pl.multiple_of(part * rows, rows), rows), :]

    def column_block(ref, part):
        return ref.at[:, pl.ds(pl.multiple_of(part * width, width), width)]

    for part, target in others:
        send(column_block(value_ref, part), row_block(me), target)
    locals_ = []

    def keep(source, target_ref):
        copy = pltpu.make_async_copy(source, target_ref, own_sem.at[len(locals_)])
        copy.start()
        locals_.append(copy)

    for source, out in ((act_ref, act_out), (dg_ref, dg_out)):
        send(source.at[1 - core], out.at[1], near)
        keep(source.at[core], out.at[0])
    for index in range(4):
        send(column_block(o_ref, index * 2 + 1 - core), o_out.at[1, index], near)
        keep(column_block(o_ref, index * 2 + core), o_out.at[0, index])
    for source, out in ((dx2_ref, dx2_out), (h2_ref, h2_out), (dx1_ref, dx1_out)):
        send(source, out, near)
    row_block(me)[...] = column_block(value_ref, me)[...]
    for copy in started:
        copy.wait()
    for copy in locals_:
        copy.wait()


def exchange_swap(value, act, dg, attended, dx2, h2, dx1):
    rows, width = value.shape
    anywhere = pl.BlockSpec(memory_space=pl.ANY)
    outs = [
        (8 * rows, width // 8), act.shape, dg.shape, (2, 4, rows, width // 8),
        dx2.shape, h2.shape, dx1.shape,
    ]
    return pl.pallas_call(
        swap_kernel,
        out_shape=[jax.ShapeDtypeStruct(shape, bf16) for shape in outs],
        in_specs=[VMEM] * 7,
        out_specs=[VMEM] + [anywhere] * 6,
        scratch_shapes=[
            pltpu.SemaphoreType.DMA((16,)),
            pltpu.SemaphoreType.DMA((16,)),
            pltpu.SemaphoreType.DMA((6,)),
        ],
        compiler_params=pltpu.CompilerParams(
            collective_id=3, has_side_effects=True, vmem_limit_bytes=BIG
        ),
        name="exchange_swap",
    )(value, act, dg, attended, dx2, h2, dx1)


wait_one, wait_two, pieces_at = 2, 4, 9
turns = 14


def finish_kernel(*refs):
    steps = (refs[0:9], refs[9:18])
    qkv_ref, do_ref, full_ref, lse_ref, rows_ref, prev_ref = refs[18:24]
    token_out, share_ref, down_ref, up_out_ref = refs[24:28]
    (dqkv_ref, kt_ref, dk_sum, dv_sum, held_ref, send_a, keep_a, one_a, two_a, own_a, deep_a,
     send_b, keep_b, one_b, two_b, own_b, deep_b, piece_send, piece_recv, piece_own, landing_ref,
     one_send, one_recv, two_send, two_recv, deep_send, deep_recv, part_send, part_recv,
     piece_send_sem, piece_recv_sem, cross_sem, own_sem) = refs[28:]
    groups = (
        (send_a, keep_a, one_a, two_a, own_a, deep_a, down_ref),
        (send_b, keep_b, one_b, two_b, own_b, deep_b, up_out_ref),
    )
    turn = pl.program_id(0)
    dp, level, core = mesh_place()
    me = dp * 2 + core
    x, y = lax.rem(dp, 2), dp // 2
    side, down = dp + 1 - 2 * x, lax.rem(dp + 2, 4)
    across = device_of(level, dp, core)
    width = do_ref.shape[1]
    heads = width // HEAD_DIM
    rows = do_ref.shape[0] // 8
    others = [
        (move, part, device_of(part // 2, level, lax.rem(part, 2))) for move, part in plane_parts(me)
    ]

    def remote(source, target_ref, send_sem, recv_sem, target):
        return pltpu.make_async_remote_copy(
            src_ref=source,
            dst_ref=target_ref,
            send_sem=send_sem,
            recv_sem=recv_sem,
            device_id=target,
            device_id_type=MESH,
        )

    def place_of(index):
        depth = lax.rem(index, 2) * 2 + index // 2
        early = 1 - depth // 2
        return depth, early

    def first_copy(group, index):
        send_ref, _, one_ref = groups[group][:3]
        depth, early = place_of(index)
        slot = index * 2 + group
        target = device_of(early * side + (1 - early) * down, level, core)
        return remote(
            send_ref.at[depth], one_ref.at[depth], one_send.at[slot], one_recv.at[slot], target
        )

    def second_copy(group, index):
        _, keep_ref, _, two_ref = groups[group][:4]
        depth, early = place_of(index)
        slot = index * 2 + group
        which = early * (1 - y) + (1 - early) * (1 - x)
        target = device_of(early * down + (1 - early) * side, level, core)
        return remote(
            keep_ref.at[depth, which], two_ref.at[depth], two_send.at[slot], two_recv.at[slot], target
        )

    def deep_copy(group, index):
        _, keep_ref, _, _, _, deep_ref = groups[group][:6]
        depth, early = place_of(index)
        slot = index * 2 + group
        which = early * y + (1 - early) * x
        place = lax.rem(level + 7 - depth, 4)
        return remote(
            keep_ref.at[depth, which],
            deep_ref.at[place],
            deep_send.at[slot],
            deep_recv.at[group * 4 + place],
            device_of(dp, depth, core),
        )

    def part_copy(move, part, target):
        return remote(
            dqkv_ref.at[pl.ds(pl.multiple_of(part * rows, rows), rows), :],
            token_out.at[:, pl.ds(pl.multiple_of(me * 3 * width, 3 * width), 3 * width)],
            part_send.at[move],
            part_recv.at[move],
            target,
        )

    def piece_copy(index):
        place = lax.rem(level + 7 - index, 4)
        return remote(
            piece_send.at[index],
            piece_recv.at[place],
            piece_send_sem.at[index],
            piece_recv_sem.at[place],
            device_of(dp, index, core),
        )

    own_part = pltpu.make_async_copy(
        dqkv_ref.at[pl.ds(pl.multiple_of(me * rows, rows), rows), :],
        token_out.at[:, pl.ds(pl.multiple_of(me * 3 * width, 3 * width), 3 * width)],
        own_sem,
    )
    crossing = remote(piece_own, landing_ref, cross_sem.at[0], cross_sem.at[1], across)

    @pl.when(turn == 0)
    def _():
        barrier = pltpu.get_barrier_semaphore()
        deep = [device_of(dp, lax.rem(level + move, 4), core) for move in (1, 2, 3)]
        for target in [target for _, _, target in others] + deep:
            pl.semaphore_signal(barrier, inc=1, device_id=target, device_id_type=MESH)

        @pl.when(dp != level)
        def _():
            pl.semaphore_signal(barrier, inc=1, device_id=across, device_id_type=MESH)
            pl.semaphore_wait(barrier, 11)

        @pl.when(dp == level)
        def _():
            pl.semaphore_wait(barrier, 10)

        kt_ref[...] = qkv_ref[:, width : 2 * width].T
        dk_sum[...] = jnp.zeros_like(dk_sum)
        dv_sum[...] = jnp.zeros_like(dv_sum)

    def summed(lefts, rights):
        total = None
        for left, right in zip(lefts, rights):
            part = lax.dot_general(left, right, TN, preferred_element_type=f32)
            total = part if total is None else total + part
        return total

    for group in range(2):
        send_ref, keep_ref, one_ref, two_ref, own_ref, deep_ref, _ = groups[group]
        height = keep_ref.shape[2]

        @pl.when((lax.rem(turn + group, 2) == 0) & (turn < 8))
        def _(group=group, send_ref=send_ref, keep_ref=keep_ref, height=height):
            index = turn // 2
            depth, early = place_of(index)
            lefts, rights, smalls, wides = [], [], [], []
            for act, dg, o, dx2, dx2_near, h2, h2_near, dx1, dx1_near in steps:
                for source in range(2):
                    if group == 0:
                        lefts.append(act[source, 0])
                        rights.append((dx2, dx2_near)[source][...])
                    else:
                        lefts.append(dg[source, 0])
                        rights.append((h2, h2_near)[source][...])
                        smalls.append(o[source, 0])
                        wides.append((dx1, dx1_near)[source][...])
            size = rights[0].shape[1] // 4
            tops = summed(lefts, rights)
            for split in range(4):
                held_ref[split, : tops.shape[0], :] = tops[:, split * size : (split + 1) * size].astype(bf16)
            if group == 1:
                ends = summed(smalls, wides)
                for split in range(4):
                    held_ref[split, tops.shape[0] : height, :] = ends[
                        :, split * size : (split + 1) * size
                    ].astype(bf16)
            for which in range(2):
                moved = early * (which * 2 + 1 - x) + (1 - early) * ((1 - y) * 2 + which)
                stays = early * (which * 2 + x) + (1 - early) * (y * 2 + which)
                send_ref[depth, which] = held_ref[moved, :height, :]
                keep_ref[depth, which] = held_ref[stays, :height, :]
            first_copy(group, index).start()

        after = turn - wait_one

        @pl.when((lax.rem(after + 8 + group, 2) == 0) & (after >= 0) & (after < 8))
        def _(group=group, keep_ref=keep_ref, one_ref=one_ref):
            index = after // 2
            depth, _ = place_of(index)
            first_copy(group, index).wait_recv()
            for which in range(2):
                keep_ref[depth, which] = (
                    keep_ref[depth, which].astype(f32) + one_ref[depth, which].astype(f32)
                ).astype(bf16)
            second_copy(group, index).start()

        later = turn - wait_two

        @pl.when((lax.rem(later + 8 + group, 2) == 0) & (later >= 0) & (later < 8))
        def _(group=group, keep_ref=keep_ref, two_ref=two_ref, own_ref=own_ref):
            index = later // 2
            depth, early = place_of(index)
            second_copy(group, index).wait_recv()
            which = early * y + (1 - early) * x
            total = keep_ref[depth, which].astype(f32) + two_ref[depth].astype(f32)

            @pl.when(depth == level)
            def _():
                own_ref[...] = total

            @pl.when(depth != level)
            def _():
                keep_ref[depth, which] = total.astype(bf16)
                deep_copy(group, index).start()

    @pl.when(turn < 8)
    def _():
        where = pl.ds(pl.multiple_of(turn * rows, rows), rows)
        sums = [lse_ref[head : head + 1, where] for head in range(heads)]
        dqkv_ref[where, :width] = attend_back_rows(
            heads, 512, qkv_ref[where, :width], do_ref[where, :], full_ref[where, :], sums,
            qkv_ref.at[:, width : 2 * width], qkv_ref.at[:, 2 * width :], kt_ref, dk_sum, dv_sum,
        )

    @pl.when(turn == 8)
    def _():
        dqkv_ref[:, width : 2 * width] = dk_sum[...].astype(bf16)
        dqkv_ref[:, 2 * width :] = dv_sum[...].astype(bf16)
        for other in others:
            part_copy(*other).start()
        own_part.start()

    for index in range(4):

        @pl.when(turn == pieces_at + index)
        def _(index=index):
            piece = prev_ref[...] + lax.dot_general(
                rows_ref[...], dqkv_ref[...], TN, preferred_element_type=f32
            )

            @pl.when(level == index)
            def _():
                piece_own[...] = piece

            @pl.when(level != index)
            def _():
                piece_send[index] = piece.astype(bf16)
                piece_copy(index).start()

    @pl.when(turn == turns - 1)
    def _():
        for place in range(3):
            remote(
                piece_send.at[0], piece_recv.at[place], piece_send_sem.at[0],
                piece_recv_sem.at[place], across,
            ).wait_recv()
        piece_own[...] += (
            piece_recv[0].astype(f32) + piece_recv[1].astype(f32) + piece_recv[2].astype(f32)
        )

        @pl.when(dp != level)
        def _():
            crossing.start()

        for group in range(2):
            _, keep_ref, _, _, own_ref, deep_ref, result_ref = groups[group]
            for place in range(3):
                remote(
                    keep_ref.at[0, 0], deep_ref.at[place], deep_send.at[0],
                    deep_recv.at[group * 4 + place], across,
                ).wait_recv()
            result_ref[...] = own_ref[...] + (
                deep_ref[0].astype(f32) + deep_ref[1].astype(f32) + deep_ref[2].astype(f32)
            )
        for other in others:
            part_copy(*other).wait()
        own_part.wait()
        for index in range(4):
            depth = (index % 2) * 2 + index // 2
            for group in range(2):
                first_copy(group, index).wait_send()
                second_copy(group, index).wait_send()

                @pl.when(depth != level)
                def _(group=group, index=index):
                    deep_copy(group, index).wait_send()

            @pl.when(level != index)
            def _(index=index):
                piece_copy(index).wait_send()

        @pl.when(dp != level)
        def _():
            crossing.wait()
            share_ref[...] = landing_ref[...]

        @pl.when(dp == level)
        def _():
            share_ref[...] = piece_own[...]


def finish_program(kept, packed, own_grad, full, logsum, rows_one, earlier):
    rows, width = own_grad.shape[0] // 8, own_grad.shape[1]
    once = lambda shape: pl.BlockSpec(
        shape, lambda i: (0,) * len(shape), pipeline_mode=pl.Buffered(1)
    )

    def chunk(shape):
        def where(i):
            index = jnp.minimum(i // 2, 3)
            return 0, lax.rem(index, 2) * 2 + index // 2, 0, 0

        return pl.BlockSpec((2, 1) + shape, where)

    in_specs, operands = [], []
    for act, dg, o, dx2, dx2_near, h2, h2_near, dx1, dx1_near in kept:
        operands += [act, dg, o, dx2, dx2_near, h2, h2_near, dx1, dx1_near]
        in_specs += [chunk(act.shape[2:]), chunk(dg.shape[2:]), chunk(o.shape[2:])]
        in_specs += [once(dx2.shape)] * 6
    piece = lambda i: jnp.clip(i - pieces_at, 0, 3)
    in_specs += [
        once(packed.shape),
        once(own_grad.shape),
        once(full.shape),
        once(logsum.shape),
        pl.BlockSpec((8 * rows, D // 4), lambda i: (0, piece(i))),
        pl.BlockSpec((D // 4, 3 * width), lambda i: (piece(i), 0)),
    ]
    operands += [packed, own_grad, full, logsum, rows_one, earlier]
    fixed = lambda shape: pl.BlockSpec(shape, lambda i: (0, 0))
    units = kept[0][0].shape[3]
    heights = (units, units + width)
    share = D // 4
    scratch = [
        pltpu.VMEM((8 * rows, 3 * width), bf16),
        pltpu.VMEM((width, 8 * rows), bf16),
        pltpu.VMEM((8 * rows, width), f32),
        pltpu.VMEM((8 * rows, width), f32),
        pltpu.VMEM((4, heights[1], share), bf16),
    ]
    for height in heights:
        scratch += [
            pltpu.VMEM((4, 2, height, share), bf16),
            pltpu.VMEM((4, 2, height, share), bf16),
            pltpu.VMEM((4, 2, height, share), bf16),
            pltpu.VMEM((4, height, share), bf16),
            pltpu.VMEM((height, share), f32),
            pltpu.VMEM((3, height, share), bf16),
        ]
    scratch += [
        pltpu.VMEM((4, share, 3 * width), bf16),
        pltpu.VMEM((3, share, 3 * width), bf16),
        pltpu.VMEM((share, 3 * width), f32),
        pltpu.VMEM((share, 3 * width), f32),
    ]
    scratch += [pltpu.SemaphoreType.DMA((8,))] * 8
    scratch += [
        pltpu.SemaphoreType.DMA((4,)),
        pltpu.SemaphoreType.DMA((4,)),
        pltpu.SemaphoreType.DMA((2,)),
        pltpu.SemaphoreType.DMA,
    ]
    return pl.pallas_call(
        finish_kernel,
        grid=(turns,),
        out_shape=[
            jax.ShapeDtypeStruct((rows, 24 * width), bf16),
            jax.ShapeDtypeStruct((share, 3 * width), f32),
            jax.ShapeDtypeStruct((heights[0], share), f32),
            jax.ShapeDtypeStruct((heights[1], share), f32),
        ],
        in_specs=in_specs,
        out_specs=[
            pl.BlockSpec(memory_space=pl.ANY),
            fixed((share, 3 * width)),
            fixed((heights[0], share)),
            fixed((heights[1], share)),
        ],
        scratch_shapes=scratch,
        compiler_params=pltpu.CompilerParams(
            collective_id=4, has_side_effects=True, vmem_limit_bytes=60 * 2**20
        ),
        name="finish_program",
    )(*operands)


def tie(*values):
    return lax.optimization_barrier(values)


def choose(value, index, axis=0):
    return lax.dynamic_index_in_dim(value, index, axis, keepdims=False)


def outer_plain(lefts, rights, by_rows):
    dp, mp = lax.axis_size("dp"), lax.axis_size("mp")
    grads = sum(
        lax.dot_general(left, right, TN, preferred_element_type=f32)
        for left, right in zip(lefts, rights)
    ).astype(bf16)
    rows, width = grads.shape
    if by_rows:
        grads = grads.reshape(dp, rows // dp, mp, width // mp).transpose(0, 2, 1, 3)
    else:
        grads = grads.reshape(mp, rows // mp, dp, width // dp).transpose(2, 0, 1, 3)
    grads = grads.reshape((dp * mp,) + grads.shape[2:])
    return lax.psum_scatter(grads, ("dp", "mp"), scatter_dimension=0, tiled=False).astype(f32)


def exchange_sum_kernel(
    x_ref, loss_ref, qkv_ref, up_out_ref, down_ref, o_ref, s_ref, work_ref, pair_ref, quad_ref, eight_ref, deep_ref, tile_ref,
    send_sem, recv_sem,
):
    dp, level, core = mesh_place()
    x, y = lax.rem(dp, 2), dp // 2
    side = device_of(dp + 1 - 2 * x, level, core)
    down = device_of(lax.rem(dp + 2, 4), level, core)
    near = device_of(dp, level, 1 - core)
    deep = [device_of(dp, lax.rem(level + step, 4), core) for step in (1, 2, 3)]
    barrier = pltpu.get_barrier_semaphore()
    for target in (side, down, near, *deep):
        pl.semaphore_signal(barrier, inc=1, device_id=target, device_id_type=MESH)
    pl.semaphore_wait(barrier, 6)
    started = []

    def send(source, target_ref, target):
        slot = len(started)
        copy = pltpu.make_async_remote_copy(
            src_ref=source,
            dst_ref=target_ref,
            send_sem=send_sem.at[slot],
            recv_sem=recv_sem.at[slot],
            device_id=target,
            device_id_type=MESH,
        )
        copy.start()
        started.append(copy)
        return copy

    half = x_ref.shape[0] // 2
    quarter, eighth, part, unit = half // 2, half // 4, half // 8, half // 16

    def rows(start, size):
        return pl.ds(pl.multiple_of(start, unit), size)

    copy = send(x_ref.at[rows((1 - core) * half, half)], pair_ref, near)
    copy.wait_recv()
    work_ref[...] = x_ref[rows(core * half, half)] + pair_ref[...]
    one = send(work_ref.at[rows((1 - x) * eighth, eighth)], quad_ref.at[0], side)
    two = send(work_ref.at[rows(quarter + (1 - y) * eighth, eighth)], quad_ref.at[1], down)
    base_a = x * eighth
    base_b = quarter + y * eighth
    wide_a, wide_b = core * half + base_a, core * half + base_b
    one.wait_recv()
    work_ref[rows(base_a, eighth)] += quad_ref[0]
    one = send(work_ref.at[rows(base_a + (1 - y) * part, part)], eight_ref.at[0], down)
    two.wait_recv()
    work_ref[rows(base_b, eighth)] += quad_ref[1]
    two = send(work_ref.at[rows(base_b + (1 - x) * part, part)], eight_ref.at[1], side)
    base_a = base_a + y * part
    base_b = base_b + x * part
    one.wait_recv()
    work_ref[rows(base_a, part)] += eight_ref[0]
    two.wait_recv()
    work_ref[rows(base_b, part)] += eight_ref[1]

    def level_start(which):
        late = which // 2
        return (1 - late) * base_a + late * base_b + lax.rem(which, 2) * unit

    copies = []
    for step in (1, 2, 3):
        source = work_ref.at[rows(level_start(lax.rem(level + step, 4)), unit)]
        copies.append(send(source, deep_ref.at[step - 1], deep[step - 1]))
    for copy in copies:
        copy.wait_recv()
    total = work_ref[rows(level_start(level), unit)] + deep_ref[0] + deep_ref[1] + deep_ref[2]
    mine = rows(core * half + level_start(level), unit)
    base_a = core * half + base_a
    base_b = core * half + base_b
    o_ref[mine] = total
    row = lax.broadcasted_iota(jnp.int32, s_ref.shape, 0)
    squares = jnp.sum(total * total)
    for ref in (qkv_ref, up_out_ref, down_ref):
        squares += jnp.sum(ref[...] * ref[...])
    tile_ref[0] = jnp.where(row == 0, squares, jnp.where(row == 1, loss_ref[...], 0.0))
    copies = []
    for step in (1, 2, 3):
        copies.append(send(o_ref.at[mine], o_ref.at[mine], deep[step - 1]))
        copies.append(send(tile_ref.at[0], tile_ref.at[step], deep[step - 1]))
    for copy in copies:
        copy.wait_recv()
    one = send(o_ref.at[rows(base_a, part)], o_ref.at[rows(base_a, part)], down)
    two = send(o_ref.at[rows(base_b, part)], o_ref.at[rows(base_b, part)], side)
    tile_ref[4] = tile_ref[0] + tile_ref[1] + tile_ref[2] + tile_ref[3]
    three = send(tile_ref.at[4], tile_ref.at[5], side)
    one.wait_recv()
    one = send(o_ref.at[rows(wide_a, eighth)], o_ref.at[rows(wide_a, eighth)], side)
    two.wait_recv()
    two = send(o_ref.at[rows(wide_b, eighth)], o_ref.at[rows(wide_b, eighth)], down)
    three.wait_recv()
    tile_ref[6] = tile_ref[4] + tile_ref[5]
    three = send(tile_ref.at[6], tile_ref.at[7], down)
    one.wait_recv()
    two.wait_recv()
    one = send(o_ref.at[rows(core * half, half)], o_ref.at[rows(core * half, half)], near)
    three.wait_recv()
    tile_ref[8] = tile_ref[6] + tile_ref[7]
    three = send(tile_ref.at[8], tile_ref.at[9], near)
    one.wait_recv()
    three.wait_recv()
    s_ref[...] = tile_ref[8] + tile_ref[9]
    for copy in started:
        copy.wait_send()


def exchange_sum(value, loss, *shares):
    rows, width = value.shape
    tile = jax.ShapeDtypeStruct((8, 128), f32)
    return pl.pallas_call(
        exchange_sum_kernel,
        out_shape=(jax.ShapeDtypeStruct(value.shape, f32), tile),
        in_specs=[VMEM] * 5,
        out_specs=[VMEM, VMEM],
        scratch_shapes=[
            pltpu.VMEM((rows // 2, width), f32),
            pltpu.VMEM((rows // 2, width), f32),
            pltpu.VMEM((2, rows // 8, width), f32),
            pltpu.VMEM((2, rows // 16, width), f32),
            pltpu.VMEM((3, rows // 32, width), f32),
            pltpu.VMEM((10,) + tile.shape, f32),
            pltpu.SemaphoreType.DMA((24,)),
            pltpu.SemaphoreType.DMA((24,)),
        ],
        compiler_params=pltpu.CompilerParams(
            collective_id=5, has_side_effects=True, vmem_limit_bytes=BIG
        ),
        name="exchange_sum",
    )(value, loss.reshape(1, 1), *shares)


def split_low(values):
    high = values.astype(bf16)
    return high, (values - high.astype(f32)).astype(bf16)


def three_products(left, right, dims=(((1,), (0,)), ((), ()))):
    def product(one, two):
        return lax.dot_general(one, two, dims, preferred_element_type=f32)

    return product(left[0], right[0]) + (product(left[1], right[0]) + product(left[0], right[1]))


def exact_product(left, right, dims=(((1,), (0,)), ((), ()))):
    return lax.dot_general(left, right, dims, precision=highest, preferred_element_type=f32)


def head_marks(width):
    head = lax.broadcasted_iota(jnp.int32, (HEADS, width), 0)
    column = lax.broadcasted_iota(jnp.int32, (HEADS, width), 1)
    return jnp.where(column // HEAD_DIM == head, 1.0, 0.0).astype(f32)


def quarter_marks(padded):
    row = lax.broadcasted_iota(jnp.int32, (padded, V), 0)
    column = lax.broadcasted_iota(jnp.int32, (padded, V), 1)
    return jnp.where(row // 4 == column, 0.25, 0.0).astype(f32)


def tables_kernel(tables_ref, hot_ref, patch_ref, var_ref, keyed_ref, bias_ref):
    padded, width = patch_ref.shape
    query = tables_ref[5 * V + LEADS : 5 * V + LEADS + 1, :]
    patch_ref[...] = jnp.zeros_like(patch_ref)
    patch_ref[: 4 * V, :] = tables_ref[: 4 * V, :]
    chosen = exact_product(hot_ref[...], tables_ref[4 * V : 5 * V, :])
    var_ref[...] = exact_product(quarter_marks(padded), chosen)
    marks = head_marks(width)
    scale = HEAD_DIM**-0.5
    keyed_ref[...] = exact_product(marks, patch_ref[...] * query, NT) * scale
    bias = exact_product(marks, var_ref[...] * query, NT) * (4.0 * scale)
    column = lax.broadcasted_iota(jnp.int32, bias.shape, 1)
    bias_ref[...] = jnp.where(column < 4 * V, bias, -1e30)


def prepare_tables(tables, var_hot):
    padded = 256
    return pl.pallas_call(
        tables_kernel,
        out_shape=(
            jax.ShapeDtypeStruct((padded, D), f32),
            jax.ShapeDtypeStruct((padded, D), f32),
            jax.ShapeDtypeStruct((HEADS, padded), f32),
            jax.ShapeDtypeStruct((HEADS, padded), f32),
        ),
        compiler_params=pltpu.CompilerParams(vmem_limit_bytes=BIG),
        name="prepare_tables",
    )(tables, var_hot)


def four_sum(values):
    size = values.shape[1]
    lane = lax.broadcasted_iota(jnp.int32, values.shape, 1)
    values = values + jnp.where(
        lane % 2 == 0, pltpu.roll(values, size - 1, 1), pltpu.roll(values, 1, 1)
    )
    return values + jnp.where(
        lane % 4 < 2, pltpu.roll(values, size - 2, 1), pltpu.roll(values, 2, 1)
    )


def cell_shares(cells, keyed, bias):
    scores = four_sum(cells * keyed) + bias
    raised = jnp.exp(scores - jnp.max(scores, axis=1, keepdims=True))
    total = jnp.sum(raised, axis=1, keepdims=True) * 0.25
    return raised * (1.0 / total)


def embed_pair(pair, cells, keyed_ref, bias_ref, patch_ref, var_ref, x0_ref):
    patch = split_low(patch_ref[...])
    variable = split_low(var_ref[...])
    outs = []
    for which in range(2):
        row = pl.ds(pair * 2 + which, 1)
        shares = cell_shares(cells, keyed_ref[row, :], bias_ref[row, :])
        outs.append(
            three_products(split_low(shares * cells), patch)
            + three_products(split_low(shares), variable)
        )
    lane = lax.broadcasted_iota(jnp.int32, outs[0].shape, 1)
    columns = pl.ds(pl.multiple_of(pair * 2 * HEAD_DIM, 2 * HEAD_DIM), 2 * HEAD_DIM)
    x0_ref[:, columns] = jnp.where(lane < HEAD_DIM, outs[0], outs[1])


def embed_kernel(
    u_ref, keyed_ref, bias_ref, patch_ref, var_ref, lead_ref, gains_ref, x0_ref, h1_ref
):
    pair = pl.program_id(0)
    embed_pair(pair, u_ref[...], keyed_ref, bias_ref, patch_ref, var_ref, x0_ref)

    @pl.when(pair == pl.num_programs(0) - 1)
    def _():
        x0_ref[...] += lead_ref[...]
        unit, _ = normed_parts(x0_ref[...])
        h1_ref[...] = (unit * gains_ref[0:1, :] + gains_ref[1:2, :]).astype(bf16)


def embed_forward(cells, prepared, lead_row, norm_gains):
    patch, variable, keyed, bias = prepared
    rows, padded = cells.shape
    fixed = lambda shape: pl.BlockSpec(shape, lambda i: (0, 0))
    by_pair = pl.BlockSpec((padded, 2 * HEAD_DIM), lambda i: (0, i))
    return pl.pallas_call(
        embed_kernel,
        grid=(HEADS // 2,),
        out_shape=(
            jax.ShapeDtypeStruct((rows, D), f32),
            jax.ShapeDtypeStruct((rows, D), bf16),
        ),
        in_specs=[
            fixed((rows, padded)),
            fixed(keyed.shape),
            fixed(bias.shape),
            by_pair,
            by_pair,
            fixed((1, D)),
            fixed(norm_gains.shape),
        ],
        out_specs=[fixed((rows, D)), fixed((rows, D))],
        compiler_params=pltpu.CompilerParams(vmem_limit_bytes=BIG),
        cost_estimate=pl.CostEstimate(
            flops=24 * rows * padded * D, bytes_accessed=14 * rows * D, transcendentals=16 * rows * padded
        ),
        name="embed_forward",
    )(cells, keyed, bias, patch, variable, lead_row, norm_gains)


def entry_back_kernel(
    grad_ref, qkv_ref, x0_ref, mid_ref, gains_ref, u_ref, keyed_ref, bias_ref, patch_ref, var_ref,
    du_ref, gain_ref, lead_ref, dpatch_ref, dvar_ref, dkeyed_ref, dbias_ref,
    dx_ref, flip_ref,
):
    pair = pl.program_id(0)

    @pl.when(pair == 0)
    def _():
        row_grad = jnp.dot(grad_ref[...], qkv_ref[...], preferred_element_type=f32)
        unit, inverse = normed_parts(x0_ref[...])
        part, gain_grad, bias_grad = norm_grad(unit, inverse, gains_ref[0:1, :], row_grad)
        total = mid_ref[...] + part
        dx_ref[...] = total
        flip_ref[...] = total.T
        lead_ref[...] = jnp.sum(total, axis=0, keepdims=True)
        gain_ref[0:1, :] = gain_grad
        gain_ref[1:2, :] = bias_grad
        du_ref[...] = jnp.zeros_like(du_ref)

    cells = u_ref[...]
    size = 2 * HEAD_DIM
    columns = pl.ds(pl.multiple_of(pair * size, size), size)
    grads = dx_ref[:, columns]
    lane = lax.broadcasted_iota(jnp.int32, grads.shape, 1)
    patch = split_low(patch_ref[...])
    variable = split_low(var_ref[...])
    cells_grad = None
    for which in range(2):
        row = pl.ds(pair * 2 + which, 1)
        keyed = keyed_ref[row, :]
        shares = cell_shares(cells, keyed, bias_ref[row, :])
        one = split_low(jnp.where(lane // HEAD_DIM == which, grads, 0.0))
        mixed_grad = three_products(one, patch, NT)
        share_grad = mixed_grad * cells + three_products(one, variable, NT)
        weighted = shares * share_grad
        inner = jnp.sum(weighted, axis=1, keepdims=True)
        score_grad = four_sum(weighted) - shares * inner
        piece = mixed_grad * shares + score_grad * keyed
        cells_grad = piece if cells_grad is None else cells_grad + piece
        scale = HEAD_DIM**-0.5
        dkeyed_ref[row, :] = jnp.sum(score_grad * cells, axis=0, keepdims=True) * scale
        dbias_ref[row, :] = jnp.sum(score_grad, axis=0, keepdims=True) * scale
        rows = pl.ds(pl.multiple_of(pair * size + which * HEAD_DIM, HEAD_DIM), HEAD_DIM)
        flipped = split_low(flip_ref[rows, :])
        mine = slice(which * HEAD_DIM, (which + 1) * HEAD_DIM)
        dpatch_ref[mine, :] = three_products(flipped, split_low(shares * cells))
        dvar_ref[mine, :] = three_products(flipped, split_low(shares))
    du_ref[...] += cells_grad


def entry_backward(token_grad, qkv_t, x_first, mid_grad, norm_gains, cells, prepared):
    patch, variable, keyed, bias = prepared
    rows, width = x_first.shape
    padded = cells.shape[1]
    fixed = lambda shape: pl.BlockSpec(shape, lambda i: (0, 0))
    by_pair = pl.BlockSpec((padded, 2 * HEAD_DIM), lambda i: (0, i))
    flipped = pl.BlockSpec((2 * HEAD_DIM, padded), lambda i: (i, 0))
    return pl.pallas_call(
        entry_back_kernel,
        grid=(HEADS // 2,),
        out_shape=(
            jax.ShapeDtypeStruct((rows, padded), f32),
            jax.ShapeDtypeStruct((2, width), f32),
            jax.ShapeDtypeStruct((1, width), f32),
            jax.ShapeDtypeStruct((width, padded), f32),
            jax.ShapeDtypeStruct((width, padded), f32),
            jax.ShapeDtypeStruct(keyed.shape, f32),
            jax.ShapeDtypeStruct(bias.shape, f32),
        ),
        in_specs=[
            fixed(token_grad.shape),
            fixed(qkv_t.shape),
            fixed((rows, width)),
            fixed((rows, width)),
            fixed(norm_gains.shape),
            fixed(cells.shape),
            fixed(keyed.shape),
            fixed(bias.shape),
            by_pair,
            by_pair,
        ],
        out_specs=[
            fixed((rows, padded)),
            fixed((2, width)),
            fixed((1, width)),
            flipped,
            flipped,
            fixed(keyed.shape),
            fixed(bias.shape),
        ],
        scratch_shapes=[pltpu.VMEM((rows, width), f32), pltpu.VMEM((width, rows), f32)],
        compiler_params=pltpu.CompilerParams(vmem_limit_bytes=BIG),
        cost_estimate=pl.CostEstimate(
            flops=60 * rows * padded * D, bytes_accessed=40 * rows * D, transcendentals=16 * rows * padded
        ),
        name="entry_backward",
    )(token_grad, qkv_t, x_first, mid_grad, norm_gains, cells, keyed, bias, patch, variable)


def table_grads_kernel(
    pa_ref, pb_ref, va_ref, vb_ref, ka_ref, kb_ref, ba_ref, bb_ref,
    patch_ref, var_ref, query_ref, hot_ref, lead_hot_ref, lead_ref, gain_ref, head_ref, high_ref, o_ref,
):
    padded, width = patch_ref.shape
    marks = head_marks(width)
    query = query_ref[...]
    keyed_grad = exact_product(ka_ref[...] + kb_ref[...], marks, TN)
    bias_grad = exact_product(ba_ref[...] + bb_ref[...], marks, TN)
    o_ref[...] = jnp.zeros_like(o_ref)
    patch_grad = (pa_ref[...] + pb_ref[...]).T + keyed_grad * query
    o_ref[: 4 * V, :] = patch_grad[: 4 * V, :]
    var_grad = (va_ref[...] + vb_ref[...]).T + bias_grad * query
    var_rows = exact_product(quarter_marks(padded), var_grad, TN)
    o_ref[4 * V : 5 * V, :] = exact_product(hot_ref[...], var_rows, TN)
    lead_rows = exact_product(lead_hot_ref[...], lead_ref[...], TN)
    o_ref[5 * V : 5 * V + LEADS, :] = lead_rows[:LEADS, :]
    query_grad = jnp.sum(
        keyed_grad * patch_ref[...] + bias_grad * var_ref[...], axis=0, keepdims=True
    )
    o_ref[5 * V + LEADS : 5 * V + LEADS + 1, :] = query_grad
    o_ref[5 * V + LEADS + 1 : 5 * V + LEADS + 3, :] = gain_ref[...]
    o_ref[padded : padded + 4 * V, :] = head_ref[...]
    o_ref[padded + 4 * V : padded + 4 * V + 4, :] = high_ref[...]


def table_grads(first, second, prepared, query, var_hot, lead_hots, leads, gain_rows, head, high):
    patch, variable, _, _ = prepared
    operands = []
    for one, two in zip(first, second):
        operands += [one, two]
    return pl.pallas_call(
        table_grads_kernel,
        out_shape=jax.ShapeDtypeStruct((2 * patch.shape[0], D), f32),
        compiler_params=pltpu.CompilerParams(vmem_limit_bytes=BIG),
        name="table_grads",
    )(*operands, patch, variable, query, var_hot, lead_hots, leads, gain_rows, head, high)


def adam_step(master, grad, first, second, rate):
    first_new = beta_first * first + (1.0 - beta_first) * grad
    second_new = beta_second * second + (1.0 - beta_second) * grad * grad
    update = first_new / first_fix / (jnp.sqrt(second_new / second_fix) + adam_eps)
    return (master - rate * (update + decay_rate * master), first_new, second_new)


def update_kernel(packed, *refs):
    where_ref, sums_ref, tile_ref, count_ref = refs[:4]
    shares = list(refs[4 : 4 + (3 if packed else 4)])
    rest = refs[4 + len(shares) :]
    states, average_ref, outs = rest[:18], rest[18], rest[19:]
    norm = jnp.sqrt(tile_ref[0:1, 0:1])
    factor = jnp.minimum(1.0, clip_norm / (norm + 1e-06))
    outs[1][...] = norm
    outs[0][...] = tile_ref[1:2, 0:1] / (2.0 * V * jnp.maximum(count_ref[...], 1.0))
    embed_rows = 5 * V + LEADS + 1
    padded = 256

    def apply(index, grad, rate, rows=slice(None)):
        master, first, second = (ref[rows, :] for ref in states[3 * index : 3 * index + 3])
        new = adam_step(master, factor * grad, first, second, rate)
        for ref, value in zip(outs[2 + 3 * index : 5 + 3 * index], new):
            ref[rows, :] = value
        return new[0]

    apply(0, sums_ref[:embed_rows, :], lr_table, slice(0, embed_rows))
    apply(0, sums_ref[padded : padded + 4 * V, :], lr_table, slice(embed_rows, embed_rows + 4 * V))
    apply(1, sums_ref[embed_rows : embed_rows + 2, :], lr_gain, slice(0, 2))
    apply(1, sums_ref[padded + 4 * V : padded + 4 * V + 4, :], lr_gain, slice(2, 6))
    if packed:
        units = shares[2].shape[0]
        grads = (
            shares[0][...], shares[1][units:, :], shares[1][:units, :].T, shares[2][...]
        )
    else:
        grads = [share[...] for share in shares]
    qkv_new = apply(2, grads[0], lr_matrix)
    for index in range(1, 4):
        apply(2 + index, grads[index], lr_matrix)
    outs[20][...] = average_keep * average_ref[...] + (1.0 - average_keep) * qkv_new


def update_all(packed, where, sums, tile, count, shares, states, average):
    operands = [sums, tile, count.reshape(1, 1), *shares]
    fixed = lambda shape: pl.BlockSpec(shape, lambda i, w: (0, 0))
    in_specs = [fixed(value.shape) for value in operands]
    out_shapes = [(1, 1), (1, 1)]
    for master, first, second in states:
        if master.shape == first.shape:
            in_specs.append(fixed(master.shape))
        elif master.shape[0] == first.shape[0]:
            in_specs.append(pl.BlockSpec(first.shape, lambda i, w: (0, w[0])))
        else:
            in_specs.append(pl.BlockSpec(first.shape, lambda i, w: (w[0], 0)))
        in_specs += [fixed(first.shape)] * 2
        operands += [master, first, second]
        out_shapes += [first.shape] * 3
    operands.append(average)
    in_specs.append(fixed(average.shape))
    out_shapes.append(average.shape)
    return pl.pallas_call(
        partial(update_kernel, packed),
        grid_spec=pltpu.PrefetchScalarGridSpec(
            num_scalar_prefetch=1,
            grid=(1,),
            in_specs=in_specs,
            out_specs=[fixed(shape) for shape in out_shapes],
        ),
        out_shape=[jax.ShapeDtypeStruct(shape, f32) for shape in out_shapes],
        compiler_params=pltpu.CompilerParams(vmem_limit_bytes=60 * 2**20),
        name="update_all",
    )(where, *operands)


def by_kind(shard):
    rows = shard.shape[0]
    return shard.reshape(rows, -1, 3, HEAD_DIM).transpose(0, 2, 1, 3).reshape(rows, -1)


def by_head(shard):
    rows = shard.shape[0]
    return shard.reshape(rows, 3, -1, HEAD_DIM).transpose(0, 2, 1, 3).reshape(rows, -1)


lag_one, lag_two, ahead = 2, 4, 3
embed_at, gather_at, project_at, attend_at = 3, 11, 14, 18


def start_kernel(halves, *refs):
    count = len(halves)
    packed_ref, keyed_ref, bias_ref, patch_ref, var_ref, lead_ref, gains_ref = refs[:7]
    shards = refs[7 : 7 + count]
    x0_ref, cells_ref, qkv_ref, o_ref, full_ref, lse_ref, count_ref, rows_out = refs[7 + count : 15 + count]
    outs = refs[15 + count : 15 + 2 * count]
    (held_ref, h1_ref, rows_ref, weight_ref, vt_ref, tile_ref, send_sem, recv_sem,
     level_send, level_recv, own_sem) = refs[15 + 2 * count :]
    step = pl.program_id(0)
    dp, level, core = mesh_place()
    x = lax.rem(dp, 2)
    columns = {"here": dp, "side": dp + 1 - 2 * x, "down": lax.rem(dp + 2, 4), "far": 3 - dp}
    side = device_of(columns["side"], level, core)
    down = device_of(columns["down"], level, core)
    near = device_of(dp, level, 1 - core)
    across = device_of(level, dp, core)
    middle = lax.rem(level, 3) != 0
    late = level // 2
    sources = (level + 1 - 2 * lax.rem(level, 2), 2 - late, 3 * (1 - late))
    onward = (3 - level, lax.rem(3 * level + 1, 4), lax.rem(3 * level + 1, 4))
    slots = [0]

    def remote(source, target_ref, target):
        slot = slots[0]
        slots[0] += 1
        return pltpu.make_async_remote_copy(
            src_ref=source,
            dst_ref=target_ref,
            send_sem=send_sem.at[slot],
            recv_sem=recv_sem.at[slot],
            device_id=target,
            device_id_type=MESH,
        )

    def place(out, source, column, half, pieces):
        rows = out.shape[1] // 4
        size = rows // pieces
        start = pl.multiple_of(columns[column] * rows + half * size, size)
        return out.at[source * 2 + core, pl.ds(start, size), :]

    def pass_on(out, source, column, target, cut):
        where = place(out, source, column, *cut)
        return remote(where, where, target)

    crossing = remote(packed_ref, held_ref, across)
    staying = pltpu.make_async_copy(packed_ref, held_ref, own_sem.at[count])
    mine = [outs[index].at[level * 2 + core] for index in range(count)]
    given = [remote(shards[index], mine[index], near) for index in range(count)]
    kept = [
        pltpu.make_async_copy(shards[index], mine[index], own_sem.at[index]) for index in range(count)
    ]
    chunks, openings = [], []
    for index in range(count):
        out, pieces = outs[index], halves[index]
        for half in range(pieces):
            group = len(openings)
            full = out.shape[1] // 4
            size = full // pieces
            own = shards[index].at[pl.ds(pl.multiple_of(dp * full + half * size, size), size), :]
            cut = (half, pieces)

            def along(source_ref, source, target_level, slot):
                return pltpu.make_async_remote_copy(
                    src_ref=source_ref,
                    dst_ref=place(out, source, "here", *cut),
                    send_sem=level_send.at[group * 5 + slot],
                    recv_sem=level_recv.at[group * 4 + source],
                    device_id=device_of(dp, target_level, core),
                    device_id_type=MESH,
                )

            openings.append(
                (
                    along(own, level, lax.rem(level + 1, 4), 0),
                    along(own, level, lax.rem(level + 3, 4), 1),
                )
            )
            for turn in range(3):
                source = sources[turn]
                chunks.append(
                    {
                        "level": along(place(out, source, "here", *cut), source, onward[turn], 2 + turn),
                        "side": pass_on(out, source, "here", side, cut),
                        "down": pass_on(out, source, "here", down, cut),
                        "hop_down": pass_on(out, source, "side", down, (2 * half, 2 * pieces)),
                        "hop_side": pass_on(out, source, "down", side, (2 * half + 1, 2 * pieces)),
                        "here_near": pass_on(out, source, "here", near, cut),
                        "side_near": pass_on(out, source, "side", near, cut),
                        "down_near": pass_on(out, source, "down", near, cut),
                        "far_near": pass_on(out, source, "far", near, cut),
                    }
                )
    groups = len(openings)
    order = []
    for number in range(groups + 2):
        for turn in range(3):
            if 0 <= number - turn < groups:
                order.append((number - turn, turn))
    chunks = [chunks[3 * group + turn] for group, turn in order]
    total = len(chunks)

    def start_group(number):
        @pl.when(level < 3)
        def _():
            openings[number][0].start()

        @pl.when(level > 0)
        def _():
            openings[number][1].start()

    rows = h1_ref.shape[0]
    cut = rows // 2

    def rows_of(owner, who, first, size):
        return rows_ref.at[pl.ds(pl.multiple_of((owner * 2 + who) * rows + first, cut), size)]

    def relay(place_ref, target):
        return remote(place_ref, place_ref, target)

    first_half, second_half = h1_ref.at[pl.ds(0, cut)], h1_ref.at[pl.ds(cut, cut)]
    beside, below, far = columns["side"], columns["down"], columns["far"]
    side_a = remote(first_half, rows_of(dp, core, 0, cut), side)
    down_b = remote(second_half, rows_of(dp, core, cut, cut), down)
    side_b = remote(second_half, rows_of(dp, core, cut, cut), side)
    down_a = remote(first_half, rows_of(dp, core, 0, cut), down)
    near_own = remote(h1_ref, rows_of(dp, core, 0, rows), near)
    far_a = relay(rows_of(beside, core, 0, cut), down)
    far_b = relay(rows_of(below, core, cut, cut), side)
    near_side = relay(rows_of(beside, core, 0, rows), near)
    near_down = relay(rows_of(below, core, 0, rows), near)
    near_far = relay(rows_of(far, core, 0, rows), near)
    tiles = [
        remote(tile_ref.at[0], tile_ref.at[1], side),
        remote(tile_ref.at[2], tile_ref.at[3], down),
        remote(tile_ref.at[4], tile_ref.at[5], near),
    ]
    deep = [device_of(dp, lax.rem(level + move, 4), core) for move in (1, 2, 3)]
    level_tiles = [remote(tile_ref.at[6], tile_ref.at[7 + move], deep[move]) for move in range(3)]
    weight = pltpu.make_async_copy(outs[0].at[dp * 2 + core], weight_ref, own_sem.at[count + 1])
    save = pltpu.make_async_copy(rows_ref, rows_out, own_sem.at[count + 2])

    @pl.when(step == 0)
    def _():
        barrier = pltpu.get_barrier_semaphore()
        for target in (side, down, near, *deep):
            pl.semaphore_signal(barrier, inc=1, device_id=target, device_id_type=MESH)

        @pl.when(dp != level)
        def _():
            pl.semaphore_signal(barrier, inc=1, device_id=across, device_id_type=MESH)
            pl.semaphore_wait(barrier, 7)
            crossing.start()

        @pl.when(dp == level)
        def _():
            pl.semaphore_wait(barrier, 6)
            staying.start()

        for number in range(ahead):
            start_group(number)
        for copy in (*given, *kept):
            copy.start()

    for number in range(total + lag_two):

        @pl.when(step == number)
        def _(number=number):
            if number < total:
                chunk = chunks[number]
                chunk["level"].wait_recv()

                @pl.when(middle)
                def _():
                    chunk["level"].start()

                chunk["side"].start()
                chunk["down"].start()
                chunk["here_near"].start()
                group, turn = order[number]
                if turn == 0 and group + ahead < groups:
                    start_group(group + ahead)
            if 0 <= number - lag_one < total:
                chunk = chunks[number - lag_one]
                chunk["side"].wait_recv()
                chunk["hop_down"].start()
                chunk["down"].wait_recv()
                chunk["hop_side"].start()
                chunk["side_near"].start()
                chunk["down_near"].start()
            if 0 <= number - lag_two < total:
                chunk = chunks[number - lag_two]
                chunk["hop_down"].wait_recv()
                chunk["hop_side"].wait_recv()
                chunk["far_near"].start()

    @pl.when(step == embed_at)
    def _():
        @pl.when(dp != level)
        def _():
            crossing.wait_recv()

        @pl.when(dp == level)
        def _():
            staying.wait()

        cells_ref[...] = held_ref[...]
        lane = lax.broadcasted_iota(jnp.int32, held_ref.shape, 1)
        ocean = jnp.where((lane >= 4 * V) & (lane < 4 * V + 4), 1.0 - held_ref[...], 0.0)
        tile_ref[0] = jnp.broadcast_to(jnp.sum(ocean), tile_ref.shape[1:])
        tiles[0].start()

    for turn in range(3):

        @pl.when(step == embed_at + 2 + turn)
        def _(turn=turn):
            tiles[turn].wait_recv()
            tile_ref[2 * turn + 2] = tile_ref[2 * turn] + tile_ref[2 * turn + 1]
            for copy in (tiles[1:2], tiles[2:3], level_tiles)[turn]:
                copy.start()

    @pl.when(step == embed_at + 6)
    def _():
        for copy in level_tiles:
            copy.wait_recv()
        count_ref[...] = tile_ref[6] + tile_ref[7] + tile_ref[8] + tile_ref[9]

    @pl.when((step >= embed_at) & (step < embed_at + HEADS // 2))
    def _():
        embed_pair(step - embed_at, held_ref[...], keyed_ref, bias_ref, patch_ref, var_ref, x0_ref)

    @pl.when(step == gather_at)
    def _():
        lead = held_ref[0:1, 4 * V + 4 : 4 * V + 5]
        row = lax.broadcasted_iota(jnp.int32, (1, 8), 1).astype(f32)
        lead_hot = jnp.where(row == lead, 1.0, 0.0).astype(f32)
        x0_ref[...] += exact_product(lead_hot, lead_ref[...])
        unit, _ = normed_parts(x0_ref[...])
        h1_ref[...] = (unit * gains_ref[0:1, :] + gains_ref[1:2, :]).astype(bf16)
        for copy in (side_a, down_b, side_b, down_a, near_own):
            copy.start()
        rows_of(dp, core, 0, rows)[...] = h1_ref[...]
        kept[0].wait()
        weight.start()

    @pl.when(step == gather_at + 1)
    def _():
        side_a.wait_recv()
        far_a.start()
        down_b.wait_recv()
        far_b.start()
        side_b.wait_recv()
        near_side.start()
        down_a.wait_recv()
        near_down.start()

    @pl.when(step == gather_at + 2)
    def _():
        far_a.wait_recv()
        far_b.wait_recv()
        near_far.start()
        for copy in (near_own, near_side, near_down):
            copy.wait_recv()

    block = rows_ref.shape[0] // 4

    @pl.when(step == project_at)
    def _():
        near_far.wait_recv()
        save.start()
        weight.wait()

    @pl.when((step >= project_at) & (step < project_at + 4))
    def _():
        where = pl.ds(pl.multiple_of((step - project_at) * block, block), block)
        qkv_ref[where, :] = lax.dot_general(
            rows_ref[where, :], weight_ref[...], NT, preferred_element_type=f32
        ).astype(bf16)

    width = o_ref.shape[1]
    heads = width // HEAD_DIM

    @pl.when(step == attend_at)
    def _():
        vt_ref[...] = qkv_ref[:, 2 * width :].T

    @pl.when((step >= attend_at) & (step < attend_at + 4))
    def _():
        where = pl.ds(pl.multiple_of((step - attend_at) * block, block), block)
        full, sums = attend_rows(
            heads, qkv_ref[where, :width], qkv_ref.at[:, width : 2 * width], vt_ref
        )
        for head in range(heads):
            lse_ref[head : head + 1, where] = sums[head]
        full_ref[where, :] = full
        o_ref[where, :] = full.astype(bf16)

    @pl.when(step == total + lag_two - 1)
    def _():
        for copy in given:
            copy.wait()
        for copy in kept[1:]:
            copy.wait()
        for number in range(groups):

            @pl.when(level < 3)
            def _(number=number):
                openings[number][0].wait_send()

            @pl.when(level > 0)
            def _(number=number):
                openings[number][1].wait_send()

        for chunk in chunks:
            for name in ("here_near", "side_near", "down_near", "far_near"):
                chunk[name].wait_recv()
            for name, copy in chunk.items():
                if name != "level":
                    copy.wait_send()

            @pl.when(middle)
            def _(chunk=chunk):
                chunk["level"].wait_send()

        for copy in (side_a, down_b, side_b, down_a, near_own, far_a, far_b, near_side, near_down, near_far):
            copy.wait_send()
        for copy in (*tiles, *level_tiles):
            copy.wait_send()
        save.wait()

        @pl.when(dp != level)
        def _():
            crossing.wait_send()


def start_program(packed, prepared, lead_table, norm_gains, shards, halves):
    patch, variable, keyed, bias = prepared
    count = len(shards)
    groups = sum(halves)
    copies = groups * 24 + count + 17
    rows, padded = packed.shape
    total = 8 * rows
    width = shards[0].shape[0] // 3
    heads = width // HEAD_DIM
    anywhere = pl.BlockSpec(memory_space=pl.ANY)
    fixed = lambda shape: pl.BlockSpec(shape, lambda i: (0, 0))
    by_pair = pl.BlockSpec(
        (padded, 2 * HEAD_DIM), lambda i: (0, jnp.clip(i - embed_at, 0, HEADS // 2 - 1))
    )
    shapes = [
        ((rows, D), f32),
        (packed.shape, f32),
        ((total, 3 * width), bf16),
        ((total, width), bf16),
        ((total, width), f32),
        ((heads, total), f32),
        ((8, 128), f32),
    ]
    return pl.pallas_call(
        partial(start_kernel, halves),
        grid=(groups * 3 + lag_two,),
        out_shape=[jax.ShapeDtypeStruct(shape, kind) for shape, kind in shapes]
        + [jax.ShapeDtypeStruct((total, D), bf16)]
        + [jax.ShapeDtypeStruct((8,) + shard.shape, bf16) for shard in shards],
        in_specs=[anywhere]
        + [fixed(keyed.shape), fixed(bias.shape), by_pair, by_pair]
        + [fixed(lead_table.shape), fixed(norm_gains.shape)]
        + [fixed(shard.shape) for shard in shards],
        out_specs=[fixed(shape) for shape, _ in shapes] + [anywhere] * (count + 1),
        scratch_shapes=[
            pltpu.VMEM(packed.shape, f32),
            pltpu.VMEM((rows, D), bf16),
            pltpu.VMEM((total, D), bf16),
            pltpu.VMEM(shards[0].shape, bf16),
            pltpu.VMEM((width, total), bf16),
            pltpu.VMEM((10, 8, 128), f32),
            pltpu.SemaphoreType.DMA((copies,)),
            pltpu.SemaphoreType.DMA((copies,)),
            pltpu.SemaphoreType.DMA((groups * 5,)),
            pltpu.SemaphoreType.DMA((groups * 4,)),
            pltpu.SemaphoreType.DMA((count + 3,)),
        ],
        compiler_params=pltpu.CompilerParams(
            collective_id=7, has_side_effects=True, vmem_limit_bytes=BIG
        ),
        name="start_program",
    )(packed, keyed, bias, patch, variable, lead_table, norm_gains, *shards)


def shards(
    crossed,
    fields,
    targets,
    land_mask,
    lead_index,
    var_ids,
    tables,
    norm_gains,
    tables_first,
    tables_second,
    gains_first,
    gains_second,
    w_qkv,
    qkv_first,
    qkv_second,
    w_out,
    out_first,
    out_second,
    w_up,
    up_first,
    up_second,
    w_down,
    down_first,
    down_second,
    qkv_average,
):
    local_samples, shard_rows, _ = fields.shape
    dp_size, parts = lax.axis_size("dp"), lax.axis_size("mp")
    dp_index = lax.axis_index("dp")
    place, level, core = mesh_place()
    part = place * 2 + core if crossed else lax.axis_index("mp")
    share_rows = D // dp_size

    def own_share(full, dim):
        return lax.dynamic_slice_in_dim(full, dp_index * share_rows, share_rows, dim)

    var_hot = (var_ids[:, None] == jnp.arange(V, dtype=jnp.int32)[None, :]).astype(f32)
    prepared = prepare_tables(tables, var_hot)
    low = lambda master: master.astype(bf16)
    qkv_low = by_kind(low(w_qkv))
    packed = jnp.concatenate(
        (
            fields[0],
            land_mask[0].astype(f32),
            jnp.broadcast_to(lead_index.astype(f32), (shard_rows, 2)),
            jnp.zeros((shard_rows, 64 - 6), f32),
        ),
        axis=1,
    )
    if crossed:
        (
            x_first, cells, packed, own_out, full, logsum, count, rows_one,
            qkv_t, w_outs, w_ups, w_downs
        ) = start_program(
            packed, prepared, tables[5 * V : 5 * V + 8], norm_gains,
            (qkv_low.T, low(w_out), low(w_up), low(w_down)), (1, 1, 2, 2),
        )
        count = count[0, 0]
    else:
        cells = packed
        answers = targets[0]
        count = lax.psum(jnp.sum(1.0 - cells[:, 4 * V : 4 * V + 4]), ("dp", "mp"))
        w_outs, w_ups, w_downs, qkv_t = [
            lax.all_gather(shard, "mp")
            for shard in (low(w_out), low(w_up), low(w_down), qkv_low.T)
        ]
    gathered = (w_outs.reshape(D, D), w_ups, w_downs.reshape(-1, D), qkv_t.reshape(3 * D, D))
    qkv_local = choose(qkv_t, part)
    leads = cells[0, 4 * V + 4 : 4 * V + 6].astype(jnp.int32)
    ocean = 1.0 - cells[:, 4 * V : 4 * V + 4]
    denom = 2.0 * V * jnp.maximum(count, 1.0)
    first_row = part * shard_rows
    patch_row = (first_row + jnp.arange(shard_rows, dtype=jnp.int32)) // PATCH_COLS
    row_hot = (patch_row[:, None] == jnp.arange(PATCH_ROWS, dtype=jnp.int32)[None, :]).astype(f32)
    lat_rows = jnp.dot(
        row_hot, lat_weights(2 * PATCH_ROWS).reshape(PATCH_ROWS, 2), precision=highest
    )
    lat_pixels = jnp.broadcast_to(lat_rows[:, :, None], (shard_rows, 2, 2)).reshape(shard_rows, 4)
    weighted = jnp.tile(ocean * lat_pixels, (1, V))
    head = tables[5 * V + LEADS + 1 :]
    loss_part = f32(0.0)
    records = []
    for rollout in range(2):
        if rollout == 1:
            cells = jnp.pad(guess, ((0, 0), (0, 64)))
        if rollout == 1 or not crossed:
            lead_row = lax.dynamic_slice_in_dim(tables, 5 * V + leads[rollout], 1, 0)
            x_first, normed = embed_forward(cells, prepared, lead_row, norm_gains)
            rows_one = spread_rows(crossed, normed)
            packed = lax.dot_general(
                rows_one, qkv_local, NT, preferred_element_type=f32
            ).astype(bf16)
            own_out, full, logsum = attend(packed)
        attended = exchange(crossed, own_out, True, 2)
        if crossed and rollout == 0:
            later_targets, attended = tie(targets[0], attended)
            answers = cross(crossed, later_targets)
        x_mid, rows_two, hidden, active, x_last, guess = branch_forward(
            attended, x_first, norm_gains, gathered, head
        )
        miss = guess - answers[rollout]
        loss_part = loss_part + jnp.sum(weighted * miss * miss)
        records.append(
            (cells, x_first, rows_one, packed, full, logsum, attended, x_mid, rows_two,
             hidden, active, x_last, 2.0 * weighted * miss / denom)
        )
    carried = jnp.zeros_like(guess)
    head_total = jnp.zeros_like(head)
    gain_high = jnp.zeros((4, D), f32)
    gain_low = jnp.zeros((2, D), f32)
    table_parts, lead_sums = [], []
    qkv_grad = jnp.zeros((D, qkv_local.shape[0]), f32)
    kept = []

    for rollout in (1, 0):
        (cells, x_first, rows_one, packed, full, logsum, attended, x_mid, rows_two,
         hidden, active, x_last, loss_grad) = records[rollout]
        last_low, hidden_grad, mid_grad, mid_low, out_grad, gain_part, head_grad = branch_backward(
            loss_grad + carried, x_last, x_mid, norm_gains, hidden, gathered, head
        )
        head_total = head_total + head_grad
        gain_high = gain_high + gain_part[2:]
        if crossed:
            (
                own_grad, act_both, dg_both, o_both, dx2_near, h2_near, dx1_near
            ) = exchange_swap(
                out_grad, active, hidden_grad, attended, last_low, rows_two, mid_low
            )
            kept.append(
                (act_both, dg_both, o_both, last_low, dx2_near, rows_two, h2_near, mid_low, dx1_near)
            )
        else:
            flat = lambda value: value.transpose(2, 1, 0, 3).reshape(shard_rows, -1)
            kept.append((attended, rows_two, flat(active), mid_low, flat(hidden_grad), last_low))
            own_grad = exchange(crossed, out_grad, False, 3)
        if crossed and rollout == 0:
            token_grad, qkv_share, down_sum, up_out_sum = finish_program(
                kept, packed, own_grad, full, logsum, rows_one, qkv_grad
            )
        else:
            packed_grad = attend_back(own_grad, packed, full, logsum)
            token_grad = exchange(crossed, packed_grad, True, 4 + 4)
            qkv_grad = qkv_grad + lax.dot_general(
                rows_one, packed_grad, TN, preferred_element_type=f32
            )
        cells_grad, gain_one, lead_sum, *table_part = entry_backward(
            token_grad, gathered[3], x_first, mid_grad, norm_gains, cells, prepared
        )
        carried = cells_grad[:, : 4 * V]
        gain_low = gain_low + gain_one
        table_parts.append(table_part)
        lead_sums.append(lead_sum)

    def pair(index):
        return (kept[0][index], kept[1][index])

    lead_hots = (leads[:, None] == jnp.arange(8, dtype=jnp.int32)[None, :]).astype(f32)
    lead_hots = jnp.pad(lead_hots, ((0, 6), (0, 0)))
    lead_rows = jnp.pad(jnp.concatenate((lead_sums[1], lead_sums[0])), ((0, 6), (0, 0)))
    query = tables[5 * V + LEADS : 5 * V + LEADS + 1]
    last_rows = table_grads(
        *table_parts, prepared, query, var_hot, lead_hots, lead_rows, gain_low, head_total, gain_high
    )
    if not crossed:
        qkv_share = lax.psum_scatter(qkv_grad, "dp", scatter_dimension=0, tiled=True)
    qkv_share = by_head(qkv_share)
    where = dp_index.astype(jnp.int32).reshape(1)
    if crossed:
        shares = (qkv_share, up_out_sum, down_sum)
        last_sum, tile = exchange_sum(last_rows, loss_part, *shares)
        masters = (w_qkv, w_out, w_up, w_down)
    else:
        shares = (
            qkv_share,
            outer_plain(pair(0), pair(3), False),
            outer_plain(pair(1), pair(4), True),
            outer_plain(pair(2), pair(5), False),
        )
        squares = sum(jnp.sum(share * share) for share in shares)
        last_sum, loss_sum, squares = lax.psum((last_rows, loss_part, squares), ("dp", "mp"))
        squares = squares + jnp.sum(last_sum * last_sum)
        row = jnp.arange(8, dtype=jnp.int32)[:, None]
        tile = jnp.where(row == 0, squares, jnp.where(row == 1, loss_sum, 0.0))
        tile = jnp.broadcast_to(tile, (8, 128))
        masters = (own_share(w_qkv, 0), own_share(w_out, 1), own_share(w_up, 0), own_share(w_down, 1))
    states = (
        (tables, tables_first, tables_second),
        (norm_gains, gains_first, gains_second),
        (masters[0], qkv_first, qkv_second),
        (masters[1], out_first, out_second),
        (masters[2], up_first, up_second),
        (masters[3], down_first, down_second),
    )
    results = update_all(crossed, where, last_sum, tile, count, shares, states, qkv_average)
    return (results[0][0, 0], results[1][0, 0], *results[2:])


def solution(mesh):
    return jax.shard_map(
        partial(shards, is_crossed(mesh.shape)),
        mesh=mesh,
        in_specs=(
            P("dp", "mp", None),
            P("dp", None, "mp", None),
            P("dp", "mp", None),
            P("dp", None),
            P(),
            P(),
            P(),
            P(),
            P(),
            P(),
            P(),
            P(None, "mp"),
            P("dp", "mp"),
            P("dp", "mp"),
            P("mp", None),
            P("mp", "dp"),
            P("mp", "dp"),
            P(None, "mp"),
            P("dp", "mp"),
            P("dp", "mp"),
            P("mp", None),
            P("mp", "dp"),
            P("mp", "dp"),
            P("dp", "mp"),
        ),
        out_specs=(
            P(),
            P(),
            P(),
            P(),
            P(),
            P(),
            P(),
            P(),
            P("dp", "mp"),
            P("dp", "mp"),
            P("dp", "mp"),
            P("mp", "dp"),
            P("mp", "dp"),
            P("mp", "dp"),
            P("dp", "mp"),
            P("dp", "mp"),
            P("dp", "mp"),
            P("mp", "dp"),
            P("mp", "dp"),
            P("mp", "dp"),
            P("dp", "mp"),
        ),
        check_vma=False,
    )
```

```python
from functools import partial
import math

import jax
import jax.numpy as jnp
from jax import lax
from jax.experimental import pallas as pl
from jax.experimental.pallas import tpu as pltpu
from jax.sharding import PartitionSpec as P

D = 1024
HEADS = 16
HEAD_DIM = 64
V = 48
PATCH_ROWS = 32
PATCH_COLS = 64
LEADS = 7


highest = lax.Precision.HIGHEST
eps_norm = 1e-05
clip_norm = 0.05
beta_first = 0.9
beta_second = 0.999
adam_eps = 1e-08
decay_rate = 0.1
lr_matrix = 0.04
lr_table = 0.1
lr_gain = 0.3
average_keep = 0.9
first_fix = 1.0 - 0.9**10
second_fix = 1.0 - 0.999**10


def layer_norm(values, gain, bias):
    center = values - jnp.mean(values, axis=-1, keepdims=True)
    spread = jnp.mean(center * center, axis=-1, keepdims=True)
    return center * lax.rsqrt(spread + eps_norm) * gain + bias


def lat_weights(pixel_rows):
    row_index = jnp.arange(pixel_rows, dtype=jnp.float32)
    cosine = jnp.cos(((row_index + 0.5) / pixel_rows - 0.5) * math.pi)
    return cosine / jnp.mean(cosine)


bf16 = jnp.bfloat16
f32 = jnp.float32
MESH = pl.DeviceIdType.MESH
NT = (((1,), (1,)), ((), ()))
TN = (((0,), (0,)), ((), ()))
VMEM = pl.BlockSpec(memory_space=pltpu.VMEM)
BIG = 56 * 2**20


def is_crossed(sizes):
    return sizes["dp"] == 4 and sizes["mp"] == 8


def mesh_place():
    dp = lax.axis_index("dp")
    mp = lax.axis_index("mp")
    return dp, mp // 2, lax.rem(mp, 2)


def device_of(dp, level, core):
    return {"dp": dp, "mp": level * 2 + core}


def cross_pairs():
    groups = lax.axis_size("dp")
    pairs = []
    for dp in range(groups):
        for level in range(groups):
            for core in range(2):
                source = (dp * groups + level) * 2 + core
                target = (level * groups + dp) * 2 + core
                pairs.append((source, target))
    return pairs


def cross(crossed, value):
    if not crossed:
        return value
    return lax.ppermute(value, ("dp", "mp"), cross_pairs())


def gather_kernel(x_ref, o_ref, send_sem, recv_sem):
    rows = x_ref.shape[0]
    half = rows // 2
    dp, level, core = mesh_place()
    side = dp + 1 - 2 * lax.rem(dp, 2)
    down = lax.rem(dp + 2, 4)
    far = 3 - dp
    to_side = device_of(side, level, core)
    to_down = device_of(down, level, core)
    to_core = device_of(dp, level, 1 - core)

    def rows_of(owner, who, first, size):
        return pl.ds(pl.multiple_of((owner * 2 + who) * rows + first, half), size)

    barrier = pltpu.get_barrier_semaphore()
    for target in (to_side, to_down, to_core):
        pl.semaphore_signal(barrier, inc=1, device_id=target, device_id_type=MESH)
    pl.semaphore_wait(barrier, 3)

    def send(slot, source, where, target):
        copy = pltpu.make_async_remote_copy(
            src_ref=source,
            dst_ref=o_ref.at[where],
            send_sem=send_sem.at[slot],
            recv_sem=recv_sem.at[slot],
            device_id=target,
            device_id_type=MESH,
        )
        copy.start()
        return copy

    first = x_ref.at[pl.ds(0, half)]
    second = x_ref.at[pl.ds(half, half)]
    side_a = send(0, first, rows_of(dp, core, 0, half), to_side)
    down_b = send(1, second, rows_of(dp, core, half, half), to_down)
    side_b = send(2, second, rows_of(dp, core, half, half), to_side)
    down_a = send(3, first, rows_of(dp, core, 0, half), to_down)
    near = send(4, x_ref, rows_of(dp, core, 0, rows), to_core)
    o_ref[rows_of(dp, core, 0, rows)] = x_ref[...]
    side_a.wait_recv()
    place = rows_of(side, core, 0, half)
    far_a = send(5, o_ref.at[place], place, to_down)
    down_b.wait_recv()
    place = rows_of(down, core, half, half)
    far_b = send(6, o_ref.at[place], place, to_side)
    side_b.wait_recv()
    place = rows_of(side, core, 0, rows)
    near_side = send(7, o_ref.at[place], place, to_core)
    down_a.wait_recv()
    place = rows_of(down, core, 0, rows)
    near_down = send(8, o_ref.at[place], place, to_core)
    far_a.wait_recv()
    far_b.wait_recv()
    place = rows_of(far, core, 0, rows)
    near_far = send(9, o_ref.at[place], place, to_core)
    for copy in (near, near_side, near_down, near_far):
        copy.wait_recv()
    for copy in (side_a, down_b, side_b, down_a, near, far_a, far_b, near_side, near_down, near_far):
        copy.wait_send()


def spread_rows(crossed, normed):
    if not crossed:
        return lax.all_gather(normed, "mp", axis=0, tiled=True)
    rows, width = normed.shape
    return pl.pallas_call(
        gather_kernel,
        out_shape=jax.ShapeDtypeStruct((8 * rows, width), normed.dtype),
        in_specs=[VMEM],
        out_specs=VMEM,
        scratch_shapes=[pltpu.SemaphoreType.DMA((10,)), pltpu.SemaphoreType.DMA((10,))],
        compiler_params=pltpu.CompilerParams(
            collective_id=1, has_side_effects=True, vmem_limit_bytes=BIG
        ),
        name="gather_rows",
    )(normed)


def exchange_kernel(to_columns, rows, width, x_ref, o_ref, send_sem, recv_sem):
    dp, level, core = mesh_place()
    me = dp * 2 + core
    barrier = pltpu.get_barrier_semaphore()
    others = []
    for step in (7, 6, 5, 4, 3, 2, 1):
        part = lax.rem(me + step, 8)
        others.append((step, part, device_of(part // 2, level, lax.rem(part, 2))))
    for step, part, target in others:
        pl.semaphore_signal(barrier, inc=1, device_id=target, device_id_type=MESH)
    pl.semaphore_wait(barrier, 7)

    def row_block(ref, part):
        return ref.at[pl.ds(pl.multiple_of(part * rows, rows), rows), :]

    def column_block(ref, part):
        return ref.at[:, pl.ds(pl.multiple_of(part * width, width), width)]

    source_block, target_block = (
        (row_block, column_block) if to_columns else (column_block, row_block)
    )
    copies = []
    for step, part, target in others:
        copy = pltpu.make_async_remote_copy(
            src_ref=source_block(x_ref, part),
            dst_ref=target_block(o_ref, me),
            send_sem=send_sem.at[step],
            recv_sem=recv_sem.at[step],
            device_id=target,
            device_id_type=MESH,
        )
        copy.start()
        copies.append(copy)
    target_block(o_ref, me)[...] = source_block(x_ref, me)[...]
    for copy in copies:
        copy.wait()


def exchange(crossed, value, to_columns, number):
    parts = lax.axis_size("mp")
    if to_columns:
        rows, width = value.shape[0] // parts, value.shape[1]
        shape = (rows, width * parts)
    else:
        rows, width = value.shape[0], value.shape[1] // parts
        shape = (rows * parts, width)
    if not crossed:
        split, joined = (0, 1) if to_columns else (1, 0)
        return lax.all_to_all(value, "mp", split_axis=split, concat_axis=joined, tiled=True)
    return pl.pallas_call(
        partial(exchange_kernel, to_columns, rows, width),
        out_shape=jax.ShapeDtypeStruct(shape, value.dtype),
        in_specs=[VMEM],
        out_specs=VMEM,
        scratch_shapes=[pltpu.SemaphoreType.DMA((8,)), pltpu.SemaphoreType.DMA((8,))],
        compiler_params=pltpu.CompilerParams(
            collective_id=number, has_side_effects=True, vmem_limit_bytes=BIG
        ),
        name="exchange_parts",
    )(value)


def pick_head(value, head, heads):
    if heads == 1:
        return value
    lane = lax.broadcasted_iota(jnp.int32, value.shape, 1) // HEAD_DIM
    return jnp.where(lane == head, value, jnp.zeros_like(value))


def attend_rows(heads, queries, k_ref, vt_ref):
    queries = queries * bf16(HEAD_DIM**-0.5)
    keys = k_ref[...]
    outs, sums = [], []
    for head in range(heads):
        scores = lax.dot_general(
            keys, pick_head(queries, head, heads), NT, preferred_element_type=f32
        )
        largest = jnp.max(scores, axis=0, keepdims=True)
        raised = jnp.exp(scores - largest)
        total = jnp.sum(raised, axis=0, keepdims=True)
        probs = (raised * (1.0 / total)).astype(bf16)
        values = vt_ref[head * HEAD_DIM : (head + 1) * HEAD_DIM, :]
        outs.append(jnp.dot(values, probs, preferred_element_type=f32))
        sums.append(largest + jnp.log(total))
    flipped = outs[0] if heads == 1 else jnp.concatenate(outs, axis=0)
    return flipped.T, sums


def attend_kernel(heads, q_ref, k_ref, v_ref, o_ref, full_ref, lse_ref, vt_ref):
    @pl.when(pl.program_id(0) == 0)
    def _():
        vt_ref[...] = v_ref[...].T

    full, sums = attend_rows(heads, q_ref[...], k_ref, vt_ref)
    for head in range(heads):
        lse_ref[head : head + 1, :] = sums[head]
    full_ref[...] = full
    o_ref[...] = full.astype(bf16)


def attend(packed):
    total, width = packed.shape[0], packed.shape[1] // 3
    heads = width // HEAD_DIM
    block = min(512, total)
    row_block = pl.BlockSpec((block, width), lambda i: (i, 0))
    return pl.pallas_call(
        partial(attend_kernel, heads),
        grid=(total // block,),
        out_shape=(
            jax.ShapeDtypeStruct((total, width), bf16),
            jax.ShapeDtypeStruct((total, width), f32),
            jax.ShapeDtypeStruct((heads, total), f32),
        ),
        in_specs=[
            row_block,
            pl.BlockSpec((total, width), lambda i: (0, 0)),
            pl.BlockSpec((total, width), lambda i: (0, 0)),
        ],
        out_specs=[row_block, row_block, pl.BlockSpec((heads, block), lambda i: (0, i))],
        scratch_shapes=[pltpu.VMEM((width, total), bf16)],
        compiler_params=pltpu.CompilerParams(vmem_limit_bytes=BIG),
        cost_estimate=pl.CostEstimate(
            flops=16 * total * total * width,
            bytes_accessed=10 * total * width,
            transcendentals=heads * total * total,
        ),
        name="attend",
    )(packed[:, :width], packed[:, width : 2 * width], packed[:, 2 * width :])


def attend_back_rows(
    heads, chunk, queries, grads, full, sums, k_ref, v_ref, kt_ref, dk_sum, dv_sum
):
    total = k_ref.shape[0]
    scale = HEAD_DIM**-0.5
    products = (grads.astype(f32) * full).T
    query_heads = [pick_head(queries, head, heads) for head in range(heads)]
    grad_heads = [pick_head(grads, head, heads) for head in range(heads)]
    inner = [
        jnp.sum(products[head * HEAD_DIM : (head + 1) * HEAD_DIM], axis=0, keepdims=True) * scale
        for head in range(heads)
    ]
    query_grads = [None] * heads
    for start in range(0, total, chunk):
        rows = slice(start, start + chunk)
        keys = k_ref[rows, :]
        values = v_ref[rows, :]
        value_part = None
        key_part = None
        for head in range(heads):
            scores = lax.dot_general(
                keys, query_heads[head] * bf16(scale), NT, preferred_element_type=f32
            )
            probs = jnp.exp(scores - sums[head])
            prob_grad = lax.dot_general(
                values, grad_heads[head] * bf16(scale), NT, preferred_element_type=f32
            )
            score_grad = (probs * (prob_grad - inner[head])).astype(bf16)
            one = jnp.dot(probs.astype(bf16), grad_heads[head], preferred_element_type=f32)
            two = jnp.dot(score_grad, query_heads[head], preferred_element_type=f32)
            value_part = one if value_part is None else value_part + one
            key_part = two if key_part is None else key_part + two
            three = jnp.dot(
                kt_ref[head * HEAD_DIM : (head + 1) * HEAD_DIM, rows],
                score_grad,
                preferred_element_type=f32,
            )
            query_grads[head] = three if query_grads[head] is None else query_grads[head] + three
        dv_sum[rows, :] += value_part
        dk_sum[rows, :] += key_part
    flipped = query_grads[0] if heads == 1 else jnp.concatenate(query_grads, axis=0)
    return flipped.T.astype(bf16)


def attend_back_kernel(
    heads, q_ref, do_ref, full_ref, lse_ref, k_ref, v_ref, dq_ref, dk_ref, dv_ref, kt_ref, dk_sum, dv_sum
):
    step = pl.program_id(0)

    @pl.when(step == 0)
    def _():
        kt_ref[...] = k_ref[...].T
        dk_sum[...] = jnp.zeros_like(dk_sum)
        dv_sum[...] = jnp.zeros_like(dv_sum)

    sums = [lse_ref[head : head + 1, :] for head in range(heads)]
    dq_ref[...] = attend_back_rows(
        heads, min(1024, k_ref.shape[0]), q_ref[...], do_ref[...], full_ref[...], sums,
        k_ref, v_ref, kt_ref, dk_sum, dv_sum,
    )

    @pl.when(step == pl.num_programs(0) - 1)
    def _():
        dk_ref[...] = dk_sum[...].astype(bf16)
        dv_ref[...] = dv_sum[...].astype(bf16)


def attend_back(grad_out, packed, full, logsum):
    total, width = grad_out.shape
    heads = width // HEAD_DIM
    block = min(256, total)
    row_block = pl.BlockSpec((block, width), lambda i: (i, 0))
    whole = pl.BlockSpec((total, width), lambda i: (0, 0))
    query_grad, key_grad, value_grad = pl.pallas_call(
        partial(attend_back_kernel, heads),
        grid=(total // block,),
        out_shape=(jax.ShapeDtypeStruct((total, width), bf16),) * 3,
        in_specs=[
            row_block,
            row_block,
            row_block,
            pl.BlockSpec((heads, block), lambda i: (0, i)),
            whole,
            whole,
        ],
        out_specs=[row_block, whole, whole],
        scratch_shapes=[
            pltpu.VMEM((width, total), bf16),
            pltpu.VMEM((total, width), f32),
            pltpu.VMEM((total, width), f32),
        ],
        compiler_params=pltpu.CompilerParams(vmem_limit_bytes=BIG),
        cost_estimate=pl.CostEstimate(
            flops=40 * total * total * width,
            bytes_accessed=16 * total * width,
            transcendentals=heads * total * total,
        ),
        name="attend_back",
    )(
        packed[:, :width],
        grad_out,
        full,
        logsum,
        packed[:, width : 2 * width],
        packed[:, 2 * width :],
    )
    return jnp.concatenate((query_grad, key_grad, value_grad), axis=1)


def normed_parts(values):
    center = values - jnp.mean(values, axis=-1, keepdims=True)
    spread = jnp.mean(center * center, axis=-1, keepdims=True)
    inverse = lax.rsqrt(spread + eps_norm)
    return center * inverse, inverse


def norm_grad(unit, inverse, gain, grad):
    scaled = grad * gain
    middle = jnp.mean(scaled, axis=-1, keepdims=True)
    along = jnp.mean(scaled * unit, axis=-1, keepdims=True)
    gain_grad = jnp.sum(grad * unit, axis=0, keepdims=True)
    bias_grad = jnp.sum(grad, axis=0, keepdims=True)
    return inverse * (scaled - middle - unit * along), gain_grad, bias_grad


def gauss_share(values):
    return 0.5 * (1.0 + lax.erf(values * (0.5**0.5)))


def branch_kernel(
    o_ref, x0_ref, gains_ref, out_ref, up_ref, down_ref, head_ref,
    x1_ref, h2_ref, g_ref, act_ref, x2_ref, pred_ref,
):
    step = pl.program_id(0)

    @pl.when(step == 0)
    def _():
        x1_ref[...] = x0_ref[...] + jnp.dot(
            o_ref[...], out_ref[...], preferred_element_type=f32
        )
        unit, _ = normed_parts(x1_ref[...])
        h2_ref[...] = (unit * gains_ref[2:3, :] + gains_ref[3:4, :]).astype(bf16)
        x2_ref[...] = x1_ref[...]

    hidden = jnp.dot(h2_ref[...], up_ref[0], preferred_element_type=f32)
    g_ref[...] = hidden
    active = (hidden * gauss_share(hidden)).astype(bf16)
    act_ref[0, 0] = active
    x2_ref[...] += jnp.dot(active, down_ref[...], preferred_element_type=f32)

    @pl.when(step == pl.num_programs(0) - 1)
    def _():
        unit, _ = normed_parts(x2_ref[...])
        last = unit * gains_ref[4:5, :] + gains_ref[5:6, :]
        pred_ref[...] = lax.dot_general(
            last, head_ref[...], NT, precision=highest, preferred_element_type=f32
        )


def weight_specs(w_out, w_up, w_down):
    _, width, units = w_up.shape
    return (
        pl.BlockSpec(w_out.shape, lambda i: (0, 0)),
        pl.BlockSpec((1, width, units), lambda i: (i, 0, 0)),
        pl.BlockSpec((units, width), lambda i: (i, 0)),
    )


def branch_forward(attended, x_first, norm_gains, gathered, head):
    w_out, w_up, w_down, _ = gathered
    rows, width = x_first.shape
    parts, units = w_up.shape[0], w_up.shape[2]
    fixed = lambda shape: pl.BlockSpec(shape, lambda i: (0, 0))
    by_units = pl.BlockSpec((rows, units), lambda i: (0, i))
    by_core = pl.BlockSpec((1, 1, rows, units), lambda i: (i % 2, i // 2, 0, 0))
    columns = head.shape[0]
    flops = 2 * rows * (width * width + 2 * width * parts * units + 6 * width * columns)
    return pl.pallas_call(
        branch_kernel,
        grid=(parts,),
        out_shape=(
            jax.ShapeDtypeStruct((rows, width), f32),
            jax.ShapeDtypeStruct((rows, width), bf16),
            jax.ShapeDtypeStruct((rows, parts * units), f32),
            jax.ShapeDtypeStruct((2, parts // 2, rows, units), bf16),
            jax.ShapeDtypeStruct((rows, width), f32),
            jax.ShapeDtypeStruct((rows, columns), f32),
        ),
        in_specs=[
            fixed((rows, width)),
            fixed((rows, width)),
            fixed(norm_gains.shape),
            *weight_specs(w_out, w_up, w_down),
            fixed(head.shape),
        ],
        out_specs=[
            fixed((rows, width)),
            fixed((rows, width)),
            by_units,
            by_core,
            fixed((rows, width)),
            fixed((rows, columns)),
        ],
        compiler_params=pltpu.CompilerParams(vmem_limit_bytes=BIG),
        cost_estimate=pl.CostEstimate(
            flops=flops,
            bytes_accessed=4 * width * parts * units + 6 * rows * parts * units,
            transcendentals=rows * parts * units,
        ),
        name="branch_forward",
    )(attended, x_first, norm_gains, w_out, w_up, w_down, head)


def branch_back_kernel(
    dpred_ref, x2_ref, x1_ref, gains_ref, g_ref, out_ref, up_ref, down_ref, head_ref,
    dx2_ref, dg_ref, dx1_ref, low_ref, do_ref, gain_ref, dhead_ref,
    wide_ref, sum_ref,
):
    step = pl.program_id(0)

    @pl.when(step == 0)
    def _():
        grad = dpred_ref[...]
        unit, inverse = normed_parts(x2_ref[...])
        gain = gains_ref[4:5, :]
        last = unit * gain + gains_ref[5:6, :]
        dhead_ref[...] = lax.dot_general(
            grad, last, TN, precision=highest, preferred_element_type=f32
        )
        row_grad = jnp.dot(grad, head_ref[...], precision=highest, preferred_element_type=f32)
        wide, gain_grad, bias_grad = norm_grad(unit, inverse, gain, row_grad)
        gain_ref[...] = jnp.zeros_like(gain_ref)
        gain_ref[4:5, :] = gain_grad
        gain_ref[5:6, :] = bias_grad
        wide_ref[...] = wide
        dx2_ref[...] = wide.astype(bf16)
        sum_ref[...] = jnp.zeros_like(sum_ref)

    active_grad = lax.dot_general(dx2_ref[...], down_ref[...], NT, preferred_element_type=f32)
    hidden = g_ref[...]
    slope = gauss_share(hidden) + hidden * (
        jnp.exp(-0.5 * hidden * hidden) * (2.0 * math.pi) ** -0.5
    )
    hidden_grad = (active_grad * slope).astype(bf16)
    dg_ref[0, 0] = hidden_grad
    sum_ref[...] += lax.dot_general(hidden_grad, up_ref[0], NT, preferred_element_type=f32)

    @pl.when(step == pl.num_programs(0) - 1)
    def _():
        unit, inverse = normed_parts(x1_ref[...])
        middle, gain_grad, bias_grad = norm_grad(unit, inverse, gains_ref[2:3, :], sum_ref[...])
        gain_ref[2:3, :] = gain_grad
        gain_ref[3:4, :] = bias_grad
        middle = wide_ref[...] + middle
        dx1_ref[...] = middle
        low_ref[...] = middle.astype(bf16)
        total = lax.dot_general(low_ref[...], out_ref[...], NT, preferred_element_type=f32)
        do_ref[...] = total.astype(bf16)


def branch_backward(pred_grad, x_last, x_mid, norm_gains, hidden, gathered, head):
    w_out, w_up, w_down, _ = gathered
    rows, width = x_last.shape
    parts, units = w_up.shape[0], w_up.shape[2]
    fixed = lambda shape: pl.BlockSpec(shape, lambda i: (0, 0))
    by_units = pl.BlockSpec((rows, units), lambda i: (0, i))
    by_core = pl.BlockSpec((1, 1, rows, units), lambda i: (i % 2, i // 2, 0, 0))
    columns = head.shape[0]
    wide = (rows, width)
    flops = 2 * rows * (width * width + 2 * width * parts * units + 12 * width * columns)
    return pl.pallas_call(
        branch_back_kernel,
        grid=(parts,),
        out_shape=(
            jax.ShapeDtypeStruct(wide, bf16),
            jax.ShapeDtypeStruct((2, parts // 2, rows, units), bf16),
            jax.ShapeDtypeStruct(wide, f32),
            jax.ShapeDtypeStruct(wide, bf16),
            jax.ShapeDtypeStruct(wide, bf16),
            jax.ShapeDtypeStruct((6, width), f32),
            jax.ShapeDtypeStruct((columns, width), f32),
        ),
        in_specs=[
            fixed((rows, columns)),
            fixed(wide),
            fixed(wide),
            fixed(norm_gains.shape),
            by_units,
            *weight_specs(w_out, w_up, w_down),
            fixed(head.shape),
        ],
        out_specs=[
            fixed(wide),
            by_core,
            fixed(wide),
            fixed(wide),
            fixed(wide),
            fixed((6, width)),
            fixed((columns, width)),
        ],
        scratch_shapes=[pltpu.VMEM(wide, f32), pltpu.VMEM(wide, f32)],
        compiler_params=pltpu.CompilerParams(vmem_limit_bytes=BIG),
        cost_estimate=pl.CostEstimate(
            flops=flops,
            bytes_accessed=4 * width * parts * units + 6 * rows * parts * units,
            transcendentals=2 * rows * parts * units,
        ),
        name="branch_backward",
    )(pred_grad, x_last, x_mid, norm_gains, hidden, w_out, w_up, w_down, head)


def plane_parts(me):
    return [(move, lax.rem(me + move, 8)) for move in (7, 6, 5, 4, 3, 2, 1)]


def swap_kernel(*refs):
    value_ref, act_ref, dg_ref, o_ref, dx2_ref, h2_ref, dx1_ref = refs[:7]
    rows_ref, act_out, dg_out, o_out, dx2_out, h2_out, dx1_out = refs[7:14]
    send_sem, recv_sem, own_sem = refs[14:]
    dp, level, core = mesh_place()
    me = dp * 2 + core
    rows, width = value_ref.shape[0], value_ref.shape[1] // 8
    near = device_of(dp, level, 1 - core)
    barrier = pltpu.get_barrier_semaphore()
    others = [
        (part, device_of(part // 2, level, lax.rem(part, 2))) for _, part in plane_parts(me)
    ]
    for _, target in others:
        pl.semaphore_signal(barrier, inc=1, device_id=target, device_id_type=MESH)
    pl.semaphore_wait(barrier, 7)
    started = []

    def send(source, target_ref, target):
        slot = len(started)
        copy = pltpu.make_async_remote_copy(
            src_ref=source,
            dst_ref=target_ref,
            send_sem=send_sem.at[slot],
            recv_sem=recv_sem.at[slot],
            device_id=target,
            device_id_type=MESH,
        )
        copy.start()
        started.append(copy)

    def row_block(part):
        return rows_ref.at[pl.ds(pl.multiple_of(part * rows, rows), rows), :]

    def column_block(ref, part):
        return ref.at[:, pl.ds(pl.multiple_of(part * width, width), width)]

    for part, target in others:
        send(column_block(value_ref, part), row_block(me), target)
    locals_ = []

    def keep(source, target_ref):
        copy = pltpu.make_async_copy(source, target_ref, own_sem.at[len(locals_)])
        copy.start()
        locals_.append(copy)

    for source, out in ((act_ref, act_out), (dg_ref, dg_out)):
        send(source.at[1 - core], out.at[1], near)
        keep(source.at[core], out.at[0])
    for index in range(4):
        send(column_block(o_ref, index * 2 + 1 - core), o_out.at[1, index], near)
        keep(column_block(o_ref, index * 2 + core), o_out.at[0, index])
    for source, out in ((dx2_ref, dx2_out), (h2_ref, h2_out), (dx1_ref, dx1_out)):
        send(source, out, near)
    row_block(me)[...] = column_block(value_ref, me)[...]
    for copy in started:
        copy.wait()
    for copy in locals_:
        copy.wait()


def exchange_swap(value, act, dg, attended, dx2, h2, dx1):
    rows, width = value.shape
    anywhere = pl.BlockSpec(memory_space=pl.ANY)
    outs = [
        (8 * rows, width // 8), act.shape, dg.shape, (2, 4, rows, width // 8),
        dx2.shape, h2.shape, dx1.shape,
    ]
    return pl.pallas_call(
        swap_kernel,
        out_shape=[jax.ShapeDtypeStruct(shape, bf16) for shape in outs],
        in_specs=[VMEM] * 7,
        out_specs=[VMEM] + [anywhere] * 6,
        scratch_shapes=[
            pltpu.SemaphoreType.DMA((16,)),
            pltpu.SemaphoreType.DMA((16,)),
            pltpu.SemaphoreType.DMA((6,)),
        ],
        compiler_params=pltpu.CompilerParams(
            collective_id=3, has_side_effects=True, vmem_limit_bytes=BIG
        ),
        name="exchange_swap",
    )(value, act, dg, attended, dx2, h2, dx1)


class Scatter:
    order = (0, 3, 1, 2)

    def __init__(self, refs, sems):
        self.send_ref, self.keep_ref, self.one_ref, self.two_ref, self.own_ref, self.deep_ref = refs
        self.one, self.two, self.deep = sems
        self.dp, self.level, self.core = mesh_place()
        self.x, self.y = lax.rem(self.dp, 2), self.dp // 2
        self.side = device_of(self.dp + 1 - 2 * self.x, self.level, self.core)
        self.down = device_of(lax.rem(self.dp + 2, 4), self.level, self.core)

    def copy(self, source, target_ref, sems, slot, place, target):
        return pltpu.make_async_remote_copy(
            src_ref=source,
            dst_ref=target_ref,
            send_sem=sems.at[0, slot],
            recv_sem=sems.at[1, place],
            device_id=target,
            device_id_type=MESH,
        )

    def first(self, depth):
        target = self.side if depth < 2 else self.down
        return self.copy(
            self.send_ref.at[depth], self.one_ref.at[depth], self.one, depth, depth, target
        )

    def second(self, depth):
        target = self.down if depth < 2 else self.side
        which = 1 - self.y if depth < 2 else 1 - self.x
        return self.copy(
            self.keep_ref.at[depth, which], self.two_ref.at[depth], self.two, depth, depth, target
        )

    def mine(self, depth):
        return self.y if depth < 2 else self.x

    def third(self, depth):
        place = lax.rem(self.level + 7 - depth, 4)
        return self.copy(
            self.keep_ref.at[depth, self.mine(depth)], self.deep_ref.at[place], self.deep, depth,
            place, device_of(self.dp, depth, self.core),
        )

    def begin(self, depth, products, held_ref):
        height = self.keep_ref.shape[2]
        top = 0
        for product in products:
            rows, size = product.shape[0], product.shape[1] // 4
            for split in range(4):
                held_ref[split, top : top + rows, :] = product[
                    :, split * size : (split + 1) * size
                ].astype(bf16)
            top += rows
        for which in range(2):
            if depth < 2:
                moved, stays = which * 2 + 1 - self.x, which * 2 + self.x
            else:
                moved, stays = (1 - self.y) * 2 + which, self.y * 2 + which
            self.send_ref[depth, which] = held_ref[moved, :height, :]
            self.keep_ref[depth, which] = held_ref[stays, :height, :]
        self.first(depth).start()

    def middle(self, depth):
        self.first(depth).wait_recv()
        for which in range(2):
            self.keep_ref[depth, which] = (
                self.keep_ref[depth, which].astype(f32) + self.one_ref[depth, which].astype(f32)
            ).astype(bf16)
        self.second(depth).start()

    def end(self, depth):
        self.second(depth).wait_recv()
        total = self.keep_ref[depth, self.mine(depth)].astype(f32) + self.two_ref[depth].astype(f32)

        @pl.when(self.level == depth)
        def _():
            self.own_ref[...] = total

        @pl.when(self.level != depth)
        def _():
            self.keep_ref[depth, self.mine(depth)] = total.astype(bf16)
            self.third(depth).start()

    def finish(self, result_ref):
        for place in range(3):
            self.copy(
                self.keep_ref.at[0, 0], self.deep_ref.at[place], self.deep, 0, place, self.side
            ).wait_recv()
        result_ref[...] = self.own_ref[...] + (
            self.deep_ref[0].astype(f32) + self.deep_ref[1].astype(f32) + self.deep_ref[2].astype(f32)
        )
        for depth in range(4):
            self.first(depth).wait_send()
            self.second(depth).wait_send()

            @pl.when(self.level != depth)
            def _(depth=depth):
                self.third(depth).wait_send()


def scatter_scratch(height, share):
    return [
        pltpu.VMEM((4, 2, height, share), bf16),
        pltpu.VMEM((4, 2, height, share), bf16),
        pltpu.VMEM((4, 2, height, share), bf16),
        pltpu.VMEM((4, height, share), bf16),
        pltpu.VMEM((height, share), f32),
        pltpu.VMEM((3, height, share), bf16),
        pltpu.VMEM((4, height, share), bf16),
        pltpu.SemaphoreType.DMA((2, 4)),
        pltpu.SemaphoreType.DMA((2, 4)),
        pltpu.SemaphoreType.DMA((2, 4)),
    ]


def summed(lefts, rights):
    total = None
    for left, right in zip(lefts, rights):
        part = lax.dot_general(left, right, TN, preferred_element_type=f32)
        total = part if total is None else total + part
    return total


def chunk_spec(shape):
    def where(i):
        index = jnp.minimum(i, 3)
        first, last = (3 - index) // 3, index // 3
        middle = 1 - first - last
        return 0, middle * (5 - 2 * index) + 2 * last, 0, 0

    return pl.BlockSpec((2, 1) + shape, where)


def once(shape):
    return pl.BlockSpec(shape, lambda i: (0,) * len(shape), pipeline_mode=pl.Buffered(1))


pieces_at, turns, entry_turns = 9, 14, 11


def finish_kernel(*refs):
    steps = (refs[0:3], refs[3:6])
    qkv_ref, do_ref, full_ref, lse_ref, rows_ref, prev_ref = refs[6:12]
    token_out, share_ref, down_ref = refs[12:15]
    dqkv_ref, kt_ref, dk_sum, dv_sum, piece_send, piece_recv, piece_own = refs[15:22]
    part_sem, piece_sem, own_sem = refs[22:25]
    scatter = Scatter(refs[25:31], refs[32:35])
    held_ref = refs[31]
    turn = pl.program_id(0)
    dp, level, core = mesh_place()
    me = dp * 2 + core
    width = do_ref.shape[1]
    heads = width // HEAD_DIM
    rows = do_ref.shape[0] // 8
    others = [
        (move, part, device_of(part // 2, level, lax.rem(part, 2))) for move, part in plane_parts(me)
    ]

    def remote(source, target_ref, send_sem, recv_sem, target):
        return pltpu.make_async_remote_copy(
            src_ref=source,
            dst_ref=target_ref,
            send_sem=send_sem,
            recv_sem=recv_sem,
            device_id=target,
            device_id_type=MESH,
        )

    def own_rows(part):
        return dqkv_ref.at[pl.ds(pl.multiple_of(part * rows, rows), rows), :]

    own_columns = token_out.at[:, pl.ds(pl.multiple_of(me * 3 * width, 3 * width), 3 * width)]

    def part_copy(move, part, target):
        return remote(
            own_rows(part), own_columns, part_sem.at[0, move], part_sem.at[1, move], target
        )

    def piece_copy(index):
        place = lax.rem(level + 7 - index, 4)
        return remote(
            piece_send.at[index], piece_recv.at[place], piece_sem.at[0, index],
            piece_sem.at[1, place], device_of(dp, index, core),
        )

    own_part = pltpu.make_async_copy(own_rows(me), own_columns, own_sem)

    @pl.when(turn == 0)
    def _():
        barrier = pltpu.get_barrier_semaphore()
        deep = [device_of(dp, lax.rem(level + move, 4), core) for move in (1, 2, 3)]
        for target in [target for _, _, target in others] + deep:
            pl.semaphore_signal(barrier, inc=1, device_id=target, device_id_type=MESH)
        pl.semaphore_wait(barrier, 10)
        kt_ref[...] = qkv_ref[:, width : 2 * width].T
        dk_sum[...] = jnp.zeros_like(dk_sum)
        dv_sum[...] = jnp.zeros_like(dv_sum)

    for index, depth in enumerate(scatter.order):

        @pl.when(turn == index)
        def _(depth=depth):
            lefts, rights = [], []
            for act, dx2, dx2_near in steps:
                lefts += [act[0, 0], act[1, 0]]
                rights += [dx2[...], dx2_near[...]]
            scatter.begin(depth, [summed(lefts, rights)], held_ref)

        @pl.when(turn == index + 3)
        def _(depth=depth):
            scatter.middle(depth)

        @pl.when(turn == index + 5)
        def _(depth=depth):
            scatter.end(depth)

    @pl.when(turn < 8)
    def _():
        where = pl.ds(pl.multiple_of(turn * rows, rows), rows)
        sums = [lse_ref[head : head + 1, where] for head in range(heads)]
        dqkv_ref[where, :width] = attend_back_rows(
            heads, 1024, qkv_ref[where, :width], do_ref[where, :], full_ref[where, :], sums,
            qkv_ref.at[:, width : 2 * width], qkv_ref.at[:, 2 * width :], kt_ref, dk_sum, dv_sum,
        )

    @pl.when(turn == 8)
    def _():
        dqkv_ref[:, width : 2 * width] = dk_sum[...].astype(bf16)
        dqkv_ref[:, 2 * width :] = dv_sum[...].astype(bf16)
        for other in others:
            part_copy(*other).start()
        own_part.start()

    for index in range(4):

        @pl.when(turn == pieces_at + index)
        def _(index=index):
            piece = prev_ref[...] + lax.dot_general(
                rows_ref[...], dqkv_ref[...], TN, preferred_element_type=f32
            )

            @pl.when(level == index)
            def _():
                piece_own[...] = piece

            @pl.when(level != index)
            def _():
                piece_send[index] = piece.astype(bf16)
                piece_copy(index).start()

    @pl.when(turn == turns - 1)
    def _():
        scatter.finish(down_ref)
        for place in range(3):
            remote(
                piece_send.at[0], piece_recv.at[place], piece_sem.at[0, 0],
                piece_sem.at[1, place], scatter.side,
            ).wait_recv()
        share_ref[...] = piece_own[...] + (
            piece_recv[0].astype(f32) + piece_recv[1].astype(f32) + piece_recv[2].astype(f32)
        )
        for other in others:
            part_copy(*other).wait()
        own_part.wait()
        for index in range(4):

            @pl.when(level != index)
            def _(index=index):
                piece_copy(index).wait_send()


def finish_program(kept, packed, own_grad, full, logsum, rows_one, earlier):
    rows, width = own_grad.shape[0] // 8, own_grad.shape[1]
    in_specs, operands = [], []
    for act, dx2, dx2_near in kept:
        operands += [act, dx2, dx2_near]
        in_specs += [chunk_spec(act.shape[2:]), once(dx2.shape), once(dx2.shape)]
    piece = lambda i: jnp.clip(i - pieces_at, 0, 3)
    in_specs += [
        once(packed.shape),
        once(own_grad.shape),
        once(full.shape),
        once(logsum.shape),
        pl.BlockSpec((8 * rows, D // 4), lambda i: (0, piece(i))),
        pl.BlockSpec((D // 4, 3 * width), lambda i: (piece(i), 0)),
    ]
    operands += [packed, own_grad, full, logsum, rows_one, earlier]
    fixed = lambda shape: pl.BlockSpec(shape, lambda i: (0, 0))
    units = kept[0][0].shape[3]
    share = D // 4
    return pl.pallas_call(
        finish_kernel,
        grid=(turns,),
        out_shape=[
            jax.ShapeDtypeStruct((rows, 24 * width), bf16),
            jax.ShapeDtypeStruct((share, 3 * width), f32),
            jax.ShapeDtypeStruct((units, share), f32),
        ],
        in_specs=in_specs,
        out_specs=[
            pl.BlockSpec(memory_space=pl.ANY),
            fixed((share, 3 * width)),
            fixed((units, share)),
        ],
        scratch_shapes=[
            pltpu.VMEM((8 * rows, 3 * width), bf16),
            pltpu.VMEM((width, 8 * rows), bf16),
            pltpu.VMEM((8 * rows, width), f32),
            pltpu.VMEM((8 * rows, width), f32),
            pltpu.VMEM((4, share, 3 * width), bf16),
            pltpu.VMEM((3, share, 3 * width), bf16),
            pltpu.VMEM((share, 3 * width), f32),
            pltpu.SemaphoreType.DMA((2, 8)),
            pltpu.SemaphoreType.DMA((2, 4)),
            pltpu.SemaphoreType.DMA,
        ]
        + scatter_scratch(units, share),
        compiler_params=pltpu.CompilerParams(
            collective_id=4, has_side_effects=True, vmem_limit_bytes=BIG
        ),
        name="finish_program",
    )(*operands)


def tie(*values):
    return lax.optimization_barrier(values)


def choose(value, index, axis=0):
    return lax.dynamic_index_in_dim(value, index, axis, keepdims=False)


def outer_plain(lefts, rights, by_rows):
    dp, mp = lax.axis_size("dp"), lax.axis_size("mp")
    grads = sum(
        lax.dot_general(left, right, TN, preferred_element_type=f32)
        for left, right in zip(lefts, rights)
    ).astype(bf16)
    rows, width = grads.shape
    if by_rows:
        grads = grads.reshape(dp, rows // dp, mp, width // mp).transpose(0, 2, 1, 3)
    else:
        grads = grads.reshape(mp, rows // mp, dp, width // dp).transpose(2, 0, 1, 3)
    grads = grads.reshape((dp * mp,) + grads.shape[2:])
    return lax.psum_scatter(grads, ("dp", "mp"), scatter_dimension=0, tiled=False).astype(f32)


def exchange_sum_kernel(
    x_ref, loss_ref, qkv_ref, up_out_ref, down_ref, o_ref, s_ref, work_ref, pair_ref, quad_ref, eight_ref, deep_ref, tile_ref,
    send_sem, recv_sem,
):
    dp, level, core = mesh_place()
    x, y = lax.rem(dp, 2), dp // 2
    side = device_of(dp + 1 - 2 * x, level, core)
    down = device_of(lax.rem(dp + 2, 4), level, core)
    near = device_of(dp, level, 1 - core)
    deep = [device_of(dp, lax.rem(level + step, 4), core) for step in (1, 2, 3)]
    barrier = pltpu.get_barrier_semaphore()
    for target in (side, down, near, *deep):
        pl.semaphore_signal(barrier, inc=1, device_id=target, device_id_type=MESH)
    pl.semaphore_wait(barrier, 6)
    started = []

    def send(source, target_ref, target):
        slot = len(started)
        copy = pltpu.make_async_remote_copy(
            src_ref=source,
            dst_ref=target_ref,
            send_sem=send_sem.at[slot],
            recv_sem=recv_sem.at[slot],
            device_id=target,
            device_id_type=MESH,
        )
        copy.start()
        started.append(copy)
        return copy

    half = x_ref.shape[0] // 2
    quarter, eighth, part, unit = half // 2, half // 4, half // 8, half // 16

    def rows(start, size):
        return pl.ds(pl.multiple_of(start, unit), size)

    copy = send(x_ref.at[rows((1 - core) * half, half)], pair_ref, near)
    copy.wait_recv()
    work_ref[...] = x_ref[rows(core * half, half)] + pair_ref[...]
    one = send(work_ref.at[rows((1 - x) * eighth, eighth)], quad_ref.at[0], side)
    two = send(work_ref.at[rows(quarter + (1 - y) * eighth, eighth)], quad_ref.at[1], down)
    base_a = x * eighth
    base_b = quarter + y * eighth
    wide_a, wide_b = core * half + base_a, core * half + base_b
    one.wait_recv()
    work_ref[rows(base_a, eighth)] += quad_ref[0]
    one = send(work_ref.at[rows(base_a + (1 - y) * part, part)], eight_ref.at[0], down)
    two.wait_recv()
    work_ref[rows(base_b, eighth)] += quad_ref[1]
    two = send(work_ref.at[rows(base_b + (1 - x) * part, part)], eight_ref.at[1], side)
    base_a = base_a + y * part
    base_b = base_b + x * part
    one.wait_recv()
    work_ref[rows(base_a, part)] += eight_ref[0]
    two.wait_recv()
    work_ref[rows(base_b, part)] += eight_ref[1]

    def level_start(which):
        late = which // 2
        return (1 - late) * base_a + late * base_b + lax.rem(which, 2) * unit

    copies = []
    for step in (1, 2, 3):
        source = work_ref.at[rows(level_start(lax.rem(level + step, 4)), unit)]
        copies.append(send(source, deep_ref.at[step - 1], deep[step - 1]))
    for copy in copies:
        copy.wait_recv()
    total = work_ref[rows(level_start(level), unit)] + deep_ref[0] + deep_ref[1] + deep_ref[2]
    mine = rows(core * half + level_start(level), unit)
    base_a = core * half + base_a
    base_b = core * half + base_b
    o_ref[mine] = total
    row = lax.broadcasted_iota(jnp.int32, s_ref.shape, 0)
    squares = jnp.sum(total * total)
    for ref in (qkv_ref, up_out_ref, down_ref):
        squares += jnp.sum(ref[...] * ref[...])
    tile_ref[0] = jnp.where(row == 0, squares, jnp.where(row == 1, loss_ref[...], 0.0))
    copies = []
    for step in (1, 2, 3):
        copies.append(send(o_ref.at[mine], o_ref.at[mine], deep[step - 1]))
        copies.append(send(tile_ref.at[0], tile_ref.at[step], deep[step - 1]))
    for copy in copies:
        copy.wait_recv()
    one = send(o_ref.at[rows(base_a, part)], o_ref.at[rows(base_a, part)], down)
    two = send(o_ref.at[rows(base_b, part)], o_ref.at[rows(base_b, part)], side)
    tile_ref[4] = tile_ref[0] + tile_ref[1] + tile_ref[2] + tile_ref[3]
    three = send(tile_ref.at[4], tile_ref.at[5], side)
    one.wait_recv()
    one = send(o_ref.at[rows(wide_a, eighth)], o_ref.at[rows(wide_a, eighth)], side)
    two.wait_recv()
    two = send(o_ref.at[rows(wide_b, eighth)], o_ref.at[rows(wide_b, eighth)], down)
    three.wait_recv()
    tile_ref[6] = tile_ref[4] + tile_ref[5]
    three = send(tile_ref.at[6], tile_ref.at[7], down)
    one.wait_recv()
    two.wait_recv()
    one = send(o_ref.at[rows(core * half, half)], o_ref.at[rows(core * half, half)], near)
    three.wait_recv()
    tile_ref[8] = tile_ref[6] + tile_ref[7]
    three = send(tile_ref.at[8], tile_ref.at[9], near)
    one.wait_recv()
    three.wait_recv()
    s_ref[...] = tile_ref[8] + tile_ref[9]
    for copy in started:
        copy.wait_send()


def exchange_sum(value, loss, *shares):
    rows, width = value.shape
    tile = jax.ShapeDtypeStruct((8, 128), f32)
    return pl.pallas_call(
        exchange_sum_kernel,
        out_shape=(jax.ShapeDtypeStruct(value.shape, f32), tile),
        in_specs=[VMEM] * 5,
        out_specs=[VMEM, VMEM],
        scratch_shapes=[
            pltpu.VMEM((rows // 2, width), f32),
            pltpu.VMEM((rows // 2, width), f32),
            pltpu.VMEM((2, rows // 8, width), f32),
            pltpu.VMEM((2, rows // 16, width), f32),
            pltpu.VMEM((3, rows // 32, width), f32),
            pltpu.VMEM((10,) + tile.shape, f32),
            pltpu.SemaphoreType.DMA((24,)),
            pltpu.SemaphoreType.DMA((24,)),
        ],
        compiler_params=pltpu.CompilerParams(
            collective_id=5, has_side_effects=True, vmem_limit_bytes=BIG
        ),
        name="exchange_sum",
    )(value, loss.reshape(1, 1), *shares)


def split_low(values):
    high = values.astype(bf16)
    return high, (values - high.astype(f32)).astype(bf16)


def three_products(left, right, dims=(((1,), (0,)), ((), ()))):
    def product(one, two):
        return lax.dot_general(one, two, dims, preferred_element_type=f32)

    return product(left[0], right[0]) + (product(left[1], right[0]) + product(left[0], right[1]))


def exact_product(left, right, dims=(((1,), (0,)), ((), ()))):
    return lax.dot_general(left, right, dims, precision=highest, preferred_element_type=f32)


def head_marks(width):
    head = lax.broadcasted_iota(jnp.int32, (HEADS, width), 0)
    column = lax.broadcasted_iota(jnp.int32, (HEADS, width), 1)
    return jnp.where(column // HEAD_DIM == head, 1.0, 0.0).astype(f32)


def quarter_marks(padded):
    row = lax.broadcasted_iota(jnp.int32, (padded, V), 0)
    column = lax.broadcasted_iota(jnp.int32, (padded, V), 1)
    return jnp.where(row // 4 == column, 0.25, 0.0).astype(f32)


def tables_kernel(tables_ref, hot_ref, patch_ref, var_ref, keyed_ref, bias_ref):
    padded, width = patch_ref.shape
    query = tables_ref[5 * V + LEADS : 5 * V + LEADS + 1, :]
    patch_ref[...] = jnp.zeros_like(patch_ref)
    patch_ref[: 4 * V, :] = tables_ref[: 4 * V, :]
    chosen = exact_product(hot_ref[...], tables_ref[4 * V : 5 * V, :])
    var_ref[...] = exact_product(quarter_marks(padded), chosen)
    marks = head_marks(width)
    scale = HEAD_DIM**-0.5
    keyed_ref[...] = exact_product(marks, patch_ref[...] * query, NT) * scale
    bias = exact_product(marks, var_ref[...] * query, NT) * (4.0 * scale)
    column = lax.broadcasted_iota(jnp.int32, bias.shape, 1)
    bias_ref[...] = jnp.where(column < 4 * V, bias, -1e30)


def prepare_tables(tables, var_hot):
    padded = 256
    return pl.pallas_call(
        tables_kernel,
        out_shape=(
            jax.ShapeDtypeStruct((padded, D), f32),
            jax.ShapeDtypeStruct((padded, D), f32),
            jax.ShapeDtypeStruct((HEADS, padded), f32),
            jax.ShapeDtypeStruct((HEADS, padded), f32),
        ),
        compiler_params=pltpu.CompilerParams(vmem_limit_bytes=BIG),
        name="prepare_tables",
    )(tables, var_hot)


def four_sum(values):
    size = values.shape[1]
    lane = lax.broadcasted_iota(jnp.int32, values.shape, 1)
    values = values + jnp.where(
        lane % 2 == 0, pltpu.roll(values, size - 1, 1), pltpu.roll(values, 1, 1)
    )
    return values + jnp.where(
        lane % 4 < 2, pltpu.roll(values, size - 2, 1), pltpu.roll(values, 2, 1)
    )


def cell_shares(cells, keyed, bias):
    scores = four_sum(cells * keyed) + bias
    raised = jnp.exp(scores - jnp.max(scores, axis=1, keepdims=True))
    total = jnp.sum(raised, axis=1, keepdims=True) * 0.25
    return raised * (1.0 / total)


def embed_pair(pair, cells, keyed_ref, bias_ref, patch_ref, var_ref, x0_ref):
    patch = split_low(patch_ref[...])
    variable = split_low(var_ref[...])
    outs = []
    for which in range(2):
        row = pl.ds(pair * 2 + which, 1)
        shares = cell_shares(cells, keyed_ref[row, :], bias_ref[row, :])
        outs.append(
            three_products(split_low(shares * cells), patch)
            + three_products(split_low(shares), variable)
        )
    lane = lax.broadcasted_iota(jnp.int32, outs[0].shape, 1)
    columns = pl.ds(pl.multiple_of(pair * 2 * HEAD_DIM, 2 * HEAD_DIM), 2 * HEAD_DIM)
    x0_ref[:, columns] = jnp.where(lane < HEAD_DIM, outs[0], outs[1])


def embed_kernel(
    u_ref, keyed_ref, bias_ref, patch_ref, var_ref, lead_ref, gains_ref, x0_ref, h1_ref
):
    pair = pl.program_id(0)
    embed_pair(pair, u_ref[...], keyed_ref, bias_ref, patch_ref, var_ref, x0_ref)

    @pl.when(pair == pl.num_programs(0) - 1)
    def _():
        x0_ref[...] += lead_ref[...]
        unit, _ = normed_parts(x0_ref[...])
        h1_ref[...] = (unit * gains_ref[0:1, :] + gains_ref[1:2, :]).astype(bf16)


def embed_forward(cells, prepared, lead_row, norm_gains):
    patch, variable, keyed, bias = prepared
    rows, padded = cells.shape
    fixed = lambda shape: pl.BlockSpec(shape, lambda i: (0, 0))
    by_pair = pl.BlockSpec((padded, 2 * HEAD_DIM), lambda i: (0, i))
    return pl.pallas_call(
        embed_kernel,
        grid=(HEADS // 2,),
        out_shape=(
            jax.ShapeDtypeStruct((rows, D), f32),
            jax.ShapeDtypeStruct((rows, D), bf16),
        ),
        in_specs=[
            fixed((rows, padded)),
            fixed(keyed.shape),
            fixed(bias.shape),
            by_pair,
            by_pair,
            fixed((1, D)),
            fixed(norm_gains.shape),
        ],
        out_specs=[fixed((rows, D)), fixed((rows, D))],
        compiler_params=pltpu.CompilerParams(vmem_limit_bytes=BIG),
        cost_estimate=pl.CostEstimate(
            flops=24 * rows * padded * D, bytes_accessed=14 * rows * D, transcendentals=16 * rows * padded
        ),
        name="embed_forward",
    )(cells, keyed, bias, patch, variable, lead_row, norm_gains)


def entry_rows(
    grad_ref, qkv_ref, x0_ref, mid_ref, gains_ref, du_ref, gain_ref, lead_ref, dx_ref, flip_ref
):
    row_grad = jnp.dot(grad_ref[...], qkv_ref[...], preferred_element_type=f32)
    unit, inverse = normed_parts(x0_ref[...])
    part, gain_grad, bias_grad = norm_grad(unit, inverse, gains_ref[0:1, :], row_grad)
    total = mid_ref[...] + part
    dx_ref[...] = total
    flip_ref[...] = total.T
    lead_ref[...] = jnp.sum(total, axis=0, keepdims=True)
    gain_ref[0:1, :] = gain_grad
    gain_ref[1:2, :] = bias_grad
    du_ref[...] = jnp.zeros_like(du_ref)


def entry_pair(
    pair, u_ref, keyed_ref, bias_ref, patch_ref, var_ref,
    du_ref, dpatch_ref, dvar_ref, dkeyed_ref, dbias_ref, dx_ref, flip_ref,
):
    cells = u_ref[...]
    size = 2 * HEAD_DIM
    columns = pl.ds(pl.multiple_of(pair * size, size), size)
    grads = dx_ref[:, columns]
    lane = lax.broadcasted_iota(jnp.int32, grads.shape, 1)
    patch = split_low(patch_ref[...])
    variable = split_low(var_ref[...])
    cells_grad = None
    for which in range(2):
        row = pl.ds(pair * 2 + which, 1)
        keyed = keyed_ref[row, :]
        shares = cell_shares(cells, keyed, bias_ref[row, :])
        one = split_low(jnp.where(lane // HEAD_DIM == which, grads, 0.0))
        mixed_grad = three_products(one, patch, NT)
        share_grad = mixed_grad * cells + three_products(one, variable, NT)
        weighted = shares * share_grad
        inner = jnp.sum(weighted, axis=1, keepdims=True)
        score_grad = four_sum(weighted) - shares * inner
        piece = mixed_grad * shares + score_grad * keyed
        cells_grad = piece if cells_grad is None else cells_grad + piece
        scale = HEAD_DIM**-0.5
        dkeyed_ref[row, :] = jnp.sum(score_grad * cells, axis=0, keepdims=True) * scale
        dbias_ref[row, :] = jnp.sum(score_grad, axis=0, keepdims=True) * scale
        rows = pl.ds(pl.multiple_of(pair * size + which * HEAD_DIM, HEAD_DIM), HEAD_DIM)
        flipped = split_low(flip_ref[rows, :])
        mine = slice(which * HEAD_DIM, (which + 1) * HEAD_DIM)
        dpatch_ref[mine, :] = three_products(flipped, split_low(shares * cells))
        dvar_ref[mine, :] = three_products(flipped, split_low(shares))
    du_ref[...] += cells_grad


def entry_back_kernel(
    grad_ref, qkv_ref, x0_ref, mid_ref, gains_ref, u_ref, keyed_ref, bias_ref, patch_ref, var_ref,
    du_ref, gain_ref, lead_ref, dpatch_ref, dvar_ref, dkeyed_ref, dbias_ref,
    dx_ref, flip_ref,
):
    pair = pl.program_id(0)

    @pl.when(pair == 0)
    def _():
        entry_rows(
            grad_ref, qkv_ref, x0_ref, mid_ref, gains_ref, du_ref, gain_ref, lead_ref, dx_ref,
            flip_ref,
        )

    entry_pair(
        pair, u_ref, keyed_ref, bias_ref, patch_ref, var_ref,
        du_ref, dpatch_ref, dvar_ref, dkeyed_ref, dbias_ref, dx_ref, flip_ref,
    )


def entry_last_kernel(*refs):
    steps = (refs[0:6], refs[6:12])
    share_ref = refs[12]
    (grad_ref, qkv_ref, x0_ref, mid_ref, gains_ref, u_ref, keyed_ref, bias_ref, patch_ref,
     var_ref) = refs[13:23]
    (du_ref, gain_ref, lead_ref, dpatch_ref, dvar_ref, dkeyed_ref, dbias_ref, up_out_ref,
     qkv_share_ref) = refs[23:32]
    dx_ref, flip_ref, low_ref, landing_ref, cross_sem = refs[32:37]
    scatter = Scatter(refs[37:43], refs[44:47])
    held_ref = refs[43]
    turn = pl.program_id(0)
    dp, level, core = mesh_place()
    across = device_of(level, dp, core)
    crossing = scatter.copy(low_ref, landing_ref, cross_sem, 0, 0, across)

    @pl.when(turn == 0)
    def _():
        barrier = pltpu.get_barrier_semaphore()
        deep = [device_of(dp, lax.rem(level + move, 4), core) for move in (1, 2, 3)]
        for target in (scatter.side, scatter.down, *deep):
            pl.semaphore_signal(barrier, inc=1, device_id=target, device_id_type=MESH)
        low_ref[...] = share_ref[...].astype(bf16)

        @pl.when(dp != level)
        def _():
            pl.semaphore_signal(barrier, inc=1, device_id=across, device_id_type=MESH)
            pl.semaphore_wait(barrier, 6)

        @pl.when(dp == level)
        def _():
            pl.semaphore_wait(barrier, 5)

    for index, depth in enumerate(scatter.order):

        @pl.when(turn == index)
        def _(depth=depth):
            lefts, rights, smalls, wides = [], [], [], []
            for dg, o, h2, h2_near, dx1, dx1_near in steps:
                lefts += [dg[0, 0], dg[1, 0]]
                rights += [h2[...], h2_near[...]]
                smalls += [o[0, 0], o[1, 0]]
                wides += [dx1[...], dx1_near[...]]
            scatter.begin(depth, [summed(lefts, rights), summed(smalls, wides)], held_ref)

        @pl.when(turn == index + 3)
        def _(depth=depth):
            scatter.middle(depth)

        @pl.when(turn == index + 6)
        def _(depth=depth):
            scatter.end(depth)

    @pl.when((turn == 2) & (dp != level))
    def _():
        crossing.start()

    @pl.when(turn == 0)
    def _():
        entry_rows(
            grad_ref, qkv_ref, x0_ref, mid_ref, gains_ref, du_ref, gain_ref, lead_ref, dx_ref,
            flip_ref,
        )

    @pl.when((turn >= 1) & (turn <= HEADS // 2))
    def _():
        entry_pair(
            turn - 1, u_ref, keyed_ref, bias_ref, patch_ref, var_ref,
            du_ref, dpatch_ref, dvar_ref, dkeyed_ref, dbias_ref, dx_ref, flip_ref,
        )

    @pl.when(turn == entry_turns - 1)
    def _():
        @pl.when(dp != level)
        def _():
            crossing.wait()
            qkv_share_ref[...] = landing_ref[...].astype(f32)

        @pl.when(dp == level)
        def _():
            qkv_share_ref[...] = share_ref[...]

        scatter.finish(up_out_ref)


def entry_last(kept, share, token_grad, qkv_t, x_first, mid_grad, norm_gains, cells, prepared):
    patch, variable, keyed, bias = prepared
    rows, width = x_first.shape
    padded = cells.shape[1]
    in_specs, operands = [], []
    for dg, o, h2, h2_near, dx1, dx1_near in kept:
        operands += [dg, o, h2, h2_near, dx1, dx1_near]
        in_specs += [chunk_spec(dg.shape[2:]), chunk_spec(o.shape[2:])]
        in_specs += [once(h2.shape)] * 4
    pair = lambda i: jnp.clip(i - 1, 0, HEADS // 2 - 1)
    by_pair = pl.BlockSpec((padded, 2 * HEAD_DIM), lambda i: (0, pair(i)))
    flipped = pl.BlockSpec((2 * HEAD_DIM, padded), lambda i: (pair(i), 0))
    fixed = lambda shape: pl.BlockSpec(shape, lambda i: (0, 0))
    values = [share, token_grad, qkv_t, x_first, mid_grad, norm_gains, cells, keyed, bias]
    in_specs += [once(value.shape) for value in values] + [by_pair, by_pair]
    height, columns = kept[0][0].shape[3] + kept[0][1].shape[3], width // 4
    outs = [
        ((rows, padded), None),
        ((2, width), None),
        ((1, width), None),
        ((width, padded), flipped),
        ((width, padded), flipped),
        (keyed.shape, None),
        (bias.shape, None),
        ((height, columns), None),
        (share.shape, None),
    ]
    return pl.pallas_call(
        entry_last_kernel,
        grid=(entry_turns,),
        out_shape=[jax.ShapeDtypeStruct(shape, f32) for shape, _ in outs],
        in_specs=in_specs,
        out_specs=[fixed(shape) if spec is None else spec for shape, spec in outs],
        scratch_shapes=[
            pltpu.VMEM((rows, width), f32),
            pltpu.VMEM((width, rows), f32),
            pltpu.VMEM(share.shape, bf16),
            pltpu.VMEM(share.shape, bf16),
            pltpu.SemaphoreType.DMA((2, 1)),
        ]
        + scatter_scratch(height, columns),
        compiler_params=pltpu.CompilerParams(
            collective_id=6, has_side_effects=True, vmem_limit_bytes=BIG
        ),
        name="entry_last",
    )(*operands, *values, patch, variable)


def entry_backward(token_grad, qkv_t, x_first, mid_grad, norm_gains, cells, prepared):
    patch, variable, keyed, bias = prepared
    rows, width = x_first.shape
    padded = cells.shape[1]
    fixed = lambda shape: pl.BlockSpec(shape, lambda i: (0, 0))
    by_pair = pl.BlockSpec((padded, 2 * HEAD_DIM), lambda i: (0, i))
    flipped = pl.BlockSpec((2 * HEAD_DIM, padded), lambda i: (i, 0))
    return pl.pallas_call(
        entry_back_kernel,
        grid=(HEADS // 2,),
        out_shape=(
            jax.ShapeDtypeStruct((rows, padded), f32),
            jax.ShapeDtypeStruct((2, width), f32),
            jax.ShapeDtypeStruct((1, width), f32),
            jax.ShapeDtypeStruct((width, padded), f32),
            jax.ShapeDtypeStruct((width, padded), f32),
            jax.ShapeDtypeStruct(keyed.shape, f32),
            jax.ShapeDtypeStruct(bias.shape, f32),
        ),
        in_specs=[
            fixed(token_grad.shape),
            fixed(qkv_t.shape),
            fixed((rows, width)),
            fixed((rows, width)),
            fixed(norm_gains.shape),
            fixed(cells.shape),
            fixed(keyed.shape),
            fixed(bias.shape),
            by_pair,
            by_pair,
        ],
        out_specs=[
            fixed((rows, padded)),
            fixed((2, width)),
            fixed((1, width)),
            flipped,
            flipped,
            fixed(keyed.shape),
            fixed(bias.shape),
        ],
        scratch_shapes=[pltpu.VMEM((rows, width), f32), pltpu.VMEM((width, rows), f32)],
        compiler_params=pltpu.CompilerParams(vmem_limit_bytes=BIG),
        cost_estimate=pl.CostEstimate(
            flops=60 * rows * padded * D, bytes_accessed=40 * rows * D, transcendentals=16 * rows * padded
        ),
        name="entry_backward",
    )(token_grad, qkv_t, x_first, mid_grad, norm_gains, cells, keyed, bias, patch, variable)


def table_grads_kernel(
    pa_ref, pb_ref, va_ref, vb_ref, ka_ref, kb_ref, ba_ref, bb_ref,
    patch_ref, var_ref, query_ref, hot_ref, lead_hot_ref, lead_ref, gain_ref, head_ref, high_ref, o_ref,
):
    padded, width = patch_ref.shape
    marks = head_marks(width)
    query = query_ref[...]
    keyed_grad = exact_product(ka_ref[...] + kb_ref[...], marks, TN)
    bias_grad = exact_product(ba_ref[...] + bb_ref[...], marks, TN)
    o_ref[...] = jnp.zeros_like(o_ref)
    patch_grad = (pa_ref[...] + pb_ref[...]).T + keyed_grad * query
    o_ref[: 4 * V, :] = patch_grad[: 4 * V, :]
    var_grad = (va_ref[...] + vb_ref[...]).T + bias_grad * query
    var_rows = exact_product(quarter_marks(padded), var_grad, TN)
    o_ref[4 * V : 5 * V, :] = exact_product(hot_ref[...], var_rows, TN)
    lead_rows = exact_product(lead_hot_ref[...], lead_ref[...], TN)
    o_ref[5 * V : 5 * V + LEADS, :] = lead_rows[:LEADS, :]
    query_grad = jnp.sum(
        keyed_grad * patch_ref[...] + bias_grad * var_ref[...], axis=0, keepdims=True
    )
    o_ref[5 * V + LEADS : 5 * V + LEADS + 1, :] = query_grad
    o_ref[5 * V + LEADS + 1 : 5 * V + LEADS + 3, :] = gain_ref[...]
    o_ref[padded : padded + 4 * V, :] = head_ref[...]
    o_ref[padded + 4 * V : padded + 4 * V + 4, :] = high_ref[...]


def table_grads(first, second, prepared, query, var_hot, lead_hots, leads, gain_rows, head, high):
    patch, variable, _, _ = prepared
    operands = []
    for one, two in zip(first, second):
        operands += [one, two]
    return pl.pallas_call(
        table_grads_kernel,
        out_shape=jax.ShapeDtypeStruct((2 * patch.shape[0], D), f32),
        compiler_params=pltpu.CompilerParams(vmem_limit_bytes=BIG),
        name="table_grads",
    )(*operands, patch, variable, query, var_hot, lead_hots, leads, gain_rows, head, high)


def adam_step(master, grad, first, second, rate):
    first_new = beta_first * first + (1.0 - beta_first) * grad
    second_new = beta_second * second + (1.0 - beta_second) * grad * grad
    update = first_new / first_fix / (jnp.sqrt(second_new / second_fix) + adam_eps)
    return (master - rate * (update + decay_rate * master), first_new, second_new)


def update_kernel(packed, *refs):
    where_ref, sums_ref, tile_ref, count_ref = refs[:4]
    shares = list(refs[4 : 4 + (3 if packed else 4)])
    rest = refs[4 + len(shares) :]
    states, average_ref, outs = rest[:18], rest[18], rest[19:]
    norm = jnp.sqrt(tile_ref[0:1, 0:1])
    factor = jnp.minimum(1.0, clip_norm / (norm + 1e-06))
    outs[1][...] = norm
    outs[0][...] = tile_ref[1:2, 0:1] / (2.0 * V * jnp.maximum(count_ref[...], 1.0))
    embed_rows = 5 * V + LEADS + 1
    padded = 256

    def apply(index, grad, rate, rows=slice(None)):
        master, first, second = (ref[rows, :] for ref in states[3 * index : 3 * index + 3])
        new = adam_step(master, factor * grad, first, second, rate)
        for ref, value in zip(outs[2 + 3 * index : 5 + 3 * index], new):
            ref[rows, :] = value
        return new[0]

    apply(0, sums_ref[:embed_rows, :], lr_table, slice(0, embed_rows))
    apply(0, sums_ref[padded : padded + 4 * V, :], lr_table, slice(embed_rows, embed_rows + 4 * V))
    apply(1, sums_ref[embed_rows : embed_rows + 2, :], lr_gain, slice(0, 2))
    apply(1, sums_ref[padded + 4 * V : padded + 4 * V + 4, :], lr_gain, slice(2, 6))
    if packed:
        units = shares[2].shape[0]
        grads = (
            shares[0][...], shares[1][units:, :], shares[1][:units, :].T, shares[2][...]
        )
    else:
        grads = [share[...] for share in shares]
    qkv_new = apply(2, grads[0], lr_matrix)
    for index in range(1, 4):
        apply(2 + index, grads[index], lr_matrix)
    outs[20][...] = average_keep * average_ref[...] + (1.0 - average_keep) * qkv_new


def update_all(packed, where, sums, tile, count, shares, states, average):
    operands = [sums, tile, count.reshape(1, 1), *shares]
    fixed = lambda shape: pl.BlockSpec(shape, lambda i, w: (0, 0))
    in_specs = [fixed(value.shape) for value in operands]
    out_shapes = [(1, 1), (1, 1)]
    for master, first, second in states:
        if master.shape == first.shape:
            in_specs.append(fixed(master.shape))
        elif master.shape[0] == first.shape[0]:
            in_specs.append(pl.BlockSpec(first.shape, lambda i, w: (0, w[0])))
        else:
            in_specs.append(pl.BlockSpec(first.shape, lambda i, w: (w[0], 0)))
        in_specs += [fixed(first.shape)] * 2
        operands += [master, first, second]
        out_shapes += [first.shape] * 3
    operands.append(average)
    in_specs.append(fixed(average.shape))
    out_shapes.append(average.shape)
    return pl.pallas_call(
        partial(update_kernel, packed),
        grid_spec=pltpu.PrefetchScalarGridSpec(
            num_scalar_prefetch=1,
            grid=(1,),
            in_specs=in_specs,
            out_specs=[fixed(shape) for shape in out_shapes],
        ),
        out_shape=[jax.ShapeDtypeStruct(shape, f32) for shape in out_shapes],
        compiler_params=pltpu.CompilerParams(vmem_limit_bytes=60 * 2**20),
        name="update_all",
    )(where, *operands)


def by_kind(shard):
    rows = shard.shape[0]
    return shard.reshape(rows, -1, 3, HEAD_DIM).transpose(0, 2, 1, 3).reshape(rows, -1)


def by_head(shard):
    rows = shard.shape[0]
    return shard.reshape(rows, 3, -1, HEAD_DIM).transpose(0, 2, 1, 3).reshape(rows, -1)


lag_one, lag_two, ahead = 2, 4, 3
embed_at, gather_at, project_at, attend_at = 3, 11, 14, 18


def start_kernel(halves, *refs):
    count = len(halves)
    packed_ref, keyed_ref, bias_ref, patch_ref, var_ref, lead_ref, gains_ref = refs[:7]
    shards = refs[7 : 7 + count]
    x0_ref, cells_ref, qkv_ref, o_ref, full_ref, lse_ref, count_ref, rows_out = refs[7 + count : 15 + count]
    outs = refs[15 + count : 15 + 2 * count]
    (held_ref, h1_ref, rows_ref, weight_ref, vt_ref, tile_ref, send_sem, recv_sem,
     level_send, level_recv, own_sem) = refs[15 + 2 * count :]
    step = pl.program_id(0)
    dp, level, core = mesh_place()
    x = lax.rem(dp, 2)
    columns = {"here": dp, "side": dp + 1 - 2 * x, "down": lax.rem(dp + 2, 4), "far": 3 - dp}
    side = device_of(columns["side"], level, core)
    down = device_of(columns["down"], level, core)
    near = device_of(dp, level, 1 - core)
    across = device_of(level, dp, core)
    middle = lax.rem(level, 3) != 0
    late = level // 2
    sources = (level + 1 - 2 * lax.rem(level, 2), 2 - late, 3 * (1 - late))
    onward = (3 - level, lax.rem(3 * level + 1, 4), lax.rem(3 * level + 1, 4))
    slots = [0]

    def remote(source, target_ref, target):
        slot = slots[0]
        slots[0] += 1
        return pltpu.make_async_remote_copy(
            src_ref=source,
            dst_ref=target_ref,
            send_sem=send_sem.at[slot],
            recv_sem=recv_sem.at[slot],
            device_id=target,
            device_id_type=MESH,
        )

    def place(out, source, column, half, pieces):
        rows = out.shape[1] // 4
        size = rows // pieces
        start = pl.multiple_of(columns[column] * rows + half * size, size)
        return out.at[source * 2 + core, pl.ds(start, size), :]

    def pass_on(out, source, column, target, cut):
        where = place(out, source, column, *cut)
        return remote(where, where, target)

    crossing = remote(packed_ref, held_ref, across)
    staying = pltpu.make_async_copy(packed_ref, held_ref, own_sem.at[count])
    mine = [outs[index].at[level * 2 + core] for index in range(count)]
    given = [remote(shards[index], mine[index], near) for index in range(count)]
    kept = [
        pltpu.make_async_copy(shards[index], mine[index], own_sem.at[index]) for index in range(count)
    ]
    chunks, openings = [], []
    for index in range(count):
        out, pieces = outs[index], halves[index]
        for half in range(pieces):
            group = len(openings)
            full = out.shape[1] // 4
            size = full // pieces
            own = shards[index].at[pl.ds(pl.multiple_of(dp * full + half * size, size), size), :]
            cut = (half, pieces)

            def along(source_ref, source, target_level, slot):
                return pltpu.make_async_remote_copy(
                    src_ref=source_ref,
                    dst_ref=place(out, source, "here", *cut),
                    send_sem=level_send.at[group * 5 + slot],
                    recv_sem=level_recv.at[group * 4 + source],
                    device_id=device_of(dp, target_level, core),
                    device_id_type=MESH,
                )

            openings.append(
                (
                    along(own, level, lax.rem(level + 1, 4), 0),
                    along(own, level, lax.rem(level + 3, 4), 1),
                )
            )
            for turn in range(3):
                source = sources[turn]
                chunks.append(
                    {
                        "level": along(place(out, source, "here", *cut), source, onward[turn], 2 + turn),
                        "side": pass_on(out, source, "here", side, cut),
                        "down": pass_on(out, source, "here", down, cut),
                        "hop_down": pass_on(out, source, "side", down, (2 * half, 2 * pieces)),
                        "hop_side": pass_on(out, source, "down", side, (2 * half + 1, 2 * pieces)),
                        "here_near": pass_on(out, source, "here", near, cut),
                        "side_near": pass_on(out, source, "side", near, cut),
                        "down_near": pass_on(out, source, "down", near, cut),
                        "far_near": pass_on(out, source, "far", near, cut),
                    }
                )
    groups = len(openings)
    order = []
    for number in range(groups + 2):
        for turn in range(3):
            if 0 <= number - turn < groups:
                order.append((number - turn, turn))
    chunks = [chunks[3 * group + turn] for group, turn in order]
    total = len(chunks)

    def start_group(number):
        @pl.when(level < 3)
        def _():
            openings[number][0].start()

        @pl.when(level > 0)
        def _():
            openings[number][1].start()

    rows = h1_ref.shape[0]
    cut = rows // 2

    def rows_of(owner, who, first, size):
        return rows_ref.at[pl.ds(pl.multiple_of((owner * 2 + who) * rows + first, cut), size)]

    def relay(place_ref, target):
        return remote(place_ref, place_ref, target)

    first_half, second_half = h1_ref.at[pl.ds(0, cut)], h1_ref.at[pl.ds(cut, cut)]
    beside, below, far = columns["side"], columns["down"], columns["far"]
    side_a = remote(first_half, rows_of(dp, core, 0, cut), side)
    down_b = remote(second_half, rows_of(dp, core, cut, cut), down)
    side_b = remote(second_half, rows_of(dp, core, cut, cut), side)
    down_a = remote(first_half, rows_of(dp, core, 0, cut), down)
    near_own = remote(h1_ref, rows_of(dp, core, 0, rows), near)
    far_a = relay(rows_of(beside, core, 0, cut), down)
    far_b = relay(rows_of(below, core, cut, cut), side)
    near_side = relay(rows_of(beside, core, 0, rows), near)
    near_down = relay(rows_of(below, core, 0, rows), near)
    near_far = relay(rows_of(far, core, 0, rows), near)
    tiles = [
        remote(tile_ref.at[0], tile_ref.at[1], side),
        remote(tile_ref.at[2], tile_ref.at[3], down),
        remote(tile_ref.at[4], tile_ref.at[5], near),
    ]
    deep = [device_of(dp, lax.rem(level + move, 4), core) for move in (1, 2, 3)]
    level_tiles = [remote(tile_ref.at[6], tile_ref.at[7 + move], deep[move]) for move in range(3)]
    weight = pltpu.make_async_copy(outs[0].at[dp * 2 + core], weight_ref, own_sem.at[count + 1])
    save = pltpu.make_async_copy(rows_ref, rows_out, own_sem.at[count + 2])

    @pl.when(step == 0)
    def _():
        barrier = pltpu.get_barrier_semaphore()
        for target in (side, down, near, *deep):
            pl.semaphore_signal(barrier, inc=1, device_id=target, device_id_type=MESH)

        @pl.when(dp != level)
        def _():
            pl.semaphore_signal(barrier, inc=1, device_id=across, device_id_type=MESH)
            pl.semaphore_wait(barrier, 7)
            crossing.start()

        @pl.when(dp == level)
        def _():
            pl.semaphore_wait(barrier, 6)
            staying.start()

        for number in range(ahead):
            start_group(number)
        for copy in (*given, *kept):
            copy.start()

    for number in range(total + lag_two):

        @pl.when(step == number)
        def _(number=number):
            if number < total:
                chunk = chunks[number]
                chunk["level"].wait_recv()

                @pl.when(middle)
                def _():
                    chunk["level"].start()

                chunk["side"].start()
                chunk["down"].start()
                chunk["here_near"].start()
                group, turn = order[number]
                if turn == 0 and group + ahead < groups:
                    start_group(group + ahead)
            if 0 <= number - lag_one < total:
                chunk = chunks[number - lag_one]
                chunk["side"].wait_recv()
                chunk["hop_down"].start()
                chunk["down"].wait_recv()
                chunk["hop_side"].start()
                chunk["side_near"].start()
                chunk["down_near"].start()
            if 0 <= number - lag_two < total:
                chunk = chunks[number - lag_two]
                chunk["hop_down"].wait_recv()
                chunk["hop_side"].wait_recv()
                chunk["far_near"].start()

    @pl.when(step == embed_at)
    def _():
        @pl.when(dp != level)
        def _():
            crossing.wait_recv()

        @pl.when(dp == level)
        def _():
            staying.wait()

        cells_ref[...] = held_ref[...]
        lane = lax.broadcasted_iota(jnp.int32, held_ref.shape, 1)
        ocean = jnp.where((lane >= 4 * V) & (lane < 4 * V + 4), 1.0 - held_ref[...], 0.0)
        tile_ref[0] = jnp.broadcast_to(jnp.sum(ocean), tile_ref.shape[1:])
        tiles[0].start()

    for turn in range(3):

        @pl.when(step == embed_at + 2 + turn)
        def _(turn=turn):
            tiles[turn].wait_recv()
            tile_ref[2 * turn + 2] = tile_ref[2 * turn] + tile_ref[2 * turn + 1]
            for copy in (tiles[1:2], tiles[2:3], level_tiles)[turn]:
                copy.start()

    @pl.when(step == embed_at + 6)
    def _():
        for copy in level_tiles:
            copy.wait_recv()
        count_ref[...] = tile_ref[6] + tile_ref[7] + tile_ref[8] + tile_ref[9]

    @pl.when((step >= embed_at) & (step < embed_at + HEADS // 2))
    def _():
        embed_pair(step - embed_at, held_ref[...], keyed_ref, bias_ref, patch_ref, var_ref, x0_ref)

    @pl.when(step == gather_at)
    def _():
        lead = held_ref[0:1, 4 * V + 4 : 4 * V + 5]
        row = lax.broadcasted_iota(jnp.int32, (1, 8), 1).astype(f32)
        lead_hot = jnp.where(row == lead, 1.0, 0.0).astype(f32)
        x0_ref[...] += exact_product(lead_hot, lead_ref[...])
        unit, _ = normed_parts(x0_ref[...])
        h1_ref[...] = (unit * gains_ref[0:1, :] + gains_ref[1:2, :]).astype(bf16)
        for copy in (side_a, down_b, side_b, down_a, near_own):
            copy.start()
        rows_of(dp, core, 0, rows)[...] = h1_ref[...]
        kept[0].wait()
        weight.start()

    @pl.when(step == gather_at + 1)
    def _():
        side_a.wait_recv()
        far_a.start()
        down_b.wait_recv()
        far_b.start()
        side_b.wait_recv()
        near_side.start()
        down_a.wait_recv()
        near_down.start()

    @pl.when(step == gather_at + 2)
    def _():
        far_a.wait_recv()
        far_b.wait_recv()
        near_far.start()
        for copy in (near_own, near_side, near_down):
            copy.wait_recv()

    block = rows_ref.shape[0] // 4

    @pl.when(step == project_at)
    def _():
        near_far.wait_recv()
        save.start()
        weight.wait()

    @pl.when((step >= project_at) & (step < project_at + 4))
    def _():
        where = pl.ds(pl.multiple_of((step - project_at) * block, block), block)
        qkv_ref[where, :] = lax.dot_general(
            rows_ref[where, :], weight_ref[...], NT, preferred_element_type=f32
        ).astype(bf16)

    width = o_ref.shape[1]
    heads = width // HEAD_DIM

    @pl.when(step == attend_at)
    def _():
        vt_ref[...] = qkv_ref[:, 2 * width :].T

    @pl.when((step >= attend_at) & (step < attend_at + 4))
    def _():
        where = pl.ds(pl.multiple_of((step - attend_at) * block, block), block)
        full, sums = attend_rows(
            heads, qkv_ref[where, :width], qkv_ref.at[:, width : 2 * width], vt_ref
        )
        for head in range(heads):
            lse_ref[head : head + 1, where] = sums[head]
        full_ref[where, :] = full
        o_ref[where, :] = full.astype(bf16)

    @pl.when(step == total + lag_two - 1)
    def _():
        for copy in given:
            copy.wait()
        for copy in kept[1:]:
            copy.wait()
        for number in range(groups):

            @pl.when(level < 3)
            def _(number=number):
                openings[number][0].wait_send()

            @pl.when(level > 0)
            def _(number=number):
                openings[number][1].wait_send()

        for chunk in chunks:
            for name in ("here_near", "side_near", "down_near", "far_near"):
                chunk[name].wait_recv()
            for name, copy in chunk.items():
                if name != "level":
                    copy.wait_send()

            @pl.when(middle)
            def _(chunk=chunk):
                chunk["level"].wait_send()

        for copy in (side_a, down_b, side_b, down_a, near_own, far_a, far_b, near_side, near_down, near_far):
            copy.wait_send()
        for copy in (*tiles, *level_tiles):
            copy.wait_send()
        save.wait()

        @pl.when(dp != level)
        def _():
            crossing.wait_send()


def start_program(packed, prepared, lead_table, norm_gains, shards, halves):
    patch, variable, keyed, bias = prepared
    count = len(shards)
    groups = sum(halves)
    copies = groups * 24 + count + 17
    rows, padded = packed.shape
    total = 8 * rows
    width = shards[0].shape[0] // 3
    heads = width // HEAD_DIM
    anywhere = pl.BlockSpec(memory_space=pl.ANY)
    fixed = lambda shape: pl.BlockSpec(shape, lambda i: (0, 0))
    by_pair = pl.BlockSpec(
        (padded, 2 * HEAD_DIM), lambda i: (0, jnp.clip(i - embed_at, 0, HEADS // 2 - 1))
    )
    shapes = [
        ((rows, D), f32),
        (packed.shape, f32),
        ((total, 3 * width), bf16),
        ((total, width), bf16),
        ((total, width), f32),
        ((heads, total), f32),
        ((8, 128), f32),
    ]
    return pl.pallas_call(
        partial(start_kernel, halves),
        grid=(groups * 3 + lag_two,),
        out_shape=[jax.ShapeDtypeStruct(shape, kind) for shape, kind in shapes]
        + [jax.ShapeDtypeStruct((total, D), bf16)]
        + [jax.ShapeDtypeStruct((8,) + shard.shape, bf16) for shard in shards],
        in_specs=[anywhere]
        + [fixed(keyed.shape), fixed(bias.shape), by_pair, by_pair]
        + [fixed(lead_table.shape), fixed(norm_gains.shape)]
        + [fixed(shard.shape) for shard in shards],
        out_specs=[fixed(shape) for shape, _ in shapes] + [anywhere] * (count + 1),
        scratch_shapes=[
            pltpu.VMEM(packed.shape, f32),
            pltpu.VMEM((rows, D), bf16),
            pltpu.VMEM((total, D), bf16),
            pltpu.VMEM(shards[0].shape, bf16),
            pltpu.VMEM((width, total), bf16),
            pltpu.VMEM((10, 8, 128), f32),
            pltpu.SemaphoreType.DMA((copies,)),
            pltpu.SemaphoreType.DMA((copies,)),
            pltpu.SemaphoreType.DMA((groups * 5,)),
            pltpu.SemaphoreType.DMA((groups * 4,)),
            pltpu.SemaphoreType.DMA((count + 3,)),
        ],
        compiler_params=pltpu.CompilerParams(
            collective_id=7, has_side_effects=True, vmem_limit_bytes=BIG
        ),
        name="start_program",
    )(packed, keyed, bias, patch, variable, lead_table, norm_gains, *shards)


def shards(
    crossed,
    fields,
    targets,
    land_mask,
    lead_index,
    var_ids,
    tables,
    norm_gains,
    tables_first,
    tables_second,
    gains_first,
    gains_second,
    w_qkv,
    qkv_first,
    qkv_second,
    w_out,
    out_first,
    out_second,
    w_up,
    up_first,
    up_second,
    w_down,
    down_first,
    down_second,
    qkv_average,
):
    local_samples, shard_rows, _ = fields.shape
    dp_size, parts = lax.axis_size("dp"), lax.axis_size("mp")
    dp_index = lax.axis_index("dp")
    place, level, core = mesh_place()
    part = place * 2 + core if crossed else lax.axis_index("mp")
    share_rows = D // dp_size

    def own_share(full, dim):
        return lax.dynamic_slice_in_dim(full, dp_index * share_rows, share_rows, dim)

    var_hot = (var_ids[:, None] == jnp.arange(V, dtype=jnp.int32)[None, :]).astype(f32)
    prepared = prepare_tables(tables, var_hot)
    low = lambda master: master.astype(bf16)
    qkv_low = by_kind(low(w_qkv))
    packed = jnp.concatenate(
        (
            fields[0],
            land_mask[0].astype(f32),
            jnp.broadcast_to(lead_index.astype(f32), (shard_rows, 2)),
            jnp.zeros((shard_rows, 64 - 6), f32),
        ),
        axis=1,
    )
    if crossed:
        (
            x_first, cells, packed, own_out, full, logsum, count, rows_one,
            qkv_t, w_outs, w_ups, w_downs
        ) = start_program(
            packed, prepared, tables[5 * V : 5 * V + 8], norm_gains,
            (qkv_low.T, low(w_out), low(w_up), low(w_down)), (1, 1, 2, 2),
        )
        count = count[0, 0]
    else:
        cells = packed
        answers = targets[0]
        count = lax.psum(jnp.sum(1.0 - cells[:, 4 * V : 4 * V + 4]), ("dp", "mp"))
        w_outs, w_ups, w_downs, qkv_t = [
            lax.all_gather(shard, "mp")
            for shard in (low(w_out), low(w_up), low(w_down), qkv_low.T)
        ]
    gathered = (w_outs.reshape(D, D), w_ups, w_downs.reshape(-1, D), qkv_t.reshape(3 * D, D))
    qkv_local = choose(qkv_t, part)
    leads = cells[0, 4 * V + 4 : 4 * V + 6].astype(jnp.int32)
    ocean = 1.0 - cells[:, 4 * V : 4 * V + 4]
    denom = 2.0 * V * jnp.maximum(count, 1.0)
    first_row = part * shard_rows
    patch_row = (first_row + jnp.arange(shard_rows, dtype=jnp.int32)) // PATCH_COLS
    row_hot = (patch_row[:, None] == jnp.arange(PATCH_ROWS, dtype=jnp.int32)[None, :]).astype(f32)
    lat_rows = jnp.dot(
        row_hot, lat_weights(2 * PATCH_ROWS).reshape(PATCH_ROWS, 2), precision=highest
    )
    lat_pixels = jnp.broadcast_to(lat_rows[:, :, None], (shard_rows, 2, 2)).reshape(shard_rows, 4)
    weighted = jnp.tile(ocean * lat_pixels, (1, V))
    head = tables[5 * V + LEADS + 1 :]
    loss_part = f32(0.0)
    records = []
    for rollout in range(2):
        if rollout == 1:
            cells = jnp.pad(guess, ((0, 0), (0, 64)))
        if rollout == 1 or not crossed:
            lead_row = lax.dynamic_slice_in_dim(tables, 5 * V + leads[rollout], 1, 0)
            x_first, normed = embed_forward(cells, prepared, lead_row, norm_gains)
            rows_one = spread_rows(crossed, normed)
            packed = lax.dot_general(
                rows_one, qkv_local, NT, preferred_element_type=f32
            ).astype(bf16)
            own_out, full, logsum = attend(packed)
        attended = exchange(crossed, own_out, True, 2)
        if crossed and rollout == 0:
            later_targets, attended = tie(targets[0], attended)
            answers = cross(crossed, later_targets)
        x_mid, rows_two, hidden, active, x_last, guess = branch_forward(
            attended, x_first, norm_gains, gathered, head
        )
        miss = guess - answers[rollout]
        loss_part = loss_part + jnp.sum(weighted * miss * miss)
        records.append(
            (cells, x_first, rows_one, packed, full, logsum, attended, x_mid, rows_two,
             hidden, active, x_last, 2.0 * weighted * miss / denom)
        )
    carried = jnp.zeros_like(guess)
    head_total = jnp.zeros_like(head)
    gain_high = jnp.zeros((4, D), f32)
    gain_low = jnp.zeros((2, D), f32)
    table_parts, lead_sums = [], []
    qkv_grad = jnp.zeros((D, qkv_local.shape[0]), f32)
    kept = []

    for rollout in (1, 0):
        (cells, x_first, rows_one, packed, full, logsum, attended, x_mid, rows_two,
         hidden, active, x_last, loss_grad) = records[rollout]
        last_low, hidden_grad, mid_grad, mid_low, out_grad, gain_part, head_grad = branch_backward(
            loss_grad + carried, x_last, x_mid, norm_gains, hidden, gathered, head
        )
        head_total = head_total + head_grad
        gain_high = gain_high + gain_part[2:]
        if crossed:
            (
                own_grad, act_both, dg_both, o_both, dx2_near, h2_near, dx1_near
            ) = exchange_swap(
                out_grad, active, hidden_grad, attended, last_low, rows_two, mid_low
            )
            kept.append(
                (act_both, dg_both, o_both, last_low, dx2_near, rows_two, h2_near, mid_low, dx1_near)
            )
        else:
            flat = lambda value: value.transpose(2, 1, 0, 3).reshape(shard_rows, -1)
            kept.append((attended, rows_two, flat(active), mid_low, flat(hidden_grad), last_low))
            own_grad = exchange(crossed, out_grad, False, 3)
        if crossed and rollout == 0:
            token_grad, level_share, down_sum = finish_program(
                [(step[0], step[3], step[4]) for step in kept],
                packed, own_grad, full, logsum, rows_one, qkv_grad,
            )
        else:
            packed_grad = attend_back(own_grad, packed, full, logsum)
            token_grad = exchange(crossed, packed_grad, True, 4 + 4)
            qkv_grad = qkv_grad + lax.dot_general(
                rows_one, packed_grad, TN, preferred_element_type=f32
            )
        entry = (token_grad, gathered[3], x_first, mid_grad, norm_gains, cells, prepared)
        if crossed and rollout == 0:
            cells_grad, gain_one, lead_sum, *table_part, up_out_sum, qkv_share = entry_last(
                [step[1:3] + step[5:] for step in kept], level_share, *entry
            )
        else:
            cells_grad, gain_one, lead_sum, *table_part = entry_backward(*entry)
        carried = cells_grad[:, : 4 * V]
        gain_low = gain_low + gain_one
        table_parts.append(table_part)
        lead_sums.append(lead_sum)

    def pair(index):
        return (kept[0][index], kept[1][index])

    lead_hots = (leads[:, None] == jnp.arange(8, dtype=jnp.int32)[None, :]).astype(f32)
    lead_hots = jnp.pad(lead_hots, ((0, 6), (0, 0)))
    lead_rows = jnp.pad(jnp.concatenate((lead_sums[1], lead_sums[0])), ((0, 6), (0, 0)))
    query = tables[5 * V + LEADS : 5 * V + LEADS + 1]
    last_rows = table_grads(
        *table_parts, prepared, query, var_hot, lead_hots, lead_rows, gain_low, head_total, gain_high
    )
    if not crossed:
        qkv_share = lax.psum_scatter(qkv_grad, "dp", scatter_dimension=0, tiled=True)
    qkv_share = by_head(qkv_share)
    where = dp_index.astype(jnp.int32).reshape(1)
    if crossed:
        shares = (qkv_share, up_out_sum, down_sum)
        last_sum, tile = exchange_sum(last_rows, loss_part, *shares)
        masters = (w_qkv, w_out, w_up, w_down)
    else:
        shares = (
            qkv_share,
            outer_plain(pair(0), pair(3), False),
            outer_plain(pair(1), pair(4), True),
            outer_plain(pair(2), pair(5), False),
        )
        squares = sum(jnp.sum(share * share) for share in shares)
        last_sum, loss_sum, squares = lax.psum((last_rows, loss_part, squares), ("dp", "mp"))
        squares = squares + jnp.sum(last_sum * last_sum)
        row = jnp.arange(8, dtype=jnp.int32)[:, None]
        tile = jnp.where(row == 0, squares, jnp.where(row == 1, loss_sum, 0.0))
        tile = jnp.broadcast_to(tile, (8, 128))
        masters = (own_share(w_qkv, 0), own_share(w_out, 1), own_share(w_up, 0), own_share(w_down, 1))
    states = (
        (tables, tables_first, tables_second),
        (norm_gains, gains_first, gains_second),
        (masters[0], qkv_first, qkv_second),
        (masters[1], out_first, out_second),
        (masters[2], up_first, up_second),
        (masters[3], down_first, down_second),
    )
    results = update_all(crossed, where, last_sum, tile, count, shares, states, qkv_average)
    return (results[0][0, 0], results[1][0, 0], *results[2:])


def solution(mesh):
    return jax.shard_map(
        partial(shards, is_crossed(mesh.shape)),
        mesh=mesh,
        in_specs=(
            P("dp", "mp", None),
            P("dp", None, "mp", None),
            P("dp", "mp", None),
            P("dp", None),
            P(),
            P(),
            P(),
            P(),
            P(),
            P(),
            P(),
            P(None, "mp"),
            P("dp", "mp"),
            P("dp", "mp"),
            P("mp", None),
            P("mp", "dp"),
            P("mp", "dp"),
            P(None, "mp"),
            P("dp", "mp"),
            P("dp", "mp"),
            P("mp", None),
            P("mp", "dp"),
            P("mp", "dp"),
            P("dp", "mp"),
        ),
        out_specs=(
            P(),
            P(),
            P(),
            P(),
            P(),
            P(),
            P(),
            P(),
            P("dp", "mp"),
            P("dp", "mp"),
            P("dp", "mp"),
            P("mp", "dp"),
            P("mp", "dp"),
            P("mp", "dp"),
            P("dp", "mp"),
            P("dp", "mp"),
            P("dp", "mp"),
            P("mp", "dp"),
            P("mp", "dp"),
            P("mp", "dp"),
            P("dp", "mp"),
        ),
        check_vma=False,
    )
```

```python
from functools import partial
import math

import jax
import jax.numpy as jnp
from jax import lax
from jax.experimental import pallas as pl
from jax.experimental.pallas import tpu as pltpu
from jax.sharding import PartitionSpec as P

D = 1024
HEADS = 16
HEAD_DIM = 64
V = 48
PATCH_ROWS = 32
PATCH_COLS = 64
LEADS = 7


highest = lax.Precision.HIGHEST
eps_norm = 1e-05
clip_norm = 0.05
beta_first = 0.9
beta_second = 0.999
adam_eps = 1e-08
decay_rate = 0.1
lr_matrix = 0.04
lr_table = 0.1
lr_gain = 0.3
average_keep = 0.9
first_fix = 1.0 - 0.9**10
second_fix = 1.0 - 0.999**10


def layer_norm(values, gain, bias):
    center = values - jnp.mean(values, axis=-1, keepdims=True)
    spread = jnp.mean(center * center, axis=-1, keepdims=True)
    return center * lax.rsqrt(spread + eps_norm) * gain + bias


def lat_weights(pixel_rows):
    row_index = jnp.arange(pixel_rows, dtype=jnp.float32)
    cosine = jnp.cos(((row_index + 0.5) / pixel_rows - 0.5) * math.pi)
    return cosine / jnp.mean(cosine)


bf16 = jnp.bfloat16
f32 = jnp.float32
MESH = pl.DeviceIdType.MESH
NT = (((1,), (1,)), ((), ()))
TN = (((0,), (0,)), ((), ()))
VMEM = pl.BlockSpec(memory_space=pltpu.VMEM)
BIG = 56 * 2**20


def is_crossed(sizes):
    return sizes["dp"] == 4 and sizes["mp"] == 8


def mesh_place():
    dp = lax.axis_index("dp")
    mp = lax.axis_index("mp")
    return dp, mp // 2, lax.rem(mp, 2)


def device_of(dp, level, core):
    return {"dp": dp, "mp": level * 2 + core}


def cross_pairs():
    groups = lax.axis_size("dp")
    pairs = []
    for dp in range(groups):
        for level in range(groups):
            for core in range(2):
                source = (dp * groups + level) * 2 + core
                target = (level * groups + dp) * 2 + core
                pairs.append((source, target))
    return pairs


def cross(crossed, value):
    if not crossed:
        return value
    return lax.ppermute(value, ("dp", "mp"), cross_pairs())


def gather_kernel(x_ref, o_ref, send_sem, recv_sem):
    rows = x_ref.shape[0]
    half = rows // 2
    dp, level, core = mesh_place()
    side = dp + 1 - 2 * lax.rem(dp, 2)
    down = lax.rem(dp + 2, 4)
    far = 3 - dp
    to_side = device_of(side, level, core)
    to_down = device_of(down, level, core)
    to_core = device_of(dp, level, 1 - core)

    def rows_of(owner, who, first, size):
        return pl.ds(pl.multiple_of((owner * 2 + who) * rows + first, half), size)

    barrier = pltpu.get_barrier_semaphore()
    for target in (to_side, to_down, to_core):
        pl.semaphore_signal(barrier, inc=1, device_id=target, device_id_type=MESH)
    pl.semaphore_wait(barrier, 3)

    def send(slot, source, where, target):
        copy = pltpu.make_async_remote_copy(
            src_ref=source,
            dst_ref=o_ref.at[where],
            send_sem=send_sem.at[slot],
            recv_sem=recv_sem.at[slot],
            device_id=target,
            device_id_type=MESH,
        )
        copy.start()
        return copy

    first = x_ref.at[pl.ds(0, half)]
    second = x_ref.at[pl.ds(half, half)]
    side_a = send(0, first, rows_of(dp, core, 0, half), to_side)
    down_b = send(1, second, rows_of(dp, core, half, half), to_down)
    side_b = send(2, second, rows_of(dp, core, half, half), to_side)
    down_a = send(3, first, rows_of(dp, core, 0, half), to_down)
    near = send(4, x_ref, rows_of(dp, core, 0, rows), to_core)
    o_ref[rows_of(dp, core, 0, rows)] = x_ref[...]
    side_a.wait_recv()
    place = rows_of(side, core, 0, half)
    far_a = send(5, o_ref.at[place], place, to_down)
    down_b.wait_recv()
    place = rows_of(down, core, half, half)
    far_b = send(6, o_ref.at[place], place, to_side)
    side_b.wait_recv()
    place = rows_of(side, core, 0, rows)
    near_side = send(7, o_ref.at[place], place, to_core)
    down_a.wait_recv()
    place = rows_of(down, core, 0, rows)
    near_down = send(8, o_ref.at[place], place, to_core)
    far_a.wait_recv()
    far_b.wait_recv()
    place = rows_of(far, core, 0, rows)
    near_far = send(9, o_ref.at[place], place, to_core)
    for copy in (near, near_side, near_down, near_far):
        copy.wait_recv()
    for copy in (side_a, down_b, side_b, down_a, near, far_a, far_b, near_side, near_down, near_far):
        copy.wait_send()


def spread_rows(crossed, normed):
    if not crossed:
        return lax.all_gather(normed, "mp", axis=0, tiled=True)
    rows, width = normed.shape
    return pl.pallas_call(
        gather_kernel,
        out_shape=jax.ShapeDtypeStruct((8 * rows, width), normed.dtype),
        in_specs=[VMEM],
        out_specs=VMEM,
        scratch_shapes=[pltpu.SemaphoreType.DMA((10,)), pltpu.SemaphoreType.DMA((10,))],
        compiler_params=pltpu.CompilerParams(
            collective_id=1, has_side_effects=True, vmem_limit_bytes=BIG
        ),
        name="gather_rows",
    )(normed)


def exchange_kernel(to_columns, rows, width, x_ref, o_ref, send_sem, recv_sem):
    dp, level, core = mesh_place()
    me = dp * 2 + core
    barrier = pltpu.get_barrier_semaphore()
    others = []
    for step in (7, 6, 5, 4, 3, 2, 1):
        part = lax.rem(me + step, 8)
        others.append((step, part, device_of(part // 2, level, lax.rem(part, 2))))
    for step, part, target in others:
        pl.semaphore_signal(barrier, inc=1, device_id=target, device_id_type=MESH)
    pl.semaphore_wait(barrier, 7)

    def row_block(ref, part):
        return ref.at[pl.ds(pl.multiple_of(part * rows, rows), rows), :]

    def column_block(ref, part):
        return ref.at[:, pl.ds(pl.multiple_of(part * width, width), width)]

    source_block, target_block = (
        (row_block, column_block) if to_columns else (column_block, row_block)
    )
    copies = []
    for step, part, target in others:
        copy = pltpu.make_async_remote_copy(
            src_ref=source_block(x_ref, part),
            dst_ref=target_block(o_ref, me),
            send_sem=send_sem.at[step],
            recv_sem=recv_sem.at[step],
            device_id=target,
            device_id_type=MESH,
        )
        copy.start()
        copies.append(copy)
    target_block(o_ref, me)[...] = source_block(x_ref, me)[...]
    for copy in copies:
        copy.wait()


def exchange(crossed, value, to_columns, number):
    parts = lax.axis_size("mp")
    if to_columns:
        rows, width = value.shape[0] // parts, value.shape[1]
        shape = (rows, width * parts)
    else:
        rows, width = value.shape[0], value.shape[1] // parts
        shape = (rows * parts, width)
    if not crossed:
        split, joined = (0, 1) if to_columns else (1, 0)
        return lax.all_to_all(value, "mp", split_axis=split, concat_axis=joined, tiled=True)
    return pl.pallas_call(
        partial(exchange_kernel, to_columns, rows, width),
        out_shape=jax.ShapeDtypeStruct(shape, value.dtype),
        in_specs=[VMEM],
        out_specs=VMEM,
        scratch_shapes=[pltpu.SemaphoreType.DMA((8,)), pltpu.SemaphoreType.DMA((8,))],
        compiler_params=pltpu.CompilerParams(
            collective_id=number, has_side_effects=True, vmem_limit_bytes=BIG
        ),
        name="exchange_parts",
    )(value)


def pick_head(value, head, heads):
    if heads == 1:
        return value
    lane = lax.broadcasted_iota(jnp.int32, value.shape, 1) // HEAD_DIM
    return jnp.where(lane == head, value, jnp.zeros_like(value))


def attend_rows(heads, queries, k_ref, vt_ref):
    queries = queries * bf16(HEAD_DIM**-0.5)
    keys = k_ref[...]
    outs, sums = [], []
    for head in range(heads):
        scores = lax.dot_general(
            keys, pick_head(queries, head, heads), NT, preferred_element_type=f32
        )
        largest = jnp.max(scores, axis=0, keepdims=True)
        raised = jnp.exp(scores - largest)
        total = jnp.sum(raised, axis=0, keepdims=True)
        probs = (raised * (1.0 / total)).astype(bf16)
        values = vt_ref[head * HEAD_DIM : (head + 1) * HEAD_DIM, :]
        outs.append(jnp.dot(values, probs, preferred_element_type=f32))
        sums.append(largest + jnp.log(total))
    flipped = outs[0] if heads == 1 else jnp.concatenate(outs, axis=0)
    return flipped.T, sums


def attend_kernel(heads, q_ref, k_ref, v_ref, o_ref, full_ref, lse_ref, vt_ref):
    @pl.when(pl.program_id(0) == 0)
    def _():
        vt_ref[...] = v_ref[...].T

    full, sums = attend_rows(heads, q_ref[...], k_ref, vt_ref)
    for head in range(heads):
        lse_ref[head : head + 1, :] = sums[head]
    full_ref[...] = full
    o_ref[...] = full.astype(bf16)


def attend(packed):
    total, width = packed.shape[0], packed.shape[1] // 3
    heads = width // HEAD_DIM
    block = min(512, total)
    row_block = pl.BlockSpec((block, width), lambda i: (i, 0))
    return pl.pallas_call(
        partial(attend_kernel, heads),
        grid=(total // block,),
        out_shape=(
            jax.ShapeDtypeStruct((total, width), bf16),
            jax.ShapeDtypeStruct((total, width), f32),
            jax.ShapeDtypeStruct((heads, total), f32),
        ),
        in_specs=[
            row_block,
            pl.BlockSpec((total, width), lambda i: (0, 0)),
            pl.BlockSpec((total, width), lambda i: (0, 0)),
        ],
        out_specs=[row_block, row_block, pl.BlockSpec((heads, block), lambda i: (0, i))],
        scratch_shapes=[pltpu.VMEM((width, total), bf16)],
        compiler_params=pltpu.CompilerParams(vmem_limit_bytes=BIG),
        cost_estimate=pl.CostEstimate(
            flops=16 * total * total * width,
            bytes_accessed=10 * total * width,
            transcendentals=heads * total * total,
        ),
        name="attend",
    )(packed[:, :width], packed[:, width : 2 * width], packed[:, 2 * width :])


def attend_back_rows(
    heads, chunk, queries, grads, full, sums, k_ref, v_ref, kt_ref, dk_sum, dv_sum
):
    total = k_ref.shape[0]
    scale = HEAD_DIM**-0.5
    products = (grads.astype(f32) * full).T
    query_heads = [pick_head(queries, head, heads) for head in range(heads)]
    grad_heads = [pick_head(grads, head, heads) for head in range(heads)]
    inner = [
        jnp.sum(products[head * HEAD_DIM : (head + 1) * HEAD_DIM], axis=0, keepdims=True) * scale
        for head in range(heads)
    ]
    query_grads = [None] * heads
    for start in range(0, total, chunk):
        rows = slice(start, start + chunk)
        keys = k_ref[rows, :]
        values = v_ref[rows, :]
        value_part = None
        key_part = None
        for head in range(heads):
            scores = lax.dot_general(
                keys, query_heads[head] * bf16(scale), NT, preferred_element_type=f32
            )
            probs = jnp.exp(scores - sums[head])
            prob_grad = lax.dot_general(
                values, grad_heads[head] * bf16(scale), NT, preferred_element_type=f32
            )
            score_grad = (probs * (prob_grad - inner[head])).astype(bf16)
            one = jnp.dot(probs.astype(bf16), grad_heads[head], preferred_element_type=f32)
            two = jnp.dot(score_grad, query_heads[head], preferred_element_type=f32)
            value_part = one if value_part is None else value_part + one
            key_part = two if key_part is None else key_part + two
            three = jnp.dot(
                kt_ref[head * HEAD_DIM : (head + 1) * HEAD_DIM, rows],
                score_grad,
                preferred_element_type=f32,
            )
            query_grads[head] = three if query_grads[head] is None else query_grads[head] + three
        dv_sum[rows, :] += value_part
        dk_sum[rows, :] += key_part
    flipped = query_grads[0] if heads == 1 else jnp.concatenate(query_grads, axis=0)
    return flipped.T.astype(bf16)


def attend_back_kernel(
    heads, q_ref, do_ref, full_ref, lse_ref, k_ref, v_ref, dq_ref, dk_ref, dv_ref, kt_ref, dk_sum, dv_sum
):
    step = pl.program_id(0)

    @pl.when(step == 0)
    def _():
        kt_ref[...] = k_ref[...].T
        dk_sum[...] = jnp.zeros_like(dk_sum)
        dv_sum[...] = jnp.zeros_like(dv_sum)

    sums = [lse_ref[head : head + 1, :] for head in range(heads)]
    dq_ref[...] = attend_back_rows(
        heads, min(1024, k_ref.shape[0]), q_ref[...], do_ref[...], full_ref[...], sums,
        k_ref, v_ref, kt_ref, dk_sum, dv_sum,
    )

    @pl.when(step == pl.num_programs(0) - 1)
    def _():
        dk_ref[...] = dk_sum[...].astype(bf16)
        dv_ref[...] = dv_sum[...].astype(bf16)


def attend_back(grad_out, packed, full, logsum):
    total, width = grad_out.shape
    heads = width // HEAD_DIM
    block = min(256, total)
    row_block = pl.BlockSpec((block, width), lambda i: (i, 0))
    whole = pl.BlockSpec((total, width), lambda i: (0, 0))
    query_grad, key_grad, value_grad = pl.pallas_call(
        partial(attend_back_kernel, heads),
        grid=(total // block,),
        out_shape=(jax.ShapeDtypeStruct((total, width), bf16),) * 3,
        in_specs=[
            row_block,
            row_block,
            row_block,
            pl.BlockSpec((heads, block), lambda i: (0, i)),
            whole,
            whole,
        ],
        out_specs=[row_block, whole, whole],
        scratch_shapes=[
            pltpu.VMEM((width, total), bf16),
            pltpu.VMEM((total, width), f32),
            pltpu.VMEM((total, width), f32),
        ],
        compiler_params=pltpu.CompilerParams(vmem_limit_bytes=BIG),
        cost_estimate=pl.CostEstimate(
            flops=40 * total * total * width,
            bytes_accessed=16 * total * width,
            transcendentals=heads * total * total,
        ),
        name="attend_back",
    )(
        packed[:, :width],
        grad_out,
        full,
        logsum,
        packed[:, width : 2 * width],
        packed[:, 2 * width :],
    )
    return jnp.concatenate((query_grad, key_grad, value_grad), axis=1)


def normed_parts(values):
    center = values - jnp.mean(values, axis=-1, keepdims=True)
    spread = jnp.mean(center * center, axis=-1, keepdims=True)
    inverse = lax.rsqrt(spread + eps_norm)
    return center * inverse, inverse


def norm_grad(unit, inverse, gain, grad):
    scaled = grad * gain
    middle = jnp.mean(scaled, axis=-1, keepdims=True)
    along = jnp.mean(scaled * unit, axis=-1, keepdims=True)
    gain_grad = jnp.sum(grad * unit, axis=0, keepdims=True)
    bias_grad = jnp.sum(grad, axis=0, keepdims=True)
    return inverse * (scaled - middle - unit * along), gain_grad, bias_grad


def gauss_share(values):
    return 0.5 * (1.0 + lax.erf(values * (0.5**0.5)))


def branch_kernel(
    o_ref, x0_ref, gains_ref, out_ref, up_ref, down_ref, head_ref,
    x1_ref, h2_ref, g_ref, act_ref, x2_ref, pred_ref,
):
    step = pl.program_id(0)

    @pl.when(step == 0)
    def _():
        x1_ref[...] = x0_ref[...] + jnp.dot(
            o_ref[...], out_ref[...], preferred_element_type=f32
        )
        unit, _ = normed_parts(x1_ref[...])
        h2_ref[...] = (unit * gains_ref[2:3, :] + gains_ref[3:4, :]).astype(bf16)
        x2_ref[...] = x1_ref[...]

    units = g_ref.shape[1]
    total = None
    for start in range(0, units, units // 2):
        some = slice(start, start + units // 2)
        hidden = jnp.dot(h2_ref[...], up_ref[0, :, some], preferred_element_type=f32)
        g_ref[:, some] = hidden
        active = (hidden * gauss_share(hidden)).astype(bf16)
        act_ref[0, 0, :, some] = active
        part = jnp.dot(active, down_ref[some, :], preferred_element_type=f32)
        total = part if total is None else total + part
    x2_ref[...] += total

    @pl.when(step == pl.num_programs(0) - 1)
    def _():
        unit, _ = normed_parts(x2_ref[...])
        last = unit * gains_ref[4:5, :] + gains_ref[5:6, :]
        pred_ref[...] = lax.dot_general(
            last, head_ref[...], NT, precision=highest, preferred_element_type=f32
        )


def weight_specs(w_out, w_up, w_down):
    _, width, units = w_up.shape
    return (
        pl.BlockSpec(w_out.shape, lambda i: (0, 0)),
        pl.BlockSpec((1, width, units), lambda i: (i, 0, 0)),
        pl.BlockSpec((units, width), lambda i: (i, 0)),
    )


def branch_forward(attended, x_first, norm_gains, gathered, head):
    w_out, w_up, w_down, _ = gathered
    rows, width = x_first.shape
    parts, units = w_up.shape[0], w_up.shape[2]
    fixed = lambda shape: pl.BlockSpec(shape, lambda i: (0, 0))
    by_units = pl.BlockSpec((rows, units), lambda i: (0, i))
    by_core = pl.BlockSpec((1, 1, rows, units), lambda i: (i % 2, i // 2, 0, 0))
    columns = head.shape[0]
    flops = 2 * rows * (width * width + 2 * width * parts * units + 6 * width * columns)
    return pl.pallas_call(
        branch_kernel,
        grid=(parts,),
        out_shape=(
            jax.ShapeDtypeStruct((rows, width), f32),
            jax.ShapeDtypeStruct((rows, width), bf16),
            jax.ShapeDtypeStruct((rows, parts * units), f32),
            jax.ShapeDtypeStruct((2, parts // 2, rows, units), bf16),
            jax.ShapeDtypeStruct((rows, width), f32),
            jax.ShapeDtypeStruct((rows, columns), f32),
        ),
        in_specs=[
            fixed((rows, width)),
            fixed((rows, width)),
            fixed(norm_gains.shape),
            *weight_specs(w_out, w_up, w_down),
            fixed(head.shape),
        ],
        out_specs=[
            fixed((rows, width)),
            fixed((rows, width)),
            by_units,
            by_core,
            fixed((rows, width)),
            fixed((rows, columns)),
        ],
        compiler_params=pltpu.CompilerParams(vmem_limit_bytes=BIG),
        cost_estimate=pl.CostEstimate(
            flops=flops,
            bytes_accessed=4 * width * parts * units + 6 * rows * parts * units,
            transcendentals=rows * parts * units,
        ),
        name="branch_forward",
    )(attended, x_first, norm_gains, w_out, w_up, w_down, head)


def branch_back_kernel(
    dpred_ref, x2_ref, x1_ref, gains_ref, g_ref, out_ref, up_ref, down_ref, head_ref,
    dx2_ref, dg_ref, dx1_ref, low_ref, do_ref, gain_ref, dhead_ref,
    wide_ref, sum_ref,
):
    step = pl.program_id(0)

    @pl.when(step == 0)
    def _():
        grad = dpred_ref[...]
        unit, inverse = normed_parts(x2_ref[...])
        gain = gains_ref[4:5, :]
        last = unit * gain + gains_ref[5:6, :]
        dhead_ref[...] = lax.dot_general(
            grad, last, TN, precision=highest, preferred_element_type=f32
        )
        row_grad = jnp.dot(grad, head_ref[...], precision=highest, preferred_element_type=f32)
        wide, gain_grad, bias_grad = norm_grad(unit, inverse, gain, row_grad)
        gain_ref[...] = jnp.zeros_like(gain_ref)
        gain_ref[4:5, :] = gain_grad
        gain_ref[5:6, :] = bias_grad
        wide_ref[...] = wide
        dx2_ref[...] = wide.astype(bf16)
        sum_ref[...] = jnp.zeros_like(sum_ref)

    units = g_ref.shape[1]
    total = None
    for start in range(0, units, units // 2):
        some = slice(start, start + units // 2)
        active_grad = lax.dot_general(
            dx2_ref[...], down_ref[some, :], NT, preferred_element_type=f32
        )
        hidden = g_ref[:, some]
        slope = gauss_share(hidden) + hidden * (
            jnp.exp(-0.5 * hidden * hidden) * (2.0 * math.pi) ** -0.5
        )
        hidden_grad = (active_grad * slope).astype(bf16)
        dg_ref[0, 0, :, some] = hidden_grad
        part = lax.dot_general(hidden_grad, up_ref[0, :, some], NT, preferred_element_type=f32)
        total = part if total is None else total + part
    sum_ref[...] += total

    @pl.when(step == pl.num_programs(0) - 1)
    def _():
        unit, inverse = normed_parts(x1_ref[...])
        middle, gain_grad, bias_grad = norm_grad(unit, inverse, gains_ref[2:3, :], sum_ref[...])
        gain_ref[2:3, :] = gain_grad
        gain_ref[3:4, :] = bias_grad
        middle = wide_ref[...] + middle
        dx1_ref[...] = middle
        low_ref[...] = middle.astype(bf16)
        total = lax.dot_general(low_ref[...], out_ref[...], NT, preferred_element_type=f32)
        do_ref[...] = total.astype(bf16)


def branch_backward(pred_grad, x_last, x_mid, norm_gains, hidden, gathered, head):
    w_out, w_up, w_down, _ = gathered
    rows, width = x_last.shape
    parts, units = w_up.shape[0], w_up.shape[2]
    fixed = lambda shape: pl.BlockSpec(shape, lambda i: (0, 0))
    by_units = pl.BlockSpec((rows, units), lambda i: (0, i))
    by_core = pl.BlockSpec((1, 1, rows, units), lambda i: (i % 2, i // 2, 0, 0))
    columns = head.shape[0]
    wide = (rows, width)
    flops = 2 * rows * (width * width + 2 * width * parts * units + 12 * width * columns)
    return pl.pallas_call(
        branch_back_kernel,
        grid=(parts,),
        out_shape=(
            jax.ShapeDtypeStruct(wide, bf16),
            jax.ShapeDtypeStruct((2, parts // 2, rows, units), bf16),
            jax.ShapeDtypeStruct(wide, f32),
            jax.ShapeDtypeStruct(wide, bf16),
            jax.ShapeDtypeStruct(wide, bf16),
            jax.ShapeDtypeStruct((6, width), f32),
            jax.ShapeDtypeStruct((columns, width), f32),
        ),
        in_specs=[
            fixed((rows, columns)),
            fixed(wide),
            fixed(wide),
            fixed(norm_gains.shape),
            by_units,
            *weight_specs(w_out, w_up, w_down),
            fixed(head.shape),
        ],
        out_specs=[
            fixed(wide),
            by_core,
            fixed(wide),
            fixed(wide),
            fixed(wide),
            fixed((6, width)),
            fixed((columns, width)),
        ],
        scratch_shapes=[pltpu.VMEM(wide, f32), pltpu.VMEM(wide, f32)],
        compiler_params=pltpu.CompilerParams(vmem_limit_bytes=BIG),
        cost_estimate=pl.CostEstimate(
            flops=flops,
            bytes_accessed=4 * width * parts * units + 6 * rows * parts * units,
            transcendentals=2 * rows * parts * units,
        ),
        name="branch_backward",
    )(pred_grad, x_last, x_mid, norm_gains, hidden, w_out, w_up, w_down, head)


def plane_parts(me):
    return [(move, lax.rem(me + move, 8)) for move in (7, 6, 5, 4, 3, 2, 1)]


def swap_kernel(*refs):
    value_ref, act_ref, dg_ref, o_ref, dx2_ref, h2_ref, dx1_ref = refs[:7]
    rows_ref, act_out, dg_out, o_out, dx2_out, h2_out, dx1_out = refs[7:14]
    send_sem, recv_sem, own_sem = refs[14:]
    dp, level, core = mesh_place()
    me = dp * 2 + core
    rows, width = value_ref.shape[0], value_ref.shape[1] // 8
    near = device_of(dp, level, 1 - core)
    barrier = pltpu.get_barrier_semaphore()
    others = [
        (part, device_of(part // 2, level, lax.rem(part, 2))) for _, part in plane_parts(me)
    ]
    for _, target in others:
        pl.semaphore_signal(barrier, inc=1, device_id=target, device_id_type=MESH)
    pl.semaphore_wait(barrier, 7)
    started = []

    def send(source, target_ref, target):
        slot = len(started)
        copy = pltpu.make_async_remote_copy(
            src_ref=source,
            dst_ref=target_ref,
            send_sem=send_sem.at[slot],
            recv_sem=recv_sem.at[slot],
            device_id=target,
            device_id_type=MESH,
        )
        copy.start()
        started.append(copy)

    def row_block(part):
        return rows_ref.at[pl.ds(pl.multiple_of(part * rows, rows), rows), :]

    def column_block(ref, part):
        return ref.at[:, pl.ds(pl.multiple_of(part * width, width), width)]

    for part, target in others:
        send(column_block(value_ref, part), row_block(me), target)
    locals_ = []

    def keep(source, target_ref):
        copy = pltpu.make_async_copy(source, target_ref, own_sem.at[len(locals_)])
        copy.start()
        locals_.append(copy)

    for source, out in ((act_ref, act_out), (dg_ref, dg_out)):
        send(source.at[1 - core], out.at[1], near)
        keep(source.at[core], out.at[0])
    for index in range(4):
        send(column_block(o_ref, index * 2 + 1 - core), o_out.at[1, index], near)
        keep(column_block(o_ref, index * 2 + core), o_out.at[0, index])
    for source, out in ((dx2_ref, dx2_out), (h2_ref, h2_out), (dx1_ref, dx1_out)):
        send(source, out, near)
    row_block(me)[...] = column_block(value_ref, me)[...]
    for copy in started:
        copy.wait()
    for copy in locals_:
        copy.wait()


def exchange_swap(value, act, dg, attended, dx2, h2, dx1):
    rows, width = value.shape
    anywhere = pl.BlockSpec(memory_space=pl.ANY)
    outs = [
        (8 * rows, width // 8), act.shape, dg.shape, (2, 4, rows, width // 8),
        dx2.shape, h2.shape, dx1.shape,
    ]
    return pl.pallas_call(
        swap_kernel,
        out_shape=[jax.ShapeDtypeStruct(shape, bf16) for shape in outs],
        in_specs=[VMEM] * 7,
        out_specs=[VMEM] + [anywhere] * 6,
        scratch_shapes=[
            pltpu.SemaphoreType.DMA((16,)),
            pltpu.SemaphoreType.DMA((16,)),
            pltpu.SemaphoreType.DMA((6,)),
        ],
        compiler_params=pltpu.CompilerParams(
            collective_id=3, has_side_effects=True, vmem_limit_bytes=BIG
        ),
        name="exchange_swap",
    )(value, act, dg, attended, dx2, h2, dx1)


class Scatter:
    order = (0, 3, 1, 2)

    def __init__(self, refs, sems):
        self.send_ref, self.keep_ref, self.one_ref, self.two_ref, self.own_ref, self.deep_ref = refs
        self.one, self.two, self.deep = sems
        self.dp, self.level, self.core = mesh_place()
        self.x, self.y = lax.rem(self.dp, 2), self.dp // 2
        self.side = device_of(self.dp + 1 - 2 * self.x, self.level, self.core)
        self.down = device_of(lax.rem(self.dp + 2, 4), self.level, self.core)

    def copy(self, source, target_ref, sems, slot, place, target):
        return pltpu.make_async_remote_copy(
            src_ref=source,
            dst_ref=target_ref,
            send_sem=sems.at[0, slot],
            recv_sem=sems.at[1, place],
            device_id=target,
            device_id_type=MESH,
        )

    def first(self, depth):
        target = self.side if depth < 2 else self.down
        return self.copy(
            self.send_ref.at[depth], self.one_ref.at[depth], self.one, depth, depth, target
        )

    def second(self, depth):
        target = self.down if depth < 2 else self.side
        which = 1 - self.y if depth < 2 else 1 - self.x
        return self.copy(
            self.keep_ref.at[depth, which], self.two_ref.at[depth], self.two, depth, depth, target
        )

    def mine(self, depth):
        return self.y if depth < 2 else self.x

    def third(self, depth):
        place = lax.rem(self.level + 7 - depth, 4)
        return self.copy(
            self.keep_ref.at[depth, self.mine(depth)], self.deep_ref.at[place], self.deep, depth,
            place, device_of(self.dp, depth, self.core),
        )

    def begin(self, depth, products, held_ref):
        height = self.keep_ref.shape[2]
        top = 0
        for product in products:
            rows, size = product.shape[0], product.shape[1] // 4
            for split in range(4):
                held_ref[split, top : top + rows, :] = product[
                    :, split * size : (split + 1) * size
                ].astype(bf16)
            top += rows
        for which in range(2):
            if depth < 2:
                moved, stays = which * 2 + 1 - self.x, which * 2 + self.x
            else:
                moved, stays = (1 - self.y) * 2 + which, self.y * 2 + which
            self.send_ref[depth, which] = held_ref[moved, :height, :]
            self.keep_ref[depth, which] = held_ref[stays, :height, :]
        self.first(depth).start()

    def middle(self, depth):
        self.first(depth).wait_recv()
        for which in range(2):
            self.keep_ref[depth, which] = (
                self.keep_ref[depth, which].astype(f32) + self.one_ref[depth, which].astype(f32)
            ).astype(bf16)
        self.second(depth).start()

    def end(self, depth):
        self.second(depth).wait_recv()
        total = self.keep_ref[depth, self.mine(depth)].astype(f32) + self.two_ref[depth].astype(f32)

        @pl.when(self.level == depth)
        def _():
            self.own_ref[...] = total

        @pl.when(self.level != depth)
        def _():
            self.keep_ref[depth, self.mine(depth)] = total.astype(bf16)
            self.third(depth).start()

    def finish(self, result_ref):
        for place in range(3):
            self.copy(
                self.keep_ref.at[0, 0], self.deep_ref.at[place], self.deep, 0, place, self.side
            ).wait_recv()
        result_ref[...] = self.own_ref[...] + (
            self.deep_ref[0].astype(f32) + self.deep_ref[1].astype(f32) + self.deep_ref[2].astype(f32)
        )
        for depth in range(4):
            self.first(depth).wait_send()
            self.second(depth).wait_send()

            @pl.when(self.level != depth)
            def _(depth=depth):
                self.third(depth).wait_send()


def scatter_scratch(height, share):
    return [
        pltpu.VMEM((4, 2, height, share), bf16),
        pltpu.VMEM((4, 2, height, share), bf16),
        pltpu.VMEM((4, 2, height, share), bf16),
        pltpu.VMEM((4, height, share), bf16),
        pltpu.VMEM((height, share), f32),
        pltpu.VMEM((3, height, share), bf16),
        pltpu.VMEM((4, height, share), bf16),
        pltpu.SemaphoreType.DMA((2, 4)),
        pltpu.SemaphoreType.DMA((2, 4)),
        pltpu.SemaphoreType.DMA((2, 4)),
    ]


def summed(lefts, rights):
    total = None
    for left, right in zip(lefts, rights):
        part = lax.dot_general(left, right, TN, preferred_element_type=f32)
        total = part if total is None else total + part
    return total


def chunk_spec(shape):
    def where(i):
        index = jnp.minimum(i, 3)
        first, last = (3 - index) // 3, index // 3
        middle = 1 - first - last
        return 0, middle * (5 - 2 * index) + 2 * last, 0, 0

    return pl.BlockSpec((2, 1) + shape, where)


def once(shape):
    return pl.BlockSpec(shape, lambda i: (0,) * len(shape), pipeline_mode=pl.Buffered(1))


class Returns:
    def __init__(self, grads_ref, token_out, width, sems, own_sem):
        self.grads_ref, self.token_out, self.width = grads_ref, token_out, width
        self.sems, self.own_sem = sems, own_sem
        dp, self.level, core = mesh_place()
        self.me = dp * 2 + core
        self.rows = grads_ref.shape[0] // 8

    def part(self, move):
        return lax.rem(self.me + move, 8)

    def refs(self, part, start, size):
        rows = pl.ds(pl.multiple_of(part * self.rows, self.rows), self.rows)
        first = self.me * 3 * self.width + start
        columns = pl.ds(pl.multiple_of(first, self.width), size)
        return self.grads_ref.at[rows, start : start + size], self.token_out.at[:, columns]

    def copy(self, move, late):
        start, size = (self.width, 2 * self.width) if late else (0, self.width)
        part = self.part(move)
        source, target_ref = self.refs(part, start, size)
        return pltpu.make_async_remote_copy(
            src_ref=source,
            dst_ref=target_ref,
            send_sem=self.sems.at[2 * late, move],
            recv_sem=self.sems.at[2 * late + 1, move],
            device_id=device_of(part // 2, self.level, lax.rem(part, 2)),
            device_id_type=MESH,
        )

    def own(self):
        source, target_ref = self.refs(self.me, 0, 3 * self.width)
        return pltpu.make_async_copy(source, target_ref, self.own_sem)

    def peers(self):
        parts = [self.part(move) for move in range(1, 8)]
        return [device_of(part // 2, self.level, lax.rem(part, 2)) for part in parts]

    def finish(self):
        for move in range(1, 8):
            self.copy(move, 0).wait()
            self.copy(move, 1).wait()
        self.own().wait()


def attend_turns(turn, returns, qkv_ref, do_ref, full_ref, lse_ref, dqkv_ref, kt_ref, dk_sum, dv_sum):
    width = do_ref.shape[1]
    heads = width // HEAD_DIM
    rows = returns.rows

    @pl.when(turn == 0)
    def _():
        kt_ref[...] = qkv_ref[:, width : 2 * width].T
        dk_sum[...] = jnp.zeros_like(dk_sum)
        dv_sum[...] = jnp.zeros_like(dv_sum)

    @pl.when(turn < 8)
    def _():
        part = returns.part(turn + 1)
        where = pl.ds(pl.multiple_of(part * rows, rows), rows)
        sums = [lse_ref[head : head + 1, where] for head in range(heads)]
        dqkv_ref[where, :width] = attend_back_rows(
            heads, 1024, qkv_ref[where, :width], do_ref[where, :], full_ref[where, :], sums,
            qkv_ref.at[:, width : 2 * width], qkv_ref.at[:, 2 * width :], kt_ref, dk_sum, dv_sum,
        )

    @pl.when(turn < 7)
    def _():
        returns.copy(turn + 1, 0).start()

    @pl.when(turn == 8)
    def _():
        dqkv_ref[:, width : 2 * width] = dk_sum[...].astype(bf16)
        dqkv_ref[:, 2 * width :] = dv_sum[...].astype(bf16)
        for move in (7, 6, 5, 4, 3, 2, 1):
            returns.copy(move, 1).start()
        returns.own().start()


def attend_exchange_kernel(
    qkv_ref, do_ref, full_ref, lse_ref, rows_ref, token_out, grad_ref,
    dqkv_ref, kt_ref, dk_sum, dv_sum, sems, own_sem,
):
    turn = pl.program_id(0)
    returns = Returns(dqkv_ref, token_out, do_ref.shape[1], sems, own_sem)

    @pl.when(turn == 0)
    def _():
        barrier = pltpu.get_barrier_semaphore()
        for target in returns.peers():
            pl.semaphore_signal(barrier, inc=1, device_id=target, device_id_type=MESH)
        pl.semaphore_wait(barrier, 7)

    attend_turns(
        turn, returns, qkv_ref, do_ref, full_ref, lse_ref, dqkv_ref, kt_ref, dk_sum, dv_sum
    )

    @pl.when(turn >= pieces_at)
    def _():
        grad_ref[...] = lax.dot_general(
            rows_ref[...], dqkv_ref[...], TN, preferred_element_type=f32
        )

    @pl.when(turn == pieces_at + 3)
    def _():
        returns.finish()


def attend_exchange(packed, own_grad, full, logsum, rows_one):
    rows, width = own_grad.shape[0] // 8, own_grad.shape[1]
    piece = lambda i: jnp.clip(i - pieces_at, 0, 3)
    return pl.pallas_call(
        attend_exchange_kernel,
        grid=(pieces_at + 4,),
        out_shape=[
            jax.ShapeDtypeStruct((rows, 24 * width), bf16),
            jax.ShapeDtypeStruct((D, 3 * width), f32),
        ],
        in_specs=[
            once(packed.shape),
            once(own_grad.shape),
            once(full.shape),
            once(logsum.shape),
            pl.BlockSpec((8 * rows, D // 4), lambda i: (0, piece(i))),
        ],
        out_specs=[
            pl.BlockSpec(memory_space=pl.ANY),
            pl.BlockSpec((D // 4, 3 * width), lambda i: (piece(i), 0)),
        ],
        scratch_shapes=[
            pltpu.VMEM((8 * rows, 3 * width), bf16),
            pltpu.VMEM((width, 8 * rows), bf16),
            pltpu.VMEM((8 * rows, width), f32),
            pltpu.VMEM((8 * rows, width), f32),
            pltpu.SemaphoreType.DMA((4, 8)),
            pltpu.SemaphoreType.DMA,
        ],
        compiler_params=pltpu.CompilerParams(
            collective_id=8, has_side_effects=True, vmem_limit_bytes=BIG
        ),
        name="attend_exchange",
    )(packed, own_grad, full, logsum, rows_one)


pieces_at, turns, entry_turns = 9, 14, 11


def finish_kernel(*refs):
    steps = (refs[0:3], refs[3:6])
    qkv_ref, do_ref, full_ref, lse_ref, rows_ref, prev_ref = refs[6:12]
    token_out, share_ref, down_ref = refs[12:15]
    dqkv_ref, kt_ref, dk_sum, dv_sum, piece_send, piece_recv, piece_own = refs[15:22]
    part_sem, piece_sem, own_sem = refs[22:25]
    scatter = Scatter(refs[25:31], refs[32:35])
    held_ref = refs[31]
    turn = pl.program_id(0)
    dp, level, core = mesh_place()
    width = do_ref.shape[1]
    returns = Returns(dqkv_ref, token_out, width, part_sem, own_sem)

    def remote(source, target_ref, send_sem, recv_sem, target):
        return pltpu.make_async_remote_copy(
            src_ref=source,
            dst_ref=target_ref,
            send_sem=send_sem,
            recv_sem=recv_sem,
            device_id=target,
            device_id_type=MESH,
        )

    def piece_copy(index):
        place = lax.rem(level + 7 - index, 4)
        return remote(
            piece_send.at[index], piece_recv.at[place], piece_sem.at[0, index],
            piece_sem.at[1, place], device_of(dp, index, core),
        )

    @pl.when(turn == 0)
    def _():
        barrier = pltpu.get_barrier_semaphore()
        deep = [device_of(dp, lax.rem(level + move, 4), core) for move in (1, 2, 3)]
        for target in returns.peers() + deep:
            pl.semaphore_signal(barrier, inc=1, device_id=target, device_id_type=MESH)
        pl.semaphore_wait(barrier, 10)

    for index, depth in enumerate(scatter.order):

        @pl.when(turn == index)
        def _(depth=depth):
            lefts, rights = [], []
            for act, dx2, dx2_near in steps:
                lefts += [act[0, 0], act[1, 0]]
                rights += [dx2[...], dx2_near[...]]
            scatter.begin(depth, [summed(lefts, rights)], held_ref)

        @pl.when(turn == index + 3)
        def _(depth=depth):
            scatter.middle(depth)

        @pl.when(turn == index + 5)
        def _(depth=depth):
            scatter.end(depth)

    attend_turns(
        turn, returns, qkv_ref, do_ref, full_ref, lse_ref, dqkv_ref, kt_ref, dk_sum, dv_sum
    )

    for index in range(4):

        @pl.when(turn == pieces_at + index)
        def _(index=index):
            piece = prev_ref[...] + lax.dot_general(
                rows_ref[...], dqkv_ref[...], TN, preferred_element_type=f32
            )

            @pl.when(level == index)
            def _():
                piece_own[...] = piece

            @pl.when(level != index)
            def _():
                piece_send[index] = piece.astype(bf16)
                piece_copy(index).start()

    @pl.when(turn == turns - 1)
    def _():
        scatter.finish(down_ref)
        for place in range(3):
            remote(
                piece_send.at[0], piece_recv.at[place], piece_sem.at[0, 0],
                piece_sem.at[1, place], scatter.side,
            ).wait_recv()
        share_ref[...] = piece_own[...] + (
            piece_recv[0].astype(f32) + piece_recv[1].astype(f32) + piece_recv[2].astype(f32)
        )
        returns.finish()
        for index in range(4):

            @pl.when(level != index)
            def _(index=index):
                piece_copy(index).wait_send()


def finish_program(kept, packed, own_grad, full, logsum, rows_one, earlier):
    rows, width = own_grad.shape[0] // 8, own_grad.shape[1]
    in_specs, operands = [], []
    for act, dx2, dx2_near in kept:
        operands += [act, dx2, dx2_near]
        in_specs += [chunk_spec(act.shape[2:]), once(dx2.shape), once(dx2.shape)]
    piece = lambda i: jnp.clip(i - pieces_at, 0, 3)
    in_specs += [
        once(packed.shape),
        once(own_grad.shape),
        once(full.shape),
        once(logsum.shape),
        pl.BlockSpec((8 * rows, D // 4), lambda i: (0, piece(i))),
        pl.BlockSpec((D // 4, 3 * width), lambda i: (piece(i), 0)),
    ]
    operands += [packed, own_grad, full, logsum, rows_one, earlier]
    fixed = lambda shape: pl.BlockSpec(shape, lambda i: (0, 0))
    units = kept[0][0].shape[3]
    share = D // 4
    return pl.pallas_call(
        finish_kernel,
        grid=(turns,),
        out_shape=[
            jax.ShapeDtypeStruct((rows, 24 * width), bf16),
            jax.ShapeDtypeStruct((share, 3 * width), f32),
            jax.ShapeDtypeStruct((units, share), f32),
        ],
        in_specs=in_specs,
        out_specs=[
            pl.BlockSpec(memory_space=pl.ANY),
            fixed((share, 3 * width)),
            fixed((units, share)),
        ],
        scratch_shapes=[
            pltpu.VMEM((8 * rows, 3 * width), bf16),
            pltpu.VMEM((width, 8 * rows), bf16),
            pltpu.VMEM((8 * rows, width), f32),
            pltpu.VMEM((8 * rows, width), f32),
            pltpu.VMEM((4, share, 3 * width), bf16),
            pltpu.VMEM((3, share, 3 * width), bf16),
            pltpu.VMEM((share, 3 * width), f32),
            pltpu.SemaphoreType.DMA((4, 8)),
            pltpu.SemaphoreType.DMA((2, 4)),
            pltpu.SemaphoreType.DMA,
        ]
        + scatter_scratch(units, share),
        compiler_params=pltpu.CompilerParams(
            collective_id=4, has_side_effects=True, vmem_limit_bytes=BIG
        ),
        name="finish_program",
    )(*operands)


def tie(*values):
    return lax.optimization_barrier(values)


def choose(value, index, axis=0):
    return lax.dynamic_index_in_dim(value, index, axis, keepdims=False)


def outer_plain(lefts, rights, by_rows):
    dp, mp = lax.axis_size("dp"), lax.axis_size("mp")
    grads = sum(
        lax.dot_general(left, right, TN, preferred_element_type=f32)
        for left, right in zip(lefts, rights)
    ).astype(bf16)
    rows, width = grads.shape
    if by_rows:
        grads = grads.reshape(dp, rows // dp, mp, width // mp).transpose(0, 2, 1, 3)
    else:
        grads = grads.reshape(mp, rows // mp, dp, width // dp).transpose(2, 0, 1, 3)
    grads = grads.reshape((dp * mp,) + grads.shape[2:])
    return lax.psum_scatter(grads, ("dp", "mp"), scatter_dimension=0, tiled=False).astype(f32)


def exchange_sum_kernel(
    x_ref, loss_ref, qkv_ref, up_out_ref, down_ref, o_ref, s_ref, work_ref, pair_ref, quad_ref, eight_ref, deep_ref, tile_ref,
    send_sem, recv_sem,
):
    dp, level, core = mesh_place()
    x, y = lax.rem(dp, 2), dp // 2
    side = device_of(dp + 1 - 2 * x, level, core)
    down = device_of(lax.rem(dp + 2, 4), level, core)
    near = device_of(dp, level, 1 - core)
    deep = [device_of(dp, lax.rem(level + step, 4), core) for step in (1, 2, 3)]
    barrier = pltpu.get_barrier_semaphore()
    for target in (side, down, near, *deep):
        pl.semaphore_signal(barrier, inc=1, device_id=target, device_id_type=MESH)
    pl.semaphore_wait(barrier, 6)
    started = []

    def send(source, target_ref, target):
        slot = len(started)
        copy = pltpu.make_async_remote_copy(
            src_ref=source,
            dst_ref=target_ref,
            send_sem=send_sem.at[slot],
            recv_sem=recv_sem.at[slot],
            device_id=target,
            device_id_type=MESH,
        )
        copy.start()
        started.append(copy)
        return copy

    half = x_ref.shape[0] // 2
    quarter, eighth, part, unit = half // 2, half // 4, half // 8, half // 16

    def rows(start, size):
        return pl.ds(pl.multiple_of(start, unit), size)

    copy = send(x_ref.at[rows((1 - core) * half, half)], pair_ref, near)
    copy.wait_recv()
    work_ref[...] = x_ref[rows(core * half, half)] + pair_ref[...]
    one = send(work_ref.at[rows((1 - x) * eighth, eighth)], quad_ref.at[0], side)
    two = send(work_ref.at[rows(quarter + (1 - y) * eighth, eighth)], quad_ref.at[1], down)
    base_a = x * eighth
    base_b = quarter + y * eighth
    wide_a, wide_b = core * half + base_a, core * half + base_b
    one.wait_recv()
    work_ref[rows(base_a, eighth)] += quad_ref[0]
    one = send(work_ref.at[rows(base_a + (1 - y) * part, part)], eight_ref.at[0], down)
    two.wait_recv()
    work_ref[rows(base_b, eighth)] += quad_ref[1]
    two = send(work_ref.at[rows(base_b + (1 - x) * part, part)], eight_ref.at[1], side)
    base_a = base_a + y * part
    base_b = base_b + x * part
    one.wait_recv()
    work_ref[rows(base_a, part)] += eight_ref[0]
    two.wait_recv()
    work_ref[rows(base_b, part)] += eight_ref[1]

    def level_start(which):
        late = which // 2
        return (1 - late) * base_a + late * base_b + lax.rem(which, 2) * unit

    copies = []
    for step in (1, 2, 3):
        source = work_ref.at[rows(level_start(lax.rem(level + step, 4)), unit)]
        copies.append(send(source, deep_ref.at[step - 1], deep[step - 1]))
    for copy in copies:
        copy.wait_recv()
    total = work_ref[rows(level_start(level), unit)] + deep_ref[0] + deep_ref[1] + deep_ref[2]
    mine = rows(core * half + level_start(level), unit)
    base_a = core * half + base_a
    base_b = core * half + base_b
    o_ref[mine] = total
    row = lax.broadcasted_iota(jnp.int32, s_ref.shape, 0)
    squares = jnp.sum(total * total)
    for ref in (qkv_ref, up_out_ref, down_ref):
        squares += jnp.sum(ref[...] * ref[...])
    tile_ref[0] = jnp.where(row == 0, squares, jnp.where(row == 1, loss_ref[...], 0.0))
    copies = []
    for step in (1, 2, 3):
        copies.append(send(o_ref.at[mine], o_ref.at[mine], deep[step - 1]))
        copies.append(send(tile_ref.at[0], tile_ref.at[step], deep[step - 1]))
    for copy in copies:
        copy.wait_recv()
    one = send(o_ref.at[rows(base_a, part)], o_ref.at[rows(base_a, part)], down)
    two = send(o_ref.at[rows(base_b, part)], o_ref.at[rows(base_b, part)], side)
    tile_ref[4] = tile_ref[0] + tile_ref[1] + tile_ref[2] + tile_ref[3]
    three = send(tile_ref.at[4], tile_ref.at[5], side)
    one.wait_recv()
    one = send(o_ref.at[rows(wide_a, eighth)], o_ref.at[rows(wide_a, eighth)], side)
    two.wait_recv()
    two = send(o_ref.at[rows(wide_b, eighth)], o_ref.at[rows(wide_b, eighth)], down)
    three.wait_recv()
    tile_ref[6] = tile_ref[4] + tile_ref[5]
    three = send(tile_ref.at[6], tile_ref.at[7], down)
    one.wait_recv()
    two.wait_recv()
    one = send(o_ref.at[rows(core * half, half)], o_ref.at[rows(core * half, half)], near)
    three.wait_recv()
    tile_ref[8] = tile_ref[6] + tile_ref[7]
    three = send(tile_ref.at[8], tile_ref.at[9], near)
    one.wait_recv()
    three.wait_recv()
    s_ref[...] = tile_ref[8] + tile_ref[9]
    for copy in started:
        copy.wait_send()


def exchange_sum(value, loss, *shares):
    rows, width = value.shape
    tile = jax.ShapeDtypeStruct((8, 128), f32)
    return pl.pallas_call(
        exchange_sum_kernel,
        out_shape=(jax.ShapeDtypeStruct(value.shape, f32), tile),
        in_specs=[VMEM] * 5,
        out_specs=[VMEM, VMEM],
        scratch_shapes=[
            pltpu.VMEM((rows // 2, width), f32),
            pltpu.VMEM((rows // 2, width), f32),
            pltpu.VMEM((2, rows // 8, width), f32),
            pltpu.VMEM((2, rows // 16, width), f32),
            pltpu.VMEM((3, rows // 32, width), f32),
            pltpu.VMEM((10,) + tile.shape, f32),
            pltpu.SemaphoreType.DMA((24,)),
            pltpu.SemaphoreType.DMA((24,)),
        ],
        compiler_params=pltpu.CompilerParams(
            collective_id=5, has_side_effects=True, vmem_limit_bytes=BIG
        ),
        name="exchange_sum",
    )(value, loss.reshape(1, 1), *shares)


def split_low(values):
    high = values.astype(bf16)
    return high, (values - high.astype(f32)).astype(bf16)


def three_products(left, right, dims=(((1,), (0,)), ((), ()))):
    def product(one, two):
        return lax.dot_general(one, two, dims, preferred_element_type=f32)

    return product(left[0], right[0]) + (product(left[1], right[0]) + product(left[0], right[1]))


def exact_product(left, right, dims=(((1,), (0,)), ((), ()))):
    return lax.dot_general(left, right, dims, precision=highest, preferred_element_type=f32)


def head_marks(width):
    head = lax.broadcasted_iota(jnp.int32, (HEADS, width), 0)
    column = lax.broadcasted_iota(jnp.int32, (HEADS, width), 1)
    return jnp.where(column // HEAD_DIM == head, 1.0, 0.0).astype(f32)


def quarter_marks(padded):
    row = lax.broadcasted_iota(jnp.int32, (padded, V), 0)
    column = lax.broadcasted_iota(jnp.int32, (padded, V), 1)
    return jnp.where(row // 4 == column, 0.25, 0.0).astype(f32)


def tables_kernel(tables_ref, hot_ref, patch_ref, var_ref, keyed_ref, bias_ref):
    padded, width = patch_ref.shape
    query = tables_ref[5 * V + LEADS : 5 * V + LEADS + 1, :]
    patch_ref[...] = jnp.zeros_like(patch_ref)
    patch_ref[: 4 * V, :] = tables_ref[: 4 * V, :]
    chosen = exact_product(hot_ref[...], tables_ref[4 * V : 5 * V, :])
    var_ref[...] = exact_product(quarter_marks(padded), chosen)
    marks = head_marks(width)
    scale = HEAD_DIM**-0.5
    keyed_ref[...] = exact_product(marks, patch_ref[...] * query, NT) * scale
    bias = exact_product(marks, var_ref[...] * query, NT) * (4.0 * scale)
    column = lax.broadcasted_iota(jnp.int32, bias.shape, 1)
    bias_ref[...] = jnp.where(column < 4 * V, bias, -1e30)


def prepare_tables(tables, var_hot):
    padded = 256
    return pl.pallas_call(
        tables_kernel,
        out_shape=(
            jax.ShapeDtypeStruct((padded, D), f32),
            jax.ShapeDtypeStruct((padded, D), f32),
            jax.ShapeDtypeStruct((HEADS, padded), f32),
            jax.ShapeDtypeStruct((HEADS, padded), f32),
        ),
        compiler_params=pltpu.CompilerParams(vmem_limit_bytes=BIG),
        name="prepare_tables",
    )(tables, var_hot)


def four_sum(values):
    size = values.shape[1]
    lane = lax.broadcasted_iota(jnp.int32, values.shape, 1)
    values = values + jnp.where(
        lane % 2 == 0, pltpu.roll(values, size - 1, 1), pltpu.roll(values, 1, 1)
    )
    return values + jnp.where(
        lane % 4 < 2, pltpu.roll(values, size - 2, 1), pltpu.roll(values, 2, 1)
    )


def cell_shares(cells, keyed, bias):
    scores = four_sum(cells * keyed) + bias
    raised = jnp.exp(scores - jnp.max(scores, axis=1, keepdims=True))
    total = jnp.sum(raised, axis=1, keepdims=True) * 0.25
    return raised * (1.0 / total)


def embed_pair(pair, cells, keyed_ref, bias_ref, patch_ref, var_ref, x0_ref):
    patch = split_low(patch_ref[...])
    variable = split_low(var_ref[...])
    outs = []
    for which in range(2):
        row = pl.ds(pair * 2 + which, 1)
        shares = cell_shares(cells, keyed_ref[row, :], bias_ref[row, :])
        outs.append(
            three_products(split_low(shares * cells), patch)
            + three_products(split_low(shares), variable)
        )
    lane = lax.broadcasted_iota(jnp.int32, outs[0].shape, 1)
    columns = pl.ds(pl.multiple_of(pair * 2 * HEAD_DIM, 2 * HEAD_DIM), 2 * HEAD_DIM)
    x0_ref[:, columns] = jnp.where(lane < HEAD_DIM, outs[0], outs[1])


def embed_kernel(
    u_ref, keyed_ref, bias_ref, patch_ref, var_ref, lead_ref, gains_ref, x0_ref, h1_ref
):
    pair = pl.program_id(0)
    embed_pair(pair, u_ref[...], keyed_ref, bias_ref, patch_ref, var_ref, x0_ref)

    @pl.when(pair == pl.num_programs(0) - 1)
    def _():
        x0_ref[...] += lead_ref[...]
        unit, _ = normed_parts(x0_ref[...])
        h1_ref[...] = (unit * gains_ref[0:1, :] + gains_ref[1:2, :]).astype(bf16)


def embed_forward(cells, prepared, lead_row, norm_gains):
    patch, variable, keyed, bias = prepared
    rows, padded = cells.shape
    fixed = lambda shape: pl.BlockSpec(shape, lambda i: (0, 0))
    by_pair = pl.BlockSpec((padded, 2 * HEAD_DIM), lambda i: (0, i))
    return pl.pallas_call(
        embed_kernel,
        grid=(HEADS // 2,),
        out_shape=(
            jax.ShapeDtypeStruct((rows, D), f32),
            jax.ShapeDtypeStruct((rows, D), bf16),
        ),
        in_specs=[
            fixed((rows, padded)),
            fixed(keyed.shape),
            fixed(bias.shape),
            by_pair,
            by_pair,
            fixed((1, D)),
            fixed(norm_gains.shape),
        ],
        out_specs=[fixed((rows, D)), fixed((rows, D))],
        compiler_params=pltpu.CompilerParams(vmem_limit_bytes=BIG),
        cost_estimate=pl.CostEstimate(
            flops=24 * rows * padded * D, bytes_accessed=14 * rows * D, transcendentals=16 * rows * padded
        ),
        name="embed_forward",
    )(cells, keyed, bias, patch, variable, lead_row, norm_gains)


def entry_rows(
    grad_ref, qkv_ref, x0_ref, mid_ref, gains_ref, du_ref, gain_ref, lead_ref, dx_ref, flip_ref
):
    row_grad = jnp.dot(grad_ref[...], qkv_ref[...], preferred_element_type=f32)
    unit, inverse = normed_parts(x0_ref[...])
    part, gain_grad, bias_grad = norm_grad(unit, inverse, gains_ref[0:1, :], row_grad)
    total = mid_ref[...] + part
    dx_ref[...] = total
    flip_ref[...] = total.T
    lead_ref[...] = jnp.sum(total, axis=0, keepdims=True)
    gain_ref[0:1, :] = gain_grad
    gain_ref[1:2, :] = bias_grad
    du_ref[...] = jnp.zeros_like(du_ref)


def entry_pair(
    pair, u_ref, keyed_ref, bias_ref, patch_ref, var_ref,
    du_ref, dpatch_ref, dvar_ref, dkeyed_ref, dbias_ref, dx_ref, flip_ref,
):
    cells = u_ref[...]
    size = 2 * HEAD_DIM
    columns = pl.ds(pl.multiple_of(pair * size, size), size)
    grads = dx_ref[:, columns]
    lane = lax.broadcasted_iota(jnp.int32, grads.shape, 1)
    patch = split_low(patch_ref[...])
    variable = split_low(var_ref[...])
    cells_grad = None
    for which in range(2):
        row = pl.ds(pair * 2 + which, 1)
        keyed = keyed_ref[row, :]
        shares = cell_shares(cells, keyed, bias_ref[row, :])
        one = split_low(jnp.where(lane // HEAD_DIM == which, grads, 0.0))
        mixed_grad = three_products(one, patch, NT)
        share_grad = mixed_grad * cells + three_products(one, variable, NT)
        weighted = shares * share_grad
        inner = jnp.sum(weighted, axis=1, keepdims=True)
        score_grad = four_sum(weighted) - shares * inner
        piece = mixed_grad * shares + score_grad * keyed
        cells_grad = piece if cells_grad is None else cells_grad + piece
        scale = HEAD_DIM**-0.5
        dkeyed_ref[row, :] = jnp.sum(score_grad * cells, axis=0, keepdims=True) * scale
        dbias_ref[row, :] = jnp.sum(score_grad, axis=0, keepdims=True) * scale
        rows = pl.ds(pl.multiple_of(pair * size + which * HEAD_DIM, HEAD_DIM), HEAD_DIM)
        flipped = split_low(flip_ref[rows, :])
        mine = slice(which * HEAD_DIM, (which + 1) * HEAD_DIM)
        dpatch_ref[mine, :] = three_products(flipped, split_low(shares * cells))
        dvar_ref[mine, :] = three_products(flipped, split_low(shares))
    du_ref[...] += cells_grad


def entry_back_kernel(
    grad_ref, qkv_ref, x0_ref, mid_ref, gains_ref, u_ref, keyed_ref, bias_ref, patch_ref, var_ref,
    du_ref, gain_ref, lead_ref, dpatch_ref, dvar_ref, dkeyed_ref, dbias_ref,
    dx_ref, flip_ref,
):
    pair = pl.program_id(0)

    @pl.when(pair == 0)
    def _():
        entry_rows(
            grad_ref, qkv_ref, x0_ref, mid_ref, gains_ref, du_ref, gain_ref, lead_ref, dx_ref,
            flip_ref,
        )

    entry_pair(
        pair, u_ref, keyed_ref, bias_ref, patch_ref, var_ref,
        du_ref, dpatch_ref, dvar_ref, dkeyed_ref, dbias_ref, dx_ref, flip_ref,
    )


def entry_last_kernel(*refs):
    steps = (refs[0:6], refs[6:12])
    share_ref = refs[12]
    grad_ref, qkv_ref, x0_ref, mid_ref, gains_ref, u_ref, keyed_ref, bias_ref = refs[13:21]
    patch_ref, var_ref, query_ref, hot_ref, lead_hot_ref, head_a, head_b, high_a, high_b = refs[21:30]
    patch_a, var_a, keyed_a, bias_a, lead_a, gain_a = refs[30:36]
    rows_out, up_out_ref, qkv_share_ref = refs[36:39]
    (dx_ref, flip_ref, low_ref, landing_ref, cross_sem, du_ref, gain_ref, lead_ref, dpatch_ref,
     dvar_ref, dkeyed_ref, dbias_ref) = refs[39:51]
    scatter = Scatter(refs[51:57], refs[58:61])
    held_ref = refs[57]
    turn = pl.program_id(0)
    dp, level, core = mesh_place()
    across = device_of(level, dp, core)
    crossing = scatter.copy(low_ref, landing_ref, cross_sem, 0, 0, across)

    @pl.when(turn == 0)
    def _():
        barrier = pltpu.get_barrier_semaphore()
        deep = [device_of(dp, lax.rem(level + move, 4), core) for move in (1, 2, 3)]
        for target in (scatter.side, scatter.down, *deep):
            pl.semaphore_signal(barrier, inc=1, device_id=target, device_id_type=MESH)
        low_ref[...] = share_ref[...]

        @pl.when(dp != level)
        def _():
            pl.semaphore_signal(barrier, inc=1, device_id=across, device_id_type=MESH)
            pl.semaphore_wait(barrier, 6)
            crossing.start()

        @pl.when(dp == level)
        def _():
            pl.semaphore_wait(barrier, 5)

    for index, depth in enumerate(scatter.order):

        @pl.when(turn == index)
        def _(depth=depth):
            lefts, rights, smalls, wides = [], [], [], []
            for dg, o, h2, h2_near, dx1, dx1_near in steps:
                lefts += [dg[0, 0], dg[1, 0]]
                rights += [h2[...], h2_near[...]]
                smalls += [o[0, 0], o[1, 0]]
                wides += [dx1[...], dx1_near[...]]
            scatter.begin(depth, [summed(lefts, rights), summed(smalls, wides)], held_ref)

        @pl.when(turn == index + 3)
        def _(depth=depth):
            scatter.middle(depth)

        @pl.when(turn == index + 6)
        def _(depth=depth):
            scatter.end(depth)

    @pl.when(turn == 0)
    def _():
        entry_rows(
            grad_ref, qkv_ref, x0_ref, mid_ref, gains_ref, du_ref, gain_ref,
            lead_ref.at[0:1, :], dx_ref, flip_ref,
        )

    @pl.when((turn >= 1) & (turn <= HEADS // 2))
    def _():
        size = 2 * HEAD_DIM
        pair = turn - 1
        some = pl.ds(pl.multiple_of(pair * size, size), size)
        entry_pair(
            pair, u_ref, keyed_ref, bias_ref, patch_ref.at[:, some], var_ref.at[:, some],
            du_ref, dpatch_ref.at[some, :], dvar_ref.at[some, :], dkeyed_ref, dbias_ref,
            dx_ref, flip_ref,
        )

    @pl.when(turn == entry_turns - 2)
    def _():
        gain_ref[...] += gain_a[...]
        lead_ref[1:2, :] = lead_a[...]
        lead_ref[2:8, :] = jnp.zeros((6, lead_ref.shape[1]), f32)
        table_rows(
            patch_a, dpatch_ref, var_a, dvar_ref, keyed_a, dkeyed_ref, bias_a, dbias_ref,
            patch_ref, var_ref, query_ref, hot_ref, lead_hot_ref, lead_ref, gain_ref,
            (head_a[...], head_b[...]), (high_a[2:6, :], high_b[2:6, :]), rows_out,
        )

    @pl.when(turn == entry_turns - 1)
    def _():
        @pl.when(dp != level)
        def _():
            crossing.wait()
            qkv_share_ref[...] = landing_ref[...]

        @pl.when(dp == level)
        def _():
            qkv_share_ref[...] = share_ref[...]

        scatter.finish(up_out_ref)


def entry_last(
    kept, share, token_grad, qkv_t, x_first, mid_grad, norm_gains, cells, prepared,
    query, var_hot, lead_hots, heads, highs, earlier,
):
    patch, variable, keyed, bias = prepared
    rows, width = x_first.shape
    padded = cells.shape[1]
    in_specs, operands = [], []
    for dg, o, h2, h2_near, dx1, dx1_near in kept:
        operands += [dg, o, h2, h2_near, dx1, dx1_near]
        in_specs += [chunk_spec(dg.shape[2:]), chunk_spec(o.shape[2:])]
        in_specs += [once(h2.shape)] * 4
    values = [
        share, token_grad, qkv_t, x_first, mid_grad, norm_gains, cells, keyed, bias,
        patch, variable, query, var_hot, lead_hots, *heads, *highs, *earlier,
    ]
    in_specs += [once(value.shape) for value in values]
    height, columns = kept[0][0].shape[3] + kept[0][1].shape[3], width // 4
    outs = [(2 * padded, width), (height, columns), share.shape]
    return pl.pallas_call(
        entry_last_kernel,
        grid=(entry_turns,),
        out_shape=[jax.ShapeDtypeStruct(shape, f32) for shape in outs],
        in_specs=in_specs,
        out_specs=[pl.BlockSpec(shape, lambda i: (0, 0)) for shape in outs],
        scratch_shapes=[
            pltpu.VMEM((rows, width), f32),
            pltpu.VMEM((width, rows), f32),
            pltpu.VMEM(share.shape, f32),
            pltpu.VMEM(share.shape, f32),
            pltpu.SemaphoreType.DMA((2, 1)),
            pltpu.VMEM((rows, padded), f32),
            pltpu.VMEM((2, width), f32),
            pltpu.VMEM((8, width), f32),
            pltpu.VMEM((width, padded), f32),
            pltpu.VMEM((width, padded), f32),
            pltpu.VMEM(keyed.shape, f32),
            pltpu.VMEM(bias.shape, f32),
        ]
        + scatter_scratch(height, columns),
        compiler_params=pltpu.CompilerParams(
            collective_id=6, has_side_effects=True, vmem_limit_bytes=BIG
        ),
        name="entry_last",
    )(*operands, *values)


def entry_backward(token_grad, qkv_t, x_first, mid_grad, norm_gains, cells, prepared):
    patch, variable, keyed, bias = prepared
    rows, width = x_first.shape
    padded = cells.shape[1]
    fixed = lambda shape: pl.BlockSpec(shape, lambda i: (0, 0))
    by_pair = pl.BlockSpec((padded, 2 * HEAD_DIM), lambda i: (0, i))
    flipped = pl.BlockSpec((2 * HEAD_DIM, padded), lambda i: (i, 0))
    return pl.pallas_call(
        entry_back_kernel,
        grid=(HEADS // 2,),
        out_shape=(
            jax.ShapeDtypeStruct((rows, padded), f32),
            jax.ShapeDtypeStruct((2, width), f32),
            jax.ShapeDtypeStruct((1, width), f32),
            jax.ShapeDtypeStruct((width, padded), f32),
            jax.ShapeDtypeStruct((width, padded), f32),
            jax.ShapeDtypeStruct(keyed.shape, f32),
            jax.ShapeDtypeStruct(bias.shape, f32),
        ),
        in_specs=[
            fixed(token_grad.shape),
            fixed(qkv_t.shape),
            fixed((rows, width)),
            fixed((rows, width)),
            fixed(norm_gains.shape),
            fixed(cells.shape),
            fixed(keyed.shape),
            fixed(bias.shape),
            by_pair,
            by_pair,
        ],
        out_specs=[
            fixed((rows, padded)),
            fixed((2, width)),
            fixed((1, width)),
            flipped,
            flipped,
            fixed(keyed.shape),
            fixed(bias.shape),
        ],
        scratch_shapes=[pltpu.VMEM((rows, width), f32), pltpu.VMEM((width, rows), f32)],
        compiler_params=pltpu.CompilerParams(vmem_limit_bytes=BIG),
        cost_estimate=pl.CostEstimate(
            flops=60 * rows * padded * D, bytes_accessed=40 * rows * D, transcendentals=16 * rows * padded
        ),
        name="entry_backward",
    )(token_grad, qkv_t, x_first, mid_grad, norm_gains, cells, keyed, bias, patch, variable)


def table_rows(
    pa_ref, pb_ref, va_ref, vb_ref, ka_ref, kb_ref, ba_ref, bb_ref,
    patch_ref, var_ref, query_ref, hot_ref, lead_hot_ref, lead_ref, gain_ref, heads, highs, o_ref,
):
    padded, width = patch_ref.shape
    marks = head_marks(width)
    query = query_ref[...]
    keyed_grad = exact_product(ka_ref[...] + kb_ref[...], marks, TN)
    bias_grad = exact_product(ba_ref[...] + bb_ref[...], marks, TN)
    o_ref[...] = jnp.zeros_like(o_ref)
    patch_grad = (pa_ref[...] + pb_ref[...]).T + keyed_grad * query
    o_ref[: 4 * V, :] = patch_grad[: 4 * V, :]
    var_grad = (va_ref[...] + vb_ref[...]).T + bias_grad * query
    var_rows = exact_product(quarter_marks(padded), var_grad, TN)
    o_ref[4 * V : 5 * V, :] = exact_product(hot_ref[...], var_rows, TN)
    lead_rows = exact_product(lead_hot_ref[...], lead_ref[...], TN)
    o_ref[5 * V : 5 * V + LEADS, :] = lead_rows[:LEADS, :]
    query_grad = jnp.sum(
        keyed_grad * patch_ref[...] + bias_grad * var_ref[...], axis=0, keepdims=True
    )
    o_ref[5 * V + LEADS : 5 * V + LEADS + 1, :] = query_grad
    o_ref[5 * V + LEADS + 1 : 5 * V + LEADS + 3, :] = gain_ref[...]
    o_ref[padded : padded + 4 * V, :] = heads[0] + heads[1]
    o_ref[padded + 4 * V : padded + 4 * V + 4, :] = highs[0] + highs[1]


def table_grads_kernel(*refs):
    head_a, head_b, high_a, high_b = refs[15:19]
    heads, highs = (head_a[...], head_b[...]), (high_a[2:6, :], high_b[2:6, :])
    table_rows(*refs[:15], heads, highs, refs[19])


def table_grads(first, second, prepared, query, var_hot, lead_hots, leads, gain_rows, heads, highs):
    patch, variable, _, _ = prepared
    operands = []
    for one, two in zip(first, second):
        operands += [one, two]
    return pl.pallas_call(
        table_grads_kernel,
        out_shape=jax.ShapeDtypeStruct((2 * patch.shape[0], D), f32),
        compiler_params=pltpu.CompilerParams(vmem_limit_bytes=BIG),
        name="table_grads",
    )(*operands, patch, variable, query, var_hot, lead_hots, leads, gain_rows, *heads, *highs)


def adam_step(master, grad, first, second, rate):
    first_new = beta_first * first + (1.0 - beta_first) * grad
    second_new = beta_second * second + (1.0 - beta_second) * grad * grad
    update = first_new / first_fix / (jnp.sqrt(second_new / second_fix) + adam_eps)
    return (master - rate * (update + decay_rate * master), first_new, second_new)


def update_kernel(packed, *refs):
    where_ref, sums_ref, tile_ref, count_ref = refs[:4]
    shares = list(refs[4 : 4 + (3 if packed else 4)])
    rest = refs[4 + len(shares) :]
    states, average_ref, outs = rest[:18], rest[18], rest[19:]
    norm = jnp.sqrt(tile_ref[0:1, 0:1])
    factor = jnp.minimum(1.0, clip_norm / (norm + 1e-06))
    outs[1][...] = norm
    outs[0][...] = tile_ref[1:2, 0:1] / (2.0 * V * jnp.maximum(count_ref[...], 1.0))
    embed_rows = 5 * V + LEADS + 1
    padded = 256

    def apply(index, grad, rate, rows=slice(None)):
        master, first, second = (ref[rows, :] for ref in states[3 * index : 3 * index + 3])
        new = adam_step(master, factor * grad, first, second, rate)
        for ref, value in zip(outs[2 + 3 * index : 5 + 3 * index], new):
            ref[rows, :] = value
        return new[0]

    apply(0, sums_ref[:embed_rows, :], lr_table, slice(0, embed_rows))
    apply(0, sums_ref[padded : padded + 4 * V, :], lr_table, slice(embed_rows, embed_rows + 4 * V))
    apply(1, sums_ref[embed_rows : embed_rows + 2, :], lr_gain, slice(0, 2))
    apply(1, sums_ref[padded + 4 * V : padded + 4 * V + 4, :], lr_gain, slice(2, 6))
    if packed:
        units = shares[2].shape[0]
        grads = (
            shares[0][...], shares[1][units:, :], shares[1][:units, :].T, shares[2][...]
        )
    else:
        grads = [share[...] for share in shares]
    qkv_new = apply(2, grads[0], lr_matrix)
    for index in range(1, 4):
        apply(2 + index, grads[index], lr_matrix)
    outs[20][...] = average_keep * average_ref[...] + (1.0 - average_keep) * qkv_new


def update_all(packed, where, sums, tile, count, shares, states, average):
    operands = [sums, tile, count.reshape(1, 1), *shares]
    fixed = lambda shape: pl.BlockSpec(shape, lambda i, w: (0, 0))
    in_specs = [fixed(value.shape) for value in operands]
    out_shapes = [(1, 1), (1, 1)]
    for master, first, second in states:
        if master.shape == first.shape:
            in_specs.append(fixed(master.shape))
        elif master.shape[0] == first.shape[0]:
            in_specs.append(pl.BlockSpec(first.shape, lambda i, w: (0, w[0])))
        else:
            in_specs.append(pl.BlockSpec(first.shape, lambda i, w: (w[0], 0)))
        in_specs += [fixed(first.shape)] * 2
        operands += [master, first, second]
        out_shapes += [first.shape] * 3
    operands.append(average)
    in_specs.append(fixed(average.shape))
    out_shapes.append(average.shape)
    return pl.pallas_call(
        partial(update_kernel, packed),
        grid_spec=pltpu.PrefetchScalarGridSpec(
            num_scalar_prefetch=1,
            grid=(1,),
            in_specs=in_specs,
            out_specs=[fixed(shape) for shape in out_shapes],
        ),
        out_shape=[jax.ShapeDtypeStruct(shape, f32) for shape in out_shapes],
        compiler_params=pltpu.CompilerParams(vmem_limit_bytes=60 * 2**20),
        name="update_all",
    )(where, *operands)


def by_kind(shard):
    rows = shard.shape[0]
    return shard.reshape(rows, -1, 3, HEAD_DIM).transpose(0, 2, 1, 3).reshape(rows, -1)


def by_head(shard):
    rows = shard.shape[0]
    return shard.reshape(rows, 3, -1, HEAD_DIM).transpose(0, 2, 1, 3).reshape(rows, -1)


lag_one, lag_two, ahead = 2, 4, 3
embed_at, gather_at, project_at, attend_at = 3, 11, 14, 18


def start_kernel(halves, *refs):
    count = len(halves)
    packed_ref, keyed_ref, bias_ref, patch_ref, var_ref, lead_ref, gains_ref = refs[:7]
    shards = refs[7 : 7 + count]
    x0_ref, cells_ref, qkv_ref, o_ref, full_ref, lse_ref, count_ref, rows_out = refs[7 + count : 15 + count]
    outs = refs[15 + count : 15 + 2 * count]
    (held_ref, h1_ref, rows_ref, weight_ref, vt_ref, tile_ref, send_sem, recv_sem,
     level_send, level_recv, own_sem) = refs[15 + 2 * count :]
    step = pl.program_id(0)
    dp, level, core = mesh_place()
    x = lax.rem(dp, 2)
    columns = {"here": dp, "side": dp + 1 - 2 * x, "down": lax.rem(dp + 2, 4), "far": 3 - dp}
    side = device_of(columns["side"], level, core)
    down = device_of(columns["down"], level, core)
    near = device_of(dp, level, 1 - core)
    across = device_of(level, dp, core)
    middle = lax.rem(level, 3) != 0
    late = level // 2
    sources = (level + 1 - 2 * lax.rem(level, 2), 2 - late, 3 * (1 - late))
    onward = (3 - level, lax.rem(3 * level + 1, 4), lax.rem(3 * level + 1, 4))
    slots = [0]

    def remote(source, target_ref, target):
        slot = slots[0]
        slots[0] += 1
        return pltpu.make_async_remote_copy(
            src_ref=source,
            dst_ref=target_ref,
            send_sem=send_sem.at[slot],
            recv_sem=recv_sem.at[slot],
            device_id=target,
            device_id_type=MESH,
        )

    def place(out, source, column, half, pieces):
        rows = out.shape[1] // 4
        size = rows // pieces
        start = pl.multiple_of(columns[column] * rows + half * size, size)
        return out.at[source * 2 + core, pl.ds(start, size), :]

    def pass_on(out, source, column, target, cut):
        where = place(out, source, column, *cut)
        return remote(where, where, target)

    crossing = remote(packed_ref, held_ref, across)
    staying = pltpu.make_async_copy(packed_ref, held_ref, own_sem.at[count])
    mine = [outs[index].at[level * 2 + core] for index in range(count)]
    given = [remote(shards[index], mine[index], near) for index in range(count)]
    kept = [
        pltpu.make_async_copy(shards[index], mine[index], own_sem.at[index]) for index in range(count)
    ]
    chunks, openings = [], []
    for index in range(count):
        out, pieces = outs[index], halves[index]
        for half in range(pieces):
            group = len(openings)
            full = out.shape[1] // 4
            size = full // pieces
            own = shards[index].at[pl.ds(pl.multiple_of(dp * full + half * size, size), size), :]
            cut = (half, pieces)

            def along(source_ref, source, target_level, slot):
                return pltpu.make_async_remote_copy(
                    src_ref=source_ref,
                    dst_ref=place(out, source, "here", *cut),
                    send_sem=level_send.at[group * 5 + slot],
                    recv_sem=level_recv.at[group * 4 + source],
                    device_id=device_of(dp, target_level, core),
                    device_id_type=MESH,
                )

            openings.append(
                (
                    along(own, level, lax.rem(level + 1, 4), 0),
                    along(own, level, lax.rem(level + 3, 4), 1),
                )
            )
            for turn in range(3):
                source = sources[turn]
                chunks.append(
                    {
                        "level": along(place(out, source, "here", *cut), source, onward[turn], 2 + turn),
                        "side": pass_on(out, source, "here", side, cut),
                        "down": pass_on(out, source, "here", down, cut),
                        "hop_down": pass_on(out, source, "side", down, (2 * half, 2 * pieces)),
                        "hop_side": pass_on(out, source, "down", side, (2 * half + 1, 2 * pieces)),
                        "here_near": pass_on(out, source, "here", near, cut),
                        "side_near": pass_on(out, source, "side", near, cut),
                        "down_near": pass_on(out, source, "down", near, cut),
                        "far_near": pass_on(out, source, "far", near, cut),
                    }
                )
    groups = len(openings)
    order = []
    for number in range(groups + 2):
        for turn in range(3):
            if 0 <= number - turn < groups:
                order.append((number - turn, turn))
    chunks = [chunks[3 * group + turn] for group, turn in order]
    total = len(chunks)

    def start_group(number):
        @pl.when(level < 3)
        def _():
            openings[number][0].start()

        @pl.when(level > 0)
        def _():
            openings[number][1].start()

    rows = h1_ref.shape[0]
    cut = rows // 2

    def rows_of(owner, who, first, size):
        return rows_ref.at[pl.ds(pl.multiple_of((owner * 2 + who) * rows + first, cut), size)]

    def relay(place_ref, target):
        return remote(place_ref, place_ref, target)

    first_half, second_half = h1_ref.at[pl.ds(0, cut)], h1_ref.at[pl.ds(cut, cut)]
    beside, below, far = columns["side"], columns["down"], columns["far"]
    side_a = remote(first_half, rows_of(dp, core, 0, cut), side)
    down_b = remote(second_half, rows_of(dp, core, cut, cut), down)
    side_b = remote(second_half, rows_of(dp, core, cut, cut), side)
    down_a = remote(first_half, rows_of(dp, core, 0, cut), down)
    near_own = remote(h1_ref, rows_of(dp, core, 0, rows), near)
    far_a = relay(rows_of(beside, core, 0, cut), down)
    far_b = relay(rows_of(below, core, cut, cut), side)
    near_side = relay(rows_of(beside, core, 0, rows), near)
    near_down = relay(rows_of(below, core, 0, rows), near)
    near_far = relay(rows_of(far, core, 0, rows), near)
    tiles = [
        remote(tile_ref.at[0], tile_ref.at[1], side),
        remote(tile_ref.at[2], tile_ref.at[3], down),
        remote(tile_ref.at[4], tile_ref.at[5], near),
    ]
    deep = [device_of(dp, lax.rem(level + move, 4), core) for move in (1, 2, 3)]
    level_tiles = [remote(tile_ref.at[6], tile_ref.at[7 + move], deep[move]) for move in range(3)]
    weight = pltpu.make_async_copy(outs[0].at[dp * 2 + core], weight_ref, own_sem.at[count + 1])
    save = pltpu.make_async_copy(rows_ref, rows_out, own_sem.at[count + 2])

    @pl.when(step == 0)
    def _():
        barrier = pltpu.get_barrier_semaphore()
        for target in (side, down, near, *deep):
            pl.semaphore_signal(barrier, inc=1, device_id=target, device_id_type=MESH)

        @pl.when(dp != level)
        def _():
            pl.semaphore_signal(barrier, inc=1, device_id=across, device_id_type=MESH)
            pl.semaphore_wait(barrier, 7)
            crossing.start()

        @pl.when(dp == level)
        def _():
            pl.semaphore_wait(barrier, 6)
            staying.start()

        for number in range(ahead):
            start_group(number)
        for copy in (*given, *kept):
            copy.start()

    for number in range(total + lag_two):

        @pl.when(step == number)
        def _(number=number):
            if number < total:
                chunk = chunks[number]
                chunk["level"].wait_recv()

                @pl.when(middle)
                def _():
                    chunk["level"].start()

                chunk["side"].start()
                chunk["down"].start()
                chunk["here_near"].start()
                group, turn = order[number]
                if turn == 0 and group + ahead < groups:
                    start_group(group + ahead)
            if 0 <= number - lag_one < total:
                chunk = chunks[number - lag_one]
                chunk["side"].wait_recv()
                chunk["hop_down"].start()
                chunk["down"].wait_recv()
                chunk["hop_side"].start()
                chunk["side_near"].start()
                chunk["down_near"].start()
            if 0 <= number - lag_two < total:
                chunk = chunks[number - lag_two]
                chunk["hop_down"].wait_recv()
                chunk["hop_side"].wait_recv()
                chunk["far_near"].start()

    @pl.when(step == embed_at)
    def _():
        @pl.when(dp != level)
        def _():
            crossing.wait_recv()

        @pl.when(dp == level)
        def _():
            staying.wait()

        cells_ref[...] = held_ref[...]
        lane = lax.broadcasted_iota(jnp.int32, held_ref.shape, 1)
        ocean = jnp.where((lane >= 4 * V) & (lane < 4 * V + 4), 1.0 - held_ref[...], 0.0)
        tile_ref[0] = jnp.broadcast_to(jnp.sum(ocean), tile_ref.shape[1:])
        tiles[0].start()

    for turn in range(3):

        @pl.when(step == embed_at + 2 + turn)
        def _(turn=turn):
            tiles[turn].wait_recv()
            tile_ref[2 * turn + 2] = tile_ref[2 * turn] + tile_ref[2 * turn + 1]
            for copy in (tiles[1:2], tiles[2:3], level_tiles)[turn]:
                copy.start()

    @pl.when(step == embed_at + 6)
    def _():
        for copy in level_tiles:
            copy.wait_recv()
        count_ref[...] = tile_ref[6] + tile_ref[7] + tile_ref[8] + tile_ref[9]

    @pl.when((step >= embed_at) & (step < embed_at + HEADS // 2))
    def _():
        embed_pair(step - embed_at, held_ref[...], keyed_ref, bias_ref, patch_ref, var_ref, x0_ref)

    @pl.when(step == gather_at)
    def _():
        lead = held_ref[0:1, 4 * V + 4 : 4 * V + 5]
        row = lax.broadcasted_iota(jnp.int32, (1, 8), 1).astype(f32)
        lead_hot = jnp.where(row == lead, 1.0, 0.0).astype(f32)
        x0_ref[...] += exact_product(lead_hot, lead_ref[...])
        unit, _ = normed_parts(x0_ref[...])
        h1_ref[...] = (unit * gains_ref[0:1, :] + gains_ref[1:2, :]).astype(bf16)
        for copy in (side_a, down_b, side_b, down_a, near_own):
            copy.start()
        rows_of(dp, core, 0, rows)[...] = h1_ref[...]
        kept[0].wait()
        weight.start()

    @pl.when(step == gather_at + 1)
    def _():
        side_a.wait_recv()
        far_a.start()
        down_b.wait_recv()
        far_b.start()
        side_b.wait_recv()
        near_side.start()
        down_a.wait_recv()
        near_down.start()

    @pl.when(step == gather_at + 2)
    def _():
        far_a.wait_recv()
        far_b.wait_recv()
        near_far.start()
        for copy in (near_own, near_side, near_down):
            copy.wait_recv()

    block = rows_ref.shape[0] // 4

    @pl.when(step == project_at)
    def _():
        near_far.wait_recv()
        save.start()
        weight.wait()

    @pl.when((step >= project_at) & (step < project_at + 4))
    def _():
        where = pl.ds(pl.multiple_of((step - project_at) * block, block), block)
        qkv_ref[where, :] = lax.dot_general(
            rows_ref[where, :], weight_ref[...], NT, preferred_element_type=f32
        ).astype(bf16)

    width = o_ref.shape[1]
    heads = width // HEAD_DIM

    @pl.when(step == attend_at)
    def _():
        vt_ref[...] = qkv_ref[:, 2 * width :].T

    @pl.when((step >= attend_at) & (step < attend_at + 4))
    def _():
        where = pl.ds(pl.multiple_of((step - attend_at) * block, block), block)
        full, sums = attend_rows(
            heads, qkv_ref[where, :width], qkv_ref.at[:, width : 2 * width], vt_ref
        )
        for head in range(heads):
            lse_ref[head : head + 1, where] = sums[head]
        full_ref[where, :] = full
        o_ref[where, :] = full.astype(bf16)

    @pl.when(step == total + lag_two - 1)
    def _():
        for copy in given:
            copy.wait()
        for copy in kept[1:]:
            copy.wait()
        for number in range(groups):

            @pl.when(level < 3)
            def _(number=number):
                openings[number][0].wait_send()

            @pl.when(level > 0)
            def _(number=number):
                openings[number][1].wait_send()

        for chunk in chunks:
            for name in ("here_near", "side_near", "down_near", "far_near"):
                chunk[name].wait_recv()
            for name, copy in chunk.items():
                if name != "level":
                    copy.wait_send()

            @pl.when(middle)
            def _(chunk=chunk):
                chunk["level"].wait_send()

        for copy in (side_a, down_b, side_b, down_a, near_own, far_a, far_b, near_side, near_down, near_far):
            copy.wait_send()
        for copy in (*tiles, *level_tiles):
            copy.wait_send()
        save.wait()

        @pl.when(dp != level)
        def _():
            crossing.wait_send()


def start_program(packed, prepared, lead_table, norm_gains, shards, halves):
    patch, variable, keyed, bias = prepared
    count = len(shards)
    groups = sum(halves)
    copies = groups * 24 + count + 17
    rows, padded = packed.shape
    total = 8 * rows
    width = shards[0].shape[0] // 3
    heads = width // HEAD_DIM
    anywhere = pl.BlockSpec(memory_space=pl.ANY)
    fixed = lambda shape: pl.BlockSpec(shape, lambda i: (0, 0))
    by_pair = pl.BlockSpec(
        (padded, 2 * HEAD_DIM), lambda i: (0, jnp.clip(i - embed_at, 0, HEADS // 2 - 1))
    )
    shapes = [
        ((rows, D), f32),
        (packed.shape, f32),
        ((total, 3 * width), bf16),
        ((total, width), bf16),
        ((total, width), f32),
        ((heads, total), f32),
        ((8, 128), f32),
    ]
    return pl.pallas_call(
        partial(start_kernel, halves),
        grid=(groups * 3 + lag_two,),
        out_shape=[jax.ShapeDtypeStruct(shape, kind) for shape, kind in shapes]
        + [jax.ShapeDtypeStruct((total, D), bf16)]
        + [jax.ShapeDtypeStruct((8,) + shard.shape, bf16) for shard in shards],
        in_specs=[anywhere]
        + [fixed(keyed.shape), fixed(bias.shape), by_pair, by_pair]
        + [fixed(lead_table.shape), fixed(norm_gains.shape)]
        + [fixed(shard.shape) for shard in shards],
        out_specs=[fixed(shape) for shape, _ in shapes] + [anywhere] * (count + 1),
        scratch_shapes=[
            pltpu.VMEM(packed.shape, f32),
            pltpu.VMEM((rows, D), bf16),
            pltpu.VMEM((total, D), bf16),
            pltpu.VMEM(shards[0].shape, bf16),
            pltpu.VMEM((width, total), bf16),
            pltpu.VMEM((10, 8, 128), f32),
            pltpu.SemaphoreType.DMA((copies,)),
            pltpu.SemaphoreType.DMA((copies,)),
            pltpu.SemaphoreType.DMA((groups * 5,)),
            pltpu.SemaphoreType.DMA((groups * 4,)),
            pltpu.SemaphoreType.DMA((count + 3,)),
        ],
        compiler_params=pltpu.CompilerParams(
            collective_id=7, has_side_effects=True, vmem_limit_bytes=BIG
        ),
        name="start_program",
    )(packed, keyed, bias, patch, variable, lead_table, norm_gains, *shards)


def shards(
    crossed,
    fields,
    targets,
    land_mask,
    lead_index,
    var_ids,
    tables,
    norm_gains,
    tables_first,
    tables_second,
    gains_first,
    gains_second,
    w_qkv,
    qkv_first,
    qkv_second,
    w_out,
    out_first,
    out_second,
    w_up,
    up_first,
    up_second,
    w_down,
    down_first,
    down_second,
    qkv_average,
):
    local_samples, shard_rows, _ = fields.shape
    dp_size, parts = lax.axis_size("dp"), lax.axis_size("mp")
    dp_index = lax.axis_index("dp")
    place, level, core = mesh_place()
    part = place * 2 + core if crossed else lax.axis_index("mp")
    share_rows = D // dp_size

    def own_share(full, dim):
        return lax.dynamic_slice_in_dim(full, dp_index * share_rows, share_rows, dim)

    var_hot = (var_ids[:, None] == jnp.arange(V, dtype=jnp.int32)[None, :]).astype(f32)
    prepared = prepare_tables(tables, var_hot)
    low = lambda master: master.astype(bf16)
    qkv_low = by_kind(low(w_qkv))
    packed = jnp.concatenate(
        (
            fields[0],
            land_mask[0].astype(f32),
            jnp.broadcast_to(lead_index.astype(f32), (shard_rows, 2)),
            jnp.zeros((shard_rows, 64 - 6), f32),
        ),
        axis=1,
    )
    if crossed:
        (
            x_first, cells, packed, own_out, full, logsum, count, rows_one,
            qkv_t, w_outs, w_ups, w_downs
        ) = start_program(
            packed, prepared, tables[5 * V : 5 * V + 8], norm_gains,
            (qkv_low.T, low(w_out), low(w_up), low(w_down)), (1, 1, 2, 2),
        )
        count = count[0, 0]
    else:
        cells = packed
        answers = targets[0]
        count = lax.psum(jnp.sum(1.0 - cells[:, 4 * V : 4 * V + 4]), ("dp", "mp"))
        w_outs, w_ups, w_downs, qkv_t = [
            lax.all_gather(shard, "mp")
            for shard in (low(w_out), low(w_up), low(w_down), qkv_low.T)
        ]
    gathered = (w_outs.reshape(D, D), w_ups, w_downs.reshape(-1, D), qkv_t.reshape(3 * D, D))
    qkv_local = choose(qkv_t, part)
    leads = cells[0, 4 * V + 4 : 4 * V + 6].astype(jnp.int32)
    ocean = 1.0 - cells[:, 4 * V : 4 * V + 4]
    denom = 2.0 * V * jnp.maximum(count, 1.0)
    first_row = part * shard_rows
    patch_row = (first_row + jnp.arange(shard_rows, dtype=jnp.int32)) // PATCH_COLS
    row_hot = (patch_row[:, None] == jnp.arange(PATCH_ROWS, dtype=jnp.int32)[None, :]).astype(f32)
    lat_rows = jnp.dot(
        row_hot, lat_weights(2 * PATCH_ROWS).reshape(PATCH_ROWS, 2), precision=highest
    )
    lat_pixels = jnp.broadcast_to(lat_rows[:, :, None], (shard_rows, 2, 2)).reshape(shard_rows, 4)
    weighted = jnp.tile(ocean * lat_pixels, (1, V))
    head = tables[5 * V + LEADS + 1 :]
    loss_part = f32(0.0)
    records = []
    for rollout in range(2):
        if rollout == 1:
            cells = jnp.pad(guess, ((0, 0), (0, 64)))
        if rollout == 1 or not crossed:
            lead_row = lax.dynamic_slice_in_dim(tables, 5 * V + leads[rollout], 1, 0)
            x_first, normed = embed_forward(cells, prepared, lead_row, norm_gains)
            rows_one = spread_rows(crossed, normed)
            packed = lax.dot_general(
                rows_one, qkv_local, NT, preferred_element_type=f32
            ).astype(bf16)
            own_out, full, logsum = attend(packed)
        attended = exchange(crossed, own_out, True, 2)
        if crossed and rollout == 0:
            later_targets, attended = tie(targets[0], attended)
            answers = cross(crossed, later_targets)
        x_mid, rows_two, hidden, active, x_last, guess = branch_forward(
            attended, x_first, norm_gains, gathered, head
        )
        miss = guess - answers[rollout]
        loss_part = loss_part + jnp.sum(weighted * miss * miss)
        records.append(
            (cells, x_first, rows_one, packed, full, logsum, attended, x_mid, rows_two,
             hidden, active, x_last, 2.0 * weighted * miss / denom)
        )
    carried = jnp.zeros_like(guess)
    heads, highs = [], []
    lead_hots = (leads[:, None] == jnp.arange(8, dtype=jnp.int32)[None, :]).astype(f32)
    lead_hots = jnp.pad(lead_hots, ((0, 6), (0, 0)))
    query = tables[5 * V + LEADS : 5 * V + LEADS + 1]
    gain_low = jnp.zeros((2, D), f32)
    table_parts, lead_sums = [], []
    qkv_grad = jnp.zeros((D, qkv_local.shape[0]), f32)
    kept = []

    for rollout in (1, 0):
        (cells, x_first, rows_one, packed, full, logsum, attended, x_mid, rows_two,
         hidden, active, x_last, loss_grad) = records[rollout]
        last_low, hidden_grad, mid_grad, mid_low, out_grad, gain_part, head_grad = branch_backward(
            loss_grad + carried, x_last, x_mid, norm_gains, hidden, gathered, head
        )
        heads.append(head_grad)
        highs.append(gain_part)
        if crossed:
            (
                own_grad, act_both, dg_both, o_both, dx2_near, h2_near, dx1_near
            ) = exchange_swap(
                out_grad, active, hidden_grad, attended, last_low, rows_two, mid_low
            )
            kept.append(
                (act_both, dg_both, o_both, last_low, dx2_near, rows_two, h2_near, mid_low, dx1_near)
            )
        else:
            flat = lambda value: value.transpose(2, 1, 0, 3).reshape(shard_rows, -1)
            kept.append((attended, rows_two, flat(active), mid_low, flat(hidden_grad), last_low))
            own_grad = exchange(crossed, out_grad, False, 3)
        if crossed and rollout == 0:
            token_grad, level_share, down_sum = finish_program(
                [(step[0], step[3], step[4]) for step in kept],
                packed, own_grad, full, logsum, rows_one, qkv_grad,
            )
        elif crossed:
            token_grad, qkv_grad = attend_exchange(packed, own_grad, full, logsum, rows_one)
        else:
            packed_grad = attend_back(own_grad, packed, full, logsum)
            token_grad = exchange(crossed, packed_grad, True, 4 + 4)
            qkv_grad = qkv_grad + lax.dot_general(
                rows_one, packed_grad, TN, preferred_element_type=f32
            )
        entry = (token_grad, gathered[3], x_first, mid_grad, norm_gains, cells, prepared)
        if crossed and rollout == 0:
            last_rows, up_out_sum, qkv_share = entry_last(
                [step[1:3] + step[5:] for step in kept], level_share, *entry,
                query, var_hot, lead_hots, heads, highs,
                (*table_parts[0], lead_sums[0], gain_low),
            )
            break
        cells_grad, gain_one, lead_sum, *table_part = entry_backward(*entry)
        carried = cells_grad[:, : 4 * V]
        gain_low = gain_low + gain_one
        table_parts.append(table_part)
        lead_sums.append(lead_sum)

    def pair(index):
        return (kept[0][index], kept[1][index])

    if not crossed:
        lead_rows = jnp.pad(jnp.concatenate((lead_sums[1], lead_sums[0])), ((0, 6), (0, 0)))
        last_rows = table_grads(
            *table_parts, prepared, query, var_hot, lead_hots, lead_rows, gain_low, heads, highs
        )
    if not crossed:
        qkv_share = lax.psum_scatter(qkv_grad, "dp", scatter_dimension=0, tiled=True)
    qkv_share = by_head(qkv_share)
    where = dp_index.astype(jnp.int32).reshape(1)
    if crossed:
        shares = (qkv_share, up_out_sum, down_sum)
        last_sum, tile = exchange_sum(last_rows, loss_part, *shares)
        masters = (w_qkv, w_out, w_up, w_down)
    else:
        shares = (
            qkv_share,
            outer_plain(pair(0), pair(3), False),
            outer_plain(pair(1), pair(4), True),
            outer_plain(pair(2), pair(5), False),
        )
        squares = sum(jnp.sum(share * share) for share in shares)
        last_sum, loss_sum, squares = lax.psum((last_rows, loss_part, squares), ("dp", "mp"))
        squares = squares + jnp.sum(last_sum * last_sum)
        row = jnp.arange(8, dtype=jnp.int32)[:, None]
        tile = jnp.where(row == 0, squares, jnp.where(row == 1, loss_sum, 0.0))
        tile = jnp.broadcast_to(tile, (8, 128))
        masters = (own_share(w_qkv, 0), own_share(w_out, 1), own_share(w_up, 0), own_share(w_down, 1))
    states = (
        (tables, tables_first, tables_second),
        (norm_gains, gains_first, gains_second),
        (masters[0], qkv_first, qkv_second),
        (masters[1], out_first, out_second),
        (masters[2], up_first, up_second),
        (masters[3], down_first, down_second),
    )
    results = update_all(crossed, where, last_sum, tile, count, shares, states, qkv_average)
    return (results[0][0, 0], results[1][0, 0], *results[2:])


def solution(mesh):
    return jax.shard_map(
        partial(shards, is_crossed(mesh.shape)),
        mesh=mesh,
        in_specs=(
            P("dp", "mp", None),
            P("dp", None, "mp", None),
            P("dp", "mp", None),
            P("dp", None),
            P(),
            P(),
            P(),
            P(),
            P(),
            P(),
            P(),
            P(None, "mp"),
            P("dp", "mp"),
            P("dp", "mp"),
            P("mp", None),
            P("mp", "dp"),
            P("mp", "dp"),
            P(None, "mp"),
            P("dp", "mp"),
            P("dp", "mp"),
            P("mp", None),
            P("mp", "dp"),
            P("mp", "dp"),
            P("dp", "mp"),
        ),
        out_specs=(
            P(),
            P(),
            P(),
            P(),
            P(),
            P(),
            P(),
            P(),
            P("dp", "mp"),
            P("dp", "mp"),
            P("dp", "mp"),
            P("mp", "dp"),
            P("mp", "dp"),
            P("mp", "dp"),
            P("dp", "mp"),
            P("dp", "mp"),
            P("dp", "mp"),
            P("mp", "dp"),
            P("mp", "dp"),
            P("mp", "dp"),
            P("dp", "mp"),
        ),
        check_vma=False,
    )
```

```python
from functools import partial
import math

import jax
import jax.numpy as jnp
from jax import lax
from jax.experimental import pallas as pl
from jax.experimental.pallas import tpu as pltpu
from jax.sharding import PartitionSpec as P

D = 1024
HEADS = 16
HEAD_DIM = 64
V = 48
PATCH_ROWS = 32
PATCH_COLS = 64
LEADS = 7


highest = lax.Precision.HIGHEST
eps_norm = 1e-05
clip_norm = 0.05
beta_first = 0.9
beta_second = 0.999
adam_eps = 1e-08
decay_rate = 0.1
lr_matrix = 0.04
lr_table = 0.1
lr_gain = 0.3
average_keep = 0.9
first_fix = 1.0 - 0.9**10
second_fix = 1.0 - 0.999**10


def layer_norm(values, gain, bias):
    center = values - jnp.mean(values, axis=-1, keepdims=True)
    spread = jnp.mean(center * center, axis=-1, keepdims=True)
    return center * lax.rsqrt(spread + eps_norm) * gain + bias


def lat_weights(pixel_rows):
    row_index = jnp.arange(pixel_rows, dtype=jnp.float32)
    cosine = jnp.cos(((row_index + 0.5) / pixel_rows - 0.5) * math.pi)
    return cosine / jnp.mean(cosine)


bf16 = jnp.bfloat16
f32 = jnp.float32
MESH = pl.DeviceIdType.MESH
NT = (((1,), (1,)), ((), ()))
TN = (((0,), (0,)), ((), ()))
VMEM = pl.BlockSpec(memory_space=pltpu.VMEM)
BIG = 56 * 2**20


def is_crossed(sizes):
    return sizes["dp"] == 4 and sizes["mp"] == 8


def mesh_place():
    dp = lax.axis_index("dp")
    mp = lax.axis_index("mp")
    return dp, mp // 2, lax.rem(mp, 2)


def device_of(dp, level, core):
    return {"dp": dp, "mp": level * 2 + core}


def cross_pairs():
    groups = lax.axis_size("dp")
    pairs = []
    for dp in range(groups):
        for level in range(groups):
            for core in range(2):
                source = (dp * groups + level) * 2 + core
                target = (level * groups + dp) * 2 + core
                pairs.append((source, target))
    return pairs


def cross(crossed, value):
    if not crossed:
        return value
    return lax.ppermute(value, ("dp", "mp"), cross_pairs())


def exchange(value, to_columns):
    split, joined = (0, 1) if to_columns else (1, 0)
    return lax.all_to_all(value, "mp", split_axis=split, concat_axis=joined, tiled=True)


def pick_head(value, head, heads):
    if heads == 1:
        return value
    lane = lax.broadcasted_iota(jnp.int32, value.shape, 1) // HEAD_DIM
    return jnp.where(lane == head, value, jnp.zeros_like(value))


def attend_rows(heads, queries, k_ref, vt_ref):
    queries = queries * bf16(HEAD_DIM**-0.5)
    keys = k_ref[...]
    outs, sums = [], []
    for head in range(heads):
        scores = lax.dot_general(
            keys, pick_head(queries, head, heads), NT, preferred_element_type=f32
        )
        largest = jnp.max(scores, axis=0, keepdims=True)
        raised = jnp.exp(scores - largest)
        total = jnp.sum(raised, axis=0, keepdims=True)
        probs = (raised * (1.0 / total)).astype(bf16)
        values = vt_ref[head * HEAD_DIM : (head + 1) * HEAD_DIM, :]
        outs.append(jnp.dot(values, probs, preferred_element_type=f32))
        sums.append(largest + jnp.log(total))
    flipped = outs[0] if heads == 1 else jnp.concatenate(outs, axis=0)
    return flipped.T, sums


def attend_kernel(heads, q_ref, k_ref, v_ref, o_ref, full_ref, lse_ref, vt_ref):
    @pl.when(pl.program_id(0) == 0)
    def _():
        vt_ref[...] = v_ref[...].T

    full, sums = attend_rows(heads, q_ref[...], k_ref, vt_ref)
    for head in range(heads):
        lse_ref[head : head + 1, :] = sums[head]
    full_ref[...] = full
    o_ref[...] = full.astype(bf16)


def attend(packed):
    total, width = packed.shape[0], packed.shape[1] // 3
    heads = width // HEAD_DIM
    block = min(512, total)
    row_block = pl.BlockSpec((block, width), lambda i: (i, 0))
    return pl.pallas_call(
        partial(attend_kernel, heads),
        grid=(total // block,),
        out_shape=(
            jax.ShapeDtypeStruct((total, width), bf16),
            jax.ShapeDtypeStruct((total, width), f32),
            jax.ShapeDtypeStruct((heads, total), f32),
        ),
        in_specs=[
            row_block,
            pl.BlockSpec((total, width), lambda i: (0, 0)),
            pl.BlockSpec((total, width), lambda i: (0, 0)),
        ],
        out_specs=[row_block, row_block, pl.BlockSpec((heads, block), lambda i: (0, i))],
        scratch_shapes=[pltpu.VMEM((width, total), bf16)],
        compiler_params=pltpu.CompilerParams(vmem_limit_bytes=BIG),
        cost_estimate=pl.CostEstimate(
            flops=16 * total * total * width,
            bytes_accessed=10 * total * width,
            transcendentals=heads * total * total,
        ),
        name="attend",
    )(packed[:, :width], packed[:, width : 2 * width], packed[:, 2 * width :])


def attend_back_rows(
    heads, chunk, queries, grads, full, sums, k_ref, v_ref, kt_ref, dk_sum, dv_sum
):
    total = k_ref.shape[0]
    scale = HEAD_DIM**-0.5
    products = (grads.astype(f32) * full).T
    query_heads = [pick_head(queries, head, heads) for head in range(heads)]
    grad_heads = [pick_head(grads, head, heads) for head in range(heads)]
    inner = [
        jnp.sum(products[head * HEAD_DIM : (head + 1) * HEAD_DIM], axis=0, keepdims=True) * scale
        for head in range(heads)
    ]
    query_grads = [None] * heads
    for start in range(0, total, chunk):
        rows = slice(start, start + chunk)
        keys = k_ref[rows, :]
        values = v_ref[rows, :]
        value_part = None
        key_part = None
        for head in range(heads):
            scores = lax.dot_general(
                keys, query_heads[head] * bf16(scale), NT, preferred_element_type=f32
            )
            probs = jnp.exp(scores - sums[head])
            prob_grad = lax.dot_general(
                values, grad_heads[head] * bf16(scale), NT, preferred_element_type=f32
            )
            score_grad = (probs * (prob_grad - inner[head])).astype(bf16)
            one = jnp.dot(probs.astype(bf16), grad_heads[head], preferred_element_type=f32)
            two = jnp.dot(score_grad, query_heads[head], preferred_element_type=f32)
            value_part = one if value_part is None else value_part + one
            key_part = two if key_part is None else key_part + two
            three = jnp.dot(
                kt_ref[head * HEAD_DIM : (head + 1) * HEAD_DIM, rows],
                score_grad,
                preferred_element_type=f32,
            )
            query_grads[head] = three if query_grads[head] is None else query_grads[head] + three
        dv_sum[rows, :] += value_part
        dk_sum[rows, :] += key_part
    flipped = query_grads[0] if heads == 1 else jnp.concatenate(query_grads, axis=0)
    return flipped.T.astype(bf16)


def attend_back_kernel(
    heads, q_ref, do_ref, full_ref, lse_ref, k_ref, v_ref, dq_ref, dk_ref, dv_ref, kt_ref, dk_sum, dv_sum
):
    step = pl.program_id(0)

    @pl.when(step == 0)
    def _():
        kt_ref[...] = k_ref[...].T
        dk_sum[...] = jnp.zeros_like(dk_sum)
        dv_sum[...] = jnp.zeros_like(dv_sum)

    sums = [lse_ref[head : head + 1, :] for head in range(heads)]
    dq_ref[...] = attend_back_rows(
        heads, min(1024, k_ref.shape[0]), q_ref[...], do_ref[...], full_ref[...], sums,
        k_ref, v_ref, kt_ref, dk_sum, dv_sum,
    )

    @pl.when(step == pl.num_programs(0) - 1)
    def _():
        dk_ref[...] = dk_sum[...].astype(bf16)
        dv_ref[...] = dv_sum[...].astype(bf16)


def attend_back(grad_out, packed, full, logsum):
    total, width = grad_out.shape
    heads = width // HEAD_DIM
    block = min(256, total)
    row_block = pl.BlockSpec((block, width), lambda i: (i, 0))
    whole = pl.BlockSpec((total, width), lambda i: (0, 0))
    query_grad, key_grad, value_grad = pl.pallas_call(
        partial(attend_back_kernel, heads),
        grid=(total // block,),
        out_shape=(jax.ShapeDtypeStruct((total, width), bf16),) * 3,
        in_specs=[
            row_block,
            row_block,
            row_block,
            pl.BlockSpec((heads, block), lambda i: (0, i)),
            whole,
            whole,
        ],
        out_specs=[row_block, whole, whole],
        scratch_shapes=[
            pltpu.VMEM((width, total), bf16),
            pltpu.VMEM((total, width), f32),
            pltpu.VMEM((total, width), f32),
        ],
        compiler_params=pltpu.CompilerParams(vmem_limit_bytes=BIG),
        cost_estimate=pl.CostEstimate(
            flops=40 * total * total * width,
            bytes_accessed=16 * total * width,
            transcendentals=heads * total * total,
        ),
        name="attend_back",
    )(
        packed[:, :width],
        grad_out,
        full,
        logsum,
        packed[:, width : 2 * width],
        packed[:, 2 * width :],
    )
    return jnp.concatenate((query_grad, key_grad, value_grad), axis=1)


def normed_parts(values):
    center = values - jnp.mean(values, axis=-1, keepdims=True)
    spread = jnp.mean(center * center, axis=-1, keepdims=True)
    inverse = lax.rsqrt(spread + eps_norm)
    return center * inverse, inverse


def norm_grad(unit, inverse, gain, grad):
    scaled = grad * gain
    middle = jnp.mean(scaled, axis=-1, keepdims=True)
    along = jnp.mean(scaled * unit, axis=-1, keepdims=True)
    gain_grad = jnp.sum(grad * unit, axis=0, keepdims=True)
    bias_grad = jnp.sum(grad, axis=0, keepdims=True)
    return inverse * (scaled - middle - unit * along), gain_grad, bias_grad


def gauss_share(values):
    return 0.5 * (1.0 + lax.erf(values * (0.5**0.5)))


def branch_kernel(
    o_ref, x0_ref, gains_ref, out_ref, up_ref, down_ref, head_ref,
    x1_ref, h2_ref, g_ref, act_ref, x2_ref, pred_ref,
):
    step = pl.program_id(0)

    @pl.when(step == 0)
    def _():
        x1_ref[...] = x0_ref[...] + jnp.dot(
            o_ref[...], out_ref[...], preferred_element_type=f32
        )
        unit, _ = normed_parts(x1_ref[...])
        h2_ref[...] = (unit * gains_ref[2:3, :] + gains_ref[3:4, :]).astype(bf16)
        x2_ref[...] = x1_ref[...]

    units = g_ref.shape[1]
    total = None
    for start in range(0, units, units // 2):
        some = slice(start, start + units // 2)
        hidden = jnp.dot(h2_ref[...], up_ref[0, :, some], preferred_element_type=f32)
        g_ref[:, some] = hidden
        active = (hidden * gauss_share(hidden)).astype(bf16)
        act_ref[0, 0, :, some] = active
        part = jnp.dot(active, down_ref[some, :], preferred_element_type=f32)
        total = part if total is None else total + part
    x2_ref[...] += total

    @pl.when(step == pl.num_programs(0) - 1)
    def _():
        unit, _ = normed_parts(x2_ref[...])
        last = unit * gains_ref[4:5, :] + gains_ref[5:6, :]
        pred_ref[...] = lax.dot_general(
            last, head_ref[...], NT, precision=highest, preferred_element_type=f32
        )


def weight_specs(w_out, w_up, w_down):
    _, width, units = w_up.shape
    return (
        pl.BlockSpec(w_out.shape, lambda i: (0, 0)),
        pl.BlockSpec((1, width, units), lambda i: (i, 0, 0)),
        pl.BlockSpec((units, width), lambda i: (i, 0)),
    )


def branch_forward(attended, x_first, norm_gains, gathered, head):
    w_out, w_up, w_down, _ = gathered
    rows, width = x_first.shape
    parts, units = w_up.shape[0], w_up.shape[2]
    fixed = lambda shape: pl.BlockSpec(shape, lambda i: (0, 0))
    by_units = pl.BlockSpec((rows, units), lambda i: (0, i))
    by_core = pl.BlockSpec((1, 1, rows, units), lambda i: (i % 2, i // 2, 0, 0))
    columns = head.shape[0]
    flops = 2 * rows * (width * width + 2 * width * parts * units + 6 * width * columns)
    return pl.pallas_call(
        branch_kernel,
        grid=(parts,),
        out_shape=(
            jax.ShapeDtypeStruct((rows, width), f32),
            jax.ShapeDtypeStruct((rows, width), bf16),
            jax.ShapeDtypeStruct((rows, parts * units), f32),
            jax.ShapeDtypeStruct((2, parts // 2, rows, units), bf16),
            jax.ShapeDtypeStruct((rows, width), f32),
            jax.ShapeDtypeStruct((rows, columns), f32),
        ),
        in_specs=[
            fixed((rows, width)),
            fixed((rows, width)),
            fixed(norm_gains.shape),
            *weight_specs(w_out, w_up, w_down),
            fixed(head.shape),
        ],
        out_specs=[
            fixed((rows, width)),
            fixed((rows, width)),
            by_units,
            by_core,
            fixed((rows, width)),
            fixed((rows, columns)),
        ],
        compiler_params=pltpu.CompilerParams(vmem_limit_bytes=BIG),
        cost_estimate=pl.CostEstimate(
            flops=flops,
            bytes_accessed=4 * width * parts * units + 6 * rows * parts * units,
            transcendentals=rows * parts * units,
        ),
        name="branch_forward",
    )(attended, x_first, norm_gains, w_out, w_up, w_down, head)


def branch_back_kernel(
    dpred_ref, x2_ref, x1_ref, gains_ref, g_ref, out_ref, up_ref, down_ref, head_ref,
    dx2_ref, dg_ref, dx1_ref, low_ref, do_ref, gain_ref, dhead_ref,
    wide_ref, sum_ref,
):
    step = pl.program_id(0)

    @pl.when(step == 0)
    def _():
        grad = dpred_ref[...]
        unit, inverse = normed_parts(x2_ref[...])
        gain = gains_ref[4:5, :]
        last = unit * gain + gains_ref[5:6, :]
        dhead_ref[...] = lax.dot_general(
            grad, last, TN, precision=highest, preferred_element_type=f32
        )
        row_grad = jnp.dot(grad, head_ref[...], precision=highest, preferred_element_type=f32)
        wide, gain_grad, bias_grad = norm_grad(unit, inverse, gain, row_grad)
        gain_ref[...] = jnp.zeros_like(gain_ref)
        gain_ref[4:5, :] = gain_grad
        gain_ref[5:6, :] = bias_grad
        wide_ref[...] = wide
        dx2_ref[...] = wide.astype(bf16)
        sum_ref[...] = jnp.zeros_like(sum_ref)

    units = g_ref.shape[1]
    total = None
    for start in range(0, units, units // 2):
        some = slice(start, start + units // 2)
        active_grad = lax.dot_general(
            dx2_ref[...], down_ref[some, :], NT, preferred_element_type=f32
        )
        hidden = g_ref[:, some]
        slope = gauss_share(hidden) + hidden * (
            jnp.exp(-0.5 * hidden * hidden) * (2.0 * math.pi) ** -0.5
        )
        hidden_grad = (active_grad * slope).astype(bf16)
        dg_ref[0, 0, :, some] = hidden_grad
        part = lax.dot_general(hidden_grad, up_ref[0, :, some], NT, preferred_element_type=f32)
        total = part if total is None else total + part
    sum_ref[...] += total

    @pl.when(step == pl.num_programs(0) - 1)
    def _():
        unit, inverse = normed_parts(x1_ref[...])
        middle, gain_grad, bias_grad = norm_grad(unit, inverse, gains_ref[2:3, :], sum_ref[...])
        gain_ref[2:3, :] = gain_grad
        gain_ref[3:4, :] = bias_grad
        middle = wide_ref[...] + middle
        dx1_ref[...] = middle
        low_ref[...] = middle.astype(bf16)
        total = lax.dot_general(low_ref[...], out_ref[...], NT, preferred_element_type=f32)
        do_ref[...] = total.astype(bf16)


def branch_backward(pred_grad, x_last, x_mid, norm_gains, hidden, gathered, head):
    w_out, w_up, w_down, _ = gathered
    rows, width = x_last.shape
    parts, units = w_up.shape[0], w_up.shape[2]
    fixed = lambda shape: pl.BlockSpec(shape, lambda i: (0, 0))
    by_units = pl.BlockSpec((rows, units), lambda i: (0, i))
    by_core = pl.BlockSpec((1, 1, rows, units), lambda i: (i % 2, i // 2, 0, 0))
    columns = head.shape[0]
    wide = (rows, width)
    flops = 2 * rows * (width * width + 2 * width * parts * units + 12 * width * columns)
    return pl.pallas_call(
        branch_back_kernel,
        grid=(parts,),
        out_shape=(
            jax.ShapeDtypeStruct(wide, bf16),
            jax.ShapeDtypeStruct((2, parts // 2, rows, units), bf16),
            jax.ShapeDtypeStruct(wide, f32),
            jax.ShapeDtypeStruct(wide, bf16),
            jax.ShapeDtypeStruct(wide, bf16),
            jax.ShapeDtypeStruct((6, width), f32),
            jax.ShapeDtypeStruct((columns, width), f32),
        ),
        in_specs=[
            fixed((rows, columns)),
            fixed(wide),
            fixed(wide),
            fixed(norm_gains.shape),
            by_units,
            *weight_specs(w_out, w_up, w_down),
            fixed(head.shape),
        ],
        out_specs=[
            fixed(wide),
            by_core,
            fixed(wide),
            fixed(wide),
            fixed(wide),
            fixed((6, width)),
            fixed((columns, width)),
        ],
        scratch_shapes=[pltpu.VMEM(wide, f32), pltpu.VMEM(wide, f32)],
        compiler_params=pltpu.CompilerParams(vmem_limit_bytes=BIG),
        cost_estimate=pl.CostEstimate(
            flops=flops,
            bytes_accessed=4 * width * parts * units + 6 * rows * parts * units,
            transcendentals=2 * rows * parts * units,
        ),
        name="branch_backward",
    )(pred_grad, x_last, x_mid, norm_gains, hidden, w_out, w_up, w_down, head)


def plane_parts(me):
    return [(move, lax.rem(me + move, 8)) for move in (7, 6, 5, 4, 3, 2, 1)]


def swap_kernel(*refs):
    value_ref, act_ref, dg_ref, o_ref, dx2_ref, h2_ref, dx1_ref = refs[:7]
    rows_ref, act_out, dg_out, o_out, dx2_out, h2_out, dx1_out = refs[7:14]
    send_sem, recv_sem, own_sem = refs[14:]
    dp, level, core = mesh_place()
    me = dp * 2 + core
    rows, width = value_ref.shape[0], value_ref.shape[1] // 8
    near = device_of(dp, level, 1 - core)
    barrier = pltpu.get_barrier_semaphore()
    others = [
        (part, device_of(part // 2, level, lax.rem(part, 2))) for _, part in plane_parts(me)
    ]
    for _, target in others:
        pl.semaphore_signal(barrier, inc=1, device_id=target, device_id_type=MESH)
    pl.semaphore_wait(barrier, 7)
    started = []

    def send(source, target_ref, target):
        slot = len(started)
        copy = pltpu.make_async_remote_copy(
            src_ref=source,
            dst_ref=target_ref,
            send_sem=send_sem.at[slot],
            recv_sem=recv_sem.at[slot],
            device_id=target,
            device_id_type=MESH,
        )
        copy.start()
        started.append(copy)

    def row_block(part):
        return rows_ref.at[pl.ds(pl.multiple_of(part * rows, rows), rows), :]

    def column_block(ref, part):
        return ref.at[:, pl.ds(pl.multiple_of(part * width, width), width)]

    for part, target in others:
        send(column_block(value_ref, part), row_block(me), target)
    locals_ = []

    def keep(source, target_ref):
        copy = pltpu.make_async_copy(source, target_ref, own_sem.at[len(locals_)])
        copy.start()
        locals_.append(copy)

    for source, out in ((act_ref, act_out), (dg_ref, dg_out)):
        send(source.at[1 - core], out.at[1], near)
        keep(source.at[core], out.at[0])
    for index in range(4):
        send(column_block(o_ref, index * 2 + 1 - core), o_out.at[1, index], near)
        keep(column_block(o_ref, index * 2 + core), o_out.at[0, index])
    for source, out in ((dx2_ref, dx2_out), (h2_ref, h2_out), (dx1_ref, dx1_out)):
        send(source, out, near)
    row_block(me)[...] = column_block(value_ref, me)[...]
    for copy in started:
        copy.wait()
    for copy in locals_:
        copy.wait()


def exchange_swap(value, act, dg, attended, dx2, h2, dx1):
    rows, width = value.shape
    anywhere = pl.BlockSpec(memory_space=pl.ANY)
    outs = [
        (8 * rows, width // 8), act.shape, dg.shape, (2, 4, rows, width // 8),
        dx2.shape, h2.shape, dx1.shape,
    ]
    return pl.pallas_call(
        swap_kernel,
        out_shape=[jax.ShapeDtypeStruct(shape, bf16) for shape in outs],
        in_specs=[VMEM] * 7,
        out_specs=[VMEM] + [anywhere] * 6,
        scratch_shapes=[
            pltpu.SemaphoreType.DMA((16,)),
            pltpu.SemaphoreType.DMA((16,)),
            pltpu.SemaphoreType.DMA((6,)),
        ],
        compiler_params=pltpu.CompilerParams(
            collective_id=3, has_side_effects=True, vmem_limit_bytes=BIG
        ),
        name="exchange_swap",
    )(value, act, dg, attended, dx2, h2, dx1)


class Scatter:
    order = (0, 3, 1, 2)

    def __init__(self, refs, sems):
        self.send_ref, self.keep_ref, self.one_ref, self.two_ref, self.own_ref, self.deep_ref = refs
        self.one, self.two, self.deep = sems
        self.dp, self.level, self.core = mesh_place()
        self.x, self.y = lax.rem(self.dp, 2), self.dp // 2
        self.side = device_of(self.dp + 1 - 2 * self.x, self.level, self.core)
        self.down = device_of(lax.rem(self.dp + 2, 4), self.level, self.core)

    def copy(self, source, target_ref, sems, slot, place, target):
        return pltpu.make_async_remote_copy(
            src_ref=source,
            dst_ref=target_ref,
            send_sem=sems.at[0, slot],
            recv_sem=sems.at[1, place],
            device_id=target,
            device_id_type=MESH,
        )

    def first(self, depth):
        target = self.side if depth < 2 else self.down
        return self.copy(
            self.send_ref.at[depth], self.one_ref.at[depth], self.one, depth, depth, target
        )

    def second(self, depth):
        target = self.down if depth < 2 else self.side
        which = 1 - self.y if depth < 2 else 1 - self.x
        return self.copy(
            self.keep_ref.at[depth, which], self.two_ref.at[depth], self.two, depth, depth, target
        )

    def mine(self, depth):
        return self.y if depth < 2 else self.x

    def third(self, depth):
        place = lax.rem(self.level + 7 - depth, 4)
        return self.copy(
            self.keep_ref.at[depth, self.mine(depth)], self.deep_ref.at[place], self.deep, depth,
            place, device_of(self.dp, depth, self.core),
        )

    def begin(self, depth, products, held_ref):
        height = self.keep_ref.shape[2]
        top = 0
        for product in products:
            rows, size = product.shape[0], product.shape[1] // 4
            for split in range(4):
                held_ref[split, top : top + rows, :] = product[
                    :, split * size : (split + 1) * size
                ].astype(bf16)
            top += rows
        for which in range(2):
            if depth < 2:
                moved, stays = which * 2 + 1 - self.x, which * 2 + self.x
            else:
                moved, stays = (1 - self.y) * 2 + which, self.y * 2 + which
            self.send_ref[depth, which] = held_ref[moved, :height, :]
            self.keep_ref[depth, which] = held_ref[stays, :height, :]
        self.first(depth).start()

    def middle(self, depth):
        self.first(depth).wait_recv()
        for which in range(2):
            self.keep_ref[depth, which] = (
                self.keep_ref[depth, which].astype(f32) + self.one_ref[depth, which].astype(f32)
            ).astype(bf16)
        self.second(depth).start()

    def end(self, depth):
        self.second(depth).wait_recv()
        total = self.keep_ref[depth, self.mine(depth)].astype(f32) + self.two_ref[depth].astype(f32)

        @pl.when(self.level == depth)
        def _():
            self.own_ref[...] = total

        @pl.when(self.level != depth)
        def _():
            self.keep_ref[depth, self.mine(depth)] = total.astype(bf16)
            self.third(depth).start()

    def finish(self, result_ref):
        for place in range(3):
            self.copy(
                self.keep_ref.at[0, 0], self.deep_ref.at[place], self.deep, 0, place, self.side
            ).wait_recv()
        result_ref[...] = self.own_ref[...] + (
            self.deep_ref[0].astype(f32) + self.deep_ref[1].astype(f32) + self.deep_ref[2].astype(f32)
        )
        for depth in range(4):
            self.first(depth).wait_send()
            self.second(depth).wait_send()

            @pl.when(self.level != depth)
            def _(depth=depth):
                self.third(depth).wait_send()


def scatter_scratch(height, share):
    return [
        pltpu.VMEM((4, 2, height, share), bf16),
        pltpu.VMEM((4, 2, height, share), bf16),
        pltpu.VMEM((4, 2, height, share), bf16),
        pltpu.VMEM((4, height, share), bf16),
        pltpu.VMEM((height, share), f32),
        pltpu.VMEM((3, height, share), bf16),
        pltpu.VMEM((4, height, share), bf16),
        pltpu.SemaphoreType.DMA((2, 4)),
        pltpu.SemaphoreType.DMA((2, 4)),
        pltpu.SemaphoreType.DMA((2, 4)),
    ]


def summed(lefts, rights):
    total = None
    for left, right in zip(lefts, rights):
        part = lax.dot_general(left, right, TN, preferred_element_type=f32)
        total = part if total is None else total + part
    return total


def chunk_spec(shape):
    def where(i):
        index = jnp.minimum(i, 3)
        first, last = (3 - index) // 3, index // 3
        middle = 1 - first - last
        return 0, middle * (5 - 2 * index) + 2 * last, 0, 0

    return pl.BlockSpec((2, 1) + shape, where)


def once(shape):
    return pl.BlockSpec(shape, lambda i: (0,) * len(shape), pipeline_mode=pl.Buffered(1))


class Returns:
    def __init__(self, grads_ref, token_out, width, sems, own_sem):
        self.grads_ref, self.token_out, self.width = grads_ref, token_out, width
        self.sems, self.own_sem = sems, own_sem
        dp, self.level, core = mesh_place()
        self.me = dp * 2 + core
        self.rows = grads_ref.shape[0] // 8

    def part(self, move):
        return lax.rem(self.me + move, 8)

    def refs(self, part, start, size):
        rows = pl.ds(pl.multiple_of(part * self.rows, self.rows), self.rows)
        first = self.me * 3 * self.width + start
        columns = pl.ds(pl.multiple_of(first, self.width), size)
        return self.grads_ref.at[rows, start : start + size], self.token_out.at[:, columns]

    def copy(self, move, late):
        start, size = (self.width, 2 * self.width) if late else (0, self.width)
        part = self.part(move)
        source, target_ref = self.refs(part, start, size)
        return pltpu.make_async_remote_copy(
            src_ref=source,
            dst_ref=target_ref,
            send_sem=self.sems.at[2 * late, move],
            recv_sem=self.sems.at[2 * late + 1, move],
            device_id=device_of(part // 2, self.level, lax.rem(part, 2)),
            device_id_type=MESH,
        )

    def own(self):
        source, target_ref = self.refs(self.me, 0, 3 * self.width)
        return pltpu.make_async_copy(source, target_ref, self.own_sem)

    def peers(self):
        parts = [self.part(move) for move in range(1, 8)]
        return [device_of(part // 2, self.level, lax.rem(part, 2)) for part in parts]

    def finish(self):
        for move in range(1, 8):
            self.copy(move, 0).wait()
            self.copy(move, 1).wait()
        self.own().wait()


def attend_turns(turn, returns, qkv_ref, do_ref, full_ref, lse_ref, dqkv_ref, kt_ref, dk_sum, dv_sum):
    width = do_ref.shape[1]
    heads = width // HEAD_DIM
    rows = returns.rows

    @pl.when(turn == 0)
    def _():
        kt_ref[...] = qkv_ref[:, width : 2 * width].T
        dk_sum[...] = jnp.zeros_like(dk_sum)
        dv_sum[...] = jnp.zeros_like(dv_sum)

    @pl.when(turn < 8)
    def _():
        part = returns.part(turn + 1)
        where = pl.ds(pl.multiple_of(part * rows, rows), rows)
        sums = [lse_ref[head : head + 1, where] for head in range(heads)]
        dqkv_ref[where, :width] = attend_back_rows(
            heads, 1024, qkv_ref[where, :width], do_ref[where, :], full_ref[where, :], sums,
            qkv_ref.at[:, width : 2 * width], qkv_ref.at[:, 2 * width :], kt_ref, dk_sum, dv_sum,
        )

    @pl.when(turn < 7)
    def _():
        returns.copy(turn + 1, 0).start()

    @pl.when(turn == 8)
    def _():
        dqkv_ref[:, width : 2 * width] = dk_sum[...].astype(bf16)
        dqkv_ref[:, 2 * width :] = dv_sum[...].astype(bf16)
        for move in (7, 6, 5, 4, 3, 2, 1):
            returns.copy(move, 1).start()
        returns.own().start()


def attend_exchange_kernel(
    qkv_ref, do_ref, full_ref, lse_ref, rows_ref, token_out, grad_ref,
    dqkv_ref, kt_ref, dk_sum, dv_sum, sems, own_sem,
):
    turn = pl.program_id(0)
    returns = Returns(dqkv_ref, token_out, do_ref.shape[1], sems, own_sem)

    @pl.when(turn == 0)
    def _():
        barrier = pltpu.get_barrier_semaphore()
        for target in returns.peers():
            pl.semaphore_signal(barrier, inc=1, device_id=target, device_id_type=MESH)
        pl.semaphore_wait(barrier, 7)

    attend_turns(
        turn, returns, qkv_ref, do_ref, full_ref, lse_ref, dqkv_ref, kt_ref, dk_sum, dv_sum
    )

    @pl.when(turn >= pieces_at)
    def _():
        grad_ref[...] = lax.dot_general(
            rows_ref[...], dqkv_ref[...], TN, preferred_element_type=f32
        )

    @pl.when(turn == pieces_at + 3)
    def _():
        returns.finish()


def attend_exchange(packed, own_grad, full, logsum, rows_one):
    rows, width = own_grad.shape[0] // 8, own_grad.shape[1]
    piece = lambda i: jnp.clip(i - pieces_at, 0, 3)
    return pl.pallas_call(
        attend_exchange_kernel,
        grid=(pieces_at + 4,),
        out_shape=[
            jax.ShapeDtypeStruct((rows, 24 * width), bf16),
            jax.ShapeDtypeStruct((D, 3 * width), f32),
        ],
        in_specs=[
            once(packed.shape),
            once(own_grad.shape),
            once(full.shape),
            once(logsum.shape),
            pl.BlockSpec((8 * rows, D // 4), lambda i: (0, piece(i))),
        ],
        out_specs=[
            pl.BlockSpec(memory_space=pl.ANY),
            pl.BlockSpec((D // 4, 3 * width), lambda i: (piece(i), 0)),
        ],
        scratch_shapes=[
            pltpu.VMEM((8 * rows, 3 * width), bf16),
            pltpu.VMEM((width, 8 * rows), bf16),
            pltpu.VMEM((8 * rows, width), f32),
            pltpu.VMEM((8 * rows, width), f32),
            pltpu.SemaphoreType.DMA((4, 8)),
            pltpu.SemaphoreType.DMA,
        ],
        compiler_params=pltpu.CompilerParams(
            collective_id=8, has_side_effects=True, vmem_limit_bytes=BIG
        ),
        name="attend_exchange",
    )(packed, own_grad, full, logsum, rows_one)


pieces_at, turns, entry_turns = 9, 14, 11


def finish_kernel(*refs):
    steps = (refs[0:3], refs[3:6])
    qkv_ref, do_ref, full_ref, lse_ref, rows_ref, prev_ref = refs[6:12]
    token_out, share_ref, down_ref = refs[12:15]
    dqkv_ref, kt_ref, dk_sum, dv_sum, piece_send, piece_recv, piece_own = refs[15:22]
    part_sem, piece_sem, own_sem = refs[22:25]
    scatter = Scatter(refs[25:31], refs[32:35])
    held_ref = refs[31]
    turn = pl.program_id(0)
    dp, level, core = mesh_place()
    width = do_ref.shape[1]
    returns = Returns(dqkv_ref, token_out, width, part_sem, own_sem)

    def remote(source, target_ref, send_sem, recv_sem, target):
        return pltpu.make_async_remote_copy(
            src_ref=source,
            dst_ref=target_ref,
            send_sem=send_sem,
            recv_sem=recv_sem,
            device_id=target,
            device_id_type=MESH,
        )

    def piece_copy(index):
        place = lax.rem(level + 7 - index, 4)
        return remote(
            piece_send.at[index], piece_recv.at[place], piece_sem.at[0, index],
            piece_sem.at[1, place], device_of(dp, index, core),
        )

    @pl.when(turn == 0)
    def _():
        barrier = pltpu.get_barrier_semaphore()
        deep = [device_of(dp, lax.rem(level + move, 4), core) for move in (1, 2, 3)]
        for target in returns.peers() + deep:
            pl.semaphore_signal(barrier, inc=1, device_id=target, device_id_type=MESH)
        pl.semaphore_wait(barrier, 10)

    for index, depth in enumerate(scatter.order):

        @pl.when(turn == index)
        def _(depth=depth):
            lefts, rights = [], []
            for act, dx2, dx2_near in steps:
                lefts += [act[0, 0], act[1, 0]]
                rights += [dx2[...], dx2_near[...]]
            scatter.begin(depth, [summed(lefts, rights)], held_ref)

        @pl.when(turn == index + 3)
        def _(depth=depth):
            scatter.middle(depth)

        @pl.when(turn == index + 5)
        def _(depth=depth):
            scatter.end(depth)

    attend_turns(
        turn, returns, qkv_ref, do_ref, full_ref, lse_ref, dqkv_ref, kt_ref, dk_sum, dv_sum
    )

    for index in range(4):

        @pl.when(turn == pieces_at + index)
        def _(index=index):
            piece = prev_ref[...] + lax.dot_general(
                rows_ref[...], dqkv_ref[...], TN, preferred_element_type=f32
            )

            @pl.when(level == index)
            def _():
                piece_own[...] = piece

            @pl.when(level != index)
            def _():
                piece_send[index] = piece.astype(bf16)
                piece_copy(index).start()

    @pl.when(turn == turns - 1)
    def _():
        scatter.finish(down_ref)
        for place in range(3):
            remote(
                piece_send.at[0], piece_recv.at[place], piece_sem.at[0, 0],
                piece_sem.at[1, place], scatter.side,
            ).wait_recv()
        share_ref[...] = piece_own[...] + (
            piece_recv[0].astype(f32) + piece_recv[1].astype(f32) + piece_recv[2].astype(f32)
        )
        returns.finish()
        for index in range(4):

            @pl.when(level != index)
            def _(index=index):
                piece_copy(index).wait_send()


def finish_program(kept, packed, own_grad, full, logsum, rows_one, earlier):
    rows, width = own_grad.shape[0] // 8, own_grad.shape[1]
    in_specs, operands = [], []
    for act, dx2, dx2_near in kept:
        operands += [act, dx2, dx2_near]
        in_specs += [chunk_spec(act.shape[2:]), once(dx2.shape), once(dx2.shape)]
    piece = lambda i: jnp.clip(i - pieces_at, 0, 3)
    in_specs += [
        once(packed.shape),
        once(own_grad.shape),
        once(full.shape),
        once(logsum.shape),
        pl.BlockSpec((8 * rows, D // 4), lambda i: (0, piece(i))),
        pl.BlockSpec((D // 4, 3 * width), lambda i: (piece(i), 0)),
    ]
    operands += [packed, own_grad, full, logsum, rows_one, earlier]
    fixed = lambda shape: pl.BlockSpec(shape, lambda i: (0, 0))
    units = kept[0][0].shape[3]
    share = D // 4
    return pl.pallas_call(
        finish_kernel,
        grid=(turns,),
        out_shape=[
            jax.ShapeDtypeStruct((rows, 24 * width), bf16),
            jax.ShapeDtypeStruct((share, 3 * width), f32),
            jax.ShapeDtypeStruct((units, share), f32),
        ],
        in_specs=in_specs,
        out_specs=[
            pl.BlockSpec(memory_space=pl.ANY),
            fixed((share, 3 * width)),
            fixed((units, share)),
        ],
        scratch_shapes=[
            pltpu.VMEM((8 * rows, 3 * width), bf16),
            pltpu.VMEM((width, 8 * rows), bf16),
            pltpu.VMEM((8 * rows, width), f32),
            pltpu.VMEM((8 * rows, width), f32),
            pltpu.VMEM((4, share, 3 * width), bf16),
            pltpu.VMEM((3, share, 3 * width), bf16),
            pltpu.VMEM((share, 3 * width), f32),
            pltpu.SemaphoreType.DMA((4, 8)),
            pltpu.SemaphoreType.DMA((2, 4)),
            pltpu.SemaphoreType.DMA,
        ]
        + scatter_scratch(units, share),
        compiler_params=pltpu.CompilerParams(
            collective_id=4, has_side_effects=True, vmem_limit_bytes=BIG
        ),
        name="finish_program",
    )(*operands)


def tie(*values):
    return lax.optimization_barrier(values)


def choose(value, index, axis=0):
    return lax.dynamic_index_in_dim(value, index, axis, keepdims=False)


def outer_plain(lefts, rights, by_rows):
    dp, mp = lax.axis_size("dp"), lax.axis_size("mp")
    grads = sum(
        lax.dot_general(left, right, TN, preferred_element_type=f32)
        for left, right in zip(lefts, rights)
    ).astype(bf16)
    rows, width = grads.shape
    if by_rows:
        grads = grads.reshape(dp, rows // dp, mp, width // mp).transpose(0, 2, 1, 3)
    else:
        grads = grads.reshape(mp, rows // mp, dp, width // dp).transpose(2, 0, 1, 3)
    grads = grads.reshape((dp * mp,) + grads.shape[2:])
    return lax.psum_scatter(grads, ("dp", "mp"), scatter_dimension=0, tiled=False).astype(f32)


def exchange_sum_kernel(
    x_ref, loss_ref, qkv_ref, up_out_ref, down_ref, o_ref, s_ref, work_ref, pair_ref, quad_ref, eight_ref, deep_ref, tile_ref,
    send_sem, recv_sem,
):
    dp, level, core = mesh_place()
    x, y = lax.rem(dp, 2), dp // 2
    side = device_of(dp + 1 - 2 * x, level, core)
    down = device_of(lax.rem(dp + 2, 4), level, core)
    near = device_of(dp, level, 1 - core)
    deep = [device_of(dp, lax.rem(level + step, 4), core) for step in (1, 2, 3)]
    barrier = pltpu.get_barrier_semaphore()
    for target in (side, down, near, *deep):
        pl.semaphore_signal(barrier, inc=1, device_id=target, device_id_type=MESH)
    pl.semaphore_wait(barrier, 6)
    started = []

    def send(source, target_ref, target):
        slot = len(started)
        copy = pltpu.make_async_remote_copy(
            src_ref=source,
            dst_ref=target_ref,
            send_sem=send_sem.at[slot],
            recv_sem=recv_sem.at[slot],
            device_id=target,
            device_id_type=MESH,
        )
        copy.start()
        started.append(copy)
        return copy

    half = x_ref.shape[0] // 2
    quarter, eighth, part, unit = half // 2, half // 4, half // 8, half // 16

    def rows(start, size):
        return pl.ds(pl.multiple_of(start, unit), size)

    copy = send(x_ref.at[rows((1 - core) * half, half)], pair_ref, near)
    copy.wait_recv()
    work_ref[...] = x_ref[rows(core * half, half)] + pair_ref[...]
    one = send(work_ref.at[rows((1 - x) * eighth, eighth)], quad_ref.at[0], side)
    two = send(work_ref.at[rows(quarter + (1 - y) * eighth, eighth)], quad_ref.at[1], down)
    base_a = x * eighth
    base_b = quarter + y * eighth
    wide_a, wide_b = core * half + base_a, core * half + base_b
    one.wait_recv()
    work_ref[rows(base_a, eighth)] += quad_ref[0]
    one = send(work_ref.at[rows(base_a + (1 - y) * part, part)], eight_ref.at[0], down)
    two.wait_recv()
    work_ref[rows(base_b, eighth)] += quad_ref[1]
    two = send(work_ref.at[rows(base_b + (1 - x) * part, part)], eight_ref.at[1], side)
    base_a = base_a + y * part
    base_b = base_b + x * part
    one.wait_recv()
    work_ref[rows(base_a, part)] += eight_ref[0]
    two.wait_recv()
    work_ref[rows(base_b, part)] += eight_ref[1]

    def level_start(which):
        late = which // 2
        return (1 - late) * base_a + late * base_b + lax.rem(which, 2) * unit

    copies = []
    for step in (1, 2, 3):
        source = work_ref.at[rows(level_start(lax.rem(level + step, 4)), unit)]
        copies.append(send(source, deep_ref.at[step - 1], deep[step - 1]))
    for copy in copies:
        copy.wait_recv()
    total = work_ref[rows(level_start(level), unit)] + deep_ref[0] + deep_ref[1] + deep_ref[2]
    mine = rows(core * half + level_start(level), unit)
    base_a = core * half + base_a
    base_b = core * half + base_b
    o_ref[mine] = total
    row = lax.broadcasted_iota(jnp.int32, s_ref.shape, 0)
    squares = jnp.sum(total * total)
    for ref in (qkv_ref, up_out_ref, down_ref):
        squares += jnp.sum(ref[...] * ref[...])
    tile_ref[0] = jnp.where(row == 0, squares, jnp.where(row == 1, loss_ref[...], 0.0))
    copies = []
    for step in (1, 2, 3):
        copies.append(send(o_ref.at[mine], o_ref.at[mine], deep[step - 1]))
        copies.append(send(tile_ref.at[0], tile_ref.at[step], deep[step - 1]))
    for copy in copies:
        copy.wait_recv()
    one = send(o_ref.at[rows(base_a, part)], o_ref.at[rows(base_a, part)], down)
    two = send(o_ref.at[rows(base_b, part)], o_ref.at[rows(base_b, part)], side)
    tile_ref[4] = tile_ref[0] + tile_ref[1] + tile_ref[2] + tile_ref[3]
    three = send(tile_ref.at[4], tile_ref.at[5], side)
    one.wait_recv()
    one = send(o_ref.at[rows(wide_a, eighth)], o_ref.at[rows(wide_a, eighth)], side)
    two.wait_recv()
    two = send(o_ref.at[rows(wide_b, eighth)], o_ref.at[rows(wide_b, eighth)], down)
    three.wait_recv()
    tile_ref[6] = tile_ref[4] + tile_ref[5]
    three = send(tile_ref.at[6], tile_ref.at[7], down)
    one.wait_recv()
    two.wait_recv()
    one = send(o_ref.at[rows(core * half, half)], o_ref.at[rows(core * half, half)], near)
    three.wait_recv()
    tile_ref[8] = tile_ref[6] + tile_ref[7]
    three = send(tile_ref.at[8], tile_ref.at[9], near)
    one.wait_recv()
    three.wait_recv()
    s_ref[...] = tile_ref[8] + tile_ref[9]
    for copy in started:
        copy.wait_send()


def exchange_sum(value, loss, *shares):
    rows, width = value.shape
    tile = jax.ShapeDtypeStruct((8, 128), f32)
    return pl.pallas_call(
        exchange_sum_kernel,
        out_shape=(jax.ShapeDtypeStruct(value.shape, f32), tile),
        in_specs=[VMEM] * 5,
        out_specs=[VMEM, VMEM],
        scratch_shapes=[
            pltpu.VMEM((rows // 2, width), f32),
            pltpu.VMEM((rows // 2, width), f32),
            pltpu.VMEM((2, rows // 8, width), f32),
            pltpu.VMEM((2, rows // 16, width), f32),
            pltpu.VMEM((3, rows // 32, width), f32),
            pltpu.VMEM((10,) + tile.shape, f32),
            pltpu.SemaphoreType.DMA((24,)),
            pltpu.SemaphoreType.DMA((24,)),
        ],
        compiler_params=pltpu.CompilerParams(
            collective_id=5, has_side_effects=True, vmem_limit_bytes=BIG
        ),
        name="exchange_sum",
    )(value, loss.reshape(1, 1), *shares)


def split_low(values):
    high = values.astype(bf16)
    return high, (values - high.astype(f32)).astype(bf16)


def three_products(left, right, dims=(((1,), (0,)), ((), ()))):
    def product(one, two):
        return lax.dot_general(one, two, dims, preferred_element_type=f32)

    return product(left[0], right[0]) + (product(left[1], right[0]) + product(left[0], right[1]))


def exact_product(left, right, dims=(((1,), (0,)), ((), ()))):
    return lax.dot_general(left, right, dims, precision=highest, preferred_element_type=f32)


def head_marks(width):
    head = lax.broadcasted_iota(jnp.int32, (HEADS, width), 0)
    column = lax.broadcasted_iota(jnp.int32, (HEADS, width), 1)
    return jnp.where(column // HEAD_DIM == head, 1.0, 0.0).astype(f32)


def quarter_marks(padded):
    row = lax.broadcasted_iota(jnp.int32, (padded, V), 0)
    column = lax.broadcasted_iota(jnp.int32, (padded, V), 1)
    return jnp.where(row // 4 == column, 0.25, 0.0).astype(f32)


def tables_kernel(tables_ref, hot_ref, patch_ref, var_ref, keyed_ref, bias_ref):
    padded, width = patch_ref.shape
    query = tables_ref[5 * V + LEADS : 5 * V + LEADS + 1, :]
    patch_ref[...] = jnp.zeros_like(patch_ref)
    patch_ref[: 4 * V, :] = tables_ref[: 4 * V, :]
    chosen = exact_product(hot_ref[...], tables_ref[4 * V : 5 * V, :])
    var_ref[...] = exact_product(quarter_marks(padded), chosen)
    marks = head_marks(width)
    scale = HEAD_DIM**-0.5
    keyed_ref[...] = exact_product(marks, patch_ref[...] * query, NT) * scale
    bias = exact_product(marks, var_ref[...] * query, NT) * (4.0 * scale)
    column = lax.broadcasted_iota(jnp.int32, bias.shape, 1)
    bias_ref[...] = jnp.where(column < 4 * V, bias, -1e30)


def prepare_tables(tables, var_hot):
    padded = 256
    return pl.pallas_call(
        tables_kernel,
        out_shape=(
            jax.ShapeDtypeStruct((padded, D), f32),
            jax.ShapeDtypeStruct((padded, D), f32),
            jax.ShapeDtypeStruct((HEADS, padded), f32),
            jax.ShapeDtypeStruct((HEADS, padded), f32),
        ),
        compiler_params=pltpu.CompilerParams(vmem_limit_bytes=BIG),
        name="prepare_tables",
    )(tables, var_hot)


def four_sum(values):
    size = values.shape[1]
    lane = lax.broadcasted_iota(jnp.int32, values.shape, 1)
    values = values + jnp.where(
        lane % 2 == 0, pltpu.roll(values, size - 1, 1), pltpu.roll(values, 1, 1)
    )
    return values + jnp.where(
        lane % 4 < 2, pltpu.roll(values, size - 2, 1), pltpu.roll(values, 2, 1)
    )


def cell_shares(cells, keyed, bias):
    scores = four_sum(cells * keyed) + bias
    raised = jnp.exp(scores - jnp.max(scores, axis=1, keepdims=True))
    total = jnp.sum(raised, axis=1, keepdims=True) * 0.25
    return raised * (1.0 / total)


def embed_pair(pair, cells, keyed_ref, bias_ref, patch_ref, var_ref, x0_ref):
    patch = split_low(patch_ref[...])
    variable = split_low(var_ref[...])
    outs = []
    for which in range(2):
        row = pl.ds(pair * 2 + which, 1)
        shares = cell_shares(cells, keyed_ref[row, :], bias_ref[row, :])
        outs.append(
            three_products(split_low(shares * cells), patch)
            + three_products(split_low(shares), variable)
        )
    lane = lax.broadcasted_iota(jnp.int32, outs[0].shape, 1)
    columns = pl.ds(pl.multiple_of(pair * 2 * HEAD_DIM, 2 * HEAD_DIM), 2 * HEAD_DIM)
    x0_ref[:, columns] = jnp.where(lane < HEAD_DIM, outs[0], outs[1])


def embed_kernel(
    u_ref, keyed_ref, bias_ref, patch_ref, var_ref, lead_ref, gains_ref, x0_ref, h1_ref
):
    pair = pl.program_id(0)
    embed_pair(pair, u_ref[...], keyed_ref, bias_ref, patch_ref, var_ref, x0_ref)

    @pl.when(pair == pl.num_programs(0) - 1)
    def _():
        x0_ref[...] += lead_ref[...]
        unit, _ = normed_parts(x0_ref[...])
        h1_ref[...] = (unit * gains_ref[0:1, :] + gains_ref[1:2, :]).astype(bf16)


def embed_forward(cells, prepared, lead_row, norm_gains):
    patch, variable, keyed, bias = prepared
    rows, padded = cells.shape
    fixed = lambda shape: pl.BlockSpec(shape, lambda i: (0, 0))
    by_pair = pl.BlockSpec((padded, 2 * HEAD_DIM), lambda i: (0, i))
    return pl.pallas_call(
        embed_kernel,
        grid=(HEADS // 2,),
        out_shape=(
            jax.ShapeDtypeStruct((rows, D), f32),
            jax.ShapeDtypeStruct((rows, D), bf16),
        ),
        in_specs=[
            fixed((rows, padded)),
            fixed(keyed.shape),
            fixed(bias.shape),
            by_pair,
            by_pair,
            fixed((1, D)),
            fixed(norm_gains.shape),
        ],
        out_specs=[fixed((rows, D)), fixed((rows, D))],
        compiler_params=pltpu.CompilerParams(vmem_limit_bytes=BIG),
        cost_estimate=pl.CostEstimate(
            flops=24 * rows * padded * D, bytes_accessed=14 * rows * D, transcendentals=16 * rows * padded
        ),
        name="embed_forward",
    )(cells, keyed, bias, patch, variable, lead_row, norm_gains)


def entry_rows(
    grad_ref, qkv_ref, x0_ref, mid_ref, gains_ref, du_ref, gain_ref, lead_ref, dx_ref, flip_ref
):
    row_grad = jnp.dot(grad_ref[...], qkv_ref[...], preferred_element_type=f32)
    unit, inverse = normed_parts(x0_ref[...])
    part, gain_grad, bias_grad = norm_grad(unit, inverse, gains_ref[0:1, :], row_grad)
    total = mid_ref[...] + part
    dx_ref[...] = total
    flip_ref[...] = total.T
    lead_ref[...] = jnp.sum(total, axis=0, keepdims=True)
    gain_ref[0:1, :] = gain_grad
    gain_ref[1:2, :] = bias_grad
    du_ref[...] = jnp.zeros_like(du_ref)


def entry_pair(
    pair, u_ref, keyed_ref, bias_ref, patch_ref, var_ref,
    du_ref, dpatch_ref, dvar_ref, dkeyed_ref, dbias_ref, dx_ref, flip_ref,
):
    cells = u_ref[...]
    size = 2 * HEAD_DIM
    columns = pl.ds(pl.multiple_of(pair * size, size), size)
    grads = dx_ref[:, columns]
    lane = lax.broadcasted_iota(jnp.int32, grads.shape, 1)
    patch = split_low(patch_ref[...])
    variable = split_low(var_ref[...])
    cells_grad = None
    for which in range(2):
        row = pl.ds(pair * 2 + which, 1)
        keyed = keyed_ref[row, :]
        shares = cell_shares(cells, keyed, bias_ref[row, :])
        one = split_low(jnp.where(lane // HEAD_DIM == which, grads, 0.0))
        mixed_grad = three_products(one, patch, NT)
        share_grad = mixed_grad * cells + three_products(one, variable, NT)
        weighted = shares * share_grad
        inner = jnp.sum(weighted, axis=1, keepdims=True)
        score_grad = four_sum(weighted) - shares * inner
        piece = mixed_grad * shares + score_grad * keyed
        cells_grad = piece if cells_grad is None else cells_grad + piece
        scale = HEAD_DIM**-0.5
        dkeyed_ref[row, :] = jnp.sum(score_grad * cells, axis=0, keepdims=True) * scale
        dbias_ref[row, :] = jnp.sum(score_grad, axis=0, keepdims=True) * scale
        rows = pl.ds(pl.multiple_of(pair * size + which * HEAD_DIM, HEAD_DIM), HEAD_DIM)
        flipped = split_low(flip_ref[rows, :])
        mine = slice(which * HEAD_DIM, (which + 1) * HEAD_DIM)
        dpatch_ref[mine, :] = three_products(flipped, split_low(shares * cells))
        dvar_ref[mine, :] = three_products(flipped, split_low(shares))
    du_ref[...] += cells_grad


def entry_back_kernel(
    grad_ref, qkv_ref, x0_ref, mid_ref, gains_ref, u_ref, keyed_ref, bias_ref, patch_ref, var_ref,
    du_ref, gain_ref, lead_ref, dpatch_ref, dvar_ref, dkeyed_ref, dbias_ref,
    dx_ref, flip_ref,
):
    pair = pl.program_id(0)

    @pl.when(pair == 0)
    def _():
        entry_rows(
            grad_ref, qkv_ref, x0_ref, mid_ref, gains_ref, du_ref, gain_ref, lead_ref, dx_ref,
            flip_ref,
        )

    entry_pair(
        pair, u_ref, keyed_ref, bias_ref, patch_ref, var_ref,
        du_ref, dpatch_ref, dvar_ref, dkeyed_ref, dbias_ref, dx_ref, flip_ref,
    )


def entry_last_kernel(*refs):
    steps = (refs[0:6], refs[6:12])
    share_ref = refs[12]
    grad_ref, qkv_ref, x0_ref, mid_ref, gains_ref, u_ref, keyed_ref, bias_ref = refs[13:21]
    patch_ref, var_ref, query_ref, hot_ref, lead_hot_ref, head_a, head_b, high_a, high_b = refs[21:30]
    patch_a, var_a, keyed_a, bias_a, lead_a, gain_a = refs[30:36]
    rows_out, up_out_ref, qkv_share_ref = refs[36:39]
    (dx_ref, flip_ref, low_ref, landing_ref, cross_sem, du_ref, gain_ref, lead_ref, dpatch_ref,
     dvar_ref, dkeyed_ref, dbias_ref) = refs[39:51]
    scatter = Scatter(refs[51:57], refs[58:61])
    held_ref = refs[57]
    turn = pl.program_id(0)
    dp, level, core = mesh_place()
    across = device_of(level, dp, core)
    crossing = scatter.copy(low_ref, landing_ref, cross_sem, 0, 0, across)

    @pl.when(turn == 0)
    def _():
        barrier = pltpu.get_barrier_semaphore()
        deep = [device_of(dp, lax.rem(level + move, 4), core) for move in (1, 2, 3)]
        for target in (scatter.side, scatter.down, *deep):
            pl.semaphore_signal(barrier, inc=1, device_id=target, device_id_type=MESH)
        low_ref[...] = share_ref[...]

        @pl.when(dp != level)
        def _():
            pl.semaphore_signal(barrier, inc=1, device_id=across, device_id_type=MESH)
            pl.semaphore_wait(barrier, 6)
            crossing.start()

        @pl.when(dp == level)
        def _():
            pl.semaphore_wait(barrier, 5)

    for index, depth in enumerate(scatter.order):

        @pl.when(turn == index)
        def _(depth=depth):
            lefts, rights, smalls, wides = [], [], [], []
            for dg, o, h2, h2_near, dx1, dx1_near in steps:
                lefts += [dg[0, 0], dg[1, 0]]
                rights += [h2[...], h2_near[...]]
                smalls += [o[0, 0], o[1, 0]]
                wides += [dx1[...], dx1_near[...]]
            scatter.begin(depth, [summed(lefts, rights), summed(smalls, wides)], held_ref)

        @pl.when(turn == index + 3)
        def _(depth=depth):
            scatter.middle(depth)

        @pl.when(turn == index + 6)
        def _(depth=depth):
            scatter.end(depth)

    @pl.when(turn == 0)
    def _():
        entry_rows(
            grad_ref, qkv_ref, x0_ref, mid_ref, gains_ref, du_ref, gain_ref,
            lead_ref.at[0:1, :], dx_ref, flip_ref,
        )

    @pl.when((turn >= 1) & (turn <= HEADS // 2))
    def _():
        size = 2 * HEAD_DIM
        pair = turn - 1
        some = pl.ds(pl.multiple_of(pair * size, size), size)
        entry_pair(
            pair, u_ref, keyed_ref, bias_ref, patch_ref.at[:, some], var_ref.at[:, some],
            du_ref, dpatch_ref.at[some, :], dvar_ref.at[some, :], dkeyed_ref, dbias_ref,
            dx_ref, flip_ref,
        )

    @pl.when(turn == entry_turns - 2)
    def _():
        gain_ref[...] += gain_a[...]
        lead_ref[1:2, :] = lead_a[...]
        lead_ref[2:8, :] = jnp.zeros((6, lead_ref.shape[1]), f32)
        table_rows(
            patch_a, dpatch_ref, var_a, dvar_ref, keyed_a, dkeyed_ref, bias_a, dbias_ref,
            patch_ref, var_ref, query_ref, hot_ref, lead_hot_ref, lead_ref, gain_ref,
            (head_a[...], head_b[...]), (high_a[2:6, :], high_b[2:6, :]), rows_out,
        )

    @pl.when(turn == entry_turns - 1)
    def _():
        @pl.when(dp != level)
        def _():
            crossing.wait()
            qkv_share_ref[...] = landing_ref[...]

        @pl.when(dp == level)
        def _():
            qkv_share_ref[...] = share_ref[...]

        scatter.finish(up_out_ref)


def entry_last(
    kept, share, token_grad, qkv_t, x_first, mid_grad, norm_gains, cells, prepared,
    query, var_hot, lead_hots, heads, highs, earlier,
):
    patch, variable, keyed, bias = prepared
    rows, width = x_first.shape
    padded = cells.shape[1]
    in_specs, operands = [], []
    for dg, o, h2, h2_near, dx1, dx1_near in kept:
        operands += [dg, o, h2, h2_near, dx1, dx1_near]
        in_specs += [chunk_spec(dg.shape[2:]), chunk_spec(o.shape[2:])]
        in_specs += [once(h2.shape)] * 4
    values = [
        share, token_grad, qkv_t, x_first, mid_grad, norm_gains, cells, keyed, bias,
        patch, variable, query, var_hot, lead_hots, *heads, *highs, *earlier,
    ]
    in_specs += [once(value.shape) for value in values]
    height, columns = kept[0][0].shape[3] + kept[0][1].shape[3], width // 4
    outs = [(2 * padded, width), (height, columns), share.shape]
    return pl.pallas_call(
        entry_last_kernel,
        grid=(entry_turns,),
        out_shape=[jax.ShapeDtypeStruct(shape, f32) for shape in outs],
        in_specs=in_specs,
        out_specs=[pl.BlockSpec(shape, lambda i: (0, 0)) for shape in outs],
        scratch_shapes=[
            pltpu.VMEM((rows, width), f32),
            pltpu.VMEM((width, rows), f32),
            pltpu.VMEM(share.shape, f32),
            pltpu.VMEM(share.shape, f32),
            pltpu.SemaphoreType.DMA((2, 1)),
            pltpu.VMEM((rows, padded), f32),
            pltpu.VMEM((2, width), f32),
            pltpu.VMEM((8, width), f32),
            pltpu.VMEM((width, padded), f32),
            pltpu.VMEM((width, padded), f32),
            pltpu.VMEM(keyed.shape, f32),
            pltpu.VMEM(bias.shape, f32),
        ]
        + scatter_scratch(height, columns),
        compiler_params=pltpu.CompilerParams(
            collective_id=6, has_side_effects=True, vmem_limit_bytes=BIG
        ),
        name="entry_last",
    )(*operands, *values)


def entry_backward(token_grad, qkv_t, x_first, mid_grad, norm_gains, cells, prepared):
    patch, variable, keyed, bias = prepared
    rows, width = x_first.shape
    padded = cells.shape[1]
    fixed = lambda shape: pl.BlockSpec(shape, lambda i: (0, 0))
    by_pair = pl.BlockSpec((padded, 2 * HEAD_DIM), lambda i: (0, i))
    flipped = pl.BlockSpec((2 * HEAD_DIM, padded), lambda i: (i, 0))
    return pl.pallas_call(
        entry_back_kernel,
        grid=(HEADS // 2,),
        out_shape=(
            jax.ShapeDtypeStruct((rows, padded), f32),
            jax.ShapeDtypeStruct((2, width), f32),
            jax.ShapeDtypeStruct((1, width), f32),
            jax.ShapeDtypeStruct((width, padded), f32),
            jax.ShapeDtypeStruct((width, padded), f32),
            jax.ShapeDtypeStruct(keyed.shape, f32),
            jax.ShapeDtypeStruct(bias.shape, f32),
        ),
        in_specs=[
            fixed(token_grad.shape),
            fixed(qkv_t.shape),
            fixed((rows, width)),
            fixed((rows, width)),
            fixed(norm_gains.shape),
            fixed(cells.shape),
            fixed(keyed.shape),
            fixed(bias.shape),
            by_pair,
            by_pair,
        ],
        out_specs=[
            fixed((rows, padded)),
            fixed((2, width)),
            fixed((1, width)),
            flipped,
            flipped,
            fixed(keyed.shape),
            fixed(bias.shape),
        ],
        scratch_shapes=[pltpu.VMEM((rows, width), f32), pltpu.VMEM((width, rows), f32)],
        compiler_params=pltpu.CompilerParams(vmem_limit_bytes=BIG),
        cost_estimate=pl.CostEstimate(
            flops=60 * rows * padded * D, bytes_accessed=40 * rows * D, transcendentals=16 * rows * padded
        ),
        name="entry_backward",
    )(token_grad, qkv_t, x_first, mid_grad, norm_gains, cells, keyed, bias, patch, variable)


def table_rows(
    pa_ref, pb_ref, va_ref, vb_ref, ka_ref, kb_ref, ba_ref, bb_ref,
    patch_ref, var_ref, query_ref, hot_ref, lead_hot_ref, lead_ref, gain_ref, heads, highs, o_ref,
):
    padded, width = patch_ref.shape
    marks = head_marks(width)
    query = query_ref[...]
    keyed_grad = exact_product(ka_ref[...] + kb_ref[...], marks, TN)
    bias_grad = exact_product(ba_ref[...] + bb_ref[...], marks, TN)
    o_ref[...] = jnp.zeros_like(o_ref)
    patch_grad = (pa_ref[...] + pb_ref[...]).T + keyed_grad * query
    o_ref[: 4 * V, :] = patch_grad[: 4 * V, :]
    var_grad = (va_ref[...] + vb_ref[...]).T + bias_grad * query
    var_rows = exact_product(quarter_marks(padded), var_grad, TN)
    o_ref[4 * V : 5 * V, :] = exact_product(hot_ref[...], var_rows, TN)
    lead_rows = exact_product(lead_hot_ref[...], lead_ref[...], TN)
    o_ref[5 * V : 5 * V + LEADS, :] = lead_rows[:LEADS, :]
    query_grad = jnp.sum(
        keyed_grad * patch_ref[...] + bias_grad * var_ref[...], axis=0, keepdims=True
    )
    o_ref[5 * V + LEADS : 5 * V + LEADS + 1, :] = query_grad
    o_ref[5 * V + LEADS + 1 : 5 * V + LEADS + 3, :] = gain_ref[...]
    o_ref[padded : padded + 4 * V, :] = heads[0] + heads[1]
    o_ref[padded + 4 * V : padded + 4 * V + 4, :] = highs[0] + highs[1]


def table_grads_kernel(*refs):
    head_a, head_b, high_a, high_b = refs[15:19]
    heads, highs = (head_a[...], head_b[...]), (high_a[2:6, :], high_b[2:6, :])
    table_rows(*refs[:15], heads, highs, refs[19])


def table_grads(first, second, prepared, query, var_hot, lead_hots, leads, gain_rows, heads, highs):
    patch, variable, _, _ = prepared
    operands = []
    for one, two in zip(first, second):
        operands += [one, two]
    return pl.pallas_call(
        table_grads_kernel,
        out_shape=jax.ShapeDtypeStruct((2 * patch.shape[0], D), f32),
        compiler_params=pltpu.CompilerParams(vmem_limit_bytes=BIG),
        name="table_grads",
    )(*operands, patch, variable, query, var_hot, lead_hots, leads, gain_rows, *heads, *highs)


def adam_step(master, grad, first, second, rate):
    first_new = beta_first * first + (1.0 - beta_first) * grad
    second_new = beta_second * second + (1.0 - beta_second) * grad * grad
    update = first_new / first_fix / (jnp.sqrt(second_new / second_fix) + adam_eps)
    return (master - rate * (update + decay_rate * master), first_new, second_new)


def update_kernel(packed, *refs):
    where_ref, sums_ref, tile_ref, count_ref = refs[:4]
    shares = list(refs[4 : 4 + (3 if packed else 4)])
    rest = refs[4 + len(shares) :]
    states, average_ref, outs = rest[:18], rest[18], rest[19:]
    norm = jnp.sqrt(tile_ref[0:1, 0:1])
    factor = jnp.minimum(1.0, clip_norm / (norm + 1e-06))
    outs[1][...] = norm
    outs[0][...] = tile_ref[1:2, 0:1] / (2.0 * V * jnp.maximum(count_ref[...], 1.0))
    embed_rows = 5 * V + LEADS + 1
    padded = 256

    def apply(index, grad, rate, rows=slice(None)):
        master, first, second = (ref[rows, :] for ref in states[3 * index : 3 * index + 3])
        new = adam_step(master, factor * grad, first, second, rate)
        for ref, value in zip(outs[2 + 3 * index : 5 + 3 * index], new):
            ref[rows, :] = value
        return new[0]

    apply(0, sums_ref[:embed_rows, :], lr_table, slice(0, embed_rows))
    apply(0, sums_ref[padded : padded + 4 * V, :], lr_table, slice(embed_rows, embed_rows + 4 * V))
    apply(1, sums_ref[embed_rows : embed_rows + 2, :], lr_gain, slice(0, 2))
    apply(1, sums_ref[padded + 4 * V : padded + 4 * V + 4, :], lr_gain, slice(2, 6))
    if packed:
        units = shares[2].shape[0]
        grads = (
            shares[0][...], shares[1][units:, :], shares[1][:units, :].T, shares[2][...]
        )
    else:
        grads = [share[...] for share in shares]
    qkv_new = apply(2, grads[0], lr_matrix)
    for index in range(1, 4):
        apply(2 + index, grads[index], lr_matrix)
    outs[20][...] = average_keep * average_ref[...] + (1.0 - average_keep) * qkv_new


def update_all(packed, where, sums, tile, count, shares, states, average):
    operands = [sums, tile, count.reshape(1, 1), *shares]
    fixed = lambda shape: pl.BlockSpec(shape, lambda i, w: (0, 0))
    in_specs = [fixed(value.shape) for value in operands]
    out_shapes = [(1, 1), (1, 1)]
    for master, first, second in states:
        if master.shape == first.shape:
            in_specs.append(fixed(master.shape))
        elif master.shape[0] == first.shape[0]:
            in_specs.append(pl.BlockSpec(first.shape, lambda i, w: (0, w[0])))
        else:
            in_specs.append(pl.BlockSpec(first.shape, lambda i, w: (w[0], 0)))
        in_specs += [fixed(first.shape)] * 2
        operands += [master, first, second]
        out_shapes += [first.shape] * 3
    operands.append(average)
    in_specs.append(fixed(average.shape))
    out_shapes.append(average.shape)
    return pl.pallas_call(
        partial(update_kernel, packed),
        grid_spec=pltpu.PrefetchScalarGridSpec(
            num_scalar_prefetch=1,
            grid=(1,),
            in_specs=in_specs,
            out_specs=[fixed(shape) for shape in out_shapes],
        ),
        out_shape=[jax.ShapeDtypeStruct(shape, f32) for shape in out_shapes],
        compiler_params=pltpu.CompilerParams(vmem_limit_bytes=60 * 2**20),
        name="update_all",
    )(where, *operands)


def by_kind(shard):
    rows = shard.shape[0]
    return shard.reshape(rows, -1, 3, HEAD_DIM).transpose(0, 2, 1, 3).reshape(rows, -1)


def by_head(shard):
    rows = shard.shape[0]
    return shard.reshape(rows, 3, -1, HEAD_DIM).transpose(0, 2, 1, 3).reshape(rows, -1)


class Rows:
    count = 11

    def __init__(self, refs, sems):
        (self.h1, self.rows_ref, self.weight, self.qkv, self.vt, self.o_ref, self.full, self.lse,
         self.attended) = refs
        self.sems, self.o_sems, self.own_sem = sems
        dp, level, core = mesh_place()
        self.dp, self.core = dp, core
        self.me = dp * 2 + core
        self.height = self.h1.shape[0]
        self.width = self.o_ref.shape[1]
        half = self.height // 2
        x = lax.rem(dp, 2)
        beside, below, far = dp + 1 - 2 * x, lax.rem(dp + 2, 4), 3 - dp
        self.owners = (beside, below, far)
        self.peers = []
        for move in range(1, 8):
            part = lax.rem(self.me + move, 8)
            self.peers.append(device_of(part // 2, level, lax.rem(part, 2)))
        side = device_of(beside, level, core)
        down = device_of(below, level, core)
        near = device_of(dp, level, 1 - core)
        self.level = level
        slots = [0]

        def remote(source, target_ref, target):
            slot = slots[0]
            slots[0] += 1
            return pltpu.make_async_remote_copy(
                src_ref=source,
                dst_ref=target_ref,
                send_sem=self.sems.at[0, slot],
                recv_sem=self.sems.at[1, slot],
                device_id=target,
                device_id_type=MESH,
            )

        def place(owner, first, size):
            start = pl.multiple_of((owner * 2 + core) * self.height + first, half)
            return self.rows_ref.at[pl.ds(start, size)]

        def relay(where, target):
            return remote(where, where, target)

        first, second = self.h1.at[pl.ds(0, half)], self.h1.at[pl.ds(half, half)]
        self.side_a = remote(first, place(dp, 0, half), side)
        self.down_b = remote(second, place(dp, half, half), down)
        self.side_b = remote(second, place(dp, half, half), side)
        self.down_a = remote(first, place(dp, 0, half), down)
        self.near_own = remote(self.h1, place(dp, 0, self.height), near)
        self.far_a = relay(place(beside, 0, half), down)
        self.far_b = relay(place(below, half, half), side)
        self.near_side = relay(place(beside, 0, self.height), near)
        self.near_down = relay(place(below, 0, self.height), near)
        self.near_far = relay(place(far, 0, self.height), near)

    def part_rows(self, part):
        return pl.ds(pl.multiple_of(part * self.height, self.height), self.height)

    def project(self, owner, core):
        where = self.part_rows(owner * 2 + core)
        self.qkv[where, :] = lax.dot_general(
            self.rows_ref[where, :], self.weight[...], NT, preferred_element_type=f32
        ).astype(bf16)

    def send_o(self, part, target):
        columns = pl.ds(pl.multiple_of(self.me * self.width, self.width), self.width)
        return pltpu.make_async_remote_copy(
            src_ref=self.o_ref.at[self.part_rows(part), :],
            dst_ref=self.attended.at[:, columns],
            send_sem=self.o_sems.at[0, lax.rem(part + 8 - self.me, 8)],
            recv_sem=self.o_sems.at[1, lax.rem(part + 8 - self.me, 8)],
            device_id=target,
            device_id_type=MESH,
        )

    def keep_o(self):
        columns = pl.ds(pl.multiple_of(self.me * self.width, self.width), self.width)
        return pltpu.make_async_copy(
            self.o_ref.at[self.part_rows(self.me), :], self.attended.at[:, columns], self.own_sem
        )

    def phase(self, number):
        beside, below, far = self.owners
        if number == 0:
            for copy in (self.side_a, self.down_b, self.side_b, self.down_a, self.near_own):
                copy.start()
            self.rows_ref[self.part_rows(self.me), :] = self.h1[...]
        elif number == 1:
            self.project(self.dp, self.core)
            self.near_own.wait_recv()
        elif number == 2:
            self.side_a.wait_recv()
            self.far_a.start()
            self.down_b.wait_recv()
            self.far_b.start()
            self.project(self.dp, 1 - self.core)
        elif number == 3:
            self.side_b.wait_recv()
            self.near_side.start()
            self.down_a.wait_recv()
            self.near_down.start()
            self.project(beside, self.core)
            self.project(below, self.core)
        elif number == 4:
            self.near_side.wait_recv()
            self.near_down.wait_recv()
            self.project(beside, 1 - self.core)
            self.project(below, 1 - self.core)
        elif number == 5:
            self.far_a.wait_recv()
            self.far_b.wait_recv()
            self.near_far.start()
            self.project(far, self.core)
        elif number == 6:
            self.near_far.wait_recv()
            self.project(far, 1 - self.core)
            self.vt[...] = self.qkv[:, 2 * self.width :].T

    def attend(self, turn):
        owner = lax.rem(self.dp + 1 + turn, 4)
        size = 2 * self.height
        where = pl.ds(pl.multiple_of(owner * size, size), size)
        heads = self.width // HEAD_DIM
        full, sums = attend_rows(
            heads, self.qkv[where, : self.width],
            self.qkv.at[:, self.width : 2 * self.width], self.vt,
        )
        for head in range(heads):
            self.lse[head : head + 1, where] = sums[head]
        self.full[where, :] = full
        self.o_ref[where, :] = full.astype(bf16)

        @pl.when(turn < 3)
        def _():
            for core in range(2):
                self.send_o(owner * 2 + core, device_of(owner, self.level, core)).start()

        @pl.when(turn == 3)
        def _():
            other = device_of(self.dp, self.level, 1 - self.core)
            self.send_o(self.dp * 2 + 1 - self.core, other).start()
            self.keep_o().start()

    def finish(self):
        for move in range(1, 8):
            part = lax.rem(self.me + move, 8)
            self.send_o(part, self.peers[move - 1]).wait()
        self.keep_o().wait()
        for copy in (
            self.side_a, self.down_b, self.side_b, self.down_a, self.near_own, self.far_a,
            self.far_b, self.near_side, self.near_down, self.near_far,
        ):
            copy.wait_send()


def row_scratch(rows, width):
    return [
        pltpu.VMEM((rows, D), bf16),
        pltpu.VMEM((8 * rows, D), bf16),
        pltpu.VMEM((3 * width, D), bf16),
        pltpu.VMEM((width, 8 * rows), bf16),
        pltpu.VMEM((8 * rows, width), bf16),
        pltpu.SemaphoreType.DMA((2, 10)),
        pltpu.SemaphoreType.DMA((2, 8)),
        pltpu.SemaphoreType.DMA((3,)),
    ]


def lead_rows_of(lead, lead_ref):
    row = lax.broadcasted_iota(jnp.int32, (1, 8), 1).astype(f32)
    lead_hot = jnp.where(row == lead, 1.0, 0.0).astype(f32)
    return exact_product(lead_hot, lead_ref[...])


def middle_kernel(
    guess_ref, first_ref, keyed_ref, bias_ref, patch_ref, var_ref, lead_ref, gains_ref, weights_ref,
    x0_ref, cells_ref, qkv_ref, full_ref, lse_ref, rows_out, attended_ref,
    h1_ref, rows_ref, weight_ref, vt_ref, o_ref, sems, o_sems, own_sem,
):
    turn = pl.program_id(0)
    dp, _, core = mesh_place()
    rows = Rows(
        (h1_ref, rows_ref, weight_ref, qkv_ref, vt_ref, o_ref, full_ref, lse_ref, attended_ref),
        (sems, o_sems, own_sem.at[0]),
    )
    size = weight_ref.shape[0]
    weight = pltpu.make_async_copy(
        weights_ref.at[pl.ds(pl.multiple_of((dp * 2 + core) * size, size), size), :],
        weight_ref, own_sem.at[1],
    )
    save = pltpu.make_async_copy(rows_ref, rows_out, own_sem.at[2])
    pairs = HEADS // 2

    @pl.when(turn == 0)
    def _():
        barrier = pltpu.get_barrier_semaphore()
        for target in rows.peers:
            pl.semaphore_signal(barrier, inc=1, device_id=target, device_id_type=MESH)
        pl.semaphore_wait(barrier, 7)
        weight.start()
        cells_ref[:, : 4 * V] = guess_ref[...]
        cells_ref[:, 4 * V :] = jnp.zeros_like(cells_ref[:, 4 * V :])

    @pl.when(turn < pairs)
    def _():
        embed_pair(turn, cells_ref[...], keyed_ref, bias_ref, patch_ref, var_ref, x0_ref)

    @pl.when(turn == pairs)
    def _():
        x0_ref[...] += lead_rows_of(first_ref[0:1, 4 * V + 5 : 4 * V + 6], lead_ref)
        unit, _ = normed_parts(x0_ref[...])
        h1_ref[...] = (unit * gains_ref[0:1, :] + gains_ref[1:2, :]).astype(bf16)
        weight.wait()

    for number in range(7):

        @pl.when(turn == pairs + number)
        def _(number=number):
            rows.phase(number)
            if number == 6:
                save.start()

    @pl.when(turn >= pairs + 7)
    def _():
        rows.attend(turn - pairs - 7)

    @pl.when(turn == pairs + 10)
    def _():
        rows.finish()
        save.wait()


def middle_program(guess, first_cells, prepared, lead_table, norm_gains, qkv_t):
    patch, variable, keyed, bias = prepared
    rows = guess.shape[0]
    padded = patch.shape[0]
    width = D // 8
    heads = width // HEAD_DIM
    total = 8 * rows
    anywhere = pl.BlockSpec(memory_space=pl.ANY)
    fixed = lambda shape: pl.BlockSpec(shape, lambda i: (0, 0))
    by_pair = pl.BlockSpec(
        (padded, 2 * HEAD_DIM), lambda i: (0, jnp.clip(i, 0, HEADS // 2 - 1))
    )
    shapes = [
        ((rows, D), f32),
        ((rows, padded), f32),
        ((total, 3 * width), bf16),
        ((total, width), f32),
        ((heads, total), f32),
    ]
    return pl.pallas_call(
        middle_kernel,
        grid=(HEADS // 2 + Rows.count,),
        out_shape=[jax.ShapeDtypeStruct(shape, kind) for shape, kind in shapes]
        + [jax.ShapeDtypeStruct((total, D), bf16), jax.ShapeDtypeStruct((rows, D), bf16)],
        in_specs=[once(value.shape) for value in (guess, first_cells, keyed, bias)]
        + [by_pair, by_pair, once(lead_table.shape), once(norm_gains.shape), anywhere],
        out_specs=[fixed(shape) for shape, _ in shapes] + [anywhere, anywhere],
        scratch_shapes=row_scratch(rows, width),
        compiler_params=pltpu.CompilerParams(
            collective_id=9, has_side_effects=True, vmem_limit_bytes=BIG
        ),
        name="middle_program",
    )(guess, first_cells, keyed, bias, patch, variable, lead_table, norm_gains, qkv_t)


lag_one, lag_two, ahead = 2, 4, 3
embed_at, gather_at = 3, 11


def start_kernel(halves, *refs):
    count = len(halves)
    packed_ref, keyed_ref, bias_ref, patch_ref, var_ref, lead_ref, gains_ref = refs[:7]
    shards = refs[7 : 7 + count]
    x0_ref, cells_ref, qkv_ref, full_ref, lse_ref, count_ref, rows_out, attended_ref = refs[
        7 + count : 15 + count
    ]
    outs = refs[15 + count : 15 + 2 * count]
    (h1_ref, rows_ref, weight_ref, vt_ref, o_ref, row_sems, o_sems, row_own, held_ref, tile_ref,
     send_sem, recv_sem, level_send, level_recv, own_sem) = refs[15 + 2 * count :]
    rows = Rows(
        (h1_ref, rows_ref, weight_ref, qkv_ref, vt_ref, o_ref, full_ref, lse_ref, attended_ref),
        (row_sems, o_sems, row_own.at[0]),
    )
    step = pl.program_id(0)
    dp, level, core = mesh_place()
    x = lax.rem(dp, 2)
    columns = {"here": dp, "side": dp + 1 - 2 * x, "down": lax.rem(dp + 2, 4), "far": 3 - dp}
    side = device_of(columns["side"], level, core)
    down = device_of(columns["down"], level, core)
    near = device_of(dp, level, 1 - core)
    across = device_of(level, dp, core)
    middle = lax.rem(level, 3) != 0
    late = level // 2
    sources = (level + 1 - 2 * lax.rem(level, 2), 2 - late, 3 * (1 - late))
    onward = (3 - level, lax.rem(3 * level + 1, 4), lax.rem(3 * level + 1, 4))
    slots = [0]

    def remote(source, target_ref, target):
        slot = slots[0]
        slots[0] += 1
        return pltpu.make_async_remote_copy(
            src_ref=source,
            dst_ref=target_ref,
            send_sem=send_sem.at[slot],
            recv_sem=recv_sem.at[slot],
            device_id=target,
            device_id_type=MESH,
        )

    def place(out, source, column, half, pieces):
        rows = out.shape[1] // 4
        size = rows // pieces
        start = pl.multiple_of(columns[column] * rows + half * size, size)
        return out.at[source * 2 + core, pl.ds(start, size), :]

    def pass_on(out, source, column, target, cut):
        where = place(out, source, column, *cut)
        return remote(where, where, target)

    crossing = remote(packed_ref, held_ref, across)
    staying = pltpu.make_async_copy(packed_ref, held_ref, own_sem.at[count])
    mine = [outs[index].at[level * 2 + core] for index in range(count)]
    given = [remote(shards[index], mine[index], near) for index in range(count)]
    kept = [
        pltpu.make_async_copy(shards[index], mine[index], own_sem.at[index]) for index in range(count)
    ]
    chunks, openings = [], []
    for index in range(count):
        out, pieces = outs[index], halves[index]
        for half in range(pieces):
            group = len(openings)
            full = out.shape[1] // 4
            size = full // pieces
            own = shards[index].at[pl.ds(pl.multiple_of(dp * full + half * size, size), size), :]
            cut = (half, pieces)

            def along(source_ref, source, target_level, slot):
                return pltpu.make_async_remote_copy(
                    src_ref=source_ref,
                    dst_ref=place(out, source, "here", *cut),
                    send_sem=level_send.at[group * 5 + slot],
                    recv_sem=level_recv.at[group * 4 + source],
                    device_id=device_of(dp, target_level, core),
                    device_id_type=MESH,
                )

            openings.append(
                (
                    along(own, level, lax.rem(level + 1, 4), 0),
                    along(own, level, lax.rem(level + 3, 4), 1),
                )
            )
            for turn in range(3):
                source = sources[turn]
                chunks.append(
                    {
                        "level": along(place(out, source, "here", *cut), source, onward[turn], 2 + turn),
                        "side": pass_on(out, source, "here", side, cut),
                        "down": pass_on(out, source, "here", down, cut),
                        "hop_down": pass_on(out, source, "side", down, (2 * half, 2 * pieces)),
                        "hop_side": pass_on(out, source, "down", side, (2 * half + 1, 2 * pieces)),
                        "here_near": pass_on(out, source, "here", near, cut),
                        "side_near": pass_on(out, source, "side", near, cut),
                        "down_near": pass_on(out, source, "down", near, cut),
                        "far_near": pass_on(out, source, "far", near, cut),
                    }
                )
    groups = len(openings)
    order = []
    for number in range(groups + 2):
        for turn in range(3):
            if 0 <= number - turn < groups:
                order.append((number - turn, turn))
    chunks = [chunks[3 * group + turn] for group, turn in order]
    total = len(chunks)

    def start_group(number):
        @pl.when(level < 3)
        def _():
            openings[number][0].start()

        @pl.when(level > 0)
        def _():
            openings[number][1].start()

    tiles = [
        remote(tile_ref.at[0], tile_ref.at[1], side),
        remote(tile_ref.at[2], tile_ref.at[3], down),
        remote(tile_ref.at[4], tile_ref.at[5], near),
    ]
    deep = [device_of(dp, lax.rem(level + move, 4), core) for move in (1, 2, 3)]
    level_tiles = [remote(tile_ref.at[6], tile_ref.at[7 + move], deep[move]) for move in range(3)]
    weight = pltpu.make_async_copy(outs[0].at[dp * 2 + core], weight_ref, row_own.at[1])
    save = pltpu.make_async_copy(rows_ref, rows_out, row_own.at[2])

    @pl.when(step == 0)
    def _():
        barrier = pltpu.get_barrier_semaphore()
        for target in (*rows.peers, *deep):
            pl.semaphore_signal(barrier, inc=1, device_id=target, device_id_type=MESH)

        @pl.when(dp != level)
        def _():
            pl.semaphore_signal(barrier, inc=1, device_id=across, device_id_type=MESH)
            pl.semaphore_wait(barrier, 11)
            crossing.start()

        @pl.when(dp == level)
        def _():
            pl.semaphore_wait(barrier, 10)
            staying.start()

        for number in range(ahead):
            start_group(number)
        for copy in (*given, *kept):
            copy.start()

    for number in range(total + lag_two):

        @pl.when(step == number)
        def _(number=number):
            if number < total:
                chunk = chunks[number]
                chunk["level"].wait_recv()

                @pl.when(middle)
                def _():
                    chunk["level"].start()

                chunk["side"].start()
                chunk["down"].start()
                chunk["here_near"].start()
                group, turn = order[number]
                if turn == 0 and group + ahead < groups:
                    start_group(group + ahead)
            if 0 <= number - lag_one < total:
                chunk = chunks[number - lag_one]
                chunk["side"].wait_recv()
                chunk["hop_down"].start()
                chunk["down"].wait_recv()
                chunk["hop_side"].start()
                chunk["side_near"].start()
                chunk["down_near"].start()
            if 0 <= number - lag_two < total:
                chunk = chunks[number - lag_two]
                chunk["hop_down"].wait_recv()
                chunk["hop_side"].wait_recv()
                chunk["far_near"].start()

    @pl.when(step == embed_at)
    def _():
        @pl.when(dp != level)
        def _():
            crossing.wait_recv()

        @pl.when(dp == level)
        def _():
            staying.wait()

        cells_ref[...] = held_ref[...]
        lane = lax.broadcasted_iota(jnp.int32, held_ref.shape, 1)
        ocean = jnp.where((lane >= 4 * V) & (lane < 4 * V + 4), 1.0 - held_ref[...], 0.0)
        tile_ref[0] = jnp.broadcast_to(jnp.sum(ocean), tile_ref.shape[1:])
        tiles[0].start()

    for turn in range(3):

        @pl.when(step == embed_at + 2 + turn)
        def _(turn=turn):
            tiles[turn].wait_recv()
            tile_ref[2 * turn + 2] = tile_ref[2 * turn] + tile_ref[2 * turn + 1]
            for copy in (tiles[1:2], tiles[2:3], level_tiles)[turn]:
                copy.start()

    @pl.when(step == embed_at + 6)
    def _():
        for copy in level_tiles:
            copy.wait_recv()
        count_ref[...] = tile_ref[6] + tile_ref[7] + tile_ref[8] + tile_ref[9]

    @pl.when((step >= embed_at) & (step < embed_at + HEADS // 2))
    def _():
        embed_pair(step - embed_at, held_ref[...], keyed_ref, bias_ref, patch_ref, var_ref, x0_ref)

    @pl.when(step == gather_at - 2)
    def _():
        kept[0].wait()
        weight.start()

    @pl.when(step == gather_at)
    def _():
        x0_ref[...] += lead_rows_of(held_ref[0:1, 4 * V + 4 : 4 * V + 5], lead_ref)
        unit, _ = normed_parts(x0_ref[...])
        h1_ref[...] = (unit * gains_ref[0:1, :] + gains_ref[1:2, :]).astype(bf16)
        weight.wait()

    for number in range(7):

        @pl.when(step == gather_at + number)
        def _(number=number):
            rows.phase(number)
            if number == 6:
                save.start()

    @pl.when((step >= gather_at + 7) & (step < gather_at + 11))
    def _():
        rows.attend(step - gather_at - 7)

    @pl.when(step == total + lag_two - 1)
    def _():
        for copy in given:
            copy.wait()
        for copy in kept[1:]:
            copy.wait()
        for number in range(groups):

            @pl.when(level < 3)
            def _(number=number):
                openings[number][0].wait_send()

            @pl.when(level > 0)
            def _(number=number):
                openings[number][1].wait_send()

        for chunk in chunks:
            for name in ("here_near", "side_near", "down_near", "far_near"):
                chunk[name].wait_recv()
            for name, copy in chunk.items():
                if name != "level":
                    copy.wait_send()

            @pl.when(middle)
            def _(chunk=chunk):
                chunk["level"].wait_send()

        rows.finish()
        for copy in (*tiles, *level_tiles):
            copy.wait_send()
        save.wait()

        @pl.when(dp != level)
        def _():
            crossing.wait_send()


def start_program(packed, prepared, lead_table, norm_gains, shards, halves):
    patch, variable, keyed, bias = prepared
    count = len(shards)
    groups = sum(halves)
    copies = groups * 24 + count + 7
    rows, padded = packed.shape
    total = 8 * rows
    width = shards[0].shape[0] // 3
    heads = width // HEAD_DIM
    anywhere = pl.BlockSpec(memory_space=pl.ANY)
    fixed = lambda shape: pl.BlockSpec(shape, lambda i: (0, 0))
    by_pair = pl.BlockSpec(
        (padded, 2 * HEAD_DIM), lambda i: (0, jnp.clip(i - embed_at, 0, HEADS // 2 - 1))
    )
    shapes = [
        ((rows, D), f32),
        (packed.shape, f32),
        ((total, 3 * width), bf16),
        ((total, width), f32),
        ((heads, total), f32),
        ((8, 128), f32),
    ]
    return pl.pallas_call(
        partial(start_kernel, halves),
        grid=(groups * 3 + lag_two,),
        out_shape=[jax.ShapeDtypeStruct(shape, kind) for shape, kind in shapes]
        + [jax.ShapeDtypeStruct((total, D), bf16), jax.ShapeDtypeStruct((rows, D), bf16)]
        + [jax.ShapeDtypeStruct((8,) + shard.shape, bf16) for shard in shards],
        in_specs=[anywhere]
        + [fixed(keyed.shape), fixed(bias.shape), by_pair, by_pair]
        + [fixed(lead_table.shape), fixed(norm_gains.shape)]
        + [fixed(shard.shape) for shard in shards],
        out_specs=[fixed(shape) for shape, _ in shapes] + [anywhere] * (count + 2),
        scratch_shapes=row_scratch(rows, width)
        + [
            pltpu.VMEM(packed.shape, f32),
            pltpu.VMEM((10, 8, 128), f32),
            pltpu.SemaphoreType.DMA((copies,)),
            pltpu.SemaphoreType.DMA((copies,)),
            pltpu.SemaphoreType.DMA((groups * 5,)),
            pltpu.SemaphoreType.DMA((groups * 4,)),
            pltpu.SemaphoreType.DMA((count + 1,)),
        ],
        compiler_params=pltpu.CompilerParams(
            collective_id=7, has_side_effects=True, vmem_limit_bytes=BIG
        ),
        name="start_program",
    )(packed, keyed, bias, patch, variable, lead_table, norm_gains, *shards)


def shards(
    crossed,
    fields,
    targets,
    land_mask,
    lead_index,
    var_ids,
    tables,
    norm_gains,
    tables_first,
    tables_second,
    gains_first,
    gains_second,
    w_qkv,
    qkv_first,
    qkv_second,
    w_out,
    out_first,
    out_second,
    w_up,
    up_first,
    up_second,
    w_down,
    down_first,
    down_second,
    qkv_average,
):
    local_samples, shard_rows, _ = fields.shape
    dp_size, parts = lax.axis_size("dp"), lax.axis_size("mp")
    dp_index = lax.axis_index("dp")
    place, level, core = mesh_place()
    part = place * 2 + core if crossed else lax.axis_index("mp")
    share_rows = D // dp_size

    def own_share(full, dim):
        return lax.dynamic_slice_in_dim(full, dp_index * share_rows, share_rows, dim)

    var_hot = (var_ids[:, None] == jnp.arange(V, dtype=jnp.int32)[None, :]).astype(f32)
    prepared = prepare_tables(tables, var_hot)
    low = lambda master: master.astype(bf16)
    qkv_low = by_kind(low(w_qkv))
    packed = jnp.concatenate(
        (
            fields[0],
            land_mask[0].astype(f32),
            jnp.broadcast_to(lead_index.astype(f32), (shard_rows, 2)),
            jnp.zeros((shard_rows, 64 - 6), f32),
        ),
        axis=1,
    )
    if crossed:
        (
            x_first, cells, packed, full, logsum, count, rows_one, attended,
            qkv_t, w_outs, w_ups, w_downs
        ) = start_program(
            packed, prepared, tables[5 * V : 5 * V + 8], norm_gains,
            (qkv_low.T, low(w_out), low(w_up), low(w_down)), (1, 1, 2, 2),
        )
        count = count[0, 0]
    else:
        cells = packed
        answers = targets[0]
        count = lax.psum(jnp.sum(1.0 - cells[:, 4 * V : 4 * V + 4]), ("dp", "mp"))
        w_outs, w_ups, w_downs, qkv_t = [
            lax.all_gather(shard, "mp")
            for shard in (low(w_out), low(w_up), low(w_down), qkv_low.T)
        ]
    gathered = (w_outs.reshape(D, D), w_ups, w_downs.reshape(-1, D), qkv_t.reshape(3 * D, D))
    if not crossed:
        qkv_local = choose(qkv_t, part)
    first_cells = cells
    leads = cells[0, 4 * V + 4 : 4 * V + 6].astype(jnp.int32)
    ocean = 1.0 - cells[:, 4 * V : 4 * V + 4]
    denom = 2.0 * V * jnp.maximum(count, 1.0)
    first_row = part * shard_rows
    patch_row = (first_row + jnp.arange(shard_rows, dtype=jnp.int32)) // PATCH_COLS
    row_hot = (patch_row[:, None] == jnp.arange(PATCH_ROWS, dtype=jnp.int32)[None, :]).astype(f32)
    lat_rows = jnp.dot(
        row_hot, lat_weights(2 * PATCH_ROWS).reshape(PATCH_ROWS, 2), precision=highest
    )
    lat_pixels = jnp.broadcast_to(lat_rows[:, :, None], (shard_rows, 2, 2)).reshape(shard_rows, 4)
    weighted = jnp.tile(ocean * lat_pixels, (1, V))
    head = tables[5 * V + LEADS + 1 :]
    loss_part = f32(0.0)
    records = []
    for rollout in range(2):
        if crossed and rollout == 1:
            x_first, cells, packed, full, logsum, rows_one, attended = middle_program(
                guess, first_cells, prepared, tables[5 * V : 5 * V + 8], norm_gains, gathered[3]
            )
        if not crossed:
            if rollout == 1:
                cells = jnp.pad(guess, ((0, 0), (0, 64)))
            lead_row = lax.dynamic_slice_in_dim(tables, 5 * V + leads[rollout], 1, 0)
            x_first, normed = embed_forward(cells, prepared, lead_row, norm_gains)
            rows_one = lax.all_gather(normed, "mp", axis=0, tiled=True)
            packed = lax.dot_general(
                rows_one, qkv_local, NT, preferred_element_type=f32
            ).astype(bf16)
            own_out, full, logsum = attend(packed)
            attended = exchange(own_out, True)
        if crossed and rollout == 0:
            later_targets, attended = tie(targets[0], attended)
            answers = cross(crossed, later_targets)
        x_mid, rows_two, hidden, active, x_last, guess = branch_forward(
            attended, x_first, norm_gains, gathered, head
        )
        miss = guess - answers[rollout]
        loss_part = loss_part + jnp.sum(weighted * miss * miss)
        records.append(
            (cells, x_first, rows_one, packed, full, logsum, attended, x_mid, rows_two,
             hidden, active, x_last, 2.0 * weighted * miss / denom)
        )
    carried = jnp.zeros_like(guess)
    heads, highs = [], []
    lead_hots = (leads[:, None] == jnp.arange(8, dtype=jnp.int32)[None, :]).astype(f32)
    lead_hots = jnp.pad(lead_hots, ((0, 6), (0, 0)))
    query = tables[5 * V + LEADS : 5 * V + LEADS + 1]
    gain_low = jnp.zeros((2, D), f32)
    table_parts, lead_sums = [], []
    qkv_grad = jnp.zeros((D, w_qkv.shape[1]), f32)
    kept = []

    for rollout in (1, 0):
        (cells, x_first, rows_one, packed, full, logsum, attended, x_mid, rows_two,
         hidden, active, x_last, loss_grad) = records[rollout]
        last_low, hidden_grad, mid_grad, mid_low, out_grad, gain_part, head_grad = branch_backward(
            loss_grad + carried, x_last, x_mid, norm_gains, hidden, gathered, head
        )
        heads.append(head_grad)
        highs.append(gain_part)
        if crossed:
            (
                own_grad, act_both, dg_both, o_both, dx2_near, h2_near, dx1_near
            ) = exchange_swap(
                out_grad, active, hidden_grad, attended, last_low, rows_two, mid_low
            )
            kept.append(
                (act_both, dg_both, o_both, last_low, dx2_near, rows_two, h2_near, mid_low, dx1_near)
            )
        else:
            flat = lambda value: value.transpose(2, 1, 0, 3).reshape(shard_rows, -1)
            kept.append((attended, rows_two, flat(active), mid_low, flat(hidden_grad), last_low))
            own_grad = exchange(out_grad, False)
        if crossed and rollout == 0:
            token_grad, level_share, down_sum = finish_program(
                [(step[0], step[3], step[4]) for step in kept],
                packed, own_grad, full, logsum, rows_one, qkv_grad,
            )
        elif crossed:
            token_grad, qkv_grad = attend_exchange(packed, own_grad, full, logsum, rows_one)
        else:
            packed_grad = attend_back(own_grad, packed, full, logsum)
            token_grad = exchange(packed_grad, True)
            qkv_grad = qkv_grad + lax.dot_general(
                rows_one, packed_grad, TN, preferred_element_type=f32
            )
        entry = (token_grad, gathered[3], x_first, mid_grad, norm_gains, cells, prepared)
        if crossed and rollout == 0:
            last_rows, up_out_sum, qkv_share = entry_last(
                [step[1:3] + step[5:] for step in kept], level_share, *entry,
                query, var_hot, lead_hots, heads, highs,
                (*table_parts[0], lead_sums[0], gain_low),
            )
            break
        cells_grad, gain_one, lead_sum, *table_part = entry_backward(*entry)
        carried = cells_grad[:, : 4 * V]
        gain_low = gain_low + gain_one
        table_parts.append(table_part)
        lead_sums.append(lead_sum)

    def pair(index):
        return (kept[0][index], kept[1][index])

    if not crossed:
        lead_rows = jnp.pad(jnp.concatenate((lead_sums[1], lead_sums[0])), ((0, 6), (0, 0)))
        last_rows = table_grads(
            *table_parts, prepared, query, var_hot, lead_hots, lead_rows, gain_low, heads, highs
        )
    if not crossed:
        qkv_share = lax.psum_scatter(qkv_grad, "dp", scatter_dimension=0, tiled=True)
    qkv_share = by_head(qkv_share)
    where = dp_index.astype(jnp.int32).reshape(1)
    if crossed:
        shares = (qkv_share, up_out_sum, down_sum)
        last_sum, tile = exchange_sum(last_rows, loss_part, *shares)
        masters = (w_qkv, w_out, w_up, w_down)
    else:
        shares = (
            qkv_share,
            outer_plain(pair(0), pair(3), False),
            outer_plain(pair(1), pair(4), True),
            outer_plain(pair(2), pair(5), False),
        )
        squares = sum(jnp.sum(share * share) for share in shares)
        last_sum, loss_sum, squares = lax.psum((last_rows, loss_part, squares), ("dp", "mp"))
        squares = squares + jnp.sum(last_sum * last_sum)
        row = jnp.arange(8, dtype=jnp.int32)[:, None]
        tile = jnp.where(row == 0, squares, jnp.where(row == 1, loss_sum, 0.0))
        tile = jnp.broadcast_to(tile, (8, 128))
        masters = (own_share(w_qkv, 0), own_share(w_out, 1), own_share(w_up, 0), own_share(w_down, 1))
    states = (
        (tables, tables_first, tables_second),
        (norm_gains, gains_first, gains_second),
        (masters[0], qkv_first, qkv_second),
        (masters[1], out_first, out_second),
        (masters[2], up_first, up_second),
        (masters[3], down_first, down_second),
    )
    results = update_all(crossed, where, last_sum, tile, count, shares, states, qkv_average)
    return (results[0][0, 0], results[1][0, 0], *results[2:])


def solution(mesh):
    return jax.shard_map(
        partial(shards, is_crossed(mesh.shape)),
        mesh=mesh,
        in_specs=(
            P("dp", "mp", None),
            P("dp", None, "mp", None),
            P("dp", "mp", None),
            P("dp", None),
            P(),
            P(),
            P(),
            P(),
            P(),
            P(),
            P(),
            P(None, "mp"),
            P("dp", "mp"),
            P("dp", "mp"),
            P("mp", None),
            P("mp", "dp"),
            P("mp", "dp"),
            P(None, "mp"),
            P("dp", "mp"),
            P("dp", "mp"),
            P("mp", None),
            P("mp", "dp"),
            P("mp", "dp"),
            P("dp", "mp"),
        ),
        out_specs=(
            P(),
            P(),
            P(),
            P(),
            P(),
            P(),
            P(),
            P(),
            P("dp", "mp"),
            P("dp", "mp"),
            P("dp", "mp"),
            P("mp", "dp"),
            P("mp", "dp"),
            P("mp", "dp"),
            P("dp", "mp"),
            P("dp", "mp"),
            P("dp", "mp"),
            P("mp", "dp"),
            P("mp", "dp"),
            P("mp", "dp"),
            P("dp", "mp"),
        ),
        check_vma=False,
    )
```

```python
from functools import partial
import math

import jax
import jax.numpy as jnp
from jax import lax
from jax.experimental import pallas as pl
from jax.experimental.pallas import tpu as pltpu
from jax.sharding import PartitionSpec as P

D = 1024
HEADS = 16
HEAD_DIM = 64
V = 48
PATCH_ROWS = 32
PATCH_COLS = 64
LEADS = 7


highest = lax.Precision.HIGHEST
eps_norm = 1e-05
clip_norm = 0.05
beta_first = 0.9
beta_second = 0.999
adam_eps = 1e-08
decay_rate = 0.1
lr_matrix = 0.04
lr_table = 0.1
lr_gain = 0.3
average_keep = 0.9
first_fix = 1.0 - 0.9**10
second_fix = 1.0 - 0.999**10


def layer_norm(values, gain, bias):
    center = values - jnp.mean(values, axis=-1, keepdims=True)
    spread = jnp.mean(center * center, axis=-1, keepdims=True)
    return center * lax.rsqrt(spread + eps_norm) * gain + bias


def lat_weights(pixel_rows):
    row_index = jnp.arange(pixel_rows, dtype=jnp.float32)
    cosine = jnp.cos(((row_index + 0.5) / pixel_rows - 0.5) * math.pi)
    return cosine / jnp.mean(cosine)


bf16 = jnp.bfloat16
f32 = jnp.float32
MESH = pl.DeviceIdType.MESH
NT = (((1,), (1,)), ((), ()))
TN = (((0,), (0,)), ((), ()))
VMEM = pl.BlockSpec(memory_space=pltpu.VMEM)
BIG = 56 * 2**20


def is_crossed(sizes):
    return sizes["dp"] == 4 and sizes["mp"] == 8


def mesh_place():
    dp = lax.axis_index("dp")
    mp = lax.axis_index("mp")
    return dp, mp // 2, lax.rem(mp, 2)


def device_of(dp, level, core):
    return {"dp": dp, "mp": level * 2 + core}


def cross_pairs():
    groups = lax.axis_size("dp")
    pairs = []
    for dp in range(groups):
        for level in range(groups):
            for core in range(2):
                source = (dp * groups + level) * 2 + core
                target = (level * groups + dp) * 2 + core
                pairs.append((source, target))
    return pairs


def cross(crossed, value):
    if not crossed:
        return value
    return lax.ppermute(value, ("dp", "mp"), cross_pairs())


def exchange(value, to_columns):
    split, joined = (0, 1) if to_columns else (1, 0)
    return lax.all_to_all(value, "mp", split_axis=split, concat_axis=joined, tiled=True)


def pick_head(value, head, heads):
    if heads == 1:
        return value
    lane = lax.broadcasted_iota(jnp.int32, value.shape, 1) // HEAD_DIM
    return jnp.where(lane == head, value, jnp.zeros_like(value))


def attend_rows(heads, queries, k_ref, vt_ref):
    queries = queries * bf16(HEAD_DIM**-0.5)
    keys = k_ref[...]
    outs, sums = [], []
    for head in range(heads):
        scores = lax.dot_general(
            keys, pick_head(queries, head, heads), NT, preferred_element_type=f32
        )
        largest = jnp.max(scores, axis=0, keepdims=True)
        raised = jnp.exp(scores - largest)
        total = jnp.sum(raised, axis=0, keepdims=True)
        probs = (raised * (1.0 / total)).astype(bf16)
        values = vt_ref[head * HEAD_DIM : (head + 1) * HEAD_DIM, :]
        outs.append(jnp.dot(values, probs, preferred_element_type=f32))
        sums.append(largest + jnp.log(total))
    flipped = outs[0] if heads == 1 else jnp.concatenate(outs, axis=0)
    return flipped.T, sums


def attend_kernel(heads, q_ref, k_ref, v_ref, o_ref, full_ref, lse_ref, vt_ref):
    @pl.when(pl.program_id(0) == 0)
    def _():
        vt_ref[...] = v_ref[...].T

    full, sums = attend_rows(heads, q_ref[...], k_ref, vt_ref)
    for head in range(heads):
        lse_ref[head : head + 1, :] = sums[head]
    full_ref[...] = full
    o_ref[...] = full.astype(bf16)


def attend(packed):
    total, width = packed.shape[0], packed.shape[1] // 3
    heads = width // HEAD_DIM
    block = min(512, total)
    row_block = pl.BlockSpec((block, width), lambda i: (i, 0))
    return pl.pallas_call(
        partial(attend_kernel, heads),
        grid=(total // block,),
        out_shape=(
            jax.ShapeDtypeStruct((total, width), bf16),
            jax.ShapeDtypeStruct((total, width), f32),
            jax.ShapeDtypeStruct((heads, total), f32),
        ),
        in_specs=[
            row_block,
            pl.BlockSpec((total, width), lambda i: (0, 0)),
            pl.BlockSpec((total, width), lambda i: (0, 0)),
        ],
        out_specs=[row_block, row_block, pl.BlockSpec((heads, block), lambda i: (0, i))],
        scratch_shapes=[pltpu.VMEM((width, total), bf16)],
        compiler_params=pltpu.CompilerParams(vmem_limit_bytes=BIG),
        cost_estimate=pl.CostEstimate(
            flops=16 * total * total * width,
            bytes_accessed=10 * total * width,
            transcendentals=heads * total * total,
        ),
        name="attend",
    )(packed[:, :width], packed[:, width : 2 * width], packed[:, 2 * width :])


def attend_back_rows(
    heads, chunk, queries, grads, full, sums, k_ref, v_ref, kt_ref, dk_sum, dv_sum
):
    total = k_ref.shape[0]
    scale = HEAD_DIM**-0.5
    products = (grads.astype(f32) * full).T
    query_heads = [pick_head(queries, head, heads) for head in range(heads)]
    grad_heads = [pick_head(grads, head, heads) for head in range(heads)]
    inner = [
        jnp.sum(products[head * HEAD_DIM : (head + 1) * HEAD_DIM], axis=0, keepdims=True) * scale
        for head in range(heads)
    ]
    query_grads = [None] * heads
    for start in range(0, total, chunk):
        rows = slice(start, start + chunk)
        keys = k_ref[rows, :]
        values = v_ref[rows, :]
        value_part = None
        key_part = None
        for head in range(heads):
            scores = lax.dot_general(
                keys, query_heads[head] * bf16(scale), NT, preferred_element_type=f32
            )
            probs = jnp.exp(scores - sums[head])
            prob_grad = lax.dot_general(
                values, grad_heads[head] * bf16(scale), NT, preferred_element_type=f32
            )
            score_grad = (probs * (prob_grad - inner[head])).astype(bf16)
            one = jnp.dot(probs.astype(bf16), grad_heads[head], preferred_element_type=f32)
            two = jnp.dot(score_grad, query_heads[head], preferred_element_type=f32)
            value_part = one if value_part is None else value_part + one
            key_part = two if key_part is None else key_part + two
            three = jnp.dot(
                kt_ref[head * HEAD_DIM : (head + 1) * HEAD_DIM, rows],
                score_grad,
                preferred_element_type=f32,
            )
            query_grads[head] = three if query_grads[head] is None else query_grads[head] + three
        dv_sum[rows, :] += value_part
        dk_sum[rows, :] += key_part
    flipped = query_grads[0] if heads == 1 else jnp.concatenate(query_grads, axis=0)
    return flipped.T.astype(bf16)


def attend_back_kernel(
    heads, q_ref, do_ref, full_ref, lse_ref, k_ref, v_ref, dq_ref, dk_ref, dv_ref, kt_ref, dk_sum, dv_sum
):
    step = pl.program_id(0)

    @pl.when(step == 0)
    def _():
        kt_ref[...] = k_ref[...].T
        dk_sum[...] = jnp.zeros_like(dk_sum)
        dv_sum[...] = jnp.zeros_like(dv_sum)

    sums = [lse_ref[head : head + 1, :] for head in range(heads)]
    dq_ref[...] = attend_back_rows(
        heads, min(1024, k_ref.shape[0]), q_ref[...], do_ref[...], full_ref[...], sums,
        k_ref, v_ref, kt_ref, dk_sum, dv_sum,
    )

    @pl.when(step == pl.num_programs(0) - 1)
    def _():
        dk_ref[...] = dk_sum[...].astype(bf16)
        dv_ref[...] = dv_sum[...].astype(bf16)


def attend_back(grad_out, packed, full, logsum):
    total, width = grad_out.shape
    heads = width // HEAD_DIM
    block = min(256, total)
    row_block = pl.BlockSpec((block, width), lambda i: (i, 0))
    whole = pl.BlockSpec((total, width), lambda i: (0, 0))
    query_grad, key_grad, value_grad = pl.pallas_call(
        partial(attend_back_kernel, heads),
        grid=(total // block,),
        out_shape=(jax.ShapeDtypeStruct((total, width), bf16),) * 3,
        in_specs=[
            row_block,
            row_block,
            row_block,
            pl.BlockSpec((heads, block), lambda i: (0, i)),
            whole,
            whole,
        ],
        out_specs=[row_block, whole, whole],
        scratch_shapes=[
            pltpu.VMEM((width, total), bf16),
            pltpu.VMEM((total, width), f32),
            pltpu.VMEM((total, width), f32),
        ],
        compiler_params=pltpu.CompilerParams(vmem_limit_bytes=BIG),
        cost_estimate=pl.CostEstimate(
            flops=40 * total * total * width,
            bytes_accessed=16 * total * width,
            transcendentals=heads * total * total,
        ),
        name="attend_back",
    )(
        packed[:, :width],
        grad_out,
        full,
        logsum,
        packed[:, width : 2 * width],
        packed[:, 2 * width :],
    )
    return jnp.concatenate((query_grad, key_grad, value_grad), axis=1)


def normed_parts(values):
    center = values - jnp.mean(values, axis=-1, keepdims=True)
    spread = jnp.mean(center * center, axis=-1, keepdims=True)
    inverse = lax.rsqrt(spread + eps_norm)
    return center * inverse, inverse


def norm_grad(unit, inverse, gain, grad):
    scaled = grad * gain
    middle = jnp.mean(scaled, axis=-1, keepdims=True)
    along = jnp.mean(scaled * unit, axis=-1, keepdims=True)
    gain_grad = jnp.sum(grad * unit, axis=0, keepdims=True)
    bias_grad = jnp.sum(grad, axis=0, keepdims=True)
    return inverse * (scaled - middle - unit * along), gain_grad, bias_grad


def gauss_share(values):
    return 0.5 * (1.0 + lax.erf(values * (0.5**0.5)))


def branch_kernel(
    o_ref, x0_ref, gains_ref, out_ref, up_ref, down_ref, head_ref,
    x1_ref, h2_ref, g_ref, act_ref, x2_ref, pred_ref,
):
    step = pl.program_id(0)

    @pl.when(step == 0)
    def _():
        x1_ref[...] = x0_ref[...] + jnp.dot(
            o_ref[...], out_ref[...], preferred_element_type=f32
        )
        unit, _ = normed_parts(x1_ref[...])
        h2_ref[...] = (unit * gains_ref[2:3, :] + gains_ref[3:4, :]).astype(bf16)
        x2_ref[...] = x1_ref[...]

    units = g_ref.shape[1]
    total = None
    for start in range(0, units, units // 2):
        some = slice(start, start + units // 2)
        hidden = jnp.dot(h2_ref[...], up_ref[0, :, some], preferred_element_type=f32)
        g_ref[:, some] = hidden
        active = (hidden * gauss_share(hidden)).astype(bf16)
        act_ref[0, 0, :, some] = active
        part = jnp.dot(active, down_ref[some, :], preferred_element_type=f32)
        total = part if total is None else total + part
    x2_ref[...] += total

    @pl.when(step == pl.num_programs(0) - 1)
    def _():
        unit, _ = normed_parts(x2_ref[...])
        last = unit * gains_ref[4:5, :] + gains_ref[5:6, :]
        pred_ref[...] = lax.dot_general(
            last, head_ref[5 * V + LEADS + 1 :, :], NT, precision=highest, preferred_element_type=f32
        )


def weight_specs(w_out, w_up, w_down):
    _, width, units = w_up.shape
    return (
        pl.BlockSpec(w_out.shape, lambda i: (0, 0)),
        pl.BlockSpec((1, width, units), lambda i: (i, 0, 0)),
        pl.BlockSpec((units, width), lambda i: (i, 0)),
    )


def branch_forward(attended, x_first, norm_gains, gathered, head):
    w_out, w_up, w_down, _ = gathered
    rows, width = x_first.shape
    parts, units = w_up.shape[0], w_up.shape[2]
    fixed = lambda shape: pl.BlockSpec(shape, lambda i: (0, 0))
    by_units = pl.BlockSpec((rows, units), lambda i: (0, i))
    by_core = pl.BlockSpec((1, 1, rows, units), lambda i: (i % 2, i // 2, 0, 0))
    columns = 4 * V
    flops = 2 * rows * (width * width + 2 * width * parts * units + 6 * width * columns)
    return pl.pallas_call(
        branch_kernel,
        grid=(parts,),
        out_shape=(
            jax.ShapeDtypeStruct((rows, width), f32),
            jax.ShapeDtypeStruct((rows, width), bf16),
            jax.ShapeDtypeStruct((rows, parts * units), f32),
            jax.ShapeDtypeStruct((2, parts // 2, rows, units), bf16),
            jax.ShapeDtypeStruct((rows, width), f32),
            jax.ShapeDtypeStruct((rows, columns), f32),
        ),
        in_specs=[
            fixed((rows, width)),
            fixed((rows, width)),
            fixed(norm_gains.shape),
            *weight_specs(w_out, w_up, w_down),
            fixed(head.shape),
        ],
        out_specs=[
            fixed((rows, width)),
            fixed((rows, width)),
            by_units,
            by_core,
            fixed((rows, width)),
            fixed((rows, columns)),
        ],
        compiler_params=pltpu.CompilerParams(vmem_limit_bytes=BIG),
        cost_estimate=pl.CostEstimate(
            flops=flops,
            bytes_accessed=4 * width * parts * units + 6 * rows * parts * units,
            transcendentals=rows * parts * units,
        ),
        name="branch_forward",
    )(attended, x_first, norm_gains, w_out, w_up, w_down, head)


def branch_back_kernel(
    dpred_ref, x2_ref, x1_ref, gains_ref, g_ref, out_ref, up_ref, down_ref, head_ref,
    dx2_ref, dg_ref, dx1_ref, low_ref, do_ref, gain_ref, dhead_ref,
    wide_ref, sum_ref,
):
    step = pl.program_id(0)

    @pl.when(step == 0)
    def _():
        grad = dpred_ref[...]
        unit, inverse = normed_parts(x2_ref[...])
        gain = gains_ref[4:5, :]
        last = unit * gain + gains_ref[5:6, :]
        dhead_ref[...] = lax.dot_general(
            grad, last, TN, precision=highest, preferred_element_type=f32
        )
        row_grad = jnp.dot(grad, head_ref[5 * V + LEADS + 1 :, :], precision=highest, preferred_element_type=f32)
        wide, gain_grad, bias_grad = norm_grad(unit, inverse, gain, row_grad)
        gain_ref[...] = jnp.zeros_like(gain_ref)
        gain_ref[4:5, :] = gain_grad
        gain_ref[5:6, :] = bias_grad
        wide_ref[...] = wide
        dx2_ref[...] = wide.astype(bf16)
        sum_ref[...] = jnp.zeros_like(sum_ref)

    units = g_ref.shape[1]
    total = None
    for start in range(0, units, units // 2):
        some = slice(start, start + units // 2)
        active_grad = lax.dot_general(
            dx2_ref[...], down_ref[some, :], NT, preferred_element_type=f32
        )
        hidden = g_ref[:, some]
        slope = gauss_share(hidden) + hidden * (
            jnp.exp(-0.5 * hidden * hidden) * (2.0 * math.pi) ** -0.5
        )
        hidden_grad = (active_grad * slope).astype(bf16)
        dg_ref[0, 0, :, some] = hidden_grad
        part = lax.dot_general(hidden_grad, up_ref[0, :, some], NT, preferred_element_type=f32)
        total = part if total is None else total + part
    sum_ref[...] += total

    @pl.when(step == pl.num_programs(0) - 1)
    def _():
        unit, inverse = normed_parts(x1_ref[...])
        middle, gain_grad, bias_grad = norm_grad(unit, inverse, gains_ref[2:3, :], sum_ref[...])
        gain_ref[2:3, :] = gain_grad
        gain_ref[3:4, :] = bias_grad
        middle = wide_ref[...] + middle
        dx1_ref[...] = middle
        low_ref[...] = middle.astype(bf16)
        total = lax.dot_general(low_ref[...], out_ref[...], NT, preferred_element_type=f32)
        do_ref[...] = total.astype(bf16)


def branch_backward(pred_grad, x_last, x_mid, norm_gains, hidden, gathered, head):
    w_out, w_up, w_down, _ = gathered
    rows, width = x_last.shape
    parts, units = w_up.shape[0], w_up.shape[2]
    fixed = lambda shape: pl.BlockSpec(shape, lambda i: (0, 0))
    by_units = pl.BlockSpec((rows, units), lambda i: (0, i))
    by_core = pl.BlockSpec((1, 1, rows, units), lambda i: (i % 2, i // 2, 0, 0))
    columns = 4 * V
    wide = (rows, width)
    flops = 2 * rows * (width * width + 2 * width * parts * units + 12 * width * columns)
    return pl.pallas_call(
        branch_back_kernel,
        grid=(parts,),
        out_shape=(
            jax.ShapeDtypeStruct(wide, bf16),
            jax.ShapeDtypeStruct((2, parts // 2, rows, units), bf16),
            jax.ShapeDtypeStruct(wide, f32),
            jax.ShapeDtypeStruct(wide, bf16),
            jax.ShapeDtypeStruct(wide, bf16),
            jax.ShapeDtypeStruct((6, width), f32),
            jax.ShapeDtypeStruct((columns, width), f32),
        ),
        in_specs=[
            fixed((rows, columns)),
            fixed(wide),
            fixed(wide),
            fixed(norm_gains.shape),
            by_units,
            *weight_specs(w_out, w_up, w_down),
            fixed(head.shape),
        ],
        out_specs=[
            fixed(wide),
            by_core,
            fixed(wide),
            fixed(wide),
            fixed(wide),
            fixed((6, width)),
            fixed((columns, width)),
        ],
        scratch_shapes=[pltpu.VMEM(wide, f32), pltpu.VMEM(wide, f32)],
        compiler_params=pltpu.CompilerParams(vmem_limit_bytes=BIG),
        cost_estimate=pl.CostEstimate(
            flops=flops,
            bytes_accessed=4 * width * parts * units + 6 * rows * parts * units,
            transcendentals=2 * rows * parts * units,
        ),
        name="branch_backward",
    )(pred_grad, x_last, x_mid, norm_gains, hidden, w_out, w_up, w_down, head)


def plane_parts(me):
    return [(move, lax.rem(me + move, 8)) for move in (7, 6, 5, 4, 3, 2, 1)]


def swap_kernel(*refs):
    value_ref, act_ref, dg_ref, o_ref, dx2_ref, h2_ref, dx1_ref = refs[:7]
    rows_ref, act_out, dg_out, o_out, dx2_out, h2_out, dx1_out = refs[7:14]
    send_sem, recv_sem, own_sem = refs[14:]
    dp, level, core = mesh_place()
    me = dp * 2 + core
    rows, width = value_ref.shape[0], value_ref.shape[1] // 8
    near = device_of(dp, level, 1 - core)
    barrier = pltpu.get_barrier_semaphore()
    others = [
        (part, device_of(part // 2, level, lax.rem(part, 2))) for _, part in plane_parts(me)
    ]
    for _, target in others:
        pl.semaphore_signal(barrier, inc=1, device_id=target, device_id_type=MESH)
    pl.semaphore_wait(barrier, 7)
    started = []

    def send(source, target_ref, target):
        slot = len(started)
        copy = pltpu.make_async_remote_copy(
            src_ref=source,
            dst_ref=target_ref,
            send_sem=send_sem.at[slot],
            recv_sem=recv_sem.at[slot],
            device_id=target,
            device_id_type=MESH,
        )
        copy.start()
        started.append(copy)

    def row_block(part):
        return rows_ref.at[pl.ds(pl.multiple_of(part * rows, rows), rows), :]

    def column_block(ref, part):
        return ref.at[:, pl.ds(pl.multiple_of(part * width, width), width)]

    for part, target in others:
        send(column_block(value_ref, part), row_block(me), target)
    locals_ = []

    def keep(source, target_ref):
        copy = pltpu.make_async_copy(source, target_ref, own_sem.at[len(locals_)])
        copy.start()
        locals_.append(copy)

    for source, out in ((act_ref, act_out), (dg_ref, dg_out)):
        send(source.at[1 - core], out.at[1], near)
        keep(source.at[core], out.at[0])
    for index in range(4):
        send(column_block(o_ref, index * 2 + 1 - core), o_out.at[1, index], near)
        keep(column_block(o_ref, index * 2 + core), o_out.at[0, index])
    for source, out in ((dx2_ref, dx2_out), (h2_ref, h2_out), (dx1_ref, dx1_out)):
        send(source, out, near)
    row_block(me)[...] = column_block(value_ref, me)[...]
    for copy in started:
        copy.wait()
    for copy in locals_:
        copy.wait()


def exchange_swap(value, act, dg, attended, dx2, h2, dx1):
    rows, width = value.shape
    anywhere = pl.BlockSpec(memory_space=pl.ANY)
    outs = [
        (8 * rows, width // 8), act.shape, dg.shape, (2, 4, rows, width // 8),
        dx2.shape, h2.shape, dx1.shape,
    ]
    return pl.pallas_call(
        swap_kernel,
        out_shape=[jax.ShapeDtypeStruct(shape, bf16) for shape in outs],
        in_specs=[VMEM] * 7,
        out_specs=[VMEM] + [anywhere] * 6,
        scratch_shapes=[
            pltpu.SemaphoreType.DMA((16,)),
            pltpu.SemaphoreType.DMA((16,)),
            pltpu.SemaphoreType.DMA((6,)),
        ],
        compiler_params=pltpu.CompilerParams(
            collective_id=3, has_side_effects=True, vmem_limit_bytes=BIG
        ),
        name="exchange_swap",
    )(value, act, dg, attended, dx2, h2, dx1)


class Scatter:
    order = (0, 3, 1, 2)

    def __init__(self, refs, sems):
        self.send_ref, self.keep_ref, self.one_ref, self.two_ref, self.own_ref, self.deep_ref = refs
        self.one, self.two, self.deep = sems
        self.dp, self.level, self.core = mesh_place()
        self.x, self.y = lax.rem(self.dp, 2), self.dp // 2
        self.side = device_of(self.dp + 1 - 2 * self.x, self.level, self.core)
        self.down = device_of(lax.rem(self.dp + 2, 4), self.level, self.core)

    def copy(self, source, target_ref, sems, slot, place, target):
        return pltpu.make_async_remote_copy(
            src_ref=source,
            dst_ref=target_ref,
            send_sem=sems.at[0, slot],
            recv_sem=sems.at[1, place],
            device_id=target,
            device_id_type=MESH,
        )

    def first(self, depth):
        target = self.side if depth < 2 else self.down
        return self.copy(
            self.send_ref.at[depth], self.one_ref.at[depth], self.one, depth, depth, target
        )

    def second(self, depth):
        target = self.down if depth < 2 else self.side
        which = 1 - self.y if depth < 2 else 1 - self.x
        return self.copy(
            self.keep_ref.at[depth, which], self.two_ref.at[depth], self.two, depth, depth, target
        )

    def mine(self, depth):
        return self.y if depth < 2 else self.x

    def third(self, depth):
        place = lax.rem(self.level + 7 - depth, 4)
        return self.copy(
            self.keep_ref.at[depth, self.mine(depth)], self.deep_ref.at[place], self.deep, depth,
            place, device_of(self.dp, depth, self.core),
        )

    def begin(self, depth, products, held_ref):
        height = self.keep_ref.shape[2]
        top = 0
        for product in products:
            rows, size = product.shape[0], product.shape[1] // 4
            for split in range(4):
                held_ref[split, top : top + rows, :] = product[
                    :, split * size : (split + 1) * size
                ].astype(bf16)
            top += rows
        for which in range(2):
            if depth < 2:
                moved, stays = which * 2 + 1 - self.x, which * 2 + self.x
            else:
                moved, stays = (1 - self.y) * 2 + which, self.y * 2 + which
            self.send_ref[depth, which] = held_ref[moved, :height, :]
            self.keep_ref[depth, which] = held_ref[stays, :height, :]
        self.first(depth).start()

    def middle(self, depth):
        self.first(depth).wait_recv()
        for which in range(2):
            self.keep_ref[depth, which] = (
                self.keep_ref[depth, which].astype(f32) + self.one_ref[depth, which].astype(f32)
            ).astype(bf16)
        self.second(depth).start()

    def end(self, depth):
        self.second(depth).wait_recv()
        total = self.keep_ref[depth, self.mine(depth)].astype(f32) + self.two_ref[depth].astype(f32)

        @pl.when(self.level == depth)
        def _():
            self.own_ref[...] = total

        @pl.when(self.level != depth)
        def _():
            self.keep_ref[depth, self.mine(depth)] = total.astype(bf16)
            self.third(depth).start()

    def finish(self, result_ref):
        for place in range(3):
            self.copy(
                self.keep_ref.at[0, 0], self.deep_ref.at[place], self.deep, 0, place, self.side
            ).wait_recv()
        result_ref[...] = self.own_ref[...] + (
            self.deep_ref[0].astype(f32) + self.deep_ref[1].astype(f32) + self.deep_ref[2].astype(f32)
        )
        for depth in range(4):
            self.first(depth).wait_send()
            self.second(depth).wait_send()

            @pl.when(self.level != depth)
            def _(depth=depth):
                self.third(depth).wait_send()


def scatter_scratch(height, share):
    return [
        pltpu.VMEM((4, 2, height, share), bf16),
        pltpu.VMEM((4, 2, height, share), bf16),
        pltpu.VMEM((4, 2, height, share), bf16),
        pltpu.VMEM((4, height, share), bf16),
        pltpu.VMEM((height, share), f32),
        pltpu.VMEM((3, height, share), bf16),
        pltpu.VMEM((4, height, share), bf16),
        pltpu.SemaphoreType.DMA((2, 4)),
        pltpu.SemaphoreType.DMA((2, 4)),
        pltpu.SemaphoreType.DMA((2, 4)),
    ]


def summed(lefts, rights):
    total = None
    for left, right in zip(lefts, rights):
        part = lax.dot_general(left, right, TN, preferred_element_type=f32)
        total = part if total is None else total + part
    return total


def chunk_spec(shape):
    def where(i):
        index = jnp.minimum(i, 3)
        first, last = (3 - index) // 3, index // 3
        middle = 1 - first - last
        return 0, middle * (5 - 2 * index) + 2 * last, 0, 0

    return pl.BlockSpec((2, 1) + shape, where)


def once(shape):
    return pl.BlockSpec(shape, lambda i: (0,) * len(shape), pipeline_mode=pl.Buffered(1))


class Returns:
    def __init__(self, grads_ref, token_out, width, sems, own_sem):
        self.grads_ref, self.token_out, self.width = grads_ref, token_out, width
        self.sems, self.own_sem = sems, own_sem
        dp, self.level, core = mesh_place()
        self.me = dp * 2 + core
        self.rows = grads_ref.shape[0] // 8

    def part(self, move):
        return lax.rem(self.me + move, 8)

    def refs(self, part, start, size):
        rows = pl.ds(pl.multiple_of(part * self.rows, self.rows), self.rows)
        first = self.me * 3 * self.width + start
        columns = pl.ds(pl.multiple_of(first, self.width), size)
        return self.grads_ref.at[rows, start : start + size], self.token_out.at[:, columns]

    def copy(self, move, late):
        start, size = (self.width, 2 * self.width) if late else (0, self.width)
        part = self.part(move)
        source, target_ref = self.refs(part, start, size)
        return pltpu.make_async_remote_copy(
            src_ref=source,
            dst_ref=target_ref,
            send_sem=self.sems.at[2 * late, move],
            recv_sem=self.sems.at[2 * late + 1, move],
            device_id=device_of(part // 2, self.level, lax.rem(part, 2)),
            device_id_type=MESH,
        )

    def own(self):
        source, target_ref = self.refs(self.me, 0, 3 * self.width)
        return pltpu.make_async_copy(source, target_ref, self.own_sem)

    def peers(self):
        parts = [self.part(move) for move in range(1, 8)]
        return [device_of(part // 2, self.level, lax.rem(part, 2)) for part in parts]

    def finish(self):
        for move in range(1, 8):
            self.copy(move, 0).wait()
            self.copy(move, 1).wait()
        self.own().wait()


def attend_turns(turn, returns, qkv_ref, do_ref, full_ref, lse_ref, dqkv_ref, kt_ref, dk_sum, dv_sum):
    width = do_ref.shape[1]
    heads = width // HEAD_DIM
    rows = returns.rows

    @pl.when(turn == 0)
    def _():
        kt_ref[...] = qkv_ref[:, width : 2 * width].T
        dk_sum[...] = jnp.zeros_like(dk_sum)
        dv_sum[...] = jnp.zeros_like(dv_sum)

    @pl.when((turn >= 0) & (turn < 8))
    def _():
        part = returns.part(turn + 1)
        where = pl.ds(pl.multiple_of(part * rows, rows), rows)
        sums = [lse_ref[head : head + 1, where] for head in range(heads)]
        dqkv_ref[where, :width] = attend_back_rows(
            heads, 1024, qkv_ref[where, :width], do_ref[where, :], full_ref[where, :], sums,
            qkv_ref.at[:, width : 2 * width], qkv_ref.at[:, 2 * width :], kt_ref, dk_sum, dv_sum,
        )

    @pl.when((turn >= 0) & (turn < 7))
    def _():
        returns.copy(turn + 1, 0).start()

    @pl.when(turn == 8)
    def _():
        dqkv_ref[:, width : 2 * width] = dk_sum[...].astype(bf16)
        dqkv_ref[:, 2 * width :] = dv_sum[...].astype(bf16)
        for move in (7, 6, 5, 4, 3, 2, 1):
            returns.copy(move, 1).start()
        returns.own().start()


def attend_exchange_kernel(
    qkv_ref, do_ref, full_ref, lse_ref, rows_ref, token_out, grad_ref,
    dqkv_ref, kt_ref, dk_sum, dv_sum, sems, own_sem,
):
    turn = pl.program_id(0)
    returns = Returns(dqkv_ref, token_out, do_ref.shape[1], sems, own_sem)

    @pl.when(turn == 0)
    def _():
        barrier = pltpu.get_barrier_semaphore()
        for target in returns.peers():
            pl.semaphore_signal(barrier, inc=1, device_id=target, device_id_type=MESH)
        pl.semaphore_wait(barrier, 7)

    attend_turns(
        turn, returns, qkv_ref, do_ref, full_ref, lse_ref, dqkv_ref, kt_ref, dk_sum, dv_sum
    )

    @pl.when(turn >= pieces_at)
    def _():
        grad_ref[...] = lax.dot_general(
            rows_ref[...], dqkv_ref[...], TN, preferred_element_type=f32
        )

    @pl.when(turn == pieces_at + 3)
    def _():
        returns.finish()


def attend_exchange(packed, own_grad, full, logsum, rows_one):
    rows, width = own_grad.shape[0] // 8, own_grad.shape[1]
    piece = lambda i: jnp.clip(i - pieces_at, 0, 3)
    return pl.pallas_call(
        attend_exchange_kernel,
        grid=(pieces_at + 4,),
        out_shape=[
            jax.ShapeDtypeStruct((rows, 24 * width), bf16),
            jax.ShapeDtypeStruct((D, 3 * width), f32),
        ],
        in_specs=[
            once(packed.shape),
            once(own_grad.shape),
            once(full.shape),
            once(logsum.shape),
            pl.BlockSpec((8 * rows, D // 4), lambda i: (0, piece(i))),
        ],
        out_specs=[
            pl.BlockSpec(memory_space=pl.ANY),
            pl.BlockSpec((D // 4, 3 * width), lambda i: (piece(i), 0)),
        ],
        scratch_shapes=[
            pltpu.VMEM((8 * rows, 3 * width), bf16),
            pltpu.VMEM((width, 8 * rows), bf16),
            pltpu.VMEM((8 * rows, width), f32),
            pltpu.VMEM((8 * rows, width), f32),
            pltpu.SemaphoreType.DMA((4, 8)),
            pltpu.SemaphoreType.DMA,
        ],
        compiler_params=pltpu.CompilerParams(
            collective_id=8, has_side_effects=True, vmem_limit_bytes=BIG
        ),
        name="attend_exchange",
    )(packed, own_grad, full, logsum, rows_one)


pieces_at, entry_turns, attend_from = 9, 15, 4
middle_at, end_at = (5, 6, 8, 9), (7, 8, 10, 11)
entry_middle_at, entry_end_at = (5, 6, 9, 10), (10, 11, 12, 13)


def finish_kernel(*refs):
    steps = (refs[0:3], refs[3:6])
    qkv_ref, do_ref, full_ref, lse_ref, rows_ref, prev_ref = refs[6:12]
    token_out, share_ref, down_ref = refs[12:15]
    dqkv_ref, kt_ref, dk_sum, dv_sum, piece_send, piece_recv, piece_own = refs[15:22]
    part_sem, piece_sem, own_sem = refs[22:25]
    scatter = Scatter(refs[25:31], refs[32:35])
    held_ref = refs[31]
    turn = pl.program_id(0)
    dp, level, core = mesh_place()
    width = do_ref.shape[1]
    returns = Returns(dqkv_ref, token_out, width, part_sem, own_sem)

    def remote(source, target_ref, send_sem, recv_sem, target):
        return pltpu.make_async_remote_copy(
            src_ref=source,
            dst_ref=target_ref,
            send_sem=send_sem,
            recv_sem=recv_sem,
            device_id=target,
            device_id_type=MESH,
        )

    def piece_copy(index):
        place = lax.rem(level + 7 - index, 4)
        return remote(
            piece_send.at[index], piece_recv.at[place], piece_sem.at[0, index],
            piece_sem.at[1, place], device_of(dp, index, core),
        )

    @pl.when(turn == 0)
    def _():
        barrier = pltpu.get_barrier_semaphore()
        deep = [device_of(dp, lax.rem(level + move, 4), core) for move in (1, 2, 3)]
        for target in returns.peers() + deep:
            pl.semaphore_signal(barrier, inc=1, device_id=target, device_id_type=MESH)
        pl.semaphore_wait(barrier, 10)

    for index, depth in enumerate(scatter.order):

        @pl.when(turn == index)
        def _(depth=depth):
            lefts, rights = [], []
            for act, dx2, dx2_near in steps:
                lefts += [act[0, 0], act[1, 0]]
                rights += [dx2[...], dx2_near[...]]
            scatter.begin(depth, [summed(lefts, rights)], held_ref)

        @pl.when(turn == middle_at[index])
        def _(depth=depth):
            scatter.middle(depth)

        @pl.when(turn == end_at[index])
        def _(depth=depth):
            scatter.end(depth)

    attend_turns(
        turn - attend_from, returns, qkv_ref, do_ref, full_ref, lse_ref, dqkv_ref, kt_ref, dk_sum, dv_sum
    )

    for index in range(4):

        @pl.when(turn == attend_from + pieces_at + index)
        def _(index=index):
            piece = prev_ref[...] + lax.dot_general(
                rows_ref[...], dqkv_ref[...], TN, preferred_element_type=f32
            )

            @pl.when(level == index)
            def _():
                piece_own[...] = piece

            @pl.when(level != index)
            def _():
                piece_send[index] = piece.astype(bf16)
                piece_copy(index).start()

    @pl.when(turn == attend_from + pieces_at + 4)
    def _():
        scatter.finish(down_ref)
        for place in range(3):
            remote(
                piece_send.at[0], piece_recv.at[place], piece_sem.at[0, 0],
                piece_sem.at[1, place], scatter.side,
            ).wait_recv()
        share_ref[...] = piece_own[...] + (
            piece_recv[0].astype(f32) + piece_recv[1].astype(f32) + piece_recv[2].astype(f32)
        )
        returns.finish()
        for index in range(4):

            @pl.when(level != index)
            def _(index=index):
                piece_copy(index).wait_send()


def finish_program(kept, packed, own_grad, full, logsum, rows_one, earlier):
    rows, width = own_grad.shape[0] // 8, own_grad.shape[1]
    in_specs, operands = [], []
    for act, dx2, dx2_near in kept:
        operands += [act, dx2, dx2_near]
        in_specs += [chunk_spec(act.shape[2:]), once(dx2.shape), once(dx2.shape)]
    piece = lambda i: jnp.clip(i - attend_from - pieces_at, 0, 3)
    in_specs += [
        once(packed.shape),
        once(own_grad.shape),
        once(full.shape),
        once(logsum.shape),
        pl.BlockSpec((8 * rows, D // 4), lambda i: (0, piece(i))),
        pl.BlockSpec((D // 4, 3 * width), lambda i: (piece(i), 0)),
    ]
    operands += [packed, own_grad, full, logsum, rows_one, earlier]
    fixed = lambda shape: pl.BlockSpec(shape, lambda i: (0, 0))
    units = kept[0][0].shape[3]
    share = D // 4
    return pl.pallas_call(
        finish_kernel,
        grid=(attend_from + pieces_at + 5,),
        out_shape=[
            jax.ShapeDtypeStruct((rows, 24 * width), bf16),
            jax.ShapeDtypeStruct((share, 3 * width), f32),
            jax.ShapeDtypeStruct((units, share), f32),
        ],
        in_specs=in_specs,
        out_specs=[
            pl.BlockSpec(memory_space=pl.ANY),
            fixed((share, 3 * width)),
            fixed((units, share)),
        ],
        scratch_shapes=[
            pltpu.VMEM((8 * rows, 3 * width), bf16),
            pltpu.VMEM((width, 8 * rows), bf16),
            pltpu.VMEM((8 * rows, width), f32),
            pltpu.VMEM((8 * rows, width), f32),
            pltpu.VMEM((4, share, 3 * width), bf16),
            pltpu.VMEM((3, share, 3 * width), bf16),
            pltpu.VMEM((share, 3 * width), f32),
            pltpu.SemaphoreType.DMA((4, 8)),
            pltpu.SemaphoreType.DMA((2, 4)),
            pltpu.SemaphoreType.DMA,
        ]
        + scatter_scratch(units, share),
        compiler_params=pltpu.CompilerParams(
            collective_id=4, has_side_effects=True, vmem_limit_bytes=BIG
        ),
        name="finish_program",
    )(*operands)


def tie(*values):
    return lax.optimization_barrier(values)


def choose(value, index, axis=0):
    return lax.dynamic_index_in_dim(value, index, axis, keepdims=False)


def outer_plain(lefts, rights, by_rows):
    dp, mp = lax.axis_size("dp"), lax.axis_size("mp")
    grads = sum(
        lax.dot_general(left, right, TN, preferred_element_type=f32)
        for left, right in zip(lefts, rights)
    ).astype(bf16)
    rows, width = grads.shape
    if by_rows:
        grads = grads.reshape(dp, rows // dp, mp, width // mp).transpose(0, 2, 1, 3)
    else:
        grads = grads.reshape(mp, rows // mp, dp, width // dp).transpose(2, 0, 1, 3)
    grads = grads.reshape((dp * mp,) + grads.shape[2:])
    return lax.psum_scatter(grads, ("dp", "mp"), scatter_dimension=0, tiled=False).astype(f32)


def exchange_sum_kernel(
    x_ref, loss_ref, qkv_ref, up_out_ref, down_ref, o_ref, s_ref, work_ref, pair_ref, quad_ref, eight_ref, deep_ref, tile_ref,
    send_sem, recv_sem,
):
    dp, level, core = mesh_place()
    x, y = lax.rem(dp, 2), dp // 2
    side = device_of(dp + 1 - 2 * x, level, core)
    down = device_of(lax.rem(dp + 2, 4), level, core)
    near = device_of(dp, level, 1 - core)
    deep = [device_of(dp, lax.rem(level + step, 4), core) for step in (1, 2, 3)]
    barrier = pltpu.get_barrier_semaphore()
    for target in (side, down, near, *deep):
        pl.semaphore_signal(barrier, inc=1, device_id=target, device_id_type=MESH)
    pl.semaphore_wait(barrier, 6)
    started = []

    def send(source, target_ref, target):
        slot = len(started)
        copy = pltpu.make_async_remote_copy(
            src_ref=source,
            dst_ref=target_ref,
            send_sem=send_sem.at[slot],
            recv_sem=recv_sem.at[slot],
            device_id=target,
            device_id_type=MESH,
        )
        copy.start()
        started.append(copy)
        return copy

    half = x_ref.shape[0] // 2
    quarter, eighth, part, unit = half // 2, half // 4, half // 8, half // 16

    def rows(start, size):
        return pl.ds(pl.multiple_of(start, unit), size)

    copy = send(x_ref.at[rows((1 - core) * half, half)], pair_ref, near)
    copy.wait_recv()
    work_ref[...] = x_ref[rows(core * half, half)] + pair_ref[...]
    one = send(work_ref.at[rows((1 - x) * eighth, eighth)], quad_ref.at[0], side)
    two = send(work_ref.at[rows(quarter + (1 - y) * eighth, eighth)], quad_ref.at[1], down)
    base_a = x * eighth
    base_b = quarter + y * eighth
    wide_a, wide_b = core * half + base_a, core * half + base_b
    one.wait_recv()
    work_ref[rows(base_a, eighth)] += quad_ref[0]
    one = send(work_ref.at[rows(base_a + (1 - y) * part, part)], eight_ref.at[0], down)
    two.wait_recv()
    work_ref[rows(base_b, eighth)] += quad_ref[1]
    two = send(work_ref.at[rows(base_b + (1 - x) * part, part)], eight_ref.at[1], side)
    base_a = base_a + y * part
    base_b = base_b + x * part
    one.wait_recv()
    work_ref[rows(base_a, part)] += eight_ref[0]
    two.wait_recv()
    work_ref[rows(base_b, part)] += eight_ref[1]

    def level_start(which):
        late = which // 2
        return (1 - late) * base_a + late * base_b + lax.rem(which, 2) * unit

    copies = []
    for step in (1, 2, 3):
        source = work_ref.at[rows(level_start(lax.rem(level + step, 4)), unit)]
        copies.append(send(source, deep_ref.at[step - 1], deep[step - 1]))
    for copy in copies:
        copy.wait_recv()
    total = work_ref[rows(level_start(level), unit)] + deep_ref[0] + deep_ref[1] + deep_ref[2]
    mine = rows(core * half + level_start(level), unit)
    base_a = core * half + base_a
    base_b = core * half + base_b
    o_ref[mine] = total
    row = lax.broadcasted_iota(jnp.int32, s_ref.shape, 0)
    squares = jnp.sum(total * total)
    for ref in (qkv_ref, up_out_ref, down_ref):
        squares += jnp.sum(ref[...] * ref[...])
    tile_ref[0] = jnp.where(row == 0, squares, jnp.where(row == 1, loss_ref[...], 0.0))
    copies = []
    for step in (1, 2, 3):
        copies.append(send(o_ref.at[mine], o_ref.at[mine], deep[step - 1]))
        copies.append(send(tile_ref.at[0], tile_ref.at[step], deep[step - 1]))
    for copy in copies:
        copy.wait_recv()
    one = send(o_ref.at[rows(base_a, part)], o_ref.at[rows(base_a, part)], down)
    two = send(o_ref.at[rows(base_b, part)], o_ref.at[rows(base_b, part)], side)
    tile_ref[4] = tile_ref[0] + tile_ref[1] + tile_ref[2] + tile_ref[3]
    three = send(tile_ref.at[4], tile_ref.at[5], side)
    one.wait_recv()
    one = send(o_ref.at[rows(wide_a, eighth)], o_ref.at[rows(wide_a, eighth)], side)
    two.wait_recv()
    two = send(o_ref.at[rows(wide_b, eighth)], o_ref.at[rows(wide_b, eighth)], down)
    three.wait_recv()
    tile_ref[6] = tile_ref[4] + tile_ref[5]
    three = send(tile_ref.at[6], tile_ref.at[7], down)
    one.wait_recv()
    two.wait_recv()
    one = send(o_ref.at[rows(core * half, half)], o_ref.at[rows(core * half, half)], near)
    three.wait_recv()
    tile_ref[8] = tile_ref[6] + tile_ref[7]
    three = send(tile_ref.at[8], tile_ref.at[9], near)
    one.wait_recv()
    three.wait_recv()
    s_ref[...] = tile_ref[8] + tile_ref[9]
    for copy in started:
        copy.wait_send()


def exchange_sum(value, loss, *shares):
    rows, width = value.shape
    tile = jax.ShapeDtypeStruct((8, 128), f32)
    return pl.pallas_call(
        exchange_sum_kernel,
        out_shape=(jax.ShapeDtypeStruct(value.shape, f32), tile),
        in_specs=[VMEM] * 5,
        out_specs=[VMEM, VMEM],
        scratch_shapes=[
            pltpu.VMEM((rows // 2, width), f32),
            pltpu.VMEM((rows // 2, width), f32),
            pltpu.VMEM((2, rows // 8, width), f32),
            pltpu.VMEM((2, rows // 16, width), f32),
            pltpu.VMEM((3, rows // 32, width), f32),
            pltpu.VMEM((10,) + tile.shape, f32),
            pltpu.SemaphoreType.DMA((24,)),
            pltpu.SemaphoreType.DMA((24,)),
        ],
        compiler_params=pltpu.CompilerParams(
            collective_id=5, has_side_effects=True, vmem_limit_bytes=BIG
        ),
        name="exchange_sum",
    )(value, loss.reshape(1, 1), *shares)


def split_low(values):
    high = values.astype(bf16)
    return high, (values - high.astype(f32)).astype(bf16)


def three_products(left, right, dims=(((1,), (0,)), ((), ()))):
    def product(one, two):
        return lax.dot_general(one, two, dims, preferred_element_type=f32)

    return product(left[0], right[0]) + (product(left[1], right[0]) + product(left[0], right[1]))


def exact_product(left, right, dims=(((1,), (0,)), ((), ()))):
    return lax.dot_general(left, right, dims, precision=highest, preferred_element_type=f32)


def head_marks(width):
    head = lax.broadcasted_iota(jnp.int32, (HEADS, width), 0)
    column = lax.broadcasted_iota(jnp.int32, (HEADS, width), 1)
    return jnp.where(column // HEAD_DIM == head, 1.0, 0.0).astype(f32)


def quarter_marks(padded):
    row = lax.broadcasted_iota(jnp.int32, (padded, V), 0)
    column = lax.broadcasted_iota(jnp.int32, (padded, V), 1)
    return jnp.where(row // 4 == column, 0.25, 0.0).astype(f32)


def tables_kernel(tables_ref, hot_ref, patch_ref, var_ref, keyed_ref, bias_ref):
    padded, width = patch_ref.shape
    query = tables_ref[5 * V + LEADS : 5 * V + LEADS + 1, :]
    patch_ref[...] = jnp.zeros_like(patch_ref)
    patch_ref[: 4 * V, :] = tables_ref[: 4 * V, :]
    chosen = exact_product(hot_ref[...], tables_ref[4 * V : 5 * V, :])
    var_ref[...] = exact_product(quarter_marks(padded), chosen)
    marks = head_marks(width)
    scale = HEAD_DIM**-0.5
    keyed_ref[...] = exact_product(marks, patch_ref[...] * query, NT) * scale
    bias = exact_product(marks, var_ref[...] * query, NT) * (4.0 * scale)
    column = lax.broadcasted_iota(jnp.int32, bias.shape, 1)
    bias_ref[...] = jnp.where(column < 4 * V, bias, -1e30)


def prepare_tables(tables, var_hot):
    padded = 256
    return pl.pallas_call(
        tables_kernel,
        out_shape=(
            jax.ShapeDtypeStruct((padded, D), f32),
            jax.ShapeDtypeStruct((padded, D), f32),
            jax.ShapeDtypeStruct((HEADS, padded), f32),
            jax.ShapeDtypeStruct((HEADS, padded), f32),
        ),
        compiler_params=pltpu.CompilerParams(vmem_limit_bytes=BIG),
        name="prepare_tables",
    )(tables, var_hot)


def four_sum(values):
    size = values.shape[1]
    lane = lax.broadcasted_iota(jnp.int32, values.shape, 1)
    values = values + jnp.where(
        lane % 2 == 0, pltpu.roll(values, size - 1, 1), pltpu.roll(values, 1, 1)
    )
    return values + jnp.where(
        lane % 4 < 2, pltpu.roll(values, size - 2, 1), pltpu.roll(values, 2, 1)
    )


def cell_shares(cells, keyed, bias):
    scores = four_sum(cells * keyed) + bias
    raised = jnp.exp(scores - jnp.max(scores, axis=1, keepdims=True))
    total = jnp.sum(raised, axis=1, keepdims=True) * 0.25
    return raised * (1.0 / total)


def embed_pair(pair, cells, keyed_ref, bias_ref, patch_ref, var_ref, x0_ref):
    patch = split_low(patch_ref[...])
    variable = split_low(var_ref[...])
    outs = []
    for which in range(2):
        row = pl.ds(pair * 2 + which, 1)
        shares = cell_shares(cells, keyed_ref[row, :], bias_ref[row, :])
        outs.append(
            three_products(split_low(shares * cells), patch)
            + three_products(split_low(shares), variable)
        )
    lane = lax.broadcasted_iota(jnp.int32, outs[0].shape, 1)
    columns = pl.ds(pl.multiple_of(pair * 2 * HEAD_DIM, 2 * HEAD_DIM), 2 * HEAD_DIM)
    x0_ref[:, columns] = jnp.where(lane < HEAD_DIM, outs[0], outs[1])


def embed_kernel(
    u_ref, keyed_ref, bias_ref, patch_ref, var_ref, lead_ref, gains_ref, x0_ref, h1_ref
):
    pair = pl.program_id(0)
    embed_pair(pair, u_ref[...], keyed_ref, bias_ref, patch_ref, var_ref, x0_ref)

    @pl.when(pair == pl.num_programs(0) - 1)
    def _():
        x0_ref[...] += lead_ref[...]
        unit, _ = normed_parts(x0_ref[...])
        h1_ref[...] = (unit * gains_ref[0:1, :] + gains_ref[1:2, :]).astype(bf16)


def embed_forward(cells, prepared, lead_row, norm_gains):
    patch, variable, keyed, bias = prepared
    rows, padded = cells.shape
    fixed = lambda shape: pl.BlockSpec(shape, lambda i: (0, 0))
    by_pair = pl.BlockSpec((padded, 2 * HEAD_DIM), lambda i: (0, i))
    return pl.pallas_call(
        embed_kernel,
        grid=(HEADS // 2,),
        out_shape=(
            jax.ShapeDtypeStruct((rows, D), f32),
            jax.ShapeDtypeStruct((rows, D), bf16),
        ),
        in_specs=[
            fixed((rows, padded)),
            fixed(keyed.shape),
            fixed(bias.shape),
            by_pair,
            by_pair,
            fixed((1, D)),
            fixed(norm_gains.shape),
        ],
        out_specs=[fixed((rows, D)), fixed((rows, D))],
        compiler_params=pltpu.CompilerParams(vmem_limit_bytes=BIG),
        cost_estimate=pl.CostEstimate(
            flops=24 * rows * padded * D, bytes_accessed=14 * rows * D, transcendentals=16 * rows * padded
        ),
        name="embed_forward",
    )(cells, keyed, bias, patch, variable, lead_row, norm_gains)


def entry_rows(
    grad_ref, qkv_ref, x0_ref, mid_ref, gains_ref, du_ref, gain_ref, lead_ref, dx_ref, flip_ref
):
    row_grad = jnp.dot(grad_ref[...], qkv_ref[...], preferred_element_type=f32)
    unit, inverse = normed_parts(x0_ref[...])
    part, gain_grad, bias_grad = norm_grad(unit, inverse, gains_ref[0:1, :], row_grad)
    total = mid_ref[...] + part
    dx_ref[...] = total
    flip_ref[...] = total.T
    lead_ref[...] = jnp.sum(total, axis=0, keepdims=True)
    gain_ref[0:1, :] = gain_grad
    gain_ref[1:2, :] = bias_grad
    du_ref[...] = jnp.zeros_like(du_ref)


def entry_pair(
    pair, u_ref, keyed_ref, bias_ref, patch_ref, var_ref,
    du_ref, dpatch_ref, dvar_ref, dkeyed_ref, dbias_ref, dx_ref, flip_ref,
):
    cells = u_ref[...]
    size = 2 * HEAD_DIM
    columns = pl.ds(pl.multiple_of(pair * size, size), size)
    grads = dx_ref[:, columns]
    lane = lax.broadcasted_iota(jnp.int32, grads.shape, 1)
    patch = split_low(patch_ref[...])
    variable = split_low(var_ref[...])
    cells_grad = None
    for which in range(2):
        row = pl.ds(pair * 2 + which, 1)
        keyed = keyed_ref[row, :]
        shares = cell_shares(cells, keyed, bias_ref[row, :])
        one = split_low(jnp.where(lane // HEAD_DIM == which, grads, 0.0))
        mixed_grad = three_products(one, patch, NT)
        share_grad = mixed_grad * cells + three_products(one, variable, NT)
        weighted = shares * share_grad
        inner = jnp.sum(weighted, axis=1, keepdims=True)
        score_grad = four_sum(weighted) - shares * inner
        piece = mixed_grad * shares + score_grad * keyed
        cells_grad = piece if cells_grad is None else cells_grad + piece
        scale = HEAD_DIM**-0.5
        dkeyed_ref[row, :] = jnp.sum(score_grad * cells, axis=0, keepdims=True) * scale
        dbias_ref[row, :] = jnp.sum(score_grad, axis=0, keepdims=True) * scale
        rows = pl.ds(pl.multiple_of(pair * size + which * HEAD_DIM, HEAD_DIM), HEAD_DIM)
        flipped = split_low(flip_ref[rows, :])
        mine = slice(which * HEAD_DIM, (which + 1) * HEAD_DIM)
        dpatch_ref[mine, :] = three_products(flipped, split_low(shares * cells))
        dvar_ref[mine, :] = three_products(flipped, split_low(shares))
    du_ref[...] += cells_grad


def entry_back_kernel(
    grad_ref, qkv_ref, x0_ref, mid_ref, gains_ref, u_ref, keyed_ref, bias_ref, patch_ref, var_ref,
    du_ref, gain_ref, lead_ref, dpatch_ref, dvar_ref, dkeyed_ref, dbias_ref,
    dx_ref, flip_ref,
):
    pair = pl.program_id(0)

    @pl.when(pair == 0)
    def _():
        entry_rows(
            grad_ref, qkv_ref, x0_ref, mid_ref, gains_ref, du_ref, gain_ref, lead_ref, dx_ref,
            flip_ref,
        )

    entry_pair(
        pair, u_ref, keyed_ref, bias_ref, patch_ref, var_ref,
        du_ref, dpatch_ref, dvar_ref, dkeyed_ref, dbias_ref, dx_ref, flip_ref,
    )


def entry_last_kernel(*refs):
    steps = (refs[0:6], refs[6:12])
    share_ref = refs[12]
    grad_ref, qkv_ref, x0_ref, mid_ref, gains_ref, u_ref, keyed_ref, bias_ref = refs[13:21]
    patch_ref, var_ref, query_ref, hot_ref, lead_hot_ref, head_a, head_b, high_a, high_b = refs[21:30]
    patch_a, var_a, keyed_a, bias_a, lead_a, gain_a = refs[30:36]
    rows_out, up_out_ref, qkv_share_ref = refs[36:39]
    (dx_ref, flip_ref, low_ref, landing_ref, cross_sem, du_ref, gain_ref, lead_ref, dpatch_ref,
     dvar_ref, dkeyed_ref, dbias_ref) = refs[39:51]
    scatter = Scatter(refs[51:57], refs[58:61])
    held_ref = refs[57]
    turn = pl.program_id(0)
    dp, level, core = mesh_place()
    across = device_of(level, dp, core)
    crossing = scatter.copy(low_ref, landing_ref, cross_sem, 0, 0, across)

    @pl.when(turn == 0)
    def _():
        barrier = pltpu.get_barrier_semaphore()
        deep = [device_of(dp, lax.rem(level + move, 4), core) for move in (1, 2, 3)]
        for target in (scatter.side, scatter.down, *deep):
            pl.semaphore_signal(barrier, inc=1, device_id=target, device_id_type=MESH)
        low_ref[...] = share_ref[...]

        @pl.when(dp != level)
        def _():
            pl.semaphore_signal(barrier, inc=1, device_id=across, device_id_type=MESH)
            pl.semaphore_wait(barrier, 6)

        @pl.when(dp == level)
        def _():
            pl.semaphore_wait(barrier, 5)

    for index, depth in enumerate(scatter.order):

        @pl.when(turn == index)
        def _(depth=depth):
            lefts, rights, smalls, wides = [], [], [], []
            for dg, o, h2, h2_near, dx1, dx1_near in steps:
                lefts += [dg[0, 0], dg[1, 0]]
                rights += [h2[...], h2_near[...]]
                smalls += [o[0, 0], o[1, 0]]
                wides += [dx1[...], dx1_near[...]]
            scatter.begin(depth, [summed(lefts, rights), summed(smalls, wides)], held_ref)

        @pl.when(turn == entry_middle_at[index])
        def _(depth=depth):
            scatter.middle(depth)

        @pl.when(turn == entry_end_at[index])
        def _(depth=depth):
            scatter.end(depth)

    @pl.when((turn == 11) & (dp != level))
    def _():
        crossing.start()

    @pl.when(turn == 4)
    def _():
        entry_rows(
            grad_ref, qkv_ref, x0_ref, mid_ref, gains_ref, du_ref, gain_ref,
            lead_ref.at[0:1, :], dx_ref, flip_ref,
        )

    @pl.when((turn >= 5) & (turn < 5 + HEADS // 2))
    def _():
        size = 2 * HEAD_DIM
        pair = turn - 5
        some = pl.ds(pl.multiple_of(pair * size, size), size)
        entry_pair(
            pair, u_ref, keyed_ref, bias_ref, patch_ref.at[:, some], var_ref.at[:, some],
            du_ref, dpatch_ref.at[some, :], dvar_ref.at[some, :], dkeyed_ref, dbias_ref,
            dx_ref, flip_ref,
        )

    @pl.when(turn == entry_turns - 2)
    def _():
        gain_ref[...] += gain_a[...]
        lead_ref[1:2, :] = lead_a[...]
        lead_ref[2:8, :] = jnp.zeros((6, lead_ref.shape[1]), f32)
        table_rows(
            patch_a, dpatch_ref, var_a, dvar_ref, keyed_a, dkeyed_ref, bias_a, dbias_ref,
            patch_ref, var_ref, query_ref, hot_ref, lead_hot_ref, lead_ref, gain_ref,
            (head_a[...], head_b[...]), (high_a[2:6, :], high_b[2:6, :]), rows_out,
        )

    @pl.when(turn == entry_turns - 1)
    def _():
        @pl.when(dp != level)
        def _():
            crossing.wait()
            qkv_share_ref[...] = landing_ref[...]

        @pl.when(dp == level)
        def _():
            qkv_share_ref[...] = share_ref[...]

        scatter.finish(up_out_ref)


def entry_last(
    kept, share, token_grad, qkv_t, x_first, mid_grad, norm_gains, cells, prepared,
    query, var_hot, lead_hots, heads, highs, earlier,
):
    patch, variable, keyed, bias = prepared
    rows, width = x_first.shape
    padded = cells.shape[1]
    in_specs, operands = [], []
    for dg, o, h2, h2_near, dx1, dx1_near in kept:
        operands += [dg, o, h2, h2_near, dx1, dx1_near]
        in_specs += [chunk_spec(dg.shape[2:]), chunk_spec(o.shape[2:])]
        in_specs += [once(h2.shape)] * 4
    values = [
        share, token_grad, qkv_t, x_first, mid_grad, norm_gains, cells, keyed, bias,
        patch, variable, query, var_hot, lead_hots, *heads, *highs, *earlier,
    ]
    in_specs += [once(value.shape) for value in values]
    height, columns = kept[0][0].shape[3] + kept[0][1].shape[3], width // 4
    outs = [(2 * padded, width), (height, columns), share.shape]
    return pl.pallas_call(
        entry_last_kernel,
        grid=(entry_turns,),
        out_shape=[jax.ShapeDtypeStruct(shape, f32) for shape in outs],
        in_specs=in_specs,
        out_specs=[pl.BlockSpec(shape, lambda i: (0, 0)) for shape in outs],
        scratch_shapes=[
            pltpu.VMEM((rows, width), f32),
            pltpu.VMEM((width, rows), f32),
            pltpu.VMEM(share.shape, f32),
            pltpu.VMEM(share.shape, f32),
            pltpu.SemaphoreType.DMA((2, 1)),
            pltpu.VMEM((rows, padded), f32),
            pltpu.VMEM((2, width), f32),
            pltpu.VMEM((8, width), f32),
            pltpu.VMEM((width, padded), f32),
            pltpu.VMEM((width, padded), f32),
            pltpu.VMEM(keyed.shape, f32),
            pltpu.VMEM(bias.shape, f32),
        ]
        + scatter_scratch(height, columns),
        compiler_params=pltpu.CompilerParams(
            collective_id=6, has_side_effects=True, vmem_limit_bytes=BIG
        ),
        name="entry_last",
    )(*operands, *values)


def entry_backward(token_grad, qkv_t, x_first, mid_grad, norm_gains, cells, prepared):
    patch, variable, keyed, bias = prepared
    rows, width = x_first.shape
    padded = cells.shape[1]
    fixed = lambda shape: pl.BlockSpec(shape, lambda i: (0, 0))
    by_pair = pl.BlockSpec((padded, 2 * HEAD_DIM), lambda i: (0, i))
    flipped = pl.BlockSpec((2 * HEAD_DIM, padded), lambda i: (i, 0))
    return pl.pallas_call(
        entry_back_kernel,
        grid=(HEADS // 2,),
        out_shape=(
            jax.ShapeDtypeStruct((rows, padded), f32),
            jax.ShapeDtypeStruct((2, width), f32),
            jax.ShapeDtypeStruct((1, width), f32),
            jax.ShapeDtypeStruct((width, padded), f32),
            jax.ShapeDtypeStruct((width, padded), f32),
            jax.ShapeDtypeStruct(keyed.shape, f32),
            jax.ShapeDtypeStruct(bias.shape, f32),
        ),
        in_specs=[
            fixed(token_grad.shape),
            fixed(qkv_t.shape),
            fixed((rows, width)),
            fixed((rows, width)),
            fixed(norm_gains.shape),
            fixed(cells.shape),
            fixed(keyed.shape),
            fixed(bias.shape),
            by_pair,
            by_pair,
        ],
        out_specs=[
            fixed((rows, padded)),
            fixed((2, width)),
            fixed((1, width)),
            flipped,
            flipped,
            fixed(keyed.shape),
            fixed(bias.shape),
        ],
        scratch_shapes=[pltpu.VMEM((rows, width), f32), pltpu.VMEM((width, rows), f32)],
        compiler_params=pltpu.CompilerParams(vmem_limit_bytes=BIG),
        cost_estimate=pl.CostEstimate(
            flops=60 * rows * padded * D, bytes_accessed=40 * rows * D, transcendentals=16 * rows * padded
        ),
        name="entry_backward",
    )(token_grad, qkv_t, x_first, mid_grad, norm_gains, cells, keyed, bias, patch, variable)


def table_rows(
    pa_ref, pb_ref, va_ref, vb_ref, ka_ref, kb_ref, ba_ref, bb_ref,
    patch_ref, var_ref, query_ref, hot_ref, lead_hot_ref, lead_ref, gain_ref, heads, highs, o_ref,
):
    padded, width = patch_ref.shape
    marks = head_marks(width)
    query = query_ref[...]
    keyed_grad = exact_product(ka_ref[...] + kb_ref[...], marks, TN)
    bias_grad = exact_product(ba_ref[...] + bb_ref[...], marks, TN)
    o_ref[...] = jnp.zeros_like(o_ref)
    patch_grad = (pa_ref[...] + pb_ref[...]).T + keyed_grad * query
    o_ref[: 4 * V, :] = patch_grad[: 4 * V, :]
    var_grad = (va_ref[...] + vb_ref[...]).T + bias_grad * query
    var_rows = exact_product(quarter_marks(padded), var_grad, TN)
    o_ref[4 * V : 5 * V, :] = exact_product(hot_ref[...], var_rows, TN)
    lead_rows = exact_product(lead_hot_ref[...], lead_ref[...], TN)
    o_ref[5 * V : 5 * V + LEADS, :] = lead_rows[:LEADS, :]
    query_grad = jnp.sum(
        keyed_grad * patch_ref[...] + bias_grad * var_ref[...], axis=0, keepdims=True
    )
    o_ref[5 * V + LEADS : 5 * V + LEADS + 1, :] = query_grad
    o_ref[5 * V + LEADS + 1 : 5 * V + LEADS + 3, :] = gain_ref[...]
    o_ref[padded : padded + 4 * V, :] = heads[0] + heads[1]
    o_ref[padded + 4 * V : padded + 4 * V + 4, :] = highs[0] + highs[1]


def table_grads_kernel(*refs):
    head_a, head_b, high_a, high_b = refs[15:19]
    heads, highs = (head_a[...], head_b[...]), (high_a[2:6, :], high_b[2:6, :])
    table_rows(*refs[:15], heads, highs, refs[19])


def table_grads(first, second, prepared, query, var_hot, lead_hots, leads, gain_rows, heads, highs):
    patch, variable, _, _ = prepared
    operands = []
    for one, two in zip(first, second):
        operands += [one, two]
    return pl.pallas_call(
        table_grads_kernel,
        out_shape=jax.ShapeDtypeStruct((2 * patch.shape[0], D), f32),
        compiler_params=pltpu.CompilerParams(vmem_limit_bytes=BIG),
        name="table_grads",
    )(*operands, patch, variable, query, var_hot, lead_hots, leads, gain_rows, *heads, *highs)


def adam_step(master, grad, first, second, rate):
    first_new = beta_first * first + (1.0 - beta_first) * grad
    second_new = beta_second * second + (1.0 - beta_second) * grad * grad
    update = first_new / first_fix / (jnp.sqrt(second_new / second_fix) + adam_eps)
    return (master - rate * (update + decay_rate * master), first_new, second_new)


def update_kernel(packed, *refs):
    where_ref, sums_ref, tile_ref, count_ref = refs[:4]
    shares = list(refs[4 : 4 + (3 if packed else 4)])
    rest = refs[4 + len(shares) :]
    states, average_ref, outs = rest[:18], rest[18], rest[19:]
    norm = jnp.sqrt(tile_ref[0:1, 0:1])
    factor = jnp.minimum(1.0, clip_norm / (norm + 1e-06))
    outs[1][...] = norm
    outs[0][...] = tile_ref[1:2, 0:1] / (2.0 * V * jnp.maximum(count_ref[...], 1.0))
    embed_rows = 5 * V + LEADS + 1
    padded = 256

    def apply(index, grad, rate, rows=slice(None)):
        master, first, second = (ref[rows, :] for ref in states[3 * index : 3 * index + 3])
        new = adam_step(master, factor * grad, first, second, rate)
        for ref, value in zip(outs[2 + 3 * index : 5 + 3 * index], new):
            ref[rows, :] = value
        return new[0]

    apply(0, sums_ref[:embed_rows, :], lr_table, slice(0, embed_rows))
    apply(0, sums_ref[padded : padded + 4 * V, :], lr_table, slice(embed_rows, embed_rows + 4 * V))
    apply(1, sums_ref[embed_rows : embed_rows + 2, :], lr_gain, slice(0, 2))
    apply(1, sums_ref[padded + 4 * V : padded + 4 * V + 4, :], lr_gain, slice(2, 6))
    if packed:
        units = shares[2].shape[0]
        grads = (
            shares[0][...], shares[1][units:, :], shares[1][:units, :].T, shares[2][...]
        )
    else:
        grads = [share[...] for share in shares]
    qkv_new = apply(2, grads[0], lr_matrix)
    for index in range(1, 4):
        apply(2 + index, grads[index], lr_matrix)
    outs[20][...] = average_keep * average_ref[...] + (1.0 - average_keep) * qkv_new


def update_all(packed, where, sums, tile, count, shares, states, average):
    operands = [sums, tile, count.reshape(1, 1), *shares]
    fixed = lambda shape: pl.BlockSpec(shape, lambda i, w: (0, 0))
    in_specs = [fixed(value.shape) for value in operands]
    out_shapes = [(1, 1), (1, 1)]
    for master, first, second in states:
        if master.shape == first.shape:
            in_specs.append(fixed(master.shape))
        elif master.shape[0] == first.shape[0]:
            in_specs.append(pl.BlockSpec(first.shape, lambda i, w: (0, w[0])))
        else:
            in_specs.append(pl.BlockSpec(first.shape, lambda i, w: (w[0], 0)))
        in_specs += [fixed(first.shape)] * 2
        operands += [master, first, second]
        out_shapes += [first.shape] * 3
    operands.append(average)
    in_specs.append(fixed(average.shape))
    out_shapes.append(average.shape)
    return pl.pallas_call(
        partial(update_kernel, packed),
        grid_spec=pltpu.PrefetchScalarGridSpec(
            num_scalar_prefetch=1,
            grid=(1,),
            in_specs=in_specs,
            out_specs=[fixed(shape) for shape in out_shapes],
        ),
        out_shape=[jax.ShapeDtypeStruct(shape, f32) for shape in out_shapes],
        compiler_params=pltpu.CompilerParams(vmem_limit_bytes=60 * 2**20),
        name="update_all",
    )(where, *operands)


def by_kind(shard):
    rows = shard.shape[0]
    return shard.reshape(rows, -1, 3, HEAD_DIM).transpose(0, 2, 1, 3).reshape(rows, -1)


def by_head(shard):
    rows = shard.shape[0]
    return shard.reshape(rows, 3, -1, HEAD_DIM).transpose(0, 2, 1, 3).reshape(rows, -1)


class Rows:
    count = 11

    def __init__(self, refs, sems):
        (self.h1, self.rows_ref, self.weight, self.qkv, self.vt, self.o_ref, self.full, self.lse,
         self.attended) = refs
        self.sems, self.o_sems, self.own_sem = sems
        dp, level, core = mesh_place()
        self.dp, self.core = dp, core
        self.me = dp * 2 + core
        self.height = self.h1.shape[0]
        self.width = self.o_ref.shape[1]
        half = self.height // 2
        x = lax.rem(dp, 2)
        beside, below, far = dp + 1 - 2 * x, lax.rem(dp + 2, 4), 3 - dp
        self.owners = (beside, below, far)
        self.peers = []
        for move in range(1, 8):
            part = lax.rem(self.me + move, 8)
            self.peers.append(device_of(part // 2, level, lax.rem(part, 2)))
        side = device_of(beside, level, core)
        down = device_of(below, level, core)
        near = device_of(dp, level, 1 - core)
        self.level = level
        slots = [0]

        def remote(source, target_ref, target):
            slot = slots[0]
            slots[0] += 1
            return pltpu.make_async_remote_copy(
                src_ref=source,
                dst_ref=target_ref,
                send_sem=self.sems.at[0, slot],
                recv_sem=self.sems.at[1, slot],
                device_id=target,
                device_id_type=MESH,
            )

        def place(owner, first, size):
            start = pl.multiple_of((owner * 2 + core) * self.height + first, half)
            return self.rows_ref.at[pl.ds(start, size)]

        def relay(where, target):
            return remote(where, where, target)

        first, second = self.h1.at[pl.ds(0, half)], self.h1.at[pl.ds(half, half)]
        self.side_a = remote(first, place(dp, 0, half), side)
        self.down_b = remote(second, place(dp, half, half), down)
        self.side_b = remote(second, place(dp, half, half), side)
        self.down_a = remote(first, place(dp, 0, half), down)
        self.near_own = remote(self.h1, place(dp, 0, self.height), near)
        self.far_a = relay(place(beside, 0, half), down)
        self.far_b = relay(place(below, half, half), side)
        self.near_side = relay(place(beside, 0, self.height), near)
        self.near_down = relay(place(below, 0, self.height), near)
        self.near_far = relay(place(far, 0, self.height), near)

    def part_rows(self, part):
        return pl.ds(pl.multiple_of(part * self.height, self.height), self.height)

    def project(self, owner, core):
        where = self.part_rows(owner * 2 + core)
        self.qkv[where, :] = lax.dot_general(
            self.rows_ref[where, :], self.weight[...], NT, preferred_element_type=f32
        ).astype(bf16)

    def send_o(self, part, target):
        columns = pl.ds(pl.multiple_of(self.me * self.width, self.width), self.width)
        return pltpu.make_async_remote_copy(
            src_ref=self.o_ref.at[self.part_rows(part), :],
            dst_ref=self.attended.at[:, columns],
            send_sem=self.o_sems.at[0, lax.rem(part + 8 - self.me, 8)],
            recv_sem=self.o_sems.at[1, lax.rem(part + 8 - self.me, 8)],
            device_id=target,
            device_id_type=MESH,
        )

    def keep_o(self):
        columns = pl.ds(pl.multiple_of(self.me * self.width, self.width), self.width)
        return pltpu.make_async_copy(
            self.o_ref.at[self.part_rows(self.me), :], self.attended.at[:, columns], self.own_sem
        )

    def phase(self, number):
        beside, below, far = self.owners
        if number == 0:
            for copy in (self.side_a, self.down_b, self.side_b, self.down_a, self.near_own):
                copy.start()
            self.rows_ref[self.part_rows(self.me), :] = self.h1[...]
        elif number == 1:
            self.project(self.dp, self.core)
            self.near_own.wait_recv()
        elif number == 2:
            self.side_a.wait_recv()
            self.far_a.start()
            self.down_b.wait_recv()
            self.far_b.start()
            self.project(self.dp, 1 - self.core)
        elif number == 3:
            self.side_b.wait_recv()
            self.near_side.start()
            self.down_a.wait_recv()
            self.near_down.start()
            self.project(beside, self.core)
            self.project(below, self.core)
        elif number == 4:
            self.near_side.wait_recv()
            self.near_down.wait_recv()
            self.project(beside, 1 - self.core)
            self.project(below, 1 - self.core)
        elif number == 5:
            self.far_a.wait_recv()
            self.far_b.wait_recv()
            self.near_far.start()
            self.project(far, self.core)
        elif number == 6:
            self.near_far.wait_recv()
            self.project(far, 1 - self.core)
            self.vt[...] = self.qkv[:, 2 * self.width :].T

    def attend(self, turn):
        owner = lax.rem(self.dp + 1 + turn, 4)
        size = 2 * self.height
        where = pl.ds(pl.multiple_of(owner * size, size), size)
        heads = self.width // HEAD_DIM
        full, sums = attend_rows(
            heads, self.qkv[where, : self.width],
            self.qkv.at[:, self.width : 2 * self.width], self.vt,
        )
        for head in range(heads):
            self.lse[head : head + 1, where] = sums[head]
        self.full[where, :] = full
        self.o_ref[where, :] = full.astype(bf16)

        @pl.when(turn < 3)
        def _():
            for core in range(2):
                self.send_o(owner * 2 + core, device_of(owner, self.level, core)).start()

        @pl.when(turn == 3)
        def _():
            other = device_of(self.dp, self.level, 1 - self.core)
            self.send_o(self.dp * 2 + 1 - self.core, other).start()
            self.keep_o().start()

    def finish(self):
        for move in range(1, 8):
            part = lax.rem(self.me + move, 8)
            self.send_o(part, self.peers[move - 1]).wait()
        self.keep_o().wait()
        for copy in (
            self.side_a, self.down_b, self.side_b, self.down_a, self.near_own, self.far_a,
            self.far_b, self.near_side, self.near_down, self.near_far,
        ):
            copy.wait_send()


def row_scratch(rows, width):
    return [
        pltpu.VMEM((rows, D), bf16),
        pltpu.VMEM((8 * rows, D), bf16),
        pltpu.VMEM((3 * width, D), bf16),
        pltpu.VMEM((width, 8 * rows), bf16),
        pltpu.VMEM((8 * rows, width), bf16),
        pltpu.SemaphoreType.DMA((2, 10)),
        pltpu.SemaphoreType.DMA((2, 8)),
        pltpu.SemaphoreType.DMA((3,)),
    ]


def lead_rows_of(lead, lead_ref):
    row = lax.broadcasted_iota(jnp.int32, (1, 8), 1).astype(f32)
    lead_hot = jnp.where(row == lead, 1.0, 0.0).astype(f32)
    return exact_product(lead_hot, lead_ref[...])


def middle_kernel(
    guess_ref, first_ref, keyed_ref, bias_ref, patch_ref, var_ref, lead_ref, gains_ref, weights_ref,
    x0_ref, cells_ref, qkv_ref, full_ref, lse_ref, rows_out, attended_ref,
    h1_ref, rows_ref, weight_ref, vt_ref, o_ref, sems, o_sems, own_sem,
):
    turn = pl.program_id(0)
    dp, _, core = mesh_place()
    rows = Rows(
        (h1_ref, rows_ref, weight_ref, qkv_ref, vt_ref, o_ref, full_ref, lse_ref, attended_ref),
        (sems, o_sems, own_sem.at[0]),
    )
    size = weight_ref.shape[0]
    weight = pltpu.make_async_copy(
        weights_ref.at[pl.ds(pl.multiple_of((dp * 2 + core) * size, size), size), :],
        weight_ref, own_sem.at[1],
    )
    save = pltpu.make_async_copy(rows_ref, rows_out, own_sem.at[2])
    pairs = HEADS // 2

    @pl.when(turn == 0)
    def _():
        barrier = pltpu.get_barrier_semaphore()
        for target in rows.peers:
            pl.semaphore_signal(barrier, inc=1, device_id=target, device_id_type=MESH)
        pl.semaphore_wait(barrier, 7)
        weight.start()
        cells_ref[:, : 4 * V] = guess_ref[...]
        cells_ref[:, 4 * V :] = jnp.zeros_like(cells_ref[:, 4 * V :])

    @pl.when(turn < pairs)
    def _():
        embed_pair(turn, cells_ref[...], keyed_ref, bias_ref, patch_ref, var_ref, x0_ref)

    @pl.when(turn == pairs)
    def _():
        x0_ref[...] += lead_rows_of(first_ref[0:1, 4 * V + 5 : 4 * V + 6], lead_ref)
        unit, _ = normed_parts(x0_ref[...])
        h1_ref[...] = (unit * gains_ref[0:1, :] + gains_ref[1:2, :]).astype(bf16)
        weight.wait()

    for number in range(7):

        @pl.when(turn == pairs + number)
        def _(number=number):
            rows.phase(number)
            if number == 6:
                save.start()

    @pl.when(turn >= pairs + 7)
    def _():
        rows.attend(turn - pairs - 7)

    @pl.when(turn == pairs + 10)
    def _():
        rows.finish()
        save.wait()


def middle_program(guess, first_cells, prepared, lead_table, norm_gains, qkv_t):
    patch, variable, keyed, bias = prepared
    rows = guess.shape[0]
    padded = patch.shape[0]
    width = D // 8
    heads = width // HEAD_DIM
    total = 8 * rows
    anywhere = pl.BlockSpec(memory_space=pl.ANY)
    fixed = lambda shape: pl.BlockSpec(shape, lambda i: (0, 0))
    by_pair = pl.BlockSpec(
        (padded, 2 * HEAD_DIM), lambda i: (0, jnp.clip(i, 0, HEADS // 2 - 1))
    )
    shapes = [
        ((rows, D), f32),
        ((rows, padded), f32),
        ((total, 3 * width), bf16),
        ((total, width), f32),
        ((heads, total), f32),
    ]
    return pl.pallas_call(
        middle_kernel,
        grid=(HEADS // 2 + Rows.count,),
        out_shape=[jax.ShapeDtypeStruct(shape, kind) for shape, kind in shapes]
        + [jax.ShapeDtypeStruct((total, D), bf16), jax.ShapeDtypeStruct((rows, D), bf16)],
        in_specs=[once(value.shape) for value in (guess, first_cells, keyed, bias)]
        + [by_pair, by_pair, once(lead_table.shape), once(norm_gains.shape), anywhere],
        out_specs=[fixed(shape) for shape, _ in shapes] + [anywhere, anywhere],
        scratch_shapes=row_scratch(rows, width),
        compiler_params=pltpu.CompilerParams(
            collective_id=9, has_side_effects=True, vmem_limit_bytes=BIG
        ),
        name="middle_program",
    )(guess, first_cells, keyed, bias, patch, variable, lead_table, norm_gains, qkv_t)


lag_one, lag_two, ahead = 2, 4, 3
embed_at, gather_at = 3, 11


def start_kernel(halves, *refs):
    count = len(halves)
    packed_ref, keyed_ref, bias_ref, patch_ref, var_ref, lead_ref, gains_ref = refs[:7]
    shards = refs[7 : 7 + count]
    x0_ref, cells_ref, qkv_ref, full_ref, lse_ref, count_ref, rows_out, attended_ref = refs[
        7 + count : 15 + count
    ]
    outs = refs[15 + count : 15 + 2 * count]
    (h1_ref, rows_ref, weight_ref, vt_ref, o_ref, row_sems, o_sems, row_own, held_ref, tile_ref,
     send_sem, recv_sem, level_send, level_recv, own_sem) = refs[15 + 2 * count :]
    rows = Rows(
        (h1_ref, rows_ref, weight_ref, qkv_ref, vt_ref, o_ref, full_ref, lse_ref, attended_ref),
        (row_sems, o_sems, row_own.at[0]),
    )
    step = pl.program_id(0)
    dp, level, core = mesh_place()
    x = lax.rem(dp, 2)
    columns = {"here": dp, "side": dp + 1 - 2 * x, "down": lax.rem(dp + 2, 4), "far": 3 - dp}
    side = device_of(columns["side"], level, core)
    down = device_of(columns["down"], level, core)
    near = device_of(dp, level, 1 - core)
    across = device_of(level, dp, core)
    middle = lax.rem(level, 3) != 0
    late = level // 2
    sources = (level + 1 - 2 * lax.rem(level, 2), 2 - late, 3 * (1 - late))
    onward = (3 - level, lax.rem(3 * level + 1, 4), lax.rem(3 * level + 1, 4))
    slots = [0]

    def remote(source, target_ref, target):
        slot = slots[0]
        slots[0] += 1
        return pltpu.make_async_remote_copy(
            src_ref=source,
            dst_ref=target_ref,
            send_sem=send_sem.at[slot],
            recv_sem=recv_sem.at[slot],
            device_id=target,
            device_id_type=MESH,
        )

    def place(out, source, column, half, pieces):
        rows = out.shape[1] // 4
        size = rows // pieces
        start = pl.multiple_of(columns[column] * rows + half * size, size)
        return out.at[source * 2 + core, pl.ds(start, size), :]

    def pass_on(out, source, column, target, cut):
        where = place(out, source, column, *cut)
        return remote(where, where, target)

    crossing = remote(packed_ref, held_ref, across)
    staying = pltpu.make_async_copy(packed_ref, held_ref, own_sem.at[count])
    mine = [outs[index].at[level * 2 + core] for index in range(count)]
    given = [remote(shards[index], mine[index], near) for index in range(count)]
    kept = [
        pltpu.make_async_copy(shards[index], mine[index], own_sem.at[index]) for index in range(count)
    ]
    chunks, openings = [], []
    for index in range(count):
        out, pieces = outs[index], halves[index]
        for half in range(pieces):
            group = len(openings)
            full = out.shape[1] // 4
            size = full // pieces
            own = shards[index].at[pl.ds(pl.multiple_of(dp * full + half * size, size), size), :]
            cut = (half, pieces)

            def along(source_ref, source, target_level, slot):
                return pltpu.make_async_remote_copy(
                    src_ref=source_ref,
                    dst_ref=place(out, source, "here", *cut),
                    send_sem=level_send.at[group * 5 + slot],
                    recv_sem=level_recv.at[group * 4 + source],
                    device_id=device_of(dp, target_level, core),
                    device_id_type=MESH,
                )

            openings.append(
                (
                    along(own, level, lax.rem(level + 1, 4), 0),
                    along(own, level, lax.rem(level + 3, 4), 1),
                )
            )
            for turn in range(3):
                source = sources[turn]
                chunks.append(
                    {
                        "level": along(place(out, source, "here", *cut), source, onward[turn], 2 + turn),
                        "side": pass_on(out, source, "here", side, cut),
                        "down": pass_on(out, source, "here", down, cut),
                        "hop_down": pass_on(out, source, "side", down, (2 * half, 2 * pieces)),
                        "hop_side": pass_on(out, source, "down", side, (2 * half + 1, 2 * pieces)),
                        "here_near": pass_on(out, source, "here", near, cut),
                        "side_near": pass_on(out, source, "side", near, cut),
                        "down_near": pass_on(out, source, "down", near, cut),
                        "far_near": pass_on(out, source, "far", near, cut),
                    }
                )
    groups = len(openings)
    order = []
    for number in range(groups + 2):
        for turn in range(3):
            if 0 <= number - turn < groups:
                order.append((number - turn, turn))
    chunks = [chunks[3 * group + turn] for group, turn in order]
    total = len(chunks)

    def start_group(number):
        @pl.when(level < 3)
        def _():
            openings[number][0].start()

        @pl.when(level > 0)
        def _():
            openings[number][1].start()

    tiles = [
        remote(tile_ref.at[0], tile_ref.at[1], side),
        remote(tile_ref.at[2], tile_ref.at[3], down),
        remote(tile_ref.at[4], tile_ref.at[5], near),
    ]
    deep = [device_of(dp, lax.rem(level + move, 4), core) for move in (1, 2, 3)]
    level_tiles = [remote(tile_ref.at[6], tile_ref.at[7 + move], deep[move]) for move in range(3)]
    weight = pltpu.make_async_copy(outs[0].at[dp * 2 + core], weight_ref, row_own.at[1])
    save = pltpu.make_async_copy(rows_ref, rows_out, row_own.at[2])

    @pl.when(step == 0)
    def _():
        barrier = pltpu.get_barrier_semaphore()
        for target in (*rows.peers, *deep):
            pl.semaphore_signal(barrier, inc=1, device_id=target, device_id_type=MESH)

        @pl.when(dp != level)
        def _():
            pl.semaphore_signal(barrier, inc=1, device_id=across, device_id_type=MESH)
            pl.semaphore_wait(barrier, 11)
            crossing.start()

        @pl.when(dp == level)
        def _():
            pl.semaphore_wait(barrier, 10)
            staying.start()

        for number in range(ahead):
            start_group(number)
        for copy in (*given, *kept):
            copy.start()

    for number in range(total + lag_two):

        @pl.when(step == number)
        def _(number=number):
            if number < total:
                chunk = chunks[number]
                chunk["level"].wait_recv()

                @pl.when(middle)
                def _():
                    chunk["level"].start()

                chunk["side"].start()
                chunk["down"].start()
                chunk["here_near"].start()
                group, turn = order[number]
                if turn == 0 and group + ahead < groups:
                    start_group(group + ahead)
            if 0 <= number - lag_one < total:
                chunk = chunks[number - lag_one]
                chunk["side"].wait_recv()
                chunk["hop_down"].start()
                chunk["down"].wait_recv()
                chunk["hop_side"].start()
                chunk["side_near"].start()
                chunk["down_near"].start()
            if 0 <= number - lag_two < total:
                chunk = chunks[number - lag_two]
                chunk["hop_down"].wait_recv()
                chunk["hop_side"].wait_recv()
                chunk["far_near"].start()

    @pl.when(step == embed_at)
    def _():
        @pl.when(dp != level)
        def _():
            crossing.wait_recv()

        @pl.when(dp == level)
        def _():
            staying.wait()

        cells_ref[...] = held_ref[...]
        lane = lax.broadcasted_iota(jnp.int32, held_ref.shape, 1)
        ocean = jnp.where((lane >= 4 * V) & (lane < 4 * V + 4), 1.0 - held_ref[...], 0.0)
        tile_ref[0] = jnp.broadcast_to(jnp.sum(ocean), tile_ref.shape[1:])
        tiles[0].start()

    for turn in range(3):

        @pl.when(step == embed_at + 2 + turn)
        def _(turn=turn):
            tiles[turn].wait_recv()
            tile_ref[2 * turn + 2] = tile_ref[2 * turn] + tile_ref[2 * turn + 1]
            for copy in (tiles[1:2], tiles[2:3], level_tiles)[turn]:
                copy.start()

    @pl.when(step == embed_at + 6)
    def _():
        for copy in level_tiles:
            copy.wait_recv()
        count_ref[...] = tile_ref[6] + tile_ref[7] + tile_ref[8] + tile_ref[9]

    @pl.when((step >= embed_at) & (step < embed_at + HEADS // 2))
    def _():
        embed_pair(step - embed_at, held_ref[...], keyed_ref, bias_ref, patch_ref, var_ref, x0_ref)

    @pl.when(step == gather_at - 2)
    def _():
        kept[0].wait()
        weight.start()

    @pl.when(step == gather_at)
    def _():
        x0_ref[...] += lead_rows_of(held_ref[0:1, 4 * V + 4 : 4 * V + 5], lead_ref)
        unit, _ = normed_parts(x0_ref[...])
        h1_ref[...] = (unit * gains_ref[0:1, :] + gains_ref[1:2, :]).astype(bf16)
        weight.wait()

    for number in range(7):

        @pl.when(step == gather_at + number)
        def _(number=number):
            rows.phase(number)
            if number == 6:
                save.start()

    @pl.when((step >= gather_at + 7) & (step < gather_at + 11))
    def _():
        rows.attend(step - gather_at - 7)

    @pl.when(step == total + lag_two - 1)
    def _():
        for copy in given:
            copy.wait()
        for copy in kept[1:]:
            copy.wait()
        for number in range(groups):

            @pl.when(level < 3)
            def _(number=number):
                openings[number][0].wait_send()

            @pl.when(level > 0)
            def _(number=number):
                openings[number][1].wait_send()

        for chunk in chunks:
            for name in ("here_near", "side_near", "down_near", "far_near"):
                chunk[name].wait_recv()
            for name, copy in chunk.items():
                if name != "level":
                    copy.wait_send()

            @pl.when(middle)
            def _(chunk=chunk):
                chunk["level"].wait_send()

        rows.finish()
        for copy in (*tiles, *level_tiles):
            copy.wait_send()
        save.wait()

        @pl.when(dp != level)
        def _():
            crossing.wait_send()


def start_program(packed, prepared, lead_table, norm_gains, shards, halves):
    patch, variable, keyed, bias = prepared
    count = len(shards)
    groups = sum(halves)
    copies = groups * 24 + count + 7
    rows, padded = packed.shape
    total = 8 * rows
    width = shards[0].shape[0] // 3
    heads = width // HEAD_DIM
    anywhere = pl.BlockSpec(memory_space=pl.ANY)
    fixed = lambda shape: pl.BlockSpec(shape, lambda i: (0, 0))
    by_pair = pl.BlockSpec(
        (padded, 2 * HEAD_DIM), lambda i: (0, jnp.clip(i - embed_at, 0, HEADS // 2 - 1))
    )
    shapes = [
        ((rows, D), f32),
        (packed.shape, f32),
        ((total, 3 * width), bf16),
        ((total, width), f32),
        ((heads, total), f32),
        ((8, 128), f32),
    ]
    return pl.pallas_call(
        partial(start_kernel, halves),
        grid=(groups * 3 + lag_two,),
        out_shape=[jax.ShapeDtypeStruct(shape, kind) for shape, kind in shapes]
        + [jax.ShapeDtypeStruct((total, D), bf16), jax.ShapeDtypeStruct((rows, D), bf16)]
        + [jax.ShapeDtypeStruct((8,) + shard.shape, bf16) for shard in shards],
        in_specs=[anywhere]
        + [fixed(keyed.shape), fixed(bias.shape), by_pair, by_pair]
        + [fixed(lead_table.shape), fixed(norm_gains.shape)]
        + [fixed(shard.shape) for shard in shards],
        out_specs=[fixed(shape) for shape, _ in shapes] + [anywhere] * (count + 2),
        scratch_shapes=row_scratch(rows, width)
        + [
            pltpu.VMEM(packed.shape, f32),
            pltpu.VMEM((10, 8, 128), f32),
            pltpu.SemaphoreType.DMA((copies,)),
            pltpu.SemaphoreType.DMA((copies,)),
            pltpu.SemaphoreType.DMA((groups * 5,)),
            pltpu.SemaphoreType.DMA((groups * 4,)),
            pltpu.SemaphoreType.DMA((count + 1,)),
        ],
        compiler_params=pltpu.CompilerParams(
            collective_id=7, has_side_effects=True, vmem_limit_bytes=BIG
        ),
        name="start_program",
    )(packed, keyed, bias, patch, variable, lead_table, norm_gains, *shards)


def shards(
    crossed,
    fields,
    targets,
    land_mask,
    lead_index,
    var_ids,
    tables,
    norm_gains,
    tables_first,
    tables_second,
    gains_first,
    gains_second,
    w_qkv,
    qkv_first,
    qkv_second,
    w_out,
    out_first,
    out_second,
    w_up,
    up_first,
    up_second,
    w_down,
    down_first,
    down_second,
    qkv_average,
):
    local_samples, shard_rows, _ = fields.shape
    dp_size, parts = lax.axis_size("dp"), lax.axis_size("mp")
    dp_index = lax.axis_index("dp")
    place, level, core = mesh_place()
    part = place * 2 + core if crossed else lax.axis_index("mp")
    share_rows = D // dp_size

    def own_share(full, dim):
        return lax.dynamic_slice_in_dim(full, dp_index * share_rows, share_rows, dim)

    var_hot = (var_ids[:, None] == jnp.arange(V, dtype=jnp.int32)[None, :]).astype(f32)
    prepared = prepare_tables(tables, var_hot)
    low = lambda master: master.astype(bf16)
    qkv_low = by_kind(low(w_qkv))
    packed = jnp.concatenate(
        (
            fields[0],
            land_mask[0].astype(f32),
            jnp.broadcast_to(lead_index.astype(f32), (shard_rows, 2)),
            jnp.zeros((shard_rows, 64 - 6), f32),
        ),
        axis=1,
    )
    if crossed:
        (
            x_first, cells, packed, full, logsum, count, rows_one, attended,
            qkv_t, w_outs, w_ups, w_downs
        ) = start_program(
            packed, prepared, tables[5 * V : 5 * V + 8], norm_gains,
            (qkv_low.T, low(w_out), low(w_up), low(w_down)), (1, 1, 2, 2),
        )
        count = count[0, 0]
    else:
        cells = packed
        answers = targets[0]
        count = lax.psum(jnp.sum(1.0 - cells[:, 4 * V : 4 * V + 4]), ("dp", "mp"))
        w_outs, w_ups, w_downs, qkv_t = [
            lax.all_gather(shard, "mp")
            for shard in (low(w_out), low(w_up), low(w_down), qkv_low.T)
        ]
    gathered = (w_outs.reshape(D, D), w_ups, w_downs.reshape(-1, D), qkv_t.reshape(3 * D, D))
    if not crossed:
        qkv_local = choose(qkv_t, part)
    first_cells = cells
    leads = cells[0, 4 * V + 4 : 4 * V + 6].astype(jnp.int32)
    ocean = 1.0 - cells[:, 4 * V : 4 * V + 4]
    denom = 2.0 * V * jnp.maximum(count, 1.0)
    first_row = part * shard_rows
    patch_row = (first_row + jnp.arange(shard_rows, dtype=jnp.int32)) // PATCH_COLS
    row_hot = (patch_row[:, None] == jnp.arange(PATCH_ROWS, dtype=jnp.int32)[None, :]).astype(f32)
    lat_rows = jnp.dot(
        row_hot, lat_weights(2 * PATCH_ROWS).reshape(PATCH_ROWS, 2), precision=highest
    )
    lat_pixels = jnp.broadcast_to(lat_rows[:, :, None], (shard_rows, 2, 2)).reshape(shard_rows, 4)
    weighted = jnp.tile(ocean * lat_pixels, (1, V))
    head = tables
    loss_part = f32(0.0)
    records = []
    for rollout in range(2):
        if crossed and rollout == 1:
            x_first, cells, packed, full, logsum, rows_one, attended = middle_program(
                guess, first_cells, prepared, tables[5 * V : 5 * V + 8], norm_gains, gathered[3]
            )
        if not crossed:
            if rollout == 1:
                cells = jnp.pad(guess, ((0, 0), (0, 64)))
            lead_row = lax.dynamic_slice_in_dim(tables, 5 * V + leads[rollout], 1, 0)
            x_first, normed = embed_forward(cells, prepared, lead_row, norm_gains)
            rows_one = lax.all_gather(normed, "mp", axis=0, tiled=True)
            packed = lax.dot_general(
                rows_one, qkv_local, NT, preferred_element_type=f32
            ).astype(bf16)
            own_out, full, logsum = attend(packed)
            attended = exchange(own_out, True)
        if crossed and rollout == 0:
            later_targets, attended = tie(targets[0], attended)
            answers = cross(crossed, later_targets)
        x_mid, rows_two, hidden, active, x_last, guess = branch_forward(
            attended, x_first, norm_gains, gathered, head
        )
        miss = guess - answers[rollout]
        loss_part = loss_part + jnp.sum(weighted * miss * miss)
        records.append(
            (cells, x_first, rows_one, packed, full, logsum, attended, x_mid, rows_two,
             hidden, active, x_last, 2.0 * weighted * miss / denom)
        )
    carried = jnp.zeros_like(guess)
    heads, highs = [], []
    lead_hots = (leads[:, None] == jnp.arange(8, dtype=jnp.int32)[None, :]).astype(f32)
    lead_hots = jnp.pad(lead_hots, ((0, 6), (0, 0)))
    query = tables[5 * V + LEADS : 5 * V + LEADS + 1]
    gain_low = jnp.zeros((2, D), f32)
    table_parts, lead_sums = [], []
    qkv_grad = jnp.zeros((D, w_qkv.shape[1]), f32)
    kept = []

    for rollout in (1, 0):
        (cells, x_first, rows_one, packed, full, logsum, attended, x_mid, rows_two,
         hidden, active, x_last, loss_grad) = records[rollout]
        last_low, hidden_grad, mid_grad, mid_low, out_grad, gain_part, head_grad = branch_backward(
            loss_grad + carried, x_last, x_mid, norm_gains, hidden, gathered, head
        )
        heads.append(head_grad)
        highs.append(gain_part)
        if crossed:
            (
                own_grad, act_both, dg_both, o_both, dx2_near, h2_near, dx1_near
            ) = exchange_swap(
                out_grad, active, hidden_grad, attended, last_low, rows_two, mid_low
            )
            kept.append(
                (act_both, dg_both, o_both, last_low, dx2_near, rows_two, h2_near, mid_low, dx1_near)
            )
        else:
            flat = lambda value: value.transpose(2, 1, 0, 3).reshape(shard_rows, -1)
            kept.append((attended, rows_two, flat(active), mid_low, flat(hidden_grad), last_low))
            own_grad = exchange(out_grad, False)
        if crossed and rollout == 0:
            token_grad, level_share, down_sum = finish_program(
                [(step[0], step[3], step[4]) for step in kept],
                packed, own_grad, full, logsum, rows_one, qkv_grad,
            )
        elif crossed:
            token_grad, qkv_grad = attend_exchange(packed, own_grad, full, logsum, rows_one)
        else:
            packed_grad = attend_back(own_grad, packed, full, logsum)
            token_grad = exchange(packed_grad, True)
            qkv_grad = qkv_grad + lax.dot_general(
                rows_one, packed_grad, TN, preferred_element_type=f32
            )
        entry = (token_grad, gathered[3], x_first, mid_grad, norm_gains, cells, prepared)
        if crossed and rollout == 0:
            last_rows, up_out_sum, qkv_share = entry_last(
                [step[1:3] + step[5:] for step in kept], level_share, *entry,
                query, var_hot, lead_hots, heads, highs,
                (*table_parts[0], lead_sums[0], gain_low),
            )
            break
        cells_grad, gain_one, lead_sum, *table_part = entry_backward(*entry)
        carried = cells_grad[:, : 4 * V]
        gain_low = gain_low + gain_one
        table_parts.append(table_part)
        lead_sums.append(lead_sum)

    def pair(index):
        return (kept[0][index], kept[1][index])

    if not crossed:
        lead_rows = jnp.pad(jnp.concatenate((lead_sums[1], lead_sums[0])), ((0, 6), (0, 0)))
        last_rows = table_grads(
            *table_parts, prepared, query, var_hot, lead_hots, lead_rows, gain_low, heads, highs
        )
    if not crossed:
        qkv_share = lax.psum_scatter(qkv_grad, "dp", scatter_dimension=0, tiled=True)
    qkv_share = by_head(qkv_share)
    where = dp_index.astype(jnp.int32).reshape(1)
    if crossed:
        shares = (qkv_share, up_out_sum, down_sum)
        last_sum, tile = exchange_sum(last_rows, loss_part, *shares)
        masters = (w_qkv, w_out, w_up, w_down)
    else:
        shares = (
            qkv_share,
            outer_plain(pair(0), pair(3), False),
            outer_plain(pair(1), pair(4), True),
            outer_plain(pair(2), pair(5), False),
        )
        squares = sum(jnp.sum(share * share) for share in shares)
        last_sum, loss_sum, squares = lax.psum((last_rows, loss_part, squares), ("dp", "mp"))
        squares = squares + jnp.sum(last_sum * last_sum)
        row = jnp.arange(8, dtype=jnp.int32)[:, None]
        tile = jnp.where(row == 0, squares, jnp.where(row == 1, loss_sum, 0.0))
        tile = jnp.broadcast_to(tile, (8, 128))
        masters = (own_share(w_qkv, 0), own_share(w_out, 1), own_share(w_up, 0), own_share(w_down, 1))
    states = (
        (tables, tables_first, tables_second),
        (norm_gains, gains_first, gains_second),
        (masters[0], qkv_first, qkv_second),
        (masters[1], out_first, out_second),
        (masters[2], up_first, up_second),
        (masters[3], down_first, down_second),
    )
    results = update_all(crossed, where, last_sum, tile, count, shares, states, qkv_average)
    return (results[0][0, 0], results[1][0, 0], *results[2:])


def solution(mesh):
    return jax.shard_map(
        partial(shards, is_crossed(mesh.shape)),
        mesh=mesh,
        in_specs=(
            P("dp", "mp", None),
            P("dp", None, "mp", None),
            P("dp", "mp", None),
            P("dp", None),
            P(),
            P(),
            P(),
            P(),
            P(),
            P(),
            P(),
            P(None, "mp"),
            P("dp", "mp"),
            P("dp", "mp"),
            P("mp", None),
            P("mp", "dp"),
            P("mp", "dp"),
            P(None, "mp"),
            P("dp", "mp"),
            P("dp", "mp"),
            P("mp", None),
            P("mp", "dp"),
            P("mp", "dp"),
            P("dp", "mp"),
        ),
        out_specs=(
            P(),
            P(),
            P(),
            P(),
            P(),
            P(),
            P(),
            P(),
            P("dp", "mp"),
            P("dp", "mp"),
            P("dp", "mp"),
            P("mp", "dp"),
            P("mp", "dp"),
            P("mp", "dp"),
            P("dp", "mp"),
            P("dp", "mp"),
            P("dp", "mp"),
            P("mp", "dp"),
            P("mp", "dp"),
            P("mp", "dp"),
            P("dp", "mp"),
        ),
        check_vma=False,
    )
```

```python
from functools import partial
import math

import jax
import jax.numpy as jnp
from jax import lax
from jax.experimental import pallas as pl
from jax.experimental.pallas import tpu as pltpu
from jax.sharding import PartitionSpec as P

D = 1024
HEADS = 16
HEAD_DIM = 64
V = 48
PATCH_ROWS = 32
PATCH_COLS = 64
LEADS = 7


highest = lax.Precision.HIGHEST
eps_norm = 1e-05
clip_norm = 0.05
beta_first = 0.9
beta_second = 0.999
adam_eps = 1e-08
decay_rate = 0.1
lr_matrix = 0.04
lr_table = 0.1
lr_gain = 0.3
average_keep = 0.9
first_fix = 1.0 - 0.9**10
second_fix = 1.0 - 0.999**10


def layer_norm(values, gain, bias):
    center = values - jnp.mean(values, axis=-1, keepdims=True)
    spread = jnp.mean(center * center, axis=-1, keepdims=True)
    return center * lax.rsqrt(spread + eps_norm) * gain + bias


def lat_weights(pixel_rows):
    row_index = jnp.arange(pixel_rows, dtype=jnp.float32)
    cosine = jnp.cos(((row_index + 0.5) / pixel_rows - 0.5) * math.pi)
    return cosine / jnp.mean(cosine)


bf16 = jnp.bfloat16
f32 = jnp.float32
MESH = pl.DeviceIdType.MESH
NT = (((1,), (1,)), ((), ()))
TN = (((0,), (0,)), ((), ()))
VMEM = pl.BlockSpec(memory_space=pltpu.VMEM)
BIG = 56 * 2**20


def is_crossed(sizes):
    return sizes["dp"] == 4 and sizes["mp"] == 8


def mesh_place():
    dp = lax.axis_index("dp")
    mp = lax.axis_index("mp")
    return dp, mp // 2, lax.rem(mp, 2)


def device_of(dp, level, core):
    return {"dp": dp, "mp": level * 2 + core}


def cross_pairs():
    groups = lax.axis_size("dp")
    pairs = []
    for dp in range(groups):
        for level in range(groups):
            for core in range(2):
                source = (dp * groups + level) * 2 + core
                target = (level * groups + dp) * 2 + core
                pairs.append((source, target))
    return pairs


def cross(crossed, value):
    if not crossed:
        return value
    return lax.ppermute(value, ("dp", "mp"), cross_pairs())


def exchange(value, to_columns):
    split, joined = (0, 1) if to_columns else (1, 0)
    return lax.all_to_all(value, "mp", split_axis=split, concat_axis=joined, tiled=True)


def pick_head(value, head, heads):
    if heads == 1:
        return value
    lane = lax.broadcasted_iota(jnp.int32, value.shape, 1) // HEAD_DIM
    return jnp.where(lane == head, value, jnp.zeros_like(value))


def attend_rows(heads, queries, k_ref, vt_ref):
    queries = queries * bf16(HEAD_DIM**-0.5)
    keys = k_ref[...]
    outs, sums = [], []
    for head in range(heads):
        scores = lax.dot_general(
            keys, pick_head(queries, head, heads), NT, preferred_element_type=f32
        )
        largest = jnp.max(scores, axis=0, keepdims=True)
        raised = jnp.exp(scores - largest)
        total = jnp.sum(raised, axis=0, keepdims=True)
        probs = (raised * (1.0 / total)).astype(bf16)
        values = vt_ref[head * HEAD_DIM : (head + 1) * HEAD_DIM, :]
        outs.append(jnp.dot(values, probs, preferred_element_type=f32))
        sums.append(largest + jnp.log(total))
    flipped = outs[0] if heads == 1 else jnp.concatenate(outs, axis=0)
    return flipped.T, sums


def attend_kernel(heads, q_ref, k_ref, v_ref, o_ref, full_ref, lse_ref, vt_ref):
    @pl.when(pl.program_id(0) == 0)
    def _():
        vt_ref[...] = v_ref[...].T

    full, sums = attend_rows(heads, q_ref[...], k_ref, vt_ref)
    for head in range(heads):
        lse_ref[head : head + 1, :] = sums[head]
    full_ref[...] = full
    o_ref[...] = full.astype(bf16)


def attend(packed):
    total, width = packed.shape[0], packed.shape[1] // 3
    heads = width // HEAD_DIM
    block = min(512, total)
    row_block = pl.BlockSpec((block, width), lambda i: (i, 0))
    return pl.pallas_call(
        partial(attend_kernel, heads),
        grid=(total // block,),
        out_shape=(
            jax.ShapeDtypeStruct((total, width), bf16),
            jax.ShapeDtypeStruct((total, width), f32),
            jax.ShapeDtypeStruct((heads, total), f32),
        ),
        in_specs=[
            row_block,
            pl.BlockSpec((total, width), lambda i: (0, 0)),
            pl.BlockSpec((total, width), lambda i: (0, 0)),
        ],
        out_specs=[row_block, row_block, pl.BlockSpec((heads, block), lambda i: (0, i))],
        scratch_shapes=[pltpu.VMEM((width, total), bf16)],
        compiler_params=pltpu.CompilerParams(vmem_limit_bytes=BIG),
        cost_estimate=pl.CostEstimate(
            flops=16 * total * total * width,
            bytes_accessed=10 * total * width,
            transcendentals=heads * total * total,
        ),
        name="attend",
    )(packed[:, :width], packed[:, width : 2 * width], packed[:, 2 * width :])


def attend_back_rows(
    heads, chunk, queries, grads, full, sums, k_ref, v_ref, kt_ref, dk_sum, dv_sum
):
    total = k_ref.shape[0]
    scale = HEAD_DIM**-0.5
    products = (grads.astype(f32) * full).T
    query_heads = [pick_head(queries, head, heads) for head in range(heads)]
    grad_heads = [pick_head(grads, head, heads) for head in range(heads)]
    inner = [
        jnp.sum(products[head * HEAD_DIM : (head + 1) * HEAD_DIM], axis=0, keepdims=True) * scale
        for head in range(heads)
    ]
    query_grads = [None] * heads
    for start in range(0, total, chunk):
        rows = slice(start, start + chunk)
        keys = k_ref[rows, :]
        values = v_ref[rows, :]
        value_part = None
        key_part = None
        for head in range(heads):
            scores = lax.dot_general(
                keys, query_heads[head] * bf16(scale), NT, preferred_element_type=f32
            )
            probs = jnp.exp(scores - sums[head])
            prob_grad = lax.dot_general(
                values, grad_heads[head] * bf16(scale), NT, preferred_element_type=f32
            )
            score_grad = (probs * (prob_grad - inner[head])).astype(bf16)
            one = jnp.dot(probs.astype(bf16), grad_heads[head], preferred_element_type=f32)
            two = jnp.dot(score_grad, query_heads[head], preferred_element_type=f32)
            value_part = one if value_part is None else value_part + one
            key_part = two if key_part is None else key_part + two
            three = jnp.dot(
                kt_ref[head * HEAD_DIM : (head + 1) * HEAD_DIM, rows],
                score_grad,
                preferred_element_type=f32,
            )
            query_grads[head] = three if query_grads[head] is None else query_grads[head] + three
        dv_sum[rows, :] += value_part
        dk_sum[rows, :] += key_part
    flipped = query_grads[0] if heads == 1 else jnp.concatenate(query_grads, axis=0)
    return flipped.T.astype(bf16)


def attend_back_kernel(
    heads, q_ref, do_ref, full_ref, lse_ref, k_ref, v_ref, dq_ref, dk_ref, dv_ref, kt_ref, dk_sum, dv_sum
):
    step = pl.program_id(0)

    @pl.when(step == 0)
    def _():
        kt_ref[...] = k_ref[...].T
        dk_sum[...] = jnp.zeros_like(dk_sum)
        dv_sum[...] = jnp.zeros_like(dv_sum)

    sums = [lse_ref[head : head + 1, :] for head in range(heads)]
    dq_ref[...] = attend_back_rows(
        heads, min(1024, k_ref.shape[0]), q_ref[...], do_ref[...], full_ref[...], sums,
        k_ref, v_ref, kt_ref, dk_sum, dv_sum,
    )

    @pl.when(step == pl.num_programs(0) - 1)
    def _():
        dk_ref[...] = dk_sum[...].astype(bf16)
        dv_ref[...] = dv_sum[...].astype(bf16)


def attend_back(grad_out, packed, full, logsum):
    total, width = grad_out.shape
    heads = width // HEAD_DIM
    block = min(256, total)
    row_block = pl.BlockSpec((block, width), lambda i: (i, 0))
    whole = pl.BlockSpec((total, width), lambda i: (0, 0))
    query_grad, key_grad, value_grad = pl.pallas_call(
        partial(attend_back_kernel, heads),
        grid=(total // block,),
        out_shape=(jax.ShapeDtypeStruct((total, width), bf16),) * 3,
        in_specs=[
            row_block,
            row_block,
            row_block,
            pl.BlockSpec((heads, block), lambda i: (0, i)),
            whole,
            whole,
        ],
        out_specs=[row_block, whole, whole],
        scratch_shapes=[
            pltpu.VMEM((width, total), bf16),
            pltpu.VMEM((total, width), f32),
            pltpu.VMEM((total, width), f32),
        ],
        compiler_params=pltpu.CompilerParams(vmem_limit_bytes=BIG),
        cost_estimate=pl.CostEstimate(
            flops=40 * total * total * width,
            bytes_accessed=16 * total * width,
            transcendentals=heads * total * total,
        ),
        name="attend_back",
    )(
        packed[:, :width],
        grad_out,
        full,
        logsum,
        packed[:, width : 2 * width],
        packed[:, 2 * width :],
    )
    return jnp.concatenate((query_grad, key_grad, value_grad), axis=1)


def normed_parts(values):
    center = values - jnp.mean(values, axis=-1, keepdims=True)
    spread = jnp.mean(center * center, axis=-1, keepdims=True)
    inverse = lax.rsqrt(spread + eps_norm)
    return center * inverse, inverse


def norm_grad(unit, inverse, gain, grad):
    scaled = grad * gain
    middle = jnp.mean(scaled, axis=-1, keepdims=True)
    along = jnp.mean(scaled * unit, axis=-1, keepdims=True)
    gain_grad = jnp.sum(grad * unit, axis=0, keepdims=True)
    bias_grad = jnp.sum(grad, axis=0, keepdims=True)
    return inverse * (scaled - middle - unit * along), gain_grad, bias_grad


def gauss_share(values):
    return 0.5 * (1.0 + lax.erf(values * (0.5**0.5)))


def branch_kernel(
    o_ref, x0_ref, gains_ref, out_ref, up_ref, down_ref, head_ref,
    x1_ref, h2_ref, g_ref, act_ref, x2_ref, pred_ref,
):
    step = pl.program_id(0)

    @pl.when(step == 0)
    def _():
        x1_ref[...] = x0_ref[...] + jnp.dot(
            o_ref[...], out_ref[...], preferred_element_type=f32
        )
        unit, _ = normed_parts(x1_ref[...])
        h2_ref[...] = (unit * gains_ref[2:3, :] + gains_ref[3:4, :]).astype(bf16)
        x2_ref[...] = x1_ref[...]

    units = g_ref.shape[1] // 2
    total = None
    for which in range(2):
        some = slice(which * units, (which + 1) * units)
        hidden = jnp.dot(h2_ref[...], up_ref[which], preferred_element_type=f32)
        g_ref[:, some] = hidden
        active = (hidden * gauss_share(hidden)).astype(bf16)
        act_ref[which, 0] = active
        part = jnp.dot(active, down_ref[some, :], preferred_element_type=f32)
        total = part if total is None else total + part
    x2_ref[...] += total

    @pl.when(step == pl.num_programs(0) - 1)
    def _():
        unit, _ = normed_parts(x2_ref[...])
        last = unit * gains_ref[4:5, :] + gains_ref[5:6, :]
        pred_ref[...] = lax.dot_general(
            last, head_ref[5 * V + LEADS + 1 :, :], NT, precision=highest, preferred_element_type=f32
        )


def weight_specs(w_out, w_up, w_down):
    _, width, units = w_up.shape
    return (
        pl.BlockSpec(w_out.shape, lambda i: (0, 0)),
        pl.BlockSpec((2, width, units), lambda i: (i, 0, 0)),
        pl.BlockSpec((2 * units, width), lambda i: (i, 0)),
    )


def branch_forward(attended, x_first, norm_gains, gathered, head):
    w_out, w_up, w_down, _ = gathered
    rows, width = x_first.shape
    parts, units = w_up.shape[0], w_up.shape[2]
    fixed = lambda shape: pl.BlockSpec(shape, lambda i: (0, 0))
    by_units = pl.BlockSpec((rows, 2 * units), lambda i: (0, i))
    by_core = pl.BlockSpec((2, 1, rows, units), lambda i: (0, i, 0, 0))
    columns = 4 * V
    flops = 2 * rows * (width * width + 2 * width * parts * units + 6 * width * columns)
    return pl.pallas_call(
        branch_kernel,
        grid=(parts // 2,),
        out_shape=(
            jax.ShapeDtypeStruct((rows, width), f32),
            jax.ShapeDtypeStruct((rows, width), bf16),
            jax.ShapeDtypeStruct((rows, parts * units), f32),
            jax.ShapeDtypeStruct((2, parts // 2, rows, units), bf16),
            jax.ShapeDtypeStruct((rows, width), f32),
            jax.ShapeDtypeStruct((rows, columns), f32),
        ),
        in_specs=[
            fixed((rows, width)),
            fixed((rows, width)),
            fixed(norm_gains.shape),
            *weight_specs(w_out, w_up, w_down),
            fixed(head.shape),
        ],
        out_specs=[
            fixed((rows, width)),
            fixed((rows, width)),
            by_units,
            by_core,
            fixed((rows, width)),
            fixed((rows, columns)),
        ],
        compiler_params=pltpu.CompilerParams(vmem_limit_bytes=BIG),
        cost_estimate=pl.CostEstimate(
            flops=flops,
            bytes_accessed=4 * width * parts * units + 6 * rows * parts * units,
            transcendentals=rows * parts * units,
        ),
        name="branch_forward",
    )(attended, x_first, norm_gains, w_out, w_up, w_down, head)


def branch_back_kernel(
    dpred_ref, x2_ref, x1_ref, gains_ref, g_ref, out_ref, up_ref, down_ref, head_ref,
    dx2_ref, dg_ref, dx1_ref, low_ref, do_ref, gain_ref, dhead_ref,
    wide_ref, sum_ref,
):
    step = pl.program_id(0)

    @pl.when(step == 0)
    def _():
        grad = dpred_ref[...]
        unit, inverse = normed_parts(x2_ref[...])
        gain = gains_ref[4:5, :]
        last = unit * gain + gains_ref[5:6, :]
        dhead_ref[...] = lax.dot_general(
            grad, last, TN, precision=highest, preferred_element_type=f32
        )
        row_grad = jnp.dot(grad, head_ref[5 * V + LEADS + 1 :, :], precision=highest, preferred_element_type=f32)
        wide, gain_grad, bias_grad = norm_grad(unit, inverse, gain, row_grad)
        gain_ref[...] = jnp.zeros_like(gain_ref)
        gain_ref[4:5, :] = gain_grad
        gain_ref[5:6, :] = bias_grad
        wide_ref[...] = wide
        dx2_ref[...] = wide.astype(bf16)
        sum_ref[...] = jnp.zeros_like(sum_ref)

    units = g_ref.shape[1] // 2
    total = None
    for which in range(2):
        some = slice(which * units, (which + 1) * units)
        active_grad = lax.dot_general(
            dx2_ref[...], down_ref[some, :], NT, preferred_element_type=f32
        )
        hidden = g_ref[:, some]
        slope = gauss_share(hidden) + hidden * (
            jnp.exp(-0.5 * hidden * hidden) * (2.0 * math.pi) ** -0.5
        )
        hidden_grad = (active_grad * slope).astype(bf16)
        dg_ref[which, 0] = hidden_grad
        part = lax.dot_general(hidden_grad, up_ref[which], NT, preferred_element_type=f32)
        total = part if total is None else total + part
    sum_ref[...] += total

    @pl.when(step == pl.num_programs(0) - 1)
    def _():
        unit, inverse = normed_parts(x1_ref[...])
        middle, gain_grad, bias_grad = norm_grad(unit, inverse, gains_ref[2:3, :], sum_ref[...])
        gain_ref[2:3, :] = gain_grad
        gain_ref[3:4, :] = bias_grad
        middle = wide_ref[...] + middle
        dx1_ref[...] = middle
        low_ref[...] = middle.astype(bf16)
        total = lax.dot_general(low_ref[...], out_ref[...], NT, preferred_element_type=f32)
        do_ref[...] = total.astype(bf16)


def branch_backward(pred_grad, x_last, x_mid, norm_gains, hidden, gathered, head):
    w_out, w_up, w_down, _ = gathered
    rows, width = x_last.shape
    parts, units = w_up.shape[0], w_up.shape[2]
    fixed = lambda shape: pl.BlockSpec(shape, lambda i: (0, 0))
    by_units = pl.BlockSpec((rows, 2 * units), lambda i: (0, i))
    by_core = pl.BlockSpec((2, 1, rows, units), lambda i: (0, i, 0, 0))
    columns = 4 * V
    wide = (rows, width)
    flops = 2 * rows * (width * width + 2 * width * parts * units + 12 * width * columns)
    return pl.pallas_call(
        branch_back_kernel,
        grid=(parts // 2,),
        out_shape=(
            jax.ShapeDtypeStruct(wide, bf16),
            jax.ShapeDtypeStruct((2, parts // 2, rows, units), bf16),
            jax.ShapeDtypeStruct(wide, f32),
            jax.ShapeDtypeStruct(wide, bf16),
            jax.ShapeDtypeStruct(wide, bf16),
            jax.ShapeDtypeStruct((6, width), f32),
            jax.ShapeDtypeStruct((columns, width), f32),
        ),
        in_specs=[
            fixed((rows, columns)),
            fixed(wide),
            fixed(wide),
            fixed(norm_gains.shape),
            by_units,
            *weight_specs(w_out, w_up, w_down),
            fixed(head.shape),
        ],
        out_specs=[
            fixed(wide),
            by_core,
            fixed(wide),
            fixed(wide),
            fixed(wide),
            fixed((6, width)),
            fixed((columns, width)),
        ],
        scratch_shapes=[pltpu.VMEM(wide, f32), pltpu.VMEM(wide, f32)],
        compiler_params=pltpu.CompilerParams(vmem_limit_bytes=BIG),
        cost_estimate=pl.CostEstimate(
            flops=flops,
            bytes_accessed=4 * width * parts * units + 6 * rows * parts * units,
            transcendentals=2 * rows * parts * units,
        ),
        name="branch_backward",
    )(pred_grad, x_last, x_mid, norm_gains, hidden, w_out, w_up, w_down, head)


def plane_parts(me):
    return [(move, lax.rem(me + move, 8)) for move in (7, 6, 5, 4, 3, 2, 1)]


def swap_kernel(*refs):
    value_ref, act_ref, dg_ref, o_ref, dx2_ref, h2_ref, dx1_ref = refs[:7]
    rows_ref, act_out, dg_out, o_out, dx2_out, h2_out, dx1_out = refs[7:14]
    send_sem, recv_sem, own_sem = refs[14:]
    dp, level, core = mesh_place()
    me = dp * 2 + core
    rows, width = value_ref.shape[0], value_ref.shape[1] // 8
    near = device_of(dp, level, 1 - core)
    barrier = pltpu.get_barrier_semaphore()
    others = [
        (part, device_of(part // 2, level, lax.rem(part, 2))) for _, part in plane_parts(me)
    ]
    for _, target in others:
        pl.semaphore_signal(barrier, inc=1, device_id=target, device_id_type=MESH)
    pl.semaphore_wait(barrier, 7)
    started = []

    def send(source, target_ref, target):
        slot = len(started)
        copy = pltpu.make_async_remote_copy(
            src_ref=source,
            dst_ref=target_ref,
            send_sem=send_sem.at[slot],
            recv_sem=recv_sem.at[slot],
            device_id=target,
            device_id_type=MESH,
        )
        copy.start()
        started.append(copy)

    def row_block(part):
        return rows_ref.at[pl.ds(pl.multiple_of(part * rows, rows), rows), :]

    def column_block(ref, part):
        return ref.at[:, pl.ds(pl.multiple_of(part * width, width), width)]

    for part, target in others:
        send(column_block(value_ref, part), row_block(me), target)
    locals_ = []

    def keep(source, target_ref):
        copy = pltpu.make_async_copy(source, target_ref, own_sem.at[len(locals_)])
        copy.start()
        locals_.append(copy)

    for source, out in ((act_ref, act_out), (dg_ref, dg_out)):
        send(source.at[1 - core], out.at[1], near)
        keep(source.at[core], out.at[0])
    for index in range(4):
        send(column_block(o_ref, index * 2 + 1 - core), o_out.at[1, index], near)
        keep(column_block(o_ref, index * 2 + core), o_out.at[0, index])
    for source, out in ((dx2_ref, dx2_out), (h2_ref, h2_out), (dx1_ref, dx1_out)):
        send(source, out, near)
    row_block(me)[...] = column_block(value_ref, me)[...]
    for copy in started:
        copy.wait()
    for copy in locals_:
        copy.wait()


def exchange_swap(value, act, dg, attended, dx2, h2, dx1):
    rows, width = value.shape
    anywhere = pl.BlockSpec(memory_space=pl.ANY)
    outs = [
        (8 * rows, width // 8), act.shape, dg.shape, (2, 4, rows, width // 8),
        dx2.shape, h2.shape, dx1.shape,
    ]
    return pl.pallas_call(
        swap_kernel,
        out_shape=[jax.ShapeDtypeStruct(shape, bf16) for shape in outs],
        in_specs=[VMEM] * 7,
        out_specs=[VMEM] + [anywhere] * 6,
        scratch_shapes=[
            pltpu.SemaphoreType.DMA((16,)),
            pltpu.SemaphoreType.DMA((16,)),
            pltpu.SemaphoreType.DMA((6,)),
        ],
        compiler_params=pltpu.CompilerParams(
            collective_id=3, has_side_effects=True, vmem_limit_bytes=BIG
        ),
        name="exchange_swap",
    )(value, act, dg, attended, dx2, h2, dx1)


class Scatter:
    order = (0, 3, 1, 2)

    def __init__(self, refs, sems):
        self.send_ref, self.keep_ref, self.one_ref, self.two_ref, self.own_ref, self.deep_ref = refs
        self.one, self.two, self.deep = sems
        self.dp, self.level, self.core = mesh_place()
        self.x, self.y = lax.rem(self.dp, 2), self.dp // 2
        self.side = device_of(self.dp + 1 - 2 * self.x, self.level, self.core)
        self.down = device_of(lax.rem(self.dp + 2, 4), self.level, self.core)

    def copy(self, source, target_ref, sems, slot, place, target):
        return pltpu.make_async_remote_copy(
            src_ref=source,
            dst_ref=target_ref,
            send_sem=sems.at[0, slot],
            recv_sem=sems.at[1, place],
            device_id=target,
            device_id_type=MESH,
        )

    def first(self, depth):
        target = self.side if depth < 2 else self.down
        return self.copy(
            self.send_ref.at[depth], self.one_ref.at[depth], self.one, depth, depth, target
        )

    def second(self, depth):
        target = self.down if depth < 2 else self.side
        which = 1 - self.y if depth < 2 else 1 - self.x
        return self.copy(
            self.keep_ref.at[depth, which], self.two_ref.at[depth], self.two, depth, depth, target
        )

    def mine(self, depth):
        return self.y if depth < 2 else self.x

    def third(self, depth):
        place = lax.rem(self.level + 7 - depth, 4)
        return self.copy(
            self.keep_ref.at[depth, self.mine(depth)], self.deep_ref.at[place], self.deep, depth,
            place, device_of(self.dp, depth, self.core),
        )

    def begin(self, depth, products, held_ref):
        height = self.keep_ref.shape[2]
        top = 0
        for product in products:
            rows, size = product.shape[0], product.shape[1] // 4
            for split in range(4):
                held_ref[split, top : top + rows, :] = product[
                    :, split * size : (split + 1) * size
                ].astype(bf16)
            top += rows
        for which in range(2):
            if depth < 2:
                moved, stays = which * 2 + 1 - self.x, which * 2 + self.x
            else:
                moved, stays = (1 - self.y) * 2 + which, self.y * 2 + which
            self.send_ref[depth, which] = held_ref[moved, :height, :]
            self.keep_ref[depth, which] = held_ref[stays, :height, :]
        self.first(depth).start()

    def middle(self, depth):
        self.first(depth).wait_recv()
        for which in range(2):
            self.keep_ref[depth, which] = (
                self.keep_ref[depth, which].astype(f32) + self.one_ref[depth, which].astype(f32)
            ).astype(bf16)
        self.second(depth).start()

    def end(self, depth):
        self.second(depth).wait_recv()
        total = self.keep_ref[depth, self.mine(depth)].astype(f32) + self.two_ref[depth].astype(f32)

        @pl.when(self.level == depth)
        def _():
            self.own_ref[...] = total

        @pl.when(self.level != depth)
        def _():
            self.keep_ref[depth, self.mine(depth)] = total.astype(bf16)
            self.third(depth).start()

    def finish(self, result_ref):
        for place in range(3):
            self.copy(
                self.keep_ref.at[0, 0], self.deep_ref.at[place], self.deep, 0, place, self.side
            ).wait_recv()
        result_ref[...] = self.own_ref[...] + (
            self.deep_ref[0].astype(f32) + self.deep_ref[1].astype(f32) + self.deep_ref[2].astype(f32)
        )
        for depth in range(4):
            self.first(depth).wait_send()
            self.second(depth).wait_send()

            @pl.when(self.level != depth)
            def _(depth=depth):
                self.third(depth).wait_send()


def scatter_scratch(height, share):
    return [
        pltpu.VMEM((4, 2, height, share), bf16),
        pltpu.VMEM((4, 2, height, share), bf16),
        pltpu.VMEM((4, 2, height, share), bf16),
        pltpu.VMEM((4, height, share), bf16),
        pltpu.VMEM((height, share), f32),
        pltpu.VMEM((3, height, share), bf16),
        pltpu.VMEM((4, height, share), bf16),
        pltpu.SemaphoreType.DMA((2, 4)),
        pltpu.SemaphoreType.DMA((2, 4)),
        pltpu.SemaphoreType.DMA((2, 4)),
    ]


def summed(lefts, rights):
    total = None
    for left, right in zip(lefts, rights):
        part = lax.dot_general(left, right, TN, preferred_element_type=f32)
        total = part if total is None else total + part
    return total


def chunk_spec(shape):
    def where(i):
        index = jnp.minimum(i, 3)
        first, last = (3 - index) // 3, index // 3
        middle = 1 - first - last
        return 0, middle * (5 - 2 * index) + 2 * last, 0, 0

    return pl.BlockSpec((2, 1) + shape, where)


def once(shape):
    return pl.BlockSpec(shape, lambda i: (0,) * len(shape), pipeline_mode=pl.Buffered(1))


class Returns:
    def __init__(self, grads_ref, token_out, width, sems, own_sem):
        self.grads_ref, self.token_out, self.width = grads_ref, token_out, width
        self.sems, self.own_sem = sems, own_sem
        dp, self.level, core = mesh_place()
        self.me = dp * 2 + core
        self.rows = grads_ref.shape[0] // 8

    def part(self, move):
        return lax.rem(self.me + move, 8)

    def refs(self, part, start, size):
        rows = pl.ds(pl.multiple_of(part * self.rows, self.rows), self.rows)
        first = self.me * 3 * self.width + start
        columns = pl.ds(pl.multiple_of(first, self.width), size)
        return self.grads_ref.at[rows, start : start + size], self.token_out.at[:, columns]

    def copy(self, move, late):
        start, size = (self.width, 2 * self.width) if late else (0, self.width)
        part = self.part(move)
        source, target_ref = self.refs(part, start, size)
        return pltpu.make_async_remote_copy(
            src_ref=source,
            dst_ref=target_ref,
            send_sem=self.sems.at[2 * late, move],
            recv_sem=self.sems.at[2 * late + 1, move],
            device_id=device_of(part // 2, self.level, lax.rem(part, 2)),
            device_id_type=MESH,
        )

    def own(self):
        source, target_ref = self.refs(self.me, 0, 3 * self.width)
        return pltpu.make_async_copy(source, target_ref, self.own_sem)

    def peers(self):
        parts = [self.part(move) for move in range(1, 8)]
        return [device_of(part // 2, self.level, lax.rem(part, 2)) for part in parts]

    def finish(self):
        for move in range(1, 8):
            self.copy(move, 0).wait()
            self.copy(move, 1).wait()
        self.own().wait()


def attend_turns(turn, returns, qkv_ref, do_ref, full_ref, lse_ref, dqkv_ref, kt_ref, dk_sum, dv_sum):
    width = do_ref.shape[1]
    heads = width // HEAD_DIM
    rows = returns.rows

    @pl.when(turn == 0)
    def _():
        kt_ref[...] = qkv_ref[:, width : 2 * width].T
        dk_sum[...] = jnp.zeros_like(dk_sum)
        dv_sum[...] = jnp.zeros_like(dv_sum)

    @pl.when((turn >= 0) & (turn < 8))
    def _():
        part = returns.part(turn + 1)
        where = pl.ds(pl.multiple_of(part * rows, rows), rows)
        sums = [lse_ref[head : head + 1, where] for head in range(heads)]
        dqkv_ref[where, :width] = attend_back_rows(
            heads, 1024, qkv_ref[where, :width], do_ref[where, :], full_ref[where, :], sums,
            qkv_ref.at[:, width : 2 * width], qkv_ref.at[:, 2 * width :], kt_ref, dk_sum, dv_sum,
        )

    @pl.when((turn >= 0) & (turn < 7))
    def _():
        returns.copy(turn + 1, 0).start()

    @pl.when(turn == 8)
    def _():
        dqkv_ref[:, width : 2 * width] = dk_sum[...].astype(bf16)
        dqkv_ref[:, 2 * width :] = dv_sum[...].astype(bf16)
        for move in (7, 6, 5, 4, 3, 2, 1):
            returns.copy(move, 1).start()
        returns.own().start()


def attend_exchange_kernel(
    qkv_ref, do_ref, full_ref, lse_ref, rows_ref, token_out, grad_ref,
    dqkv_ref, kt_ref, dk_sum, dv_sum, sems, own_sem,
):
    turn = pl.program_id(0)
    returns = Returns(dqkv_ref, token_out, do_ref.shape[1], sems, own_sem)

    @pl.when(turn == 0)
    def _():
        barrier = pltpu.get_barrier_semaphore()
        for target in returns.peers():
            pl.semaphore_signal(barrier, inc=1, device_id=target, device_id_type=MESH)
        pl.semaphore_wait(barrier, 7)

    attend_turns(
        turn, returns, qkv_ref, do_ref, full_ref, lse_ref, dqkv_ref, kt_ref, dk_sum, dv_sum
    )

    @pl.when(turn >= pieces_at)
    def _():
        grad_ref[...] = lax.dot_general(
            rows_ref[...], dqkv_ref[...], TN, preferred_element_type=f32
        )

    @pl.when(turn == pieces_at + 3)
    def _():
        returns.finish()


def attend_exchange(packed, own_grad, full, logsum, rows_one):
    rows, width = own_grad.shape[0] // 8, own_grad.shape[1]
    piece = lambda i: jnp.clip(i - pieces_at, 0, 3)
    return pl.pallas_call(
        attend_exchange_kernel,
        grid=(pieces_at + 4,),
        out_shape=[
            jax.ShapeDtypeStruct((rows, 24 * width), bf16),
            jax.ShapeDtypeStruct((D, 3 * width), f32),
        ],
        in_specs=[
            once(packed.shape),
            once(own_grad.shape),
            once(full.shape),
            once(logsum.shape),
            pl.BlockSpec((8 * rows, D // 4), lambda i: (0, piece(i))),
        ],
        out_specs=[
            pl.BlockSpec(memory_space=pl.ANY),
            pl.BlockSpec((D // 4, 3 * width), lambda i: (piece(i), 0)),
        ],
        scratch_shapes=[
            pltpu.VMEM((8 * rows, 3 * width), bf16),
            pltpu.VMEM((width, 8 * rows), bf16),
            pltpu.VMEM((8 * rows, width), f32),
            pltpu.VMEM((8 * rows, width), f32),
            pltpu.SemaphoreType.DMA((4, 8)),
            pltpu.SemaphoreType.DMA,
        ],
        compiler_params=pltpu.CompilerParams(
            collective_id=8, has_side_effects=True, vmem_limit_bytes=BIG
        ),
        name="attend_exchange",
    )(packed, own_grad, full, logsum, rows_one)


pieces_at, entry_turns, attend_from = 9, 11, 4
middle_at, end_at = (5, 6, 8, 9), (7, 8, 10, 11)


def finish_kernel(*refs):
    steps = (refs[0:3], refs[3:6])
    qkv_ref, do_ref, full_ref, lse_ref, rows_ref, prev_ref = refs[6:12]
    token_out, share_ref, down_ref = refs[12:15]
    dqkv_ref, kt_ref, dk_sum, dv_sum, piece_send, piece_recv, piece_own = refs[15:22]
    part_sem, piece_sem, own_sem = refs[22:25]
    scatter = Scatter(refs[25:31], refs[32:35])
    held_ref = refs[31]
    turn = pl.program_id(0)
    dp, level, core = mesh_place()
    width = do_ref.shape[1]
    returns = Returns(dqkv_ref, token_out, width, part_sem, own_sem)

    def remote(source, target_ref, send_sem, recv_sem, target):
        return pltpu.make_async_remote_copy(
            src_ref=source,
            dst_ref=target_ref,
            send_sem=send_sem,
            recv_sem=recv_sem,
            device_id=target,
            device_id_type=MESH,
        )

    def piece_copy(index):
        place = lax.rem(level + 7 - index, 4)
        return remote(
            piece_send.at[index], piece_recv.at[place], piece_sem.at[0, index],
            piece_sem.at[1, place], device_of(dp, index, core),
        )

    @pl.when(turn == 0)
    def _():
        barrier = pltpu.get_barrier_semaphore()
        deep = [device_of(dp, lax.rem(level + move, 4), core) for move in (1, 2, 3)]
        for target in returns.peers() + deep:
            pl.semaphore_signal(barrier, inc=1, device_id=target, device_id_type=MESH)
        pl.semaphore_wait(barrier, 10)

    for index, depth in enumerate(scatter.order):

        @pl.when(turn == index)
        def _(depth=depth):
            lefts, rights = [], []
            for act, dx2, dx2_near in steps:
                lefts += [act[0, 0], act[1, 0]]
                rights += [dx2[...], dx2_near[...]]
            scatter.begin(depth, [summed(lefts, rights)], held_ref)

        @pl.when(turn == middle_at[index])
        def _(depth=depth):
            scatter.middle(depth)

        @pl.when(turn == end_at[index])
        def _(depth=depth):
            scatter.end(depth)

    attend_turns(
        turn - attend_from, returns, qkv_ref, do_ref, full_ref, lse_ref, dqkv_ref, kt_ref, dk_sum, dv_sum
    )

    for index in range(4):

        @pl.when(turn == attend_from + pieces_at + index)
        def _(index=index):
            piece = prev_ref[...] + lax.dot_general(
                rows_ref[...], dqkv_ref[...], TN, preferred_element_type=f32
            )

            @pl.when(level == index)
            def _():
                piece_own[...] = piece

            @pl.when(level != index)
            def _():
                piece_send[index] = piece.astype(bf16)
                piece_copy(index).start()

    @pl.when(turn == attend_from + pieces_at + 4)
    def _():
        scatter.finish(down_ref)
        for place in range(3):
            remote(
                piece_send.at[0], piece_recv.at[place], piece_sem.at[0, 0],
                piece_sem.at[1, place], scatter.side,
            ).wait_recv()
        share_ref[...] = piece_own[...] + (
            piece_recv[0].astype(f32) + piece_recv[1].astype(f32) + piece_recv[2].astype(f32)
        )
        returns.finish()
        for index in range(4):

            @pl.when(level != index)
            def _(index=index):
                piece_copy(index).wait_send()


def finish_program(kept, packed, own_grad, full, logsum, rows_one, earlier):
    rows, width = own_grad.shape[0] // 8, own_grad.shape[1]
    in_specs, operands = [], []
    for act, dx2, dx2_near in kept:
        operands += [act, dx2, dx2_near]
        in_specs += [chunk_spec(act.shape[2:]), once(dx2.shape), once(dx2.shape)]
    piece = lambda i: jnp.clip(i - attend_from - pieces_at, 0, 3)
    in_specs += [
        once(packed.shape),
        once(own_grad.shape),
        once(full.shape),
        once(logsum.shape),
        pl.BlockSpec((8 * rows, D // 4), lambda i: (0, piece(i))),
        pl.BlockSpec((D // 4, 3 * width), lambda i: (piece(i), 0)),
    ]
    operands += [packed, own_grad, full, logsum, rows_one, earlier]
    fixed = lambda shape: pl.BlockSpec(shape, lambda i: (0, 0))
    units = kept[0][0].shape[3]
    share = D // 4
    return pl.pallas_call(
        finish_kernel,
        grid=(attend_from + pieces_at + 5,),
        out_shape=[
            jax.ShapeDtypeStruct((rows, 24 * width), bf16),
            jax.ShapeDtypeStruct((share, 3 * width), f32),
            jax.ShapeDtypeStruct((units, share), f32),
        ],
        in_specs=in_specs,
        out_specs=[
            pl.BlockSpec(memory_space=pl.ANY),
            fixed((share, 3 * width)),
            fixed((units, share)),
        ],
        scratch_shapes=[
            pltpu.VMEM((8 * rows, 3 * width), bf16),
            pltpu.VMEM((width, 8 * rows), bf16),
            pltpu.VMEM((8 * rows, width), f32),
            pltpu.VMEM((8 * rows, width), f32),
            pltpu.VMEM((4, share, 3 * width), bf16),
            pltpu.VMEM((3, share, 3 * width), bf16),
            pltpu.VMEM((share, 3 * width), f32),
            pltpu.SemaphoreType.DMA((4, 8)),
            pltpu.SemaphoreType.DMA((2, 4)),
            pltpu.SemaphoreType.DMA,
        ]
        + scatter_scratch(units, share),
        compiler_params=pltpu.CompilerParams(
            collective_id=4, has_side_effects=True, vmem_limit_bytes=BIG
        ),
        name="finish_program",
    )(*operands)


def tie(*values):
    return lax.optimization_barrier(values)


def choose(value, index, axis=0):
    return lax.dynamic_index_in_dim(value, index, axis, keepdims=False)


def outer_plain(lefts, rights, by_rows):
    dp, mp = lax.axis_size("dp"), lax.axis_size("mp")
    grads = sum(
        lax.dot_general(left, right, TN, preferred_element_type=f32)
        for left, right in zip(lefts, rights)
    ).astype(bf16)
    rows, width = grads.shape
    if by_rows:
        grads = grads.reshape(dp, rows // dp, mp, width // mp).transpose(0, 2, 1, 3)
    else:
        grads = grads.reshape(mp, rows // mp, dp, width // dp).transpose(2, 0, 1, 3)
    grads = grads.reshape((dp * mp,) + grads.shape[2:])
    return lax.psum_scatter(grads, ("dp", "mp"), scatter_dimension=0, tiled=False).astype(f32)


def exchange_sum_kernel(
    x_ref, loss_ref, qkv_ref, up_out_ref, down_ref, o_ref, s_ref, work_ref, pair_ref, quad_ref, eight_ref, deep_ref, tile_ref,
    send_sem, recv_sem,
):
    dp, level, core = mesh_place()
    x, y = lax.rem(dp, 2), dp // 2
    side = device_of(dp + 1 - 2 * x, level, core)
    down = device_of(lax.rem(dp + 2, 4), level, core)
    near = device_of(dp, level, 1 - core)
    deep = [device_of(dp, lax.rem(level + step, 4), core) for step in (1, 2, 3)]
    barrier = pltpu.get_barrier_semaphore()
    for target in (side, down, near, *deep):
        pl.semaphore_signal(barrier, inc=1, device_id=target, device_id_type=MESH)
    pl.semaphore_wait(barrier, 6)
    started = []

    def send(source, target_ref, target):
        slot = len(started)
        copy = pltpu.make_async_remote_copy(
            src_ref=source,
            dst_ref=target_ref,
            send_sem=send_sem.at[slot],
            recv_sem=recv_sem.at[slot],
            device_id=target,
            device_id_type=MESH,
        )
        copy.start()
        started.append(copy)
        return copy

    half = x_ref.shape[0] // 2
    quarter, eighth, part, unit = half // 2, half // 4, half // 8, half // 16

    def rows(start, size):
        return pl.ds(pl.multiple_of(start, unit), size)

    copy = send(x_ref.at[rows((1 - core) * half, half)], pair_ref, near)
    copy.wait_recv()
    work_ref[...] = x_ref[rows(core * half, half)] + pair_ref[...]
    one = send(work_ref.at[rows((1 - x) * eighth, eighth)], quad_ref.at[0], side)
    two = send(work_ref.at[rows(quarter + (1 - y) * eighth, eighth)], quad_ref.at[1], down)
    base_a = x * eighth
    base_b = quarter + y * eighth
    wide_a, wide_b = core * half + base_a, core * half + base_b
    one.wait_recv()
    work_ref[rows(base_a, eighth)] += quad_ref[0]
    one = send(work_ref.at[rows(base_a + (1 - y) * part, part)], eight_ref.at[0], down)
    two.wait_recv()
    work_ref[rows(base_b, eighth)] += quad_ref[1]
    two = send(work_ref.at[rows(base_b + (1 - x) * part, part)], eight_ref.at[1], side)
    base_a = base_a + y * part
    base_b = base_b + x * part
    one.wait_recv()
    work_ref[rows(base_a, part)] += eight_ref[0]
    two.wait_recv()
    work_ref[rows(base_b, part)] += eight_ref[1]

    def level_start(which):
        late = which // 2
        return (1 - late) * base_a + late * base_b + lax.rem(which, 2) * unit

    copies = []
    for step in (1, 2, 3):
        source = work_ref.at[rows(level_start(lax.rem(level + step, 4)), unit)]
        copies.append(send(source, deep_ref.at[step - 1], deep[step - 1]))
    for copy in copies:
        copy.wait_recv()
    total = work_ref[rows(level_start(level), unit)] + deep_ref[0] + deep_ref[1] + deep_ref[2]
    mine = rows(core * half + level_start(level), unit)
    base_a = core * half + base_a
    base_b = core * half + base_b
    o_ref[mine] = total
    row = lax.broadcasted_iota(jnp.int32, s_ref.shape, 0)
    squares = jnp.sum(total * total)
    for ref in (qkv_ref, up_out_ref, down_ref):
        squares += jnp.sum(ref[...] * ref[...])
    tile_ref[0] = jnp.where(row == 0, squares, jnp.where(row == 1, loss_ref[...], 0.0))
    copies = []
    for step in (1, 2, 3):
        copies.append(send(o_ref.at[mine], o_ref.at[mine], deep[step - 1]))
        copies.append(send(tile_ref.at[0], tile_ref.at[step], deep[step - 1]))
    for copy in copies:
        copy.wait_recv()
    one = send(o_ref.at[rows(base_a, part)], o_ref.at[rows(base_a, part)], down)
    two = send(o_ref.at[rows(base_b, part)], o_ref.at[rows(base_b, part)], side)
    tile_ref[4] = tile_ref[0] + tile_ref[1] + tile_ref[2] + tile_ref[3]
    three = send(tile_ref.at[4], tile_ref.at[5], side)
    one.wait_recv()
    one = send(o_ref.at[rows(wide_a, eighth)], o_ref.at[rows(wide_a, eighth)], side)
    two.wait_recv()
    two = send(o_ref.at[rows(wide_b, eighth)], o_ref.at[rows(wide_b, eighth)], down)
    three.wait_recv()
    tile_ref[6] = tile_ref[4] + tile_ref[5]
    three = send(tile_ref.at[6], tile_ref.at[7], down)
    one.wait_recv()
    two.wait_recv()
    one = send(o_ref.at[rows(core * half, half)], o_ref.at[rows(core * half, half)], near)
    three.wait_recv()
    tile_ref[8] = tile_ref[6] + tile_ref[7]
    three = send(tile_ref.at[8], tile_ref.at[9], near)
    one.wait_recv()
    three.wait_recv()
    s_ref[...] = tile_ref[8] + tile_ref[9]
    for copy in started:
        copy.wait_send()


def exchange_sum(value, loss, *shares):
    rows, width = value.shape
    tile = jax.ShapeDtypeStruct((8, 128), f32)
    return pl.pallas_call(
        exchange_sum_kernel,
        out_shape=(jax.ShapeDtypeStruct(value.shape, f32), tile),
        in_specs=[VMEM] * 5,
        out_specs=[VMEM, VMEM],
        scratch_shapes=[
            pltpu.VMEM((rows // 2, width), f32),
            pltpu.VMEM((rows // 2, width), f32),
            pltpu.VMEM((2, rows // 8, width), f32),
            pltpu.VMEM((2, rows // 16, width), f32),
            pltpu.VMEM((3, rows // 32, width), f32),
            pltpu.VMEM((10,) + tile.shape, f32),
            pltpu.SemaphoreType.DMA((24,)),
            pltpu.SemaphoreType.DMA((24,)),
        ],
        compiler_params=pltpu.CompilerParams(
            collective_id=5, has_side_effects=True, vmem_limit_bytes=BIG
        ),
        name="exchange_sum",
    )(value, loss.reshape(1, 1), *shares)


def split_low(values):
    high = values.astype(bf16)
    return high, (values - high.astype(f32)).astype(bf16)


def three_products(left, right, dims=(((1,), (0,)), ((), ()))):
    def product(one, two):
        return lax.dot_general(one, two, dims, preferred_element_type=f32)

    return product(left[0], right[0]) + (product(left[1], right[0]) + product(left[0], right[1]))


def exact_product(left, right, dims=(((1,), (0,)), ((), ()))):
    return lax.dot_general(left, right, dims, precision=highest, preferred_element_type=f32)


def head_marks(width):
    head = lax.broadcasted_iota(jnp.int32, (HEADS, width), 0)
    column = lax.broadcasted_iota(jnp.int32, (HEADS, width), 1)
    return jnp.where(column // HEAD_DIM == head, 1.0, 0.0).astype(f32)


def quarter_marks(padded):
    row = lax.broadcasted_iota(jnp.int32, (padded, V), 0)
    column = lax.broadcasted_iota(jnp.int32, (padded, V), 1)
    return jnp.where(row // 4 == column, 0.25, 0.0).astype(f32)


def tables_kernel(tables_ref, hot_ref, patch_ref, var_ref, keyed_ref, bias_ref):
    padded, width = patch_ref.shape
    query = tables_ref[5 * V + LEADS : 5 * V + LEADS + 1, :]
    patch_ref[...] = jnp.zeros_like(patch_ref)
    patch_ref[: 4 * V, :] = tables_ref[: 4 * V, :]
    chosen = exact_product(hot_ref[...], tables_ref[4 * V : 5 * V, :])
    var_ref[...] = exact_product(quarter_marks(padded), chosen)
    marks = head_marks(width)
    scale = HEAD_DIM**-0.5
    keyed_ref[...] = exact_product(marks, patch_ref[...] * query, NT) * scale
    bias = exact_product(marks, var_ref[...] * query, NT) * (4.0 * scale)
    column = lax.broadcasted_iota(jnp.int32, bias.shape, 1)
    bias_ref[...] = jnp.where(column < 4 * V, bias, -1e30)


def prepare_tables(tables, var_hot):
    padded = 256
    return pl.pallas_call(
        tables_kernel,
        out_shape=(
            jax.ShapeDtypeStruct((padded, D), f32),
            jax.ShapeDtypeStruct((padded, D), f32),
            jax.ShapeDtypeStruct((HEADS, padded), f32),
            jax.ShapeDtypeStruct((HEADS, padded), f32),
        ),
        compiler_params=pltpu.CompilerParams(vmem_limit_bytes=BIG),
        name="prepare_tables",
    )(tables, var_hot)


def four_sum(values):
    size = values.shape[1]
    lane = lax.broadcasted_iota(jnp.int32, values.shape, 1)
    values = values + jnp.where(
        lane % 2 == 0, pltpu.roll(values, size - 1, 1), pltpu.roll(values, 1, 1)
    )
    return values + jnp.where(
        lane % 4 < 2, pltpu.roll(values, size - 2, 1), pltpu.roll(values, 2, 1)
    )


def cell_shares(cells, keyed, bias):
    scores = four_sum(cells * keyed) + bias
    raised = jnp.exp(scores - jnp.max(scores, axis=1, keepdims=True))
    total = jnp.sum(raised, axis=1, keepdims=True) * 0.25
    return raised * (1.0 / total)


def embed_pair(pair, cells, keyed_ref, bias_ref, patch_ref, var_ref, x0_ref):
    patch = split_low(patch_ref[...])
    variable = split_low(var_ref[...])
    outs = []
    for which in range(2):
        row = pl.ds(pair * 2 + which, 1)
        shares = cell_shares(cells, keyed_ref[row, :], bias_ref[row, :])
        outs.append(
            three_products(split_low(shares * cells), patch)
            + three_products(split_low(shares), variable)
        )
    lane = lax.broadcasted_iota(jnp.int32, outs[0].shape, 1)
    columns = pl.ds(pl.multiple_of(pair * 2 * HEAD_DIM, 2 * HEAD_DIM), 2 * HEAD_DIM)
    x0_ref[:, columns] = jnp.where(lane < HEAD_DIM, outs[0], outs[1])


def embed_kernel(
    u_ref, keyed_ref, bias_ref, patch_ref, var_ref, lead_ref, gains_ref, x0_ref, h1_ref
):
    pair = pl.program_id(0)
    embed_pair(pair, u_ref[...], keyed_ref, bias_ref, patch_ref, var_ref, x0_ref)

    @pl.when(pair == pl.num_programs(0) - 1)
    def _():
        x0_ref[...] += lead_ref[...]
        unit, _ = normed_parts(x0_ref[...])
        h1_ref[...] = (unit * gains_ref[0:1, :] + gains_ref[1:2, :]).astype(bf16)


def embed_forward(cells, prepared, lead_row, norm_gains):
    patch, variable, keyed, bias = prepared
    rows, padded = cells.shape
    fixed = lambda shape: pl.BlockSpec(shape, lambda i: (0, 0))
    by_pair = pl.BlockSpec((padded, 2 * HEAD_DIM), lambda i: (0, i))
    return pl.pallas_call(
        embed_kernel,
        grid=(HEADS // 2,),
        out_shape=(
            jax.ShapeDtypeStruct((rows, D), f32),
            jax.ShapeDtypeStruct((rows, D), bf16),
        ),
        in_specs=[
            fixed((rows, padded)),
            fixed(keyed.shape),
            fixed(bias.shape),
            by_pair,
            by_pair,
            fixed((1, D)),
            fixed(norm_gains.shape),
        ],
        out_specs=[fixed((rows, D)), fixed((rows, D))],
        compiler_params=pltpu.CompilerParams(vmem_limit_bytes=BIG),
        cost_estimate=pl.CostEstimate(
            flops=24 * rows * padded * D, bytes_accessed=14 * rows * D, transcendentals=16 * rows * padded
        ),
        name="embed_forward",
    )(cells, keyed, bias, patch, variable, lead_row, norm_gains)


def entry_rows(
    grad_ref, qkv_ref, x0_ref, mid_ref, gains_ref, du_ref, gain_ref, lead_ref, dx_ref, flip_ref
):
    row_grad = jnp.dot(grad_ref[...], qkv_ref[...], preferred_element_type=f32)
    unit, inverse = normed_parts(x0_ref[...])
    part, gain_grad, bias_grad = norm_grad(unit, inverse, gains_ref[0:1, :], row_grad)
    total = mid_ref[...] + part
    dx_ref[...] = total
    flip_ref[...] = total.T
    lead_ref[...] = jnp.sum(total, axis=0, keepdims=True)
    gain_ref[0:1, :] = gain_grad
    gain_ref[1:2, :] = bias_grad
    du_ref[...] = jnp.zeros_like(du_ref)


def entry_pair(
    pair, u_ref, keyed_ref, bias_ref, patch_ref, var_ref,
    du_ref, dpatch_ref, dvar_ref, dkeyed_ref, dbias_ref, dx_ref, flip_ref,
):
    cells = u_ref[...]
    size = 2 * HEAD_DIM
    columns = pl.ds(pl.multiple_of(pair * size, size), size)
    grads = dx_ref[:, columns]
    lane = lax.broadcasted_iota(jnp.int32, grads.shape, 1)
    patch = split_low(patch_ref[...])
    variable = split_low(var_ref[...])
    cells_grad = None
    for which in range(2):
        row = pl.ds(pair * 2 + which, 1)
        keyed = keyed_ref[row, :]
        shares = cell_shares(cells, keyed, bias_ref[row, :])
        one = split_low(jnp.where(lane // HEAD_DIM == which, grads, 0.0))
        mixed_grad = three_products(one, patch, NT)
        share_grad = mixed_grad * cells + three_products(one, variable, NT)
        weighted = shares * share_grad
        inner = jnp.sum(weighted, axis=1, keepdims=True)
        score_grad = four_sum(weighted) - shares * inner
        piece = mixed_grad * shares + score_grad * keyed
        cells_grad = piece if cells_grad is None else cells_grad + piece
        scale = HEAD_DIM**-0.5
        dkeyed_ref[row, :] = jnp.sum(score_grad * cells, axis=0, keepdims=True) * scale
        dbias_ref[row, :] = jnp.sum(score_grad, axis=0, keepdims=True) * scale
        rows = pl.ds(pl.multiple_of(pair * size + which * HEAD_DIM, HEAD_DIM), HEAD_DIM)
        flipped = split_low(flip_ref[rows, :])
        mine = slice(which * HEAD_DIM, (which + 1) * HEAD_DIM)
        dpatch_ref[mine, :] = three_products(flipped, split_low(shares * cells))
        dvar_ref[mine, :] = three_products(flipped, split_low(shares))
    du_ref[...] += cells_grad


def entry_back_kernel(
    grad_ref, qkv_ref, x0_ref, mid_ref, gains_ref, u_ref, keyed_ref, bias_ref, patch_ref, var_ref,
    du_ref, gain_ref, lead_ref, dpatch_ref, dvar_ref, dkeyed_ref, dbias_ref,
    dx_ref, flip_ref,
):
    pair = pl.program_id(0)

    @pl.when(pair == 0)
    def _():
        entry_rows(
            grad_ref, qkv_ref, x0_ref, mid_ref, gains_ref, du_ref, gain_ref, lead_ref, dx_ref,
            flip_ref,
        )

    size = 2 * HEAD_DIM
    for which in range(2):
        some = slice(which * size, (which + 1) * size)
        entry_pair(
            pair * 2 + which, u_ref, keyed_ref, bias_ref, patch_ref.at[:, some],
            var_ref.at[:, some], du_ref, dpatch_ref.at[some, :], dvar_ref.at[some, :],
            dkeyed_ref, dbias_ref, dx_ref, flip_ref,
        )


def entry_last_kernel(*refs):
    steps = (refs[0:6], refs[6:12])
    share_ref = refs[12]
    grad_ref, qkv_ref, x0_ref, mid_ref, gains_ref, u_ref, keyed_ref, bias_ref = refs[13:21]
    patch_ref, var_ref, query_ref, hot_ref, lead_hot_ref, head_a, head_b, high_a, high_b = refs[21:30]
    patch_a, var_a, keyed_a, bias_a, lead_a, gain_a = refs[30:36]
    rows_out, up_out_ref, qkv_share_ref = refs[36:39]
    (dx_ref, flip_ref, low_ref, landing_ref, cross_sem, du_ref, gain_ref, lead_ref, dpatch_ref,
     dvar_ref, dkeyed_ref, dbias_ref) = refs[39:51]
    scatter = Scatter(refs[51:57], refs[58:61])
    held_ref = refs[57]
    turn = pl.program_id(0)
    dp, level, core = mesh_place()
    across = device_of(level, dp, core)
    crossing = scatter.copy(low_ref, landing_ref, cross_sem, 0, 0, across)

    @pl.when(turn == 0)
    def _():
        barrier = pltpu.get_barrier_semaphore()
        deep = [device_of(dp, lax.rem(level + move, 4), core) for move in (1, 2, 3)]
        for target in (scatter.side, scatter.down, *deep):
            pl.semaphore_signal(barrier, inc=1, device_id=target, device_id_type=MESH)
        low_ref[...] = share_ref[...]

        @pl.when(dp != level)
        def _():
            pl.semaphore_signal(barrier, inc=1, device_id=across, device_id_type=MESH)
            pl.semaphore_wait(barrier, 6)
            crossing.start()

        @pl.when(dp == level)
        def _():
            pl.semaphore_wait(barrier, 5)

    for index, depth in enumerate(scatter.order):

        @pl.when(turn == index)
        def _(depth=depth):
            lefts, rights, smalls, wides = [], [], [], []
            for dg, o, h2, h2_near, dx1, dx1_near in steps:
                lefts += [dg[0, 0], dg[1, 0]]
                rights += [h2[...], h2_near[...]]
                smalls += [o[0, 0], o[1, 0]]
                wides += [dx1[...], dx1_near[...]]
            scatter.begin(depth, [summed(lefts, rights), summed(smalls, wides)], held_ref)

        @pl.when(turn == index + 3)
        def _(depth=depth):
            scatter.middle(depth)

        @pl.when(turn == index + 6)
        def _(depth=depth):
            scatter.end(depth)

    @pl.when(turn == 0)
    def _():
        entry_rows(
            grad_ref, qkv_ref, x0_ref, mid_ref, gains_ref, du_ref, gain_ref,
            lead_ref.at[0:1, :], dx_ref, flip_ref,
        )

    @pl.when((turn >= 1) & (turn <= HEADS // 2))
    def _():
        size = 2 * HEAD_DIM
        pair = turn - 1
        some = pl.ds(pl.multiple_of(pair * size, size), size)
        entry_pair(
            pair, u_ref, keyed_ref, bias_ref, patch_ref.at[:, some], var_ref.at[:, some],
            du_ref, dpatch_ref.at[some, :], dvar_ref.at[some, :], dkeyed_ref, dbias_ref,
            dx_ref, flip_ref,
        )

    @pl.when(turn == entry_turns - 2)
    def _():
        gain_ref[...] += gain_a[...]
        lead_ref[1:2, :] = lead_a[...]
        lead_ref[2:8, :] = jnp.zeros((6, lead_ref.shape[1]), f32)
        table_rows(
            patch_a, dpatch_ref, var_a, dvar_ref, keyed_a, dkeyed_ref, bias_a, dbias_ref,
            patch_ref, var_ref, query_ref, hot_ref, lead_hot_ref, lead_ref, gain_ref,
            (head_a[...], head_b[...]), (high_a[2:6, :], high_b[2:6, :]), rows_out,
        )

    @pl.when(turn == entry_turns - 1)
    def _():
        @pl.when(dp != level)
        def _():
            crossing.wait()
            qkv_share_ref[...] = landing_ref[...]

        @pl.when(dp == level)
        def _():
            qkv_share_ref[...] = share_ref[...]

        scatter.finish(up_out_ref)


def entry_last(
    kept, share, token_grad, qkv_t, x_first, mid_grad, norm_gains, cells, prepared,
    query, var_hot, lead_hots, heads, highs, earlier,
):
    patch, variable, keyed, bias = prepared
    rows, width = x_first.shape
    padded = cells.shape[1]
    in_specs, operands = [], []
    for dg, o, h2, h2_near, dx1, dx1_near in kept:
        operands += [dg, o, h2, h2_near, dx1, dx1_near]
        in_specs += [chunk_spec(dg.shape[2:]), chunk_spec(o.shape[2:])]
        in_specs += [once(h2.shape)] * 4
    values = [
        share, token_grad, qkv_t, x_first, mid_grad, norm_gains, cells, keyed, bias,
        patch, variable, query, var_hot, lead_hots, *heads, *highs, *earlier,
    ]
    in_specs += [once(value.shape) for value in values]
    height, columns = kept[0][0].shape[3] + kept[0][1].shape[3], width // 4
    outs = [(2 * padded, width), (height, columns), share.shape]
    return pl.pallas_call(
        entry_last_kernel,
        grid=(entry_turns,),
        out_shape=[jax.ShapeDtypeStruct(shape, f32) for shape in outs],
        in_specs=in_specs,
        out_specs=[pl.BlockSpec(shape, lambda i: (0, 0)) for shape in outs],
        scratch_shapes=[
            pltpu.VMEM((rows, width), f32),
            pltpu.VMEM((width, rows), f32),
            pltpu.VMEM(share.shape, f32),
            pltpu.VMEM(share.shape, f32),
            pltpu.SemaphoreType.DMA((2, 1)),
            pltpu.VMEM((rows, padded), f32),
            pltpu.VMEM((2, width), f32),
            pltpu.VMEM((8, width), f32),
            pltpu.VMEM((width, padded), f32),
            pltpu.VMEM((width, padded), f32),
            pltpu.VMEM(keyed.shape, f32),
            pltpu.VMEM(bias.shape, f32),
        ]
        + scatter_scratch(height, columns),
        compiler_params=pltpu.CompilerParams(
            collective_id=6, has_side_effects=True, vmem_limit_bytes=BIG
        ),
        name="entry_last",
    )(*operands, *values)


def entry_backward(token_grad, qkv_t, x_first, mid_grad, norm_gains, cells, prepared):
    patch, variable, keyed, bias = prepared
    rows, width = x_first.shape
    padded = cells.shape[1]
    fixed = lambda shape: pl.BlockSpec(shape, lambda i: (0, 0))
    by_pair = pl.BlockSpec((padded, 4 * HEAD_DIM), lambda i: (0, i))
    flipped = pl.BlockSpec((4 * HEAD_DIM, padded), lambda i: (i, 0))
    return pl.pallas_call(
        entry_back_kernel,
        grid=(HEADS // 4,),
        out_shape=(
            jax.ShapeDtypeStruct((rows, padded), f32),
            jax.ShapeDtypeStruct((2, width), f32),
            jax.ShapeDtypeStruct((1, width), f32),
            jax.ShapeDtypeStruct((width, padded), f32),
            jax.ShapeDtypeStruct((width, padded), f32),
            jax.ShapeDtypeStruct(keyed.shape, f32),
            jax.ShapeDtypeStruct(bias.shape, f32),
        ),
        in_specs=[
            fixed(token_grad.shape),
            fixed(qkv_t.shape),
            fixed((rows, width)),
            fixed((rows, width)),
            fixed(norm_gains.shape),
            fixed(cells.shape),
            fixed(keyed.shape),
            fixed(bias.shape),
            by_pair,
            by_pair,
        ],
        out_specs=[
            fixed((rows, padded)),
            fixed((2, width)),
            fixed((1, width)),
            flipped,
            flipped,
            fixed(keyed.shape),
            fixed(bias.shape),
        ],
        scratch_shapes=[pltpu.VMEM((rows, width), f32), pltpu.VMEM((width, rows), f32)],
        compiler_params=pltpu.CompilerParams(vmem_limit_bytes=BIG),
        cost_estimate=pl.CostEstimate(
            flops=60 * rows * padded * D, bytes_accessed=40 * rows * D, transcendentals=16 * rows * padded
        ),
        name="entry_backward",
    )(token_grad, qkv_t, x_first, mid_grad, norm_gains, cells, keyed, bias, patch, variable)


def table_rows(
    pa_ref, pb_ref, va_ref, vb_ref, ka_ref, kb_ref, ba_ref, bb_ref,
    patch_ref, var_ref, query_ref, hot_ref, lead_hot_ref, lead_ref, gain_ref, heads, highs, o_ref,
):
    padded, width = patch_ref.shape
    marks = head_marks(width)
    query = query_ref[5 * V + LEADS : 5 * V + LEADS + 1, :]
    keyed_grad = exact_product(ka_ref[...] + kb_ref[...], marks, TN)
    bias_grad = exact_product(ba_ref[...] + bb_ref[...], marks, TN)
    o_ref[...] = jnp.zeros_like(o_ref)
    patch_grad = (pa_ref[...] + pb_ref[...]).T + keyed_grad * query
    o_ref[: 4 * V, :] = patch_grad[: 4 * V, :]
    var_grad = (va_ref[...] + vb_ref[...]).T + bias_grad * query
    var_rows = exact_product(quarter_marks(padded), var_grad, TN)
    o_ref[4 * V : 5 * V, :] = exact_product(hot_ref[...], var_rows, TN)
    lead_rows = exact_product(lead_hot_ref[...], lead_ref[...], TN)
    o_ref[5 * V : 5 * V + LEADS, :] = lead_rows[:LEADS, :]
    query_grad = jnp.sum(
        keyed_grad * patch_ref[...] + bias_grad * var_ref[...], axis=0, keepdims=True
    )
    o_ref[5 * V + LEADS : 5 * V + LEADS + 1, :] = query_grad
    o_ref[5 * V + LEADS + 1 : 5 * V + LEADS + 3, :] = gain_ref[...]
    o_ref[padded : padded + 4 * V, :] = heads[0] + heads[1]
    o_ref[padded + 4 * V : padded + 4 * V + 4, :] = highs[0] + highs[1]


def table_grads_kernel(*refs):
    head_a, head_b, high_a, high_b = refs[15:19]
    heads, highs = (head_a[...], head_b[...]), (high_a[2:6, :], high_b[2:6, :])
    table_rows(*refs[:15], heads, highs, refs[19])


def table_grads(first, second, prepared, query, var_hot, lead_hots, leads, gain_rows, heads, highs):
    patch, variable, _, _ = prepared
    operands = []
    for one, two in zip(first, second):
        operands += [one, two]
    return pl.pallas_call(
        table_grads_kernel,
        out_shape=jax.ShapeDtypeStruct((2 * patch.shape[0], D), f32),
        compiler_params=pltpu.CompilerParams(vmem_limit_bytes=BIG),
        name="table_grads",
    )(*operands, patch, variable, query, var_hot, lead_hots, leads, gain_rows, *heads, *highs)


def adam_step(master, grad, first, second, rate):
    first_new = beta_first * first + (1.0 - beta_first) * grad
    second_new = beta_second * second + (1.0 - beta_second) * grad * grad
    update = first_new / first_fix / (jnp.sqrt(second_new / second_fix) + adam_eps)
    return (master - rate * (update + decay_rate * master), first_new, second_new)


def update_kernel(packed, *refs):
    where_ref, sums_ref, tile_ref, count_ref = refs[:4]
    shares = list(refs[4 : 4 + (3 if packed else 4)])
    rest = refs[4 + len(shares) :]
    states, average_ref, outs = rest[:18], rest[18], rest[19:]
    norm = jnp.sqrt(tile_ref[0:1, 0:1])
    factor = jnp.minimum(1.0, clip_norm / (norm + 1e-06))
    outs[1][...] = norm
    outs[0][...] = tile_ref[1:2, 0:1] / (2.0 * V * jnp.maximum(count_ref[...], 1.0))
    embed_rows = 5 * V + LEADS + 1
    padded = 256

    def apply(index, grad, rate, rows=slice(None)):
        master, first, second = (ref[rows, :] for ref in states[3 * index : 3 * index + 3])
        new = adam_step(master, factor * grad, first, second, rate)
        for ref, value in zip(outs[2 + 3 * index : 5 + 3 * index], new):
            ref[rows, :] = value
        return new[0]

    apply(0, sums_ref[:embed_rows, :], lr_table, slice(0, embed_rows))
    apply(0, sums_ref[padded : padded + 4 * V, :], lr_table, slice(embed_rows, embed_rows + 4 * V))
    apply(1, sums_ref[embed_rows : embed_rows + 2, :], lr_gain, slice(0, 2))
    apply(1, sums_ref[padded + 4 * V : padded + 4 * V + 4, :], lr_gain, slice(2, 6))
    if packed:
        units = shares[2].shape[0]
        grads = (
            shares[0][...], shares[1][units:, :], shares[1][:units, :].T, shares[2][...]
        )
    else:
        grads = [share[...] for share in shares]
    qkv_new = apply(2, grads[0], lr_matrix)
    for index in range(1, 4):
        apply(2 + index, grads[index], lr_matrix)
    outs[20][...] = average_keep * average_ref[...] + (1.0 - average_keep) * qkv_new


def update_all(packed, where, sums, tile, count, shares, states, average):
    operands = [sums, tile, count.reshape(1, 1), *shares]
    fixed = lambda shape: pl.BlockSpec(shape, lambda i, w: (0, 0))
    in_specs = [fixed(value.shape) for value in operands]
    out_shapes = [(1, 1), (1, 1)]
    for master, first, second in states:
        if master.shape == first.shape:
            in_specs.append(fixed(master.shape))
        elif master.shape[0] == first.shape[0]:
            in_specs.append(pl.BlockSpec(first.shape, lambda i, w: (0, w[0])))
        else:
            in_specs.append(pl.BlockSpec(first.shape, lambda i, w: (w[0], 0)))
        in_specs += [fixed(first.shape)] * 2
        operands += [master, first, second]
        out_shapes += [first.shape] * 3
    operands.append(average)
    in_specs.append(fixed(average.shape))
    out_shapes.append(average.shape)
    return pl.pallas_call(
        partial(update_kernel, packed),
        grid_spec=pltpu.PrefetchScalarGridSpec(
            num_scalar_prefetch=1,
            grid=(1,),
            in_specs=in_specs,
            out_specs=[fixed(shape) for shape in out_shapes],
        ),
        out_shape=[jax.ShapeDtypeStruct(shape, f32) for shape in out_shapes],
        compiler_params=pltpu.CompilerParams(vmem_limit_bytes=60 * 2**20),
        name="update_all",
    )(where, *operands)


def by_kind(shard):
    rows = shard.shape[0]
    return shard.reshape(rows, -1, 3, HEAD_DIM).transpose(0, 2, 1, 3).reshape(rows, -1)


def by_head(shard):
    rows = shard.shape[0]
    return shard.reshape(rows, 3, -1, HEAD_DIM).transpose(0, 2, 1, 3).reshape(rows, -1)


class Rows:
    count = 11

    def __init__(self, refs, sems):
        (self.h1, self.rows_ref, self.weight, self.qkv, self.vt, self.o_ref, self.full, self.lse,
         self.attended) = refs
        self.sems, self.o_sems, self.own_sem = sems
        dp, level, core = mesh_place()
        self.dp, self.core = dp, core
        self.me = dp * 2 + core
        self.height = self.h1.shape[0]
        self.width = self.o_ref.shape[1]
        half = self.height // 2
        x = lax.rem(dp, 2)
        beside, below, far = dp + 1 - 2 * x, lax.rem(dp + 2, 4), 3 - dp
        self.owners = (beside, below, far)
        self.peers = []
        for move in range(1, 8):
            part = lax.rem(self.me + move, 8)
            self.peers.append(device_of(part // 2, level, lax.rem(part, 2)))
        side = device_of(beside, level, core)
        down = device_of(below, level, core)
        near = device_of(dp, level, 1 - core)
        self.level = level
        slots = [0]

        def remote(source, target_ref, target):
            slot = slots[0]
            slots[0] += 1
            return pltpu.make_async_remote_copy(
                src_ref=source,
                dst_ref=target_ref,
                send_sem=self.sems.at[0, slot],
                recv_sem=self.sems.at[1, slot],
                device_id=target,
                device_id_type=MESH,
            )

        def place(owner, first, size):
            start = pl.multiple_of((owner * 2 + core) * self.height + first, half)
            return self.rows_ref.at[pl.ds(start, size)]

        def relay(where, target):
            return remote(where, where, target)

        first, second = self.h1.at[pl.ds(0, half)], self.h1.at[pl.ds(half, half)]
        self.side_a = remote(first, place(dp, 0, half), side)
        self.down_b = remote(second, place(dp, half, half), down)
        self.side_b = remote(second, place(dp, half, half), side)
        self.down_a = remote(first, place(dp, 0, half), down)
        self.near_own = remote(self.h1, place(dp, 0, self.height), near)
        self.far_a = relay(place(beside, 0, half), down)
        self.far_b = relay(place(below, half, half), side)
        self.near_side = relay(place(beside, 0, self.height), near)
        self.near_down = relay(place(below, 0, self.height), near)
        self.near_far = relay(place(far, 0, self.height), near)

    def part_rows(self, part):
        return pl.ds(pl.multiple_of(part * self.height, self.height), self.height)

    def project(self, owner, core):
        where = self.part_rows(owner * 2 + core)
        self.qkv[where, :] = lax.dot_general(
            self.rows_ref[where, :], self.weight[...], NT, preferred_element_type=f32
        ).astype(bf16)

    def send_o(self, part, target):
        columns = pl.ds(pl.multiple_of(self.me * self.width, self.width), self.width)
        return pltpu.make_async_remote_copy(
            src_ref=self.o_ref.at[self.part_rows(part), :],
            dst_ref=self.attended.at[:, columns],
            send_sem=self.o_sems.at[0, lax.rem(part + 8 - self.me, 8)],
            recv_sem=self.o_sems.at[1, lax.rem(part + 8 - self.me, 8)],
            device_id=target,
            device_id_type=MESH,
        )

    def keep_o(self):
        columns = pl.ds(pl.multiple_of(self.me * self.width, self.width), self.width)
        return pltpu.make_async_copy(
            self.o_ref.at[self.part_rows(self.me), :], self.attended.at[:, columns], self.own_sem
        )

    def phase(self, number):
        beside, below, far = self.owners
        if number == 0:
            for copy in (self.side_a, self.down_b, self.side_b, self.down_a, self.near_own):
                copy.start()
            self.rows_ref[self.part_rows(self.me), :] = self.h1[...]
        elif number == 1:
            self.project(self.dp, self.core)
            self.near_own.wait_recv()
        elif number == 2:
            self.side_a.wait_recv()
            self.far_a.start()
            self.down_b.wait_recv()
            self.far_b.start()
            self.project(self.dp, 1 - self.core)
        elif number == 3:
            self.side_b.wait_recv()
            self.near_side.start()
            self.down_a.wait_recv()
            self.near_down.start()
            self.project(beside, self.core)
            self.project(below, self.core)
        elif number == 4:
            self.near_side.wait_recv()
            self.near_down.wait_recv()
            self.project(beside, 1 - self.core)
            self.project(below, 1 - self.core)
        elif number == 5:
            self.far_a.wait_recv()
            self.far_b.wait_recv()
            self.near_far.start()
            self.project(far, self.core)
        elif number == 6:
            self.near_far.wait_recv()
            self.project(far, 1 - self.core)
            self.vt[...] = self.qkv[:, 2 * self.width :].T

    def attend(self, turn):
        owner = lax.rem(self.dp + 1 + turn, 4)
        size = 2 * self.height
        where = pl.ds(pl.multiple_of(owner * size, size), size)
        heads = self.width // HEAD_DIM
        full, sums = attend_rows(
            heads, self.qkv[where, : self.width],
            self.qkv.at[:, self.width : 2 * self.width], self.vt,
        )
        for head in range(heads):
            self.lse[head : head + 1, where] = sums[head]
        self.full[where, :] = full
        self.o_ref[where, :] = full.astype(bf16)

        @pl.when(turn < 3)
        def _():
            for core in range(2):
                self.send_o(owner * 2 + core, device_of(owner, self.level, core)).start()

        @pl.when(turn == 3)
        def _():
            other = device_of(self.dp, self.level, 1 - self.core)
            self.send_o(self.dp * 2 + 1 - self.core, other).start()
            self.keep_o().start()

    def finish(self):
        for move in range(1, 8):
            part = lax.rem(self.me + move, 8)
            self.send_o(part, self.peers[move - 1]).wait()
        self.keep_o().wait()
        for copy in (
            self.side_a, self.down_b, self.side_b, self.down_a, self.near_own, self.far_a,
            self.far_b, self.near_side, self.near_down, self.near_far,
        ):
            copy.wait_send()


def row_scratch(rows, width):
    return [
        pltpu.VMEM((rows, D), bf16),
        pltpu.VMEM((8 * rows, D), bf16),
        pltpu.VMEM((3 * width, D), bf16),
        pltpu.VMEM((width, 8 * rows), bf16),
        pltpu.VMEM((8 * rows, width), bf16),
        pltpu.SemaphoreType.DMA((2, 10)),
        pltpu.SemaphoreType.DMA((2, 8)),
        pltpu.SemaphoreType.DMA((3,)),
    ]


def lead_rows_of(lead, lead_ref):
    row = lax.broadcasted_iota(jnp.int32, (1, 8), 1).astype(f32)
    lead_hot = jnp.where(row == lead, 1.0, 0.0).astype(f32)
    return exact_product(lead_hot, lead_ref[5 * V : 5 * V + 8, :])


def middle_kernel(
    guess_ref, first_ref, keyed_ref, bias_ref, patch_ref, var_ref, lead_ref, gains_ref, weights_ref,
    x0_ref, cells_ref, qkv_ref, full_ref, lse_ref, rows_out, attended_ref,
    h1_ref, rows_ref, weight_ref, vt_ref, o_ref, sems, o_sems, own_sem,
):
    turn = pl.program_id(0)
    dp, _, core = mesh_place()
    rows = Rows(
        (h1_ref, rows_ref, weight_ref, qkv_ref, vt_ref, o_ref, full_ref, lse_ref, attended_ref),
        (sems, o_sems, own_sem.at[0]),
    )
    size = weight_ref.shape[0]
    weight = pltpu.make_async_copy(
        weights_ref.at[pl.ds(pl.multiple_of((dp * 2 + core) * size, size), size), :],
        weight_ref, own_sem.at[1],
    )
    save = pltpu.make_async_copy(rows_ref, rows_out, own_sem.at[2])
    pairs = HEADS // 2

    @pl.when(turn == 0)
    def _():
        barrier = pltpu.get_barrier_semaphore()
        for target in rows.peers:
            pl.semaphore_signal(barrier, inc=1, device_id=target, device_id_type=MESH)
        pl.semaphore_wait(barrier, 7)
        weight.start()
        cells_ref[:, : 4 * V] = guess_ref[...]
        cells_ref[:, 4 * V :] = jnp.zeros_like(cells_ref[:, 4 * V :])

    @pl.when(turn < pairs)
    def _():
        embed_pair(turn, cells_ref[...], keyed_ref, bias_ref, patch_ref, var_ref, x0_ref)

    @pl.when(turn == pairs)
    def _():
        x0_ref[...] += lead_rows_of(first_ref[0:1, 4 * V + 5 : 4 * V + 6], lead_ref)
        unit, _ = normed_parts(x0_ref[...])
        h1_ref[...] = (unit * gains_ref[0:1, :] + gains_ref[1:2, :]).astype(bf16)
        weight.wait()

    for number in range(7):

        @pl.when(turn == pairs + number)
        def _(number=number):
            rows.phase(number)
            if number == 6:
                save.start()

    @pl.when(turn >= pairs + 7)
    def _():
        rows.attend(turn - pairs - 7)

    @pl.when(turn == pairs + 10)
    def _():
        rows.finish()
        save.wait()


def middle_program(guess, first_cells, prepared, lead_table, norm_gains, qkv_t):
    patch, variable, keyed, bias = prepared
    rows = guess.shape[0]
    padded = patch.shape[0]
    width = D // 8
    heads = width // HEAD_DIM
    total = 8 * rows
    anywhere = pl.BlockSpec(memory_space=pl.ANY)
    fixed = lambda shape: pl.BlockSpec(shape, lambda i: (0, 0))
    by_pair = pl.BlockSpec(
        (padded, 2 * HEAD_DIM), lambda i: (0, jnp.clip(i, 0, HEADS // 2 - 1))
    )
    shapes = [
        ((rows, D), f32),
        ((rows, padded), f32),
        ((total, 3 * width), bf16),
        ((total, width), f32),
        ((heads, total), f32),
    ]
    return pl.pallas_call(
        middle_kernel,
        grid=(HEADS // 2 + Rows.count,),
        out_shape=[jax.ShapeDtypeStruct(shape, kind) for shape, kind in shapes]
        + [jax.ShapeDtypeStruct((total, D), bf16), jax.ShapeDtypeStruct((rows, D), bf16)],
        in_specs=[once(value.shape) for value in (guess, first_cells, keyed, bias)]
        + [by_pair, by_pair, once(lead_table.shape), once(norm_gains.shape), anywhere],
        out_specs=[fixed(shape) for shape, _ in shapes] + [anywhere, anywhere],
        scratch_shapes=row_scratch(rows, width),
        compiler_params=pltpu.CompilerParams(
            collective_id=9, has_side_effects=True, vmem_limit_bytes=BIG
        ),
        name="middle_program",
    )(guess, first_cells, keyed, bias, patch, variable, lead_table, norm_gains, qkv_t)


lag_one, lag_two, ahead = 2, 4, 3
embed_at, gather_at = 3, 11


def start_kernel(halves, *refs):
    count = len(halves)
    packed_ref, keyed_ref, bias_ref, patch_ref, var_ref, lead_ref, gains_ref = refs[:7]
    shards = refs[7 : 7 + count]
    x0_ref, cells_ref, qkv_ref, full_ref, lse_ref, count_ref, rows_out, attended_ref = refs[
        7 + count : 15 + count
    ]
    outs = refs[15 + count : 15 + 2 * count]
    (h1_ref, rows_ref, weight_ref, vt_ref, o_ref, row_sems, o_sems, row_own, held_ref, tile_ref,
     send_sem, recv_sem, level_send, level_recv, own_sem) = refs[15 + 2 * count :]
    rows = Rows(
        (h1_ref, rows_ref, weight_ref, qkv_ref, vt_ref, o_ref, full_ref, lse_ref, attended_ref),
        (row_sems, o_sems, row_own.at[0]),
    )
    step = pl.program_id(0)
    dp, level, core = mesh_place()
    x = lax.rem(dp, 2)
    columns = {"here": dp, "side": dp + 1 - 2 * x, "down": lax.rem(dp + 2, 4), "far": 3 - dp}
    side = device_of(columns["side"], level, core)
    down = device_of(columns["down"], level, core)
    near = device_of(dp, level, 1 - core)
    across = device_of(level, dp, core)
    middle = lax.rem(level, 3) != 0
    late = level // 2
    sources = (level + 1 - 2 * lax.rem(level, 2), 2 - late, 3 * (1 - late))
    onward = (3 - level, lax.rem(3 * level + 1, 4), lax.rem(3 * level + 1, 4))
    slots = [0]

    def remote(source, target_ref, target):
        slot = slots[0]
        slots[0] += 1
        return pltpu.make_async_remote_copy(
            src_ref=source,
            dst_ref=target_ref,
            send_sem=send_sem.at[slot],
            recv_sem=recv_sem.at[slot],
            device_id=target,
            device_id_type=MESH,
        )

    def place(out, source, column, half, pieces):
        rows = out.shape[1] // 4
        size = rows // pieces
        start = pl.multiple_of(columns[column] * rows + half * size, size)
        return out.at[source * 2 + core, pl.ds(start, size), :]

    def pass_on(out, source, column, target, cut):
        where = place(out, source, column, *cut)
        return remote(where, where, target)

    crossing = remote(packed_ref, held_ref, across)
    staying = pltpu.make_async_copy(packed_ref, held_ref, own_sem.at[count])
    mine = [outs[index].at[level * 2 + core] for index in range(count)]
    given = [remote(shards[index], mine[index], near) for index in range(count)]
    kept = [
        pltpu.make_async_copy(shards[index], mine[index], own_sem.at[index]) for index in range(count)
    ]
    chunks, openings = [], []
    for index in range(count):
        out, pieces = outs[index], halves[index]
        for half in range(pieces):
            group = len(openings)
            full = out.shape[1] // 4
            size = full // pieces
            own = shards[index].at[pl.ds(pl.multiple_of(dp * full + half * size, size), size), :]
            cut = (half, pieces)

            def along(source_ref, source, target_level, slot):
                return pltpu.make_async_remote_copy(
                    src_ref=source_ref,
                    dst_ref=place(out, source, "here", *cut),
                    send_sem=level_send.at[group * 5 + slot],
                    recv_sem=level_recv.at[group * 4 + source],
                    device_id=device_of(dp, target_level, core),
                    device_id_type=MESH,
                )

            openings.append(
                (
                    along(own, level, lax.rem(level + 1, 4), 0),
                    along(own, level, lax.rem(level + 3, 4), 1),
                )
            )
            for turn in range(3):
                source = sources[turn]
                chunks.append(
                    {
                        "level": along(place(out, source, "here", *cut), source, onward[turn], 2 + turn),
                        "side": pass_on(out, source, "here", side, cut),
                        "down": pass_on(out, source, "here", down, cut),
                        "hop_down": pass_on(out, source, "side", down, (2 * half, 2 * pieces)),
                        "hop_side": pass_on(out, source, "down", side, (2 * half + 1, 2 * pieces)),
                        "here_near": pass_on(out, source, "here", near, cut),
                        "side_near": pass_on(out, source, "side", near, cut),
                        "down_near": pass_on(out, source, "down", near, cut),
                        "far_near": pass_on(out, source, "far", near, cut),
                    }
                )
    groups = len(openings)
    order = []
    for number in range(groups + 2):
        for turn in range(3):
            if 0 <= number - turn < groups:
                order.append((number - turn, turn))
    chunks = [chunks[3 * group + turn] for group, turn in order]
    total = len(chunks)

    def start_group(number):
        @pl.when(level < 3)
        def _():
            openings[number][0].start()

        @pl.when(level > 0)
        def _():
            openings[number][1].start()

    tiles = [
        remote(tile_ref.at[0], tile_ref.at[1], side),
        remote(tile_ref.at[2], tile_ref.at[3], down),
        remote(tile_ref.at[4], tile_ref.at[5], near),
    ]
    deep = [device_of(dp, lax.rem(level + move, 4), core) for move in (1, 2, 3)]
    level_tiles = [remote(tile_ref.at[6], tile_ref.at[7 + move], deep[move]) for move in range(3)]
    weight = pltpu.make_async_copy(outs[0].at[dp * 2 + core], weight_ref, row_own.at[1])
    save = pltpu.make_async_copy(rows_ref, rows_out, row_own.at[2])

    @pl.when(step == 0)
    def _():
        barrier = pltpu.get_barrier_semaphore()
        for target in (*rows.peers, *deep):
            pl.semaphore_signal(barrier, inc=1, device_id=target, device_id_type=MESH)

        @pl.when(dp != level)
        def _():
            pl.semaphore_signal(barrier, inc=1, device_id=across, device_id_type=MESH)
            pl.semaphore_wait(barrier, 11)
            crossing.start()

        @pl.when(dp == level)
        def _():
            pl.semaphore_wait(barrier, 10)
            staying.start()

        for number in range(ahead):
            start_group(number)
        for copy in (*given, *kept):
            copy.start()

    for number in range(total + lag_two):

        @pl.when(step == number)
        def _(number=number):
            if number < total:
                chunk = chunks[number]
                chunk["level"].wait_recv()

                @pl.when(middle)
                def _():
                    chunk["level"].start()

                chunk["side"].start()
                chunk["down"].start()
                chunk["here_near"].start()
                group, turn = order[number]
                if turn == 0 and group + ahead < groups:
                    start_group(group + ahead)
            if 0 <= number - lag_one < total:
                chunk = chunks[number - lag_one]
                chunk["side"].wait_recv()
                chunk["hop_down"].start()
                chunk["down"].wait_recv()
                chunk["hop_side"].start()
                chunk["side_near"].start()
                chunk["down_near"].start()
            if 0 <= number - lag_two < total:
                chunk = chunks[number - lag_two]
                chunk["hop_down"].wait_recv()
                chunk["hop_side"].wait_recv()
                chunk["far_near"].start()

    @pl.when(step == embed_at)
    def _():
        @pl.when(dp != level)
        def _():
            crossing.wait_recv()

        @pl.when(dp == level)
        def _():
            staying.wait()

        cells_ref[...] = held_ref[...]
        lane = lax.broadcasted_iota(jnp.int32, held_ref.shape, 1)
        ocean = jnp.where((lane >= 4 * V) & (lane < 4 * V + 4), 1.0 - held_ref[...], 0.0)
        tile_ref[0] = jnp.broadcast_to(jnp.sum(ocean), tile_ref.shape[1:])
        tiles[0].start()

    for turn in range(3):

        @pl.when(step == embed_at + 2 + turn)
        def _(turn=turn):
            tiles[turn].wait_recv()
            tile_ref[2 * turn + 2] = tile_ref[2 * turn] + tile_ref[2 * turn + 1]
            for copy in (tiles[1:2], tiles[2:3], level_tiles)[turn]:
                copy.start()

    @pl.when(step == embed_at + 6)
    def _():
        for copy in level_tiles:
            copy.wait_recv()
        count_ref[...] = tile_ref[6] + tile_ref[7] + tile_ref[8] + tile_ref[9]

    @pl.when((step >= embed_at) & (step < embed_at + HEADS // 2))
    def _():
        embed_pair(step - embed_at, held_ref[...], keyed_ref, bias_ref, patch_ref, var_ref, x0_ref)

    @pl.when(step == gather_at - 2)
    def _():
        kept[0].wait()
        weight.start()

    @pl.when(step == gather_at)
    def _():
        x0_ref[...] += lead_rows_of(held_ref[0:1, 4 * V + 4 : 4 * V + 5], lead_ref)
        unit, _ = normed_parts(x0_ref[...])
        h1_ref[...] = (unit * gains_ref[0:1, :] + gains_ref[1:2, :]).astype(bf16)
        weight.wait()

    for number in range(7):

        @pl.when(step == gather_at + number)
        def _(number=number):
            rows.phase(number)
            if number == 6:
                save.start()

    @pl.when((step >= gather_at + 7) & (step < gather_at + 11))
    def _():
        rows.attend(step - gather_at - 7)

    @pl.when(step == total + lag_two - 1)
    def _():
        for copy in given:
            copy.wait()
        for copy in kept[1:]:
            copy.wait()
        for number in range(groups):

            @pl.when(level < 3)
            def _(number=number):
                openings[number][0].wait_send()

            @pl.when(level > 0)
            def _(number=number):
                openings[number][1].wait_send()

        for chunk in chunks:
            for name in ("here_near", "side_near", "down_near", "far_near"):
                chunk[name].wait_recv()
            for name, copy in chunk.items():
                if name != "level":
                    copy.wait_send()

            @pl.when(middle)
            def _(chunk=chunk):
                chunk["level"].wait_send()

        rows.finish()
        for copy in (*tiles, *level_tiles):
            copy.wait_send()
        save.wait()

        @pl.when(dp != level)
        def _():
            crossing.wait_send()


def start_program(packed, prepared, lead_table, norm_gains, shards, halves):
    patch, variable, keyed, bias = prepared
    count = len(shards)
    groups = sum(halves)
    copies = groups * 24 + count + 7
    rows, padded = packed.shape
    total = 8 * rows
    width = shards[0].shape[0] // 3
    heads = width // HEAD_DIM
    anywhere = pl.BlockSpec(memory_space=pl.ANY)
    fixed = lambda shape: pl.BlockSpec(shape, lambda i: (0, 0))
    by_pair = pl.BlockSpec(
        (padded, 2 * HEAD_DIM), lambda i: (0, jnp.clip(i - embed_at, 0, HEADS // 2 - 1))
    )
    shapes = [
        ((rows, D), f32),
        (packed.shape, f32),
        ((total, 3 * width), bf16),
        ((total, width), f32),
        ((heads, total), f32),
        ((8, 128), f32),
    ]
    return pl.pallas_call(
        partial(start_kernel, halves),
        grid=(groups * 3 + lag_two,),
        out_shape=[jax.ShapeDtypeStruct(shape, kind) for shape, kind in shapes]
        + [jax.ShapeDtypeStruct((total, D), bf16), jax.ShapeDtypeStruct((rows, D), bf16)]
        + [jax.ShapeDtypeStruct((8,) + shard.shape, bf16) for shard in shards],
        in_specs=[anywhere]
        + [fixed(keyed.shape), fixed(bias.shape), by_pair, by_pair]
        + [fixed(lead_table.shape), fixed(norm_gains.shape)]
        + [fixed(shard.shape) for shard in shards],
        out_specs=[fixed(shape) for shape, _ in shapes] + [anywhere] * (count + 2),
        scratch_shapes=row_scratch(rows, width)
        + [
            pltpu.VMEM(packed.shape, f32),
            pltpu.VMEM((10, 8, 128), f32),
            pltpu.SemaphoreType.DMA((copies,)),
            pltpu.SemaphoreType.DMA((copies,)),
            pltpu.SemaphoreType.DMA((groups * 5,)),
            pltpu.SemaphoreType.DMA((groups * 4,)),
            pltpu.SemaphoreType.DMA((count + 1,)),
        ],
        compiler_params=pltpu.CompilerParams(
            collective_id=7, has_side_effects=True, vmem_limit_bytes=BIG
        ),
        name="start_program",
    )(packed, keyed, bias, patch, variable, lead_table, norm_gains, *shards)


def shards(
    crossed,
    fields,
    targets,
    land_mask,
    lead_index,
    var_ids,
    tables,
    norm_gains,
    tables_first,
    tables_second,
    gains_first,
    gains_second,
    w_qkv,
    qkv_first,
    qkv_second,
    w_out,
    out_first,
    out_second,
    w_up,
    up_first,
    up_second,
    w_down,
    down_first,
    down_second,
    qkv_average,
):
    local_samples, shard_rows, _ = fields.shape
    dp_size, parts = lax.axis_size("dp"), lax.axis_size("mp")
    dp_index = lax.axis_index("dp")
    place, level, core = mesh_place()
    part = place * 2 + core if crossed else lax.axis_index("mp")
    share_rows = D // dp_size

    def own_share(full, dim):
        return lax.dynamic_slice_in_dim(full, dp_index * share_rows, share_rows, dim)

    var_hot = (var_ids[:, None] == jnp.arange(V, dtype=jnp.int32)[None, :]).astype(f32)
    prepared = prepare_tables(tables, var_hot)
    low = lambda master: master.astype(bf16)
    qkv_low = by_kind(low(w_qkv))
    packed = jnp.concatenate(
        (
            fields[0],
            land_mask[0].astype(f32),
            jnp.broadcast_to(lead_index.astype(f32), (shard_rows, 2)),
            jnp.zeros((shard_rows, 64 - 6), f32),
        ),
        axis=1,
    )
    if crossed:
        (
            x_first, cells, packed, full, logsum, count, rows_one, attended,
            qkv_t, w_outs, w_ups, w_downs
        ) = start_program(
            packed, prepared, tables, norm_gains,
            (qkv_low.T, low(w_out), low(w_up), low(w_down)), (1, 1, 2, 2),
        )
        count = count[0, 0]
    else:
        cells = packed
        answers = targets[0]
        count = lax.psum(jnp.sum(1.0 - cells[:, 4 * V : 4 * V + 4]), ("dp", "mp"))
        w_outs, w_ups, w_downs, qkv_t = [
            lax.all_gather(shard, "mp")
            for shard in (low(w_out), low(w_up), low(w_down), qkv_low.T)
        ]
    gathered = (w_outs.reshape(D, D), w_ups, w_downs.reshape(-1, D), qkv_t.reshape(3 * D, D))
    if not crossed:
        qkv_local = choose(qkv_t, part)
    first_cells = cells
    leads = cells[0, 4 * V + 4 : 4 * V + 6].astype(jnp.int32)
    ocean = 1.0 - cells[:, 4 * V : 4 * V + 4]
    denom = 2.0 * V * jnp.maximum(count, 1.0)
    first_row = part * shard_rows
    patch_row = (first_row + jnp.arange(shard_rows, dtype=jnp.int32)) // PATCH_COLS
    row_hot = (patch_row[:, None] == jnp.arange(PATCH_ROWS, dtype=jnp.int32)[None, :]).astype(f32)
    lat_rows = jnp.dot(
        row_hot, lat_weights(2 * PATCH_ROWS).reshape(PATCH_ROWS, 2), precision=highest
    )
    lat_pixels = jnp.broadcast_to(lat_rows[:, :, None], (shard_rows, 2, 2)).reshape(shard_rows, 4)
    weighted = jnp.tile(ocean * lat_pixels, (1, V))
    head = tables
    loss_part = f32(0.0)
    records = []
    for rollout in range(2):
        if crossed and rollout == 1:
            x_first, cells, packed, full, logsum, rows_one, attended = middle_program(
                guess, first_cells, prepared, tables, norm_gains, gathered[3]
            )
        if not crossed:
            if rollout == 1:
                cells = jnp.pad(guess, ((0, 0), (0, 64)))
            lead_row = lax.dynamic_slice_in_dim(tables, 5 * V + leads[rollout], 1, 0)
            x_first, normed = embed_forward(cells, prepared, lead_row, norm_gains)
            rows_one = lax.all_gather(normed, "mp", axis=0, tiled=True)
            packed = lax.dot_general(
                rows_one, qkv_local, NT, preferred_element_type=f32
            ).astype(bf16)
            own_out, full, logsum = attend(packed)
            attended = exchange(own_out, True)
        if crossed and rollout == 0:
            later_targets, attended = tie(targets[0], attended)
            answers = cross(crossed, later_targets)
        x_mid, rows_two, hidden, active, x_last, guess = branch_forward(
            attended, x_first, norm_gains, gathered, head
        )
        miss = guess - answers[rollout]
        loss_part = loss_part + jnp.sum(weighted * miss * miss)
        records.append(
            (cells, x_first, rows_one, packed, full, logsum, attended, x_mid, rows_two,
             hidden, active, x_last, 2.0 * weighted * miss / denom)
        )
    carried = jnp.zeros_like(guess)
    heads, highs = [], []
    lead_hots = (leads[:, None] == jnp.arange(8, dtype=jnp.int32)[None, :]).astype(f32)
    lead_hots = jnp.pad(lead_hots, ((0, 6), (0, 0)))
    query = tables
    gain_low = jnp.zeros((2, D), f32)
    table_parts, lead_sums = [], []
    qkv_grad = jnp.zeros((D, w_qkv.shape[1]), f32)
    kept = []

    for rollout in (1, 0):
        (cells, x_first, rows_one, packed, full, logsum, attended, x_mid, rows_two,
         hidden, active, x_last, loss_grad) = records[rollout]
        last_low, hidden_grad, mid_grad, mid_low, out_grad, gain_part, head_grad = branch_backward(
            loss_grad + carried, x_last, x_mid, norm_gains, hidden, gathered, head
        )
        heads.append(head_grad)
        highs.append(gain_part)
        if crossed:
            (
                own_grad, act_both, dg_both, o_both, dx2_near, h2_near, dx1_near
            ) = exchange_swap(
                out_grad, active, hidden_grad, attended, last_low, rows_two, mid_low
            )
            kept.append(
                (act_both, dg_both, o_both, last_low, dx2_near, rows_two, h2_near, mid_low, dx1_near)
            )
        else:
            flat = lambda value: value.transpose(2, 1, 0, 3).reshape(shard_rows, -1)
            kept.append((attended, rows_two, flat(active), mid_low, flat(hidden_grad), last_low))
            own_grad = exchange(out_grad, False)
        if crossed and rollout == 0:
            token_grad, level_share, down_sum = finish_program(
                [(step[0], step[3], step[4]) for step in kept],
                packed, own_grad, full, logsum, rows_one, qkv_grad,
            )
        elif crossed:
            token_grad, qkv_grad = attend_exchange(packed, own_grad, full, logsum, rows_one)
        else:
            packed_grad = attend_back(own_grad, packed, full, logsum)
            token_grad = exchange(packed_grad, True)
            qkv_grad = qkv_grad + lax.dot_general(
                rows_one, packed_grad, TN, preferred_element_type=f32
            )
        entry = (token_grad, gathered[3], x_first, mid_grad, norm_gains, cells, prepared)
        if crossed and rollout == 0:
            last_rows, up_out_sum, qkv_share = entry_last(
                [step[1:3] + step[5:] for step in kept], level_share, *entry,
                query, var_hot, lead_hots, heads, highs,
                (*table_parts[0], lead_sums[0], gain_low),
            )
            break
        cells_grad, gain_one, lead_sum, *table_part = entry_backward(*entry)
        carried = cells_grad[:, : 4 * V]
        gain_low = gain_low + gain_one
        table_parts.append(table_part)
        lead_sums.append(lead_sum)

    def pair(index):
        return (kept[0][index], kept[1][index])

    if not crossed:
        lead_rows = jnp.pad(jnp.concatenate((lead_sums[1], lead_sums[0])), ((0, 6), (0, 0)))
        last_rows = table_grads(
            *table_parts, prepared, query, var_hot, lead_hots, lead_rows, gain_low, heads, highs
        )
    if not crossed:
        qkv_share = lax.psum_scatter(qkv_grad, "dp", scatter_dimension=0, tiled=True)
    qkv_share = by_head(qkv_share)
    where = dp_index.astype(jnp.int32).reshape(1)
    if crossed:
        shares = (qkv_share, up_out_sum, down_sum)
        last_sum, tile = exchange_sum(last_rows, loss_part, *shares)
        masters = (w_qkv, w_out, w_up, w_down)
    else:
        shares = (
            qkv_share,
            outer_plain(pair(0), pair(3), False),
            outer_plain(pair(1), pair(4), True),
            outer_plain(pair(2), pair(5), False),
        )
        squares = sum(jnp.sum(share * share) for share in shares)
        last_sum, loss_sum, squares = lax.psum((last_rows, loss_part, squares), ("dp", "mp"))
        squares = squares + jnp.sum(last_sum * last_sum)
        row = jnp.arange(8, dtype=jnp.int32)[:, None]
        tile = jnp.where(row == 0, squares, jnp.where(row == 1, loss_sum, 0.0))
        tile = jnp.broadcast_to(tile, (8, 128))
        masters = (own_share(w_qkv, 0), own_share(w_out, 1), own_share(w_up, 0), own_share(w_down, 1))
    states = (
        (tables, tables_first, tables_second),
        (norm_gains, gains_first, gains_second),
        (masters[0], qkv_first, qkv_second),
        (masters[1], out_first, out_second),
        (masters[2], up_first, up_second),
        (masters[3], down_first, down_second),
    )
    results = update_all(crossed, where, last_sum, tile, count, shares, states, qkv_average)
    return (results[0][0, 0], results[1][0, 0], *results[2:])


def solution(mesh):
    return jax.shard_map(
        partial(shards, is_crossed(mesh.shape)),
        mesh=mesh,
        in_specs=(
            P("dp", "mp", None),
            P("dp", None, "mp", None),
            P("dp", "mp", None),
            P("dp", None),
            P(),
            P(),
            P(),
            P(),
            P(),
            P(),
            P(),
            P(None, "mp"),
            P("dp", "mp"),
            P("dp", "mp"),
            P("mp", None),
            P("mp", "dp"),
            P("mp", "dp"),
            P(None, "mp"),
            P("dp", "mp"),
            P("dp", "mp"),
            P("mp", None),
            P("mp", "dp"),
            P("mp", "dp"),
            P("dp", "mp"),
        ),
        out_specs=(
            P(),
            P(),
            P(),
            P(),
            P(),
            P(),
            P(),
            P(),
            P("dp", "mp"),
            P("dp", "mp"),
            P("dp", "mp"),
            P("mp", "dp"),
            P("mp", "dp"),
            P("mp", "dp"),
            P("dp", "mp"),
            P("dp", "mp"),
            P("dp", "mp"),
            P("mp", "dp"),
            P("mp", "dp"),
            P("mp", "dp"),
            P("dp", "mp"),
        ),
        check_vma=False,
    )
```

```python
from functools import partial
import math

import jax
import jax.numpy as jnp
from jax import lax
from jax.experimental import pallas as pl
from jax.experimental.pallas import tpu as pltpu
from jax.sharding import PartitionSpec as P

D = 1024
HEADS = 16
HEAD_DIM = 64
V = 48
PATCH_ROWS = 32
PATCH_COLS = 64
LEADS = 7


highest = lax.Precision.HIGHEST
eps_norm = 1e-05
clip_norm = 0.05
beta_first = 0.9
beta_second = 0.999
adam_eps = 1e-08
decay_rate = 0.1
lr_matrix = 0.04
lr_table = 0.1
lr_gain = 0.3
average_keep = 0.9
first_fix = 1.0 - 0.9**10
second_fix = 1.0 - 0.999**10


def layer_norm(values, gain, bias):
    center = values - jnp.mean(values, axis=-1, keepdims=True)
    spread = jnp.mean(center * center, axis=-1, keepdims=True)
    return center * lax.rsqrt(spread + eps_norm) * gain + bias


def lat_weights(pixel_rows):
    row_index = jnp.arange(pixel_rows, dtype=jnp.float32)
    cosine = jnp.cos(((row_index + 0.5) / pixel_rows - 0.5) * math.pi)
    return cosine / jnp.mean(cosine)


bf16 = jnp.bfloat16
f32 = jnp.float32
MESH = pl.DeviceIdType.MESH
NT = (((1,), (1,)), ((), ()))
TN = (((0,), (0,)), ((), ()))
VMEM = pl.BlockSpec(memory_space=pltpu.VMEM)
BIG = 56 * 2**20


def is_crossed(sizes):
    return sizes["dp"] == 4 and sizes["mp"] == 8


def mesh_place():
    dp = lax.axis_index("dp")
    mp = lax.axis_index("mp")
    return dp, mp // 2, lax.rem(mp, 2)


def device_of(dp, level, core):
    return {"dp": dp, "mp": level * 2 + core}


def cross_pairs():
    groups = lax.axis_size("dp")
    pairs = []
    for dp in range(groups):
        for level in range(groups):
            for core in range(2):
                source = (dp * groups + level) * 2 + core
                target = (level * groups + dp) * 2 + core
                pairs.append((source, target))
    return pairs


def cross(crossed, value):
    if not crossed:
        return value
    return lax.ppermute(value, ("dp", "mp"), cross_pairs())


def exchange(value, to_columns):
    split, joined = (0, 1) if to_columns else (1, 0)
    return lax.all_to_all(value, "mp", split_axis=split, concat_axis=joined, tiled=True)


def pick_head(value, head, heads):
    if heads == 1:
        return value
    lane = lax.broadcasted_iota(jnp.int32, value.shape, 1) // HEAD_DIM
    return jnp.where(lane == head, value, jnp.zeros_like(value))


def attend_rows(heads, queries, k_ref, vt_ref):
    queries = queries * bf16(HEAD_DIM**-0.5)
    keys = k_ref[...]
    outs, sums = [], []
    for head in range(heads):
        scores = lax.dot_general(
            keys, pick_head(queries, head, heads), NT, preferred_element_type=f32
        )
        largest = jnp.max(scores, axis=0, keepdims=True)
        raised = jnp.exp(scores - largest)
        total = jnp.sum(raised, axis=0, keepdims=True)
        probs = (raised * (1.0 / total)).astype(bf16)
        values = vt_ref[head * HEAD_DIM : (head + 1) * HEAD_DIM, :]
        outs.append(jnp.dot(values, probs, preferred_element_type=f32))
        sums.append(largest + jnp.log(total))
    flipped = outs[0] if heads == 1 else jnp.concatenate(outs, axis=0)
    return flipped.T, sums


def attend_kernel(heads, q_ref, k_ref, v_ref, o_ref, full_ref, lse_ref, vt_ref):
    @pl.when(pl.program_id(0) == 0)
    def _():
        vt_ref[...] = v_ref[...].T

    full, sums = attend_rows(heads, q_ref[...], k_ref, vt_ref)
    for head in range(heads):
        lse_ref[head : head + 1, :] = sums[head]
    full_ref[...] = full
    o_ref[...] = full.astype(bf16)


def attend(packed):
    total, width = packed.shape[0], packed.shape[1] // 3
    heads = width // HEAD_DIM
    block = min(512, total)
    row_block = pl.BlockSpec((block, width), lambda i: (i, 0))
    return pl.pallas_call(
        partial(attend_kernel, heads),
        grid=(total // block,),
        out_shape=(
            jax.ShapeDtypeStruct((total, width), bf16),
            jax.ShapeDtypeStruct((total, width), f32),
            jax.ShapeDtypeStruct((heads, total), f32),
        ),
        in_specs=[
            row_block,
            pl.BlockSpec((total, width), lambda i: (0, 0)),
            pl.BlockSpec((total, width), lambda i: (0, 0)),
        ],
        out_specs=[row_block, row_block, pl.BlockSpec((heads, block), lambda i: (0, i))],
        scratch_shapes=[pltpu.VMEM((width, total), bf16)],
        compiler_params=pltpu.CompilerParams(vmem_limit_bytes=BIG),
        cost_estimate=pl.CostEstimate(
            flops=16 * total * total * width,
            bytes_accessed=10 * total * width,
            transcendentals=heads * total * total,
        ),
        name="attend",
    )(packed[:, :width], packed[:, width : 2 * width], packed[:, 2 * width :])


def attend_back_rows(
    heads, chunk, queries, grads, full, sums, k_ref, v_ref, kt_ref, dk_sum, dv_sum
):
    total = k_ref.shape[0]
    scale = HEAD_DIM**-0.5
    products = (grads.astype(f32) * full).T
    query_heads = [pick_head(queries, head, heads) for head in range(heads)]
    grad_heads = [pick_head(grads, head, heads) for head in range(heads)]
    inner = [
        jnp.sum(products[head * HEAD_DIM : (head + 1) * HEAD_DIM], axis=0, keepdims=True) * scale
        for head in range(heads)
    ]
    query_grads = [None] * heads
    for start in range(0, total, chunk):
        rows = slice(start, start + chunk)
        keys = k_ref[rows, :]
        values = v_ref[rows, :]
        value_part = None
        key_part = None
        for head in range(heads):
            scores = lax.dot_general(
                keys, query_heads[head] * bf16(scale), NT, preferred_element_type=f32
            )
            probs = jnp.exp(scores - sums[head])
            prob_grad = lax.dot_general(
                values, grad_heads[head] * bf16(scale), NT, preferred_element_type=f32
            )
            score_grad = (probs * (prob_grad - inner[head])).astype(bf16)
            one = jnp.dot(probs.astype(bf16), grad_heads[head], preferred_element_type=f32)
            two = jnp.dot(score_grad, query_heads[head], preferred_element_type=f32)
            value_part = one if value_part is None else value_part + one
            key_part = two if key_part is None else key_part + two
            three = jnp.dot(
                kt_ref[head * HEAD_DIM : (head + 1) * HEAD_DIM, rows],
                score_grad,
                preferred_element_type=f32,
            )
            query_grads[head] = three if query_grads[head] is None else query_grads[head] + three
        dv_sum[rows, :] += value_part
        dk_sum[rows, :] += key_part
    flipped = query_grads[0] if heads == 1 else jnp.concatenate(query_grads, axis=0)
    return flipped.T.astype(bf16)


def attend_back_kernel(
    heads, q_ref, do_ref, full_ref, lse_ref, k_ref, v_ref, dq_ref, dk_ref, dv_ref, kt_ref, dk_sum, dv_sum
):
    step = pl.program_id(0)

    @pl.when(step == 0)
    def _():
        kt_ref[...] = k_ref[...].T
        dk_sum[...] = jnp.zeros_like(dk_sum)
        dv_sum[...] = jnp.zeros_like(dv_sum)

    sums = [lse_ref[head : head + 1, :] for head in range(heads)]
    dq_ref[...] = attend_back_rows(
        heads, min(1024, k_ref.shape[0]), q_ref[...], do_ref[...], full_ref[...], sums,
        k_ref, v_ref, kt_ref, dk_sum, dv_sum,
    )

    @pl.when(step == pl.num_programs(0) - 1)
    def _():
        dk_ref[...] = dk_sum[...].astype(bf16)
        dv_ref[...] = dv_sum[...].astype(bf16)


def attend_back(grad_out, packed, full, logsum):
    total, width = grad_out.shape
    heads = width // HEAD_DIM
    block = min(256, total)
    row_block = pl.BlockSpec((block, width), lambda i: (i, 0))
    whole = pl.BlockSpec((total, width), lambda i: (0, 0))
    query_grad, key_grad, value_grad = pl.pallas_call(
        partial(attend_back_kernel, heads),
        grid=(total // block,),
        out_shape=(jax.ShapeDtypeStruct((total, width), bf16),) * 3,
        in_specs=[
            row_block,
            row_block,
            row_block,
            pl.BlockSpec((heads, block), lambda i: (0, i)),
            whole,
            whole,
        ],
        out_specs=[row_block, whole, whole],
        scratch_shapes=[
            pltpu.VMEM((width, total), bf16),
            pltpu.VMEM((total, width), f32),
            pltpu.VMEM((total, width), f32),
        ],
        compiler_params=pltpu.CompilerParams(vmem_limit_bytes=BIG),
        cost_estimate=pl.CostEstimate(
            flops=40 * total * total * width,
            bytes_accessed=16 * total * width,
            transcendentals=heads * total * total,
        ),
        name="attend_back",
    )(
        packed[:, :width],
        grad_out,
        full,
        logsum,
        packed[:, width : 2 * width],
        packed[:, 2 * width :],
    )
    return jnp.concatenate((query_grad, key_grad, value_grad), axis=1)


def normed_parts(values):
    center = values - jnp.mean(values, axis=-1, keepdims=True)
    spread = jnp.mean(center * center, axis=-1, keepdims=True)
    inverse = lax.rsqrt(spread + eps_norm)
    return center * inverse, inverse


def norm_grad(unit, inverse, gain, grad):
    scaled = grad * gain
    middle = jnp.mean(scaled, axis=-1, keepdims=True)
    along = jnp.mean(scaled * unit, axis=-1, keepdims=True)
    gain_grad = jnp.sum(grad * unit, axis=0, keepdims=True)
    bias_grad = jnp.sum(grad, axis=0, keepdims=True)
    return inverse * (scaled - middle - unit * along), gain_grad, bias_grad


def gauss_share(values):
    return 0.5 * (1.0 + lax.erf(values * (0.5**0.5)))


def branch_kernel(
    o_ref, x0_ref, gains_ref, out_ref, up_ref, down_ref, head_ref,
    x1_ref, h2_ref, g_ref, act_ref, x2_ref, pred_ref,
):
    step = pl.program_id(0)

    @pl.when(step == 0)
    def _():
        x1_ref[...] = x0_ref[...] + jnp.dot(
            o_ref[...], out_ref[...], preferred_element_type=f32
        )
        unit, _ = normed_parts(x1_ref[...])
        h2_ref[...] = (unit * gains_ref[2:3, :] + gains_ref[3:4, :]).astype(bf16)
        x2_ref[...] = x1_ref[...]

    units = g_ref.shape[1] // 2
    total = None
    for which in range(2):
        some = slice(which * units, (which + 1) * units)
        hidden = jnp.dot(h2_ref[...], up_ref[which], preferred_element_type=f32)
        g_ref[:, some] = hidden
        active = (hidden * gauss_share(hidden)).astype(bf16)
        act_ref[which, 0] = active
        part = jnp.dot(active, down_ref[some, :], preferred_element_type=f32)
        total = part if total is None else total + part
    x2_ref[...] += total

    @pl.when(step == pl.num_programs(0) - 1)
    def _():
        unit, _ = normed_parts(x2_ref[...])
        last = unit * gains_ref[4:5, :] + gains_ref[5:6, :]
        pred_ref[...] = lax.dot_general(
            last, head_ref[5 * V + LEADS + 1 :, :], NT, precision=highest, preferred_element_type=f32
        )


def weight_specs(w_out, w_up, w_down):
    _, width, units = w_up.shape
    return (
        pl.BlockSpec(w_out.shape, lambda i: (0, 0)),
        pl.BlockSpec((2, width, units), lambda i: (i, 0, 0)),
        pl.BlockSpec((2 * units, width), lambda i: (i, 0)),
    )


def branch_forward(attended, x_first, norm_gains, gathered, head):
    w_out, w_up, w_down, _ = gathered
    rows, width = x_first.shape
    parts, units = w_up.shape[0], w_up.shape[2]
    fixed = lambda shape: pl.BlockSpec(shape, lambda i: (0, 0))
    by_units = pl.BlockSpec((rows, 2 * units), lambda i: (0, i))
    by_core = pl.BlockSpec((2, 1, rows, units), lambda i: (0, i, 0, 0))
    columns = 4 * V
    flops = 2 * rows * (width * width + 2 * width * parts * units + 6 * width * columns)
    return pl.pallas_call(
        branch_kernel,
        grid=(parts // 2,),
        out_shape=(
            jax.ShapeDtypeStruct((rows, width), f32),
            jax.ShapeDtypeStruct((rows, width), bf16),
            jax.ShapeDtypeStruct((rows, parts * units), f32),
            jax.ShapeDtypeStruct((2, parts // 2, rows, units), bf16),
            jax.ShapeDtypeStruct((rows, width), f32),
            jax.ShapeDtypeStruct((rows, columns), f32),
        ),
        in_specs=[
            fixed((rows, width)),
            fixed((rows, width)),
            fixed(norm_gains.shape),
            *weight_specs(w_out, w_up, w_down),
            fixed(head.shape),
        ],
        out_specs=[
            fixed((rows, width)),
            fixed((rows, width)),
            by_units,
            by_core,
            fixed((rows, width)),
            fixed((rows, columns)),
        ],
        compiler_params=pltpu.CompilerParams(vmem_limit_bytes=BIG),
        cost_estimate=pl.CostEstimate(
            flops=flops,
            bytes_accessed=4 * width * parts * units + 6 * rows * parts * units,
            transcendentals=rows * parts * units,
        ),
        name="branch_forward",
    )(attended, x_first, norm_gains, w_out, w_up, w_down, head)


def branch_back_kernel(
    dpred_ref, x2_ref, x1_ref, gains_ref, g_ref, out_ref, up_ref, down_ref, head_ref,
    dx2_ref, dg_ref, dx1_ref, low_ref, do_ref, gain_ref, dhead_ref,
    wide_ref, sum_ref,
):
    step = pl.program_id(0)

    @pl.when(step == 0)
    def _():
        grad = dpred_ref[...]
        unit, inverse = normed_parts(x2_ref[...])
        gain = gains_ref[4:5, :]
        last = unit * gain + gains_ref[5:6, :]
        dhead_ref[...] = lax.dot_general(
            grad, last, TN, precision=highest, preferred_element_type=f32
        )
        row_grad = jnp.dot(grad, head_ref[5 * V + LEADS + 1 :, :], precision=highest, preferred_element_type=f32)
        wide, gain_grad, bias_grad = norm_grad(unit, inverse, gain, row_grad)
        gain_ref[...] = jnp.zeros_like(gain_ref)
        gain_ref[4:5, :] = gain_grad
        gain_ref[5:6, :] = bias_grad
        wide_ref[...] = wide
        dx2_ref[...] = wide.astype(bf16)
        sum_ref[...] = jnp.zeros_like(sum_ref)

    units = g_ref.shape[1] // 2
    total = None
    for which in range(2):
        some = slice(which * units, (which + 1) * units)
        active_grad = lax.dot_general(
            dx2_ref[...], down_ref[some, :], NT, preferred_element_type=f32
        )
        hidden = g_ref[:, some]
        slope = gauss_share(hidden) + hidden * (
            jnp.exp(-0.5 * hidden * hidden) * (2.0 * math.pi) ** -0.5
        )
        hidden_grad = (active_grad * slope).astype(bf16)
        dg_ref[which, 0] = hidden_grad
        part = lax.dot_general(hidden_grad, up_ref[which], NT, preferred_element_type=f32)
        total = part if total is None else total + part
    sum_ref[...] += total

    @pl.when(step == pl.num_programs(0) - 1)
    def _():
        unit, inverse = normed_parts(x1_ref[...])
        middle, gain_grad, bias_grad = norm_grad(unit, inverse, gains_ref[2:3, :], sum_ref[...])
        gain_ref[2:3, :] = gain_grad
        gain_ref[3:4, :] = bias_grad
        middle = wide_ref[...] + middle
        dx1_ref[...] = middle
        low_ref[...] = middle.astype(bf16)
        total = lax.dot_general(low_ref[...], out_ref[...], NT, preferred_element_type=f32)
        do_ref[...] = total.astype(bf16)


def branch_backward(pred_grad, x_last, x_mid, norm_gains, hidden, gathered, head):
    w_out, w_up, w_down, _ = gathered
    rows, width = x_last.shape
    parts, units = w_up.shape[0], w_up.shape[2]
    fixed = lambda shape: pl.BlockSpec(shape, lambda i: (0, 0))
    by_units = pl.BlockSpec((rows, 2 * units), lambda i: (0, i))
    by_core = pl.BlockSpec((2, 1, rows, units), lambda i: (0, i, 0, 0))
    columns = 4 * V
    wide = (rows, width)
    flops = 2 * rows * (width * width + 2 * width * parts * units + 12 * width * columns)
    return pl.pallas_call(
        branch_back_kernel,
        grid=(parts // 2,),
        out_shape=(
            jax.ShapeDtypeStruct(wide, bf16),
            jax.ShapeDtypeStruct((2, parts // 2, rows, units), bf16),
            jax.ShapeDtypeStruct(wide, f32),
            jax.ShapeDtypeStruct(wide, bf16),
            jax.ShapeDtypeStruct(wide, bf16),
            jax.ShapeDtypeStruct((6, width), f32),
            jax.ShapeDtypeStruct((columns, width), f32),
        ),
        in_specs=[
            fixed((rows, columns)),
            fixed(wide),
            fixed(wide),
            fixed(norm_gains.shape),
            by_units,
            *weight_specs(w_out, w_up, w_down),
            fixed(head.shape),
        ],
        out_specs=[
            fixed(wide),
            by_core,
            fixed(wide),
            fixed(wide),
            fixed(wide),
            fixed((6, width)),
            fixed((columns, width)),
        ],
        scratch_shapes=[pltpu.VMEM(wide, f32), pltpu.VMEM(wide, f32)],
        compiler_params=pltpu.CompilerParams(vmem_limit_bytes=BIG),
        cost_estimate=pl.CostEstimate(
            flops=flops,
            bytes_accessed=4 * width * parts * units + 6 * rows * parts * units,
            transcendentals=2 * rows * parts * units,
        ),
        name="branch_backward",
    )(pred_grad, x_last, x_mid, norm_gains, hidden, w_out, w_up, w_down, head)


def plane_parts(me):
    return [(move, lax.rem(me + move, 8)) for move in (7, 6, 5, 4, 3, 2, 1)]


def swap_kernel(*refs):
    value_ref, act_ref, dg_ref, o_ref, dx2_ref, h2_ref, dx1_ref = refs[:7]
    rows_ref, act_out, dg_out, o_out, dx2_out, h2_out, dx1_out = refs[7:14]
    send_sem, recv_sem, own_sem = refs[14:]
    dp, level, core = mesh_place()
    me = dp * 2 + core
    rows, width = value_ref.shape[0], value_ref.shape[1] // 8
    near = device_of(dp, level, 1 - core)
    barrier = pltpu.get_barrier_semaphore()
    others = [
        (part, device_of(part // 2, level, lax.rem(part, 2))) for _, part in plane_parts(me)
    ]
    for _, target in others:
        pl.semaphore_signal(barrier, inc=1, device_id=target, device_id_type=MESH)
    pl.semaphore_wait(barrier, 7)
    started = []

    def send(source, target_ref, target):
        slot = len(started)
        copy = pltpu.make_async_remote_copy(
            src_ref=source,
            dst_ref=target_ref,
            send_sem=send_sem.at[slot],
            recv_sem=recv_sem.at[slot],
            device_id=target,
            device_id_type=MESH,
        )
        copy.start()
        started.append(copy)

    def row_block(part):
        return rows_ref.at[pl.ds(pl.multiple_of(part * rows, rows), rows), :]

    def column_block(ref, part):
        return ref.at[:, pl.ds(pl.multiple_of(part * width, width), width)]

    for part, target in others:
        send(column_block(value_ref, part), row_block(me), target)
    locals_ = []

    def keep(source, target_ref):
        copy = pltpu.make_async_copy(source, target_ref, own_sem.at[len(locals_)])
        copy.start()
        locals_.append(copy)

    for source, out in ((act_ref, act_out), (dg_ref, dg_out)):
        send(source.at[1 - core], out.at[1], near)
        keep(source.at[core], out.at[0])
    for index in range(4):
        send(column_block(o_ref, index * 2 + 1 - core), o_out.at[1, index], near)
        keep(column_block(o_ref, index * 2 + core), o_out.at[0, index])
    for source, out in ((dx2_ref, dx2_out), (h2_ref, h2_out), (dx1_ref, dx1_out)):
        send(source, out, near)
    row_block(me)[...] = column_block(value_ref, me)[...]
    for copy in started:
        copy.wait()
    for copy in locals_:
        copy.wait()


def exchange_swap(value, act, dg, attended, dx2, h2, dx1):
    rows, width = value.shape
    anywhere = pl.BlockSpec(memory_space=pl.ANY)
    outs = [
        (8 * rows, width // 8), act.shape, dg.shape, (2, 4, rows, width // 8),
        dx2.shape, h2.shape, dx1.shape,
    ]
    return pl.pallas_call(
        swap_kernel,
        out_shape=[jax.ShapeDtypeStruct(shape, bf16) for shape in outs],
        in_specs=[VMEM] * 7,
        out_specs=[VMEM] + [anywhere] * 6,
        scratch_shapes=[
            pltpu.SemaphoreType.DMA((16,)),
            pltpu.SemaphoreType.DMA((16,)),
            pltpu.SemaphoreType.DMA((6,)),
        ],
        compiler_params=pltpu.CompilerParams(
            collective_id=3, has_side_effects=True, vmem_limit_bytes=BIG
        ),
        name="exchange_swap",
    )(value, act, dg, attended, dx2, h2, dx1)


class Scatter:
    order = (0, 3, 1, 2)

    def __init__(self, refs, sems):
        self.send_ref, self.keep_ref, self.one_ref, self.two_ref, self.own_ref, self.deep_ref = refs
        self.one, self.two, self.deep = sems
        self.dp, self.level, self.core = mesh_place()
        self.x, self.y = lax.rem(self.dp, 2), self.dp // 2
        self.side = device_of(self.dp + 1 - 2 * self.x, self.level, self.core)
        self.down = device_of(lax.rem(self.dp + 2, 4), self.level, self.core)

    def copy(self, source, target_ref, sems, slot, place, target):
        return pltpu.make_async_remote_copy(
            src_ref=source,
            dst_ref=target_ref,
            send_sem=sems.at[0, slot],
            recv_sem=sems.at[1, place],
            device_id=target,
            device_id_type=MESH,
        )

    def first(self, depth):
        target = self.side if depth < 2 else self.down
        return self.copy(
            self.send_ref.at[depth], self.one_ref.at[depth], self.one, depth, depth, target
        )

    def second(self, depth):
        target = self.down if depth < 2 else self.side
        which = 1 - self.y if depth < 2 else 1 - self.x
        return self.copy(
            self.keep_ref.at[depth, which], self.two_ref.at[depth], self.two, depth, depth, target
        )

    def mine(self, depth):
        return self.y if depth < 2 else self.x

    def third(self, depth):
        place = lax.rem(self.level + 7 - depth, 4)
        return self.copy(
            self.keep_ref.at[depth, self.mine(depth)], self.deep_ref.at[place], self.deep, depth,
            place, device_of(self.dp, depth, self.core),
        )

    def begin(self, depth, products, held_ref):
        height = self.keep_ref.shape[2]
        top = 0
        for product in products:
            rows, size = product.shape[0], product.shape[1] // 4
            for split in range(4):
                held_ref[split, top : top + rows, :] = product[
                    :, split * size : (split + 1) * size
                ].astype(bf16)
            top += rows
        for which in range(2):
            if depth < 2:
                moved, stays = which * 2 + 1 - self.x, which * 2 + self.x
            else:
                moved, stays = (1 - self.y) * 2 + which, self.y * 2 + which
            self.send_ref[depth, which] = held_ref[moved, :height, :]
            self.keep_ref[depth, which] = held_ref[stays, :height, :]
        self.first(depth).start()

    def middle(self, depth):
        self.first(depth).wait_recv()
        for which in range(2):
            self.keep_ref[depth, which] = (
                self.keep_ref[depth, which].astype(f32) + self.one_ref[depth, which].astype(f32)
            ).astype(bf16)
        self.second(depth).start()

    def end(self, depth):
        self.second(depth).wait_recv()
        total = self.keep_ref[depth, self.mine(depth)].astype(f32) + self.two_ref[depth].astype(f32)

        @pl.when(self.level == depth)
        def _():
            self.own_ref[...] = total

        @pl.when(self.level != depth)
        def _():
            self.keep_ref[depth, self.mine(depth)] = total.astype(bf16)
            self.third(depth).start()

    def finish(self, result_ref):
        for place in range(3):
            self.copy(
                self.keep_ref.at[0, 0], self.deep_ref.at[place], self.deep, 0, place, self.side
            ).wait_recv()
        result_ref[...] = self.own_ref[...] + (
            self.deep_ref[0].astype(f32) + self.deep_ref[1].astype(f32) + self.deep_ref[2].astype(f32)
        )
        for depth in range(4):
            self.first(depth).wait_send()
            self.second(depth).wait_send()

            @pl.when(self.level != depth)
            def _(depth=depth):
                self.third(depth).wait_send()


def scatter_scratch(height, share):
    return [
        pltpu.VMEM((4, 2, height, share), bf16),
        pltpu.VMEM((4, 2, height, share), bf16),
        pltpu.VMEM((4, 2, height, share), bf16),
        pltpu.VMEM((4, height, share), bf16),
        pltpu.VMEM((height, share), f32),
        pltpu.VMEM((3, height, share), bf16),
        pltpu.VMEM((4, height, share), bf16),
        pltpu.SemaphoreType.DMA((2, 4)),
        pltpu.SemaphoreType.DMA((2, 4)),
        pltpu.SemaphoreType.DMA((2, 4)),
    ]


def summed(lefts, rights):
    total = None
    for left, right in zip(lefts, rights):
        part = lax.dot_general(left, right, TN, preferred_element_type=f32)
        total = part if total is None else total + part
    return total


def chunk_spec(shape):
    def where(i):
        index = jnp.minimum(i, 3)
        first, last = (3 - index) // 3, index // 3
        middle = 1 - first - last
        return 0, middle * (5 - 2 * index) + 2 * last, 0, 0

    return pl.BlockSpec((2, 1) + shape, where)


def once(shape):
    return pl.BlockSpec(shape, lambda i: (0,) * len(shape), pipeline_mode=pl.Buffered(1))


class Returns:
    def __init__(self, grads_ref, token_out, width, sems, own_sem):
        self.grads_ref, self.token_out, self.width = grads_ref, token_out, width
        self.sems, self.own_sem = sems, own_sem
        dp, self.level, core = mesh_place()
        self.me = dp * 2 + core
        self.rows = grads_ref.shape[0] // 8

    def part(self, move):
        return lax.rem(self.me + move, 8)

    def refs(self, part, start, size):
        rows = pl.ds(pl.multiple_of(part * self.rows, self.rows), self.rows)
        first = self.me * 3 * self.width + start
        columns = pl.ds(pl.multiple_of(first, self.width), size)
        return self.grads_ref.at[rows, start : start + size], self.token_out.at[:, columns]

    def copy(self, move, late):
        start, size = (self.width, 2 * self.width) if late else (0, self.width)
        part = self.part(move)
        source, target_ref = self.refs(part, start, size)
        return pltpu.make_async_remote_copy(
            src_ref=source,
            dst_ref=target_ref,
            send_sem=self.sems.at[2 * late, move],
            recv_sem=self.sems.at[2 * late + 1, move],
            device_id=device_of(part // 2, self.level, lax.rem(part, 2)),
            device_id_type=MESH,
        )

    def own(self):
        source, target_ref = self.refs(self.me, 0, 3 * self.width)
        return pltpu.make_async_copy(source, target_ref, self.own_sem)

    def peers(self):
        parts = [self.part(move) for move in range(1, 8)]
        return [device_of(part // 2, self.level, lax.rem(part, 2)) for part in parts]

    def finish(self):
        for move in range(1, 8):
            self.copy(move, 0).wait()
            self.copy(move, 1).wait()
        self.own().wait()


def attend_turns(turn, returns, qkv_ref, do_ref, full_ref, lse_ref, dqkv_ref, kt_ref, dk_sum, dv_sum):
    width = do_ref.shape[1]
    heads = width // HEAD_DIM
    rows = returns.rows

    @pl.when(turn == 0)
    def _():
        kt_ref[...] = qkv_ref[:, width : 2 * width].T
        dk_sum[...] = jnp.zeros_like(dk_sum)
        dv_sum[...] = jnp.zeros_like(dv_sum)

    @pl.when((turn >= 0) & (turn < 8))
    def _():
        part = returns.part(turn + 1)
        where = pl.ds(pl.multiple_of(part * rows, rows), rows)
        sums = [lse_ref[head : head + 1, where] for head in range(heads)]
        dqkv_ref[where, :width] = attend_back_rows(
            heads, 1024, qkv_ref[where, :width], do_ref[where, :], full_ref[where, :], sums,
            qkv_ref.at[:, width : 2 * width], qkv_ref.at[:, 2 * width :], kt_ref, dk_sum, dv_sum,
        )

    @pl.when((turn >= 0) & (turn < 7))
    def _():
        returns.copy(turn + 1, 0).start()

    @pl.when(turn == 8)
    def _():
        dqkv_ref[:, width : 2 * width] = dk_sum[...].astype(bf16)
        dqkv_ref[:, 2 * width :] = dv_sum[...].astype(bf16)
        for move in (7, 6, 5, 4, 3, 2, 1):
            returns.copy(move, 1).start()
        returns.own().start()


def attend_exchange_kernel(
    qkv_ref, do_ref, full_ref, lse_ref, rows_ref, token_out, grad_ref,
    dqkv_ref, kt_ref, dk_sum, dv_sum, sems, own_sem,
):
    turn = pl.program_id(0)
    returns = Returns(dqkv_ref, token_out, do_ref.shape[1], sems, own_sem)

    @pl.when(turn == 0)
    def _():
        barrier = pltpu.get_barrier_semaphore()
        for target in returns.peers():
            pl.semaphore_signal(barrier, inc=1, device_id=target, device_id_type=MESH)
        pl.semaphore_wait(barrier, 7)

    attend_turns(
        turn, returns, qkv_ref, do_ref, full_ref, lse_ref, dqkv_ref, kt_ref, dk_sum, dv_sum
    )

    @pl.when(turn >= pieces_at)
    def _():
        grad_ref[...] = lax.dot_general(
            rows_ref[...], dqkv_ref[...], TN, preferred_element_type=f32
        )

    @pl.when(turn == pieces_at + 3)
    def _():
        returns.finish()


def attend_exchange(packed, own_grad, full, logsum, rows_one):
    rows, width = own_grad.shape[0] // 8, own_grad.shape[1]
    piece = lambda i: jnp.clip(i - pieces_at, 0, 3)
    return pl.pallas_call(
        attend_exchange_kernel,
        grid=(pieces_at + 4,),
        out_shape=[
            jax.ShapeDtypeStruct((rows, 24 * width), bf16),
            jax.ShapeDtypeStruct((D, 3 * width), f32),
        ],
        in_specs=[
            once(packed.shape),
            once(own_grad.shape),
            once(full.shape),
            once(logsum.shape),
            pl.BlockSpec((8 * rows, D // 4), lambda i: (0, piece(i))),
        ],
        out_specs=[
            pl.BlockSpec(memory_space=pl.ANY),
            pl.BlockSpec((D // 4, 3 * width), lambda i: (piece(i), 0)),
        ],
        scratch_shapes=[
            pltpu.VMEM((8 * rows, 3 * width), bf16),
            pltpu.VMEM((width, 8 * rows), bf16),
            pltpu.VMEM((8 * rows, width), f32),
            pltpu.VMEM((8 * rows, width), f32),
            pltpu.SemaphoreType.DMA((4, 8)),
            pltpu.SemaphoreType.DMA,
        ],
        compiler_params=pltpu.CompilerParams(
            collective_id=8, has_side_effects=True, vmem_limit_bytes=BIG
        ),
        name="attend_exchange",
    )(packed, own_grad, full, logsum, rows_one)


pieces_at, entry_turns, attend_from = 9, 11, 4
middle_at, end_at = (5, 6, 8, 9), (7, 8, 10, 11)


def finish_kernel(*refs):
    steps = (refs[0:3], refs[3:6])
    qkv_ref, do_ref, full_ref, lse_ref, rows_ref, prev_ref = refs[6:12]
    token_out, share_ref, down_ref = refs[12:15]
    dqkv_ref, kt_ref, dk_sum, dv_sum, piece_send, piece_recv, piece_own = refs[15:22]
    part_sem, piece_sem, own_sem = refs[22:25]
    scatter = Scatter(refs[25:31], refs[32:35])
    held_ref = refs[31]
    turn = pl.program_id(0)
    dp, level, core = mesh_place()
    width = do_ref.shape[1]
    returns = Returns(dqkv_ref, token_out, width, part_sem, own_sem)

    def remote(source, target_ref, send_sem, recv_sem, target):
        return pltpu.make_async_remote_copy(
            src_ref=source,
            dst_ref=target_ref,
            send_sem=send_sem,
            recv_sem=recv_sem,
            device_id=target,
            device_id_type=MESH,
        )

    def piece_copy(index):
        place = lax.rem(level + 7 - index, 4)
        return remote(
            piece_send.at[index], piece_recv.at[place], piece_sem.at[0, index],
            piece_sem.at[1, place], device_of(dp, index, core),
        )

    @pl.when(turn == 0)
    def _():
        barrier = pltpu.get_barrier_semaphore()
        deep = [device_of(dp, lax.rem(level + move, 4), core) for move in (1, 2, 3)]
        for target in returns.peers() + deep:
            pl.semaphore_signal(barrier, inc=1, device_id=target, device_id_type=MESH)
        pl.semaphore_wait(barrier, 10)

    for index, depth in enumerate(scatter.order):

        @pl.when(turn == index)
        def _(depth=depth):
            lefts, rights = [], []
            for act, dx2, dx2_near in steps:
                lefts += [act[0, 0], act[1, 0]]
                rights += [dx2[...], dx2_near[...]]
            scatter.begin(depth, [summed(lefts, rights)], held_ref)

        @pl.when(turn == middle_at[index])
        def _(depth=depth):
            scatter.middle(depth)

        @pl.when(turn == end_at[index])
        def _(depth=depth):
            scatter.end(depth)

    attend_turns(
        turn - attend_from, returns, qkv_ref, do_ref, full_ref, lse_ref, dqkv_ref, kt_ref, dk_sum, dv_sum
    )

    for index in range(4):

        @pl.when(turn == attend_from + pieces_at + index)
        def _(index=index):
            piece = prev_ref[...] + lax.dot_general(
                rows_ref[...], dqkv_ref[...], TN, preferred_element_type=f32
            )

            @pl.when(level == index)
            def _():
                piece_own[...] = piece

            @pl.when(level != index)
            def _():
                piece_send[index] = piece.astype(bf16)
                piece_copy(index).start()

    @pl.when(turn == attend_from + pieces_at + 4)
    def _():
        scatter.finish(down_ref)
        for place in range(3):
            remote(
                piece_send.at[0], piece_recv.at[place], piece_sem.at[0, 0],
                piece_sem.at[1, place], scatter.side,
            ).wait_recv()
        share_ref[...] = piece_own[...] + (
            piece_recv[0].astype(f32) + piece_recv[1].astype(f32) + piece_recv[2].astype(f32)
        )
        returns.finish()
        for index in range(4):

            @pl.when(level != index)
            def _(index=index):
                piece_copy(index).wait_send()


def finish_program(kept, packed, own_grad, full, logsum, rows_one, earlier):
    rows, width = own_grad.shape[0] // 8, own_grad.shape[1]
    in_specs, operands = [], []
    for act, dx2, dx2_near in kept:
        operands += [act, dx2, dx2_near]
        in_specs += [chunk_spec(act.shape[2:]), once(dx2.shape), once(dx2.shape)]
    piece = lambda i: jnp.clip(i - attend_from - pieces_at, 0, 3)
    in_specs += [
        once(packed.shape),
        once(own_grad.shape),
        once(full.shape),
        once(logsum.shape),
        pl.BlockSpec((8 * rows, D // 4), lambda i: (0, piece(i))),
        pl.BlockSpec((D // 4, 3 * width), lambda i: (piece(i), 0)),
    ]
    operands += [packed, own_grad, full, logsum, rows_one, earlier]
    fixed = lambda shape: pl.BlockSpec(shape, lambda i: (0, 0))
    units = kept[0][0].shape[3]
    share = D // 4
    return pl.pallas_call(
        finish_kernel,
        grid=(attend_from + pieces_at + 5,),
        out_shape=[
            jax.ShapeDtypeStruct((rows, 24 * width), bf16),
            jax.ShapeDtypeStruct((share, 3 * width), f32),
            jax.ShapeDtypeStruct((units, share), f32),
        ],
        in_specs=in_specs,
        out_specs=[
            pl.BlockSpec(memory_space=pl.ANY),
            fixed((share, 3 * width)),
            fixed((units, share)),
        ],
        scratch_shapes=[
            pltpu.VMEM((8 * rows, 3 * width), bf16),
            pltpu.VMEM((width, 8 * rows), bf16),
            pltpu.VMEM((8 * rows, width), f32),
            pltpu.VMEM((8 * rows, width), f32),
            pltpu.VMEM((4, share, 3 * width), bf16),
            pltpu.VMEM((3, share, 3 * width), bf16),
            pltpu.VMEM((share, 3 * width), f32),
            pltpu.SemaphoreType.DMA((4, 8)),
            pltpu.SemaphoreType.DMA((2, 4)),
            pltpu.SemaphoreType.DMA,
        ]
        + scatter_scratch(units, share),
        compiler_params=pltpu.CompilerParams(
            collective_id=4, has_side_effects=True, vmem_limit_bytes=BIG
        ),
        name="finish_program",
    )(*operands)


def tie(*values):
    return lax.optimization_barrier(values)


def choose(value, index, axis=0):
    return lax.dynamic_index_in_dim(value, index, axis, keepdims=False)


def outer_plain(lefts, rights, by_rows):
    dp, mp = lax.axis_size("dp"), lax.axis_size("mp")
    grads = sum(
        lax.dot_general(left, right, TN, preferred_element_type=f32)
        for left, right in zip(lefts, rights)
    ).astype(bf16)
    rows, width = grads.shape
    if by_rows:
        grads = grads.reshape(dp, rows // dp, mp, width // mp).transpose(0, 2, 1, 3)
    else:
        grads = grads.reshape(mp, rows // mp, dp, width // dp).transpose(2, 0, 1, 3)
    grads = grads.reshape((dp * mp,) + grads.shape[2:])
    return lax.psum_scatter(grads, ("dp", "mp"), scatter_dimension=0, tiled=False).astype(f32)


def exchange_sum_kernel(
    x_ref, loss_ref, qkv_ref, up_out_ref, down_ref, o_ref, s_ref, share_ref, work_ref, pair_ref, quad_ref, eight_ref, deep_ref, tile_ref,
    landing_ref, cross_sem, send_sem, recv_sem,
):
    dp, level, core = mesh_place()
    x, y = lax.rem(dp, 2), dp // 2
    side = device_of(dp + 1 - 2 * x, level, core)
    down = device_of(lax.rem(dp + 2, 4), level, core)
    near = device_of(dp, level, 1 - core)
    deep = [device_of(dp, lax.rem(level + step, 4), core) for step in (1, 2, 3)]
    barrier = pltpu.get_barrier_semaphore()
    for target in (side, down, near, *deep):
        pl.semaphore_signal(barrier, inc=1, device_id=target, device_id_type=MESH)
    across = device_of(level, dp, core)
    crossing = pltpu.make_async_remote_copy(
        src_ref=qkv_ref,
        dst_ref=landing_ref,
        send_sem=cross_sem.at[0],
        recv_sem=cross_sem.at[1],
        device_id=across,
        device_id_type=MESH,
    )

    @pl.when(dp != level)
    def _():
        pl.semaphore_signal(barrier, inc=1, device_id=across, device_id_type=MESH)
        pl.semaphore_wait(barrier, 7)
        crossing.start()

    @pl.when(dp == level)
    def _():
        pl.semaphore_wait(barrier, 6)

    started = []

    def send(source, target_ref, target):
        slot = len(started)
        copy = pltpu.make_async_remote_copy(
            src_ref=source,
            dst_ref=target_ref,
            send_sem=send_sem.at[slot],
            recv_sem=recv_sem.at[slot],
            device_id=target,
            device_id_type=MESH,
        )
        copy.start()
        started.append(copy)
        return copy

    half = x_ref.shape[0] // 2
    quarter, eighth, part, unit = half // 2, half // 4, half // 8, half // 16

    def rows(start, size):
        return pl.ds(pl.multiple_of(start, unit), size)

    copy = send(x_ref.at[rows((1 - core) * half, half)], pair_ref, near)
    copy.wait_recv()
    work_ref[...] = x_ref[rows(core * half, half)] + pair_ref[...]
    one = send(work_ref.at[rows((1 - x) * eighth, eighth)], quad_ref.at[0], side)
    two = send(work_ref.at[rows(quarter + (1 - y) * eighth, eighth)], quad_ref.at[1], down)
    base_a = x * eighth
    base_b = quarter + y * eighth
    wide_a, wide_b = core * half + base_a, core * half + base_b
    one.wait_recv()
    work_ref[rows(base_a, eighth)] += quad_ref[0]
    one = send(work_ref.at[rows(base_a + (1 - y) * part, part)], eight_ref.at[0], down)
    two.wait_recv()
    work_ref[rows(base_b, eighth)] += quad_ref[1]
    two = send(work_ref.at[rows(base_b + (1 - x) * part, part)], eight_ref.at[1], side)
    base_a = base_a + y * part
    base_b = base_b + x * part
    one.wait_recv()
    work_ref[rows(base_a, part)] += eight_ref[0]
    two.wait_recv()
    work_ref[rows(base_b, part)] += eight_ref[1]

    def level_start(which):
        late = which // 2
        return (1 - late) * base_a + late * base_b + lax.rem(which, 2) * unit

    copies = []
    for step in (1, 2, 3):
        source = work_ref.at[rows(level_start(lax.rem(level + step, 4)), unit)]
        copies.append(send(source, deep_ref.at[step - 1], deep[step - 1]))
    for copy in copies:
        copy.wait_recv()
    total = work_ref[rows(level_start(level), unit)] + deep_ref[0] + deep_ref[1] + deep_ref[2]
    mine = rows(core * half + level_start(level), unit)
    base_a = core * half + base_a
    base_b = core * half + base_b
    o_ref[mine] = total
    row = lax.broadcasted_iota(jnp.int32, s_ref.shape, 0)
    squares = jnp.sum(total * total)
    for ref in (qkv_ref, up_out_ref, down_ref):
        squares += jnp.sum(ref[...] * ref[...])
    tile_ref[0] = jnp.where(row == 0, squares, jnp.where(row == 1, loss_ref[...], 0.0))
    copies = []
    for step in (1, 2, 3):
        copies.append(send(o_ref.at[mine], o_ref.at[mine], deep[step - 1]))
        copies.append(send(tile_ref.at[0], tile_ref.at[step], deep[step - 1]))
    for copy in copies:
        copy.wait_recv()
    one = send(o_ref.at[rows(base_a, part)], o_ref.at[rows(base_a, part)], down)
    two = send(o_ref.at[rows(base_b, part)], o_ref.at[rows(base_b, part)], side)
    tile_ref[4] = tile_ref[0] + tile_ref[1] + tile_ref[2] + tile_ref[3]
    three = send(tile_ref.at[4], tile_ref.at[5], side)
    one.wait_recv()
    one = send(o_ref.at[rows(wide_a, eighth)], o_ref.at[rows(wide_a, eighth)], side)
    two.wait_recv()
    two = send(o_ref.at[rows(wide_b, eighth)], o_ref.at[rows(wide_b, eighth)], down)
    three.wait_recv()
    tile_ref[6] = tile_ref[4] + tile_ref[5]
    three = send(tile_ref.at[6], tile_ref.at[7], down)
    one.wait_recv()
    two.wait_recv()
    one = send(o_ref.at[rows(core * half, half)], o_ref.at[rows(core * half, half)], near)
    three.wait_recv()
    tile_ref[8] = tile_ref[6] + tile_ref[7]
    three = send(tile_ref.at[8], tile_ref.at[9], near)
    one.wait_recv()
    three.wait_recv()
    s_ref[...] = tile_ref[8] + tile_ref[9]
    for copy in started:
        copy.wait_send()

    @pl.when(dp != level)
    def _():
        crossing.wait()
        share_ref[...] = landing_ref[...]

    @pl.when(dp == level)
    def _():
        share_ref[...] = qkv_ref[...]


def exchange_sum(value, loss, *shares):
    rows, width = value.shape
    tile = jax.ShapeDtypeStruct((8, 128), f32)
    return pl.pallas_call(
        exchange_sum_kernel,
        out_shape=(
            jax.ShapeDtypeStruct(value.shape, f32), tile, jax.ShapeDtypeStruct(shares[0].shape, f32)
        ),
        in_specs=[VMEM] * 5,
        out_specs=[VMEM] * 3,
        scratch_shapes=[
            pltpu.VMEM((rows // 2, width), f32),
            pltpu.VMEM((rows // 2, width), f32),
            pltpu.VMEM((2, rows // 8, width), f32),
            pltpu.VMEM((2, rows // 16, width), f32),
            pltpu.VMEM((3, rows // 32, width), f32),
            pltpu.VMEM((10,) + tile.shape, f32),
            pltpu.VMEM(shares[0].shape, f32),
            pltpu.SemaphoreType.DMA((2,)),
            pltpu.SemaphoreType.DMA((24,)),
            pltpu.SemaphoreType.DMA((24,)),
        ],
        compiler_params=pltpu.CompilerParams(
            collective_id=5, has_side_effects=True, vmem_limit_bytes=BIG
        ),
        name="exchange_sum",
    )(value, loss.reshape(1, 1), *shares)


def split_low(values):
    high = values.astype(bf16)
    return high, (values - high.astype(f32)).astype(bf16)


def three_products(left, right, dims=(((1,), (0,)), ((), ()))):
    def product(one, two):
        return lax.dot_general(one, two, dims, preferred_element_type=f32)

    return product(left[0], right[0]) + (product(left[1], right[0]) + product(left[0], right[1]))


def exact_product(left, right, dims=(((1,), (0,)), ((), ()))):
    return lax.dot_general(left, right, dims, precision=highest, preferred_element_type=f32)


def head_marks(width):
    head = lax.broadcasted_iota(jnp.int32, (HEADS, width), 0)
    column = lax.broadcasted_iota(jnp.int32, (HEADS, width), 1)
    return jnp.where(column // HEAD_DIM == head, 1.0, 0.0).astype(f32)


def quarter_marks(padded):
    row = lax.broadcasted_iota(jnp.int32, (padded, V), 0)
    column = lax.broadcasted_iota(jnp.int32, (padded, V), 1)
    return jnp.where(row // 4 == column, 0.25, 0.0).astype(f32)


def tables_kernel(tables_ref, hot_ref, patch_ref, var_ref, keyed_ref, bias_ref):
    padded, width = patch_ref.shape
    query = tables_ref[5 * V + LEADS : 5 * V + LEADS + 1, :]
    patch_ref[...] = jnp.zeros_like(patch_ref)
    patch_ref[: 4 * V, :] = tables_ref[: 4 * V, :]
    chosen = exact_product(hot_ref[...], tables_ref[4 * V : 5 * V, :])
    var_ref[...] = exact_product(quarter_marks(padded), chosen)
    marks = head_marks(width)
    scale = HEAD_DIM**-0.5
    keyed_ref[...] = exact_product(marks, patch_ref[...] * query, NT) * scale
    bias = exact_product(marks, var_ref[...] * query, NT) * (4.0 * scale)
    column = lax.broadcasted_iota(jnp.int32, bias.shape, 1)
    bias_ref[...] = jnp.where(column < 4 * V, bias, -1e30)


def prepare_tables(tables, var_hot):
    padded = 256
    return pl.pallas_call(
        tables_kernel,
        out_shape=(
            jax.ShapeDtypeStruct((padded, D), f32),
            jax.ShapeDtypeStruct((padded, D), f32),
            jax.ShapeDtypeStruct((HEADS, padded), f32),
            jax.ShapeDtypeStruct((HEADS, padded), f32),
        ),
        compiler_params=pltpu.CompilerParams(vmem_limit_bytes=BIG),
        name="prepare_tables",
    )(tables, var_hot)


def four_sum(values):
    size = values.shape[1]
    lane = lax.broadcasted_iota(jnp.int32, values.shape, 1)
    values = values + jnp.where(
        lane % 2 == 0, pltpu.roll(values, size - 1, 1), pltpu.roll(values, 1, 1)
    )
    return values + jnp.where(
        lane % 4 < 2, pltpu.roll(values, size - 2, 1), pltpu.roll(values, 2, 1)
    )


def cell_shares(cells, keyed, bias):
    scores = four_sum(cells * keyed) + bias
    raised = jnp.exp(scores - jnp.max(scores, axis=1, keepdims=True))
    total = jnp.sum(raised, axis=1, keepdims=True) * 0.25
    return raised * (1.0 / total)


def embed_pair(pair, cells, keyed_ref, bias_ref, patch_ref, var_ref, x0_ref):
    patch = split_low(patch_ref[...])
    variable = split_low(var_ref[...])
    outs = []
    for which in range(2):
        row = pl.ds(pair * 2 + which, 1)
        shares = cell_shares(cells, keyed_ref[row, :], bias_ref[row, :])
        outs.append(
            three_products(split_low(shares * cells), patch)
            + three_products(split_low(shares), variable)
        )
    lane = lax.broadcasted_iota(jnp.int32, outs[0].shape, 1)
    columns = pl.ds(pl.multiple_of(pair * 2 * HEAD_DIM, 2 * HEAD_DIM), 2 * HEAD_DIM)
    x0_ref[:, columns] = jnp.where(lane < HEAD_DIM, outs[0], outs[1])


def embed_kernel(
    u_ref, keyed_ref, bias_ref, patch_ref, var_ref, lead_ref, gains_ref, x0_ref, h1_ref
):
    pair = pl.program_id(0)
    embed_pair(pair, u_ref[...], keyed_ref, bias_ref, patch_ref, var_ref, x0_ref)

    @pl.when(pair == pl.num_programs(0) - 1)
    def _():
        x0_ref[...] += lead_ref[...]
        unit, _ = normed_parts(x0_ref[...])
        h1_ref[...] = (unit * gains_ref[0:1, :] + gains_ref[1:2, :]).astype(bf16)


def embed_forward(cells, prepared, lead_row, norm_gains):
    patch, variable, keyed, bias = prepared
    rows, padded = cells.shape
    fixed = lambda shape: pl.BlockSpec(shape, lambda i: (0, 0))
    by_pair = pl.BlockSpec((padded, 2 * HEAD_DIM), lambda i: (0, i))
    return pl.pallas_call(
        embed_kernel,
        grid=(HEADS // 2,),
        out_shape=(
            jax.ShapeDtypeStruct((rows, D), f32),
            jax.ShapeDtypeStruct((rows, D), bf16),
        ),
        in_specs=[
            fixed((rows, padded)),
            fixed(keyed.shape),
            fixed(bias.shape),
            by_pair,
            by_pair,
            fixed((1, D)),
            fixed(norm_gains.shape),
        ],
        out_specs=[fixed((rows, D)), fixed((rows, D))],
        compiler_params=pltpu.CompilerParams(vmem_limit_bytes=BIG),
        cost_estimate=pl.CostEstimate(
            flops=24 * rows * padded * D, bytes_accessed=14 * rows * D, transcendentals=16 * rows * padded
        ),
        name="embed_forward",
    )(cells, keyed, bias, patch, variable, lead_row, norm_gains)


def entry_rows(
    grad_ref, qkv_ref, x0_ref, mid_ref, gains_ref, du_ref, gain_ref, lead_ref, dx_ref, flip_ref
):
    row_grad = jnp.dot(grad_ref[...], qkv_ref[...], preferred_element_type=f32)
    unit, inverse = normed_parts(x0_ref[...])
    part, gain_grad, bias_grad = norm_grad(unit, inverse, gains_ref[0:1, :], row_grad)
    total = mid_ref[...] + part
    dx_ref[...] = total
    flip_ref[...] = total.T
    lead_ref[...] = jnp.sum(total, axis=0, keepdims=True)
    gain_ref[0:1, :] = gain_grad
    gain_ref[1:2, :] = bias_grad
    du_ref[...] = jnp.zeros_like(du_ref)


def entry_pair(
    pair, u_ref, keyed_ref, bias_ref, patch_ref, var_ref,
    du_ref, dpatch_ref, dvar_ref, dkeyed_ref, dbias_ref, dx_ref, flip_ref,
):
    cells = u_ref[...]
    size = 2 * HEAD_DIM
    columns = pl.ds(pl.multiple_of(pair * size, size), size)
    grads = dx_ref[:, columns]
    lane = lax.broadcasted_iota(jnp.int32, grads.shape, 1)
    patch = split_low(patch_ref[...])
    variable = split_low(var_ref[...])
    cells_grad = None
    for which in range(2):
        row = pl.ds(pair * 2 + which, 1)
        keyed = keyed_ref[row, :]
        shares = cell_shares(cells, keyed, bias_ref[row, :])
        one = split_low(jnp.where(lane // HEAD_DIM == which, grads, 0.0))
        mixed_grad = three_products(one, patch, NT)
        share_grad = mixed_grad * cells + three_products(one, variable, NT)
        weighted = shares * share_grad
        inner = jnp.sum(weighted, axis=1, keepdims=True)
        score_grad = four_sum(weighted) - shares * inner
        piece = mixed_grad * shares + score_grad * keyed
        cells_grad = piece if cells_grad is None else cells_grad + piece
        scale = HEAD_DIM**-0.5
        dkeyed_ref[row, :] = jnp.sum(score_grad * cells, axis=0, keepdims=True) * scale
        dbias_ref[row, :] = jnp.sum(score_grad, axis=0, keepdims=True) * scale
        rows = pl.ds(pl.multiple_of(pair * size + which * HEAD_DIM, HEAD_DIM), HEAD_DIM)
        flipped = split_low(flip_ref[rows, :])
        mine = slice(which * HEAD_DIM, (which + 1) * HEAD_DIM)
        dpatch_ref[mine, :] = three_products(flipped, split_low(shares * cells))
        dvar_ref[mine, :] = three_products(flipped, split_low(shares))
    du_ref[...] += cells_grad


def entry_back_kernel(
    grad_ref, qkv_ref, x0_ref, mid_ref, gains_ref, u_ref, keyed_ref, bias_ref, patch_ref, var_ref,
    du_ref, gain_ref, lead_ref, dpatch_ref, dvar_ref, dkeyed_ref, dbias_ref,
    dx_ref, flip_ref,
):
    pair = pl.program_id(0)

    @pl.when(pair == 0)
    def _():
        entry_rows(
            grad_ref, qkv_ref, x0_ref, mid_ref, gains_ref, du_ref, gain_ref, lead_ref, dx_ref,
            flip_ref,
        )

    size = 2 * HEAD_DIM
    for which in range(2):
        some = slice(which * size, (which + 1) * size)
        entry_pair(
            pair * 2 + which, u_ref, keyed_ref, bias_ref, patch_ref.at[:, some],
            var_ref.at[:, some], du_ref, dpatch_ref.at[some, :], dvar_ref.at[some, :],
            dkeyed_ref, dbias_ref, dx_ref, flip_ref,
        )


def entry_last_kernel(*refs):
    steps = (refs[0:6], refs[6:12])
    grad_ref, qkv_ref, x0_ref, mid_ref, gains_ref, u_ref, keyed_ref, bias_ref = refs[12:20]
    patch_ref, var_ref, query_ref, hot_ref, lead_hot_ref, head_a, head_b, high_a, high_b = refs[20:29]
    patch_a, var_a, keyed_a, bias_a, lead_a, gain_a = refs[29:35]
    rows_out, up_out_ref = refs[35:37]
    (dx_ref, flip_ref, du_ref, gain_ref, lead_ref, dpatch_ref, dvar_ref, dkeyed_ref,
     dbias_ref) = refs[37:46]
    scatter = Scatter(refs[46:52], refs[53:56])
    held_ref = refs[52]
    turn = pl.program_id(0)
    dp, level, core = mesh_place()

    @pl.when(turn == 0)
    def _():
        barrier = pltpu.get_barrier_semaphore()
        deep = [device_of(dp, lax.rem(level + move, 4), core) for move in (1, 2, 3)]
        for target in (scatter.side, scatter.down, *deep):
            pl.semaphore_signal(barrier, inc=1, device_id=target, device_id_type=MESH)
        pl.semaphore_wait(barrier, 5)

    for index, depth in enumerate(scatter.order):

        @pl.when(turn == index)
        def _(depth=depth):
            lefts, rights, smalls, wides = [], [], [], []
            for dg, o, h2, h2_near, dx1, dx1_near in steps:
                lefts += [dg[0, 0], dg[1, 0]]
                rights += [h2[...], h2_near[...]]
                smalls += [o[0, 0], o[1, 0]]
                wides += [dx1[...], dx1_near[...]]
            scatter.begin(depth, [summed(lefts, rights), summed(smalls, wides)], held_ref)

        @pl.when(turn == index + 3)
        def _(depth=depth):
            scatter.middle(depth)

        @pl.when(turn == index + 6)
        def _(depth=depth):
            scatter.end(depth)

    @pl.when(turn == 0)
    def _():
        entry_rows(
            grad_ref, qkv_ref, x0_ref, mid_ref, gains_ref, du_ref, gain_ref,
            lead_ref.at[0:1, :], dx_ref, flip_ref,
        )

    @pl.when((turn >= 1) & (turn <= HEADS // 2))
    def _():
        size = 2 * HEAD_DIM
        pair = turn - 1
        some = pl.ds(pl.multiple_of(pair * size, size), size)
        entry_pair(
            pair, u_ref, keyed_ref, bias_ref, patch_ref.at[:, some], var_ref.at[:, some],
            du_ref, dpatch_ref.at[some, :], dvar_ref.at[some, :], dkeyed_ref, dbias_ref,
            dx_ref, flip_ref,
        )

    @pl.when(turn == entry_turns - 2)
    def _():
        gain_ref[...] += gain_a[...]
        lead_ref[1:2, :] = lead_a[...]
        lead_ref[2:8, :] = jnp.zeros((6, lead_ref.shape[1]), f32)
        table_rows(
            patch_a, dpatch_ref, var_a, dvar_ref, keyed_a, dkeyed_ref, bias_a, dbias_ref,
            patch_ref, var_ref, query_ref, hot_ref, lead_hot_ref, lead_ref, gain_ref,
            (head_a[...], head_b[...]), (high_a[2:6, :], high_b[2:6, :]), rows_out,
        )

    @pl.when(turn == entry_turns - 1)
    def _():
        scatter.finish(up_out_ref)


def entry_last(
    kept, token_grad, qkv_t, x_first, mid_grad, norm_gains, cells, prepared,
    query, var_hot, lead_hots, heads, highs, earlier,
):
    patch, variable, keyed, bias = prepared
    rows, width = x_first.shape
    padded = cells.shape[1]
    in_specs, operands = [], []
    for dg, o, h2, h2_near, dx1, dx1_near in kept:
        operands += [dg, o, h2, h2_near, dx1, dx1_near]
        in_specs += [chunk_spec(dg.shape[2:]), chunk_spec(o.shape[2:])]
        in_specs += [once(h2.shape)] * 4
    values = [
        token_grad, qkv_t, x_first, mid_grad, norm_gains, cells, keyed, bias,
        patch, variable, query, var_hot, lead_hots, *heads, *highs, *earlier,
    ]
    in_specs += [once(value.shape) for value in values]
    height, columns = kept[0][0].shape[3] + kept[0][1].shape[3], width // 4
    outs = [(2 * padded, width), (height, columns)]
    return pl.pallas_call(
        entry_last_kernel,
        grid=(entry_turns,),
        out_shape=[jax.ShapeDtypeStruct(shape, f32) for shape in outs],
        in_specs=in_specs,
        out_specs=[pl.BlockSpec(shape, lambda i: (0, 0)) for shape in outs],
        scratch_shapes=[
            pltpu.VMEM((rows, width), f32),
            pltpu.VMEM((width, rows), f32),
            pltpu.VMEM((rows, padded), f32),
            pltpu.VMEM((2, width), f32),
            pltpu.VMEM((8, width), f32),
            pltpu.VMEM((width, padded), f32),
            pltpu.VMEM((width, padded), f32),
            pltpu.VMEM(keyed.shape, f32),
            pltpu.VMEM(bias.shape, f32),
        ]
        + scatter_scratch(height, columns),
        compiler_params=pltpu.CompilerParams(
            collective_id=6, has_side_effects=True, vmem_limit_bytes=BIG
        ),
        name="entry_last",
    )(*operands, *values)


def entry_backward(token_grad, qkv_t, x_first, mid_grad, norm_gains, cells, prepared):
    patch, variable, keyed, bias = prepared
    rows, width = x_first.shape
    padded = cells.shape[1]
    fixed = lambda shape: pl.BlockSpec(shape, lambda i: (0, 0))
    by_pair = pl.BlockSpec((padded, 4 * HEAD_DIM), lambda i: (0, i))
    flipped = pl.BlockSpec((4 * HEAD_DIM, padded), lambda i: (i, 0))
    return pl.pallas_call(
        entry_back_kernel,
        grid=(HEADS // 4,),
        out_shape=(
            jax.ShapeDtypeStruct((rows, padded), f32),
            jax.ShapeDtypeStruct((2, width), f32),
            jax.ShapeDtypeStruct((1, width), f32),
            jax.ShapeDtypeStruct((width, padded), f32),
            jax.ShapeDtypeStruct((width, padded), f32),
            jax.ShapeDtypeStruct(keyed.shape, f32),
            jax.ShapeDtypeStruct(bias.shape, f32),
        ),
        in_specs=[
            fixed(token_grad.shape),
            fixed(qkv_t.shape),
            fixed((rows, width)),
            fixed((rows, width)),
            fixed(norm_gains.shape),
            fixed(cells.shape),
            fixed(keyed.shape),
            fixed(bias.shape),
            by_pair,
            by_pair,
        ],
        out_specs=[
            fixed((rows, padded)),
            fixed((2, width)),
            fixed((1, width)),
            flipped,
            flipped,
            fixed(keyed.shape),
            fixed(bias.shape),
        ],
        scratch_shapes=[pltpu.VMEM((rows, width), f32), pltpu.VMEM((width, rows), f32)],
        compiler_params=pltpu.CompilerParams(vmem_limit_bytes=BIG),
        cost_estimate=pl.CostEstimate(
            flops=60 * rows * padded * D, bytes_accessed=40 * rows * D, transcendentals=16 * rows * padded
        ),
        name="entry_backward",
    )(token_grad, qkv_t, x_first, mid_grad, norm_gains, cells, keyed, bias, patch, variable)


def table_rows(
    pa_ref, pb_ref, va_ref, vb_ref, ka_ref, kb_ref, ba_ref, bb_ref,
    patch_ref, var_ref, query_ref, hot_ref, lead_hot_ref, lead_ref, gain_ref, heads, highs, o_ref,
):
    padded, width = patch_ref.shape
    marks = head_marks(width)
    query = query_ref[5 * V + LEADS : 5 * V + LEADS + 1, :]
    keyed_grad = exact_product(ka_ref[...] + kb_ref[...], marks, TN)
    bias_grad = exact_product(ba_ref[...] + bb_ref[...], marks, TN)
    o_ref[...] = jnp.zeros_like(o_ref)
    patch_grad = (pa_ref[...] + pb_ref[...]).T + keyed_grad * query
    o_ref[: 4 * V, :] = patch_grad[: 4 * V, :]
    var_grad = (va_ref[...] + vb_ref[...]).T + bias_grad * query
    var_rows = exact_product(quarter_marks(padded), var_grad, TN)
    o_ref[4 * V : 5 * V, :] = exact_product(hot_ref[...], var_rows, TN)
    lead_rows = exact_product(lead_hot_ref[...], lead_ref[...], TN)
    o_ref[5 * V : 5 * V + LEADS, :] = lead_rows[:LEADS, :]
    query_grad = jnp.sum(
        keyed_grad * patch_ref[...] + bias_grad * var_ref[...], axis=0, keepdims=True
    )
    o_ref[5 * V + LEADS : 5 * V + LEADS + 1, :] = query_grad
    o_ref[5 * V + LEADS + 1 : 5 * V + LEADS + 3, :] = gain_ref[...]
    o_ref[padded : padded + 4 * V, :] = heads[0] + heads[1]
    o_ref[padded + 4 * V : padded + 4 * V + 4, :] = highs[0] + highs[1]


def table_grads_kernel(*refs):
    head_a, head_b, high_a, high_b = refs[15:19]
    heads, highs = (head_a[...], head_b[...]), (high_a[2:6, :], high_b[2:6, :])
    table_rows(*refs[:15], heads, highs, refs[19])


def table_grads(first, second, prepared, query, var_hot, lead_hots, leads, gain_rows, heads, highs):
    patch, variable, _, _ = prepared
    operands = []
    for one, two in zip(first, second):
        operands += [one, two]
    return pl.pallas_call(
        table_grads_kernel,
        out_shape=jax.ShapeDtypeStruct((2 * patch.shape[0], D), f32),
        compiler_params=pltpu.CompilerParams(vmem_limit_bytes=BIG),
        name="table_grads",
    )(*operands, patch, variable, query, var_hot, lead_hots, leads, gain_rows, *heads, *highs)


def adam_step(master, grad, first, second, rate):
    first_new = beta_first * first + (1.0 - beta_first) * grad
    second_new = beta_second * second + (1.0 - beta_second) * grad * grad
    update = first_new / first_fix / (jnp.sqrt(second_new / second_fix) + adam_eps)
    return (master - rate * (update + decay_rate * master), first_new, second_new)


def update_kernel(packed, *refs):
    where_ref, sums_ref, tile_ref, count_ref = refs[:4]
    shares = list(refs[4 : 4 + (3 if packed else 4)])
    rest = refs[4 + len(shares) :]
    states, average_ref, outs = rest[:18], rest[18], rest[19:]
    norm = jnp.sqrt(tile_ref[0:1, 0:1])
    factor = jnp.minimum(1.0, clip_norm / (norm + 1e-06))
    outs[1][...] = norm
    outs[0][...] = tile_ref[1:2, 0:1] / (2.0 * V * jnp.maximum(count_ref[...], 1.0))
    embed_rows = 5 * V + LEADS + 1
    padded = 256

    def apply(index, grad, rate, rows=slice(None)):
        master, first, second = (ref[rows, :] for ref in states[3 * index : 3 * index + 3])
        new = adam_step(master, factor * grad, first, second, rate)
        for ref, value in zip(outs[2 + 3 * index : 5 + 3 * index], new):
            ref[rows, :] = value
        return new[0]

    apply(0, sums_ref[:embed_rows, :], lr_table, slice(0, embed_rows))
    apply(0, sums_ref[padded : padded + 4 * V, :], lr_table, slice(embed_rows, embed_rows + 4 * V))
    apply(1, sums_ref[embed_rows : embed_rows + 2, :], lr_gain, slice(0, 2))
    apply(1, sums_ref[padded + 4 * V : padded + 4 * V + 4, :], lr_gain, slice(2, 6))
    if packed:
        units = shares[2].shape[0]
        grads = (
            shares[0][...], shares[1][units:, :], shares[1][:units, :].T, shares[2][...]
        )
    else:
        grads = [share[...] for share in shares]
    qkv_new = apply(2, grads[0], lr_matrix)
    for index in range(1, 4):
        apply(2 + index, grads[index], lr_matrix)
    outs[20][...] = average_keep * average_ref[...] + (1.0 - average_keep) * qkv_new


def update_all(packed, where, sums, tile, count, shares, states, average):
    operands = [sums, tile, count.reshape(1, 1), *shares]
    fixed = lambda shape: pl.BlockSpec(shape, lambda i, w: (0, 0))
    in_specs = [fixed(value.shape) for value in operands]
    out_shapes = [(1, 1), (1, 1)]
    for master, first, second in states:
        if master.shape == first.shape:
            in_specs.append(fixed(master.shape))
        elif master.shape[0] == first.shape[0]:
            in_specs.append(pl.BlockSpec(first.shape, lambda i, w: (0, w[0])))
        else:
            in_specs.append(pl.BlockSpec(first.shape, lambda i, w: (w[0], 0)))
        in_specs += [fixed(first.shape)] * 2
        operands += [master, first, second]
        out_shapes += [first.shape] * 3
    operands.append(average)
    in_specs.append(fixed(average.shape))
    out_shapes.append(average.shape)
    return pl.pallas_call(
        partial(update_kernel, packed),
        grid_spec=pltpu.PrefetchScalarGridSpec(
            num_scalar_prefetch=1,
            grid=(1,),
            in_specs=in_specs,
            out_specs=[fixed(shape) for shape in out_shapes],
        ),
        out_shape=[jax.ShapeDtypeStruct(shape, f32) for shape in out_shapes],
        compiler_params=pltpu.CompilerParams(vmem_limit_bytes=60 * 2**20),
        name="update_all",
    )(where, *operands)


def by_kind(shard):
    rows = shard.shape[0]
    return shard.reshape(rows, -1, 3, HEAD_DIM).transpose(0, 2, 1, 3).reshape(rows, -1)


def by_head(shard):
    rows = shard.shape[0]
    return shard.reshape(rows, 3, -1, HEAD_DIM).transpose(0, 2, 1, 3).reshape(rows, -1)


class Rows:
    count = 11

    def __init__(self, refs, sems):
        (self.h1, self.rows_ref, self.weight, self.qkv, self.vt, self.o_ref, self.full, self.lse,
         self.attended) = refs
        self.sems, self.o_sems, self.own_sem = sems
        dp, level, core = mesh_place()
        self.dp, self.core = dp, core
        self.me = dp * 2 + core
        self.height = self.h1.shape[0]
        self.width = self.o_ref.shape[1]
        half = self.height // 2
        x = lax.rem(dp, 2)
        beside, below, far = dp + 1 - 2 * x, lax.rem(dp + 2, 4), 3 - dp
        self.owners = (beside, below, far)
        self.peers = []
        for move in range(1, 8):
            part = lax.rem(self.me + move, 8)
            self.peers.append(device_of(part // 2, level, lax.rem(part, 2)))
        side = device_of(beside, level, core)
        down = device_of(below, level, core)
        near = device_of(dp, level, 1 - core)
        self.level = level
        slots = [0]

        def remote(source, target_ref, target):
            slot = slots[0]
            slots[0] += 1
            return pltpu.make_async_remote_copy(
                src_ref=source,
                dst_ref=target_ref,
                send_sem=self.sems.at[0, slot],
                recv_sem=self.sems.at[1, slot],
                device_id=target,
                device_id_type=MESH,
            )

        def place(owner, first, size):
            start = pl.multiple_of((owner * 2 + core) * self.height + first, half)
            return self.rows_ref.at[pl.ds(start, size)]

        def relay(where, target):
            return remote(where, where, target)

        first, second = self.h1.at[pl.ds(0, half)], self.h1.at[pl.ds(half, half)]
        self.side_a = remote(first, place(dp, 0, half), side)
        self.down_b = remote(second, place(dp, half, half), down)
        self.side_b = remote(second, place(dp, half, half), side)
        self.down_a = remote(first, place(dp, 0, half), down)
        self.near_own = remote(self.h1, place(dp, 0, self.height), near)
        self.far_a = relay(place(beside, 0, half), down)
        self.far_b = relay(place(below, half, half), side)
        self.near_side = relay(place(beside, 0, self.height), near)
        self.near_down = relay(place(below, 0, self.height), near)
        self.near_far = relay(place(far, 0, self.height), near)

    def part_rows(self, part):
        return pl.ds(pl.multiple_of(part * self.height, self.height), self.height)

    def project(self, owner, core):
        where = self.part_rows(owner * 2 + core)
        self.qkv[where, :] = lax.dot_general(
            self.rows_ref[where, :], self.weight[...], NT, preferred_element_type=f32
        ).astype(bf16)

    def send_o(self, part, target):
        columns = pl.ds(pl.multiple_of(self.me * self.width, self.width), self.width)
        return pltpu.make_async_remote_copy(
            src_ref=self.o_ref.at[self.part_rows(part), :],
            dst_ref=self.attended.at[:, columns],
            send_sem=self.o_sems.at[0, lax.rem(part + 8 - self.me, 8)],
            recv_sem=self.o_sems.at[1, lax.rem(part + 8 - self.me, 8)],
            device_id=target,
            device_id_type=MESH,
        )

    def keep_o(self):
        columns = pl.ds(pl.multiple_of(self.me * self.width, self.width), self.width)
        return pltpu.make_async_copy(
            self.o_ref.at[self.part_rows(self.me), :], self.attended.at[:, columns], self.own_sem
        )

    def phase(self, number):
        beside, below, far = self.owners
        if number == 0:
            for copy in (self.side_a, self.down_b, self.side_b, self.down_a, self.near_own):
                copy.start()
            self.rows_ref[self.part_rows(self.me), :] = self.h1[...]
        elif number == 1:
            self.project(self.dp, self.core)
            self.near_own.wait_recv()
        elif number == 2:
            self.side_a.wait_recv()
            self.far_a.start()
            self.down_b.wait_recv()
            self.far_b.start()
            self.project(self.dp, 1 - self.core)
        elif number == 3:
            self.side_b.wait_recv()
            self.near_side.start()
            self.down_a.wait_recv()
            self.near_down.start()
            self.project(beside, self.core)
            self.project(below, self.core)
        elif number == 4:
            self.near_side.wait_recv()
            self.near_down.wait_recv()
            self.project(beside, 1 - self.core)
            self.project(below, 1 - self.core)
        elif number == 5:
            self.far_a.wait_recv()
            self.far_b.wait_recv()
            self.near_far.start()
            self.project(far, self.core)
        elif number == 6:
            self.near_far.wait_recv()
            self.project(far, 1 - self.core)
            self.vt[...] = self.qkv[:, 2 * self.width :].T

    def attend(self, turn):
        owner = lax.rem(self.dp + 1 + turn, 4)
        size = 2 * self.height
        where = pl.ds(pl.multiple_of(owner * size, size), size)
        heads = self.width // HEAD_DIM
        full, sums = attend_rows(
            heads, self.qkv[where, : self.width],
            self.qkv.at[:, self.width : 2 * self.width], self.vt,
        )
        for head in range(heads):
            self.lse[head : head + 1, where] = sums[head]
        self.full[where, :] = full
        self.o_ref[where, :] = full.astype(bf16)

        @pl.when(turn < 3)
        def _():
            for core in range(2):
                self.send_o(owner * 2 + core, device_of(owner, self.level, core)).start()

        @pl.when(turn == 3)
        def _():
            other = device_of(self.dp, self.level, 1 - self.core)
            self.send_o(self.dp * 2 + 1 - self.core, other).start()
            self.keep_o().start()

    def finish(self):
        for move in range(1, 8):
            part = lax.rem(self.me + move, 8)
            self.send_o(part, self.peers[move - 1]).wait()
        self.keep_o().wait()
        for copy in (
            self.side_a, self.down_b, self.side_b, self.down_a, self.near_own, self.far_a,
            self.far_b, self.near_side, self.near_down, self.near_far,
        ):
            copy.wait_send()


def row_scratch(rows, width):
    return [
        pltpu.VMEM((rows, D), bf16),
        pltpu.VMEM((8 * rows, D), bf16),
        pltpu.VMEM((3 * width, D), bf16),
        pltpu.VMEM((width, 8 * rows), bf16),
        pltpu.VMEM((8 * rows, width), bf16),
        pltpu.SemaphoreType.DMA((2, 10)),
        pltpu.SemaphoreType.DMA((2, 8)),
        pltpu.SemaphoreType.DMA((3,)),
    ]


def lead_rows_of(lead, lead_ref):
    row = lax.broadcasted_iota(jnp.int32, (1, 8), 1).astype(f32)
    lead_hot = jnp.where(row == lead, 1.0, 0.0).astype(f32)
    return exact_product(lead_hot, lead_ref[5 * V : 5 * V + 8, :])


def middle_kernel(
    guess_ref, first_ref, keyed_ref, bias_ref, patch_ref, var_ref, lead_ref, gains_ref, weights_ref,
    x0_ref, cells_ref, qkv_ref, full_ref, lse_ref, rows_out, attended_ref,
    h1_ref, rows_ref, weight_ref, vt_ref, o_ref, sems, o_sems, own_sem,
):
    turn = pl.program_id(0)
    dp, _, core = mesh_place()
    rows = Rows(
        (h1_ref, rows_ref, weight_ref, qkv_ref, vt_ref, o_ref, full_ref, lse_ref, attended_ref),
        (sems, o_sems, own_sem.at[0]),
    )
    size = weight_ref.shape[0]
    weight = pltpu.make_async_copy(
        weights_ref.at[pl.ds(pl.multiple_of((dp * 2 + core) * size, size), size), :],
        weight_ref, own_sem.at[1],
    )
    save = pltpu.make_async_copy(rows_ref, rows_out, own_sem.at[2])
    pairs = HEADS // 2

    @pl.when(turn == 0)
    def _():
        barrier = pltpu.get_barrier_semaphore()
        for target in rows.peers:
            pl.semaphore_signal(barrier, inc=1, device_id=target, device_id_type=MESH)
        pl.semaphore_wait(barrier, 7)
        weight.start()
        cells_ref[:, : 4 * V] = guess_ref[...]
        cells_ref[:, 4 * V :] = jnp.zeros_like(cells_ref[:, 4 * V :])

    @pl.when(turn < pairs)
    def _():
        embed_pair(turn, cells_ref[...], keyed_ref, bias_ref, patch_ref, var_ref, x0_ref)

    @pl.when(turn == pairs)
    def _():
        x0_ref[...] += lead_rows_of(first_ref[0:1, 4 * V + 5 : 4 * V + 6], lead_ref)
        unit, _ = normed_parts(x0_ref[...])
        h1_ref[...] = (unit * gains_ref[0:1, :] + gains_ref[1:2, :]).astype(bf16)
        weight.wait()

    for number in range(7):

        @pl.when(turn == pairs + number)
        def _(number=number):
            rows.phase(number)
            if number == 6:
                save.start()

    @pl.when(turn >= pairs + 7)
    def _():
        rows.attend(turn - pairs - 7)

    @pl.when(turn == pairs + 10)
    def _():
        rows.finish()
        save.wait()


def middle_program(guess, first_cells, prepared, lead_table, norm_gains, qkv_t):
    patch, variable, keyed, bias = prepared
    rows = guess.shape[0]
    padded = patch.shape[0]
    width = D // 8
    heads = width // HEAD_DIM
    total = 8 * rows
    anywhere = pl.BlockSpec(memory_space=pl.ANY)
    fixed = lambda shape: pl.BlockSpec(shape, lambda i: (0, 0))
    by_pair = pl.BlockSpec(
        (padded, 2 * HEAD_DIM), lambda i: (0, jnp.clip(i, 0, HEADS // 2 - 1))
    )
    shapes = [
        ((rows, D), f32),
        ((rows, padded), f32),
        ((total, 3 * width), bf16),
        ((total, width), f32),
        ((heads, total), f32),
    ]
    return pl.pallas_call(
        middle_kernel,
        grid=(HEADS // 2 + Rows.count,),
        out_shape=[jax.ShapeDtypeStruct(shape, kind) for shape, kind in shapes]
        + [jax.ShapeDtypeStruct((total, D), bf16), jax.ShapeDtypeStruct((rows, D), bf16)],
        in_specs=[once(value.shape) for value in (guess, first_cells, keyed, bias)]
        + [by_pair, by_pair, once(lead_table.shape), once(norm_gains.shape), anywhere],
        out_specs=[fixed(shape) for shape, _ in shapes] + [anywhere, anywhere],
        scratch_shapes=row_scratch(rows, width),
        compiler_params=pltpu.CompilerParams(
            collective_id=9, has_side_effects=True, vmem_limit_bytes=BIG
        ),
        name="middle_program",
    )(guess, first_cells, keyed, bias, patch, variable, lead_table, norm_gains, qkv_t)


lag_one, lag_two, ahead = 2, 4, 3
embed_at, gather_at = 3, 11


def start_kernel(halves, *refs):
    count = len(halves)
    packed_ref, keyed_ref, bias_ref, patch_ref, var_ref, lead_ref, gains_ref = refs[:7]
    shards = refs[7 : 7 + count]
    x0_ref, cells_ref, qkv_ref, full_ref, lse_ref, count_ref, rows_out, attended_ref = refs[
        7 + count : 15 + count
    ]
    outs = refs[15 + count : 15 + 2 * count]
    (h1_ref, rows_ref, weight_ref, vt_ref, o_ref, row_sems, o_sems, row_own, held_ref, tile_ref,
     send_sem, recv_sem, level_send, level_recv, own_sem) = refs[15 + 2 * count :]
    rows = Rows(
        (h1_ref, rows_ref, weight_ref, qkv_ref, vt_ref, o_ref, full_ref, lse_ref, attended_ref),
        (row_sems, o_sems, row_own.at[0]),
    )
    step = pl.program_id(0)
    dp, level, core = mesh_place()
    x = lax.rem(dp, 2)
    columns = {"here": dp, "side": dp + 1 - 2 * x, "down": lax.rem(dp + 2, 4), "far": 3 - dp}
    side = device_of(columns["side"], level, core)
    down = device_of(columns["down"], level, core)
    near = device_of(dp, level, 1 - core)
    across = device_of(level, dp, core)
    middle = lax.rem(level, 3) != 0
    late = level // 2
    sources = (level + 1 - 2 * lax.rem(level, 2), 2 - late, 3 * (1 - late))
    onward = (3 - level, lax.rem(3 * level + 1, 4), lax.rem(3 * level + 1, 4))
    slots = [0]

    def remote(source, target_ref, target):
        slot = slots[0]
        slots[0] += 1
        return pltpu.make_async_remote_copy(
            src_ref=source,
            dst_ref=target_ref,
            send_sem=send_sem.at[slot],
            recv_sem=recv_sem.at[slot],
            device_id=target,
            device_id_type=MESH,
        )

    def place(out, source, column, half, pieces):
        rows = out.shape[1] // 4
        size = rows // pieces
        start = pl.multiple_of(columns[column] * rows + half * size, size)
        return out.at[source * 2 + core, pl.ds(start, size), :]

    def pass_on(out, source, column, target, cut):
        where = place(out, source, column, *cut)
        return remote(where, where, target)

    crossing = remote(packed_ref, held_ref, across)
    staying = pltpu.make_async_copy(packed_ref, held_ref, own_sem.at[count])
    mine = [outs[index].at[level * 2 + core] for index in range(count)]
    given = [remote(shards[index], mine[index], near) for index in range(count)]
    kept = [
        pltpu.make_async_copy(shards[index], mine[index], own_sem.at[index]) for index in range(count)
    ]
    chunks, openings = [], []
    for index in range(count):
        out, pieces = outs[index], halves[index]
        for half in range(pieces):
            group = len(openings)
            full = out.shape[1] // 4
            size = full // pieces
            own = shards[index].at[pl.ds(pl.multiple_of(dp * full + half * size, size), size), :]
            cut = (half, pieces)

            def along(source_ref, source, target_level, slot):
                return pltpu.make_async_remote_copy(
                    src_ref=source_ref,
                    dst_ref=place(out, source, "here", *cut),
                    send_sem=level_send.at[group * 5 + slot],
                    recv_sem=level_recv.at[group * 4 + source],
                    device_id=device_of(dp, target_level, core),
                    device_id_type=MESH,
                )

            openings.append(
                (
                    along(own, level, lax.rem(level + 1, 4), 0),
                    along(own, level, lax.rem(level + 3, 4), 1),
                )
            )
            for turn in range(3):
                source = sources[turn]
                chunks.append(
                    {
                        "level": along(place(out, source, "here", *cut), source, onward[turn], 2 + turn),
                        "side": pass_on(out, source, "here", side, cut),
                        "down": pass_on(out, source, "here", down, cut),
                        "hop_down": pass_on(out, source, "side", down, (2 * half, 2 * pieces)),
                        "hop_side": pass_on(out, source, "down", side, (2 * half + 1, 2 * pieces)),
                        "here_near": pass_on(out, source, "here", near, cut),
                        "side_near": pass_on(out, source, "side", near, cut),
                        "down_near": pass_on(out, source, "down", near, cut),
                        "far_near": pass_on(out, source, "far", near, cut),
                    }
                )
    groups = len(openings)
    order = []
    for number in range(groups + 2):
        for turn in range(3):
            if 0 <= number - turn < groups:
                order.append((number - turn, turn))
    chunks = [chunks[3 * group + turn] for group, turn in order]
    total = len(chunks)

    def start_group(number):
        @pl.when(level < 3)
        def _():
            openings[number][0].start()

        @pl.when(level > 0)
        def _():
            openings[number][1].start()

    tiles = [
        remote(tile_ref.at[0], tile_ref.at[1], side),
        remote(tile_ref.at[2], tile_ref.at[3], down),
        remote(tile_ref.at[4], tile_ref.at[5], near),
    ]
    deep = [device_of(dp, lax.rem(level + move, 4), core) for move in (1, 2, 3)]
    level_tiles = [remote(tile_ref.at[6], tile_ref.at[7 + move], deep[move]) for move in range(3)]
    weight = pltpu.make_async_copy(outs[0].at[dp * 2 + core], weight_ref, row_own.at[1])
    save = pltpu.make_async_copy(rows_ref, rows_out, row_own.at[2])

    @pl.when(step == 0)
    def _():
        barrier = pltpu.get_barrier_semaphore()
        for target in (*rows.peers, *deep):
            pl.semaphore_signal(barrier, inc=1, device_id=target, device_id_type=MESH)

        @pl.when(dp != level)
        def _():
            pl.semaphore_signal(barrier, inc=1, device_id=across, device_id_type=MESH)
            pl.semaphore_wait(barrier, 11)
            crossing.start()

        @pl.when(dp == level)
        def _():
            pl.semaphore_wait(barrier, 10)
            staying.start()

        for number in range(ahead):
            start_group(number)
        for copy in (*given, *kept):
            copy.start()

    for number in range(total + lag_two):

        @pl.when(step == number)
        def _(number=number):
            if number < total:
                chunk = chunks[number]
                chunk["level"].wait_recv()

                @pl.when(middle)
                def _():
                    chunk["level"].start()

                chunk["side"].start()
                chunk["down"].start()
                chunk["here_near"].start()
                group, turn = order[number]
                if turn == 0 and group + ahead < groups:
                    start_group(group + ahead)
            if 0 <= number - lag_one < total:
                chunk = chunks[number - lag_one]
                chunk["side"].wait_recv()
                chunk["hop_down"].start()
                chunk["down"].wait_recv()
                chunk["hop_side"].start()
                chunk["side_near"].start()
                chunk["down_near"].start()
            if 0 <= number - lag_two < total:
                chunk = chunks[number - lag_two]
                chunk["hop_down"].wait_recv()
                chunk["hop_side"].wait_recv()
                chunk["far_near"].start()

    @pl.when(step == embed_at)
    def _():
        @pl.when(dp != level)
        def _():
            crossing.wait_recv()

        @pl.when(dp == level)
        def _():
            staying.wait()

        cells_ref[...] = held_ref[...]
        lane = lax.broadcasted_iota(jnp.int32, held_ref.shape, 1)
        ocean = jnp.where((lane >= 4 * V) & (lane < 4 * V + 4), 1.0 - held_ref[...], 0.0)
        tile_ref[0] = jnp.broadcast_to(jnp.sum(ocean), tile_ref.shape[1:])
        tiles[0].start()

    for turn in range(3):

        @pl.when(step == embed_at + 2 + turn)
        def _(turn=turn):
            tiles[turn].wait_recv()
            tile_ref[2 * turn + 2] = tile_ref[2 * turn] + tile_ref[2 * turn + 1]
            for copy in (tiles[1:2], tiles[2:3], level_tiles)[turn]:
                copy.start()

    @pl.when(step == embed_at + 6)
    def _():
        for copy in level_tiles:
            copy.wait_recv()
        count_ref[...] = tile_ref[6] + tile_ref[7] + tile_ref[8] + tile_ref[9]

    @pl.when((step >= embed_at) & (step < embed_at + HEADS // 2))
    def _():
        embed_pair(step - embed_at, held_ref[...], keyed_ref, bias_ref, patch_ref, var_ref, x0_ref)

    @pl.when(step == gather_at - 2)
    def _():
        kept[0].wait()
        weight.start()

    @pl.when(step == gather_at)
    def _():
        x0_ref[...] += lead_rows_of(held_ref[0:1, 4 * V + 4 : 4 * V + 5], lead_ref)
        unit, _ = normed_parts(x0_ref[...])
        h1_ref[...] = (unit * gains_ref[0:1, :] + gains_ref[1:2, :]).astype(bf16)
        weight.wait()

    for number in range(7):

        @pl.when(step == gather_at + number)
        def _(number=number):
            rows.phase(number)
            if number == 6:
                save.start()

    @pl.when((step >= gather_at + 7) & (step < gather_at + 11))
    def _():
        rows.attend(step - gather_at - 7)

    @pl.when(step == total + lag_two - 1)
    def _():
        for copy in given:
            copy.wait()
        for copy in kept[1:]:
            copy.wait()
        for number in range(groups):

            @pl.when(level < 3)
            def _(number=number):
                openings[number][0].wait_send()

            @pl.when(level > 0)
            def _(number=number):
                openings[number][1].wait_send()

        for chunk in chunks:
            for name in ("here_near", "side_near", "down_near", "far_near"):
                chunk[name].wait_recv()
            for name, copy in chunk.items():
                if name != "level":
                    copy.wait_send()

            @pl.when(middle)
            def _(chunk=chunk):
                chunk["level"].wait_send()

        rows.finish()
        for copy in (*tiles, *level_tiles):
            copy.wait_send()
        save.wait()

        @pl.when(dp != level)
        def _():
            crossing.wait_send()


def start_program(packed, prepared, lead_table, norm_gains, shards, halves):
    patch, variable, keyed, bias = prepared
    count = len(shards)
    groups = sum(halves)
    copies = groups * 24 + count + 7
    rows, padded = packed.shape
    total = 8 * rows
    width = shards[0].shape[0] // 3
    heads = width // HEAD_DIM
    anywhere = pl.BlockSpec(memory_space=pl.ANY)
    fixed = lambda shape: pl.BlockSpec(shape, lambda i: (0, 0))
    by_pair = pl.BlockSpec(
        (padded, 2 * HEAD_DIM), lambda i: (0, jnp.clip(i - embed_at, 0, HEADS // 2 - 1))
    )
    shapes = [
        ((rows, D), f32),
        (packed.shape, f32),
        ((total, 3 * width), bf16),
        ((total, width), f32),
        ((heads, total), f32),
        ((8, 128), f32),
    ]
    return pl.pallas_call(
        partial(start_kernel, halves),
        grid=(groups * 3 + lag_two,),
        out_shape=[jax.ShapeDtypeStruct(shape, kind) for shape, kind in shapes]
        + [jax.ShapeDtypeStruct((total, D), bf16), jax.ShapeDtypeStruct((rows, D), bf16)]
        + [jax.ShapeDtypeStruct((8,) + shard.shape, bf16) for shard in shards],
        in_specs=[anywhere]
        + [fixed(keyed.shape), fixed(bias.shape), by_pair, by_pair]
        + [fixed(lead_table.shape), fixed(norm_gains.shape)]
        + [fixed(shard.shape) for shard in shards],
        out_specs=[fixed(shape) for shape, _ in shapes] + [anywhere] * (count + 2),
        scratch_shapes=row_scratch(rows, width)
        + [
            pltpu.VMEM(packed.shape, f32),
            pltpu.VMEM((10, 8, 128), f32),
            pltpu.SemaphoreType.DMA((copies,)),
            pltpu.SemaphoreType.DMA((copies,)),
            pltpu.SemaphoreType.DMA((groups * 5,)),
            pltpu.SemaphoreType.DMA((groups * 4,)),
            pltpu.SemaphoreType.DMA((count + 1,)),
        ],
        compiler_params=pltpu.CompilerParams(
            collective_id=7, has_side_effects=True, vmem_limit_bytes=BIG
        ),
        name="start_program",
    )(packed, keyed, bias, patch, variable, lead_table, norm_gains, *shards)


def shards(
    crossed,
    fields,
    targets,
    land_mask,
    lead_index,
    var_ids,
    tables,
    norm_gains,
    tables_first,
    tables_second,
    gains_first,
    gains_second,
    w_qkv,
    qkv_first,
    qkv_second,
    w_out,
    out_first,
    out_second,
    w_up,
    up_first,
    up_second,
    w_down,
    down_first,
    down_second,
    qkv_average,
):
    local_samples, shard_rows, _ = fields.shape
    dp_size, parts = lax.axis_size("dp"), lax.axis_size("mp")
    dp_index = lax.axis_index("dp")
    place, level, core = mesh_place()
    part = place * 2 + core if crossed else lax.axis_index("mp")
    share_rows = D // dp_size

    def own_share(full, dim):
        return lax.dynamic_slice_in_dim(full, dp_index * share_rows, share_rows, dim)

    var_hot = (var_ids[:, None] == jnp.arange(V, dtype=jnp.int32)[None, :]).astype(f32)
    prepared = prepare_tables(tables, var_hot)
    low = lambda master: master.astype(bf16)
    qkv_low = by_kind(low(w_qkv))
    packed = jnp.concatenate(
        (
            fields[0],
            land_mask[0].astype(f32),
            jnp.broadcast_to(lead_index.astype(f32), (shard_rows, 2)),
            jnp.zeros((shard_rows, 64 - 6), f32),
        ),
        axis=1,
    )
    if crossed:
        (
            x_first, cells, packed, full, logsum, count, rows_one, attended,
            qkv_t, w_outs, w_ups, w_downs
        ) = start_program(
            packed, prepared, tables, norm_gains,
            (qkv_low.T, low(w_out), low(w_up), low(w_down)), (1, 1, 2, 2),
        )
        count = count[0, 0]
    else:
        cells = packed
        answers = targets[0]
        count = lax.psum(jnp.sum(1.0 - cells[:, 4 * V : 4 * V + 4]), ("dp", "mp"))
        w_outs, w_ups, w_downs, qkv_t = [
            lax.all_gather(shard, "mp")
            for shard in (low(w_out), low(w_up), low(w_down), qkv_low.T)
        ]
    gathered = (w_outs.reshape(D, D), w_ups, w_downs.reshape(-1, D), qkv_t.reshape(3 * D, D))
    if not crossed:
        qkv_local = choose(qkv_t, part)
    first_cells = cells
    leads = cells[0, 4 * V + 4 : 4 * V + 6].astype(jnp.int32)
    ocean = 1.0 - cells[:, 4 * V : 4 * V + 4]
    denom = 2.0 * V * jnp.maximum(count, 1.0)
    first_row = part * shard_rows
    patch_row = (first_row + jnp.arange(shard_rows, dtype=jnp.int32)) // PATCH_COLS
    row_hot = (patch_row[:, None] == jnp.arange(PATCH_ROWS, dtype=jnp.int32)[None, :]).astype(f32)
    lat_rows = jnp.dot(
        row_hot, lat_weights(2 * PATCH_ROWS).reshape(PATCH_ROWS, 2), precision=highest
    )
    lat_pixels = jnp.broadcast_to(lat_rows[:, :, None], (shard_rows, 2, 2)).reshape(shard_rows, 4)
    weighted = jnp.tile(ocean * lat_pixels, (1, V))
    head = tables
    loss_part = f32(0.0)
    records = []
    for rollout in range(2):
        if crossed and rollout == 1:
            x_first, cells, packed, full, logsum, rows_one, attended = middle_program(
                guess, first_cells, prepared, tables, norm_gains, gathered[3]
            )
        if not crossed:
            if rollout == 1:
                cells = jnp.pad(guess, ((0, 0), (0, 64)))
            lead_row = lax.dynamic_slice_in_dim(tables, 5 * V + leads[rollout], 1, 0)
            x_first, normed = embed_forward(cells, prepared, lead_row, norm_gains)
            rows_one = lax.all_gather(normed, "mp", axis=0, tiled=True)
            packed = lax.dot_general(
                rows_one, qkv_local, NT, preferred_element_type=f32
            ).astype(bf16)
            own_out, full, logsum = attend(packed)
            attended = exchange(own_out, True)
        if crossed and rollout == 0:
            later_targets, attended = tie(targets[0], attended)
            answers = cross(crossed, later_targets)
        x_mid, rows_two, hidden, active, x_last, guess = branch_forward(
            attended, x_first, norm_gains, gathered, head
        )
        miss = guess - answers[rollout]
        loss_part = loss_part + jnp.sum(weighted * miss * miss)
        records.append(
            (cells, x_first, rows_one, packed, full, logsum, attended, x_mid, rows_two,
             hidden, active, x_last, 2.0 * weighted * miss / denom)
        )
    carried = jnp.zeros_like(guess)
    heads, highs = [], []
    lead_hots = (leads[:, None] == jnp.arange(8, dtype=jnp.int32)[None, :]).astype(f32)
    lead_hots = jnp.pad(lead_hots, ((0, 6), (0, 0)))
    query = tables
    gain_low = jnp.zeros((2, D), f32)
    table_parts, lead_sums = [], []
    qkv_grad = jnp.zeros((D, w_qkv.shape[1]), f32)
    kept = []

    for rollout in (1, 0):
        (cells, x_first, rows_one, packed, full, logsum, attended, x_mid, rows_two,
         hidden, active, x_last, loss_grad) = records[rollout]
        last_low, hidden_grad, mid_grad, mid_low, out_grad, gain_part, head_grad = branch_backward(
            loss_grad + carried, x_last, x_mid, norm_gains, hidden, gathered, head
        )
        heads.append(head_grad)
        highs.append(gain_part)
        if crossed:
            (
                own_grad, act_both, dg_both, o_both, dx2_near, h2_near, dx1_near
            ) = exchange_swap(
                out_grad, active, hidden_grad, attended, last_low, rows_two, mid_low
            )
            kept.append(
                (act_both, dg_both, o_both, last_low, dx2_near, rows_two, h2_near, mid_low, dx1_near)
            )
        else:
            flat = lambda value: value.transpose(2, 1, 0, 3).reshape(shard_rows, -1)
            kept.append((attended, rows_two, flat(active), mid_low, flat(hidden_grad), last_low))
            own_grad = exchange(out_grad, False)
        if crossed and rollout == 0:
            token_grad, level_share, down_sum = finish_program(
                [(step[0], step[3], step[4]) for step in kept],
                packed, own_grad, full, logsum, rows_one, qkv_grad,
            )
        elif crossed:
            token_grad, qkv_grad = attend_exchange(packed, own_grad, full, logsum, rows_one)
        else:
            packed_grad = attend_back(own_grad, packed, full, logsum)
            token_grad = exchange(packed_grad, True)
            qkv_grad = qkv_grad + lax.dot_general(
                rows_one, packed_grad, TN, preferred_element_type=f32
            )
        entry = (token_grad, gathered[3], x_first, mid_grad, norm_gains, cells, prepared)
        if crossed and rollout == 0:
            last_rows, up_out_sum = entry_last(
                [step[1:3] + step[5:] for step in kept], *entry,
                query, var_hot, lead_hots, heads, highs,
                (*table_parts[0], lead_sums[0], gain_low),
            )
            break
        cells_grad, gain_one, lead_sum, *table_part = entry_backward(*entry)
        carried = cells_grad[:, : 4 * V]
        gain_low = gain_low + gain_one
        table_parts.append(table_part)
        lead_sums.append(lead_sum)

    def pair(index):
        return (kept[0][index], kept[1][index])

    if not crossed:
        lead_rows = jnp.pad(jnp.concatenate((lead_sums[1], lead_sums[0])), ((0, 6), (0, 0)))
        last_rows = table_grads(
            *table_parts, prepared, query, var_hot, lead_hots, lead_rows, gain_low, heads, highs
        )
    if not crossed:
        qkv_share = by_head(lax.psum_scatter(qkv_grad, "dp", scatter_dimension=0, tiled=True))
    where = dp_index.astype(jnp.int32).reshape(1)
    if crossed:
        last_sum, tile, qkv_share = exchange_sum(
            last_rows, loss_part, level_share, up_out_sum, down_sum
        )
        shares = (by_head(qkv_share), up_out_sum, down_sum)
        masters = (w_qkv, w_out, w_up, w_down)
    else:
        shares = (
            qkv_share,
            outer_plain(pair(0), pair(3), False),
            outer_plain(pair(1), pair(4), True),
            outer_plain(pair(2), pair(5), False),
        )
        squares = sum(jnp.sum(share * share) for share in shares)
        last_sum, loss_sum, squares = lax.psum((last_rows, loss_part, squares), ("dp", "mp"))
        squares = squares + jnp.sum(last_sum * last_sum)
        row = jnp.arange(8, dtype=jnp.int32)[:, None]
        tile = jnp.where(row == 0, squares, jnp.where(row == 1, loss_sum, 0.0))
        tile = jnp.broadcast_to(tile, (8, 128))
        masters = (own_share(w_qkv, 0), own_share(w_out, 1), own_share(w_up, 0), own_share(w_down, 1))
    states = (
        (tables, tables_first, tables_second),
        (norm_gains, gains_first, gains_second),
        (masters[0], qkv_first, qkv_second),
        (masters[1], out_first, out_second),
        (masters[2], up_first, up_second),
        (masters[3], down_first, down_second),
    )
    results = update_all(crossed, where, last_sum, tile, count, shares, states, qkv_average)
    return (results[0][0, 0], results[1][0, 0], *results[2:])


def solution(mesh):
    return jax.shard_map(
        partial(shards, is_crossed(mesh.shape)),
        mesh=mesh,
        in_specs=(
            P("dp", "mp", None),
            P("dp", None, "mp", None),
            P("dp", "mp", None),
            P("dp", None),
            P(),
            P(),
            P(),
            P(),
            P(),
            P(),
            P(),
            P(None, "mp"),
            P("dp", "mp"),
            P("dp", "mp"),
            P("mp", None),
            P("mp", "dp"),
            P("mp", "dp"),
            P(None, "mp"),
            P("dp", "mp"),
            P("dp", "mp"),
            P("mp", None),
            P("mp", "dp"),
            P("mp", "dp"),
            P("dp", "mp"),
        ),
        out_specs=(
            P(),
            P(),
            P(),
            P(),
            P(),
            P(),
            P(),
            P(),
            P("dp", "mp"),
            P("dp", "mp"),
            P("dp", "mp"),
            P("mp", "dp"),
            P("mp", "dp"),
            P("mp", "dp"),
            P("dp", "mp"),
            P("dp", "mp"),
            P("dp", "mp"),
            P("mp", "dp"),
            P("mp", "dp"),
            P("mp", "dp"),
            P("dp", "mp"),
        ),
        check_vma=False,
    )
```
